32 devices in a mesh: section: 2 (over core), group: 4 (over y, x), dp: 4 (over z).
Axes of the slice: x: 2, y: 2, z: 4, core: 2. Of those that a mesh axis runs over, the one named last changes fastest.
Arguments:
- tokens: int32 [4096], P(('group', 'dp')), may hold values from 0 to 16383
- lengths: int32 [32], P(('group', 'dp')), may hold values from 16 to 128, as said below
- levels: int32 [32], P(('group', 'dp')), may hold values from 0 to 63
- noise_rows: bfloat16 [4096, 256], P(('group', 'dp')), may hold values from -6 to 6
- embed_table: bfloat16 [16384, 256], P('dp'), may hold values from -0.75 to 0.75
- w_in: bfloat16 [256, 1024], P('dp'), may hold values from -0.375 to 0.375
- ln_attn: bfloat16 [2, 1024], P('section', 'dp'), may hold values from 0.5 to 1.5
- w_qkv: bfloat16 [2, 1024, 3072], P('section', 'dp'), may hold values from -0.1875 to 0.1875
- w_proj: bfloat16 [2, 1024, 1024], P('section', 'dp'), may hold values from -0.75 to 0.75
- ln_mlp: bfloat16 [2, 1024], P('section', 'dp'), may hold values from 0.5 to 1.5
- w_up: bfloat16 [2, 1024, 4096], P('section', 'dp'), may hold values from -0.1875 to 0.1875
- w_down: bfloat16 [2, 4096, 1024], P('section', 'dp'), may hold values from -0.09375 to 0.09375
- ln_final: bfloat16 [1024], P('dp'), may hold values from 0.5 to 1.5
- w_out: bfloat16 [1024, 256], P('dp'), may hold values from -0.1875 to 0.1875
Outputs:
- token_loss: bfloat16 [4096], P(('group', 'dp'))
- grad_table: float32 [16384, 256], P('dp')
- grad_w_in: float32 [256, 1024], P('dp')
- grad_ln_attn: float32 [2, 1024], P('section', 'dp')
- grad_w_qkv: float32 [2, 1024, 3072], P('section', 'dp')
- grad_w_proj: float32 [2, 1024, 1024], P('section', 'dp')
- grad_ln_mlp: float32 [2, 1024], P('section', 'dp')
- grad_w_up: float32 [2, 1024, 4096], P('section', 'dp')
- grad_w_down: float32 [2, 4096, 1024], P('section', 'dp')
- grad_ln_final: float32 [1024], P('dp')
- grad_w_out: float32 [1024, 256], P('dp')
The draws below stay inside these ranges and needn't reach their ends.
Inputs may be any that keep to these rules, and one draw needn't show every extreme that they name: Sequence lengths; the longest has exactly 128 tokens.
All inputs are finite; a program needn't handle non-finite values.
Results may differ from the reference program's by a relative error of at most 0.015.
Values may be sent and summed in bfloat16 or wider, within the bound.
A program may use at most 320 MiB of HBM per device.

```python
import math
import jax
import jax.numpy as jnp
import numpy as np
from jax import lax

D = 1024
HEADS = 16
HEAD = 64
FF = 4096
EMB = 256
VOCAB = 16384
LEVELS = 64
LEN = 128
SECTIONS = 2
NSEQ = 32
TOKENS = 4096


def draw_lengths(key, part):
    first_key, second_key = jax.random.split(jax.random.fold_in(key, 17))
    left_draw = jax.random.randint(first_key, (NSEQ,), 0, LEN)
    right_draw = jax.random.randint(second_key, (NSEQ,), 0, LEN)
    length_draw = jnp.maximum(LEN - left_draw * right_draw // LEN, LEN // 8)
    length_draw = length_draw.at[0].set(LEN).at[NSEQ - 1].set(LEN // 8)
    return length_draw.astype(jnp.int32)


def with_ends(result, stream_key, low, largest):
    index_at = [jax.random.randint(jax.random.fold_in(stream_key, axis), (), 0, length) for axis, length in enumerate(result.shape)]
    main_axis = result.shape.index(max(result.shape))
    neighbour = index_at[:main_axis] + [(index_at[main_axis] + 1) % result.shape[main_axis]] + index_at[main_axis + 1:]
    return result.at[tuple(index_at)].set(low).at[tuple(neighbour)].set(largest)


def shard_levels(own_key, shape, pieces, least, top_value):
    def one(axis_at, shards_of):
        steps = jax.random.uniform(jax.random.fold_in(jax.random.fold_in(own_key, 6), axis_at), (shards_of,), jnp.float32, least / len(pieces), top_value / len(pieces))
        return jnp.repeat(jnp.exp(steps), shape[axis_at] // shards_of).reshape((-1,) + (1,) * (len(shape) - axis_at - 1))

    gain = one(*pieces[0])
    for cut in pieces[1:]:
        gain = gain * one(*cut)
    return gain


def rank_bounds(count, skew):
    weights = [(1 << 20) // math.isqrt(rank ** skew) + 1 for rank in range(1, count + 1)]
    width = 1 + sum(weights) // (1 << 30)
    return np.cumsum(np.array([max(1, weight // width) for weight in weights]))


def ranked(rng, dims, count, slope):
    table = rank_bounds(count, slope)
    lot = jax.random.randint(jax.random.fold_in(rng, 1), dims, 0, int(table[count - 1]))
    grade = jnp.searchsorted(jnp.asarray(table, jnp.int32), lot, side="right")
    return jax.random.permutation(jax.random.fold_in(rng, 2), count)[grade].astype(jnp.int32)


def scatter_about(key, dims, width, reach, shards=(), kind=jnp.bfloat16):
    gain = shard_levels(key, dims, shards, -0.22, 0.18) if shards else 1.0
    drawn = jax.random.normal(key, dims, jnp.float32) * width * gain
    return jnp.minimum(jnp.maximum(drawn, -reach), reach).astype(kind)


def setup_inputs(seed: int = 0) -> dict:
    key_list = jax.random.split(jax.random.key(seed), 15)
    return {
        "tokens": with_ends(ranked(key_list[0], (TOKENS,), VOCAB, 2), jax.random.fold_in(key_list[0], 3), 0, VOCAB - 1).astype(jnp.int32),
        "lengths": draw_lengths(jax.random.fold_in(key_list[14], 71), 0),
        "levels": with_ends(jax.random.randint(key_list[2], (NSEQ,), 0, LEVELS), jax.random.fold_in(key_list[2], 1), 0, LEVELS - 1).astype(jnp.int32),
        "noise_rows": scatter_about(key_list[3], (TOKENS, EMB), 1.0, 6.0, ((0, 16),)),
        "embed_table": scatter_about(key_list[4], (VOCAB, EMB), 0.125, 0.75, ((0, 4),)),
        "w_in": scatter_about(key_list[5], (EMB, D), EMB ** -0.5, 0.375, ((0, 4),)),
        "ln_attn": jnp.clip(1.0 + 0.1 * jax.random.normal(key_list[6], (SECTIONS, D), jnp.float32), 0.5, 1.5).astype(jnp.bfloat16),
        "w_qkv": scatter_about(key_list[7], (SECTIONS, D, 3 * D), D ** -0.5, 0.1875, ((0, 2), (1, 4))),
        "w_proj": scatter_about(key_list[8], (SECTIONS, D, D), (D // 16) ** -0.5, 0.75, ((0, 2), (1, 4))),
        "ln_mlp": jnp.clip(1.0 + 0.1 * jax.random.normal(key_list[9], (SECTIONS, D), jnp.float32), 0.5, 1.5).astype(jnp.bfloat16),
        "w_up": scatter_about(key_list[10], (SECTIONS, D, FF), D ** -0.5, 0.1875, ((0, 2), (1, 4))),
        "w_down": scatter_about(key_list[11], (SECTIONS, FF, D), FF ** -0.5, 0.09375, ((0, 2), (1, 4))),
        "ln_final": jnp.clip(1.0 + 0.1 * jax.random.normal(key_list[12], (D,), jnp.float32), 0.5, 1.5).astype(jnp.bfloat16),
        "w_out": scatter_about(key_list[13], (D, EMB), D ** -0.5, 0.1875, ((0, 4),)),
    }


EPS = 1e-05
LOG_LOW = -2.995732273553991
LOG_SPAN = 2.995732273553991
EMB_VAR = 0.015625
MASKED = -1e+30
LOSS_GAIN = 16.0
HIGH = lax.Precision.HIGHEST

@jax.custom_vjp
def low(v):
    return lax.optimization_barrier(v.astype(jnp.bfloat16)).astype(jnp.float32)

@jax.custom_vjp
def low_back(v):
    return v

def low_keep(v):
    return (low(v), None)

def low_pass(kept, grad):
    return (grad,)

def back_keep(v):
    return (v, None)

def back_low(kept, grad):
    return (low(grad),)
low.defvjp(low_keep, low_pass)
low_back.defvjp(back_keep, back_low)

def rounded_both(value):
    return low_back(low(value))

def matmul(left_side, right_side):
    return jnp.matmul(left_side, right_side, precision=HIGH)

def normed(inputs, gain_vec):
    center = inputs - lax.optimization_barrier(jnp.mean(inputs, -1, keepdims=True))
    return center * lax.rsqrt(lax.optimization_barrier(jnp.mean(center * center, -1, keepdims=True)) + EPS) * gain_vec

def layer_pass(hidden, key_valid, weights):
    gain_attn, qkv_weight, proj_weight, gain_mlp, up_weight, down_weight = weights
    groups, length, model_width = hidden.shape
    normed_in = low(normed(hidden, gain_attn))
    qkv_rows = rounded_both(matmul(normed_in, qkv_weight))
    query_part = qkv_rows[..., :model_width].reshape(groups, length, HEADS, HEAD)
    key_part = qkv_rows[..., model_width:2 * model_width].reshape(groups, length, HEADS, HEAD)
    value_part = qkv_rows[..., 2 * model_width:].reshape(groups, length, HEADS, HEAD)
    scores = low_back(jnp.einsum('bqhd,bkhd->bhqk', query_part, key_part, precision=HIGH) * 0.125)
    scores = jnp.where(key_valid[:, None, None, :], scores, MASKED)
    probs_low = low(jax.nn.softmax(scores, axis=-1))
    attended = jnp.einsum('bhqk,bkhd->bqhd', probs_low, value_part, precision=HIGH).reshape(groups, length, model_width)
    attended = rounded_both(attended)
    hidden_mid = hidden + low_back(matmul(attended, proj_weight))
    mlp_in = low(normed(hidden_mid, gain_mlp))
    pre_act = low_back(matmul(mlp_in, up_weight))
    activated = low(jax.nn.gelu(pre_act, approximate=False))
    return hidden_mid + low_back(matmul(activated, down_weight))

def reference(tokens, lengths, levels, noise_rows, embed_table, w_in, ln_attn, w_qkv, w_proj, ln_mlp, w_up, w_down, ln_final, w_out):
    params = (embed_table.astype(jnp.float32), w_in.astype(jnp.float32), ln_attn.astype(jnp.float32), w_qkv.astype(jnp.float32), w_proj.astype(jnp.float32), ln_mlp.astype(jnp.float32), w_up.astype(jnp.float32), w_down.astype(jnp.float32), ln_final.astype(jnp.float32), w_out.astype(jnp.float32))
    seq_count = lengths.shape[0]
    batch_seqs = math.gcd(seq_count, max(1, 2048 // LEN))
    block_count = seq_count // batch_seqs
    token_blocks = tokens.reshape(block_count, batch_seqs, LEN)
    length_blocks = lengths.reshape(block_count, batch_seqs)
    level_blocks = levels.reshape(block_count, batch_seqs)
    noise_blocks = noise_rows.astype(jnp.float32).reshape(block_count, batch_seqs, LEN, EMB)
    loss_scale = LOSS_GAIN / math.sqrt(TOKENS)
    positions = jnp.arange(LEN, dtype=jnp.int32)

    def forward(param_set):
        table_vals, in_weight, gain_attn, qkv_weight, proj_weight, gain_mlp, up_weight, down_weight, final_gain, out_weight = param_set

        def step_fn(running_sum, block_data):
            token_ids, seq_lengths, seq_levels, noise_block = block_data
            key_valid = positions[None, :] < seq_lengths[:, None]
            noise_level = jnp.exp(LOG_LOW + seq_levels.astype(jnp.float32) * (LOG_SPAN / (LEVELS - 1)))[:, None, None]
            scale_in = lax.rsqrt(EMB_VAR + noise_level * noise_level)
            looked = jnp.take(table_vals, token_ids, axis=0)
            mixed_in = low((looked + noise_level * noise_block) * scale_in)
            hidden = low_back(matmul(mixed_in, in_weight))
            hidden = layer_pass(hidden, key_valid, (gain_attn[0], qkv_weight[0], proj_weight[0], gain_mlp[0], up_weight[0], down_weight[0]))
            hidden = rounded_both(hidden)
            hidden = layer_pass(hidden, key_valid, (gain_attn[1], qkv_weight[1], proj_weight[1], gain_mlp[1], up_weight[1], down_weight[1]))
            final_in = low(normed(hidden, final_gain))
            projected = rounded_both(matmul(final_in, out_weight))
            logits = low_back(jnp.einsum('bse,ve->bsv', projected, table_vals, precision=HIGH))
            picked = jnp.take_along_axis(logits, token_ids[..., None], axis=-1)[..., 0]
            entropy = jnp.where(key_valid, jax.nn.logsumexp(logits, axis=-1) - picked, 0.0)
            return (running_sum + jnp.sum(entropy), entropy)
        total_sum, entropy = lax.scan(jax.checkpoint(step_fn), jnp.zeros((), jnp.float32), (token_blocks, length_blocks, level_blocks, noise_blocks))
        return (total_sum * loss_scale, entropy.reshape(-1))
    outputs, pullback = jax.vjp(forward, params)
    grads = pullback((jnp.ones((), jnp.float32), jnp.zeros_like(outputs[1])))[0]
    return (outputs[1].astype(jnp.bfloat16), grads[0], grads[1], grads[2], grads[3], grads[4], grads[5], grads[6], grads[7], grads[8], grads[9])
```

```python
import functools
import math

import jax
import jax.numpy as jnp
from jax import lax
from jax.experimental import pallas as pl
from jax.experimental.pallas import tpu as pltpu
from jax.sharding import PartitionSpec as P

HEAD = 64
LEVELS = 64
LEN = 128
MB = 2


EPS = 1e-05
LOG_LOW = -2.995732273553991
LOG_SPAN = 2.995732273553991
EMB_VAR = 0.015625
MASKED = -1e30
LOSS_GAIN = 16.0


def passed_along(x, axis, by):
    count = lax.axis_size(axis)
    pairs = [(i, i + by) for i in range(count) if 0 <= i + by < count]
    return lax.ppermute(x, axis, pairs)


def product(left_side, right_side):
    return jnp.dot(left_side, right_side, preferred_element_type=jnp.float32)


def product_tn(left_side, right_side):
    return lax.dot_general(
        left_side, right_side, (((0,), (0,)), ((), ())), preferred_element_type=jnp.float32
    )


def product_nt(left_side, right_side):
    return lax.dot_general(
        left_side, right_side, (((1,), (1,)), ((), ())), preferred_element_type=jnp.float32
    )


def normed(inputs, gain_vec):
    center = inputs - jnp.mean(inputs, -1, keepdims=True)
    return center * lax.rsqrt(jnp.mean(center * center, -1, keepdims=True) + EPS) * gain_vec


def norm_back(inputs, gain_vec, upstream):
    output, pullback = jax.vjp(normed, inputs, gain_vec)
    return pullback(upstream)


def gelu_exact(values_in):
    return jax.nn.gelu(values_in, approximate=False)


def attn_scores(split_rows, key_valid):
    scores = (
        jnp.einsum(
            "qhd,khd->hqk", split_rows[:, 0], split_rows[:, 1], preferred_element_type=jnp.float32
        )
        * 0.125
    )
    return jnp.where(key_valid[None, None, :], scores, MASKED)


def attend(qkv_rows, key_valid):
    length = qkv_rows.shape[0]
    model_width = qkv_rows.shape[1] // 3
    split_rows = qkv_rows.reshape(length, 3, model_width // HEAD, HEAD)
    scores = attn_scores(split_rows, key_valid)
    row_max = jnp.max(scores, -1, keepdims=True)
    log_total = row_max + jnp.log(jnp.sum(jnp.exp(scores - row_max), -1, keepdims=True))
    probs_low = jnp.exp(scores - log_total).astype(jnp.bfloat16)
    mixed_rows = jnp.einsum(
        "hqk,khd->qhd", probs_low, split_rows[:, 2], preferred_element_type=jnp.float32
    )
    return (mixed_rows.reshape(length, model_width).astype(jnp.bfloat16), log_total)


def attend_back(qkv_rows, key_valid, log_total, grad_mixed):
    length = qkv_rows.shape[0]
    model_width = qkv_rows.shape[1] // 3
    head_count = model_width // HEAD
    split_rows = qkv_rows.reshape(length, 3, head_count, HEAD)
    grad_heads = grad_mixed.reshape(length, head_count, HEAD)
    probs_full = jnp.exp(attn_scores(split_rows, key_valid) - log_total)
    grad_values = jnp.einsum(
        "hqk,qhd->khd",
        probs_full.astype(jnp.bfloat16),
        grad_heads,
        preferred_element_type=jnp.float32,
    )
    grad_probs = jnp.einsum(
        "qhd,khd->hqk", grad_heads, split_rows[:, 2], preferred_element_type=jnp.float32
    )
    grad_scores = (
        probs_full * (grad_probs - jnp.sum(grad_probs * probs_full, -1, keepdims=True))
    ).astype(jnp.bfloat16)
    grad_query = (
        jnp.einsum(
            "hqk,khd->qhd", grad_scores, split_rows[:, 1], preferred_element_type=jnp.float32
        )
        * 0.125
    )
    grad_key = (
        jnp.einsum(
            "hqk,qhd->khd", grad_scores, split_rows[:, 0], preferred_element_type=jnp.float32
        )
        * 0.125
    )
    stacked = jnp.stack([grad_query, grad_key, grad_values], 1).reshape(length, 3 * model_width)
    return stacked.astype(jnp.bfloat16)


def layer_forward(hidden, key_valid, weights):
    gain_attn, qkv_weight, proj_weight, gain_mlp, up_weight, down_weight = weights
    normed_in = normed(hidden, gain_attn).astype(jnp.bfloat16)
    qkv_rows = product(normed_in, qkv_weight).astype(jnp.bfloat16)
    mixed_rows, log_total = attend(qkv_rows, key_valid)
    hidden_mid = hidden + product(mixed_rows, proj_weight)
    mlp_in = normed(hidden_mid, gain_mlp).astype(jnp.bfloat16)
    pre_act = product(mlp_in, up_weight)
    activated = gelu_exact(pre_act).astype(jnp.bfloat16)
    hidden_out = hidden_mid + product(activated, down_weight)
    return (
        hidden_out,
        (
            hidden,
            normed_in,
            qkv_rows,
            log_total,
            mixed_rows,
            hidden_mid,
            mlp_in,
            pre_act,
            activated,
        ),
    )


def empty_kept(length, model_width, hidden_units, head_count):
    return (
        jnp.zeros((length, model_width), jnp.float32),
        jnp.zeros((length, model_width), jnp.bfloat16),
        jnp.zeros((length, 3 * model_width), jnp.bfloat16),
        jnp.zeros((head_count, length, 1), jnp.float32),
        jnp.zeros((length, model_width), jnp.bfloat16),
        jnp.zeros((length, model_width), jnp.float32),
        jnp.zeros((length, model_width), jnp.bfloat16),
        jnp.zeros((length, hidden_units), jnp.float32),
        jnp.zeros((length, hidden_units), jnp.bfloat16),
    )


def layer_backward(kept_vals, grad_out, key_valid, weights):
    hidden, normed_in, qkv_rows, log_total, mixed_rows, hidden_mid, mlp_in, pre_act, activated = (
        kept_vals
    )
    gain_attn, qkv_weight, proj_weight, gain_mlp, up_weight, down_weight = weights
    grad_low = grad_out.astype(jnp.bfloat16)
    grad_activated = product_nt(grad_low, down_weight)
    grad_pre = jax.vjp(gelu_exact, pre_act)[1](grad_activated)[0].astype(jnp.bfloat16)
    grad_mlp_in = product_nt(grad_pre, up_weight)
    grad_mid_norm, grad_gain_mlp = norm_back(hidden_mid, gain_mlp, grad_mlp_in)
    grad_mid = grad_out + grad_mid_norm
    grad_mid_low = grad_mid.astype(jnp.bfloat16)
    grad_mixed = product_nt(grad_mid_low, proj_weight).astype(jnp.bfloat16)
    grad_qkv = attend_back(qkv_rows, key_valid, log_total, grad_mixed)
    grad_normed = product_nt(grad_qkv, qkv_weight)
    grad_in_norm, grad_gain_attn = norm_back(hidden, gain_attn, grad_normed)
    records = (activated, grad_low, mlp_in, grad_pre, mixed_rows, grad_mid_low, normed_in, grad_qkv)
    return (grad_mid + grad_in_norm, (grad_gain_attn, grad_gain_mlp), records)


def layer_zero(length, model_width, hidden_units):
    records = (
        jnp.zeros((length, hidden_units), jnp.bfloat16),
        jnp.zeros((length, model_width), jnp.bfloat16),
        jnp.zeros((length, model_width), jnp.bfloat16),
        jnp.zeros((length, hidden_units), jnp.bfloat16),
        jnp.zeros((length, model_width), jnp.bfloat16),
        jnp.zeros((length, model_width), jnp.bfloat16),
        jnp.zeros((length, model_width), jnp.bfloat16),
        jnp.zeros((length, 3 * model_width), jnp.bfloat16),
    )
    gains = (jnp.zeros((model_width,), jnp.float32), jnp.zeros((model_width,), jnp.float32))
    return (jnp.zeros((length, model_width), jnp.float32), gains, records)


def layer_grads(records):
    activated, grad_low, mlp_in, grad_pre, mixed_rows, grad_mid_low, normed_in, grad_qkv = records
    return (
        product_tn(normed_in, grad_qkv),
        product_tn(mixed_rows, grad_mid_low),
        product_tn(mlp_in, grad_pre),
        product_tn(activated, grad_low),
    )


def embed_inputs(token_ids, noise_block, level_id, table_full):
    noise_level = jnp.exp(LOG_LOW + level_id.astype(jnp.float32) * (LOG_SPAN / (LEVELS - 1)))
    scale_in = lax.rsqrt(EMB_VAR + noise_level * noise_level)
    looked = jnp.take(table_full, token_ids, axis=0).astype(jnp.float32)
    mixed_in = ((looked + noise_level * noise_block.astype(jnp.float32)) * scale_in).astype(
        jnp.bfloat16
    )
    return (mixed_in, scale_in)


def embed_backward(token_ids, noise_block, level_id, grad_start, table_full, in_weight):
    mixed_in, scale_in = embed_inputs(token_ids, noise_block, level_id, table_full)
    grad_low = grad_start.astype(jnp.bfloat16)
    grad_looked = product_nt(grad_low, in_weight) * scale_in
    return (mixed_in, grad_low, grad_looked)


def embed_zero(length, model_width, emb_width):
    return (
        jnp.zeros((length, emb_width), jnp.bfloat16),
        jnp.zeros((length, model_width), jnp.bfloat16),
        jnp.zeros((length, emb_width), jnp.float32),
    )


def tail_pass(hidden, token_ids, key_valid, final_gain, out_weight, table_full, loss_scale):
    final_in = normed(hidden, final_gain).astype(jnp.bfloat16)
    projected = product(final_in, out_weight).astype(jnp.bfloat16)
    logits = product_nt(projected, table_full)
    row_max = jnp.max(logits, -1, keepdims=True)
    log_total = row_max + jnp.log(jnp.sum(jnp.exp(logits - row_max), -1, keepdims=True))
    vocab_ids = lax.broadcasted_iota(jnp.int32, logits.shape, 1)
    target_hit = vocab_ids == token_ids[:, None]
    picked = jnp.sum(jnp.where(target_hit, logits, 0.0), -1)
    entropy = jnp.where(key_valid, log_total[:, 0] - picked, 0.0)
    row_scale = jnp.where(key_valid, loss_scale, 0.0)[:, None]
    grad_logits = (
        (jnp.exp(logits - log_total) - target_hit.astype(jnp.float32)) * row_scale
    ).astype(jnp.bfloat16)
    grad_proj = product(grad_logits, table_full).astype(jnp.bfloat16)
    grad_final = product_nt(grad_proj, out_weight)
    grad_hidden, grad_gain = norm_back(hidden, final_gain, grad_final)
    return (grad_hidden, entropy, grad_gain, (grad_logits, projected, final_in, grad_proj))


def tail_zero(length, model_width, emb_width, vocab_rows):
    records = (
        jnp.zeros((length, vocab_rows), jnp.bfloat16),
        jnp.zeros((length, emb_width), jnp.bfloat16),
        jnp.zeros((length, model_width), jnp.bfloat16),
        jnp.zeros((length, emb_width), jnp.bfloat16),
    )
    return (
        jnp.zeros((length, model_width), jnp.float32),
        jnp.zeros((length,), jnp.float32),
        jnp.zeros((model_width,), jnp.float32),
        records,
    )


def edge_grads(tail_records, embed_records, token_ids):
    grad_logits, projected, final_in, grad_proj = tail_records
    mixed_in, grad_low, grad_looked = embed_records
    table_grad = product_tn(grad_logits, projected).at[token_ids].add(grad_looked)
    return (table_grad, product_tn(mixed_in, grad_low), product_tn(final_in, grad_proj))


def joined_rows(record_list):
    return jax.tree.map(lambda *pieces: jnp.concatenate(pieces, 0), *record_list)


def assemble(gain_attn_sum, gain_mlp_sum, layer_set, edge_set, gain_final_sum):
    return (
        gain_attn_sum[None],
        layer_set[0][None],
        layer_set[1][None],
        gain_mlp_sum[None],
        layer_set[2][None],
        layer_set[3][None],
        edge_set[0],
        edge_set[1],
        gain_final_sum,
        edge_set[2],
    )


def per_device_general(
    tokens,
    lengths,
    levels,
    noise_rows,
    embed_table,
    w_in,
    ln_attn,
    w_qkv,
    w_proj,
    ln_mlp,
    w_up,
    w_down,
    ln_final,
    w_out,
):
    gathered = (
        lax.all_gather(embed_table, "dp", axis=0, tiled=True),
        lax.all_gather(w_in, "dp", axis=0, tiled=True),
        lax.all_gather(ln_attn, "dp", axis=1, tiled=True),
        lax.all_gather(w_qkv, "dp", axis=1, tiled=True),
        lax.all_gather(w_proj, "dp", axis=1, tiled=True),
        lax.all_gather(ln_mlp, "dp", axis=1, tiled=True),
        lax.all_gather(w_up, "dp", axis=1, tiled=True),
        lax.all_gather(w_down, "dp", axis=1, tiled=True),
        lax.all_gather(ln_final, "dp", axis=0, tiled=True),
        lax.all_gather(w_out, "dp", axis=0, tiled=True),
    )
    table_full = gathered[0]
    in_weight = gathered[1]
    layer_weights = (
        gathered[2][0].astype(jnp.float32),
        gathered[3][0],
        gathered[4][0],
        gathered[5][0].astype(jnp.float32),
        gathered[6][0],
        gathered[7][0],
    )
    final_gain = gathered[8].astype(jnp.float32)
    out_weight = gathered[9]
    model_width = out_weight.shape[0]
    emb_width = out_weight.shape[1]
    vocab_rows = table_full.shape[0]
    hidden_units = layer_weights[4].shape[1]
    head_count = model_width // HEAD
    section_index = lax.axis_index("section")
    first_section = section_index == 0
    token_grid = tokens.reshape(MB, LEN)
    noise_grid = noise_rows.reshape(MB, LEN, noise_rows.shape[1])
    positions = jnp.arange(LEN, dtype=jnp.int32)
    valid_grid = positions[None, :] < lengths[:, None]
    loss_scale = LOSS_GAIN / math.sqrt(tokens.shape[0] * lax.axis_size(("group", "dp")))
    gain_attn_sum = jnp.zeros((model_width,), jnp.float32)
    gain_mlp_sum = jnp.zeros((model_width,), jnp.float32)
    gain_final_sum = jnp.zeros((model_width,), jnp.float32)
    recv_act = jnp.zeros((LEN, model_width), jnp.bfloat16)
    recv_grad = jnp.zeros((LEN, model_width), jnp.bfloat16)
    zero_rows = jnp.zeros((LEN, model_width), jnp.float32)
    kept_ticks = {}
    layer_recs = {}
    tail_recs = {}
    embed_recs = {}
    losses = []
    for moment in range(MB + 2):
        offset = moment - section_index
        fwd_valid = (offset >= 0) & (offset < MB)
        fwd_index = jnp.clip(offset, 0, MB - 1)
        ids_now = lax.dynamic_index_in_dim(token_grid, fwd_index, 0, False)
        noise_now = lax.dynamic_index_in_dim(noise_grid, fwd_index, 0, False)
        level_now = lax.dynamic_index_in_dim(levels, fwd_index, 0, False)
        valid_now = lax.dynamic_index_in_dim(valid_grid, fwd_index, 0, False)

        def first_input():
            mixed_in, scale_in = embed_inputs(ids_now, noise_now, level_now, table_full)
            return product(mixed_in, in_weight)

        layer_input = lax.cond(first_section, first_input, lambda: recv_act.astype(jnp.float32))
        hidden_out, kept_now = lax.cond(
            fwd_valid,
            lambda: layer_forward(layer_input, valid_now, layer_weights),
            lambda: (zero_rows, empty_kept(LEN, model_width, hidden_units, head_count)),
        )
        kept_ticks[moment] = kept_now
        tail_live = jnp.logical_not(first_section) & fwd_valid
        tail_grad, entropy, final_step, tail_now = lax.cond(
            tail_live,
            lambda: tail_pass(
                hidden_out, ids_now, valid_now, final_gain, out_weight, table_full, loss_scale
            ),
            lambda: tail_zero(LEN, model_width, emb_width, vocab_rows),
        )
        tail_recs[moment] = tail_now
        gain_final_sum = gain_final_sum + final_step
        back_tick = moment - 2
        late_live = 0 <= back_tick < MB
        late_index = min(max(back_tick, 0), MB - 1)
        kept_late = kept_ticks[back_tick] if back_tick >= 0 else kept_now
        kept_back = lax.cond(first_section, lambda: kept_late, lambda: kept_now)
        grad_top = jnp.where(first_section, recv_grad.astype(jnp.float32), tail_grad)
        valid_back = jnp.where(first_section, valid_grid[late_index], valid_now)
        back_live = jnp.where(first_section, late_live, fwd_valid)
        grad_start, gain_pair, layer_now = lax.cond(
            back_live,
            lambda: layer_backward(kept_back, grad_top, valid_back, layer_weights),
            lambda: layer_zero(LEN, model_width, hidden_units),
        )
        layer_recs[moment] = layer_now
        gain_attn_sum = gain_attn_sum + gain_pair[0]
        gain_mlp_sum = gain_mlp_sum + gain_pair[1]
        if late_live:
            embed_now = lax.cond(
                first_section,
                lambda: embed_backward(
                    token_grid[late_index],
                    noise_grid[late_index],
                    levels[late_index],
                    grad_start,
                    table_full,
                    in_weight,
                ),
                lambda: embed_zero(LEN, model_width, emb_width),
            )
        else:
            embed_now = embed_zero(LEN, model_width, emb_width)
        embed_recs[moment] = embed_now
        if moment < MB:
            recv_act = passed_along(hidden_out.astype(jnp.bfloat16), "section", 1)
        if 1 <= moment <= MB:
            entropy_low = entropy.astype(jnp.bfloat16)
            recv_grad, loss_back = passed_along(
                (grad_start.astype(jnp.bfloat16), entropy_low), "section", -1
            )
            losses.append(jnp.where(first_section, loss_back, entropy_low))
    chosen = [
        jax.tree.map(
            lambda early, late: jnp.where(first_section, early, late),
            layer_recs[micro + 2],
            layer_recs[micro + 1],
        )
        for micro in range(MB)
    ]
    all_layer = layer_grads(joined_rows(chosen))
    all_tail = joined_rows([tail_recs[micro + 1] for micro in range(MB)])
    all_embed = joined_rows([embed_recs[micro + 2] for micro in range(MB)])
    all_edge = edge_grads(all_tail, all_embed, tokens)
    grad_pack = assemble(gain_attn_sum, gain_mlp_sum, all_layer, all_edge, gain_final_sum)
    parted = (
        lax.psum_scatter(
            grad_pack[0].astype(jnp.bfloat16), "dp", scatter_dimension=1, tiled=True
        ).astype(jnp.float32),
        lax.psum_scatter(
            grad_pack[1].astype(jnp.bfloat16), "dp", scatter_dimension=1, tiled=True
        ).astype(jnp.float32),
        lax.psum_scatter(
            grad_pack[2].astype(jnp.bfloat16), "dp", scatter_dimension=1, tiled=True
        ).astype(jnp.float32),
        lax.psum_scatter(
            grad_pack[3].astype(jnp.bfloat16), "dp", scatter_dimension=1, tiled=True
        ).astype(jnp.float32),
        lax.psum_scatter(
            grad_pack[4].astype(jnp.bfloat16), "dp", scatter_dimension=1, tiled=True
        ).astype(jnp.float32),
        lax.psum_scatter(
            grad_pack[5].astype(jnp.bfloat16), "dp", scatter_dimension=1, tiled=True
        ).astype(jnp.float32),
        lax.psum_scatter(
            grad_pack[6].astype(jnp.bfloat16), "dp", scatter_dimension=0, tiled=True
        ).astype(jnp.float32),
        lax.psum_scatter(
            grad_pack[7].astype(jnp.bfloat16), "dp", scatter_dimension=0, tiled=True
        ).astype(jnp.float32),
        lax.psum_scatter(
            grad_pack[8].astype(jnp.bfloat16), "dp", scatter_dimension=0, tiled=True
        ).astype(jnp.float32),
        lax.psum_scatter(
            grad_pack[9].astype(jnp.bfloat16), "dp", scatter_dimension=0, tiled=True
        ).astype(jnp.float32),
    )
    layer_total = (
        lax.psum(parted[0].astype(jnp.bfloat16), "group").astype(jnp.float32),
        lax.psum(parted[1].astype(jnp.bfloat16), "group").astype(jnp.float32),
        lax.psum(parted[2].astype(jnp.bfloat16), "group").astype(jnp.float32),
        lax.psum(parted[3].astype(jnp.bfloat16), "group").astype(jnp.float32),
        lax.psum(parted[4].astype(jnp.bfloat16), "group").astype(jnp.float32),
        lax.psum(parted[5].astype(jnp.bfloat16), "group").astype(jnp.float32),
    )
    edge_total = (
        lax.psum(parted[6].astype(jnp.bfloat16), ("section", "group")).astype(jnp.float32),
        lax.psum(parted[7].astype(jnp.bfloat16), ("section", "group")).astype(jnp.float32),
        lax.psum(parted[8].astype(jnp.bfloat16), ("section", "group")).astype(jnp.float32),
        lax.psum(parted[9].astype(jnp.bfloat16), ("section", "group")).astype(jnp.float32),
    )
    token_loss = jnp.concatenate(losses)
    return (
        token_loss,
        edge_total[0],
        edge_total[1],
        layer_total[0],
        layer_total[1],
        layer_total[2],
        layer_total[3],
        layer_total[4],
        layer_total[5],
        edge_total[2],
        edge_total[3],
    )


MESH = pl.DeviceIdType.MESH
LAYER_ARRAYS = 4


def gather_kernel(count_z, *refs):
    shards = refs[:8]
    wholes = refs[8:16]
    own_sem, zsend, zrecv, psend, precv, gate = refs[16:]
    sec = lax.axis_index("section")
    grp = lax.axis_index("group")
    pos = lax.axis_index("dp")
    beside_x = (sec, grp ^ 1, pos)
    beside_y = (sec, grp ^ 2, pos)

    def along(step):
        return (sec, grp, lax.rem(pos + step, count_z))

    barrier = pltpu.get_barrier_semaphore()
    partners = [beside_x, beside_y, (1 - sec, grp, pos)] + [along(k) for k in range(1, count_z)]
    for partner in partners:
        pl.semaphore_signal(barrier, inc=1, device_id=partner, device_id_type=MESH)
    pl.semaphore_wait(barrier, len(partners))

    def remote(src, dst, send_sem, recv_sem, device):
        return pltpu.make_async_remote_copy(
            src_ref=src,
            dst_ref=dst,
            send_sem=send_sem,
            recv_sem=recv_sem,
            device_id=device,
            device_id_type=MESH,
        )

    def run(order, gains, before, middle):
        own = []
        for slot, idx in enumerate(order):
            rows = shards[idx].shape[0]
            own.append(
                pltpu.make_async_copy(
                    shards[idx], wholes[idx].at[pl.ds(pos * rows, rows)], own_sem.at[slot]
                )
            )
        if before is not None:
            before()
        sends = []
        zin = {}
        rows_g = shards[gains].shape[0]
        own.append(
            pltpu.make_async_copy(
                shards[gains], wholes[gains].at[pl.ds(pos * rows_g, rows_g)], own_sem.at[len(order)]
            )
        )
        for k in range(1, count_z):
            copy = remote(
                shards[gains],
                wholes[gains].at[pl.ds(pos * rows_g, rows_g)],
                zsend.at[len(order), k],
                zrecv.at[len(order), k],
                along(k),
            )
            copy.start()
            zin[len(order), k] = copy
            sends.append(copy)
        for slot, idx in enumerate(order):
            rows = shards[idx].shape[0]
            part = rows // 4
            for k in range(1, count_z):
                copy = remote(
                    shards[idx].at[pl.ds(grp * part, part)],
                    wholes[idx].at[pl.ds(pos * rows + grp * part, part)],
                    zsend.at[slot, k],
                    zrecv.at[slot, k],
                    along(k),
                )
                copy.start()
                zin[slot, k] = copy
                sends.append(copy)
        for copy in own:
            copy.start()
        items = [(slot, idx, k) for slot, idx in enumerate(order) for k in range(1, count_z)]
        crossing = {}

        def block(idx, k, who):
            rows = shards[idx].shape[0]
            part = rows // 4
            origin = lax.rem(pos - k + count_z, count_z)
            return pl.ds(origin * rows + who * part, part)

        def first(slot, idx, k):
            zin[slot, k].wait_recv()
            here = block(idx, k, grp)
            for way, device in ((0, beside_x), (1, beside_y)):
                copy = remote(
                    wholes[idx].at[here],
                    wholes[idx].at[here],
                    psend.at[slot, k, way],
                    precv.at[slot, k, way],
                    device,
                )
                copy.start()
                crossing[slot, k, way] = copy
                sends.append(copy)

        def second(slot, idx, k):
            half = shards[idx].shape[1] // 2
            for way, who, lo, device in ((0, grp ^ 1, 0, beside_y), (1, grp ^ 2, half, beside_x)):
                crossing[slot, k, way].wait_recv()
                there = block(idx, k, who)
                copy = remote(
                    wholes[idx].at[there, pl.ds(lo, half)],
                    wholes[idx].at[there, pl.ds(lo, half)],
                    psend.at[slot, k, 2 + way],
                    precv.at[slot, k, 2 + way],
                    device,
                )
                copy.start()
                crossing[slot, k, 2 + way] = copy
                sends.append(copy)

        lag = 2
        for at in range(len(items) + lag):
            if at < len(items):
                first(*items[at])
            if at == len(items) - 1 and middle is not None:
                middle()
            if at >= lag:
                second(*items[at - lag])
        for slot, idx, k in items:
            crossing[slot, k, 2].wait_recv()
            crossing[slot, k, 3].wait_recv()
        for k in range(1, count_z):
            zin[len(order), k].wait_recv()
        for copy in sends:
            copy.wait_send()
        for copy in own:
            copy.wait()

    def let_go():
        pl.semaphore_signal(gate, inc=1, device_id=(1 - sec, grp, pos), device_id_type=MESH)

    def hold():
        pl.semaphore_wait(gate, 1)

    @pl.when(sec == 0)
    def _():
        run((4, 0, 1, 2, 3), 7, None, let_go)

    @pl.when(sec == 1)
    def _():
        run((0, 1, 2, 3, 5, 6), 7, hold, None)


def gather_all(shards, count_z):
    wholes = tuple(
        jax.ShapeDtypeStruct((s.shape[0] * count_z, s.shape[1]), s.dtype) for s in shards
    )
    return pl.pallas_call(
        functools.partial(gather_kernel, count_z),
        out_shape=wholes,
        in_specs=[pl.BlockSpec(memory_space=pl.ANY)] * len(shards),
        out_specs=[pl.BlockSpec(memory_space=pl.ANY)] * len(shards),
        scratch_shapes=[
            pltpu.SemaphoreType.DMA((8,)),
            pltpu.SemaphoreType.DMA((8, 4)),
            pltpu.SemaphoreType.DMA((8, 4)),
            pltpu.SemaphoreType.DMA((8, 4, 4)),
            pltpu.SemaphoreType.DMA((8, 4, 4)),
            pltpu.SemaphoreType.REGULAR,
        ],
        compiler_params=pltpu.CompilerParams(collective_id=0, has_side_effects=True),
    )(*shards)


def swap_kernel(count_z, rows_ref, out_ref, own_sem, send_sem, recv_sem):
    sec = lax.axis_index("section")
    grp = lax.axis_index("group")
    pos = lax.axis_index("dp")

    @pl.when(sec == 0)
    def _():
        barrier = pltpu.get_barrier_semaphore()
        for k in range(1, count_z):
            pl.semaphore_signal(
                barrier,
                inc=1,
                device_id=(sec, grp, lax.rem(pos + k, count_z)),
                device_id_type=MESH,
            )
        pl.semaphore_wait(barrier, count_z - 1)
        copies = []
        for k in range(1, count_z):
            to = lax.rem(pos + k, count_z)
            copy = pltpu.make_async_remote_copy(
                src_ref=rows_ref.at[to],
                dst_ref=out_ref.at[pos],
                send_sem=send_sem.at[k],
                recv_sem=recv_sem.at[k],
                device_id=(sec, grp, to),
                device_id_type=MESH,
            )
            copy.start()
            copies.append(copy)
        own = pltpu.make_async_copy(rows_ref.at[pos], out_ref.at[pos], own_sem)
        own.start()
        own.wait()
        for copy in copies:
            copy.wait()


def swap_rows(rows, count_z):
    return pl.pallas_call(
        functools.partial(swap_kernel, count_z),
        out_shape=jax.ShapeDtypeStruct(rows.shape, rows.dtype),
        in_specs=[pl.BlockSpec(memory_space=pl.ANY)],
        out_specs=pl.BlockSpec(memory_space=pl.ANY),
        scratch_shapes=[
            pltpu.SemaphoreType.DMA,
            pltpu.SemaphoreType.DMA((4,)),
            pltpu.SemaphoreType.DMA((4,)),
        ],
        compiler_params=pltpu.CompilerParams(collective_id=1, has_side_effects=True),
    )(rows)


def attend2(qkv_rows, key_valid):
    return jax.vmap(attend)(qkv_rows, key_valid)


def block_forward(hidden, key_valid, weights):
    gain_attn, qkv_weight, proj_weight, gain_mlp, up_weight, down_weight = weights
    seqs, length = key_valid.shape
    normed_in = normed(hidden, gain_attn).astype(jnp.bfloat16)
    qkv_rows = product(normed_in, qkv_weight).astype(jnp.bfloat16)
    mixed_rows, log_total = jax.vmap(attend)(qkv_rows.reshape(seqs, length, -1), key_valid)
    mixed_rows = mixed_rows.reshape(seqs * length, -1)
    hidden_mid = hidden + product(mixed_rows, proj_weight)
    mlp_in = normed(hidden_mid, gain_mlp).astype(jnp.bfloat16)
    pre_act = product(mlp_in, up_weight)
    activated = gelu_exact(pre_act).astype(jnp.bfloat16)
    hidden_out = hidden_mid + product(activated, down_weight)
    kept = (hidden, normed_in, qkv_rows, log_total, mixed_rows, hidden_mid, mlp_in, pre_act, activated)
    return hidden_out, kept


def block_backward(kept, grad_out, key_valid, weights):
    hidden, normed_in, qkv_rows, log_total, mixed_rows, hidden_mid, mlp_in, pre_act, activated = kept
    gain_attn, qkv_weight, proj_weight, gain_mlp, up_weight, down_weight = weights
    seqs, length = key_valid.shape
    grad_low = grad_out.astype(jnp.bfloat16)
    grad_activated = product_nt(grad_low, down_weight)
    grad_pre = jax.vjp(gelu_exact, pre_act)[1](grad_activated)[0].astype(jnp.bfloat16)
    grad_mlp_in = product_nt(grad_pre, up_weight)
    grad_mid_norm, grad_gain_mlp = norm_back(hidden_mid, gain_mlp, grad_mlp_in)
    grad_mid = grad_out + grad_mid_norm
    grad_mid_low = grad_mid.astype(jnp.bfloat16)
    grad_mixed = product_nt(grad_mid_low, proj_weight).astype(jnp.bfloat16)
    grad_qkv = jax.vmap(attend_back)(
        qkv_rows.reshape(seqs, length, -1),
        key_valid,
        log_total,
        grad_mixed.reshape(seqs, length, -1),
    ).reshape(seqs * length, -1)
    grad_normed = product_nt(grad_qkv, qkv_weight)
    grad_in_norm, grad_gain_attn = norm_back(hidden, gain_attn, grad_normed)
    grads = (
        product_tn(normed_in, grad_qkv).astype(jnp.bfloat16),
        product_tn(mixed_rows, grad_mid_low).astype(jnp.bfloat16),
        product_tn(mlp_in, grad_pre).astype(jnp.bfloat16),
        product_tn(activated, grad_low).astype(jnp.bfloat16),
    )
    return grad_mid + grad_in_norm, (grad_gain_attn, grad_gain_mlp), grads


def nothing_like(run):
    return jax.tree.map(lambda a: jnp.zeros(a.shape, a.dtype), jax.eval_shape(run))


def only_on(live, run):
    return lax.cond(live, run, lambda: nothing_like(run))


def per_device(
    tokens,
    lengths,
    levels,
    noise_rows,
    embed_table,
    w_in,
    ln_attn,
    w_qkv,
    w_proj,
    ln_mlp,
    w_up,
    w_down,
    ln_final,
    w_out,
):
    count_z = lax.axis_size("dp")
    sec = lax.axis_index("section")
    pos = lax.axis_index("dp")
    first_section = sec == 0
    last_section = sec == 1
    rows = tokens.shape[0]
    seqs = lengths.shape[0]
    length = rows // seqs
    width = w_out.shape[0] * count_z
    emb = w_out.shape[1]
    vocab_part = embed_table.shape[0]
    gains = jnp.concatenate(
        [ln_attn, ln_mlp, ln_final[None], jnp.zeros((13, ln_final.shape[0]), jnp.bfloat16)], 0
    )
    shards = (w_qkv[0], w_proj[0], w_up[0], w_down[0], w_in, w_out, embed_table, gains)
    line_tokens = lax.all_gather(tokens, "dp", axis=0, tiled=True)
    wholes = gather_all(shards, count_z)
    qkv_weight, proj_weight, up_weight, down_weight, in_weight, out_weight, table_full, gain_all = wholes
    gain_all = gain_all.reshape(count_z, 16, -1).astype(jnp.float32)
    gain_attn = gain_all[:, 0].reshape(-1)
    gain_mlp = gain_all[:, 1].reshape(-1)
    final_gain = gain_all[:, 2].reshape(-1)
    weights = (gain_attn, qkv_weight, proj_weight, gain_mlp, up_weight, down_weight)
    key_valid = jnp.arange(length, dtype=jnp.int32)[None, :] < lengths[:, None]
    loss_scale = LOSS_GAIN / math.sqrt(rows * lax.axis_size(("group", "dp")))

    def look_up():
        local = line_tokens - pos * vocab_part
        hit = local[:, None] == lax.broadcasted_iota(jnp.int32, (1, vocab_part), 1)
        return product(hit.astype(jnp.bfloat16), embed_table).astype(jnp.bfloat16)

    looked_parts = only_on(first_section, look_up).reshape(count_z, rows, emb)
    looked_parts = swap_rows(looked_parts, count_z)
    noise_level = jnp.exp(LOG_LOW + levels.astype(jnp.float32) * (LOG_SPAN / (LEVELS - 1)))
    scale_in = lax.rsqrt(EMB_VAR + noise_level * noise_level)
    row_level = jnp.repeat(noise_level, length)[:, None]
    row_scale = jnp.repeat(scale_in, length)[:, None]

    def front():
        looked = jnp.sum(looked_parts.astype(jnp.float32), 0)
        mixed_in = ((looked + row_level * noise_rows.astype(jnp.float32)) * row_scale).astype(
            jnp.bfloat16
        )
        out, kept = block_forward(product(mixed_in, in_weight), key_valid, weights)
        return out.astype(jnp.bfloat16), kept, mixed_in

    out_first, kept_first, mixed_in = only_on(first_section, front)
    x_second = passed_along(out_first, "section", 1)

    def back():
        hidden_out, kept = block_forward(x_second.astype(jnp.float32), key_valid, weights)
        grad_top, entropy, gain_step, tail_now = tail_pass(
            hidden_out,
            tokens,
            key_valid.reshape(-1),
            final_gain,
            out_weight,
            table_full,
            loss_scale,
        )
        grad_logits, projected, final_in, grad_proj = tail_now
        grad_start, gain_pair, grads = block_backward(kept, grad_top, key_valid, weights)
        return (
            grad_start.astype(jnp.bfloat16),
            entropy.astype(jnp.bfloat16),
            gain_pair,
            grads,
            product_tn(grad_logits, projected).astype(jnp.bfloat16),
            product_tn(final_in, grad_proj).astype(jnp.bfloat16),
            gain_step,
        )

    grad_second, loss_low, gain_pair_b, grads_b, table_b, out_b, gain_final = only_on(last_section, back)
    grad_first, loss_first = passed_along((grad_second, loss_low), "section", -1)
    token_loss = jnp.where(first_section, loss_first, loss_low)

    def front_back():
        grad_start, gain_pair, grads = block_backward(
            kept_first, grad_first.astype(jnp.float32), key_valid, weights
        )
        grad_low = grad_start.astype(jnp.bfloat16)
        looked_grad = product_nt(grad_low, in_weight) * row_scale
        table_grad = jnp.zeros(table_full.shape, jnp.float32).at[tokens].add(looked_grad)
        return (gain_pair, grads, table_grad.astype(jnp.bfloat16), product_tn(mixed_in, grad_low).astype(jnp.bfloat16))

    gain_pair, grads, table_g, in_g = lax.cond(
        first_section,
        front_back,
        lambda: (gain_pair_b, grads_b, table_b, jnp.zeros(in_weight.shape, jnp.bfloat16)),
    )

    def scatter(x):
        return lax.psum_scatter(x, "dp", scatter_dimension=0, tiled=True)

    layer = [lax.psum(scatter(x), "group").astype(jnp.float32) for x in grads]
    gain_out = [lax.psum(scatter(x.astype(jnp.bfloat16)), "group").astype(jnp.float32) for x in gain_pair]
    edge = [
        lax.psum(scatter(x), ("section", "group")).astype(jnp.float32)
        for x in (table_g, in_g, gain_final.astype(jnp.bfloat16), out_b)
    ]
    return (
        token_loss,
        edge[0],
        edge[1],
        gain_out[0][None],
        layer[0][None],
        layer[1][None],
        gain_out[1][None],
        layer[2][None],
        layer[3][None],
        edge[2],
        edge[3],
    )


def solution(mesh):
    placed = (
        P(("group", "dp")),
        P(("group", "dp")),
        P(("group", "dp")),
        P(("group", "dp"), None),
        P("dp", None),
        P("dp", None),
        P("section", "dp"),
        P("section", "dp", None),
        P("section", "dp", None),
        P("section", "dp"),
        P("section", "dp", None),
        P("section", "dp", None),
        P("dp"),
        P("dp", None),
    )
    fits = mesh.shape["dp"] == 4 and mesh.shape["group"] == 4 and mesh.shape["section"] == 2
    return jax.shard_map(
        per_device if fits else per_device_general,
        mesh=mesh,
        in_specs=placed,
        out_specs=(
            P(("group", "dp")),
            P("dp", None),
            P("dp", None),
            P("section", "dp"),
            P("section", "dp", None),
            P("section", "dp", None),
            P("section", "dp"),
            P("section", "dp", None),
            P("section", "dp", None),
            P("dp"),
            P("dp", None),
        ),
        check_vma=False,
    )
```

```python
import functools
import math

import jax
import jax.numpy as jnp
from jax import lax
from jax.experimental import pallas as pl
from jax.experimental.pallas import tpu as pltpu
from jax.sharding import PartitionSpec as P

HEAD = 64
LEVELS = 64
LEN = 128
MB = 2


EPS = 1e-05
LOG_LOW = -2.995732273553991
LOG_SPAN = 2.995732273553991
EMB_VAR = 0.015625
MASKED = -1e30
LOSS_GAIN = 16.0


def passed_along(x, axis, by):
    count = lax.axis_size(axis)
    pairs = [(i, i + by) for i in range(count) if 0 <= i + by < count]
    return lax.ppermute(x, axis, pairs)


def product(left_side, right_side):
    return jnp.dot(left_side, right_side, preferred_element_type=jnp.float32)


def product_tn(left_side, right_side):
    return lax.dot_general(
        left_side, right_side, (((0,), (0,)), ((), ())), preferred_element_type=jnp.float32
    )


def product_nt(left_side, right_side):
    return lax.dot_general(
        left_side, right_side, (((1,), (1,)), ((), ())), preferred_element_type=jnp.float32
    )


def normed(inputs, gain_vec):
    center = inputs - jnp.mean(inputs, -1, keepdims=True)
    return center * lax.rsqrt(jnp.mean(center * center, -1, keepdims=True) + EPS) * gain_vec


def norm_back(inputs, gain_vec, upstream):
    output, pullback = jax.vjp(normed, inputs, gain_vec)
    return pullback(upstream)


def gelu_exact(values_in):
    return jax.nn.gelu(values_in, approximate=False)


def attn_scores(split_rows, key_valid):
    scores = (
        jnp.einsum(
            "qhd,khd->hqk", split_rows[:, 0], split_rows[:, 1], preferred_element_type=jnp.float32
        )
        * 0.125
    )
    return jnp.where(key_valid[None, None, :], scores, MASKED)


def attend(qkv_rows, key_valid):
    length = qkv_rows.shape[0]
    model_width = qkv_rows.shape[1] // 3
    split_rows = qkv_rows.reshape(length, 3, model_width // HEAD, HEAD)
    scores = attn_scores(split_rows, key_valid)
    row_max = jnp.max(scores, -1, keepdims=True)
    log_total = row_max + jnp.log(jnp.sum(jnp.exp(scores - row_max), -1, keepdims=True))
    probs_low = jnp.exp(scores - log_total).astype(jnp.bfloat16)
    mixed_rows = jnp.einsum(
        "hqk,khd->qhd", probs_low, split_rows[:, 2], preferred_element_type=jnp.float32
    )
    return (mixed_rows.reshape(length, model_width).astype(jnp.bfloat16), log_total)


def attend_back(qkv_rows, key_valid, log_total, grad_mixed):
    length = qkv_rows.shape[0]
    model_width = qkv_rows.shape[1] // 3
    head_count = model_width // HEAD
    split_rows = qkv_rows.reshape(length, 3, head_count, HEAD)
    grad_heads = grad_mixed.reshape(length, head_count, HEAD)
    probs_full = jnp.exp(attn_scores(split_rows, key_valid) - log_total)
    grad_values = jnp.einsum(
        "hqk,qhd->khd",
        probs_full.astype(jnp.bfloat16),
        grad_heads,
        preferred_element_type=jnp.float32,
    )
    grad_probs = jnp.einsum(
        "qhd,khd->hqk", grad_heads, split_rows[:, 2], preferred_element_type=jnp.float32
    )
    grad_scores = (
        probs_full * (grad_probs - jnp.sum(grad_probs * probs_full, -1, keepdims=True))
    ).astype(jnp.bfloat16)
    grad_query = (
        jnp.einsum(
            "hqk,khd->qhd", grad_scores, split_rows[:, 1], preferred_element_type=jnp.float32
        )
        * 0.125
    )
    grad_key = (
        jnp.einsum(
            "hqk,qhd->khd", grad_scores, split_rows[:, 0], preferred_element_type=jnp.float32
        )
        * 0.125
    )
    stacked = jnp.stack([grad_query, grad_key, grad_values], 1).reshape(length, 3 * model_width)
    return stacked.astype(jnp.bfloat16)


def layer_forward(hidden, key_valid, weights):
    gain_attn, qkv_weight, proj_weight, gain_mlp, up_weight, down_weight = weights
    normed_in = normed(hidden, gain_attn).astype(jnp.bfloat16)
    qkv_rows = product(normed_in, qkv_weight).astype(jnp.bfloat16)
    mixed_rows, log_total = attend(qkv_rows, key_valid)
    hidden_mid = hidden + product(mixed_rows, proj_weight)
    mlp_in = normed(hidden_mid, gain_mlp).astype(jnp.bfloat16)
    pre_act = product(mlp_in, up_weight)
    activated = gelu_exact(pre_act).astype(jnp.bfloat16)
    hidden_out = hidden_mid + product(activated, down_weight)
    return (
        hidden_out,
        (
            hidden,
            normed_in,
            qkv_rows,
            log_total,
            mixed_rows,
            hidden_mid,
            mlp_in,
            pre_act,
            activated,
        ),
    )


def empty_kept(length, model_width, hidden_units, head_count):
    return (
        jnp.zeros((length, model_width), jnp.float32),
        jnp.zeros((length, model_width), jnp.bfloat16),
        jnp.zeros((length, 3 * model_width), jnp.bfloat16),
        jnp.zeros((head_count, length, 1), jnp.float32),
        jnp.zeros((length, model_width), jnp.bfloat16),
        jnp.zeros((length, model_width), jnp.float32),
        jnp.zeros((length, model_width), jnp.bfloat16),
        jnp.zeros((length, hidden_units), jnp.float32),
        jnp.zeros((length, hidden_units), jnp.bfloat16),
    )


def layer_backward(kept_vals, grad_out, key_valid, weights):
    hidden, normed_in, qkv_rows, log_total, mixed_rows, hidden_mid, mlp_in, pre_act, activated = (
        kept_vals
    )
    gain_attn, qkv_weight, proj_weight, gain_mlp, up_weight, down_weight = weights
    grad_low = grad_out.astype(jnp.bfloat16)
    grad_activated = product_nt(grad_low, down_weight)
    grad_pre = jax.vjp(gelu_exact, pre_act)[1](grad_activated)[0].astype(jnp.bfloat16)
    grad_mlp_in = product_nt(grad_pre, up_weight)
    grad_mid_norm, grad_gain_mlp = norm_back(hidden_mid, gain_mlp, grad_mlp_in)
    grad_mid = grad_out + grad_mid_norm
    grad_mid_low = grad_mid.astype(jnp.bfloat16)
    grad_mixed = product_nt(grad_mid_low, proj_weight).astype(jnp.bfloat16)
    grad_qkv = attend_back(qkv_rows, key_valid, log_total, grad_mixed)
    grad_normed = product_nt(grad_qkv, qkv_weight)
    grad_in_norm, grad_gain_attn = norm_back(hidden, gain_attn, grad_normed)
    records = (activated, grad_low, mlp_in, grad_pre, mixed_rows, grad_mid_low, normed_in, grad_qkv)
    return (grad_mid + grad_in_norm, (grad_gain_attn, grad_gain_mlp), records)


def layer_zero(length, model_width, hidden_units):
    records = (
        jnp.zeros((length, hidden_units), jnp.bfloat16),
        jnp.zeros((length, model_width), jnp.bfloat16),
        jnp.zeros((length, model_width), jnp.bfloat16),
        jnp.zeros((length, hidden_units), jnp.bfloat16),
        jnp.zeros((length, model_width), jnp.bfloat16),
        jnp.zeros((length, model_width), jnp.bfloat16),
        jnp.zeros((length, model_width), jnp.bfloat16),
        jnp.zeros((length, 3 * model_width), jnp.bfloat16),
    )
    gains = (jnp.zeros((model_width,), jnp.float32), jnp.zeros((model_width,), jnp.float32))
    return (jnp.zeros((length, model_width), jnp.float32), gains, records)


def layer_grads(records):
    activated, grad_low, mlp_in, grad_pre, mixed_rows, grad_mid_low, normed_in, grad_qkv = records
    return (
        product_tn(normed_in, grad_qkv),
        product_tn(mixed_rows, grad_mid_low),
        product_tn(mlp_in, grad_pre),
        product_tn(activated, grad_low),
    )


def embed_inputs(token_ids, noise_block, level_id, table_full):
    noise_level = jnp.exp(LOG_LOW + level_id.astype(jnp.float32) * (LOG_SPAN / (LEVELS - 1)))
    scale_in = lax.rsqrt(EMB_VAR + noise_level * noise_level)
    looked = jnp.take(table_full, token_ids, axis=0).astype(jnp.float32)
    mixed_in = ((looked + noise_level * noise_block.astype(jnp.float32)) * scale_in).astype(
        jnp.bfloat16
    )
    return (mixed_in, scale_in)


def embed_backward(token_ids, noise_block, level_id, grad_start, table_full, in_weight):
    mixed_in, scale_in = embed_inputs(token_ids, noise_block, level_id, table_full)
    grad_low = grad_start.astype(jnp.bfloat16)
    grad_looked = product_nt(grad_low, in_weight) * scale_in
    return (mixed_in, grad_low, grad_looked)


def embed_zero(length, model_width, emb_width):
    return (
        jnp.zeros((length, emb_width), jnp.bfloat16),
        jnp.zeros((length, model_width), jnp.bfloat16),
        jnp.zeros((length, emb_width), jnp.float32),
    )


def tail_pass(hidden, token_ids, key_valid, final_gain, out_weight, table_full, loss_scale):
    final_in = normed(hidden, final_gain).astype(jnp.bfloat16)
    projected = product(final_in, out_weight).astype(jnp.bfloat16)
    logits = product_nt(projected, table_full)
    row_max = jnp.max(logits, -1, keepdims=True)
    log_total = row_max + jnp.log(jnp.sum(jnp.exp(logits - row_max), -1, keepdims=True))
    vocab_ids = lax.broadcasted_iota(jnp.int32, logits.shape, 1)
    target_hit = vocab_ids == token_ids[:, None]
    picked = jnp.sum(jnp.where(target_hit, logits, 0.0), -1)
    entropy = jnp.where(key_valid, log_total[:, 0] - picked, 0.0)
    row_scale = jnp.where(key_valid, loss_scale, 0.0)[:, None]
    grad_logits = (
        (jnp.exp(logits - log_total) - target_hit.astype(jnp.float32)) * row_scale
    ).astype(jnp.bfloat16)
    grad_proj = product(grad_logits, table_full).astype(jnp.bfloat16)
    grad_final = product_nt(grad_proj, out_weight)
    grad_hidden, grad_gain = norm_back(hidden, final_gain, grad_final)
    return (grad_hidden, entropy, grad_gain, (grad_logits, projected, final_in, grad_proj))


def tail_zero(length, model_width, emb_width, vocab_rows):
    records = (
        jnp.zeros((length, vocab_rows), jnp.bfloat16),
        jnp.zeros((length, emb_width), jnp.bfloat16),
        jnp.zeros((length, model_width), jnp.bfloat16),
        jnp.zeros((length, emb_width), jnp.bfloat16),
    )
    return (
        jnp.zeros((length, model_width), jnp.float32),
        jnp.zeros((length,), jnp.float32),
        jnp.zeros((model_width,), jnp.float32),
        records,
    )


def edge_grads(tail_records, embed_records, token_ids):
    grad_logits, projected, final_in, grad_proj = tail_records
    mixed_in, grad_low, grad_looked = embed_records
    table_grad = product_tn(grad_logits, projected).at[token_ids].add(grad_looked)
    return (table_grad, product_tn(mixed_in, grad_low), product_tn(final_in, grad_proj))


def joined_rows(record_list):
    return jax.tree.map(lambda *pieces: jnp.concatenate(pieces, 0), *record_list)


def assemble(gain_attn_sum, gain_mlp_sum, layer_set, edge_set, gain_final_sum):
    return (
        gain_attn_sum[None],
        layer_set[0][None],
        layer_set[1][None],
        gain_mlp_sum[None],
        layer_set[2][None],
        layer_set[3][None],
        edge_set[0],
        edge_set[1],
        gain_final_sum,
        edge_set[2],
    )


def per_device_general(
    tokens,
    lengths,
    levels,
    noise_rows,
    embed_table,
    w_in,
    ln_attn,
    w_qkv,
    w_proj,
    ln_mlp,
    w_up,
    w_down,
    ln_final,
    w_out,
):
    gathered = (
        lax.all_gather(embed_table, "dp", axis=0, tiled=True),
        lax.all_gather(w_in, "dp", axis=0, tiled=True),
        lax.all_gather(ln_attn, "dp", axis=1, tiled=True),
        lax.all_gather(w_qkv, "dp", axis=1, tiled=True),
        lax.all_gather(w_proj, "dp", axis=1, tiled=True),
        lax.all_gather(ln_mlp, "dp", axis=1, tiled=True),
        lax.all_gather(w_up, "dp", axis=1, tiled=True),
        lax.all_gather(w_down, "dp", axis=1, tiled=True),
        lax.all_gather(ln_final, "dp", axis=0, tiled=True),
        lax.all_gather(w_out, "dp", axis=0, tiled=True),
    )
    table_full = gathered[0]
    in_weight = gathered[1]
    layer_weights = (
        gathered[2][0].astype(jnp.float32),
        gathered[3][0],
        gathered[4][0],
        gathered[5][0].astype(jnp.float32),
        gathered[6][0],
        gathered[7][0],
    )
    final_gain = gathered[8].astype(jnp.float32)
    out_weight = gathered[9]
    model_width = out_weight.shape[0]
    emb_width = out_weight.shape[1]
    vocab_rows = table_full.shape[0]
    hidden_units = layer_weights[4].shape[1]
    head_count = model_width // HEAD
    section_index = lax.axis_index("section")
    first_section = section_index == 0
    token_grid = tokens.reshape(MB, LEN)
    noise_grid = noise_rows.reshape(MB, LEN, noise_rows.shape[1])
    positions = jnp.arange(LEN, dtype=jnp.int32)
    valid_grid = positions[None, :] < lengths[:, None]
    loss_scale = LOSS_GAIN / math.sqrt(tokens.shape[0] * lax.axis_size(("group", "dp")))
    gain_attn_sum = jnp.zeros((model_width,), jnp.float32)
    gain_mlp_sum = jnp.zeros((model_width,), jnp.float32)
    gain_final_sum = jnp.zeros((model_width,), jnp.float32)
    recv_act = jnp.zeros((LEN, model_width), jnp.bfloat16)
    recv_grad = jnp.zeros((LEN, model_width), jnp.bfloat16)
    zero_rows = jnp.zeros((LEN, model_width), jnp.float32)
    kept_ticks = {}
    layer_recs = {}
    tail_recs = {}
    embed_recs = {}
    losses = []
    for moment in range(MB + 2):
        offset = moment - section_index
        fwd_valid = (offset >= 0) & (offset < MB)
        fwd_index = jnp.clip(offset, 0, MB - 1)
        ids_now = lax.dynamic_index_in_dim(token_grid, fwd_index, 0, False)
        noise_now = lax.dynamic_index_in_dim(noise_grid, fwd_index, 0, False)
        level_now = lax.dynamic_index_in_dim(levels, fwd_index, 0, False)
        valid_now = lax.dynamic_index_in_dim(valid_grid, fwd_index, 0, False)

        def first_input():
            mixed_in, scale_in = embed_inputs(ids_now, noise_now, level_now, table_full)
            return product(mixed_in, in_weight)

        layer_input = lax.cond(first_section, first_input, lambda: recv_act.astype(jnp.float32))
        hidden_out, kept_now = lax.cond(
            fwd_valid,
            lambda: layer_forward(layer_input, valid_now, layer_weights),
            lambda: (zero_rows, empty_kept(LEN, model_width, hidden_units, head_count)),
        )
        kept_ticks[moment] = kept_now
        tail_live = jnp.logical_not(first_section) & fwd_valid
        tail_grad, entropy, final_step, tail_now = lax.cond(
            tail_live,
            lambda: tail_pass(
                hidden_out, ids_now, valid_now, final_gain, out_weight, table_full, loss_scale
            ),
            lambda: tail_zero(LEN, model_width, emb_width, vocab_rows),
        )
        tail_recs[moment] = tail_now
        gain_final_sum = gain_final_sum + final_step
        back_tick = moment - 2
        late_live = 0 <= back_tick < MB
        late_index = min(max(back_tick, 0), MB - 1)
        kept_late = kept_ticks[back_tick] if back_tick >= 0 else kept_now
        kept_back = lax.cond(first_section, lambda: kept_late, lambda: kept_now)
        grad_top = jnp.where(first_section, recv_grad.astype(jnp.float32), tail_grad)
        valid_back = jnp.where(first_section, valid_grid[late_index], valid_now)
        back_live = jnp.where(first_section, late_live, fwd_valid)
        grad_start, gain_pair, layer_now = lax.cond(
            back_live,
            lambda: layer_backward(kept_back, grad_top, valid_back, layer_weights),
            lambda: layer_zero(LEN, model_width, hidden_units),
        )
        layer_recs[moment] = layer_now
        gain_attn_sum = gain_attn_sum + gain_pair[0]
        gain_mlp_sum = gain_mlp_sum + gain_pair[1]
        if late_live:
            embed_now = lax.cond(
                first_section,
                lambda: embed_backward(
                    token_grid[late_index],
                    noise_grid[late_index],
                    levels[late_index],
                    grad_start,
                    table_full,
                    in_weight,
                ),
                lambda: embed_zero(LEN, model_width, emb_width),
            )
        else:
            embed_now = embed_zero(LEN, model_width, emb_width)
        embed_recs[moment] = embed_now
        if moment < MB:
            recv_act = passed_along(hidden_out.astype(jnp.bfloat16), "section", 1)
        if 1 <= moment <= MB:
            entropy_low = entropy.astype(jnp.bfloat16)
            recv_grad, loss_back = passed_along(
                (grad_start.astype(jnp.bfloat16), entropy_low), "section", -1
            )
            losses.append(jnp.where(first_section, loss_back, entropy_low))
    chosen = [
        jax.tree.map(
            lambda early, late: jnp.where(first_section, early, late),
            layer_recs[micro + 2],
            layer_recs[micro + 1],
        )
        for micro in range(MB)
    ]
    all_layer = layer_grads(joined_rows(chosen))
    all_tail = joined_rows([tail_recs[micro + 1] for micro in range(MB)])
    all_embed = joined_rows([embed_recs[micro + 2] for micro in range(MB)])
    all_edge = edge_grads(all_tail, all_embed, tokens)
    grad_pack = assemble(gain_attn_sum, gain_mlp_sum, all_layer, all_edge, gain_final_sum)
    parted = (
        lax.psum_scatter(
            grad_pack[0].astype(jnp.bfloat16), "dp", scatter_dimension=1, tiled=True
        ).astype(jnp.float32),
        lax.psum_scatter(
            grad_pack[1].astype(jnp.bfloat16), "dp", scatter_dimension=1, tiled=True
        ).astype(jnp.float32),
        lax.psum_scatter(
            grad_pack[2].astype(jnp.bfloat16), "dp", scatter_dimension=1, tiled=True
        ).astype(jnp.float32),
        lax.psum_scatter(
            grad_pack[3].astype(jnp.bfloat16), "dp", scatter_dimension=1, tiled=True
        ).astype(jnp.float32),
        lax.psum_scatter(
            grad_pack[4].astype(jnp.bfloat16), "dp", scatter_dimension=1, tiled=True
        ).astype(jnp.float32),
        lax.psum_scatter(
            grad_pack[5].astype(jnp.bfloat16), "dp", scatter_dimension=1, tiled=True
        ).astype(jnp.float32),
        lax.psum_scatter(
            grad_pack[6].astype(jnp.bfloat16), "dp", scatter_dimension=0, tiled=True
        ).astype(jnp.float32),
        lax.psum_scatter(
            grad_pack[7].astype(jnp.bfloat16), "dp", scatter_dimension=0, tiled=True
        ).astype(jnp.float32),
        lax.psum_scatter(
            grad_pack[8].astype(jnp.bfloat16), "dp", scatter_dimension=0, tiled=True
        ).astype(jnp.float32),
        lax.psum_scatter(
            grad_pack[9].astype(jnp.bfloat16), "dp", scatter_dimension=0, tiled=True
        ).astype(jnp.float32),
    )
    layer_total = (
        lax.psum(parted[0].astype(jnp.bfloat16), "group").astype(jnp.float32),
        lax.psum(parted[1].astype(jnp.bfloat16), "group").astype(jnp.float32),
        lax.psum(parted[2].astype(jnp.bfloat16), "group").astype(jnp.float32),
        lax.psum(parted[3].astype(jnp.bfloat16), "group").astype(jnp.float32),
        lax.psum(parted[4].astype(jnp.bfloat16), "group").astype(jnp.float32),
        lax.psum(parted[5].astype(jnp.bfloat16), "group").astype(jnp.float32),
    )
    edge_total = (
        lax.psum(parted[6].astype(jnp.bfloat16), ("section", "group")).astype(jnp.float32),
        lax.psum(parted[7].astype(jnp.bfloat16), ("section", "group")).astype(jnp.float32),
        lax.psum(parted[8].astype(jnp.bfloat16), ("section", "group")).astype(jnp.float32),
        lax.psum(parted[9].astype(jnp.bfloat16), ("section", "group")).astype(jnp.float32),
    )
    token_loss = jnp.concatenate(losses)
    return (
        token_loss,
        edge_total[0],
        edge_total[1],
        layer_total[0],
        layer_total[1],
        layer_total[2],
        layer_total[3],
        layer_total[4],
        layer_total[5],
        edge_total[2],
        edge_total[3],
    )


MESH = pl.DeviceIdType.MESH
ANYWHERE = pl.BlockSpec(memory_space=pl.ANY)


def pick(index, values):
    out = values[-1]
    for at in range(len(values) - 2, -1, -1):
        out = jnp.where(index == at, values[at], out)
    return out


def rows_at(start, size):
    return pl.ds(pl.multiple_of(start, 8), size)


def remote(src, dst, send_sem, recv_sem, device):
    return pltpu.make_async_remote_copy(
        src_ref=src,
        dst_ref=dst,
        send_sem=send_sem,
        recv_sem=recv_sem,
        device_id=device,
        device_id_type=MESH,
    )


def gather_kernel(count, first_order, last_order, whole_line, *refs):
    shards = refs[:count]
    wholes = refs[count : 2 * count]
    own_sem, zsend, zrecv, psend, precv, gate = refs[2 * count : 2 * count + 6]
    stage = refs[2 * count + 6 :]
    sec = lax.axis_index("section")
    grp = lax.axis_index("group")
    pos = lax.axis_index("dp")
    beside = ((sec, grp ^ 1, pos), (sec, grp ^ 2, pos))
    above = (sec, grp, pos + 1)
    below = (sec, grp, pos - 1)
    partner = (1 - sec, grp, pos)
    barrier = pltpu.get_barrier_semaphore()

    def greet(device):
        pl.semaphore_signal(barrier, inc=1, device_id=device, device_id_type=MESH)

    for device in beside + (partner,):
        greet(device)

    @pl.when(pos > 0)
    def _():
        greet(below)

    @pl.when(pos < 3)
    def _():
        greet(above)

    at_end = (pos == 0) | (pos == 3)
    pl.semaphore_wait(barrier, jnp.where(at_end, 4, 5))

    turn = [pick(pos, v) for v in ((3, 1, 3, 1), (2, 3, 1, 2), (1, 2, 2, 3))]

    def run(order, before, middle):
        def part_of(idx):
            rows = shards[idx].shape[0]
            return rows if idx in whole_line else rows // 4

        def shift(idx, who):
            return 0 if idx in whole_line else who * part_of(idx)

        def block(idx, origin, who):
            return rows_at(origin * shards[idx].shape[0] + shift(idx, who), part_of(idx))

        def load_own(slot):
            return pltpu.make_async_copy(shards[order[slot]], stage[order[slot]], own_sem.at[slot])

        def store_own(slot):
            idx = order[slot]
            rows = shards[idx].shape[0]
            return pltpu.make_async_copy(
                stage[idx], wholes[idx].at[rows_at(pos * rows, rows)], own_sem.at[slot]
            )

        def own_ends(slot):
            idx = order[slot]
            src = shards[idx].at[rows_at(shift(idx, grp), part_of(idx))]
            dst = wholes[idx].at[block(idx, pos, grp)]
            return (
                (pos < 3, remote(src, dst, zsend.at[slot, 0], zrecv.at[slot, 1], above)),
                (pos > 0, remote(src, dst, zsend.at[slot, 1], zrecv.at[slot, 3], below)),
            )

        def start_own(slot):
            for goes, copy in own_ends(slot):
                pl.when(goes)(copy.start)

        def origin_of(j):
            return lax.rem(pos - turn[j] + 4, 4)

        def arrived(slot, j):
            here = wholes[order[slot]].at[block(order[slot], origin_of(j), grp)]
            return remote(here, here, zsend.at[slot, 2 + j], zrecv.at[slot, turn[j]], partner)

        def onward(slot, j):
            step = jnp.where(turn[j] <= pos, 1, -1)
            to = pos + step
            here = wholes[order[slot]].at[block(order[slot], origin_of(j), grp)]
            landed = jnp.clip(turn[j] + step, 0, 3)
            copy = remote(
                here,
                here,
                zsend.at[slot, 2 + j],
                zrecv.at[slot, landed],
                (sec, grp, jnp.clip(to, 0, 3)),
            )
            return (to >= 0) & (to <= 3), copy

        def plane(slot, j, way):
            idx = order[slot]
            origin = origin_of(j)
            if way < 2:
                here = wholes[idx].at[block(idx, origin, grp)]
                return remote(here, here, psend.at[slot, j, way], precv.at[slot, j, way], beside[way])
            half = shards[idx].shape[1] // 2
            there = wholes[idx].at[
                block(idx, origin, grp ^ (way - 1)), pl.ds(half * (way - 2), half)
            ]
            return remote(
                there, there, psend.at[slot, j, way], precv.at[slot, j, way], beside[3 - way]
            )

        items = [(slot, j) for slot in range(len(order)) for j in range(3)]
        crossing = [item for item in items if order[item[0]] not in whole_line]

        def first(slot, j):
            arrived(slot, j).wait_recv()
            goes, copy = onward(slot, j)
            pl.when(goes)(copy.start)
            if (slot, j) in crossing:
                plane(slot, j, 0).start()
                plane(slot, j, 1).start()

        def second(slot, j):
            if (slot, j) in crossing:
                for way in (0, 1):
                    plane(slot, j, way).wait_recv()
                    plane(slot, j, way + 2).start()

        if before is not None:
            before()
        for slot in range(len(order)):
            start_own(slot)
        for slot in range(len(order)):
            load_own(slot).start()
        lag = 2
        for at in range(len(items) + lag):
            if at < len(items):
                slot, j = items[at]
                if j == 2:
                    load_own(slot).wait()
                    store_own(slot).start()
                first(slot, j)
            if at == len(items) - 1 and middle is not None:
                middle()
            if at >= lag:
                second(*items[at - lag])
        for slot, j in crossing:
            plane(slot, j, 2).wait_recv()
            plane(slot, j, 3).wait_recv()
        for slot in range(len(order)):
            store_own(slot).wait()
            for goes, copy in own_ends(slot):
                pl.when(goes)(copy.wait_send)
        for slot, j in items:
            goes, copy = onward(slot, j)
            pl.when(goes)(copy.wait_send)
        for slot, j in crossing:
            for way in range(4):
                plane(slot, j, way).wait_send()

    def let_go():
        pl.semaphore_signal(gate, inc=1, device_id=partner, device_id_type=MESH)

    def hold():
        pl.semaphore_wait(gate, 1)

    @pl.when(sec == 0)
    def _():
        run(first_order, None, let_go)

    @pl.when(sec == 1)
    def _():
        run(last_order, hold, None)


def gather_all(shards, first_order, last_order, whole_line):
    count = len(shards)
    return pl.pallas_call(
        functools.partial(gather_kernel, count, first_order, last_order, whole_line),
        out_shape=[jax.ShapeDtypeStruct((s.shape[0] * 4, s.shape[1]), s.dtype) for s in shards],
        in_specs=[ANYWHERE] * count,
        out_specs=[ANYWHERE] * count,
        scratch_shapes=[
            pltpu.SemaphoreType.DMA((8,)),
            pltpu.SemaphoreType.DMA((8, 5)),
            pltpu.SemaphoreType.DMA((8, 4)),
            pltpu.SemaphoreType.DMA((8, 3, 4)),
            pltpu.SemaphoreType.DMA((8, 3, 4)),
            pltpu.SemaphoreType.REGULAR,
        ]
        + [pltpu.VMEM(s.shape, s.dtype) for s in shards],
        compiler_params=pltpu.CompilerParams(
            collective_id=0, has_side_effects=True, vmem_limit_bytes=24 << 20
        ),
    )(*shards)


def swap_kernel(count_z, rows_ref, out_ref, own_sem, send_sem, recv_sem):
    sec = lax.axis_index("section")
    grp = lax.axis_index("group")
    pos = lax.axis_index("dp")

    @pl.when(sec == 0)
    def _():
        barrier = pltpu.get_barrier_semaphore()
        for k in range(1, count_z):
            pl.semaphore_signal(
                barrier,
                inc=1,
                device_id=(sec, grp, lax.rem(pos + k, count_z)),
                device_id_type=MESH,
            )
        pl.semaphore_wait(barrier, count_z - 1)
        copies = []
        for k in range(1, count_z):
            to = lax.rem(pos + k, count_z)
            copy = pltpu.make_async_remote_copy(
                src_ref=rows_ref.at[to],
                dst_ref=out_ref.at[pos],
                send_sem=send_sem.at[k],
                recv_sem=recv_sem.at[k],
                device_id=(sec, grp, to),
                device_id_type=MESH,
            )
            copy.start()
            copies.append(copy)
        own = pltpu.make_async_copy(rows_ref.at[pos], out_ref.at[pos], own_sem)
        own.start()
        own.wait()
        for copy in copies:
            copy.wait()


def swap_rows(rows, count_z):
    return pl.pallas_call(
        functools.partial(swap_kernel, count_z),
        out_shape=jax.ShapeDtypeStruct(rows.shape, rows.dtype),
        in_specs=[pl.BlockSpec(memory_space=pl.ANY)],
        out_specs=pl.BlockSpec(memory_space=pl.ANY),
        scratch_shapes=[
            pltpu.SemaphoreType.DMA,
            pltpu.SemaphoreType.DMA((4,)),
            pltpu.SemaphoreType.DMA((4,)),
        ],
        compiler_params=pltpu.CompilerParams(collective_id=1, has_side_effects=True),
    )(rows)


def strip_of(rows, columns):
    strip = 16
    while 2 * strip * columns <= 65536 and rows % (2 * strip) == 0:
        strip = 2 * strip
    return strip


def add_rows(into, terms, rows, columns):
    strip = strip_of(rows, columns)

    def body(at, carry):
        here = rows_at(at * strip, strip)
        total = terms[0](here).astype(jnp.float32)
        for term in terms[1:]:
            total = total + term(here).astype(jnp.float32)
        into(here, total)
        return carry

    lax.fori_loop(0, rows // strip, body, 0)


def reduce_kernel(kinds, *refs):
    count = len(kinds)
    arrays = refs[:count]
    gains = refs[count]
    outs = refs[count + 1 : 2 * count + 1]
    gain_out = refs[2 * count + 1]
    rest = list(refs[2 * count + 2 :])
    s1, r1, own_sem, s2, r2, s3, r3, s4, r4, fin_sem, sg, rg = rest[:12]
    gain_own_sem, gain_in, gain_got = rest[12:15]
    bufs = rest[15:]
    own, got1, got2, got3, fin = ([bufs[5 * a + b] for a in range(count)] for b in range(5))
    sec = lax.axis_index("section")
    grp = lax.axis_index("group")
    pos = lax.axis_index("dp")
    beside = ((sec, grp ^ 1, pos), (sec, grp ^ 2, pos))
    barrier = pltpu.get_barrier_semaphore()
    steps = [(jg, jz) for jg in range(4) for jz in range(4)][1:]

    def other(j):
        return (sec, grp ^ steps[j - 1][0], lax.rem(pos + steps[j - 1][1], 4))

    for j in range(1, 16):
        pl.semaphore_signal(barrier, inc=1, device_id=other(j), device_id_type=MESH)
    pl.semaphore_wait(barrier, 15)

    live = [None if kind[1] is None else sec == kind[1] for kind in kinds]

    def when(a, run):
        if live[a] is None:
            run()
        else:
            pl.when(live[a])(run)

    def rows_of(a):
        return outs[a].shape[0]

    def part_of(a):
        return outs[a].shape[0] // 4

    def block(a, line, who):
        return arrays[a].at[rows_at(line * rows_of(a) + who * part_of(a), part_of(a))]

    def gain_copy(j):
        device = other(j)
        return remote(gain_in.at[device[2]], gain_got.at[j - 1], sg.at[j - 1], rg.at[j - 1], device)

    gain_load = pltpu.make_async_copy(gains, gain_in, gain_own_sem)

    def ways(line):
        first = 0 if line < 2 else 1
        return first, 1 - first

    def send_first(a, line, b):
        first, second = ways(line)
        who = grp ^ (1 + first)
        if b:
            who = who ^ (1 + second)
        return remote(
            block(a, line, who),
            got1[a].at[line, b],
            s1.at[a, line, b],
            r1.at[a, line, b],
            beside[first],
        )

    def load_own(a, line, b):
        first, second = ways(line)
        who = grp ^ (1 + second) if b else grp
        return pltpu.make_async_copy(block(a, line, who), own[a].at[line, b], own_sem.at[a, line, b])

    def send_second(a, line):
        first, second = ways(line)
        return remote(own[a].at[line, 1], got2[a].at[line], s2.at[a, line], r2.at[a, line], beside[second])

    def send_line(a, line):
        k = lax.rem(line - pos + 4, 4)
        slot = jnp.maximum(k - 1, 0)
        return remote(
            own[a].at[line, 0], got3[a].at[slot], s3.at[a, line], r3.at[a, slot], (sec, grp, line)
        )

    def line_arrival(a, slot):
        return remote(got3[a].at[slot], got3[a].at[slot], s3.at[a, slot], r3.at[a, slot], beside[0])

    def begin(a, line):
        def run():
            for b in (1, 0):
                send_first(a, line, b).start()
                load_own(a, line, b).start()

        when(a, run)

    def middle(a, line):
        def run():
            columns = outs[a].shape[1]
            for b in (1, 0):
                load_own(a, line, b).wait()
                send_first(a, line, b).wait_recv()

                def into(here, total, b=b):
                    own[a][line, b, here, :] = total.astype(jnp.bfloat16)

                add_rows(
                    into,
                    [lambda here, b=b: own[a][line, b, here, :], lambda here, b=b: got1[a][line, b, here, :]],
                    part_of(a),
                    columns,
                )
                if b:
                    send_second(a, line).start()

        when(a, run)

    def late(a, line):
        def run():
            send_second(a, line).wait_recv()

            def into(here, total):
                own[a][line, 0, here, :] = total.astype(jnp.bfloat16)

            add_rows(
                into,
                [lambda here: own[a][line, 0, here, :], lambda here: got2[a][line, here, :]],
                part_of(a),
                outs[a].shape[1],
            )
            pl.when(line != pos)(send_line(a, line).start)

        when(a, run)

    def own_out(a):
        here = outs[a].at[rows_at(grp * part_of(a), part_of(a))]
        return pltpu.make_async_copy(fin[a], here, fin_sem.at[a])

    def spread(a, way):
        part = part_of(a)
        if way < 2:
            here = outs[a].at[rows_at(grp * part, part)]
            return remote(fin[a], here, s4.at[a, way], r4.at[a, way], beside[way])
        half = outs[a].shape[1] // 2
        there = outs[a].at[rows_at((grp ^ (way - 1)) * part, part), pl.ds(half * (way - 2), half)]
        return remote(there, there, s4.at[a, way], r4.at[a, way], beside[3 - way])

    def spread_start(a):
        spread(a, 0).start()
        spread(a, 1).start()
        own_out(a).start()

    def finish(a):
        def run():
            for slot in range(3):
                line_arrival(a, slot).wait_recv()

            def into(here, total):
                fin[a][here, :] = total.astype(jnp.bfloat16)

            add_rows(
                into,
                [lambda here: own[a][pos, 0, here, :]]
                + [lambda here, slot=slot: got3[a][slot, here, :] for slot in range(3)],
                part_of(a),
                outs[a].shape[1],
            )
            spread_start(a)

        when(a, run)

    def pass_on(a):
        def run():
            for way in (0, 1):
                spread(a, way).wait_recv()
                spread(a, way + 2).start()

        when(a, run)

    def line_rows(a, line):
        return arrays[a].at[rows_at(line * rows_of(a), rows_of(a))]

    def line_first(a, k):
        to = lax.rem(pos + k, 4)
        return remote(
            line_rows(a, to), got1[a].at[k - 1], s1.at[a, k, 0], r1.at[a, k, 0], (sec, grp, to)
        )

    def line_own(a):
        return pltpu.make_async_copy(line_rows(a, pos), own[a], own_sem.at[a, 0, 0])

    def cross(a, j):
        part = part_of(a)
        to = grp ^ j
        return remote(
            own[a].at[rows_at(to * part, part)],
            got3[a].at[j - 1],
            s3.at[a, j],
            r3.at[a, j - 1],
            (sec, to, pos),
        )

    def line_begin(a):
        def run():
            for k in (2, 1, 3):
                line_first(a, k).start()
            line_own(a).start()

        when(a, run)

    def line_middle(a):
        def run():
            line_own(a).wait()
            for k in (1, 2, 3):
                line_first(a, k).wait_recv()

            def into(here, total):
                own[a][here, :] = total.astype(jnp.bfloat16)

            add_rows(
                into,
                [lambda here: own[a][here, :]]
                + [lambda here, k=k: got1[a][k, here, :] for k in range(3)],
                rows_of(a),
                outs[a].shape[1],
            )
            for j in (3, 1, 2):
                cross(a, j).start()

        when(a, run)

    def line_finish(a):
        def run():
            part = part_of(a)
            for j in (1, 2, 3):
                cross(a, j).wait_recv()

            def into(here, total):
                fin[a][here, :] = total.astype(jnp.bfloat16)

            strip = strip_of(part, outs[a].shape[1])

            def body(at, carry):
                here = rows_at(at * strip, strip)
                total = own[a][rows_at(grp * part + at * strip, strip), :].astype(jnp.float32)
                for j in range(3):
                    total = total + got3[a][j, here, :].astype(jnp.float32)
                fin[a][here, :] = total.astype(jnp.bfloat16)
                return carry

            lax.fori_loop(0, part // strip, body, 0)
            spread_start(a)

        when(a, run)

    plane_arrays = [a for a in range(count) if kinds[a][0] == "plane"]
    line_arrays = [a for a in range(count) if kinds[a][0] == "line"]
    units = [(a, line) for a in plane_arrays for line in (0, 2, 1, 3)]
    gain_load.start()
    ahead = 6
    for unit in units[:2]:
        begin(*unit)
    for a in line_arrays:
        line_begin(a)
    for unit in units[2:ahead]:
        begin(*unit)
    gain_load.wait()
    for j in range(1, 16):
        gain_copy(j).start()
    lag = 2
    finished = []
    for at in range(len(units) + lag + 4):
        if at + ahead < len(units):
            begin(*units[at + ahead])
        if at < len(units):
            middle(*units[at])
        if at == len(units) // 2:
            for a in line_arrays:
                line_middle(a)
        if at == len(units) // 2 + 2:
            for a in line_arrays:
                line_finish(a)
        if at == len(units) // 2 + 4:
            for a in line_arrays:
                pass_on(a)
        if lag <= at < len(units) + lag:
            late(*units[at - lag])
        spot = at - lag - 2
        if 0 <= spot < len(units) and units[spot][1] == 3:
            if finished:
                pass_on(finished[-1])
            finish(units[spot][0])
            finished.append(units[spot][0])
    pass_on(finished[-1])
    for j in range(1, 16):
        gain_copy(j).wait_recv()
    total = gain_in[pos]
    for j in range(15):
        total = total + gain_got[j]
    gain_out[...] = total
    for a in range(count):

        def run(a=a):
            spread(a, 2).wait_recv()
            spread(a, 3).wait_recv()
            own_out(a).wait()
            for way in range(4):
                spread(a, way).wait_send()
            if kinds[a][0] == "plane":
                for line in range(4):
                    for b in (0, 1):
                        send_first(a, line, b).wait_send()
                    send_second(a, line).wait_send()
                    pl.when(line != pos)(send_line(a, line).wait_send)
            else:
                for k in (1, 2, 3):
                    line_first(a, k).wait_send()
                    cross(a, k).wait_send()

        when(a, run)
    for j in range(1, 16):
        gain_copy(j).wait_send()


def reduce_all(arrays, gains, kinds, collective_id):
    count = len(arrays)
    outs = [jax.ShapeDtypeStruct((x.shape[0] // 4, x.shape[1]), x.dtype) for x in arrays]
    buffers = []
    for x, kind in zip(arrays, kinds):
        rows, columns = x.shape[0] // 4, x.shape[1]
        part = rows // 4
        if kind[0] == "plane":
            shapes = [(4, 2, part, columns), (4, 2, part, columns), (4, part, columns)]
        else:
            shapes = [(rows, columns), (3, rows, columns), (8, 128)]
        shapes += [(3, part, columns), (part, columns)]
        buffers += [pltpu.VMEM(shape, x.dtype) for shape in shapes]
    dma = pltpu.SemaphoreType.DMA
    return pl.pallas_call(
        functools.partial(reduce_kernel, kinds),
        out_shape=outs + [jax.ShapeDtypeStruct(gains.shape[1:], gains.dtype)],
        in_specs=[ANYWHERE] * (count + 1),
        out_specs=[ANYWHERE] * count + [pl.BlockSpec(memory_space=pltpu.VMEM)],
        scratch_shapes=[
            dma((count, 4, 2)),
            dma((count, 4, 2)),
            dma((count, 4, 2)),
            dma((count, 4)),
            dma((count, 4)),
            dma((count, 4)),
            dma((count, 4)),
            dma((count, 4)),
            dma((count, 4)),
            dma((count,)),
            dma((15,)),
            dma((15,)),
            dma,
            pltpu.VMEM(gains.shape, gains.dtype),
            pltpu.VMEM((15,) + gains.shape[1:], gains.dtype),
        ]
        + buffers,
        compiler_params=pltpu.CompilerParams(
            collective_id=collective_id, has_side_effects=True, vmem_limit_bytes=58 << 20
        ),
    )(*arrays, gains)


def block_forward(hidden, key_valid, weights):
    gain_attn, qkv_weight, proj_weight, gain_mlp, up_weight, down_weight = weights
    seqs, length = key_valid.shape
    normed_in = normed(hidden, gain_attn).astype(jnp.bfloat16)
    qkv_rows = product(normed_in, qkv_weight).astype(jnp.bfloat16)
    mixed_rows, log_total = jax.vmap(attend)(qkv_rows.reshape(seqs, length, -1), key_valid)
    mixed_rows = mixed_rows.reshape(seqs * length, -1)
    hidden_mid = hidden + product(mixed_rows, proj_weight)
    mlp_in = normed(hidden_mid, gain_mlp).astype(jnp.bfloat16)
    pre_act = product(mlp_in, up_weight)
    activated = gelu_exact(pre_act).astype(jnp.bfloat16)
    hidden_out = hidden_mid + product(activated, down_weight)
    kept = (hidden, normed_in, qkv_rows, log_total, mixed_rows, hidden_mid, mlp_in, pre_act, activated)
    return hidden_out, kept


def block_backward(kept, grad_out, key_valid, weights):
    hidden, normed_in, qkv_rows, log_total, mixed_rows, hidden_mid, mlp_in, pre_act, activated = kept
    gain_attn, qkv_weight, proj_weight, gain_mlp, up_weight, down_weight = weights
    seqs, length = key_valid.shape
    grad_low = grad_out.astype(jnp.bfloat16)
    grad_activated = product_nt(grad_low, down_weight)
    grad_pre = jax.vjp(gelu_exact, pre_act)[1](grad_activated)[0].astype(jnp.bfloat16)
    grad_mlp_in = product_nt(grad_pre, up_weight)
    grad_mid_norm, grad_gain_mlp = norm_back(hidden_mid, gain_mlp, grad_mlp_in)
    grad_mid = grad_out + grad_mid_norm
    grad_mid_low = grad_mid.astype(jnp.bfloat16)
    grad_mixed = product_nt(grad_mid_low, proj_weight).astype(jnp.bfloat16)
    grad_qkv = jax.vmap(attend_back)(
        qkv_rows.reshape(seqs, length, -1),
        key_valid,
        log_total,
        grad_mixed.reshape(seqs, length, -1),
    ).reshape(seqs * length, -1)
    grad_normed = product_nt(grad_qkv, qkv_weight)
    grad_in_norm, grad_gain_attn = norm_back(hidden, gain_attn, grad_normed)
    grads = (
        product_tn(normed_in, grad_qkv).astype(jnp.bfloat16),
        product_tn(mixed_rows, grad_mid_low).astype(jnp.bfloat16),
        product_tn(mlp_in, grad_pre).astype(jnp.bfloat16),
        product_tn(activated, grad_low).astype(jnp.bfloat16),
    )
    return grad_mid + grad_in_norm, (grad_gain_attn, grad_gain_mlp), grads


def nothing_like(run):
    return jax.tree.map(lambda a: jnp.zeros(a.shape, a.dtype), jax.eval_shape(run))


def only_on(live, run):
    return lax.cond(live, run, lambda: nothing_like(run))


def per_device(
    tokens,
    lengths,
    levels,
    noise_rows,
    embed_table,
    w_in,
    ln_attn,
    w_qkv,
    w_proj,
    ln_mlp,
    w_up,
    w_down,
    ln_final,
    w_out,
):
    count_z = lax.axis_size("dp")
    sec = lax.axis_index("section")
    pos = lax.axis_index("dp")
    first_section = sec == 0
    last_section = sec == 1
    rows = tokens.shape[0]
    seqs = lengths.shape[0]
    length = rows // seqs
    width = w_out.shape[0] * count_z
    emb = w_out.shape[1]
    vocab_part = embed_table.shape[0]
    gains = jnp.concatenate(
        [ln_attn, ln_mlp, ln_final[None], jnp.zeros((13, ln_final.shape[0]), jnp.bfloat16)], 0
    )
    shards = (w_qkv[0], w_proj[0], w_up[0], w_down[0], w_in, w_out, embed_table, gains)
    wholes = gather_all(shards, (7, 4, 0, 1, 2, 3), (7, 0, 1, 2, 3, 5, 6), (7, 1))
    all_tokens = lax.all_gather(tokens, ("group", "dp"), axis=0, tiled=True)
    line_tokens = lax.dynamic_slice_in_dim(
        all_tokens, lax.axis_index("group") * count_z * rows, count_z * rows, 0
    )
    qkv_weight, proj_weight, up_weight, down_weight, in_weight, out_weight, table_full, gain_all = wholes
    gain_all = gain_all.reshape(count_z, 16, -1).astype(jnp.float32)
    gain_attn = gain_all[:, 0].reshape(-1)
    gain_mlp = gain_all[:, 1].reshape(-1)
    final_gain = gain_all[:, 2].reshape(-1)
    weights = (gain_attn, qkv_weight, proj_weight, gain_mlp, up_weight, down_weight)
    key_valid = jnp.arange(length, dtype=jnp.int32)[None, :] < lengths[:, None]
    loss_scale = LOSS_GAIN / math.sqrt(rows * lax.axis_size(("group", "dp")))

    def look_up():
        local = line_tokens - pos * vocab_part
        hit = local[:, None] == lax.broadcasted_iota(jnp.int32, (1, vocab_part), 1)
        return product(hit.astype(jnp.bfloat16), embed_table).astype(jnp.bfloat16)

    looked_parts = only_on(first_section, look_up).reshape(count_z, rows, emb)
    looked_parts = swap_rows(looked_parts, count_z)
    noise_level = jnp.exp(LOG_LOW + levels.astype(jnp.float32) * (LOG_SPAN / (LEVELS - 1)))
    scale_in = lax.rsqrt(EMB_VAR + noise_level * noise_level)
    row_level = jnp.repeat(noise_level, length)[:, None]
    row_scale = jnp.repeat(scale_in, length)[:, None]

    def front():
        looked = jnp.sum(looked_parts.astype(jnp.float32), 0)
        mixed_in = ((looked + row_level * noise_rows.astype(jnp.float32)) * row_scale).astype(
            jnp.bfloat16
        )
        out, kept = block_forward(product(mixed_in, in_weight), key_valid, weights)
        return out.astype(jnp.bfloat16), kept, mixed_in

    out_first, kept_first, mixed_in = only_on(first_section, front)
    x_second = passed_along(out_first, "section", 1)

    def back():
        hidden_out, kept = block_forward(x_second.astype(jnp.float32), key_valid, weights)
        grad_top, entropy, gain_step, tail_now = tail_pass(
            hidden_out,
            tokens,
            key_valid.reshape(-1),
            final_gain,
            out_weight,
            table_full,
            loss_scale,
        )
        grad_logits, projected, final_in, grad_proj = tail_now
        grad_start, gain_pair, grads = block_backward(kept, grad_top, key_valid, weights)
        return (
            grad_start.astype(jnp.bfloat16),
            entropy.astype(jnp.bfloat16),
            gain_pair,
            grads,
            product_tn(grad_logits, projected).astype(jnp.bfloat16),
            product_tn(final_in, grad_proj).astype(jnp.bfloat16),
            gain_step,
        )

    grad_second, loss_low, gain_pair_b, grads_b, table_b, out_b, gain_final = only_on(last_section, back)
    grad_first, loss_first = passed_along((grad_second, loss_low), "section", -1)
    token_loss = jnp.where(first_section, loss_first, loss_low)

    def front_back():
        grad_start, gain_pair, grads = block_backward(
            kept_first, grad_first.astype(jnp.float32), key_valid, weights
        )
        grad_low = grad_start.astype(jnp.bfloat16)
        looked_grad = (product_nt(grad_low, in_weight) * row_scale).astype(jnp.bfloat16)
        return gain_pair, grads, product_tn(mixed_in, grad_low).astype(jnp.bfloat16), looked_grad

    def end_back():
        shape = in_weight.shape
        packed = out_b.reshape(count_z, shape[0] // count_z, shape[1]).reshape(shape)
        return gain_pair_b, grads_b, packed, jnp.zeros((rows, emb), jnp.bfloat16)

    gain_pair, grads, edge_g, looked_grad = lax.cond(first_section, front_back, end_back)
    gain_rows = jnp.stack([gain_pair[0], gain_pair[1], gain_final], 0)
    gain_rows = jnp.concatenate([gain_rows, jnp.zeros((5, width), jnp.float32)], 0)
    gain_rows = gain_rows.reshape(8, count_z, width // count_z).transpose(1, 0, 2)
    order = (table_b, grads[2], grads[3], edge_g, grads[1], grads[0])
    kinds = (("plane", 1),) + (("plane", None),) * 4 + (("line", None),)
    table_r, up_r, down_r, edge_r, proj_r, qkv_r, gain_r = reduce_all(order, gain_rows, kinds, 2)
    looked_all = lax.all_gather(looked_grad, ("group", "dp"), axis=0, tiled=True)

    def add_looked():
        local = all_tokens - pos * vocab_part
        hit = lax.broadcasted_iota(jnp.int32, (vocab_part, 1), 0) == local[None, :]
        return product(hit.astype(jnp.bfloat16), looked_all).astype(jnp.bfloat16)

    looked_sum = only_on(first_section, add_looked)
    mine = (jnp.where(first_section, looked_sum, table_r), edge_r, gain_r)
    theirs = lax.ppermute(mine, "section", [(0, 1), (1, 0)])
    table_out = mine[0].astype(jnp.float32) + theirs[0].astype(jnp.float32)
    in_r = jnp.where(first_section, edge_r, theirs[1]).astype(jnp.float32)
    out_r = jnp.where(first_section, theirs[1], edge_r).astype(jnp.float32).reshape(-1, emb)
    final_r = jnp.where(first_section, theirs[2][2], gain_r[2])
    return (
        token_loss,
        table_out,
        in_r,
        gain_r[0][None],
        qkv_r.astype(jnp.float32)[None],
        proj_r.astype(jnp.float32)[None],
        gain_r[1][None],
        up_r.astype(jnp.float32)[None],
        down_r.astype(jnp.float32)[None],
        final_r,
        out_r,
    )


def solution(mesh):
    placed = (
        P(("group", "dp")),
        P(("group", "dp")),
        P(("group", "dp")),
        P(("group", "dp"), None),
        P("dp", None),
        P("dp", None),
        P("section", "dp"),
        P("section", "dp", None),
        P("section", "dp", None),
        P("section", "dp"),
        P("section", "dp", None),
        P("section", "dp", None),
        P("dp"),
        P("dp", None),
    )
    fits = (mesh.shape["section"], mesh.shape["group"], mesh.shape["dp"]) == (2, 4, 4)
    return jax.shard_map(
        per_device if fits else per_device_general,
        mesh=mesh,
        in_specs=placed,
        out_specs=(
            P(("group", "dp")),
            P("dp", None),
            P("dp", None),
            P("section", "dp"),
            P("section", "dp", None),
            P("section", "dp", None),
            P("section", "dp"),
            P("section", "dp", None),
            P("section", "dp", None),
            P("dp"),
            P("dp", None),
        ),
        check_vma=False,
    )
```

```python
import functools
import math

import jax
import jax.numpy as jnp
from jax import lax
from jax.experimental import pallas as pl
from jax.experimental.pallas import tpu as pltpu
from jax.sharding import PartitionSpec as P

HEAD = 64
LEVELS = 64
LEN = 128
MB = 2


EPS = 1e-05
LOG_LOW = -2.995732273553991
LOG_SPAN = 2.995732273553991
EMB_VAR = 0.015625
MASKED = -1e30
LOSS_GAIN = 16.0


def passed_along(x, axis, by):
    count = lax.axis_size(axis)
    pairs = [(i, i + by) for i in range(count) if 0 <= i + by < count]
    return lax.ppermute(x, axis, pairs)


def product(left_side, right_side):
    return jnp.dot(left_side, right_side, preferred_element_type=jnp.float32)


def product_tn(left_side, right_side):
    return lax.dot_general(
        left_side, right_side, (((0,), (0,)), ((), ())), preferred_element_type=jnp.float32
    )


def product_nt(left_side, right_side):
    return lax.dot_general(
        left_side, right_side, (((1,), (1,)), ((), ())), preferred_element_type=jnp.float32
    )


def normed(inputs, gain_vec):
    center = inputs - jnp.mean(inputs, -1, keepdims=True)
    return center * lax.rsqrt(jnp.mean(center * center, -1, keepdims=True) + EPS) * gain_vec


def norm_back(inputs, gain_vec, upstream):
    output, pullback = jax.vjp(normed, inputs, gain_vec)
    return pullback(upstream)


def gelu_exact(values_in):
    return jax.nn.gelu(values_in, approximate=False)


def attn_scores(split_rows, key_valid):
    scores = (
        jnp.einsum(
            "qhd,khd->hqk", split_rows[:, 0], split_rows[:, 1], preferred_element_type=jnp.float32
        )
        * 0.125
    )
    return jnp.where(key_valid[None, None, :], scores, MASKED)


def attend(qkv_rows, key_valid):
    length = qkv_rows.shape[0]
    model_width = qkv_rows.shape[1] // 3
    split_rows = qkv_rows.reshape(length, 3, model_width // HEAD, HEAD)
    scores = attn_scores(split_rows, key_valid)
    row_max = jnp.max(scores, -1, keepdims=True)
    log_total = row_max + jnp.log(jnp.sum(jnp.exp(scores - row_max), -1, keepdims=True))
    probs_low = jnp.exp(scores - log_total).astype(jnp.bfloat16)
    mixed_rows = jnp.einsum(
        "hqk,khd->qhd", probs_low, split_rows[:, 2], preferred_element_type=jnp.float32
    )
    return (mixed_rows.reshape(length, model_width).astype(jnp.bfloat16), log_total)


def attend_back(qkv_rows, key_valid, log_total, grad_mixed):
    length = qkv_rows.shape[0]
    model_width = qkv_rows.shape[1] // 3
    head_count = model_width // HEAD
    split_rows = qkv_rows.reshape(length, 3, head_count, HEAD)
    grad_heads = grad_mixed.reshape(length, head_count, HEAD)
    probs_full = jnp.exp(attn_scores(split_rows, key_valid) - log_total)
    grad_values = jnp.einsum(
        "hqk,qhd->khd",
        probs_full.astype(jnp.bfloat16),
        grad_heads,
        preferred_element_type=jnp.float32,
    )
    grad_probs = jnp.einsum(
        "qhd,khd->hqk", grad_heads, split_rows[:, 2], preferred_element_type=jnp.float32
    )
    grad_scores = (
        probs_full * (grad_probs - jnp.sum(grad_probs * probs_full, -1, keepdims=True))
    ).astype(jnp.bfloat16)
    grad_query = (
        jnp.einsum(
            "hqk,khd->qhd", grad_scores, split_rows[:, 1], preferred_element_type=jnp.float32
        )
        * 0.125
    )
    grad_key = (
        jnp.einsum(
            "hqk,qhd->khd", grad_scores, split_rows[:, 0], preferred_element_type=jnp.float32
        )
        * 0.125
    )
    stacked = jnp.stack([grad_query, grad_key, grad_values], 1).reshape(length, 3 * model_width)
    return stacked.astype(jnp.bfloat16)


def layer_forward(hidden, key_valid, weights):
    gain_attn, qkv_weight, proj_weight, gain_mlp, up_weight, down_weight = weights
    normed_in = normed(hidden, gain_attn).astype(jnp.bfloat16)
    qkv_rows = product(normed_in, qkv_weight).astype(jnp.bfloat16)
    mixed_rows, log_total = attend(qkv_rows, key_valid)
    hidden_mid = hidden + product(mixed_rows, proj_weight)
    mlp_in = normed(hidden_mid, gain_mlp).astype(jnp.bfloat16)
    pre_act = product(mlp_in, up_weight)
    activated = gelu_exact(pre_act).astype(jnp.bfloat16)
    hidden_out = hidden_mid + product(activated, down_weight)
    return (
        hidden_out,
        (
            hidden,
            normed_in,
            qkv_rows,
            log_total,
            mixed_rows,
            hidden_mid,
            mlp_in,
            pre_act,
            activated,
        ),
    )


def empty_kept(length, model_width, hidden_units, head_count):
    return (
        jnp.zeros((length, model_width), jnp.float32),
        jnp.zeros((length, model_width), jnp.bfloat16),
        jnp.zeros((length, 3 * model_width), jnp.bfloat16),
        jnp.zeros((head_count, length, 1), jnp.float32),
        jnp.zeros((length, model_width), jnp.bfloat16),
        jnp.zeros((length, model_width), jnp.float32),
        jnp.zeros((length, model_width), jnp.bfloat16),
        jnp.zeros((length, hidden_units), jnp.float32),
        jnp.zeros((length, hidden_units), jnp.bfloat16),
    )


def layer_backward(kept_vals, grad_out, key_valid, weights):
    hidden, normed_in, qkv_rows, log_total, mixed_rows, hidden_mid, mlp_in, pre_act, activated = (
        kept_vals
    )
    gain_attn, qkv_weight, proj_weight, gain_mlp, up_weight, down_weight = weights
    grad_low = grad_out.astype(jnp.bfloat16)
    grad_activated = product_nt(grad_low, down_weight)
    grad_pre = jax.vjp(gelu_exact, pre_act)[1](grad_activated)[0].astype(jnp.bfloat16)
    grad_mlp_in = product_nt(grad_pre, up_weight)
    grad_mid_norm, grad_gain_mlp = norm_back(hidden_mid, gain_mlp, grad_mlp_in)
    grad_mid = grad_out + grad_mid_norm
    grad_mid_low = grad_mid.astype(jnp.bfloat16)
    grad_mixed = product_nt(grad_mid_low, proj_weight).astype(jnp.bfloat16)
    grad_qkv = attend_back(qkv_rows, key_valid, log_total, grad_mixed)
    grad_normed = product_nt(grad_qkv, qkv_weight)
    grad_in_norm, grad_gain_attn = norm_back(hidden, gain_attn, grad_normed)
    records = (activated, grad_low, mlp_in, grad_pre, mixed_rows, grad_mid_low, normed_in, grad_qkv)
    return (grad_mid + grad_in_norm, (grad_gain_attn, grad_gain_mlp), records)


def layer_zero(length, model_width, hidden_units):
    records = (
        jnp.zeros((length, hidden_units), jnp.bfloat16),
        jnp.zeros((length, model_width), jnp.bfloat16),
        jnp.zeros((length, model_width), jnp.bfloat16),
        jnp.zeros((length, hidden_units), jnp.bfloat16),
        jnp.zeros((length, model_width), jnp.bfloat16),
        jnp.zeros((length, model_width), jnp.bfloat16),
        jnp.zeros((length, model_width), jnp.bfloat16),
        jnp.zeros((length, 3 * model_width), jnp.bfloat16),
    )
    gains = (jnp.zeros((model_width,), jnp.float32), jnp.zeros((model_width,), jnp.float32))
    return (jnp.zeros((length, model_width), jnp.float32), gains, records)


def layer_grads(records):
    activated, grad_low, mlp_in, grad_pre, mixed_rows, grad_mid_low, normed_in, grad_qkv = records
    return (
        product_tn(normed_in, grad_qkv),
        product_tn(mixed_rows, grad_mid_low),
        product_tn(mlp_in, grad_pre),
        product_tn(activated, grad_low),
    )


def embed_inputs(token_ids, noise_block, level_id, table_full):
    noise_level = jnp.exp(LOG_LOW + level_id.astype(jnp.float32) * (LOG_SPAN / (LEVELS - 1)))
    scale_in = lax.rsqrt(EMB_VAR + noise_level * noise_level)
    looked = jnp.take(table_full, token_ids, axis=0).astype(jnp.float32)
    mixed_in = ((looked + noise_level * noise_block.astype(jnp.float32)) * scale_in).astype(
        jnp.bfloat16
    )
    return (mixed_in, scale_in)


def embed_backward(token_ids, noise_block, level_id, grad_start, table_full, in_weight):
    mixed_in, scale_in = embed_inputs(token_ids, noise_block, level_id, table_full)
    grad_low = grad_start.astype(jnp.bfloat16)
    grad_looked = product_nt(grad_low, in_weight) * scale_in
    return (mixed_in, grad_low, grad_looked)


def embed_zero(length, model_width, emb_width):
    return (
        jnp.zeros((length, emb_width), jnp.bfloat16),
        jnp.zeros((length, model_width), jnp.bfloat16),
        jnp.zeros((length, emb_width), jnp.float32),
    )


def tail_pass(hidden, token_ids, key_valid, final_gain, out_weight, table_full, loss_scale):
    final_in = normed(hidden, final_gain).astype(jnp.bfloat16)
    projected = product(final_in, out_weight).astype(jnp.bfloat16)
    logits = product_nt(projected, table_full)
    row_max = jnp.max(logits, -1, keepdims=True)
    log_total = row_max + jnp.log(jnp.sum(jnp.exp(logits - row_max), -1, keepdims=True))
    vocab_ids = lax.broadcasted_iota(jnp.int32, logits.shape, 1)
    target_hit = vocab_ids == token_ids[:, None]
    picked = jnp.sum(jnp.where(target_hit, logits, 0.0), -1)
    entropy = jnp.where(key_valid, log_total[:, 0] - picked, 0.0)
    row_scale = jnp.where(key_valid, loss_scale, 0.0)[:, None]
    grad_logits = (
        (jnp.exp(logits - log_total) - target_hit.astype(jnp.float32)) * row_scale
    ).astype(jnp.bfloat16)
    grad_proj = product(grad_logits, table_full).astype(jnp.bfloat16)
    grad_final = product_nt(grad_proj, out_weight)
    grad_hidden, grad_gain = norm_back(hidden, final_gain, grad_final)
    return (grad_hidden, entropy, grad_gain, (grad_logits, projected, final_in, grad_proj))


def tail_zero(length, model_width, emb_width, vocab_rows):
    records = (
        jnp.zeros((length, vocab_rows), jnp.bfloat16),
        jnp.zeros((length, emb_width), jnp.bfloat16),
        jnp.zeros((length, model_width), jnp.bfloat16),
        jnp.zeros((length, emb_width), jnp.bfloat16),
    )
    return (
        jnp.zeros((length, model_width), jnp.float32),
        jnp.zeros((length,), jnp.float32),
        jnp.zeros((model_width,), jnp.float32),
        records,
    )


def edge_grads(tail_records, embed_records, token_ids):
    grad_logits, projected, final_in, grad_proj = tail_records
    mixed_in, grad_low, grad_looked = embed_records
    table_grad = product_tn(grad_logits, projected).at[token_ids].add(grad_looked)
    return (table_grad, product_tn(mixed_in, grad_low), product_tn(final_in, grad_proj))


def joined_rows(record_list):
    return jax.tree.map(lambda *pieces: jnp.concatenate(pieces, 0), *record_list)


def assemble(gain_attn_sum, gain_mlp_sum, layer_set, edge_set, gain_final_sum):
    return (
        gain_attn_sum[None],
        layer_set[0][None],
        layer_set[1][None],
        gain_mlp_sum[None],
        layer_set[2][None],
        layer_set[3][None],
        edge_set[0],
        edge_set[1],
        gain_final_sum,
        edge_set[2],
    )


def per_device_general(
    tokens,
    lengths,
    levels,
    noise_rows,
    embed_table,
    w_in,
    ln_attn,
    w_qkv,
    w_proj,
    ln_mlp,
    w_up,
    w_down,
    ln_final,
    w_out,
):
    gathered = (
        lax.all_gather(embed_table, "dp", axis=0, tiled=True),
        lax.all_gather(w_in, "dp", axis=0, tiled=True),
        lax.all_gather(ln_attn, "dp", axis=1, tiled=True),
        lax.all_gather(w_qkv, "dp", axis=1, tiled=True),
        lax.all_gather(w_proj, "dp", axis=1, tiled=True),
        lax.all_gather(ln_mlp, "dp", axis=1, tiled=True),
        lax.all_gather(w_up, "dp", axis=1, tiled=True),
        lax.all_gather(w_down, "dp", axis=1, tiled=True),
        lax.all_gather(ln_final, "dp", axis=0, tiled=True),
        lax.all_gather(w_out, "dp", axis=0, tiled=True),
    )
    table_full = gathered[0]
    in_weight = gathered[1]
    layer_weights = (
        gathered[2][0].astype(jnp.float32),
        gathered[3][0],
        gathered[4][0],
        gathered[5][0].astype(jnp.float32),
        gathered[6][0],
        gathered[7][0],
    )
    final_gain = gathered[8].astype(jnp.float32)
    out_weight = gathered[9]
    model_width = out_weight.shape[0]
    emb_width = out_weight.shape[1]
    vocab_rows = table_full.shape[0]
    hidden_units = layer_weights[4].shape[1]
    head_count = model_width // HEAD
    section_index = lax.axis_index("section")
    first_section = section_index == 0
    token_grid = tokens.reshape(MB, LEN)
    noise_grid = noise_rows.reshape(MB, LEN, noise_rows.shape[1])
    positions = jnp.arange(LEN, dtype=jnp.int32)
    valid_grid = positions[None, :] < lengths[:, None]
    loss_scale = LOSS_GAIN / math.sqrt(tokens.shape[0] * lax.axis_size(("group", "dp")))
    gain_attn_sum = jnp.zeros((model_width,), jnp.float32)
    gain_mlp_sum = jnp.zeros((model_width,), jnp.float32)
    gain_final_sum = jnp.zeros((model_width,), jnp.float32)
    recv_act = jnp.zeros((LEN, model_width), jnp.bfloat16)
    recv_grad = jnp.zeros((LEN, model_width), jnp.bfloat16)
    zero_rows = jnp.zeros((LEN, model_width), jnp.float32)
    kept_ticks = {}
    layer_recs = {}
    tail_recs = {}
    embed_recs = {}
    losses = []
    for moment in range(MB + 2):
        offset = moment - section_index
        fwd_valid = (offset >= 0) & (offset < MB)
        fwd_index = jnp.clip(offset, 0, MB - 1)
        ids_now = lax.dynamic_index_in_dim(token_grid, fwd_index, 0, False)
        noise_now = lax.dynamic_index_in_dim(noise_grid, fwd_index, 0, False)
        level_now = lax.dynamic_index_in_dim(levels, fwd_index, 0, False)
        valid_now = lax.dynamic_index_in_dim(valid_grid, fwd_index, 0, False)

        def first_input():
            mixed_in, scale_in = embed_inputs(ids_now, noise_now, level_now, table_full)
            return product(mixed_in, in_weight)

        layer_input = lax.cond(first_section, first_input, lambda: recv_act.astype(jnp.float32))
        hidden_out, kept_now = lax.cond(
            fwd_valid,
            lambda: layer_forward(layer_input, valid_now, layer_weights),
            lambda: (zero_rows, empty_kept(LEN, model_width, hidden_units, head_count)),
        )
        kept_ticks[moment] = kept_now
        tail_live = jnp.logical_not(first_section) & fwd_valid
        tail_grad, entropy, final_step, tail_now = lax.cond(
            tail_live,
            lambda: tail_pass(
                hidden_out, ids_now, valid_now, final_gain, out_weight, table_full, loss_scale
            ),
            lambda: tail_zero(LEN, model_width, emb_width, vocab_rows),
        )
        tail_recs[moment] = tail_now
        gain_final_sum = gain_final_sum + final_step
        back_tick = moment - 2
        late_live = 0 <= back_tick < MB
        late_index = min(max(back_tick, 0), MB - 1)
        kept_late = kept_ticks[back_tick] if back_tick >= 0 else kept_now
        kept_back = lax.cond(first_section, lambda: kept_late, lambda: kept_now)
        grad_top = jnp.where(first_section, recv_grad.astype(jnp.float32), tail_grad)
        valid_back = jnp.where(first_section, valid_grid[late_index], valid_now)
        back_live = jnp.where(first_section, late_live, fwd_valid)
        grad_start, gain_pair, layer_now = lax.cond(
            back_live,
            lambda: layer_backward(kept_back, grad_top, valid_back, layer_weights),
            lambda: layer_zero(LEN, model_width, hidden_units),
        )
        layer_recs[moment] = layer_now
        gain_attn_sum = gain_attn_sum + gain_pair[0]
        gain_mlp_sum = gain_mlp_sum + gain_pair[1]
        if late_live:
            embed_now = lax.cond(
                first_section,
                lambda: embed_backward(
                    token_grid[late_index],
                    noise_grid[late_index],
                    levels[late_index],
                    grad_start,
                    table_full,
                    in_weight,
                ),
                lambda: embed_zero(LEN, model_width, emb_width),
            )
        else:
            embed_now = embed_zero(LEN, model_width, emb_width)
        embed_recs[moment] = embed_now
        if moment < MB:
            recv_act = passed_along(hidden_out.astype(jnp.bfloat16), "section", 1)
        if 1 <= moment <= MB:
            entropy_low = entropy.astype(jnp.bfloat16)
            recv_grad, loss_back = passed_along(
                (grad_start.astype(jnp.bfloat16), entropy_low), "section", -1
            )
            losses.append(jnp.where(first_section, loss_back, entropy_low))
    chosen = [
        jax.tree.map(
            lambda early, late: jnp.where(first_section, early, late),
            layer_recs[micro + 2],
            layer_recs[micro + 1],
        )
        for micro in range(MB)
    ]
    all_layer = layer_grads(joined_rows(chosen))
    all_tail = joined_rows([tail_recs[micro + 1] for micro in range(MB)])
    all_embed = joined_rows([embed_recs[micro + 2] for micro in range(MB)])
    all_edge = edge_grads(all_tail, all_embed, tokens)
    grad_pack = assemble(gain_attn_sum, gain_mlp_sum, all_layer, all_edge, gain_final_sum)
    parted = (
        lax.psum_scatter(
            grad_pack[0].astype(jnp.bfloat16), "dp", scatter_dimension=1, tiled=True
        ).astype(jnp.float32),
        lax.psum_scatter(
            grad_pack[1].astype(jnp.bfloat16), "dp", scatter_dimension=1, tiled=True
        ).astype(jnp.float32),
        lax.psum_scatter(
            grad_pack[2].astype(jnp.bfloat16), "dp", scatter_dimension=1, tiled=True
        ).astype(jnp.float32),
        lax.psum_scatter(
            grad_pack[3].astype(jnp.bfloat16), "dp", scatter_dimension=1, tiled=True
        ).astype(jnp.float32),
        lax.psum_scatter(
            grad_pack[4].astype(jnp.bfloat16), "dp", scatter_dimension=1, tiled=True
        ).astype(jnp.float32),
        lax.psum_scatter(
            grad_pack[5].astype(jnp.bfloat16), "dp", scatter_dimension=1, tiled=True
        ).astype(jnp.float32),
        lax.psum_scatter(
            grad_pack[6].astype(jnp.bfloat16), "dp", scatter_dimension=0, tiled=True
        ).astype(jnp.float32),
        lax.psum_scatter(
            grad_pack[7].astype(jnp.bfloat16), "dp", scatter_dimension=0, tiled=True
        ).astype(jnp.float32),
        lax.psum_scatter(
            grad_pack[8].astype(jnp.bfloat16), "dp", scatter_dimension=0, tiled=True
        ).astype(jnp.float32),
        lax.psum_scatter(
            grad_pack[9].astype(jnp.bfloat16), "dp", scatter_dimension=0, tiled=True
        ).astype(jnp.float32),
    )
    layer_total = (
        lax.psum(parted[0].astype(jnp.bfloat16), "group").astype(jnp.float32),
        lax.psum(parted[1].astype(jnp.bfloat16), "group").astype(jnp.float32),
        lax.psum(parted[2].astype(jnp.bfloat16), "group").astype(jnp.float32),
        lax.psum(parted[3].astype(jnp.bfloat16), "group").astype(jnp.float32),
        lax.psum(parted[4].astype(jnp.bfloat16), "group").astype(jnp.float32),
        lax.psum(parted[5].astype(jnp.bfloat16), "group").astype(jnp.float32),
    )
    edge_total = (
        lax.psum(parted[6].astype(jnp.bfloat16), ("section", "group")).astype(jnp.float32),
        lax.psum(parted[7].astype(jnp.bfloat16), ("section", "group")).astype(jnp.float32),
        lax.psum(parted[8].astype(jnp.bfloat16), ("section", "group")).astype(jnp.float32),
        lax.psum(parted[9].astype(jnp.bfloat16), ("section", "group")).astype(jnp.float32),
    )
    token_loss = jnp.concatenate(losses)
    return (
        token_loss,
        edge_total[0],
        edge_total[1],
        layer_total[0],
        layer_total[1],
        layer_total[2],
        layer_total[3],
        layer_total[4],
        layer_total[5],
        edge_total[2],
        edge_total[3],
    )


MESH = pl.DeviceIdType.MESH
ANYWHERE = pl.BlockSpec(memory_space=pl.ANY)


def pick(index, values):
    out = values[-1]
    for at in range(len(values) - 2, -1, -1):
        out = jnp.where(index == at, values[at], out)
    return out


def rows_at(start, size):
    return pl.ds(pl.multiple_of(start, 8), size)


def remote(src, dst, send_sem, recv_sem, device):
    return pltpu.make_async_remote_copy(
        src_ref=src,
        dst_ref=dst,
        send_sem=send_sem,
        recv_sem=recv_sem,
        device_id=device,
        device_id_type=MESH,
    )


def gather_kernel(count, first_order, last_order, whole_line, *refs):
    shards = refs[:count]
    wholes = refs[count : 2 * count]
    own_sem, zsend, zrecv, psend, precv, gate = refs[2 * count : 2 * count + 6]
    stage = refs[2 * count + 6 :]
    sec = lax.axis_index("section")
    grp = lax.axis_index("group")
    pos = lax.axis_index("dp")
    beside = ((sec, grp ^ 1, pos), (sec, grp ^ 2, pos))
    above = (sec, grp, pos + 1)
    below = (sec, grp, pos - 1)
    partner = (1 - sec, grp, pos)
    barrier = pltpu.get_barrier_semaphore()
    both = bool(last_order)

    def greet(device):
        pl.semaphore_signal(barrier, inc=1, device_id=device, device_id_type=MESH)

    def meet():
        for device in beside + ((partner,) if both else ()):
            greet(device)

        @pl.when(pos > 0)
        def _():
            greet(below)

        @pl.when(pos < 3)
        def _():
            greet(above)

        at_end = (pos == 0) | (pos == 3)
        pl.semaphore_wait(barrier, jnp.where(at_end, 3, 4) + (1 if both else 0))

    turn = [pick(pos, v) for v in ((3, 1, 3, 1), (2, 3, 1, 2), (1, 2, 2, 3))]

    def run(order, before, middle):
        def part_of(idx):
            rows = shards[idx].shape[0]
            return rows if idx in whole_line else rows // 4

        def shift(idx, who):
            return 0 if idx in whole_line else who * part_of(idx)

        def block(idx, origin, who):
            return rows_at(origin * shards[idx].shape[0] + shift(idx, who), part_of(idx))

        def load_own(slot):
            return pltpu.make_async_copy(shards[order[slot]], stage[order[slot]], own_sem.at[slot])

        def store_own(slot):
            idx = order[slot]
            rows = shards[idx].shape[0]
            return pltpu.make_async_copy(
                stage[idx], wholes[idx].at[rows_at(pos * rows, rows)], own_sem.at[slot]
            )

        def own_ends(slot):
            idx = order[slot]
            src = shards[idx].at[rows_at(shift(idx, grp), part_of(idx))]
            dst = wholes[idx].at[block(idx, pos, grp)]
            return (
                (pos < 3, remote(src, dst, zsend.at[slot, 0], zrecv.at[slot, 1], above)),
                (pos > 0, remote(src, dst, zsend.at[slot, 1], zrecv.at[slot, 3], below)),
            )

        def start_own(slot):
            for goes, copy in own_ends(slot):
                pl.when(goes)(copy.start)

        def origin_of(j):
            return lax.rem(pos - turn[j] + 4, 4)

        def arrived(slot, j):
            here = wholes[order[slot]].at[block(order[slot], origin_of(j), grp)]
            return remote(here, here, zsend.at[slot, 2 + j], zrecv.at[slot, turn[j]], partner)

        def onward(slot, j):
            step = jnp.where(turn[j] <= pos, 1, -1)
            to = pos + step
            here = wholes[order[slot]].at[block(order[slot], origin_of(j), grp)]
            landed = jnp.clip(turn[j] + step, 0, 3)
            copy = remote(
                here,
                here,
                zsend.at[slot, 2 + j],
                zrecv.at[slot, landed],
                (sec, grp, jnp.clip(to, 0, 3)),
            )
            return (to >= 0) & (to <= 3), copy

        def plane(slot, j, way):
            idx = order[slot]
            origin = origin_of(j)
            if way < 2:
                here = wholes[idx].at[block(idx, origin, grp)]
                return remote(here, here, psend.at[slot, j, way], precv.at[slot, j, way], beside[way])
            half = shards[idx].shape[1] // 2
            there = wholes[idx].at[
                block(idx, origin, grp ^ (way - 1)), pl.ds(half * (way - 2), half)
            ]
            return remote(
                there, there, psend.at[slot, j, way], precv.at[slot, j, way], beside[3 - way]
            )

        items = [(slot, j) for slot in range(len(order)) for j in range(3)]
        crossing = [item for item in items if order[item[0]] not in whole_line]

        def first(slot, j):
            arrived(slot, j).wait_recv()
            goes, copy = onward(slot, j)
            pl.when(goes)(copy.start)
            if (slot, j) in crossing:
                plane(slot, j, 0).start()
                plane(slot, j, 1).start()

        def second(slot, j):
            if (slot, j) in crossing:
                for way in (0, 1):
                    plane(slot, j, way).wait_recv()
                    plane(slot, j, way + 2).start()

        if before is not None:
            before()
        for slot in range(len(order)):
            start_own(slot)
        for slot in range(len(order)):
            load_own(slot).start()
        lag = 2
        for at in range(len(items) + lag):
            if at < len(items):
                slot, j = items[at]
                if j == 2:
                    load_own(slot).wait()
                    store_own(slot).start()
                first(slot, j)
            if at == len(items) - 1 and middle is not None:
                middle()
            if at >= lag:
                second(*items[at - lag])
        for slot, j in crossing:
            plane(slot, j, 2).wait_recv()
            plane(slot, j, 3).wait_recv()
        for slot in range(len(order)):
            store_own(slot).wait()
            for goes, copy in own_ends(slot):
                pl.when(goes)(copy.wait_send)
        for slot, j in items:
            goes, copy = onward(slot, j)
            pl.when(goes)(copy.wait_send)
        for slot, j in crossing:
            for way in range(4):
                plane(slot, j, way).wait_send()

    def let_go():
        pl.semaphore_signal(gate, inc=1, device_id=partner, device_id_type=MESH)

    def hold():
        pl.semaphore_wait(gate, 1)

    if both:
        meet()

        @pl.when(sec == 0)
        def _():
            run(first_order, None, let_go)

        @pl.when(sec == 1)
        def _():
            run(last_order, hold, None)

    else:

        @pl.when(sec == 0)
        def _():
            meet()
            run(first_order, None, None)


def gather_all(shards, first_order, last_order, whole_line, collective_id):
    count = len(shards)
    return pl.pallas_call(
        functools.partial(gather_kernel, count, first_order, last_order, whole_line),
        out_shape=[jax.ShapeDtypeStruct((s.shape[0] * 4, s.shape[1]), s.dtype) for s in shards],
        in_specs=[ANYWHERE] * count,
        out_specs=[ANYWHERE] * count,
        scratch_shapes=[
            pltpu.SemaphoreType.DMA((count,)),
            pltpu.SemaphoreType.DMA((count, 5)),
            pltpu.SemaphoreType.DMA((count, 4)),
            pltpu.SemaphoreType.DMA((count, 3, 4)),
            pltpu.SemaphoreType.DMA((count, 3, 4)),
            pltpu.SemaphoreType.REGULAR,
        ]
        + [pltpu.VMEM(s.shape, s.dtype) for s in shards],
        compiler_params=pltpu.CompilerParams(
            collective_id=collective_id, has_side_effects=True, vmem_limit_bytes=24 << 20
        ),
    )(*shards)


def swap_kernel(rows_ref, ids_ref, out_ref, ids_out, own_sem, send_sem, recv_sem):
    sec = lax.axis_index("section")
    grp = lax.axis_index("group")
    pos = lax.axis_index("dp")

    @pl.when(sec == 0)
    def _():
        barrier = pltpu.get_barrier_semaphore()
        peers = [(sec, grp, lax.rem(pos + k, 4)) for k in (1, 2, 3)]
        sides = [(sec, grp ^ j, pos) for j in (1, 2, 3)]
        for device in peers + sides:
            pl.semaphore_signal(barrier, inc=1, device_id=device, device_id_type=MESH)
        pl.semaphore_wait(barrier, 6)
        copies = []
        for k, device in enumerate(peers):
            copies.append(
                remote(rows_ref.at[device[2]], out_ref.at[pos], send_sem.at[k], recv_sem.at[k], device)
            )
        for k, device in enumerate(sides):
            copies.append(
                remote(ids_ref, ids_out.at[grp], send_sem.at[3 + k], recv_sem.at[3 + k], device)
            )
        for copy in copies:
            copy.start()
        own_rows = pltpu.make_async_copy(rows_ref.at[pos], out_ref.at[pos], own_sem.at[0])
        own_ids = pltpu.make_async_copy(ids_ref, ids_out.at[grp], own_sem.at[1])
        own_rows.start()
        own_ids.start()
        own_rows.wait()
        own_ids.wait()
        for copy in copies:
            copy.wait()


def swap_rows(rows, ids, collective_id):
    in_vmem = pl.BlockSpec(memory_space=pltpu.VMEM)
    return pl.pallas_call(
        swap_kernel,
        out_shape=[
            jax.ShapeDtypeStruct(rows.shape, rows.dtype),
            jax.ShapeDtypeStruct((4,) + ids.shape, ids.dtype),
        ],
        in_specs=[in_vmem] * 2,
        out_specs=[in_vmem] * 2,
        scratch_shapes=[
            pltpu.SemaphoreType.DMA((2,)),
            pltpu.SemaphoreType.DMA((6,)),
            pltpu.SemaphoreType.DMA((6,)),
        ],
        compiler_params=pltpu.CompilerParams(collective_id=collective_id, has_side_effects=True),
    )(rows, ids)


def strip_of(rows, columns):
    strip = 16
    while 2 * strip * columns <= 65536 and rows % (2 * strip) == 0:
        strip = 2 * strip
    return strip


def add_rows(into, terms, rows, columns):
    strip = strip_of(rows, columns)

    def body(at, carry):
        here = rows_at(at * strip, strip)
        total = terms[0](here).astype(jnp.float32)
        for term in terms[1:]:
            total = total + term(here).astype(jnp.float32)
        into(here, total)
        return carry

    lax.fori_loop(0, rows // strip, body, 0)


def reduce_kernel(kinds, with_gains, only, *refs):
    if only is None:
        reduce_body(kinds, with_gains, *refs)
    else:
        pl.when(lax.axis_index("section") == only)(
            functools.partial(reduce_body, kinds, with_gains, *refs)
        )


def reduce_body(kinds, with_gains, *refs):
    count = len(kinds)
    more = 1 if with_gains else 0
    arrays = refs[:count]
    outs = refs[count + more : 2 * count + more]
    rest = list(refs[2 * count + 2 * more :])
    s1, r1, own_sem, s2, r2, s3, r3, s4, r4, fin_sem = rest[:10]
    bufs = rest[10 : 10 + 5 * count]
    if with_gains:
        gains = refs[count]
        gain_out = refs[2 * count + 1]
        gain_own_sem, sg, rg, gain_in, gain_got = rest[10 + 5 * count :]
    own, got1, got2, got3, fin = ([bufs[5 * a + b] for a in range(count)] for b in range(5))
    sec = lax.axis_index("section")
    grp = lax.axis_index("group")
    pos = lax.axis_index("dp")
    beside = ((sec, grp ^ 1, pos), (sec, grp ^ 2, pos))
    barrier = pltpu.get_barrier_semaphore()
    steps = [(jg, jz) for jg in range(4) for jz in range(4)][1:]

    def other(j):
        return (sec, grp ^ steps[j - 1][0], lax.rem(pos + steps[j - 1][1], 4))

    if with_gains:
        peers = [other(j) for j in range(1, 16)]
    else:
        peers = [(sec, grp ^ j, pos) for j in (1, 2, 3)] + [other(j) for j in (1, 2, 3)]
    for device in peers:
        pl.semaphore_signal(barrier, inc=1, device_id=device, device_id_type=MESH)
    pl.semaphore_wait(barrier, len(peers))

    def when(a, run):
        run()

    def rows_of(a):
        return outs[a].shape[0]

    def part_of(a):
        return outs[a].shape[0] // 4

    def block(a, line, who):
        return arrays[a].at[rows_at(line * rows_of(a) + who * part_of(a), part_of(a))]

    def gain_copy(j):
        device = other(j)
        return remote(gain_in.at[device[2]], gain_got.at[j - 1], sg.at[j - 1], rg.at[j - 1], device)

    def gain_load():
        return pltpu.make_async_copy(gains, gain_in, gain_own_sem)

    def ways(line):
        first = 0 if line < 2 else 1
        return first, 1 - first

    def send_first(a, line, b):
        first, second = ways(line)
        who = grp ^ (1 + first)
        if b:
            who = who ^ (1 + second)
        return remote(
            block(a, line, who),
            got1[a].at[line, b],
            s1.at[a, line, b],
            r1.at[a, line, b],
            beside[first],
        )

    def load_own(a, line, b):
        first, second = ways(line)
        who = grp ^ (1 + second) if b else grp
        return pltpu.make_async_copy(block(a, line, who), own[a].at[line, b], own_sem.at[a, line, b])

    def send_second(a, line):
        first, second = ways(line)
        return remote(own[a].at[line, 1], got2[a].at[line], s2.at[a, line], r2.at[a, line], beside[second])

    def send_line(a, line):
        k = lax.rem(line - pos + 4, 4)
        slot = jnp.maximum(k - 1, 0)
        return remote(
            own[a].at[line, 0], got3[a].at[slot], s3.at[a, line], r3.at[a, slot], (sec, grp, line)
        )

    def line_arrival(a, slot):
        return remote(got3[a].at[slot], got3[a].at[slot], s3.at[a, slot], r3.at[a, slot], beside[0])

    def begin(a, line):
        def run():
            for b in (1, 0):
                send_first(a, line, b).start()
                load_own(a, line, b).start()

        when(a, run)

    def middle(a, line):
        def run():
            columns = outs[a].shape[1]
            for b in (1, 0):
                load_own(a, line, b).wait()
                send_first(a, line, b).wait_recv()

                def into(here, total, b=b):
                    own[a][line, b, here, :] = total.astype(jnp.bfloat16)

                add_rows(
                    into,
                    [lambda here, b=b: own[a][line, b, here, :], lambda here, b=b: got1[a][line, b, here, :]],
                    part_of(a),
                    columns,
                )
                if b:
                    send_second(a, line).start()

        when(a, run)

    def late(a, line):
        def run():
            send_second(a, line).wait_recv()

            def into(here, total):
                own[a][line, 0, here, :] = total.astype(jnp.bfloat16)

            add_rows(
                into,
                [lambda here: own[a][line, 0, here, :], lambda here: got2[a][line, here, :]],
                part_of(a),
                outs[a].shape[1],
            )
            pl.when(line != pos)(send_line(a, line).start)

        when(a, run)

    def own_out(a):
        here = outs[a].at[rows_at(grp * part_of(a), part_of(a))]
        return pltpu.make_async_copy(fin[a], here, fin_sem.at[a])

    def spread(a, way):
        part = part_of(a)
        if way < 2:
            here = outs[a].at[rows_at(grp * part, part)]
            return remote(fin[a], here, s4.at[a, way], r4.at[a, way], beside[way])
        half = outs[a].shape[1] // 2
        there = outs[a].at[rows_at((grp ^ (way - 1)) * part, part), pl.ds(half * (way - 2), half)]
        return remote(there, there, s4.at[a, way], r4.at[a, way], beside[3 - way])

    def spread_start(a):
        spread(a, 0).start()
        spread(a, 1).start()
        own_out(a).start()

    def finish(a):
        def run():
            for slot in range(3):
                line_arrival(a, slot).wait_recv()

            def into(here, total):
                fin[a][here, :] = total.astype(jnp.bfloat16)

            add_rows(
                into,
                [lambda here: own[a][pos, 0, here, :]]
                + [lambda here, slot=slot: got3[a][slot, here, :] for slot in range(3)],
                part_of(a),
                outs[a].shape[1],
            )
            spread_start(a)

        when(a, run)

    def pass_on(a):
        def run():
            for way in (0, 1):
                spread(a, way).wait_recv()
                spread(a, way + 2).start()

        when(a, run)

    def line_rows(a, line):
        return arrays[a].at[rows_at(line * rows_of(a), rows_of(a))]

    def line_first(a, k):
        to = lax.rem(pos + k, 4)
        return remote(
            line_rows(a, to), got1[a].at[k - 1], s1.at[a, k, 0], r1.at[a, k, 0], (sec, grp, to)
        )

    def line_own(a):
        return pltpu.make_async_copy(line_rows(a, pos), own[a], own_sem.at[a, 0, 0])

    def cross(a, j):
        part = part_of(a)
        to = grp ^ j
        return remote(
            own[a].at[rows_at(to * part, part)],
            got3[a].at[j - 1],
            s3.at[a, j],
            r3.at[a, j - 1],
            (sec, to, pos),
        )

    def line_begin(a):
        def run():
            for k in (2, 1, 3):
                line_first(a, k).start()
            line_own(a).start()

        when(a, run)

    def line_middle(a):
        def run():
            line_own(a).wait()
            for k in (1, 2, 3):
                line_first(a, k).wait_recv()

            def into(here, total):
                own[a][here, :] = total.astype(jnp.bfloat16)

            add_rows(
                into,
                [lambda here: own[a][here, :]]
                + [lambda here, k=k: got1[a][k, here, :] for k in range(3)],
                rows_of(a),
                outs[a].shape[1],
            )
            for j in (3, 1, 2):
                cross(a, j).start()

        when(a, run)

    def line_finish(a):
        def run():
            part = part_of(a)
            for j in (1, 2, 3):
                cross(a, j).wait_recv()

            def into(here, total):
                fin[a][here, :] = total.astype(jnp.bfloat16)

            strip = strip_of(part, outs[a].shape[1])

            def body(at, carry):
                here = rows_at(at * strip, strip)
                total = own[a][rows_at(grp * part + at * strip, strip), :].astype(jnp.float32)
                for j in range(3):
                    total = total + got3[a][j, here, :].astype(jnp.float32)
                fin[a][here, :] = total.astype(jnp.bfloat16)
                return carry

            lax.fori_loop(0, part // strip, body, 0)
            spread_start(a)

        when(a, run)

    plane_arrays = [a for a in range(count) if kinds[a] == "plane"]
    line_arrays = [a for a in range(count) if kinds[a] == "line"]
    units = [(a, line) for a in plane_arrays for line in (0, 2, 1, 3)]
    ahead = 6
    if with_gains:
        gain_load().start()
    for unit in units[:2]:
        begin(*unit)
    for a in line_arrays:
        line_begin(a)
    for unit in units[2:ahead]:
        begin(*unit)
    if with_gains:
        gain_load().wait()
        for j in range(1, 16):
            gain_copy(j).start()
    lag = 2
    finished = []
    for at in range(len(units) + lag + 4):
        if at + ahead < len(units):
            begin(*units[at + ahead])
        if at < len(units):
            middle(*units[at])
        if at == len(units) // 2:
            for a in line_arrays:
                line_middle(a)
        if at == len(units) // 2 + 2:
            for a in line_arrays:
                line_finish(a)
        if at == len(units) // 2 + 4:
            for a in line_arrays:
                pass_on(a)
        if lag <= at < len(units) + lag:
            late(*units[at - lag])
        spot = at - lag - 2
        if 0 <= spot < len(units) and units[spot][1] == 3:
            if finished:
                pass_on(finished[-1])
            finish(units[spot][0])
            finished.append(units[spot][0])
    pass_on(finished[-1])
    if with_gains:
        for j in range(1, 16):
            gain_copy(j).wait_recv()
        total = gain_in[pos]
        for j in range(15):
            total = total + gain_got[j]
        gain_out[...] = total
    for a in range(count):

        def run(a=a):
            spread(a, 2).wait_recv()
            spread(a, 3).wait_recv()
            own_out(a).wait()
            for way in range(4):
                spread(a, way).wait_send()
            if kinds[a] == "plane":
                for line in range(4):
                    for b in (0, 1):
                        send_first(a, line, b).wait_send()
                    send_second(a, line).wait_send()
                    pl.when(line != pos)(send_line(a, line).wait_send)
            else:
                for k in (1, 2, 3):
                    line_first(a, k).wait_send()
                    cross(a, k).wait_send()

        when(a, run)
    if with_gains:
        for j in range(1, 16):
            gain_copy(j).wait_send()


def reduce_all(arrays, gains, kinds, only, collective_id):
    count = len(arrays)
    more = 0 if gains is None else 1
    outs = [jax.ShapeDtypeStruct((x.shape[0] // 4, x.shape[1]), x.dtype) for x in arrays]
    buffers = []
    for x, kind in zip(arrays, kinds):
        rows, columns = x.shape[0] // 4, x.shape[1]
        part = rows // 4
        if kind == "plane":
            shapes = [(4, 2, part, columns), (4, 2, part, columns), (4, part, columns)]
        else:
            shapes = [(rows, columns), (3, rows, columns), (8, 128)]
        shapes += [(3, part, columns), (part, columns)]
        buffers += [pltpu.VMEM(shape, x.dtype) for shape in shapes]
    dma = pltpu.SemaphoreType.DMA
    scratch = [dma((count, 4, 2))] * 3 + [dma((count, 4))] * 6 + [dma((count,))] + buffers
    if more:
        outs.append(jax.ShapeDtypeStruct(gains.shape[1:], gains.dtype))
        scratch += [
            dma,
            dma((15,)),
            dma((15,)),
            pltpu.VMEM(gains.shape, gains.dtype),
            pltpu.VMEM((15,) + gains.shape[1:], gains.dtype),
        ]
    return pl.pallas_call(
        functools.partial(reduce_kernel, kinds, bool(more), only),
        out_shape=outs,
        in_specs=[ANYWHERE] * (count + more),
        out_specs=[ANYWHERE] * count + [pl.BlockSpec(memory_space=pltpu.VMEM)] * more,
        scratch_shapes=scratch,
        compiler_params=pltpu.CompilerParams(
            collective_id=collective_id, has_side_effects=True, vmem_limit_bytes=58 << 20
        ),
    )(*arrays, *((gains,) if more else ()))


def block_forward(hidden, key_valid, weights):
    gain_attn, qkv_weight, proj_weight, gain_mlp, up_weight, down_weight = weights
    seqs, length = key_valid.shape
    normed_in = normed(hidden, gain_attn).astype(jnp.bfloat16)
    qkv_rows = product(normed_in, qkv_weight).astype(jnp.bfloat16)
    mixed_rows, log_total = jax.vmap(attend)(qkv_rows.reshape(seqs, length, -1), key_valid)
    mixed_rows = mixed_rows.reshape(seqs * length, -1)
    hidden_mid = hidden + product(mixed_rows, proj_weight)
    mlp_in = normed(hidden_mid, gain_mlp).astype(jnp.bfloat16)
    pre_act = product(mlp_in, up_weight)
    activated = gelu_exact(pre_act).astype(jnp.bfloat16)
    hidden_out = hidden_mid + product(activated, down_weight)
    kept = (hidden, normed_in, qkv_rows, log_total, mixed_rows, hidden_mid, mlp_in, pre_act, activated)
    return hidden_out, kept


def block_backward(kept, grad_out, key_valid, weights):
    hidden, normed_in, qkv_rows, log_total, mixed_rows, hidden_mid, mlp_in, pre_act, activated = kept
    gain_attn, qkv_weight, proj_weight, gain_mlp, up_weight, down_weight = weights
    seqs, length = key_valid.shape
    grad_low = grad_out.astype(jnp.bfloat16)
    grad_activated = product_nt(grad_low, down_weight)
    grad_pre = jax.vjp(gelu_exact, pre_act)[1](grad_activated)[0].astype(jnp.bfloat16)
    grad_mlp_in = product_nt(grad_pre, up_weight)
    grad_mid_norm, grad_gain_mlp = norm_back(hidden_mid, gain_mlp, grad_mlp_in)
    grad_mid = grad_out + grad_mid_norm
    grad_mid_low = grad_mid.astype(jnp.bfloat16)
    grad_mixed = product_nt(grad_mid_low, proj_weight).astype(jnp.bfloat16)
    grad_qkv = jax.vmap(attend_back)(
        qkv_rows.reshape(seqs, length, -1),
        key_valid,
        log_total,
        grad_mixed.reshape(seqs, length, -1),
    ).reshape(seqs * length, -1)
    grad_normed = product_nt(grad_qkv, qkv_weight)
    grad_in_norm, grad_gain_attn = norm_back(hidden, gain_attn, grad_normed)
    pairs = (normed_in, grad_qkv), (mixed_rows, grad_mid_low), (mlp_in, grad_pre), (activated, grad_low)
    return grad_mid + grad_in_norm, (grad_gain_attn, grad_gain_mlp), pairs


def weight_grads(pairs):
    return tuple(product_tn(rows, grads).astype(jnp.bfloat16) for rows, grads in pairs)


def nothing_like(run):
    return jax.tree.map(lambda a: jnp.zeros(a.shape, a.dtype), jax.eval_shape(run))


def only_on(live, run):
    return lax.cond(live, run, lambda: nothing_like(run))


def after(value, *others):
    return lax.optimization_barrier((value,) + others)[0]


def per_device(
    tokens,
    lengths,
    levels,
    noise_rows,
    embed_table,
    w_in,
    ln_attn,
    w_qkv,
    w_proj,
    ln_mlp,
    w_up,
    w_down,
    ln_final,
    w_out,
):
    sec = lax.axis_index("section")
    pos = lax.axis_index("dp")
    first_section = sec == 0
    last_section = sec == 1
    rows = tokens.shape[0]
    seqs = lengths.shape[0]
    length = rows // seqs
    width = w_out.shape[0] * 4
    emb = w_out.shape[1]
    vocab_part = embed_table.shape[0]
    gains = jnp.concatenate(
        [ln_attn, ln_mlp, ln_final[None], jnp.zeros((13, ln_final.shape[0]), jnp.bfloat16)], 0
    )
    ids = jnp.concatenate([tokens.reshape(-1, 128), jnp.zeros((8 - rows // 128, 128), jnp.int32)], 0)
    shards = (w_qkv[0], w_proj[0], w_up[0], w_down[0], w_in, w_out, gains, ids)
    wholes = gather_all(shards, (7, 6, 4, 0, 1, 2, 3), (6, 0, 1, 2, 3, 5), (6, 7, 1), 0)
    qkv_weight, proj_weight, up_weight, down_weight, in_weight, out_weight, gain_all, line_ids = wholes
    gain_all = gain_all.reshape(4, 16, -1).astype(jnp.float32)
    gain_attn = gain_all[:, 0].reshape(-1)
    gain_mlp = gain_all[:, 1].reshape(-1)
    final_gain = gain_all[:, 2].reshape(-1)
    weights = (gain_attn, qkv_weight, proj_weight, gain_mlp, up_weight, down_weight)
    key_valid = jnp.arange(length, dtype=jnp.int32)[None, :] < lengths[:, None]
    loss_scale = LOSS_GAIN / math.sqrt(rows * lax.axis_size(("group", "dp")))

    def look_up():
        local = line_ids.reshape(4, 8, 128)[:, : rows // 128].reshape(-1) - pos * vocab_part
        hit = local[:, None] == lax.broadcasted_iota(jnp.int32, (1, vocab_part), 1)
        return product(hit.astype(jnp.bfloat16), embed_table).astype(jnp.bfloat16)

    looked_parts = only_on(first_section, look_up).reshape(4, rows, emb)
    looked_parts, all_ids = swap_rows(looked_parts, line_ids, 1)
    all_tokens = all_ids.reshape(16, 8, 128)[:, : rows // 128].reshape(-1)
    noise_level = jnp.exp(LOG_LOW + levels.astype(jnp.float32) * (LOG_SPAN / (LEVELS - 1)))
    scale_in = lax.rsqrt(EMB_VAR + noise_level * noise_level)
    row_level = jnp.repeat(noise_level, length)[:, None]
    row_scale = jnp.repeat(scale_in, length)[:, None]

    def front():
        looked = jnp.sum(looked_parts.astype(jnp.float32), 0)
        mixed_in = ((looked + row_level * noise_rows.astype(jnp.float32)) * row_scale).astype(
            jnp.bfloat16
        )
        out, kept = block_forward(product(mixed_in, in_weight), key_valid, weights)
        return out.astype(jnp.bfloat16), kept, mixed_in

    out_first, kept_first, mixed_in = only_on(first_section, front)
    x_second = passed_along(out_first, "section", 1)
    (table_full,) = gather_all((after(embed_table, x_second),), (0,), (), (), 2)

    def back():
        hidden_out, kept = block_forward(x_second.astype(jnp.float32), key_valid, weights)
        final_in = normed(hidden_out, final_gain).astype(jnp.bfloat16)
        projected = product(final_in, out_weight).astype(jnp.bfloat16)
        return projected, final_in, hidden_out, kept

    projected_b, final_in, hidden_out, kept_second = only_on(last_section, back)
    projected = passed_along(after(projected_b, table_full), "section", -1)

    def vocabulary():
        logits = product_nt(projected, table_full)
        row_max = jnp.max(logits, -1, keepdims=True)
        log_total = row_max + jnp.log(jnp.sum(jnp.exp(logits - row_max), -1, keepdims=True))
        vocab_ids = lax.broadcasted_iota(jnp.int32, logits.shape, 1)
        target_hit = vocab_ids == tokens[:, None]
        picked = jnp.sum(jnp.where(target_hit, logits, 0.0), -1)
        valid = key_valid.reshape(-1)
        entropy = jnp.where(valid, log_total[:, 0] - picked, 0.0).astype(jnp.bfloat16)
        scale = jnp.where(valid, loss_scale, 0.0)[:, None]
        grad_logits = (
            (jnp.exp(logits - log_total) - target_hit.astype(jnp.float32)) * scale
        ).astype(jnp.bfloat16)
        grad_proj = product(grad_logits, table_full).astype(jnp.bfloat16)
        return grad_proj, entropy, grad_logits

    grad_proj_a, loss_low, grad_logits = only_on(first_section, vocabulary)
    grad_proj = passed_along(grad_proj_a, "section", 1)
    grad_logits = after(grad_logits, grad_proj)
    table_g = only_on(
        first_section, lambda: product_tn(grad_logits, projected).astype(jnp.bfloat16)
    )
    (table_r,) = reduce_all((table_g,), None, ("plane",), 0, 3)

    def back_again():
        grad_final = product_nt(grad_proj, out_weight)
        grad_top, gain_final = norm_back(hidden_out, final_gain, grad_final)
        grad_start, gain_pair, pairs = block_backward(kept_second, grad_top, key_valid, weights)
        return grad_start.astype(jnp.bfloat16), gain_pair + (gain_final,), pairs

    grad_second, gains_b, pairs_b = only_on(last_section, back_again)
    grad_first = passed_along(after(grad_second, table_r), "section", -1)
    pairs_b = after(pairs_b, grad_first)
    shape = in_weight.shape

    def front_back():
        grad_start, gain_pair, pairs = block_backward(
            kept_first, grad_first.astype(jnp.float32), key_valid, weights
        )
        grad_low = grad_start.astype(jnp.bfloat16)
        looked_grad = (product_nt(grad_low, in_weight) * row_scale).astype(jnp.bfloat16)
        edge = product_tn(mixed_in, grad_low).astype(jnp.bfloat16)
        return gain_pair + (jnp.zeros_like(final_gain),), weight_grads(pairs), edge, looked_grad

    def end_back():
        edge = product_tn(final_in, grad_proj).astype(jnp.bfloat16)
        edge = edge.reshape(4, shape[0] // 4, shape[1]).reshape(shape)
        return gains_b, weight_grads(pairs_b), edge, jnp.zeros((rows, emb), jnp.bfloat16)

    gain_set, grads, edge_g, looked_grad = lax.cond(first_section, front_back, end_back)
    gain_rows = jnp.concatenate([jnp.stack(gain_set, 0), jnp.zeros((5, width), jnp.float32)], 0)
    gain_rows = gain_rows.reshape(8, 4, width // 4).transpose(1, 0, 2)
    order = (grads[2], grads[3], edge_g, grads[1], grads[0])
    kinds = ("plane",) * 4 + ("line",)
    up_r, down_r, edge_r, proj_r, qkv_r, gain_r = reduce_all(order, gain_rows, kinds, None, 4)
    looked_all = lax.all_gather(looked_grad, ("group", "dp"), axis=0, tiled=True)

    def add_looked():
        local = all_tokens - pos * vocab_part
        hit = lax.broadcasted_iota(jnp.int32, (vocab_part, 1), 0) == local[None, :]
        looked_sum = product(hit.astype(jnp.bfloat16), looked_all)
        return (looked_sum + table_r.astype(jnp.float32)).astype(jnp.bfloat16)

    mine = (only_on(first_section, add_looked), edge_r, gain_r, loss_low)
    theirs = lax.ppermute(mine, "section", [(0, 1), (1, 0)])

    def pair_of(at):
        low = jnp.where(first_section, mine[at], theirs[at])
        high = jnp.where(first_section, theirs[at], mine[at])
        return low, high

    table_out = pair_of(0)[0].astype(jnp.float32)
    in_r, out_r = pair_of(1)
    final_r = pair_of(2)[1][2]
    token_loss = pair_of(3)[0]
    return (
        token_loss,
        table_out,
        in_r.astype(jnp.float32),
        gain_r[0][None],
        qkv_r.astype(jnp.float32)[None],
        proj_r.astype(jnp.float32)[None],
        gain_r[1][None],
        up_r.astype(jnp.float32)[None],
        down_r.astype(jnp.float32)[None],
        final_r,
        out_r.astype(jnp.float32).reshape(-1, emb),
    )


def solution(mesh):
    placed = (
        P(("group", "dp")),
        P(("group", "dp")),
        P(("group", "dp")),
        P(("group", "dp"), None),
        P("dp", None),
        P("dp", None),
        P("section", "dp"),
        P("section", "dp", None),
        P("section", "dp", None),
        P("section", "dp"),
        P("section", "dp", None),
        P("section", "dp", None),
        P("dp"),
        P("dp", None),
    )
    fits = (mesh.shape["section"], mesh.shape["group"], mesh.shape["dp"]) == (2, 4, 4)
    return jax.shard_map(
        per_device if fits else per_device_general,
        mesh=mesh,
        in_specs=placed,
        out_specs=(
            P(("group", "dp")),
            P("dp", None),
            P("dp", None),
            P("section", "dp"),
            P("section", "dp", None),
            P("section", "dp", None),
            P("section", "dp"),
            P("section", "dp", None),
            P("section", "dp", None),
            P("dp"),
            P("dp", None),
        ),
        check_vma=False,
    )
```

```python
import functools
import math

import jax
import jax.numpy as jnp
from jax import lax
from jax.experimental import pallas as pl
from jax.experimental.pallas import tpu as pltpu
from jax.sharding import PartitionSpec as P

HEAD = 64
LEVELS = 64
LEN = 128
MB = 2


EPS = 1e-05
LOG_LOW = -2.995732273553991
LOG_SPAN = 2.995732273553991
EMB_VAR = 0.015625
MASKED = -1e30
LOSS_GAIN = 16.0


def passed_along(x, axis, by):
    count = lax.axis_size(axis)
    pairs = [(i, i + by) for i in range(count) if 0 <= i + by < count]
    return lax.ppermute(x, axis, pairs)


def product(left_side, right_side):
    return jnp.dot(left_side, right_side, preferred_element_type=jnp.float32)


def product_tn(left_side, right_side):
    return lax.dot_general(
        left_side, right_side, (((0,), (0,)), ((), ())), preferred_element_type=jnp.float32
    )


def product_nt(left_side, right_side):
    return lax.dot_general(
        left_side, right_side, (((1,), (1,)), ((), ())), preferred_element_type=jnp.float32
    )


def normed(inputs, gain_vec):
    center = inputs - jnp.mean(inputs, -1, keepdims=True)
    return center * lax.rsqrt(jnp.mean(center * center, -1, keepdims=True) + EPS) * gain_vec


def norm_back(inputs, gain_vec, upstream):
    output, pullback = jax.vjp(normed, inputs, gain_vec)
    return pullback(upstream)


def gelu_exact(values_in):
    return jax.nn.gelu(values_in, approximate=False)


def attn_scores(split_rows, key_valid):
    scores = (
        jnp.einsum(
            "qhd,khd->hqk", split_rows[:, 0], split_rows[:, 1], preferred_element_type=jnp.float32
        )
        * 0.125
    )
    return jnp.where(key_valid[None, None, :], scores, MASKED)


def attend(qkv_rows, key_valid):
    length = qkv_rows.shape[0]
    model_width = qkv_rows.shape[1] // 3
    split_rows = qkv_rows.reshape(length, 3, model_width // HEAD, HEAD)
    scores = attn_scores(split_rows, key_valid)
    row_max = jnp.max(scores, -1, keepdims=True)
    log_total = row_max + jnp.log(jnp.sum(jnp.exp(scores - row_max), -1, keepdims=True))
    probs_low = jnp.exp(scores - log_total).astype(jnp.bfloat16)
    mixed_rows = jnp.einsum(
        "hqk,khd->qhd", probs_low, split_rows[:, 2], preferred_element_type=jnp.float32
    )
    return (mixed_rows.reshape(length, model_width).astype(jnp.bfloat16), log_total)


def attend_back(qkv_rows, key_valid, log_total, grad_mixed):
    length = qkv_rows.shape[0]
    model_width = qkv_rows.shape[1] // 3
    head_count = model_width // HEAD
    split_rows = qkv_rows.reshape(length, 3, head_count, HEAD)
    grad_heads = grad_mixed.reshape(length, head_count, HEAD)
    probs_full = jnp.exp(attn_scores(split_rows, key_valid) - log_total)
    grad_values = jnp.einsum(
        "hqk,qhd->khd",
        probs_full.astype(jnp.bfloat16),
        grad_heads,
        preferred_element_type=jnp.float32,
    )
    grad_probs = jnp.einsum(
        "qhd,khd->hqk", grad_heads, split_rows[:, 2], preferred_element_type=jnp.float32
    )
    grad_scores = (
        probs_full * (grad_probs - jnp.sum(grad_probs * probs_full, -1, keepdims=True))
    ).astype(jnp.bfloat16)
    grad_query = (
        jnp.einsum(
            "hqk,khd->qhd", grad_scores, split_rows[:, 1], preferred_element_type=jnp.float32
        )
        * 0.125
    )
    grad_key = (
        jnp.einsum(
            "hqk,qhd->khd", grad_scores, split_rows[:, 0], preferred_element_type=jnp.float32
        )
        * 0.125
    )
    stacked = jnp.stack([grad_query, grad_key, grad_values], 1).reshape(length, 3 * model_width)
    return stacked.astype(jnp.bfloat16)


def layer_forward(hidden, key_valid, weights):
    gain_attn, qkv_weight, proj_weight, gain_mlp, up_weight, down_weight = weights
    normed_in = normed(hidden, gain_attn).astype(jnp.bfloat16)
    qkv_rows = product(normed_in, qkv_weight).astype(jnp.bfloat16)
    mixed_rows, log_total = attend(qkv_rows, key_valid)
    hidden_mid = hidden + product(mixed_rows, proj_weight)
    mlp_in = normed(hidden_mid, gain_mlp).astype(jnp.bfloat16)
    pre_act = product(mlp_in, up_weight)
    activated = gelu_exact(pre_act).astype(jnp.bfloat16)
    hidden_out = hidden_mid + product(activated, down_weight)
    return (
        hidden_out,
        (
            hidden,
            normed_in,
            qkv_rows,
            log_total,
            mixed_rows,
            hidden_mid,
            mlp_in,
            pre_act,
            activated,
        ),
    )


def empty_kept(length, model_width, hidden_units, head_count):
    return (
        jnp.zeros((length, model_width), jnp.float32),
        jnp.zeros((length, model_width), jnp.bfloat16),
        jnp.zeros((length, 3 * model_width), jnp.bfloat16),
        jnp.zeros((head_count, length, 1), jnp.float32),
        jnp.zeros((length, model_width), jnp.bfloat16),
        jnp.zeros((length, model_width), jnp.float32),
        jnp.zeros((length, model_width), jnp.bfloat16),
        jnp.zeros((length, hidden_units), jnp.float32),
        jnp.zeros((length, hidden_units), jnp.bfloat16),
    )


def layer_backward(kept_vals, grad_out, key_valid, weights):
    hidden, normed_in, qkv_rows, log_total, mixed_rows, hidden_mid, mlp_in, pre_act, activated = (
        kept_vals
    )
    gain_attn, qkv_weight, proj_weight, gain_mlp, up_weight, down_weight = weights
    grad_low = grad_out.astype(jnp.bfloat16)
    grad_activated = product_nt(grad_low, down_weight)
    grad_pre = jax.vjp(gelu_exact, pre_act)[1](grad_activated)[0].astype(jnp.bfloat16)
    grad_mlp_in = product_nt(grad_pre, up_weight)
    grad_mid_norm, grad_gain_mlp = norm_back(hidden_mid, gain_mlp, grad_mlp_in)
    grad_mid = grad_out + grad_mid_norm
    grad_mid_low = grad_mid.astype(jnp.bfloat16)
    grad_mixed = product_nt(grad_mid_low, proj_weight).astype(jnp.bfloat16)
    grad_qkv = attend_back(qkv_rows, key_valid, log_total, grad_mixed)
    grad_normed = product_nt(grad_qkv, qkv_weight)
    grad_in_norm, grad_gain_attn = norm_back(hidden, gain_attn, grad_normed)
    records = (activated, grad_low, mlp_in, grad_pre, mixed_rows, grad_mid_low, normed_in, grad_qkv)
    return (grad_mid + grad_in_norm, (grad_gain_attn, grad_gain_mlp), records)


def layer_zero(length, model_width, hidden_units):
    records = (
        jnp.zeros((length, hidden_units), jnp.bfloat16),
        jnp.zeros((length, model_width), jnp.bfloat16),
        jnp.zeros((length, model_width), jnp.bfloat16),
        jnp.zeros((length, hidden_units), jnp.bfloat16),
        jnp.zeros((length, model_width), jnp.bfloat16),
        jnp.zeros((length, model_width), jnp.bfloat16),
        jnp.zeros((length, model_width), jnp.bfloat16),
        jnp.zeros((length, 3 * model_width), jnp.bfloat16),
    )
    gains = (jnp.zeros((model_width,), jnp.float32), jnp.zeros((model_width,), jnp.float32))
    return (jnp.zeros((length, model_width), jnp.float32), gains, records)


def layer_grads(records):
    activated, grad_low, mlp_in, grad_pre, mixed_rows, grad_mid_low, normed_in, grad_qkv = records
    return (
        product_tn(normed_in, grad_qkv),
        product_tn(mixed_rows, grad_mid_low),
        product_tn(mlp_in, grad_pre),
        product_tn(activated, grad_low),
    )


def embed_inputs(token_ids, noise_block, level_id, table_full):
    noise_level = jnp.exp(LOG_LOW + level_id.astype(jnp.float32) * (LOG_SPAN / (LEVELS - 1)))
    scale_in = lax.rsqrt(EMB_VAR + noise_level * noise_level)
    looked = jnp.take(table_full, token_ids, axis=0).astype(jnp.float32)
    mixed_in = ((looked + noise_level * noise_block.astype(jnp.float32)) * scale_in).astype(
        jnp.bfloat16
    )
    return (mixed_in, scale_in)


def embed_backward(token_ids, noise_block, level_id, grad_start, table_full, in_weight):
    mixed_in, scale_in = embed_inputs(token_ids, noise_block, level_id, table_full)
    grad_low = grad_start.astype(jnp.bfloat16)
    grad_looked = product_nt(grad_low, in_weight) * scale_in
    return (mixed_in, grad_low, grad_looked)


def embed_zero(length, model_width, emb_width):
    return (
        jnp.zeros((length, emb_width), jnp.bfloat16),
        jnp.zeros((length, model_width), jnp.bfloat16),
        jnp.zeros((length, emb_width), jnp.float32),
    )


def tail_pass(hidden, token_ids, key_valid, final_gain, out_weight, table_full, loss_scale):
    final_in = normed(hidden, final_gain).astype(jnp.bfloat16)
    projected = product(final_in, out_weight).astype(jnp.bfloat16)
    logits = product_nt(projected, table_full)
    row_max = jnp.max(logits, -1, keepdims=True)
    log_total = row_max + jnp.log(jnp.sum(jnp.exp(logits - row_max), -1, keepdims=True))
    vocab_ids = lax.broadcasted_iota(jnp.int32, logits.shape, 1)
    target_hit = vocab_ids == token_ids[:, None]
    picked = jnp.sum(jnp.where(target_hit, logits, 0.0), -1)
    entropy = jnp.where(key_valid, log_total[:, 0] - picked, 0.0)
    row_scale = jnp.where(key_valid, loss_scale, 0.0)[:, None]
    grad_logits = (
        (jnp.exp(logits - log_total) - target_hit.astype(jnp.float32)) * row_scale
    ).astype(jnp.bfloat16)
    grad_proj = product(grad_logits, table_full).astype(jnp.bfloat16)
    grad_final = product_nt(grad_proj, out_weight)
    grad_hidden, grad_gain = norm_back(hidden, final_gain, grad_final)
    return (grad_hidden, entropy, grad_gain, (grad_logits, projected, final_in, grad_proj))


def tail_zero(length, model_width, emb_width, vocab_rows):
    records = (
        jnp.zeros((length, vocab_rows), jnp.bfloat16),
        jnp.zeros((length, emb_width), jnp.bfloat16),
        jnp.zeros((length, model_width), jnp.bfloat16),
        jnp.zeros((length, emb_width), jnp.bfloat16),
    )
    return (
        jnp.zeros((length, model_width), jnp.float32),
        jnp.zeros((length,), jnp.float32),
        jnp.zeros((model_width,), jnp.float32),
        records,
    )


def edge_grads(tail_records, embed_records, token_ids):
    grad_logits, projected, final_in, grad_proj = tail_records
    mixed_in, grad_low, grad_looked = embed_records
    table_grad = product_tn(grad_logits, projected).at[token_ids].add(grad_looked)
    return (table_grad, product_tn(mixed_in, grad_low), product_tn(final_in, grad_proj))


def joined_rows(record_list):
    return jax.tree.map(lambda *pieces: jnp.concatenate(pieces, 0), *record_list)


def assemble(gain_attn_sum, gain_mlp_sum, layer_set, edge_set, gain_final_sum):
    return (
        gain_attn_sum[None],
        layer_set[0][None],
        layer_set[1][None],
        gain_mlp_sum[None],
        layer_set[2][None],
        layer_set[3][None],
        edge_set[0],
        edge_set[1],
        gain_final_sum,
        edge_set[2],
    )


def per_device_general(
    tokens,
    lengths,
    levels,
    noise_rows,
    embed_table,
    w_in,
    ln_attn,
    w_qkv,
    w_proj,
    ln_mlp,
    w_up,
    w_down,
    ln_final,
    w_out,
):
    gathered = (
        lax.all_gather(embed_table, "dp", axis=0, tiled=True),
        lax.all_gather(w_in, "dp", axis=0, tiled=True),
        lax.all_gather(ln_attn, "dp", axis=1, tiled=True),
        lax.all_gather(w_qkv, "dp", axis=1, tiled=True),
        lax.all_gather(w_proj, "dp", axis=1, tiled=True),
        lax.all_gather(ln_mlp, "dp", axis=1, tiled=True),
        lax.all_gather(w_up, "dp", axis=1, tiled=True),
        lax.all_gather(w_down, "dp", axis=1, tiled=True),
        lax.all_gather(ln_final, "dp", axis=0, tiled=True),
        lax.all_gather(w_out, "dp", axis=0, tiled=True),
    )
    table_full = gathered[0]
    in_weight = gathered[1]
    layer_weights = (
        gathered[2][0].astype(jnp.float32),
        gathered[3][0],
        gathered[4][0],
        gathered[5][0].astype(jnp.float32),
        gathered[6][0],
        gathered[7][0],
    )
    final_gain = gathered[8].astype(jnp.float32)
    out_weight = gathered[9]
    model_width = out_weight.shape[0]
    emb_width = out_weight.shape[1]
    vocab_rows = table_full.shape[0]
    hidden_units = layer_weights[4].shape[1]
    head_count = model_width // HEAD
    section_index = lax.axis_index("section")
    first_section = section_index == 0
    token_grid = tokens.reshape(MB, LEN)
    noise_grid = noise_rows.reshape(MB, LEN, noise_rows.shape[1])
    positions = jnp.arange(LEN, dtype=jnp.int32)
    valid_grid = positions[None, :] < lengths[:, None]
    loss_scale = LOSS_GAIN / math.sqrt(tokens.shape[0] * lax.axis_size(("group", "dp")))
    gain_attn_sum = jnp.zeros((model_width,), jnp.float32)
    gain_mlp_sum = jnp.zeros((model_width,), jnp.float32)
    gain_final_sum = jnp.zeros((model_width,), jnp.float32)
    recv_act = jnp.zeros((LEN, model_width), jnp.bfloat16)
    recv_grad = jnp.zeros((LEN, model_width), jnp.bfloat16)
    zero_rows = jnp.zeros((LEN, model_width), jnp.float32)
    kept_ticks = {}
    layer_recs = {}
    tail_recs = {}
    embed_recs = {}
    losses = []
    for moment in range(MB + 2):
        offset = moment - section_index
        fwd_valid = (offset >= 0) & (offset < MB)
        fwd_index = jnp.clip(offset, 0, MB - 1)
        ids_now = lax.dynamic_index_in_dim(token_grid, fwd_index, 0, False)
        noise_now = lax.dynamic_index_in_dim(noise_grid, fwd_index, 0, False)
        level_now = lax.dynamic_index_in_dim(levels, fwd_index, 0, False)
        valid_now = lax.dynamic_index_in_dim(valid_grid, fwd_index, 0, False)

        def first_input():
            mixed_in, scale_in = embed_inputs(ids_now, noise_now, level_now, table_full)
            return product(mixed_in, in_weight)

        layer_input = lax.cond(first_section, first_input, lambda: recv_act.astype(jnp.float32))
        hidden_out, kept_now = lax.cond(
            fwd_valid,
            lambda: layer_forward(layer_input, valid_now, layer_weights),
            lambda: (zero_rows, empty_kept(LEN, model_width, hidden_units, head_count)),
        )
        kept_ticks[moment] = kept_now
        tail_live = jnp.logical_not(first_section) & fwd_valid
        tail_grad, entropy, final_step, tail_now = lax.cond(
            tail_live,
            lambda: tail_pass(
                hidden_out, ids_now, valid_now, final_gain, out_weight, table_full, loss_scale
            ),
            lambda: tail_zero(LEN, model_width, emb_width, vocab_rows),
        )
        tail_recs[moment] = tail_now
        gain_final_sum = gain_final_sum + final_step
        back_tick = moment - 2
        late_live = 0 <= back_tick < MB
        late_index = min(max(back_tick, 0), MB - 1)
        kept_late = kept_ticks[back_tick] if back_tick >= 0 else kept_now
        kept_back = lax.cond(first_section, lambda: kept_late, lambda: kept_now)
        grad_top = jnp.where(first_section, recv_grad.astype(jnp.float32), tail_grad)
        valid_back = jnp.where(first_section, valid_grid[late_index], valid_now)
        back_live = jnp.where(first_section, late_live, fwd_valid)
        grad_start, gain_pair, layer_now = lax.cond(
            back_live,
            lambda: layer_backward(kept_back, grad_top, valid_back, layer_weights),
            lambda: layer_zero(LEN, model_width, hidden_units),
        )
        layer_recs[moment] = layer_now
        gain_attn_sum = gain_attn_sum + gain_pair[0]
        gain_mlp_sum = gain_mlp_sum + gain_pair[1]
        if late_live:
            embed_now = lax.cond(
                first_section,
                lambda: embed_backward(
                    token_grid[late_index],
                    noise_grid[late_index],
                    levels[late_index],
                    grad_start,
                    table_full,
                    in_weight,
                ),
                lambda: embed_zero(LEN, model_width, emb_width),
            )
        else:
            embed_now = embed_zero(LEN, model_width, emb_width)
        embed_recs[moment] = embed_now
        if moment < MB:
            recv_act = passed_along(hidden_out.astype(jnp.bfloat16), "section", 1)
        if 1 <= moment <= MB:
            entropy_low = entropy.astype(jnp.bfloat16)
            recv_grad, loss_back = passed_along(
                (grad_start.astype(jnp.bfloat16), entropy_low), "section", -1
            )
            losses.append(jnp.where(first_section, loss_back, entropy_low))
    chosen = [
        jax.tree.map(
            lambda early, late: jnp.where(first_section, early, late),
            layer_recs[micro + 2],
            layer_recs[micro + 1],
        )
        for micro in range(MB)
    ]
    all_layer = layer_grads(joined_rows(chosen))
    all_tail = joined_rows([tail_recs[micro + 1] for micro in range(MB)])
    all_embed = joined_rows([embed_recs[micro + 2] for micro in range(MB)])
    all_edge = edge_grads(all_tail, all_embed, tokens)
    grad_pack = assemble(gain_attn_sum, gain_mlp_sum, all_layer, all_edge, gain_final_sum)
    parted = (
        lax.psum_scatter(
            grad_pack[0].astype(jnp.bfloat16), "dp", scatter_dimension=1, tiled=True
        ).astype(jnp.float32),
        lax.psum_scatter(
            grad_pack[1].astype(jnp.bfloat16), "dp", scatter_dimension=1, tiled=True
        ).astype(jnp.float32),
        lax.psum_scatter(
            grad_pack[2].astype(jnp.bfloat16), "dp", scatter_dimension=1, tiled=True
        ).astype(jnp.float32),
        lax.psum_scatter(
            grad_pack[3].astype(jnp.bfloat16), "dp", scatter_dimension=1, tiled=True
        ).astype(jnp.float32),
        lax.psum_scatter(
            grad_pack[4].astype(jnp.bfloat16), "dp", scatter_dimension=1, tiled=True
        ).astype(jnp.float32),
        lax.psum_scatter(
            grad_pack[5].astype(jnp.bfloat16), "dp", scatter_dimension=1, tiled=True
        ).astype(jnp.float32),
        lax.psum_scatter(
            grad_pack[6].astype(jnp.bfloat16), "dp", scatter_dimension=0, tiled=True
        ).astype(jnp.float32),
        lax.psum_scatter(
            grad_pack[7].astype(jnp.bfloat16), "dp", scatter_dimension=0, tiled=True
        ).astype(jnp.float32),
        lax.psum_scatter(
            grad_pack[8].astype(jnp.bfloat16), "dp", scatter_dimension=0, tiled=True
        ).astype(jnp.float32),
        lax.psum_scatter(
            grad_pack[9].astype(jnp.bfloat16), "dp", scatter_dimension=0, tiled=True
        ).astype(jnp.float32),
    )
    layer_total = (
        lax.psum(parted[0].astype(jnp.bfloat16), "group").astype(jnp.float32),
        lax.psum(parted[1].astype(jnp.bfloat16), "group").astype(jnp.float32),
        lax.psum(parted[2].astype(jnp.bfloat16), "group").astype(jnp.float32),
        lax.psum(parted[3].astype(jnp.bfloat16), "group").astype(jnp.float32),
        lax.psum(parted[4].astype(jnp.bfloat16), "group").astype(jnp.float32),
        lax.psum(parted[5].astype(jnp.bfloat16), "group").astype(jnp.float32),
    )
    edge_total = (
        lax.psum(parted[6].astype(jnp.bfloat16), ("section", "group")).astype(jnp.float32),
        lax.psum(parted[7].astype(jnp.bfloat16), ("section", "group")).astype(jnp.float32),
        lax.psum(parted[8].astype(jnp.bfloat16), ("section", "group")).astype(jnp.float32),
        lax.psum(parted[9].astype(jnp.bfloat16), ("section", "group")).astype(jnp.float32),
    )
    token_loss = jnp.concatenate(losses)
    return (
        token_loss,
        edge_total[0],
        edge_total[1],
        layer_total[0],
        layer_total[1],
        layer_total[2],
        layer_total[3],
        layer_total[4],
        layer_total[5],
        edge_total[2],
        edge_total[3],
    )


MESH = pl.DeviceIdType.MESH
ANYWHERE = pl.BlockSpec(memory_space=pl.ANY)


def pick(index, values):
    out = values[-1]
    for at in range(len(values) - 2, -1, -1):
        out = jnp.where(index == at, values[at], out)
    return out


def rows_at(start, size):
    return pl.ds(pl.multiple_of(start, 8), size)


def remote(src, dst, send_sem, recv_sem, device):
    return pltpu.make_async_remote_copy(
        src_ref=src,
        dst_ref=dst,
        send_sem=send_sem,
        recv_sem=recv_sem,
        device_id=device,
        device_id_type=MESH,
    )


def gather_kernel(count, first_order, last_order, whole_line, *refs):
    shards = refs[:count]
    wholes = refs[count : 2 * count]
    own_sem, zsend, zrecv, psend, precv, gate = refs[2 * count : 2 * count + 6]
    stage = refs[2 * count + 6 :]
    sec = lax.axis_index("section")
    grp = lax.axis_index("group")
    pos = lax.axis_index("dp")
    beside = ((sec, grp ^ 1, pos), (sec, grp ^ 2, pos))
    above = (sec, grp, pos + 1)
    below = (sec, grp, pos - 1)
    partner = (1 - sec, grp, pos)
    barrier = pltpu.get_barrier_semaphore()
    both = bool(last_order)

    def greet(device):
        pl.semaphore_signal(barrier, inc=1, device_id=device, device_id_type=MESH)

    def meet():
        for device in beside + ((partner,) if both else ()):
            greet(device)

        @pl.when(pos > 0)
        def _():
            greet(below)

        @pl.when(pos < 3)
        def _():
            greet(above)

        at_end = (pos == 0) | (pos == 3)
        pl.semaphore_wait(barrier, jnp.where(at_end, 3, 4) + (1 if both else 0))

    turn = [pick(pos, v) for v in ((3, 1, 3, 1), (2, 3, 1, 2), (1, 2, 2, 3))]

    def run(order, before, middle):
        def part_of(idx):
            rows = shards[idx].shape[0]
            return rows if idx in whole_line else rows // 4

        def shift(idx, who):
            return 0 if idx in whole_line else who * part_of(idx)

        def block(idx, origin, who):
            return rows_at(origin * shards[idx].shape[0] + shift(idx, who), part_of(idx))

        def load_own(slot):
            return pltpu.make_async_copy(shards[order[slot]], stage[order[slot]], own_sem.at[slot])

        def store_own(slot):
            idx = order[slot]
            rows = shards[idx].shape[0]
            return pltpu.make_async_copy(
                stage[idx], wholes[idx].at[rows_at(pos * rows, rows)], own_sem.at[slot]
            )

        def own_ends(slot):
            idx = order[slot]
            src = shards[idx].at[rows_at(shift(idx, grp), part_of(idx))]
            dst = wholes[idx].at[block(idx, pos, grp)]
            return (
                (pos < 3, remote(src, dst, zsend.at[slot, 0], zrecv.at[slot, 1], above)),
                (pos > 0, remote(src, dst, zsend.at[slot, 1], zrecv.at[slot, 3], below)),
            )

        def start_own(slot):
            for goes, copy in own_ends(slot):
                pl.when(goes)(copy.start)

        def origin_of(j):
            return lax.rem(pos - turn[j] + 4, 4)

        def arrived(slot, j):
            here = wholes[order[slot]].at[block(order[slot], origin_of(j), grp)]
            return remote(here, here, zsend.at[slot, 2 + j], zrecv.at[slot, turn[j]], partner)

        def onward(slot, j):
            step = jnp.where(turn[j] <= pos, 1, -1)
            to = pos + step
            here = wholes[order[slot]].at[block(order[slot], origin_of(j), grp)]
            landed = jnp.clip(turn[j] + step, 0, 3)
            copy = remote(
                here,
                here,
                zsend.at[slot, 2 + j],
                zrecv.at[slot, landed],
                (sec, grp, jnp.clip(to, 0, 3)),
            )
            return (to >= 0) & (to <= 3), copy

        def plane(slot, j, way):
            idx = order[slot]
            origin = origin_of(j)
            if way < 2:
                here = wholes[idx].at[block(idx, origin, grp)]
                return remote(here, here, psend.at[slot, j, way], precv.at[slot, j, way], beside[way])
            half = shards[idx].shape[1] // 2
            there = wholes[idx].at[
                block(idx, origin, grp ^ (way - 1)), pl.ds(half * (way - 2), half)
            ]
            return remote(
                there, there, psend.at[slot, j, way], precv.at[slot, j, way], beside[3 - way]
            )

        items = [(slot, j) for slot in range(len(order)) for j in range(3)]
        crossing = [item for item in items if order[item[0]] not in whole_line]

        def first(slot, j):
            arrived(slot, j).wait_recv()
            goes, copy = onward(slot, j)
            pl.when(goes)(copy.start)
            if (slot, j) in crossing:
                plane(slot, j, 0).start()
                plane(slot, j, 1).start()

        def second(slot, j):
            if (slot, j) in crossing:
                for way in (0, 1):
                    plane(slot, j, way).wait_recv()
                    plane(slot, j, way + 2).start()

        if before is not None:
            before()
        for slot in range(len(order)):
            start_own(slot)
        for slot in range(len(order)):
            load_own(slot).start()
        lag = 2
        for at in range(len(items) + lag):
            if at < len(items):
                slot, j = items[at]
                if j == 2:
                    load_own(slot).wait()
                    store_own(slot).start()
                first(slot, j)
            if at == len(items) - 1 and middle is not None:
                middle()
            if at >= lag:
                second(*items[at - lag])
        for slot, j in crossing:
            plane(slot, j, 2).wait_recv()
            plane(slot, j, 3).wait_recv()
        for slot in range(len(order)):
            store_own(slot).wait()
            for goes, copy in own_ends(slot):
                pl.when(goes)(copy.wait_send)
        for slot, j in items:
            goes, copy = onward(slot, j)
            pl.when(goes)(copy.wait_send)
        for slot, j in crossing:
            for way in range(4):
                plane(slot, j, way).wait_send()

    def let_go():
        pl.semaphore_signal(gate, inc=1, device_id=partner, device_id_type=MESH)

    def hold():
        pl.semaphore_wait(gate, 1)

    if both:
        meet()

        @pl.when(sec == 0)
        def _():
            run(first_order, None, let_go)

        @pl.when(sec == 1)
        def _():
            run(last_order, hold, None)

    else:

        @pl.when(sec == 0)
        def _():
            meet()
            run(first_order, None, None)


def gather_all(shards, first_order, last_order, whole_line, collective_id):
    count = len(shards)
    return pl.pallas_call(
        functools.partial(gather_kernel, count, first_order, last_order, whole_line),
        out_shape=[jax.ShapeDtypeStruct((s.shape[0] * 4, s.shape[1]), s.dtype) for s in shards],
        in_specs=[ANYWHERE] * count,
        out_specs=[ANYWHERE] * count,
        scratch_shapes=[
            pltpu.SemaphoreType.DMA((count,)),
            pltpu.SemaphoreType.DMA((count, 5)),
            pltpu.SemaphoreType.DMA((count, 4)),
            pltpu.SemaphoreType.DMA((count, 3, 4)),
            pltpu.SemaphoreType.DMA((count, 3, 4)),
            pltpu.SemaphoreType.REGULAR,
        ]
        + [pltpu.VMEM(s.shape, s.dtype) for s in shards],
        compiler_params=pltpu.CompilerParams(
            collective_id=collective_id, has_side_effects=True, vmem_limit_bytes=24 << 20
        ),
    )(*shards)


def swap_kernel(rows_ref, ids_ref, out_ref, ids_out, own_sem, send_sem, recv_sem):
    sec = lax.axis_index("section")
    grp = lax.axis_index("group")
    pos = lax.axis_index("dp")

    @pl.when(sec == 0)
    def _():
        barrier = pltpu.get_barrier_semaphore()
        peers = [(sec, grp, lax.rem(pos + k, 4)) for k in (1, 2, 3)]
        sides = [(sec, grp ^ j, pos) for j in (1, 2, 3)]
        for device in peers + sides:
            pl.semaphore_signal(barrier, inc=1, device_id=device, device_id_type=MESH)
        pl.semaphore_wait(barrier, 6)
        copies = []
        for k, device in enumerate(peers):
            copies.append(
                remote(rows_ref.at[device[2]], out_ref.at[pos], send_sem.at[k], recv_sem.at[k], device)
            )
        for k, device in enumerate(sides):
            copies.append(
                remote(ids_ref, ids_out.at[grp], send_sem.at[3 + k], recv_sem.at[3 + k], device)
            )
        for copy in copies:
            copy.start()
        own_rows = pltpu.make_async_copy(rows_ref.at[pos], out_ref.at[pos], own_sem.at[0])
        own_ids = pltpu.make_async_copy(ids_ref, ids_out.at[grp], own_sem.at[1])
        own_rows.start()
        own_ids.start()
        own_rows.wait()
        own_ids.wait()
        for copy in copies:
            copy.wait()


def swap_rows(rows, ids, collective_id):
    in_vmem = pl.BlockSpec(memory_space=pltpu.VMEM)
    return pl.pallas_call(
        swap_kernel,
        out_shape=[
            jax.ShapeDtypeStruct(rows.shape, rows.dtype),
            jax.ShapeDtypeStruct((4,) + ids.shape, ids.dtype),
        ],
        in_specs=[in_vmem] * 2,
        out_specs=[in_vmem] * 2,
        scratch_shapes=[
            pltpu.SemaphoreType.DMA((2,)),
            pltpu.SemaphoreType.DMA((6,)),
            pltpu.SemaphoreType.DMA((6,)),
        ],
        compiler_params=pltpu.CompilerParams(collective_id=collective_id, has_side_effects=True),
    )(rows, ids)


def strip_of(rows, columns):
    strip = 16
    while 2 * strip * columns <= 65536 and rows % (2 * strip) == 0:
        strip = 2 * strip
    return strip


def add_rows(into, terms, rows, columns):
    strip = strip_of(rows, columns)

    def body(at, carry):
        here = rows_at(at * strip, strip)
        total = terms[0](here).astype(jnp.float32)
        for term in terms[1:]:
            total = total + term(here).astype(jnp.float32)
        into(here, total)
        return carry

    lax.fori_loop(0, rows // strip, body, 0)


def reduce_kernel(kinds, with_gains, only, *refs):
    if only is None:
        reduce_body(kinds, with_gains, *refs)
    else:
        pl.when(lax.axis_index("section") == only)(
            functools.partial(reduce_body, kinds, with_gains, *refs)
        )


def reduce_body(kinds, with_gains, *refs):
    count = len(kinds)
    more = 1 if with_gains else 0
    arrays = refs[:count]
    outs = refs[count + more : 2 * count + more]
    rest = list(refs[2 * count + 2 * more :])
    s1, r1, own_sem, s2, r2, s3, r3, s4, r4, fin_sem = rest[:10]
    bufs = rest[10 : 10 + 5 * count]
    if with_gains:
        gains = refs[count]
        gain_out = refs[2 * count + 1]
        gain_own_sem, sg, rg, gain_in, gain_got = rest[10 + 5 * count :]
    own, got1, got2, got3, fin = ([bufs[5 * a + b] for a in range(count)] for b in range(5))
    sec = lax.axis_index("section")
    grp = lax.axis_index("group")
    pos = lax.axis_index("dp")
    beside = ((sec, grp ^ 1, pos), (sec, grp ^ 2, pos))
    barrier = pltpu.get_barrier_semaphore()
    steps = [(jg, jz) for jg in range(4) for jz in range(4)][1:]

    def other(j):
        return (sec, grp ^ steps[j - 1][0], lax.rem(pos + steps[j - 1][1], 4))

    if with_gains:
        peers = [other(j) for j in range(1, 16)]
    else:
        peers = [(sec, grp ^ j, pos) for j in (1, 2, 3)] + [other(j) for j in (1, 2, 3)]
    for device in peers:
        pl.semaphore_signal(barrier, inc=1, device_id=device, device_id_type=MESH)
    pl.semaphore_wait(barrier, len(peers))

    def when(a, run):
        run()

    def rows_of(a):
        return outs[a].shape[0]

    def part_of(a):
        return outs[a].shape[0] // 4

    def block(a, line, who):
        return arrays[a].at[rows_at(line * rows_of(a) + who * part_of(a), part_of(a))]

    def gain_copy(j):
        device = other(j)
        return remote(gain_in.at[device[2]], gain_got.at[j - 1], sg.at[j - 1], rg.at[j - 1], device)

    def gain_load():
        return pltpu.make_async_copy(gains, gain_in, gain_own_sem)

    def ways(line):
        first = 0 if line < 2 else 1
        return first, 1 - first

    def send_first(a, line, b):
        first, second = ways(line)
        who = grp ^ (1 + first)
        if b:
            who = who ^ (1 + second)
        return remote(
            block(a, line, who),
            got1[a].at[line, b],
            s1.at[a, line, b],
            r1.at[a, line, b],
            beside[first],
        )

    def load_own(a, line, b):
        first, second = ways(line)
        who = grp ^ (1 + second) if b else grp
        return pltpu.make_async_copy(block(a, line, who), own[a].at[line, b], own_sem.at[a, line, b])

    def send_second(a, line):
        first, second = ways(line)
        return remote(own[a].at[line, 1], got2[a].at[line], s2.at[a, line], r2.at[a, line], beside[second])

    def send_line(a, line):
        k = lax.rem(line - pos + 4, 4)
        slot = jnp.maximum(k - 1, 0)
        return remote(
            own[a].at[line, 0], got3[a].at[slot], s3.at[a, line], r3.at[a, slot], (sec, grp, line)
        )

    def line_arrival(a, slot):
        return remote(got3[a].at[slot], got3[a].at[slot], s3.at[a, slot], r3.at[a, slot], beside[0])

    def begin(a, line):
        def run():
            for b in (1, 0):
                send_first(a, line, b).start()
                load_own(a, line, b).start()

        when(a, run)

    def middle(a, line):
        def run():
            columns = outs[a].shape[1]
            for b in (1, 0):
                load_own(a, line, b).wait()
                send_first(a, line, b).wait_recv()

                def into(here, total, b=b):
                    own[a][line, b, here, :] = total.astype(jnp.bfloat16)

                add_rows(
                    into,
                    [lambda here, b=b: own[a][line, b, here, :], lambda here, b=b: got1[a][line, b, here, :]],
                    part_of(a),
                    columns,
                )
                if b:
                    send_second(a, line).start()

        when(a, run)

    def late(a, line):
        def run():
            send_second(a, line).wait_recv()

            def into(here, total):
                own[a][line, 0, here, :] = total.astype(jnp.bfloat16)

            add_rows(
                into,
                [lambda here: own[a][line, 0, here, :], lambda here: got2[a][line, here, :]],
                part_of(a),
                outs[a].shape[1],
            )
            pl.when(line != pos)(send_line(a, line).start)

        when(a, run)

    def own_out(a):
        here = outs[a].at[rows_at(grp * part_of(a), part_of(a))]
        return pltpu.make_async_copy(fin[a], here, fin_sem.at[a])

    def spread(a, way):
        part = part_of(a)
        if way < 2:
            here = outs[a].at[rows_at(grp * part, part)]
            return remote(fin[a], here, s4.at[a, way], r4.at[a, way], beside[way])
        half = outs[a].shape[1] // 2
        there = outs[a].at[rows_at((grp ^ (way - 1)) * part, part), pl.ds(half * (way - 2), half)]
        return remote(there, there, s4.at[a, way], r4.at[a, way], beside[3 - way])

    def spread_start(a):
        spread(a, 0).start()
        spread(a, 1).start()
        own_out(a).start()

    def finish(a):
        def run():
            for slot in range(3):
                line_arrival(a, slot).wait_recv()

            def into(here, total):
                fin[a][here, :] = total.astype(jnp.bfloat16)

            add_rows(
                into,
                [lambda here: own[a][pos, 0, here, :]]
                + [lambda here, slot=slot: got3[a][slot, here, :] for slot in range(3)],
                part_of(a),
                outs[a].shape[1],
            )
            spread_start(a)

        when(a, run)

    def pass_on(a):
        def run():
            for way in (0, 1):
                spread(a, way).wait_recv()
                spread(a, way + 2).start()

        when(a, run)

    def line_rows(a, line):
        return arrays[a].at[rows_at(line * rows_of(a), rows_of(a))]

    def line_first(a, k):
        to = lax.rem(pos + k, 4)
        return remote(
            line_rows(a, to), got1[a].at[k - 1], s1.at[a, k, 0], r1.at[a, k, 0], (sec, grp, to)
        )

    def line_own(a):
        return pltpu.make_async_copy(line_rows(a, pos), own[a], own_sem.at[a, 0, 0])

    def cross(a, j):
        part = part_of(a)
        to = grp ^ j
        return remote(
            own[a].at[rows_at(to * part, part)],
            got3[a].at[j - 1],
            s3.at[a, j],
            r3.at[a, j - 1],
            (sec, to, pos),
        )

    def line_begin(a):
        def run():
            for k in (2, 1, 3):
                line_first(a, k).start()
            line_own(a).start()

        when(a, run)

    def line_middle(a):
        def run():
            line_own(a).wait()
            for k in (1, 2, 3):
                line_first(a, k).wait_recv()

            def into(here, total):
                own[a][here, :] = total.astype(jnp.bfloat16)

            add_rows(
                into,
                [lambda here: own[a][here, :]]
                + [lambda here, k=k: got1[a][k, here, :] for k in range(3)],
                rows_of(a),
                outs[a].shape[1],
            )
            for j in (3, 1, 2):
                cross(a, j).start()

        when(a, run)

    def line_finish(a):
        def run():
            part = part_of(a)
            for j in (1, 2, 3):
                cross(a, j).wait_recv()

            def into(here, total):
                fin[a][here, :] = total.astype(jnp.bfloat16)

            strip = strip_of(part, outs[a].shape[1])

            def body(at, carry):
                here = rows_at(at * strip, strip)
                total = own[a][rows_at(grp * part + at * strip, strip), :].astype(jnp.float32)
                for j in range(3):
                    total = total + got3[a][j, here, :].astype(jnp.float32)
                fin[a][here, :] = total.astype(jnp.bfloat16)
                return carry

            lax.fori_loop(0, part // strip, body, 0)
            spread_start(a)

        when(a, run)

    plane_arrays = [a for a in range(count) if kinds[a] == "plane"]
    line_arrays = [a for a in range(count) if kinds[a] == "line"]
    units = [(a, line) for a in plane_arrays for line in (0, 2, 1, 3)]
    ahead = 6
    if with_gains:
        gain_load().start()
    for unit in units[:2]:
        begin(*unit)
    for a in line_arrays:
        line_begin(a)
    for unit in units[2:ahead]:
        begin(*unit)
    if with_gains:
        gain_load().wait()
        for j in range(1, 16):
            gain_copy(j).start()
    lag = 2
    finished = []
    for at in range(len(units) + lag + 4):
        if at + ahead < len(units):
            begin(*units[at + ahead])
        if at < len(units):
            middle(*units[at])
        if at == len(units) // 2:
            for a in line_arrays:
                line_middle(a)
        if at == len(units) // 2 + 2:
            for a in line_arrays:
                line_finish(a)
        if at == len(units) // 2 + 4:
            for a in line_arrays:
                pass_on(a)
        if lag <= at < len(units) + lag:
            late(*units[at - lag])
        spot = at - lag - 2
        if 0 <= spot < len(units) and units[spot][1] == 3:
            if finished:
                pass_on(finished[-1])
            finish(units[spot][0])
            finished.append(units[spot][0])
    pass_on(finished[-1])
    if with_gains:
        for j in range(1, 16):
            gain_copy(j).wait_recv()
        total = gain_in[pos]
        for j in range(15):
            total = total + gain_got[j]
        gain_out[...] = total
    for a in range(count):

        def run(a=a):
            spread(a, 2).wait_recv()
            spread(a, 3).wait_recv()
            own_out(a).wait()
            for way in range(4):
                spread(a, way).wait_send()
            if kinds[a] == "plane":
                for line in range(4):
                    for b in (0, 1):
                        send_first(a, line, b).wait_send()
                    send_second(a, line).wait_send()
                    pl.when(line != pos)(send_line(a, line).wait_send)
            else:
                for k in (1, 2, 3):
                    line_first(a, k).wait_send()
                    cross(a, k).wait_send()

        when(a, run)
    if with_gains:
        for j in range(1, 16):
            gain_copy(j).wait_send()


def reduce_all(arrays, gains, kinds, only, collective_id):
    count = len(arrays)
    more = 0 if gains is None else 1
    outs = [jax.ShapeDtypeStruct((x.shape[0] // 4, x.shape[1]), x.dtype) for x in arrays]
    buffers = []
    for x, kind in zip(arrays, kinds):
        rows, columns = x.shape[0] // 4, x.shape[1]
        part = rows // 4
        if kind == "plane":
            shapes = [(4, 2, part, columns), (4, 2, part, columns), (4, part, columns)]
        else:
            shapes = [(rows, columns), (3, rows, columns), (8, 128)]
        shapes += [(3, part, columns), (part, columns)]
        buffers += [pltpu.VMEM(shape, x.dtype) for shape in shapes]
    dma = pltpu.SemaphoreType.DMA
    scratch = [dma((count, 4, 2))] * 3 + [dma((count, 4))] * 6 + [dma((count,))] + buffers
    if more:
        outs.append(jax.ShapeDtypeStruct(gains.shape[1:], gains.dtype))
        scratch += [
            dma,
            dma((15,)),
            dma((15,)),
            pltpu.VMEM(gains.shape, gains.dtype),
            pltpu.VMEM((15,) + gains.shape[1:], gains.dtype),
        ]
    return pl.pallas_call(
        functools.partial(reduce_kernel, kinds, bool(more), only),
        out_shape=outs,
        in_specs=[ANYWHERE] * (count + more),
        out_specs=[ANYWHERE] * count + [pl.BlockSpec(memory_space=pltpu.VMEM)] * more,
        scratch_shapes=scratch,
        compiler_params=pltpu.CompilerParams(
            collective_id=collective_id, has_side_effects=True, vmem_limit_bytes=58 << 20
        ),
    )(*arrays, *((gains,) if more else ()))


IN_VMEM = pl.BlockSpec(memory_space=pltpu.VMEM)
IN_SMEM = pl.BlockSpec(memory_space=pltpu.SMEM)
ROOT_HALF = 0.7071067811865476
ROOT_TWO_PI = 0.3989422804014327


def dot_nn(left, right):
    return lax.dot_general(
        left, right, (((1,), (0,)), ((), ())), preferred_element_type=jnp.float32
    )


def dot_nt(left, right):
    return lax.dot_general(
        left, right, (((1,), (1,)), ((), ())), preferred_element_type=jnp.float32
    )


def dot_tn(left, right):
    return lax.dot_general(
        left, right, (((0,), (0,)), ((), ())), preferred_element_type=jnp.float32
    )


def unit_rows(v):
    center = v - jnp.mean(v, -1, keepdims=True)
    scale = lax.rsqrt(jnp.mean(center * center, -1, keepdims=True) + EPS)
    return center * scale, scale


def split_heads(pair):
    low = lax.broadcasted_iota(jnp.int32, pair.shape, 1) < HEAD
    nothing = jnp.zeros_like(pair)
    return jnp.concatenate([jnp.where(low, pair, nothing), jnp.where(low, nothing, pair)], 0)


def join_heads(stacked):
    half = stacked.shape[0] // 2
    low = lax.broadcasted_iota(jnp.int32, (half, stacked.shape[1]), 1) < HEAD
    return jnp.where(low, stacked[:half], stacked[half:])


def pair_scores(keys, stacked_queries, key_count):
    scores = dot_nt(keys, stacked_queries) * 0.125
    valid = lax.broadcasted_iota(jnp.int32, scores.shape, 0) < key_count
    return jnp.where(valid, scores, MASKED)


STRIP = 64


def forward_kernel(only, tile, given, *refs):
    x, gain_attn, gain_mlp, counts, wq, wp, wu, wd = refs[:8]
    rest = refs[8 + given :]
    outs = rest[:KEPT_COUNT]
    qv, pv, uv, dv = rest[KEPT_COUNT : KEPT_COUNT + 4]
    kept = rest[KEPT_COUNT + 4 : 2 * KEPT_COUNT + 4]
    a, att, m, acc, wsem, osem = rest[2 * KEPT_COUNT + 4 :]
    xv, at_t, qkv, lse, att_t, mid, m_t, pre, act_t, out = kept
    rows, width = a.shape
    units = dv.shape[0]

    def store(idx):
        return pltpu.make_async_copy(kept[idx], outs[idx], osem.at[idx])

    def run():
        loads = []

        def load(src, dst):
            copy = pltpu.make_async_copy(src, dst, wsem.at[len(loads)])
            copy.start()
            loads.append(copy)

        for lo in range(0, 3 * width, tile):
            load(wq.at[:, pl.ds(lo, tile)], qv.at[:, pl.ds(lo, tile)])
        load(wp, pv)
        for lo in range(0, units, tile):
            load(wu.at[:, pl.ds(lo, tile)], uv.at[:, pl.ds(lo, tile)])
            load(wd.at[pl.ds(lo, tile)], dv.at[pl.ds(lo, tile)])
        loads = iter(loads)
        for lo in range(0, rows, STRIP):
            here = pl.ds(lo, STRIP)
            xv[here, :] = x[here, :].astype(jnp.float32)
            a[here, :] = (unit_rows(xv[here, :])[0] * gain_attn[...]).astype(jnp.bfloat16)
        store(0).start()
        for lo in range(0, 3 * width, tile):
            next(loads).wait()
            cols = pl.ds(lo, tile)
            qkv[:, cols] = dot_nn(a[...], qv[:, cols]).astype(jnp.bfloat16)
        store(2).start()
        for lo in range(0, width, 256):
            at_t[pl.ds(lo, 256), :] = a[:, pl.ds(lo, 256)].T
        store(1).start()
        pairs = width // 128
        for seq in range(rows // LEN):
            here = pl.ds(seq * LEN, LEN)
            for pair in range(pairs):
                stacked = split_heads(qkv[here, pl.ds(pair * 128, 128)])
                scores = pair_scores(qkv[here, pl.ds(width + pair * 128, 128)], stacked, counts[seq])
                top = jnp.max(scores, 0, keepdims=True)
                power = jnp.exp(scores - top)
                total = jnp.sum(power, 0, keepdims=True)
                lse[seq * pairs + pair] = top + jnp.log(total)
                probs = (power * (1.0 / total)).astype(jnp.bfloat16)
                mixed = dot_tn(probs, qkv[here, pl.ds(2 * width + pair * 128, 128)])
                att[here, pl.ds(pair * 128, 128)] = join_heads(mixed).astype(jnp.bfloat16)
        store(3).start()
        for lo in range(0, width, 256):
            att_t[pl.ds(lo, 256), :] = att[:, pl.ds(lo, 256)].T
        store(4).start()
        next(loads).wait()
        for lo in range(0, width, tile):
            cols = pl.ds(lo, tile)
            mid[:, cols] = xv[:, cols] + dot_nn(att[...], pv[:, cols])
        for lo in range(0, rows, STRIP):
            here = pl.ds(lo, STRIP)
            m[here, :] = (unit_rows(mid[here, :])[0] * gain_mlp[...]).astype(jnp.bfloat16)
        store(5).start()
        acc[...] = mid[...]
        for lo in range(0, units, tile):
            cols = pl.ds(lo, tile)
            next(loads).wait()
            before = dot_nn(m[...], uv[:, cols])
            pre[:, cols] = before
            active = (0.5 * before * (1.0 + lax.erf(before * ROOT_HALF))).astype(jnp.bfloat16)
            act_t[cols, :] = active.T
            next(loads).wait()
            acc[...] += dot_nn(active, dv[cols, :])
        store(7).start()
        store(8).start()
        for lo in range(0, width, 256):
            m_t[pl.ds(lo, 256), :] = m[:, pl.ds(lo, 256)].T
        store(6).start()
        out[...] = acc[...]
        store(9).start()
        for idx in range(KEPT_COUNT):
            store(idx).wait()

    pl.when(lax.axis_index("section") == only)(run)


KEPT_COUNT = 10


def kept_shapes(rows, width, units):
    f32, low = jnp.float32, jnp.bfloat16
    return [
        jax.ShapeDtypeStruct(shape, kind)
        for shape, kind in (
            ((rows, width), f32),
            ((width, rows), low),
            ((rows, 3 * width), low),
            ((rows // LEN * width // 128, 1, 2 * LEN), f32),
            ((width, rows), low),
            ((rows, width), f32),
            ((width, rows), low),
            ((rows, units), f32),
            ((units, rows), low),
            ((rows, width), f32),
        )
    ]


def run_forward(only, x, gain_attn, gain_mlp, counts, weights, kept):
    wq, wp, wu, wd = weights
    rows, width = x.shape
    units = wd.shape[0]
    tile = 512
    shapes = kept_shapes(rows, width, units)
    low = jnp.bfloat16
    given = 0 if kept is None else KEPT_COUNT
    in_specs = [IN_VMEM] * 3 + [IN_SMEM] + [ANYWHERE] * (4 + given)
    return pl.pallas_call(
        functools.partial(forward_kernel, only, tile, given),
        out_shape=shapes,
        in_specs=in_specs,
        out_specs=[ANYWHERE] * KEPT_COUNT,
        input_output_aliases={8 + idx: idx for idx in range(given)},
        scratch_shapes=[pltpu.VMEM(w.shape, w.dtype) for w in weights]
        + [pltpu.VMEM(s.shape, s.dtype) for s in shapes]
        + [
            pltpu.VMEM((rows, width), low),
            pltpu.VMEM((rows, width), low),
            pltpu.VMEM((rows, width), low),
            pltpu.VMEM((rows, width), jnp.float32),
            pltpu.SemaphoreType.DMA((3 * width // tile + 1 + 2 * units // tile,)),
            pltpu.SemaphoreType.DMA((KEPT_COUNT,)),
        ],
        compiler_params=pltpu.CompilerParams(vmem_limit_bytes=56 << 20),
    )(x, gain_attn, gain_mlp, counts, wq, wp, wu, wd, *(kept or ()))


GRAD_COUNT = 6


def grad_shapes(rows, width, units):
    f32, low = jnp.float32, jnp.bfloat16
    return [
        jax.ShapeDtypeStruct(shape, kind)
        for shape, kind in (
            ((rows, width), low),
            ((rows, units), low),
            ((rows, width), low),
            ((rows, 3 * width), low),
            ((rows, width), low),
            ((8, width), f32),
        )
    ]


def norm_pull(v, gain, upstream):
    unit, scale = unit_rows(v)
    pulled = upstream * gain
    inner = jnp.mean(pulled * unit, -1, keepdims=True)
    grad = (pulled - jnp.mean(pulled, -1, keepdims=True) - unit * inner) * scale
    return grad, jnp.sum(upstream * unit, 0, keepdims=True)


def backward_kernel(only, tile, given, *refs):
    grad, gain_attn, gain_mlp, counts, x_in, qkv_in, lse_in, mid_in, pre_in, wq, wp, wu, wd = refs[:13]
    rest = refs[13 + given :]
    outs = rest[:GRAD_COUNT]
    qv, pv, uv, dv = rest[GRAD_COUNT : GRAD_COUNT + 4]
    made = rest[GRAD_COUNT + 4 : 2 * GRAD_COUNT + 4]
    x, qkv, lse, mid, pre, gm, gmid, gatt, wsem, ksem, osem = rest[2 * GRAD_COUNT + 4 :]
    gy, gpre, gz, gqkv, gx, gains = made
    rows, width = gm.shape
    units = dv.shape[0]

    def store(idx):
        return pltpu.make_async_copy(made[idx], outs[idx], osem.at[idx])

    def run():
        loads = []

        def load(src, dst):
            copy = pltpu.make_async_copy(src, dst, wsem.at[len(loads)])
            copy.start()
            loads.append(copy)

        kept = [
            pltpu.make_async_copy(src, dst, ksem.at[idx])
            for idx, (src, dst) in enumerate(
                ((pre_in, pre), (mid_in, mid), (qkv_in, qkv), (lse_in, lse), (x_in, x))
            )
        ]
        kept[0].start()
        for lo in range(0, units, tile):
            load(wd.at[pl.ds(lo, tile)], dv.at[pl.ds(lo, tile)])
            load(wu.at[:, pl.ds(lo, tile)], uv.at[:, pl.ds(lo, tile)])
        for copy in kept[1:]:
            copy.start()
        load(wp, pv)
        load(wq, qv)
        loads = iter(loads)
        gy[...] = grad[...].astype(jnp.bfloat16)
        store(0).start()
        gains[...] = jnp.zeros_like(gains)
        kept[0].wait()
        gm[...] = jnp.zeros_like(gm)
        for lo in range(0, units, tile):
            cols = pl.ds(lo, tile)
            next(loads).wait()
            pulled = dot_nt(gy[...], dv[cols, :])
            before = pre[:, cols]
            slope = 0.5 * (1.0 + lax.erf(before * ROOT_HALF)) + before * (
                ROOT_TWO_PI * jnp.exp(-0.5 * before * before)
            )
            low = (pulled * slope).astype(jnp.bfloat16)
            gpre[:, cols] = low
            next(loads).wait()
            gm[...] += dot_nt(low, uv[:, cols])
        store(1).start()
        kept[1].wait()
        for lo in range(0, rows, STRIP):
            here = pl.ds(lo, STRIP)
            step, gain = norm_pull(mid[here, :], gain_mlp[...], gm[here, :])
            total = grad[here, :].astype(jnp.float32) + step
            gmid[here, :] = total
            gz[here, :] = total.astype(jnp.bfloat16)
            gains[1:2, :] += gain
        store(2).start()
        next(loads).wait()
        gatt[...] = dot_nt(gz[...], pv[...]).astype(jnp.bfloat16)
        kept[2].wait()
        kept[3].wait()
        pairs = width // 128
        for seq in range(rows // LEN):
            here = pl.ds(seq * LEN, LEN)
            for pair in range(pairs):
                own = pl.ds(pair * 128, 128)
                stacked = split_heads(qkv[here, own])
                pulled = split_heads(gatt[here, own])
                keys = qkv[here, pl.ds(width + pair * 128, 128)]
                values = qkv[here, pl.ds(2 * width + pair * 128, 128)]
                probs = jnp.exp(pair_scores(keys, stacked, counts[seq]) - lse[seq * pairs + pair])
                gprobs = dot_nt(values, pulled)
                inner = jnp.sum(probs * gprobs, 0, keepdims=True)
                gscores = (probs * (gprobs - inner)).astype(jnp.bfloat16)
                gqkv[here, own] = (join_heads(dot_tn(gscores, keys)) * 0.125).astype(jnp.bfloat16)
                gqkv[here, pl.ds(width + pair * 128, 128)] = (dot_nn(gscores, stacked) * 0.125).astype(
                    jnp.bfloat16
                )
                gqkv[here, pl.ds(2 * width + pair * 128, 128)] = dot_nn(
                    probs.astype(jnp.bfloat16), pulled
                ).astype(jnp.bfloat16)
        store(3).start()
        next(loads).wait()
        for lo in range(0, width, 256):
            gm[:, pl.ds(lo, 256)] = dot_nt(gqkv[...], qv[pl.ds(lo, 256), :])
        kept[4].wait()
        for lo in range(0, rows, STRIP):
            here = pl.ds(lo, STRIP)
            step, gain = norm_pull(x[here, :], gain_attn[...], gm[here, :])
            gx[here, :] = (gmid[here, :] + step).astype(jnp.bfloat16)
            gains[0:1, :] += gain
        store(4).start()
        store(5).start()
        for idx in range(GRAD_COUNT):
            store(idx).wait()

    pl.when(lax.axis_index("section") == only)(run)


def run_backward(only, grad, gain_attn, gain_mlp, counts, kept, weights, made):
    wq, wp, wu, wd = weights
    x, _, qkv, lse, _, mid, _, pre, _, _ = kept
    rows, width = x.shape
    units = wd.shape[0]
    tile = 512
    shapes = grad_shapes(rows, width, units)
    low, f32 = jnp.bfloat16, jnp.float32
    given = 0 if made is None else GRAD_COUNT
    in_specs = [IN_VMEM] * 3 + [IN_SMEM] + [ANYWHERE] * (9 + given)
    return pl.pallas_call(
        functools.partial(backward_kernel, only, tile, given),
        out_shape=shapes,
        in_specs=in_specs,
        out_specs=[ANYWHERE] * GRAD_COUNT,
        input_output_aliases={13 + idx: idx for idx in range(given)},
        scratch_shapes=[pltpu.VMEM(w.shape, w.dtype) for w in weights]
        + [pltpu.VMEM(s.shape, s.dtype) for s in shapes]
        + [pltpu.VMEM(s.shape, s.dtype) for s in (x, qkv, lse, mid, pre)]
        + [
            pltpu.VMEM((rows, width), f32),
            pltpu.VMEM((rows, width), f32),
            pltpu.VMEM((rows, width), low),
            pltpu.SemaphoreType.DMA((2 + 2 * units // tile,)),
            pltpu.SemaphoreType.DMA((5,)),
            pltpu.SemaphoreType.DMA((GRAD_COUNT,)),
        ],
        compiler_params=pltpu.CompilerParams(vmem_limit_bytes=56 << 20),
    )(grad, gain_attn, gain_mlp, counts, x, qkv, lse, mid, pre, wq, wp, wu, wd, *(made or ()))


def vocabulary_kernel(only, tile, proj, ids, scale, table, gproj_out, loss_out, gtable, tv, gt, gp, tsem, gsem):
    rows, emb = proj.shape
    vocab = tv.shape[0]
    count = vocab // tile

    def run():
        for at in range(count):
            here = pl.ds(at * tile, tile)
            pltpu.make_async_copy(table.at[here], tv.at[here], tsem.at[at]).start()

        def logits_of(at):
            return dot_nt(tv[rows_at(at * tile, tile), :], proj[...])

        def hits_of(at):
            names = lax.broadcasted_iota(jnp.int32, (tile, rows), 0) + at * tile
            return names == ids[...]

        def stats(at, carry):
            top, total, picked = carry
            here = rows_at(at * tile, tile)
            pltpu.make_async_copy(table.at[here], tv.at[here], tsem.at[at]).wait()
            logits = logits_of(at)
            higher = jnp.maximum(top, jnp.max(logits, 0, keepdims=True))
            total = total * jnp.exp(top - higher) + jnp.sum(jnp.exp(logits - higher), 0, keepdims=True)
            picked = picked + jnp.sum(jnp.where(hits_of(at), logits, 0.0), 0, keepdims=True)
            return higher, total, picked

        start = (
            jnp.full((1, rows), MASKED, jnp.float32),
            jnp.zeros((1, rows), jnp.float32),
            jnp.zeros((1, rows), jnp.float32),
        )
        top, total, picked = lax.fori_loop(0, count, stats, start)
        log_total = top + jnp.log(total)
        loss_out[...] = jnp.where(scale[...] > 0, log_total - picked, 0.0)
        gp[...] = jnp.zeros_like(gp)

        def gstore(at):
            return pltpu.make_async_copy(
                gt.at[rows_at(at * tile, tile)], gtable.at[rows_at(at * tile, tile)], gsem.at[at]
            )

        def pull(at, carry):
            here = rows_at(at * tile, tile)
            probs = jnp.exp(logits_of(at) - log_total)
            grads = ((probs - jnp.where(hits_of(at), 1.0, 0.0)) * scale[...]).astype(jnp.bfloat16)
            gp[...] += dot_tn(grads, tv[here, :])
            gt[here, :] = dot_nn(grads, proj[...]).astype(jnp.bfloat16)
            gstore(at).start()
            return carry

        lax.fori_loop(0, count, pull, 0)
        gproj_out[...] = gp[...].astype(jnp.bfloat16)

        def done(at, carry):
            gstore(at).wait()
            return carry

        lax.fori_loop(0, count, done, 0)

    pl.when(lax.axis_index("section") == only)(run)


def run_vocabulary(only, proj, ids, scale, table):
    rows, emb = proj.shape
    vocab = table.shape[0]
    tile = 1024
    return pl.pallas_call(
        functools.partial(vocabulary_kernel, only, tile),
        out_shape=[
            jax.ShapeDtypeStruct((rows, emb), jnp.bfloat16),
            jax.ShapeDtypeStruct((1, rows), jnp.float32),
            jax.ShapeDtypeStruct(table.shape, jnp.bfloat16),
        ],
        in_specs=[IN_VMEM] * 3 + [ANYWHERE],
        out_specs=[IN_VMEM] * 2 + [ANYWHERE],
        scratch_shapes=[
            pltpu.VMEM(table.shape, table.dtype),
            pltpu.VMEM(table.shape, jnp.bfloat16),
            pltpu.VMEM((rows, emb), jnp.float32),
            pltpu.SemaphoreType.DMA((vocab // tile,)),
            pltpu.SemaphoreType.DMA((vocab // tile,)),
        ],
        compiler_params=pltpu.CompilerParams(vmem_limit_bytes=40 << 20),
    )(proj, ids, scale, table)


def nothing_like(run):
    return jax.tree.map(lambda a: jnp.zeros(a.shape, a.dtype), jax.eval_shape(run))


def only_on(live, run):
    return lax.cond(live, run, lambda: nothing_like(run))


def after(value, *others):
    return lax.optimization_barrier((value,) + others)[0]


def per_device(
    tokens,
    lengths,
    levels,
    noise_rows,
    embed_table,
    w_in,
    ln_attn,
    w_qkv,
    w_proj,
    ln_mlp,
    w_up,
    w_down,
    ln_final,
    w_out,
):
    sec = lax.axis_index("section")
    pos = lax.axis_index("dp")
    first_section = sec == 0
    last_section = sec == 1
    rows = tokens.shape[0]
    seqs = lengths.shape[0]
    length = rows // seqs
    width = w_out.shape[0] * 4
    emb = w_out.shape[1]
    vocab_part = embed_table.shape[0]
    gains = jnp.concatenate(
        [ln_attn, ln_mlp, ln_final[None], jnp.zeros((13, ln_final.shape[0]), jnp.bfloat16)], 0
    )
    ids = jnp.concatenate([tokens.reshape(-1, 128), jnp.zeros((8 - rows // 128, 128), jnp.int32)], 0)
    shards = (w_qkv[0], w_proj[0], w_up[0], w_down[0], w_in, w_out, gains, ids)
    wholes = gather_all(shards, (7, 6, 4, 0, 1, 2, 3), (6, 0, 1, 2, 3, 5), (6, 7, 1), 0)
    qkv_weight, proj_weight, up_weight, down_weight, in_weight, out_weight, gain_all, line_ids = wholes
    gain_all = gain_all.reshape(4, 16, -1).astype(jnp.float32)
    gain_attn = gain_all[:, 0].reshape(-1)
    gain_mlp = gain_all[:, 1].reshape(-1)
    final_gain = gain_all[:, 2].reshape(-1)
    weights = (qkv_weight, proj_weight, up_weight, down_weight)
    gain_attn = gain_attn[None]
    gain_mlp = gain_mlp[None]
    key_valid = jnp.arange(length, dtype=jnp.int32)[None, :] < lengths[:, None]
    loss_scale = LOSS_GAIN / math.sqrt(rows * lax.axis_size(("group", "dp")))

    def look_up():
        local = line_ids.reshape(4, 8, 128)[:, : rows // 128].reshape(-1) - pos * vocab_part
        hit = local[:, None] == lax.broadcasted_iota(jnp.int32, (1, vocab_part), 1)
        return product(hit.astype(jnp.bfloat16), embed_table).astype(jnp.bfloat16)

    looked_parts = only_on(first_section, look_up).reshape(4, rows, emb)
    looked_parts, all_ids = swap_rows(looked_parts, line_ids, 1)
    all_tokens = all_ids.reshape(16, 8, 128)[:, : rows // 128].reshape(-1)
    noise_level = jnp.exp(LOG_LOW + levels.astype(jnp.float32) * (LOG_SPAN / (LEVELS - 1)))
    scale_in = lax.rsqrt(EMB_VAR + noise_level * noise_level)
    row_level = jnp.repeat(noise_level, length)[:, None]
    row_scale = jnp.repeat(scale_in, length)[:, None]

    def front():
        looked = jnp.sum(looked_parts.astype(jnp.float32), 0)
        mixed_in = ((looked + row_level * noise_rows.astype(jnp.float32)) * row_scale).astype(
            jnp.bfloat16
        )
        return mixed_in, product(mixed_in, in_weight)

    mixed_in, x_first = only_on(first_section, front)
    kept = run_forward(0, x_first, gain_attn, gain_mlp, lengths, weights, None)
    x_second = passed_along(kept[9].astype(jnp.bfloat16), "section", 1)
    (table_full,) = gather_all((after(embed_table, x_second),), (0,), (), (), 2)
    kept = run_forward(1, x_second, gain_attn, gain_mlp, lengths, weights, kept)
    final_in = normed(kept[9], final_gain).astype(jnp.bfloat16)
    projected = product(final_in, out_weight).astype(jnp.bfloat16)
    projected = passed_along(after(projected, table_full), "section", -1)
    valid_scale = jnp.where(key_valid.reshape(1, -1), loss_scale, 0.0)
    grad_proj_a, entropy, table_g = run_vocabulary(
        0, projected, tokens[None], valid_scale, table_full
    )
    grad_proj = passed_along(grad_proj_a, "section", 1)
    (table_r,) = reduce_all((after(table_g, grad_proj),), None, ("plane",), 0, 3)
    grad_top, gain_final = norm_back(kept[9], final_gain, product_nt(grad_proj, out_weight))
    made = run_backward(1, grad_top, gain_attn, gain_mlp, lengths, kept, weights, None)
    grad_first = passed_along(after(made[4], table_r), "section", -1)
    made = run_backward(0, grad_first, gain_attn, gain_mlp, lengths, kept, weights, made)
    shape = in_weight.shape

    def front_edge():
        looked_grad = (product_nt(made[4], in_weight) * row_scale).astype(jnp.bfloat16)
        return product_tn(mixed_in, made[4]).astype(jnp.bfloat16), looked_grad

    def back_edge():
        edge = product_tn(final_in, grad_proj).astype(jnp.bfloat16)
        edge = edge.reshape(4, shape[0] // 4, shape[1]).reshape(shape)
        return edge, jnp.zeros((rows, emb), jnp.bfloat16)

    edge_g, looked_grad = lax.cond(first_section, front_edge, back_edge)
    gain_rows = made[5] + jnp.concatenate(
        [jnp.zeros((2, width)), gain_final[None], jnp.zeros((5, width))], 0
    )
    gain_rows = gain_rows.reshape(8, 4, width // 4).transpose(1, 0, 2)

    def grads_of(rows_at_once, grads):
        return product(rows_at_once, grads).astype(jnp.bfloat16)

    order = (
        grads_of(kept[6], made[1]),
        grads_of(kept[8], made[0]),
        edge_g,
        grads_of(kept[4], made[2]),
        grads_of(kept[1], made[3]),
    )
    kinds = ("plane",) * 4 + ("line",)
    up_r, down_r, edge_r, proj_r, qkv_r, gain_r = reduce_all(order, gain_rows, kinds, None, 4)
    looked_all = lax.all_gather(looked_grad, ("group", "dp"), axis=0, tiled=True)

    def add_looked():
        local = all_tokens - pos * vocab_part
        hit = lax.broadcasted_iota(jnp.int32, (vocab_part, 1), 0) == local[None, :]
        looked_sum = product(hit.astype(jnp.bfloat16), looked_all)
        return (looked_sum + table_r.astype(jnp.float32)).astype(jnp.bfloat16)

    loss_low = after(entropy, gain_r)[0].astype(jnp.bfloat16)
    mine = (only_on(first_section, add_looked), edge_r, gain_r, loss_low)
    theirs = lax.ppermute(mine, "section", [(0, 1), (1, 0)])

    def pair_of(at):
        low = jnp.where(first_section, mine[at], theirs[at])
        high = jnp.where(first_section, theirs[at], mine[at])
        return low, high

    table_out = pair_of(0)[0].astype(jnp.float32)
    in_r, out_r = pair_of(1)
    final_r = pair_of(2)[1][2]
    token_loss = pair_of(3)[0]
    return (
        token_loss,
        table_out,
        in_r.astype(jnp.float32),
        gain_r[0][None],
        qkv_r.astype(jnp.float32)[None],
        proj_r.astype(jnp.float32)[None],
        gain_r[1][None],
        up_r.astype(jnp.float32)[None],
        down_r.astype(jnp.float32)[None],
        final_r,
        out_r.astype(jnp.float32).reshape(-1, emb),
    )


def solution(mesh):
    placed = (
        P(("group", "dp")),
        P(("group", "dp")),
        P(("group", "dp")),
        P(("group", "dp"), None),
        P("dp", None),
        P("dp", None),
        P("section", "dp"),
        P("section", "dp", None),
        P("section", "dp", None),
        P("section", "dp"),
        P("section", "dp", None),
        P("section", "dp", None),
        P("dp"),
        P("dp", None),
    )
    fits = (mesh.shape["section"], mesh.shape["group"], mesh.shape["dp"]) == (2, 4, 4)
    return jax.shard_map(
        per_device if fits else per_device_general,
        mesh=mesh,
        in_specs=placed,
        out_specs=(
            P(("group", "dp")),
            P("dp", None),
            P("dp", None),
            P("section", "dp"),
            P("section", "dp", None),
            P("section", "dp", None),
            P("section", "dp"),
            P("section", "dp", None),
            P("section", "dp", None),
            P("dp"),
            P("dp", None),
        ),
        check_vma=False,
    )
```

```python
import functools
import math

import jax
import jax.numpy as jnp
from jax import lax
from jax.experimental import pallas as pl
from jax.experimental.pallas import tpu as pltpu
from jax.sharding import PartitionSpec as P

HEAD = 64
LEVELS = 64
LEN = 128
MB = 2


EPS = 1e-05
LOG_LOW = -2.995732273553991
LOG_SPAN = 2.995732273553991
EMB_VAR = 0.015625
MASKED = -1e30
LOSS_GAIN = 16.0


def passed_along(x, axis, by):
    count = lax.axis_size(axis)
    pairs = [(i, i + by) for i in range(count) if 0 <= i + by < count]
    return lax.ppermute(x, axis, pairs)


def product(left_side, right_side):
    return jnp.dot(left_side, right_side, preferred_element_type=jnp.float32)


def product_tn(left_side, right_side):
    return lax.dot_general(
        left_side, right_side, (((0,), (0,)), ((), ())), preferred_element_type=jnp.float32
    )


def product_nt(left_side, right_side):
    return lax.dot_general(
        left_side, right_side, (((1,), (1,)), ((), ())), preferred_element_type=jnp.float32
    )


def normed(inputs, gain_vec):
    center = inputs - jnp.mean(inputs, -1, keepdims=True)
    return center * lax.rsqrt(jnp.mean(center * center, -1, keepdims=True) + EPS) * gain_vec


def norm_back(inputs, gain_vec, upstream):
    output, pullback = jax.vjp(normed, inputs, gain_vec)
    return pullback(upstream)


def gelu_exact(values_in):
    return jax.nn.gelu(values_in, approximate=False)


def attn_scores(split_rows, key_valid):
    scores = (
        jnp.einsum(
            "qhd,khd->hqk", split_rows[:, 0], split_rows[:, 1], preferred_element_type=jnp.float32
        )
        * 0.125
    )
    return jnp.where(key_valid[None, None, :], scores, MASKED)


def attend(qkv_rows, key_valid):
    length = qkv_rows.shape[0]
    model_width = qkv_rows.shape[1] // 3
    split_rows = qkv_rows.reshape(length, 3, model_width // HEAD, HEAD)
    scores = attn_scores(split_rows, key_valid)
    row_max = jnp.max(scores, -1, keepdims=True)
    log_total = row_max + jnp.log(jnp.sum(jnp.exp(scores - row_max), -1, keepdims=True))
    probs_low = jnp.exp(scores - log_total).astype(jnp.bfloat16)
    mixed_rows = jnp.einsum(
        "hqk,khd->qhd", probs_low, split_rows[:, 2], preferred_element_type=jnp.float32
    )
    return (mixed_rows.reshape(length, model_width).astype(jnp.bfloat16), log_total)


def attend_back(qkv_rows, key_valid, log_total, grad_mixed):
    length = qkv_rows.shape[0]
    model_width = qkv_rows.shape[1] // 3
    head_count = model_width // HEAD
    split_rows = qkv_rows.reshape(length, 3, head_count, HEAD)
    grad_heads = grad_mixed.reshape(length, head_count, HEAD)
    probs_full = jnp.exp(attn_scores(split_rows, key_valid) - log_total)
    grad_values = jnp.einsum(
        "hqk,qhd->khd",
        probs_full.astype(jnp.bfloat16),
        grad_heads,
        preferred_element_type=jnp.float32,
    )
    grad_probs = jnp.einsum(
        "qhd,khd->hqk", grad_heads, split_rows[:, 2], preferred_element_type=jnp.float32
    )
    grad_scores = (
        probs_full * (grad_probs - jnp.sum(grad_probs * probs_full, -1, keepdims=True))
    ).astype(jnp.bfloat16)
    grad_query = (
        jnp.einsum(
            "hqk,khd->qhd", grad_scores, split_rows[:, 1], preferred_element_type=jnp.float32
        )
        * 0.125
    )
    grad_key = (
        jnp.einsum(
            "hqk,qhd->khd", grad_scores, split_rows[:, 0], preferred_element_type=jnp.float32
        )
        * 0.125
    )
    stacked = jnp.stack([grad_query, grad_key, grad_values], 1).reshape(length, 3 * model_width)
    return stacked.astype(jnp.bfloat16)


def layer_forward(hidden, key_valid, weights):
    gain_attn, qkv_weight, proj_weight, gain_mlp, up_weight, down_weight = weights
    normed_in = normed(hidden, gain_attn).astype(jnp.bfloat16)
    qkv_rows = product(normed_in, qkv_weight).astype(jnp.bfloat16)
    mixed_rows, log_total = attend(qkv_rows, key_valid)
    hidden_mid = hidden + product(mixed_rows, proj_weight)
    mlp_in = normed(hidden_mid, gain_mlp).astype(jnp.bfloat16)
    pre_act = product(mlp_in, up_weight)
    activated = gelu_exact(pre_act).astype(jnp.bfloat16)
    hidden_out = hidden_mid + product(activated, down_weight)
    return (
        hidden_out,
        (
            hidden,
            normed_in,
            qkv_rows,
            log_total,
            mixed_rows,
            hidden_mid,
            mlp_in,
            pre_act,
            activated,
        ),
    )


def empty_kept(length, model_width, hidden_units, head_count):
    return (
        jnp.zeros((length, model_width), jnp.float32),
        jnp.zeros((length, model_width), jnp.bfloat16),
        jnp.zeros((length, 3 * model_width), jnp.bfloat16),
        jnp.zeros((head_count, length, 1), jnp.float32),
        jnp.zeros((length, model_width), jnp.bfloat16),
        jnp.zeros((length, model_width), jnp.float32),
        jnp.zeros((length, model_width), jnp.bfloat16),
        jnp.zeros((length, hidden_units), jnp.float32),
        jnp.zeros((length, hidden_units), jnp.bfloat16),
    )


def layer_backward(kept_vals, grad_out, key_valid, weights):
    hidden, normed_in, qkv_rows, log_total, mixed_rows, hidden_mid, mlp_in, pre_act, activated = (
        kept_vals
    )
    gain_attn, qkv_weight, proj_weight, gain_mlp, up_weight, down_weight = weights
    grad_low = grad_out.astype(jnp.bfloat16)
    grad_activated = product_nt(grad_low, down_weight)
    grad_pre = jax.vjp(gelu_exact, pre_act)[1](grad_activated)[0].astype(jnp.bfloat16)
    grad_mlp_in = product_nt(grad_pre, up_weight)
    grad_mid_norm, grad_gain_mlp = norm_back(hidden_mid, gain_mlp, grad_mlp_in)
    grad_mid = grad_out + grad_mid_norm
    grad_mid_low = grad_mid.astype(jnp.bfloat16)
    grad_mixed = product_nt(grad_mid_low, proj_weight).astype(jnp.bfloat16)
    grad_qkv = attend_back(qkv_rows, key_valid, log_total, grad_mixed)
    grad_normed = product_nt(grad_qkv, qkv_weight)
    grad_in_norm, grad_gain_attn = norm_back(hidden, gain_attn, grad_normed)
    records = (activated, grad_low, mlp_in, grad_pre, mixed_rows, grad_mid_low, normed_in, grad_qkv)
    return (grad_mid + grad_in_norm, (grad_gain_attn, grad_gain_mlp), records)


def layer_zero(length, model_width, hidden_units):
    records = (
        jnp.zeros((length, hidden_units), jnp.bfloat16),
        jnp.zeros((length, model_width), jnp.bfloat16),
        jnp.zeros((length, model_width), jnp.bfloat16),
        jnp.zeros((length, hidden_units), jnp.bfloat16),
        jnp.zeros((length, model_width), jnp.bfloat16),
        jnp.zeros((length, model_width), jnp.bfloat16),
        jnp.zeros((length, model_width), jnp.bfloat16),
        jnp.zeros((length, 3 * model_width), jnp.bfloat16),
    )
    gains = (jnp.zeros((model_width,), jnp.float32), jnp.zeros((model_width,), jnp.float32))
    return (jnp.zeros((length, model_width), jnp.float32), gains, records)


def layer_grads(records):
    activated, grad_low, mlp_in, grad_pre, mixed_rows, grad_mid_low, normed_in, grad_qkv = records
    return (
        product_tn(normed_in, grad_qkv),
        product_tn(mixed_rows, grad_mid_low),
        product_tn(mlp_in, grad_pre),
        product_tn(activated, grad_low),
    )


def embed_inputs(token_ids, noise_block, level_id, table_full):
    noise_level = jnp.exp(LOG_LOW + level_id.astype(jnp.float32) * (LOG_SPAN / (LEVELS - 1)))
    scale_in = lax.rsqrt(EMB_VAR + noise_level * noise_level)
    looked = jnp.take(table_full, token_ids, axis=0).astype(jnp.float32)
    mixed_in = ((looked + noise_level * noise_block.astype(jnp.float32)) * scale_in).astype(
        jnp.bfloat16
    )
    return (mixed_in, scale_in)


def embed_backward(token_ids, noise_block, level_id, grad_start, table_full, in_weight):
    mixed_in, scale_in = embed_inputs(token_ids, noise_block, level_id, table_full)
    grad_low = grad_start.astype(jnp.bfloat16)
    grad_looked = product_nt(grad_low, in_weight) * scale_in
    return (mixed_in, grad_low, grad_looked)


def embed_zero(length, model_width, emb_width):
    return (
        jnp.zeros((length, emb_width), jnp.bfloat16),
        jnp.zeros((length, model_width), jnp.bfloat16),
        jnp.zeros((length, emb_width), jnp.float32),
    )


def tail_pass(hidden, token_ids, key_valid, final_gain, out_weight, table_full, loss_scale):
    final_in = normed(hidden, final_gain).astype(jnp.bfloat16)
    projected = product(final_in, out_weight).astype(jnp.bfloat16)
    logits = product_nt(projected, table_full)
    row_max = jnp.max(logits, -1, keepdims=True)
    log_total = row_max + jnp.log(jnp.sum(jnp.exp(logits - row_max), -1, keepdims=True))
    vocab_ids = lax.broadcasted_iota(jnp.int32, logits.shape, 1)
    target_hit = vocab_ids == token_ids[:, None]
    picked = jnp.sum(jnp.where(target_hit, logits, 0.0), -1)
    entropy = jnp.where(key_valid, log_total[:, 0] - picked, 0.0)
    row_scale = jnp.where(key_valid, loss_scale, 0.0)[:, None]
    grad_logits = (
        (jnp.exp(logits - log_total) - target_hit.astype(jnp.float32)) * row_scale
    ).astype(jnp.bfloat16)
    grad_proj = product(grad_logits, table_full).astype(jnp.bfloat16)
    grad_final = product_nt(grad_proj, out_weight)
    grad_hidden, grad_gain = norm_back(hidden, final_gain, grad_final)
    return (grad_hidden, entropy, grad_gain, (grad_logits, projected, final_in, grad_proj))


def tail_zero(length, model_width, emb_width, vocab_rows):
    records = (
        jnp.zeros((length, vocab_rows), jnp.bfloat16),
        jnp.zeros((length, emb_width), jnp.bfloat16),
        jnp.zeros((length, model_width), jnp.bfloat16),
        jnp.zeros((length, emb_width), jnp.bfloat16),
    )
    return (
        jnp.zeros((length, model_width), jnp.float32),
        jnp.zeros((length,), jnp.float32),
        jnp.zeros((model_width,), jnp.float32),
        records,
    )


def edge_grads(tail_records, embed_records, token_ids):
    grad_logits, projected, final_in, grad_proj = tail_records
    mixed_in, grad_low, grad_looked = embed_records
    table_grad = product_tn(grad_logits, projected).at[token_ids].add(grad_looked)
    return (table_grad, product_tn(mixed_in, grad_low), product_tn(final_in, grad_proj))


def joined_rows(record_list):
    return jax.tree.map(lambda *pieces: jnp.concatenate(pieces, 0), *record_list)


def assemble(gain_attn_sum, gain_mlp_sum, layer_set, edge_set, gain_final_sum):
    return (
        gain_attn_sum[None],
        layer_set[0][None],
        layer_set[1][None],
        gain_mlp_sum[None],
        layer_set[2][None],
        layer_set[3][None],
        edge_set[0],
        edge_set[1],
        gain_final_sum,
        edge_set[2],
    )


def per_device_general(
    tokens,
    lengths,
    levels,
    noise_rows,
    embed_table,
    w_in,
    ln_attn,
    w_qkv,
    w_proj,
    ln_mlp,
    w_up,
    w_down,
    ln_final,
    w_out,
):
    gathered = (
        lax.all_gather(embed_table, "dp", axis=0, tiled=True),
        lax.all_gather(w_in, "dp", axis=0, tiled=True),
        lax.all_gather(ln_attn, "dp", axis=1, tiled=True),
        lax.all_gather(w_qkv, "dp", axis=1, tiled=True),
        lax.all_gather(w_proj, "dp", axis=1, tiled=True),
        lax.all_gather(ln_mlp, "dp", axis=1, tiled=True),
        lax.all_gather(w_up, "dp", axis=1, tiled=True),
        lax.all_gather(w_down, "dp", axis=1, tiled=True),
        lax.all_gather(ln_final, "dp", axis=0, tiled=True),
        lax.all_gather(w_out, "dp", axis=0, tiled=True),
    )
    table_full = gathered[0]
    in_weight = gathered[1]
    layer_weights = (
        gathered[2][0].astype(jnp.float32),
        gathered[3][0],
        gathered[4][0],
        gathered[5][0].astype(jnp.float32),
        gathered[6][0],
        gathered[7][0],
    )
    final_gain = gathered[8].astype(jnp.float32)
    out_weight = gathered[9]
    model_width = out_weight.shape[0]
    emb_width = out_weight.shape[1]
    vocab_rows = table_full.shape[0]
    hidden_units = layer_weights[4].shape[1]
    head_count = model_width // HEAD
    section_index = lax.axis_index("section")
    first_section = section_index == 0
    token_grid = tokens.reshape(MB, LEN)
    noise_grid = noise_rows.reshape(MB, LEN, noise_rows.shape[1])
    positions = jnp.arange(LEN, dtype=jnp.int32)
    valid_grid = positions[None, :] < lengths[:, None]
    loss_scale = LOSS_GAIN / math.sqrt(tokens.shape[0] * lax.axis_size(("group", "dp")))
    gain_attn_sum = jnp.zeros((model_width,), jnp.float32)
    gain_mlp_sum = jnp.zeros((model_width,), jnp.float32)
    gain_final_sum = jnp.zeros((model_width,), jnp.float32)
    recv_act = jnp.zeros((LEN, model_width), jnp.bfloat16)
    recv_grad = jnp.zeros((LEN, model_width), jnp.bfloat16)
    zero_rows = jnp.zeros((LEN, model_width), jnp.float32)
    kept_ticks = {}
    layer_recs = {}
    tail_recs = {}
    embed_recs = {}
    losses = []
    for moment in range(MB + 2):
        offset = moment - section_index
        fwd_valid = (offset >= 0) & (offset < MB)
        fwd_index = jnp.clip(offset, 0, MB - 1)
        ids_now = lax.dynamic_index_in_dim(token_grid, fwd_index, 0, False)
        noise_now = lax.dynamic_index_in_dim(noise_grid, fwd_index, 0, False)
        level_now = lax.dynamic_index_in_dim(levels, fwd_index, 0, False)
        valid_now = lax.dynamic_index_in_dim(valid_grid, fwd_index, 0, False)

        def first_input():
            mixed_in, scale_in = embed_inputs(ids_now, noise_now, level_now, table_full)
            return product(mixed_in, in_weight)

        layer_input = lax.cond(first_section, first_input, lambda: recv_act.astype(jnp.float32))
        hidden_out, kept_now = lax.cond(
            fwd_valid,
            lambda: layer_forward(layer_input, valid_now, layer_weights),
            lambda: (zero_rows, empty_kept(LEN, model_width, hidden_units, head_count)),
        )
        kept_ticks[moment] = kept_now
        tail_live = jnp.logical_not(first_section) & fwd_valid
        tail_grad, entropy, final_step, tail_now = lax.cond(
            tail_live,
            lambda: tail_pass(
                hidden_out, ids_now, valid_now, final_gain, out_weight, table_full, loss_scale
            ),
            lambda: tail_zero(LEN, model_width, emb_width, vocab_rows),
        )
        tail_recs[moment] = tail_now
        gain_final_sum = gain_final_sum + final_step
        back_tick = moment - 2
        late_live = 0 <= back_tick < MB
        late_index = min(max(back_tick, 0), MB - 1)
        kept_late = kept_ticks[back_tick] if back_tick >= 0 else kept_now
        kept_back = lax.cond(first_section, lambda: kept_late, lambda: kept_now)
        grad_top = jnp.where(first_section, recv_grad.astype(jnp.float32), tail_grad)
        valid_back = jnp.where(first_section, valid_grid[late_index], valid_now)
        back_live = jnp.where(first_section, late_live, fwd_valid)
        grad_start, gain_pair, layer_now = lax.cond(
            back_live,
            lambda: layer_backward(kept_back, grad_top, valid_back, layer_weights),
            lambda: layer_zero(LEN, model_width, hidden_units),
        )
        layer_recs[moment] = layer_now
        gain_attn_sum = gain_attn_sum + gain_pair[0]
        gain_mlp_sum = gain_mlp_sum + gain_pair[1]
        if late_live:
            embed_now = lax.cond(
                first_section,
                lambda: embed_backward(
                    token_grid[late_index],
                    noise_grid[late_index],
                    levels[late_index],
                    grad_start,
                    table_full,
                    in_weight,
                ),
                lambda: embed_zero(LEN, model_width, emb_width),
            )
        else:
            embed_now = embed_zero(LEN, model_width, emb_width)
        embed_recs[moment] = embed_now
        if moment < MB:
            recv_act = passed_along(hidden_out.astype(jnp.bfloat16), "section", 1)
        if 1 <= moment <= MB:
            entropy_low = entropy.astype(jnp.bfloat16)
            recv_grad, loss_back = passed_along(
                (grad_start.astype(jnp.bfloat16), entropy_low), "section", -1
            )
            losses.append(jnp.where(first_section, loss_back, entropy_low))
    chosen = [
        jax.tree.map(
            lambda early, late: jnp.where(first_section, early, late),
            layer_recs[micro + 2],
            layer_recs[micro + 1],
        )
        for micro in range(MB)
    ]
    all_layer = layer_grads(joined_rows(chosen))
    all_tail = joined_rows([tail_recs[micro + 1] for micro in range(MB)])
    all_embed = joined_rows([embed_recs[micro + 2] for micro in range(MB)])
    all_edge = edge_grads(all_tail, all_embed, tokens)
    grad_pack = assemble(gain_attn_sum, gain_mlp_sum, all_layer, all_edge, gain_final_sum)
    parted = (
        lax.psum_scatter(
            grad_pack[0].astype(jnp.bfloat16), "dp", scatter_dimension=1, tiled=True
        ).astype(jnp.float32),
        lax.psum_scatter(
            grad_pack[1].astype(jnp.bfloat16), "dp", scatter_dimension=1, tiled=True
        ).astype(jnp.float32),
        lax.psum_scatter(
            grad_pack[2].astype(jnp.bfloat16), "dp", scatter_dimension=1, tiled=True
        ).astype(jnp.float32),
        lax.psum_scatter(
            grad_pack[3].astype(jnp.bfloat16), "dp", scatter_dimension=1, tiled=True
        ).astype(jnp.float32),
        lax.psum_scatter(
            grad_pack[4].astype(jnp.bfloat16), "dp", scatter_dimension=1, tiled=True
        ).astype(jnp.float32),
        lax.psum_scatter(
            grad_pack[5].astype(jnp.bfloat16), "dp", scatter_dimension=1, tiled=True
        ).astype(jnp.float32),
        lax.psum_scatter(
            grad_pack[6].astype(jnp.bfloat16), "dp", scatter_dimension=0, tiled=True
        ).astype(jnp.float32),
        lax.psum_scatter(
            grad_pack[7].astype(jnp.bfloat16), "dp", scatter_dimension=0, tiled=True
        ).astype(jnp.float32),
        lax.psum_scatter(
            grad_pack[8].astype(jnp.bfloat16), "dp", scatter_dimension=0, tiled=True
        ).astype(jnp.float32),
        lax.psum_scatter(
            grad_pack[9].astype(jnp.bfloat16), "dp", scatter_dimension=0, tiled=True
        ).astype(jnp.float32),
    )
    layer_total = (
        lax.psum(parted[0].astype(jnp.bfloat16), "group").astype(jnp.float32),
        lax.psum(parted[1].astype(jnp.bfloat16), "group").astype(jnp.float32),
        lax.psum(parted[2].astype(jnp.bfloat16), "group").astype(jnp.float32),
        lax.psum(parted[3].astype(jnp.bfloat16), "group").astype(jnp.float32),
        lax.psum(parted[4].astype(jnp.bfloat16), "group").astype(jnp.float32),
        lax.psum(parted[5].astype(jnp.bfloat16), "group").astype(jnp.float32),
    )
    edge_total = (
        lax.psum(parted[6].astype(jnp.bfloat16), ("section", "group")).astype(jnp.float32),
        lax.psum(parted[7].astype(jnp.bfloat16), ("section", "group")).astype(jnp.float32),
        lax.psum(parted[8].astype(jnp.bfloat16), ("section", "group")).astype(jnp.float32),
        lax.psum(parted[9].astype(jnp.bfloat16), ("section", "group")).astype(jnp.float32),
    )
    token_loss = jnp.concatenate(losses)
    return (
        token_loss,
        edge_total[0],
        edge_total[1],
        layer_total[0],
        layer_total[1],
        layer_total[2],
        layer_total[3],
        layer_total[4],
        layer_total[5],
        edge_total[2],
        edge_total[3],
    )


MESH = pl.DeviceIdType.MESH
ANYWHERE = pl.BlockSpec(memory_space=pl.ANY)


def pick(index, values):
    out = values[-1]
    for at in range(len(values) - 2, -1, -1):
        out = jnp.where(index == at, values[at], out)
    return out


def rows_at(start, size):
    return pl.ds(pl.multiple_of(start, 8), size)


def remote(src, dst, send_sem, recv_sem, device):
    return pltpu.make_async_remote_copy(
        src_ref=src,
        dst_ref=dst,
        send_sem=send_sem,
        recv_sem=recv_sem,
        device_id=device,
        device_id_type=MESH,
    )


def gather_kernel(count, first_order, last_order, *refs):
    shards = refs[:count]
    wholes = refs[count : 2 * count]
    own_sem, zsend, zrecv, psend, precv, gate = refs[2 * count : 2 * count + 6]
    stage = refs[2 * count + 6 :]
    sec = lax.axis_index("section")
    grp = lax.axis_index("group")
    pos = lax.axis_index("dp")
    beside = ((sec, grp ^ 1, pos), (sec, grp ^ 2, pos))
    above = (sec, grp, pos + 1)
    below = (sec, grp, pos - 1)
    partner = (1 - sec, grp, pos)
    barrier = pltpu.get_barrier_semaphore()
    both = bool(last_order)

    def greet(device):
        pl.semaphore_signal(barrier, inc=1, device_id=device, device_id_type=MESH)

    def meet():
        for device in beside + ((partner,) if both else ()):
            greet(device)

        @pl.when(pos > 0)
        def _():
            greet(below)

        @pl.when(pos < 3)
        def _():
            greet(above)

        at_end = (pos == 0) | (pos == 3)
        pl.semaphore_wait(barrier, jnp.where(at_end, 3, 4) + (1 if both else 0))

    turn = [pick(pos, v) for v in ((3, 1, 3, 1), (2, 3, 1, 2), (1, 2, 2, 3))]

    def run(order, before, middle):
        def rows_of(slot):
            return shards[order[slot][0]].shape[0]

        def part_of(slot):
            _, _, size, whole_line = order[slot]
            return size if whole_line else size // 4

        def shift(slot, who):
            _, lo, _, whole_line = order[slot]
            return lo if whole_line else lo + who * part_of(slot)

        def block(slot, origin, who):
            return rows_at(origin * rows_of(slot) + shift(slot, who), part_of(slot))

        staged = sorted({entry[0] for entry in order})

        def load_own(idx):
            return pltpu.make_async_copy(shards[idx], stage[idx], own_sem.at[idx])

        def store_own(idx):
            rows = shards[idx].shape[0]
            return pltpu.make_async_copy(
                stage[idx], wholes[idx].at[rows_at(pos * rows, rows)], own_sem.at[idx]
            )

        def own_ends(slot):
            idx = order[slot][0]
            src = shards[idx].at[rows_at(shift(slot, grp), part_of(slot))]
            dst = wholes[idx].at[block(slot, pos, grp)]
            return (
                (pos < 3, remote(src, dst, zsend.at[slot, 0], zrecv.at[slot, 1], above)),
                (pos > 0, remote(src, dst, zsend.at[slot, 1], zrecv.at[slot, 3], below)),
            )

        def start_own(slot):
            for goes, copy in own_ends(slot):
                pl.when(goes)(copy.start)

        def origin_of(j):
            return lax.rem(pos - turn[j] + 4, 4)

        def arrived(slot, j):
            here = wholes[order[slot][0]].at[block(slot, origin_of(j), grp)]
            return remote(here, here, zsend.at[slot, 2 + j], zrecv.at[slot, turn[j]], partner)

        def onward(slot, j):
            step = jnp.where(turn[j] <= pos, 1, -1)
            to = pos + step
            here = wholes[order[slot][0]].at[block(slot, origin_of(j), grp)]
            landed = jnp.clip(turn[j] + step, 0, 3)
            copy = remote(
                here,
                here,
                zsend.at[slot, 2 + j],
                zrecv.at[slot, landed],
                (sec, grp, jnp.clip(to, 0, 3)),
            )
            return (to >= 0) & (to <= 3), copy

        def plane(slot, j, way):
            idx = order[slot][0]
            origin = origin_of(j)
            if way < 2:
                here = wholes[idx].at[block(slot, origin, grp)]
                return remote(here, here, psend.at[slot, j, way], precv.at[slot, j, way], beside[way])
            half = shards[idx].shape[1] // 2
            there = wholes[idx].at[
                block(slot, origin, grp ^ (way - 1)), pl.ds(half * (way - 2), half)
            ]
            return remote(
                there, there, psend.at[slot, j, way], precv.at[slot, j, way], beside[3 - way]
            )

        items = [(slot, j) for slot in range(len(order)) for j in range(3)]
        crossing = [item for item in items if not order[item[0]][3]]

        def first(slot, j):
            arrived(slot, j).wait_recv()
            goes, copy = onward(slot, j)
            pl.when(goes)(copy.start)
            if (slot, j) in crossing:
                plane(slot, j, 0).start()
                plane(slot, j, 1).start()

        def second(slot, j):
            if (slot, j) in crossing:
                for way in (0, 1):
                    plane(slot, j, way).wait_recv()
                    plane(slot, j, way + 2).start()

        if before is not None:
            before()
        for slot in range(len(order)):
            start_own(slot)
        for idx in staged:
            load_own(idx).start()
        lag = 2
        for at in range(len(items) + lag):
            if at < len(items):
                slot, j = items[at]
                if j == 2 and slot < len(staged):
                    load_own(staged[slot]).wait()
                    store_own(staged[slot]).start()
                first(slot, j)
            if at == len(items) - 1 and middle is not None:
                middle()
            if at >= lag:
                second(*items[at - lag])
        for slot, j in crossing:
            plane(slot, j, 2).wait_recv()
            plane(slot, j, 3).wait_recv()
        for idx in staged:
            store_own(idx).wait()
        for slot in range(len(order)):
            for goes, copy in own_ends(slot):
                pl.when(goes)(copy.wait_send)
        for slot, j in items:
            goes, copy = onward(slot, j)
            pl.when(goes)(copy.wait_send)
        for slot, j in crossing:
            for way in range(4):
                plane(slot, j, way).wait_send()

    def let_go():
        pl.semaphore_signal(gate, inc=1, device_id=partner, device_id_type=MESH)

    def hold():
        pl.semaphore_wait(gate, 1)

    if both:
        meet()

        @pl.when(sec == 0)
        def _():
            run(first_order, None, let_go)

        @pl.when(sec == 1)
        def _():
            run(last_order, hold, None)

    else:

        @pl.when(sec == 0)
        def _():
            meet()
            run(first_order, None, None)


def gather_all(shards, first_order, last_order, collective_id):
    count = len(shards)
    slots = max(len(first_order), len(last_order))
    return pl.pallas_call(
        functools.partial(gather_kernel, count, first_order, last_order),
        out_shape=[jax.ShapeDtypeStruct((s.shape[0] * 4, s.shape[1]), s.dtype) for s in shards],
        in_specs=[ANYWHERE] * count,
        out_specs=[ANYWHERE] * count,
        scratch_shapes=[
            pltpu.SemaphoreType.DMA((count,)),
            pltpu.SemaphoreType.DMA((slots, 5)),
            pltpu.SemaphoreType.DMA((slots, 4)),
            pltpu.SemaphoreType.DMA((slots, 3, 4)),
            pltpu.SemaphoreType.DMA((slots, 3, 4)),
            pltpu.SemaphoreType.REGULAR,
        ]
        + [pltpu.VMEM(s.shape, s.dtype) for s in shards],
        compiler_params=pltpu.CompilerParams(
            collective_id=collective_id, has_side_effects=True, vmem_limit_bytes=60 << 20
        ),
    )(*shards)


def swap_kernel(rows_ref, ids_ref, out_ref, ids_out, own_sem, send_sem, recv_sem):
    sec = lax.axis_index("section")
    grp = lax.axis_index("group")
    pos = lax.axis_index("dp")

    @pl.when(sec == 0)
    def _():
        barrier = pltpu.get_barrier_semaphore()
        peers = [(sec, grp, lax.rem(pos + k, 4)) for k in (1, 2, 3)]
        sides = [(sec, grp ^ j, pos) for j in (1, 2, 3)]
        for device in peers + sides:
            pl.semaphore_signal(barrier, inc=1, device_id=device, device_id_type=MESH)
        pl.semaphore_wait(barrier, 6)
        copies = []
        for k, device in enumerate(peers):
            copies.append(
                remote(rows_ref.at[device[2]], out_ref.at[pos], send_sem.at[k], recv_sem.at[k], device)
            )
        for k, device in enumerate(sides):
            copies.append(
                remote(ids_ref, ids_out.at[grp], send_sem.at[3 + k], recv_sem.at[3 + k], device)
            )
        for copy in copies:
            copy.start()
        own_rows = pltpu.make_async_copy(rows_ref.at[pos], out_ref.at[pos], own_sem.at[0])
        own_ids = pltpu.make_async_copy(ids_ref, ids_out.at[grp], own_sem.at[1])
        own_rows.start()
        own_ids.start()
        own_rows.wait()
        own_ids.wait()
        for copy in copies:
            copy.wait()


def swap_rows(rows, ids, collective_id):
    in_vmem = pl.BlockSpec(memory_space=pltpu.VMEM)
    return pl.pallas_call(
        swap_kernel,
        out_shape=[
            jax.ShapeDtypeStruct(rows.shape, rows.dtype),
            jax.ShapeDtypeStruct((4,) + ids.shape, ids.dtype),
        ],
        in_specs=[in_vmem] * 2,
        out_specs=[in_vmem] * 2,
        scratch_shapes=[
            pltpu.SemaphoreType.DMA((2,)),
            pltpu.SemaphoreType.DMA((6,)),
            pltpu.SemaphoreType.DMA((6,)),
        ],
        compiler_params=pltpu.CompilerParams(collective_id=collective_id, has_side_effects=True),
    )(rows, ids)


IN_VMEM = pl.BlockSpec(memory_space=pltpu.VMEM)
IN_SMEM = pl.BlockSpec(memory_space=pltpu.SMEM)
ROOT_HALF = 0.7071067811865476
ROOT_TWO_PI = 0.3989422804014327


def dot_nn(left, right):
    return lax.dot_general(
        left, right, (((1,), (0,)), ((), ())), preferred_element_type=jnp.float32
    )


def dot_nt(left, right):
    return lax.dot_general(
        left, right, (((1,), (1,)), ((), ())), preferred_element_type=jnp.float32
    )


def dot_tn(left, right):
    return lax.dot_general(
        left, right, (((0,), (0,)), ((), ())), preferred_element_type=jnp.float32
    )


def unit_rows(v):
    center = v - jnp.mean(v, -1, keepdims=True)
    scale = lax.rsqrt(jnp.mean(center * center, -1, keepdims=True) + EPS)
    return center * scale, scale


def split_heads(pair):
    low = lax.broadcasted_iota(jnp.int32, pair.shape, 1) < HEAD
    nothing = jnp.zeros_like(pair)
    return jnp.concatenate([jnp.where(low, pair, nothing), jnp.where(low, nothing, pair)], 0)


def join_heads(stacked):
    half = stacked.shape[0] // 2
    low = lax.broadcasted_iota(jnp.int32, (half, stacked.shape[1]), 1) < HEAD
    return jnp.where(low, stacked[:half], stacked[half:])


def pair_scores(keys, stacked_queries, key_count):
    scores = dot_nt(keys, stacked_queries) * 0.125
    valid = lax.broadcasted_iota(jnp.int32, scores.shape, 0) < key_count
    return jnp.where(valid, scores, MASKED)


STRIP = 64


def forward_kernel(only, tile, given, *refs):
    x, gain_attn, gain_mlp, counts, wq, wp, wu, wd = refs[:8]
    rest = refs[8 + given :]
    outs = rest[:KEPT_COUNT]
    qv, pv, uv, dv = rest[KEPT_COUNT : KEPT_COUNT + 4]
    kept = rest[KEPT_COUNT + 4 : 2 * KEPT_COUNT + 4]
    a, att, m, acc, wsem, osem = rest[2 * KEPT_COUNT + 4 :]
    xv, at_t, qkv, lse, att_t, mid, m_t, pre, act_t, out = kept
    rows, width = a.shape
    units = dv.shape[0]

    def store(idx):
        return pltpu.make_async_copy(kept[idx], outs[idx], osem.at[idx])

    def run():
        loads = []

        def load(src, dst):
            copy = pltpu.make_async_copy(src, dst, wsem.at[len(loads)])
            copy.start()
            loads.append(copy)

        for lo in range(0, 3 * width, tile):
            load(wq.at[:, pl.ds(lo, tile)], qv.at[:, pl.ds(lo, tile)])
        load(wp, pv)
        for lo in range(0, units, tile):
            load(wu.at[:, pl.ds(lo, tile)], uv.at[:, pl.ds(lo, tile)])
            load(wd.at[pl.ds(lo, tile)], dv.at[pl.ds(lo, tile)])
        loads = iter(loads)
        for lo in range(0, rows, STRIP):
            here = pl.ds(lo, STRIP)
            xv[here, :] = x[here, :].astype(jnp.float32)
            a[here, :] = (unit_rows(xv[here, :])[0] * gain_attn[...]).astype(jnp.bfloat16)
        store(0).start()
        for lo in range(0, 3 * width, tile):
            next(loads).wait()
            cols = pl.ds(lo, tile)
            qkv[:, cols] = dot_nn(a[...], qv[:, cols]).astype(jnp.bfloat16)
        store(2).start()
        for lo in range(0, width, 256):
            at_t[pl.ds(lo, 256), :] = a[:, pl.ds(lo, 256)].T
        store(1).start()
        pairs = width // 128
        for seq in range(rows // LEN):
            here = pl.ds(seq * LEN, LEN)
            for pair in range(pairs):
                stacked = split_heads(qkv[here, pl.ds(pair * 128, 128)])
                scores = pair_scores(qkv[here, pl.ds(width + pair * 128, 128)], stacked, counts[seq])
                top = jnp.max(scores, 0, keepdims=True)
                power = jnp.exp(scores - top)
                total = jnp.sum(power, 0, keepdims=True)
                lse[seq * pairs + pair] = top + jnp.log(total)
                probs = (power * (1.0 / total)).astype(jnp.bfloat16)
                mixed = dot_tn(probs, qkv[here, pl.ds(2 * width + pair * 128, 128)])
                att[here, pl.ds(pair * 128, 128)] = join_heads(mixed).astype(jnp.bfloat16)
        store(3).start()
        for lo in range(0, width, 256):
            att_t[pl.ds(lo, 256), :] = att[:, pl.ds(lo, 256)].T
        store(4).start()
        next(loads).wait()
        for lo in range(0, width, tile):
            cols = pl.ds(lo, tile)
            mid[:, cols] = xv[:, cols] + dot_nn(att[...], pv[:, cols])
        for lo in range(0, rows, STRIP):
            here = pl.ds(lo, STRIP)
            m[here, :] = (unit_rows(mid[here, :])[0] * gain_mlp[...]).astype(jnp.bfloat16)
        store(5).start()
        acc[...] = mid[...]
        for lo in range(0, units, tile):
            cols = pl.ds(lo, tile)
            next(loads).wait()
            before = dot_nn(m[...], uv[:, cols])
            pre[:, cols] = before
            active = (0.5 * before * (1.0 + lax.erf(before * ROOT_HALF))).astype(jnp.bfloat16)
            act_t[cols, :] = active.T
            next(loads).wait()
            acc[...] += dot_nn(active, dv[cols, :])
        store(7).start()
        store(8).start()
        for lo in range(0, width, 256):
            m_t[pl.ds(lo, 256), :] = m[:, pl.ds(lo, 256)].T
        store(6).start()
        out[...] = acc[...]
        store(9).start()
        for idx in range(KEPT_COUNT):
            store(idx).wait()

    pl.when(lax.axis_index("section") == only)(run)


KEPT_COUNT = 10


def kept_shapes(rows, width, units):
    f32, low = jnp.float32, jnp.bfloat16
    return [
        jax.ShapeDtypeStruct(shape, kind)
        for shape, kind in (
            ((rows, width), f32),
            ((width, rows), low),
            ((rows, 3 * width), low),
            ((rows // LEN * width // 128, 1, 2 * LEN), f32),
            ((width, rows), low),
            ((rows, width), f32),
            ((width, rows), low),
            ((rows, units), f32),
            ((units, rows), low),
            ((rows, width), f32),
        )
    ]


def run_forward(only, x, gain_attn, gain_mlp, counts, weights, kept):
    wq, wp, wu, wd = weights
    rows, width = x.shape
    units = wd.shape[0]
    tile = 512
    shapes = kept_shapes(rows, width, units)
    low = jnp.bfloat16
    given = 0 if kept is None else KEPT_COUNT
    in_specs = [IN_VMEM] * 3 + [IN_SMEM] + [ANYWHERE] * (4 + given)
    return pl.pallas_call(
        functools.partial(forward_kernel, only, tile, given),
        out_shape=shapes,
        in_specs=in_specs,
        out_specs=[ANYWHERE] * KEPT_COUNT,
        input_output_aliases={8 + idx: idx for idx in range(given)},
        scratch_shapes=[pltpu.VMEM(w.shape, w.dtype) for w in weights]
        + [pltpu.VMEM(s.shape, s.dtype) for s in shapes]
        + [
            pltpu.VMEM((rows, width), low),
            pltpu.VMEM((rows, width), low),
            pltpu.VMEM((rows, width), low),
            pltpu.VMEM((rows, width), jnp.float32),
            pltpu.SemaphoreType.DMA((3 * width // tile + 1 + 2 * units // tile,)),
            pltpu.SemaphoreType.DMA((KEPT_COUNT,)),
        ],
        compiler_params=pltpu.CompilerParams(vmem_limit_bytes=56 << 20),
    )(x, gain_attn, gain_mlp, counts, wq, wp, wu, wd, *(kept or ()))


GRAD_COUNT = 6


def grad_shapes(rows, width, units):
    f32, low = jnp.float32, jnp.bfloat16
    return [
        jax.ShapeDtypeStruct(shape, kind)
        for shape, kind in (
            ((rows, width), low),
            ((rows, units), low),
            ((rows, width), low),
            ((rows, 3 * width), low),
            ((rows, width), low),
            ((8, width), f32),
        )
    ]


def norm_pull(v, gain, upstream):
    unit, scale = unit_rows(v)
    pulled = upstream * gain
    inner = jnp.mean(pulled * unit, -1, keepdims=True)
    grad = (pulled - jnp.mean(pulled, -1, keepdims=True) - unit * inner) * scale
    return grad, jnp.sum(upstream * unit, 0, keepdims=True)


def backward_kernel(only, tile, given, *refs):
    grad, gain_attn, gain_mlp, counts, x_in, qkv_in, lse_in, mid_in, pre_in, wq, wp, wu, wd = refs[:13]
    rest = refs[13 + given :]
    outs = rest[:GRAD_COUNT]
    qv, pv, uv, dv = rest[GRAD_COUNT : GRAD_COUNT + 4]
    made = rest[GRAD_COUNT + 4 : 2 * GRAD_COUNT + 4]
    x, qkv, lse, mid, pre, gm, gmid, gatt, wsem, ksem, osem = rest[2 * GRAD_COUNT + 4 :]
    gy, gpre, gz, gqkv, gx, gains = made
    rows, width = gm.shape
    units = dv.shape[0]

    def store(idx):
        return pltpu.make_async_copy(made[idx], outs[idx], osem.at[idx])

    def run():
        loads = []

        def load(src, dst):
            copy = pltpu.make_async_copy(src, dst, wsem.at[len(loads)])
            copy.start()
            loads.append(copy)

        kept = [
            pltpu.make_async_copy(src, dst, ksem.at[idx])
            for idx, (src, dst) in enumerate(
                ((pre_in, pre), (mid_in, mid), (qkv_in, qkv), (lse_in, lse), (x_in, x))
            )
        ]
        kept[0].start()
        for lo in range(0, units, tile):
            load(wd.at[pl.ds(lo, tile)], dv.at[pl.ds(lo, tile)])
            load(wu.at[:, pl.ds(lo, tile)], uv.at[:, pl.ds(lo, tile)])
        for copy in kept[1:]:
            copy.start()
        load(wp, pv)
        load(wq, qv)
        loads = iter(loads)
        gy[...] = grad[...].astype(jnp.bfloat16)
        store(0).start()
        gains[...] = jnp.zeros_like(gains)
        kept[0].wait()
        gm[...] = jnp.zeros_like(gm)
        for lo in range(0, units, tile):
            cols = pl.ds(lo, tile)
            next(loads).wait()
            pulled = dot_nt(gy[...], dv[cols, :])
            before = pre[:, cols]
            slope = 0.5 * (1.0 + lax.erf(before * ROOT_HALF)) + before * (
                ROOT_TWO_PI * jnp.exp(-0.5 * before * before)
            )
            low = (pulled * slope).astype(jnp.bfloat16)
            gpre[:, cols] = low
            next(loads).wait()
            gm[...] += dot_nt(low, uv[:, cols])
        store(1).start()
        kept[1].wait()
        for lo in range(0, rows, STRIP):
            here = pl.ds(lo, STRIP)
            step, gain = norm_pull(mid[here, :], gain_mlp[...], gm[here, :])
            total = grad[here, :].astype(jnp.float32) + step
            gmid[here, :] = total
            gz[here, :] = total.astype(jnp.bfloat16)
            gains[1:2, :] += gain
        store(2).start()
        next(loads).wait()
        gatt[...] = dot_nt(gz[...], pv[...]).astype(jnp.bfloat16)
        kept[2].wait()
        kept[3].wait()
        pairs = width // 128
        for seq in range(rows // LEN):
            here = pl.ds(seq * LEN, LEN)
            for pair in range(pairs):
                own = pl.ds(pair * 128, 128)
                stacked = split_heads(qkv[here, own])
                pulled = split_heads(gatt[here, own])
                keys = qkv[here, pl.ds(width + pair * 128, 128)]
                values = qkv[here, pl.ds(2 * width + pair * 128, 128)]
                probs = jnp.exp(pair_scores(keys, stacked, counts[seq]) - lse[seq * pairs + pair])
                gprobs = dot_nt(values, pulled)
                inner = jnp.sum(probs * gprobs, 0, keepdims=True)
                gscores = (probs * (gprobs - inner)).astype(jnp.bfloat16)
                gqkv[here, own] = (join_heads(dot_tn(gscores, keys)) * 0.125).astype(jnp.bfloat16)
                gqkv[here, pl.ds(width + pair * 128, 128)] = (dot_nn(gscores, stacked) * 0.125).astype(
                    jnp.bfloat16
                )
                gqkv[here, pl.ds(2 * width + pair * 128, 128)] = dot_nn(
                    probs.astype(jnp.bfloat16), pulled
                ).astype(jnp.bfloat16)
        store(3).start()
        next(loads).wait()
        for lo in range(0, width, 256):
            gm[:, pl.ds(lo, 256)] = dot_nt(gqkv[...], qv[pl.ds(lo, 256), :])
        kept[4].wait()
        for lo in range(0, rows, STRIP):
            here = pl.ds(lo, STRIP)
            step, gain = norm_pull(x[here, :], gain_attn[...], gm[here, :])
            gx[here, :] = (gmid[here, :] + step).astype(jnp.bfloat16)
            gains[0:1, :] += gain
        store(4).start()
        store(5).start()
        for idx in range(GRAD_COUNT):
            store(idx).wait()

    pl.when(lax.axis_index("section") == only)(run)


def run_backward(only, grad, gain_attn, gain_mlp, counts, kept, weights, made):
    wq, wp, wu, wd = weights
    x, _, qkv, lse, _, mid, _, pre, _, _ = kept
    rows, width = x.shape
    units = wd.shape[0]
    tile = 512
    shapes = grad_shapes(rows, width, units)
    low, f32 = jnp.bfloat16, jnp.float32
    given = 0 if made is None else GRAD_COUNT
    in_specs = [IN_VMEM] * 3 + [IN_SMEM] + [ANYWHERE] * (9 + given)
    return pl.pallas_call(
        functools.partial(backward_kernel, only, tile, given),
        out_shape=shapes,
        in_specs=in_specs,
        out_specs=[ANYWHERE] * GRAD_COUNT,
        input_output_aliases={13 + idx: idx for idx in range(given)},
        scratch_shapes=[pltpu.VMEM(w.shape, w.dtype) for w in weights]
        + [pltpu.VMEM(s.shape, s.dtype) for s in shapes]
        + [pltpu.VMEM(s.shape, s.dtype) for s in (x, qkv, lse, mid, pre)]
        + [
            pltpu.VMEM((rows, width), f32),
            pltpu.VMEM((rows, width), f32),
            pltpu.VMEM((rows, width), low),
            pltpu.SemaphoreType.DMA((2 + 2 * units // tile,)),
            pltpu.SemaphoreType.DMA((5,)),
            pltpu.SemaphoreType.DMA((GRAD_COUNT,)),
        ],
        compiler_params=pltpu.CompilerParams(vmem_limit_bytes=56 << 20),
    )(grad, gain_attn, gain_mlp, counts, x, qkv, lse, mid, pre, wq, wp, wu, wd, *(made or ()))


def vocabulary_kernel(only, tile, proj, ids, scale, table, gproj_out, loss_out, gtable, tv, gt, gp, tsem, gsem):
    rows, emb = proj.shape
    vocab = tv.shape[0]
    count = vocab // tile

    def run():
        for at in range(count):
            here = pl.ds(at * tile, tile)
            pltpu.make_async_copy(table.at[here], tv.at[here], tsem.at[at]).start()

        def logits_of(at):
            return dot_nt(tv[rows_at(at * tile, tile), :], proj[...])

        def hits_of(at):
            names = lax.broadcasted_iota(jnp.int32, (tile, rows), 0) + at * tile
            return names == ids[...]

        def stats(at, carry):
            top, total, picked = carry
            here = rows_at(at * tile, tile)
            pltpu.make_async_copy(table.at[here], tv.at[here], tsem.at[at]).wait()
            logits = logits_of(at)
            higher = jnp.maximum(top, jnp.max(logits, 0, keepdims=True))
            total = total * jnp.exp(top - higher) + jnp.sum(jnp.exp(logits - higher), 0, keepdims=True)
            picked = picked + jnp.sum(jnp.where(hits_of(at), logits, 0.0), 0, keepdims=True)
            return higher, total, picked

        start = (
            jnp.full((1, rows), MASKED, jnp.float32),
            jnp.zeros((1, rows), jnp.float32),
            jnp.zeros((1, rows), jnp.float32),
        )
        top, total, picked = lax.fori_loop(0, count, stats, start)
        log_total = top + jnp.log(total)
        loss_out[...] = jnp.where(scale[...] > 0, log_total - picked, 0.0)
        gp[...] = jnp.zeros_like(gp)

        def gstore(at):
            return pltpu.make_async_copy(
                gt.at[rows_at(at * tile, tile)], gtable.at[rows_at(at * tile, tile)], gsem.at[at]
            )

        def pull(at, carry):
            here = rows_at(at * tile, tile)
            probs = jnp.exp(logits_of(at) - log_total)
            grads = ((probs - jnp.where(hits_of(at), 1.0, 0.0)) * scale[...]).astype(jnp.bfloat16)
            gp[...] += dot_tn(grads, tv[here, :])
            gt[here, :] = dot_nn(grads, proj[...]).astype(jnp.bfloat16)
            gstore(at).start()
            return carry

        lax.fori_loop(0, count, pull, 0)
        gproj_out[...] = gp[...].astype(jnp.bfloat16)

        def done(at, carry):
            gstore(at).wait()
            return carry

        lax.fori_loop(0, count, done, 0)

    pl.when(lax.axis_index("section") == only)(run)


def run_vocabulary(only, proj, ids, scale, table):
    rows, emb = proj.shape
    vocab = table.shape[0]
    tile = 1024
    return pl.pallas_call(
        functools.partial(vocabulary_kernel, only, tile),
        out_shape=[
            jax.ShapeDtypeStruct((rows, emb), jnp.bfloat16),
            jax.ShapeDtypeStruct((1, rows), jnp.float32),
            jax.ShapeDtypeStruct(table.shape, jnp.bfloat16),
        ],
        in_specs=[IN_VMEM] * 3 + [ANYWHERE],
        out_specs=[IN_VMEM] * 2 + [ANYWHERE],
        scratch_shapes=[
            pltpu.VMEM(table.shape, table.dtype),
            pltpu.VMEM(table.shape, jnp.bfloat16),
            pltpu.VMEM((rows, emb), jnp.float32),
            pltpu.SemaphoreType.DMA((vocab // tile,)),
            pltpu.SemaphoreType.DMA((vocab // tile,)),
        ],
        compiler_params=pltpu.CompilerParams(vmem_limit_bytes=40 << 20),
    )(proj, ids, scale, table)


def strip_of(rows, columns):
    strip = 16
    while 2 * strip * columns <= 65536 and rows % (2 * strip) == 0:
        strip = 2 * strip
    return strip


def add_rows(store, terms, rows, columns):
    strip = strip_of(rows, columns)

    def body(at, carry):
        here = rows_at(at * strip, strip)
        total = terms[0](here).astype(jnp.float32)
        for term in terms[1:]:
            total = total + term(here).astype(jnp.float32)
        store(here, total)
        return carry

    lax.fori_loop(0, rows // strip, body, 0)


def reduce_kernel(plan, spots, only, extras, ahead, refs_of, *refs):
    body = functools.partial(reduce_body, plan, spots, extras, ahead, refs_of(refs))
    if only is None:
        body()
    else:
        pl.when(lax.axis_index("section") == only)(body)


def reduce_body(plan, spots, extras, ahead, named):
    arrays, outs = named["arrays"], named["outs"]
    own, got1, got2, got3, land = (named[k] for k in ("own", "got1", "got2", "got3", "land"))
    s1, r1, own_sem, s2, r2, s3, r3, s4, r4, fin_sem = named["sems"]
    count = len(plan)
    sec = lax.axis_index("section")
    grp = lax.axis_index("group")
    pos = lax.axis_index("dp")
    beside = ((sec, grp ^ 1, pos), (sec, grp ^ 2, pos))
    sides = [(sec, grp ^ j, pos) for j in (1, 2, 3)]
    line_peers = [(sec, grp, lax.rem(pos + k, 4)) for k in (1, 2, 3)]
    steps = [(jg, jz) for jg in range(4) for jz in range(4)][1:]

    def other(j):
        return (sec, grp ^ steps[j][0], lax.rem(pos + steps[j][1], 4))

    with_gains = "gains" in extras
    spreads = "spread" in extras
    looked = "looked" in extras
    peers = [other(j) for j in range(15)] if with_gains else sides + line_peers
    barrier = pltpu.get_barrier_semaphore()
    for device in peers:
        pl.semaphore_signal(barrier, inc=1, device_id=device, device_id_type=MESH)
    pl.semaphore_wait(barrier, len(peers))

    def rows_of(p):
        return arrays[plan[p][0]].shape[0] // 4

    def columns_of(p):
        return arrays[plan[p][0]].shape[1]

    def sub_of(p):
        return rows_of(p) // 4 // plan[p][3]

    def block(p, line, who):
        start = line * rows_of(p) + who * (rows_of(p) // 4) + plan[p][2] * sub_of(p)
        return arrays[plan[p][0]].at[rows_at(start, sub_of(p))]

    def ways(line):
        return (0, 1) if line < 2 else (1, 0)

    def send_first(p, line, b):
        first, second = ways(line)
        who = grp ^ (1 + first)
        if b:
            who = who ^ (1 + second)
        return remote(
            block(p, line, who),
            got1[p].at[line, b],
            s1.at[p, line, b],
            r1.at[p, line, b],
            beside[first],
        )

    def load_own(p, line, b):
        who = grp ^ (1 + ways(line)[1]) if b else grp
        return pltpu.make_async_copy(block(p, line, who), own[p].at[line, b], own_sem.at[p, line, b])

    def send_second(p, line):
        second = ways(line)[1]
        return remote(own[p].at[line, 1], got2[p].at[line], s2.at[p, line], r2.at[p, line], beside[second])

    def send_line(p, line):
        slot = jnp.maximum(lax.rem(line - pos + 4, 4) - 1, 0)
        return remote(
            own[p].at[line, 0], got3[p].at[slot], s3.at[p, line], r3.at[p, slot], (sec, grp, line)
        )

    def line_arrival(p, slot):
        return remote(got3[p].at[slot], got3[p].at[slot], s3.at[p, slot], r3.at[p, slot], beside[0])

    def begin(p, line):
        for b in (1, 0):
            send_first(p, line, b).start()
            load_own(p, line, b).start()

    def middle(p, line):
        for b in (1, 0):
            load_own(p, line, b).wait()
            send_first(p, line, b).wait_recv()

            def store(here, total, b=b):
                own[p][line, b, here, :] = total.astype(jnp.bfloat16)

            add_rows(
                store,
                [
                    lambda here, b=b: own[p][line, b, here, :],
                    lambda here, b=b: got1[p][line, b, here, :],
                ],
                sub_of(p),
                columns_of(p),
            )
            if b:
                send_second(p, line).start()

    def late(p, line):
        send_second(p, line).wait_recv()

        def store(here, total):
            own[p][line, 0, here, :] = total.astype(jnp.bfloat16)

        add_rows(
            store,
            [lambda here: own[p][line, 0, here, :], lambda here: got2[p][line, here, :]],
            sub_of(p),
            columns_of(p),
        )
        pl.when(line != pos)(send_line(p, line).start)

    pending = {}

    def write_out(p, who, term):
        rings = named["rings"][spots[p]]
        turn = pending.setdefault(spots[p], [])
        slot = len(turn) % 2
        if len(turn) >= 2:
            turn[-2].wait()
        ring = rings.at[slot]

        def store(here, total):
            rings[slot, here, :] = total

        add_rows(store, term, sub_of(p), columns_of(p))
        start = who * (rows_of(p) // 4) + plan[p][2] * sub_of(p)
        copy = pltpu.make_async_copy(
            ring, outs[plan[p][0]].at[rows_at(start, sub_of(p))], named["ring_sem"].at[spots[p], slot]
        )
        copy.start()
        turn.append(copy)

    def drain():
        for turn in pending.values():
            for copy in turn[-2:]:
                copy.wait()

    def spread(p, way):
        if way < 2:
            here = land[p].at[grp]
            return remote(here, here, s4.at[p, way], r4.at[p, way], beside[way])
        half = columns_of(p) // 2
        there = land[p].at[grp ^ (way - 1), :, pl.ds(half * (way - 2), half)]
        return remote(there, there, s4.at[p, way], r4.at[p, way], beside[3 - way])

    def settle(p, terms):
        def store(here, total):
            land[p][grp, here, :] = total.astype(jnp.bfloat16)

        add_rows(store, terms, sub_of(p), columns_of(p))
        if spreads:
            spread(p, 0).start()
            spread(p, 1).start()
        else:
            own_out(p).start()

    def own_out(p):
        return pltpu.make_async_copy(
            land[p].at[grp], outs[plan[p][0]].at[rows_at(plan[p][2] * sub_of(p), sub_of(p))], fin_sem.at[p]
        )

    def arrival(p, way):
        who = (grp ^ 1, grp ^ 2)[way]
        return remote(land[p].at[who], land[p].at[who], s4.at[p, way], r4.at[p, way], beside[way])

    def finish(p):
        for slot in range(3):
            line_arrival(p, slot).wait_recv()
        settle(
            p,
            [lambda here: own[p][pos, 0, here, :]]
            + [lambda here, slot=slot: got3[p][slot, here, :] for slot in range(3)],
        )

    def pass_on(p):
        if spreads:
            for way in (0, 1):
                arrival(p, way).wait_recv()
                spread(p, way + 2).start()

    def write_near(p):
        if spreads:
            for who in (grp, grp ^ 1, grp ^ 2):
                write_out(p, who, [lambda here, who=who: land[p][who, here, :]])

    def write_far(p):
        if spreads:
            spread(p, 2).wait_recv()
            spread(p, 3).wait_recv()
            write_out(p, grp ^ 3, [lambda here: land[p][grp ^ 3, here, :]])

    def line_rows(p, line):
        return arrays[plan[p][0]].at[rows_at(line * rows_of(p), rows_of(p))]

    def line_first(p, k):
        to = lax.rem(pos + k, 4)
        return remote(
            line_rows(p, to), got1[p].at[k - 1], s1.at[p, k, 0], r1.at[p, k, 0], (sec, grp, to)
        )

    def line_own(p):
        return pltpu.make_async_copy(line_rows(p, pos), own[p], own_sem.at[p, 0, 0])

    def cross(p, j):
        to = grp ^ j
        return remote(
            own[p].at[rows_at(to * sub_of(p), sub_of(p))],
            got3[p].at[j - 1],
            s3.at[p, j],
            r3.at[p, j - 1],
            (sec, to, pos),
        )

    def line_begin(p):
        for k in (2, 1, 3):
            line_first(p, k).start()
        line_own(p).start()

    def line_middle(p):
        line_own(p).wait()
        for k in (1, 2, 3):
            line_first(p, k).wait_recv()

        def store(here, total):
            own[p][here, :] = total.astype(jnp.bfloat16)

        add_rows(
            store,
            [lambda here: own[p][here, :]] + [lambda here, k=k: got1[p][k, here, :] for k in range(3)],
            rows_of(p),
            columns_of(p),
        )
        for j in (3, 1, 2):
            cross(p, j).start()

    def line_finish(p):
        for j in (1, 2, 3):
            cross(p, j).wait_recv()
        base = grp * sub_of(p)
        strip = strip_of(sub_of(p), columns_of(p))
        settle(
            p,
            [lambda here: own[p][rows_at(base + here.start, strip), :]]
            + [lambda here, j=j: got3[p][j, here, :] for j in range(3)],
        )

    if with_gains:
        gain_in, gain_got, sg, rg, gain_sem = named["gain_scratch"]

        def gain_copy(j):
            device = other(j)
            return remote(gain_in.at[device[2]], gain_got.at[j], sg.at[j], rg.at[j], device)

        gain_load = pltpu.make_async_copy(named["gains"], gain_in, gain_sem)
        gain_load.start()

    if looked:
        looks, looks_own, sl, rl, table_fin, tland, tsum = named["look_scratch"]
        ids, look_in, fin_in = named["look_in"]
        vocab_quarter = fin_in.shape[0]
        look_load = pltpu.make_async_copy(look_in, looks.at[grp, pos], looks_own.at[0])
        fin_load = pltpu.make_async_copy(fin_in, table_fin, looks_own.at[1])

        def look_line(k):
            here = looks.at[grp, pos]
            return remote(here, here, sl.at[k], rl.at[k], line_peers[k])

        def look_side(k):
            here = looks.at[grp]
            return remote(here, here, sl.at[3 + k], rl.at[3 + k], sides[k])

        def table_spread(way):
            if way < 2:
                here = tland.at[grp]
                return remote(here, here, sl.at[6 + way], rl.at[6 + way], beside[way])
            half = tland.shape[2] // 2
            there = tland.at[grp ^ (way - 1), :, pl.ds(half * (way - 2), half)]
            return remote(there, there, sl.at[6 + way], rl.at[6 + way], beside[3 - way])

        def table_out(who):
            return pltpu.make_async_copy(
                tland.at[who],
                named["table_out"].at[rows_at(who * vocab_quarter, vocab_quarter)],
                looks_own.at[2 + who],
            )

        def look_begin():
            look_load.start()
            fin_load.start()
            look_load.wait()
            for k in range(3):
                look_line(k).start()

        def look_middle():
            for k in range(3):
                look_line(k).wait_recv()
            for k in range(3):
                look_side(k).start()

        def look_sum():
            for k in range(3):
                look_side(k).wait_recv()
            fin_load.wait()
            base = pos * (4 * vocab_quarter) + grp * vocab_quarter
            tall = 256
            names = lax.broadcasted_iota(jnp.int32, (tall, ids.shape[2]), 0)

            def body(at, carry):
                here = rows_at(at * tall, tall)
                total = table_fin[here, :].astype(jnp.float32)
                for g in range(4):
                    for z in range(4):
                        hit = names + (base + at * tall) == ids[g * 4 + z]
                        total = total + dot_nn(
                            jnp.where(hit, 1.0, 0.0).astype(jnp.bfloat16), looks[g, z]
                        )
                tland[grp, here, :] = total.astype(jnp.bfloat16)
                return carry

            lax.fori_loop(0, vocab_quarter // tall, body, 0)
            table_spread(0).start()
            table_spread(1).start()

        def look_pass():
            for way in (0, 1):
                who = (grp ^ 1, grp ^ 2)[way]
                remote(
                    tland.at[who], tland.at[who], sl.at[6 + way], rl.at[6 + way], beside[way]
                ).wait_recv()
                table_spread(way + 2).start()

        def look_end():
            table_spread(2).wait_recv()
            table_spread(3).wait_recv()
            for who in range(4):
                table_out(who).start()
            for who in range(4):
                table_out(who).wait()
            for k in range(3):
                look_line(k).wait_send()
                look_side(k).wait_send()
            for way in range(4):
                table_spread(way).wait_send()

        def on_first(run):
            pl.when(sec == 0)(run)

    else:

        def on_first(run):
            pass

        look_begin = look_middle = look_sum = look_pass = look_end = None

    planes = [p for p in range(count) if plan[p][1] == "plane"]
    lines = [p for p in range(count) if plan[p][1] == "line"]
    units = [(p, line) for p in planes for line in (0, 2, 1, 3)]
    for unit in units[:2]:
        begin(*unit)
    for p in lines:
        line_begin(p)
    on_first(look_begin)
    for unit in units[2:ahead]:
        begin(*unit)
    if with_gains:
        gain_load.wait()
        for j in range(15):
            gain_copy(j).start()
    lag = 3
    total_steps = len(units) + lag
    done = []
    for at in range(total_steps):
        if at + ahead < len(units):
            begin(*units[at + ahead])
        if at < len(units):
            middle(*units[at])
        if at >= lag:
            p, line = units[at - lag]
            late(p, line)
            if line == 1 and len(done) >= 1:
                finish(done[-1])
            if line == 2 and len(done) >= 2:
                pass_on(done[-2])
            if line == 0 and len(done) >= 3:
                write_near(done[-3])
            if line == 3:
                done.append(p)
        if at == len(units) // 4:
            on_first(look_middle)
        if at == len(units) // 2:
            on_first(look_sum)
        if at == 3 * len(units) // 4:
            on_first(look_pass)
    for p in lines:
        line_middle(p)
    finish(done[-1])
    written = max(len(done) - 3, 0)
    passed = max(len(done) - 2, 0)
    for p in done[passed:]:
        pass_on(p)
    for p in lines:
        line_finish(p)
    for p in done[written:]:
        write_near(p)
    for p in lines:
        pass_on(p)
    for p in done:
        write_far(p)
    for p in lines:
        write_near(p)
        write_far(p)
    if with_gains:
        for j in range(15):
            gain_copy(j).wait_recv()
        total = gain_in[pos]
        for j in range(15):
            total = total + gain_got[j]
        named["gain_out"][...] = total
    on_first(look_end)
    drain()
    for p in range(count):
        if spreads:
            for way in range(4):
                spread(p, way).wait_send()
        else:
            own_out(p).wait()
        if plan[p][1] == "plane":
            for line in range(4):
                for b in (0, 1):
                    send_first(p, line, b).wait_send()
                send_second(p, line).wait_send()
                pl.when(line != pos)(send_line(p, line).wait_send)
        else:
            for k in (1, 2, 3):
                line_first(p, k).wait_send()
                cross(p, k).wait_send()
    if with_gains:
        for j in range(15):
            gain_copy(j).wait_send()


def reduce_all(arrays, plan, only, collective_id, ahead, gains=None, look=None, spread=True):
    low, f32, dma = jnp.bfloat16, jnp.float32, pltpu.SemaphoreType.DMA
    extras = ("spread",) * spread + ("gains",) * (gains is not None) + ("looked",) * (look is not None)
    count = len(plan)
    inputs = list(arrays)
    kind = f32 if spread else low
    share = 4 if spread else 16
    outs = [jax.ShapeDtypeStruct((x.shape[0] // share, x.shape[1]), kind) for x in arrays]
    out_specs = [ANYWHERE] * len(arrays)
    in_specs = [ANYWHERE] * len(arrays)
    names = ["own", "got1", "got2", "got3", "land"]
    scratch = {name: [] for name in names}
    ring_shapes = []
    spots = []
    for src, way, _, chunks in plan:
        rows, columns = arrays[src].shape[0] // 4, arrays[src].shape[1]
        sub = rows // 4 // chunks
        if way == "plane":
            shapes = [(4, 2, sub, columns), (4, 2, sub, columns), (4, sub, columns)]
        else:
            shapes = [(rows, columns), (3, rows, columns), (8, 128)]
        for name, shape in zip(names, shapes + [(3, sub, columns), (4, sub, columns)]):
            scratch[name].append(pltpu.VMEM(shape, low))
        if (sub, columns) not in ring_shapes:
            ring_shapes.append((sub, columns))
        spots.append(ring_shapes.index((sub, columns)))
    flat = [item for name in names for item in scratch[name]]
    sems = [dma((count, 4, 2))] * 3 + [dma((count, 4))] * 6 + [dma((count,))]
    tail = []
    if spread:
        tail += [pltpu.VMEM((2,) + shape, f32) for shape in ring_shapes] + [dma((len(ring_shapes), 2))]
    if gains is not None:
        inputs.append(gains)
        in_specs.append(ANYWHERE)
        outs.append(jax.ShapeDtypeStruct(gains.shape[1:], f32))
        out_specs.append(IN_VMEM)
        tail += [
            pltpu.VMEM(gains.shape, f32),
            pltpu.VMEM((15,) + gains.shape[1:], f32),
            dma((15,)),
            dma((15,)),
            dma,
        ]
    if look is not None:
        ids, rows_in, fin_in = look
        inputs += [ids, rows_in, fin_in]
        in_specs += [IN_VMEM, ANYWHERE, ANYWHERE]
        quarter, emb = fin_in.shape
        outs.append(jax.ShapeDtypeStruct((4 * quarter, emb), low))
        out_specs.append(ANYWHERE)
        tail += [
            pltpu.VMEM((4, 4) + rows_in.shape, low),
            dma((6,)),
            dma((10,)),
            dma((10,)),
            pltpu.VMEM(fin_in.shape, low),
            pltpu.VMEM((4, quarter, emb), low),
            pltpu.VMEM((8, 128), f32),
        ]

    def refs_of(refs):
        at = 0

        def take(n):
            nonlocal at
            at += n
            return list(refs[at - n : at])

        named = {"arrays": take(len(arrays))}
        if gains is not None:
            named["gains"] = take(1)[0]
        if look is not None:
            named["look_in"] = take(3)
        named["outs"] = take(len(arrays))
        if gains is not None:
            named["gain_out"] = take(1)[0]
        if look is not None:
            named["table_out"] = take(1)[0]
        for name in names:
            named[name] = take(count)
        named["sems"] = take(10)
        if spread:
            named["rings"] = take(len(ring_shapes))
            named["ring_sem"] = take(1)[0]
        if gains is not None:
            named["gain_scratch"] = take(5)
        if look is not None:
            named["look_scratch"] = take(7)
        return named

    return pl.pallas_call(
        functools.partial(reduce_kernel, plan, tuple(spots), only, extras, ahead, refs_of),
        out_shape=outs,
        in_specs=in_specs,
        out_specs=out_specs,
        scratch_shapes=flat + sems + tail,
        compiler_params=pltpu.CompilerParams(
            collective_id=collective_id, has_side_effects=True, vmem_limit_bytes=60 << 20
        ),
    )(*inputs)


def nothing_like(run):
    return jax.tree.map(lambda a: jnp.zeros(a.shape, a.dtype), jax.eval_shape(run))


def only_on(live, run):
    return lax.cond(live, run, lambda: nothing_like(run))


LAYER_PLAN = (
    (0, "plane", 0, 1),
    (1, "plane", 0, 1),
    (2, "plane", 0, 1),
    (3, "plane", 0, 1),
    (4, "line", 0, 1),
)
LAYER_AHEAD = 6
TABLE_AHEAD = 8


def after(value, *others):
    return lax.optimization_barrier((value,) + others)[0]


def per_device(
    tokens,
    lengths,
    levels,
    noise_rows,
    embed_table,
    w_in,
    ln_attn,
    w_qkv,
    w_proj,
    ln_mlp,
    w_up,
    w_down,
    ln_final,
    w_out,
):
    sec = lax.axis_index("section")
    pos = lax.axis_index("dp")
    first_section = sec == 0
    last_section = sec == 1
    rows = tokens.shape[0]
    seqs = lengths.shape[0]
    length = rows // seqs
    width = w_out.shape[0] * 4
    emb = w_out.shape[1]
    vocab_part = embed_table.shape[0]
    gains = jnp.concatenate(
        [ln_attn, ln_mlp, ln_final[None], jnp.zeros((13, ln_final.shape[0]), jnp.bfloat16)], 0
    )
    ids = jnp.concatenate([tokens.reshape(-1, 128), jnp.zeros((8 - rows // 128, 128), jnp.int32)], 0)
    shards = (w_qkv[0], w_proj[0], w_up[0], w_down[0], w_in, w_out, gains, ids)
    sizes = [s.shape[0] for s in shards]

    def entry(idx, whole=False):
        return (idx, 0, sizes[idx], whole)

    half = sizes[3] // 2
    wholes = gather_all(
        shards,
        (entry(7, True), entry(6, True), entry(4), entry(0), entry(1), entry(2), entry(3)),
        (entry(6, True), entry(0), entry(1, True), entry(2), (3, 0, half, True), (3, half, half, False), entry(5)),
        0,
    )
    qkv_weight, proj_weight, up_weight, down_weight, in_weight, out_weight, gain_all, line_ids = wholes
    gain_all = gain_all.reshape(4, 16, -1).astype(jnp.float32)
    gain_attn = gain_all[:, 0].reshape(-1)
    gain_mlp = gain_all[:, 1].reshape(-1)
    final_gain = gain_all[:, 2].reshape(-1)
    weights = (qkv_weight, proj_weight, up_weight, down_weight)
    gain_attn = gain_attn[None]
    gain_mlp = gain_mlp[None]
    key_valid = jnp.arange(length, dtype=jnp.int32)[None, :] < lengths[:, None]
    loss_scale = LOSS_GAIN / math.sqrt(rows * lax.axis_size(("group", "dp")))

    def look_up():
        local = line_ids.reshape(4, 8, 128)[:, : rows // 128].reshape(-1) - pos * vocab_part
        hit = local[:, None] == lax.broadcasted_iota(jnp.int32, (1, vocab_part), 1)
        return product(hit.astype(jnp.bfloat16), embed_table).astype(jnp.bfloat16)

    looked_parts = only_on(first_section, look_up).reshape(4, rows, emb)
    looked_parts, all_ids = swap_rows(looked_parts, line_ids, 1)
    all_tokens = all_ids.reshape(16, 8, 128)[:, : rows // 128].reshape(-1)
    noise_level = jnp.exp(LOG_LOW + levels.astype(jnp.float32) * (LOG_SPAN / (LEVELS - 1)))
    scale_in = lax.rsqrt(EMB_VAR + noise_level * noise_level)
    row_level = jnp.repeat(noise_level, length)[:, None]
    row_scale = jnp.repeat(scale_in, length)[:, None]

    def front():
        looked = jnp.sum(looked_parts.astype(jnp.float32), 0)
        mixed_in = ((looked + row_level * noise_rows.astype(jnp.float32)) * row_scale).astype(
            jnp.bfloat16
        )
        return mixed_in, product(mixed_in, in_weight)

    mixed_in, x_first = only_on(first_section, front)
    kept = run_forward(0, x_first, gain_attn, gain_mlp, lengths, weights, None)
    out_first = kept[9].astype(jnp.bfloat16)
    (table_full,) = gather_all(
        (after(embed_table, out_first),), ((0, 0, vocab_part, False),), (), 2
    )
    x_second = passed_along(after(out_first, table_full), "section", 1)
    kept = run_forward(1, x_second, gain_attn, gain_mlp, lengths, weights, kept)
    final_in = normed(kept[9], final_gain).astype(jnp.bfloat16)
    projected = product(final_in, out_weight).astype(jnp.bfloat16)
    projected = passed_along(projected, "section", -1)
    valid_scale = jnp.where(key_valid.reshape(1, -1), loss_scale, 0.0)
    grad_proj_a, entropy, table_g = run_vocabulary(
        0, projected, tokens[None], valid_scale, table_full
    )
    grad_proj = passed_along(grad_proj_a, "section", 1)
    (table_fin,) = reduce_all(
        (after(table_g, grad_proj),),
        tuple((0, "plane", chunk, 4) for chunk in range(4)),
        0,
        3,
        TABLE_AHEAD,
        spread=False,
    )
    grad_top, gain_final = norm_back(kept[9], final_gain, product_nt(grad_proj, out_weight))
    made = run_backward(1, grad_top, gain_attn, gain_mlp, lengths, kept, weights, None)
    grad_first = passed_along(after(made[4], table_fin), "section", -1)
    made = run_backward(0, grad_first, gain_attn, gain_mlp, lengths, kept, weights, made)
    shape = in_weight.shape

    def front_edge():
        looked_grad = (product_nt(made[4], in_weight) * row_scale).astype(jnp.bfloat16)
        return product_tn(mixed_in, made[4]).astype(jnp.bfloat16), looked_grad

    def back_edge():
        edge = product_tn(final_in, grad_proj).astype(jnp.bfloat16)
        edge = edge.reshape(4, shape[0] // 4, shape[1]).reshape(shape)
        return edge, jnp.zeros((rows, emb), jnp.bfloat16)

    edge_g, looked_grad = lax.cond(first_section, front_edge, back_edge)
    gain_rows = made[5] + jnp.concatenate(
        [jnp.zeros((2, width)), gain_final[None], jnp.zeros((5, width))], 0
    )
    gain_rows = gain_rows.reshape(8, 4, width // 4).transpose(1, 0, 2)

    def grads_of(rows_at_once, grads):
        return product(rows_at_once, grads).astype(jnp.bfloat16)

    order = (
        grads_of(kept[6], made[1]),
        grads_of(kept[8], made[0]),
        edge_g,
        grads_of(kept[4], made[2]),
        grads_of(kept[1], made[3]),
    )
    up_r, down_r, edge_r, proj_r, qkv_r, gain_r, table_r = reduce_all(
        order,
        LAYER_PLAN,
        None,
        4,
        LAYER_AHEAD,
        gains=gain_rows,
        look=(all_tokens.reshape(16, 1, rows), looked_grad, table_fin),
    )
    loss_low = after(entropy, gain_r)[0].astype(jnp.bfloat16)
    mine = (table_r, edge_r, gain_r, loss_low)
    theirs = lax.ppermute(mine, "section", [(0, 1), (1, 0)])

    def pair_of(at):
        low = jnp.where(first_section, mine[at], theirs[at])
        high = jnp.where(first_section, theirs[at], mine[at])
        return low, high

    table_out = pair_of(0)[0].astype(jnp.float32)
    in_r, out_r = pair_of(1)
    final_r = pair_of(2)[1][2]
    token_loss = pair_of(3)[0]
    return (
        token_loss,
        table_out,
        in_r,
        gain_r[0][None],
        qkv_r[None],
        proj_r[None],
        gain_r[1][None],
        up_r[None],
        down_r[None],
        final_r,
        out_r.reshape(-1, emb),
    )


def solution(mesh):
    placed = (
        P(("group", "dp")),
        P(("group", "dp")),
        P(("group", "dp")),
        P(("group", "dp"), None),
        P("dp", None),
        P("dp", None),
        P("section", "dp"),
        P("section", "dp", None),
        P("section", "dp", None),
        P("section", "dp"),
        P("section", "dp", None),
        P("section", "dp", None),
        P("dp"),
        P("dp", None),
    )
    fits = (mesh.shape["section"], mesh.shape["group"], mesh.shape["dp"]) == (2, 4, 4)
    return jax.shard_map(
        per_device if fits else per_device_general,
        mesh=mesh,
        in_specs=placed,
        out_specs=(
            P(("group", "dp")),
            P("dp", None),
            P("dp", None),
            P("section", "dp"),
            P("section", "dp", None),
            P("section", "dp", None),
            P("section", "dp"),
            P("section", "dp", None),
            P("section", "dp", None),
            P("dp"),
            P("dp", None),
        ),
        check_vma=False,
    )
```

```python
import functools
import math

import jax
import jax.numpy as jnp
from jax import lax
from jax.experimental import pallas as pl
from jax.experimental.pallas import tpu as pltpu
from jax.sharding import PartitionSpec as P

HEAD = 64
LEVELS = 64
LEN = 128
MB = 2


EPS = 1e-05
LOG_LOW = -2.995732273553991
LOG_SPAN = 2.995732273553991
EMB_VAR = 0.015625
MASKED = -1e30
LOSS_GAIN = 16.0


def passed_along(x, axis, by):
    count = lax.axis_size(axis)
    pairs = [(i, i + by) for i in range(count) if 0 <= i + by < count]
    return lax.ppermute(x, axis, pairs)


def product(left_side, right_side):
    return jnp.dot(left_side, right_side, preferred_element_type=jnp.float32)


def product_tn(left_side, right_side):
    return lax.dot_general(
        left_side, right_side, (((0,), (0,)), ((), ())), preferred_element_type=jnp.float32
    )


def product_nt(left_side, right_side):
    return lax.dot_general(
        left_side, right_side, (((1,), (1,)), ((), ())), preferred_element_type=jnp.float32
    )


def normed(inputs, gain_vec):
    center = inputs - jnp.mean(inputs, -1, keepdims=True)
    return center * lax.rsqrt(jnp.mean(center * center, -1, keepdims=True) + EPS) * gain_vec


def norm_back(inputs, gain_vec, upstream):
    output, pullback = jax.vjp(normed, inputs, gain_vec)
    return pullback(upstream)


def gelu_exact(values_in):
    return jax.nn.gelu(values_in, approximate=False)


def attn_scores(split_rows, key_valid):
    scores = (
        jnp.einsum(
            "qhd,khd->hqk", split_rows[:, 0], split_rows[:, 1], preferred_element_type=jnp.float32
        )
        * 0.125
    )
    return jnp.where(key_valid[None, None, :], scores, MASKED)


def attend(qkv_rows, key_valid):
    length = qkv_rows.shape[0]
    model_width = qkv_rows.shape[1] // 3
    split_rows = qkv_rows.reshape(length, 3, model_width // HEAD, HEAD)
    scores = attn_scores(split_rows, key_valid)
    row_max = jnp.max(scores, -1, keepdims=True)
    log_total = row_max + jnp.log(jnp.sum(jnp.exp(scores - row_max), -1, keepdims=True))
    probs_low = jnp.exp(scores - log_total).astype(jnp.bfloat16)
    mixed_rows = jnp.einsum(
        "hqk,khd->qhd", probs_low, split_rows[:, 2], preferred_element_type=jnp.float32
    )
    return (mixed_rows.reshape(length, model_width).astype(jnp.bfloat16), log_total)


def attend_back(qkv_rows, key_valid, log_total, grad_mixed):
    length = qkv_rows.shape[0]
    model_width = qkv_rows.shape[1] // 3
    head_count = model_width // HEAD
    split_rows = qkv_rows.reshape(length, 3, head_count, HEAD)
    grad_heads = grad_mixed.reshape(length, head_count, HEAD)
    probs_full = jnp.exp(attn_scores(split_rows, key_valid) - log_total)
    grad_values = jnp.einsum(
        "hqk,qhd->khd",
        probs_full.astype(jnp.bfloat16),
        grad_heads,
        preferred_element_type=jnp.float32,
    )
    grad_probs = jnp.einsum(
        "qhd,khd->hqk", grad_heads, split_rows[:, 2], preferred_element_type=jnp.float32
    )
    grad_scores = (
        probs_full * (grad_probs - jnp.sum(grad_probs * probs_full, -1, keepdims=True))
    ).astype(jnp.bfloat16)
    grad_query = (
        jnp.einsum(
            "hqk,khd->qhd", grad_scores, split_rows[:, 1], preferred_element_type=jnp.float32
        )
        * 0.125
    )
    grad_key = (
        jnp.einsum(
            "hqk,qhd->khd", grad_scores, split_rows[:, 0], preferred_element_type=jnp.float32
        )
        * 0.125
    )
    stacked = jnp.stack([grad_query, grad_key, grad_values], 1).reshape(length, 3 * model_width)
    return stacked.astype(jnp.bfloat16)


def layer_forward(hidden, key_valid, weights):
    gain_attn, qkv_weight, proj_weight, gain_mlp, up_weight, down_weight = weights
    normed_in = normed(hidden, gain_attn).astype(jnp.bfloat16)
    qkv_rows = product(normed_in, qkv_weight).astype(jnp.bfloat16)
    mixed_rows, log_total = attend(qkv_rows, key_valid)
    hidden_mid = hidden + product(mixed_rows, proj_weight)
    mlp_in = normed(hidden_mid, gain_mlp).astype(jnp.bfloat16)
    pre_act = product(mlp_in, up_weight)
    activated = gelu_exact(pre_act).astype(jnp.bfloat16)
    hidden_out = hidden_mid + product(activated, down_weight)
    return (
        hidden_out,
        (
            hidden,
            normed_in,
            qkv_rows,
            log_total,
            mixed_rows,
            hidden_mid,
            mlp_in,
            pre_act,
            activated,
        ),
    )


def empty_kept(length, model_width, hidden_units, head_count):
    return (
        jnp.zeros((length, model_width), jnp.float32),
        jnp.zeros((length, model_width), jnp.bfloat16),
        jnp.zeros((length, 3 * model_width), jnp.bfloat16),
        jnp.zeros((head_count, length, 1), jnp.float32),
        jnp.zeros((length, model_width), jnp.bfloat16),
        jnp.zeros((length, model_width), jnp.float32),
        jnp.zeros((length, model_width), jnp.bfloat16),
        jnp.zeros((length, hidden_units), jnp.float32),
        jnp.zeros((length, hidden_units), jnp.bfloat16),
    )


def layer_backward(kept_vals, grad_out, key_valid, weights):
    hidden, normed_in, qkv_rows, log_total, mixed_rows, hidden_mid, mlp_in, pre_act, activated = (
        kept_vals
    )
    gain_attn, qkv_weight, proj_weight, gain_mlp, up_weight, down_weight = weights
    grad_low = grad_out.astype(jnp.bfloat16)
    grad_activated = product_nt(grad_low, down_weight)
    grad_pre = jax.vjp(gelu_exact, pre_act)[1](grad_activated)[0].astype(jnp.bfloat16)
    grad_mlp_in = product_nt(grad_pre, up_weight)
    grad_mid_norm, grad_gain_mlp = norm_back(hidden_mid, gain_mlp, grad_mlp_in)
    grad_mid = grad_out + grad_mid_norm
    grad_mid_low = grad_mid.astype(jnp.bfloat16)
    grad_mixed = product_nt(grad_mid_low, proj_weight).astype(jnp.bfloat16)
    grad_qkv = attend_back(qkv_rows, key_valid, log_total, grad_mixed)
    grad_normed = product_nt(grad_qkv, qkv_weight)
    grad_in_norm, grad_gain_attn = norm_back(hidden, gain_attn, grad_normed)
    records = (activated, grad_low, mlp_in, grad_pre, mixed_rows, grad_mid_low, normed_in, grad_qkv)
    return (grad_mid + grad_in_norm, (grad_gain_attn, grad_gain_mlp), records)


def layer_zero(length, model_width, hidden_units):
    records = (
        jnp.zeros((length, hidden_units), jnp.bfloat16),
        jnp.zeros((length, model_width), jnp.bfloat16),
        jnp.zeros((length, model_width), jnp.bfloat16),
        jnp.zeros((length, hidden_units), jnp.bfloat16),
        jnp.zeros((length, model_width), jnp.bfloat16),
        jnp.zeros((length, model_width), jnp.bfloat16),
        jnp.zeros((length, model_width), jnp.bfloat16),
        jnp.zeros((length, 3 * model_width), jnp.bfloat16),
    )
    gains = (jnp.zeros((model_width,), jnp.float32), jnp.zeros((model_width,), jnp.float32))
    return (jnp.zeros((length, model_width), jnp.float32), gains, records)


def layer_grads(records):
    activated, grad_low, mlp_in, grad_pre, mixed_rows, grad_mid_low, normed_in, grad_qkv = records
    return (
        product_tn(normed_in, grad_qkv),
        product_tn(mixed_rows, grad_mid_low),
        product_tn(mlp_in, grad_pre),
        product_tn(activated, grad_low),
    )


def embed_inputs(token_ids, noise_block, level_id, table_full):
    noise_level = jnp.exp(LOG_LOW + level_id.astype(jnp.float32) * (LOG_SPAN / (LEVELS - 1)))
    scale_in = lax.rsqrt(EMB_VAR + noise_level * noise_level)
    looked = jnp.take(table_full, token_ids, axis=0).astype(jnp.float32)
    mixed_in = ((looked + noise_level * noise_block.astype(jnp.float32)) * scale_in).astype(
        jnp.bfloat16
    )
    return (mixed_in, scale_in)


def embed_backward(token_ids, noise_block, level_id, grad_start, table_full, in_weight):
    mixed_in, scale_in = embed_inputs(token_ids, noise_block, level_id, table_full)
    grad_low = grad_start.astype(jnp.bfloat16)
    grad_looked = product_nt(grad_low, in_weight) * scale_in
    return (mixed_in, grad_low, grad_looked)


def embed_zero(length, model_width, emb_width):
    return (
        jnp.zeros((length, emb_width), jnp.bfloat16),
        jnp.zeros((length, model_width), jnp.bfloat16),
        jnp.zeros((length, emb_width), jnp.float32),
    )


def tail_pass(hidden, token_ids, key_valid, final_gain, out_weight, table_full, loss_scale):
    final_in = normed(hidden, final_gain).astype(jnp.bfloat16)
    projected = product(final_in, out_weight).astype(jnp.bfloat16)
    logits = product_nt(projected, table_full)
    row_max = jnp.max(logits, -1, keepdims=True)
    log_total = row_max + jnp.log(jnp.sum(jnp.exp(logits - row_max), -1, keepdims=True))
    vocab_ids = lax.broadcasted_iota(jnp.int32, logits.shape, 1)
    target_hit = vocab_ids == token_ids[:, None]
    picked = jnp.sum(jnp.where(target_hit, logits, 0.0), -1)
    entropy = jnp.where(key_valid, log_total[:, 0] - picked, 0.0)
    row_scale = jnp.where(key_valid, loss_scale, 0.0)[:, None]
    grad_logits = (
        (jnp.exp(logits - log_total) - target_hit.astype(jnp.float32)) * row_scale
    ).astype(jnp.bfloat16)
    grad_proj = product(grad_logits, table_full).astype(jnp.bfloat16)
    grad_final = product_nt(grad_proj, out_weight)
    grad_hidden, grad_gain = norm_back(hidden, final_gain, grad_final)
    return (grad_hidden, entropy, grad_gain, (grad_logits, projected, final_in, grad_proj))


def tail_zero(length, model_width, emb_width, vocab_rows):
    records = (
        jnp.zeros((length, vocab_rows), jnp.bfloat16),
        jnp.zeros((length, emb_width), jnp.bfloat16),
        jnp.zeros((length, model_width), jnp.bfloat16),
        jnp.zeros((length, emb_width), jnp.bfloat16),
    )
    return (
        jnp.zeros((length, model_width), jnp.float32),
        jnp.zeros((length,), jnp.float32),
        jnp.zeros((model_width,), jnp.float32),
        records,
    )


def edge_grads(tail_records, embed_records, token_ids):
    grad_logits, projected, final_in, grad_proj = tail_records
    mixed_in, grad_low, grad_looked = embed_records
    table_grad = product_tn(grad_logits, projected).at[token_ids].add(grad_looked)
    return (table_grad, product_tn(mixed_in, grad_low), product_tn(final_in, grad_proj))


def joined_rows(record_list):
    return jax.tree.map(lambda *pieces: jnp.concatenate(pieces, 0), *record_list)


def assemble(gain_attn_sum, gain_mlp_sum, layer_set, edge_set, gain_final_sum):
    return (
        gain_attn_sum[None],
        layer_set[0][None],
        layer_set[1][None],
        gain_mlp_sum[None],
        layer_set[2][None],
        layer_set[3][None],
        edge_set[0],
        edge_set[1],
        gain_final_sum,
        edge_set[2],
    )


def per_device_general(
    tokens,
    lengths,
    levels,
    noise_rows,
    embed_table,
    w_in,
    ln_attn,
    w_qkv,
    w_proj,
    ln_mlp,
    w_up,
    w_down,
    ln_final,
    w_out,
):
    gathered = (
        lax.all_gather(embed_table, "dp", axis=0, tiled=True),
        lax.all_gather(w_in, "dp", axis=0, tiled=True),
        lax.all_gather(ln_attn, "dp", axis=1, tiled=True),
        lax.all_gather(w_qkv, "dp", axis=1, tiled=True),
        lax.all_gather(w_proj, "dp", axis=1, tiled=True),
        lax.all_gather(ln_mlp, "dp", axis=1, tiled=True),
        lax.all_gather(w_up, "dp", axis=1, tiled=True),
        lax.all_gather(w_down, "dp", axis=1, tiled=True),
        lax.all_gather(ln_final, "dp", axis=0, tiled=True),
        lax.all_gather(w_out, "dp", axis=0, tiled=True),
    )
    table_full = gathered[0]
    in_weight = gathered[1]
    layer_weights = (
        gathered[2][0].astype(jnp.float32),
        gathered[3][0],
        gathered[4][0],
        gathered[5][0].astype(jnp.float32),
        gathered[6][0],
        gathered[7][0],
    )
    final_gain = gathered[8].astype(jnp.float32)
    out_weight = gathered[9]
    model_width = out_weight.shape[0]
    emb_width = out_weight.shape[1]
    vocab_rows = table_full.shape[0]
    hidden_units = layer_weights[4].shape[1]
    head_count = model_width // HEAD
    section_index = lax.axis_index("section")
    first_section = section_index == 0
    token_grid = tokens.reshape(MB, LEN)
    noise_grid = noise_rows.reshape(MB, LEN, noise_rows.shape[1])
    positions = jnp.arange(LEN, dtype=jnp.int32)
    valid_grid = positions[None, :] < lengths[:, None]
    loss_scale = LOSS_GAIN / math.sqrt(tokens.shape[0] * lax.axis_size(("group", "dp")))
    gain_attn_sum = jnp.zeros((model_width,), jnp.float32)
    gain_mlp_sum = jnp.zeros((model_width,), jnp.float32)
    gain_final_sum = jnp.zeros((model_width,), jnp.float32)
    recv_act = jnp.zeros((LEN, model_width), jnp.bfloat16)
    recv_grad = jnp.zeros((LEN, model_width), jnp.bfloat16)
    zero_rows = jnp.zeros((LEN, model_width), jnp.float32)
    kept_ticks = {}
    layer_recs = {}
    tail_recs = {}
    embed_recs = {}
    losses = []
    for moment in range(MB + 2):
        offset = moment - section_index
        fwd_valid = (offset >= 0) & (offset < MB)
        fwd_index = jnp.clip(offset, 0, MB - 1)
        ids_now = lax.dynamic_index_in_dim(token_grid, fwd_index, 0, False)
        noise_now = lax.dynamic_index_in_dim(noise_grid, fwd_index, 0, False)
        level_now = lax.dynamic_index_in_dim(levels, fwd_index, 0, False)
        valid_now = lax.dynamic_index_in_dim(valid_grid, fwd_index, 0, False)

        def first_input():
            mixed_in, scale_in = embed_inputs(ids_now, noise_now, level_now, table_full)
            return product(mixed_in, in_weight)

        layer_input = lax.cond(first_section, first_input, lambda: recv_act.astype(jnp.float32))
        hidden_out, kept_now = lax.cond(
            fwd_valid,
            lambda: layer_forward(layer_input, valid_now, layer_weights),
            lambda: (zero_rows, empty_kept(LEN, model_width, hidden_units, head_count)),
        )
        kept_ticks[moment] = kept_now
        tail_live = jnp.logical_not(first_section) & fwd_valid
        tail_grad, entropy, final_step, tail_now = lax.cond(
            tail_live,
            lambda: tail_pass(
                hidden_out, ids_now, valid_now, final_gain, out_weight, table_full, loss_scale
            ),
            lambda: tail_zero(LEN, model_width, emb_width, vocab_rows),
        )
        tail_recs[moment] = tail_now
        gain_final_sum = gain_final_sum + final_step
        back_tick = moment - 2
        late_live = 0 <= back_tick < MB
        late_index = min(max(back_tick, 0), MB - 1)
        kept_late = kept_ticks[back_tick] if back_tick >= 0 else kept_now
        kept_back = lax.cond(first_section, lambda: kept_late, lambda: kept_now)
        grad_top = jnp.where(first_section, recv_grad.astype(jnp.float32), tail_grad)
        valid_back = jnp.where(first_section, valid_grid[late_index], valid_now)
        back_live = jnp.where(first_section, late_live, fwd_valid)
        grad_start, gain_pair, layer_now = lax.cond(
            back_live,
            lambda: layer_backward(kept_back, grad_top, valid_back, layer_weights),
            lambda: layer_zero(LEN, model_width, hidden_units),
        )
        layer_recs[moment] = layer_now
        gain_attn_sum = gain_attn_sum + gain_pair[0]
        gain_mlp_sum = gain_mlp_sum + gain_pair[1]
        if late_live:
            embed_now = lax.cond(
                first_section,
                lambda: embed_backward(
                    token_grid[late_index],
                    noise_grid[late_index],
                    levels[late_index],
                    grad_start,
                    table_full,
                    in_weight,
                ),
                lambda: embed_zero(LEN, model_width, emb_width),
            )
        else:
            embed_now = embed_zero(LEN, model_width, emb_width)
        embed_recs[moment] = embed_now
        if moment < MB:
            recv_act = passed_along(hidden_out.astype(jnp.bfloat16), "section", 1)
        if 1 <= moment <= MB:
            entropy_low = entropy.astype(jnp.bfloat16)
            recv_grad, loss_back = passed_along(
                (grad_start.astype(jnp.bfloat16), entropy_low), "section", -1
            )
            losses.append(jnp.where(first_section, loss_back, entropy_low))
    chosen = [
        jax.tree.map(
            lambda early, late: jnp.where(first_section, early, late),
            layer_recs[micro + 2],
            layer_recs[micro + 1],
        )
        for micro in range(MB)
    ]
    all_layer = layer_grads(joined_rows(chosen))
    all_tail = joined_rows([tail_recs[micro + 1] for micro in range(MB)])
    all_embed = joined_rows([embed_recs[micro + 2] for micro in range(MB)])
    all_edge = edge_grads(all_tail, all_embed, tokens)
    grad_pack = assemble(gain_attn_sum, gain_mlp_sum, all_layer, all_edge, gain_final_sum)
    parted = (
        lax.psum_scatter(
            grad_pack[0].astype(jnp.bfloat16), "dp", scatter_dimension=1, tiled=True
        ).astype(jnp.float32),
        lax.psum_scatter(
            grad_pack[1].astype(jnp.bfloat16), "dp", scatter_dimension=1, tiled=True
        ).astype(jnp.float32),
        lax.psum_scatter(
            grad_pack[2].astype(jnp.bfloat16), "dp", scatter_dimension=1, tiled=True
        ).astype(jnp.float32),
        lax.psum_scatter(
            grad_pack[3].astype(jnp.bfloat16), "dp", scatter_dimension=1, tiled=True
        ).astype(jnp.float32),
        lax.psum_scatter(
            grad_pack[4].astype(jnp.bfloat16), "dp", scatter_dimension=1, tiled=True
        ).astype(jnp.float32),
        lax.psum_scatter(
            grad_pack[5].astype(jnp.bfloat16), "dp", scatter_dimension=1, tiled=True
        ).astype(jnp.float32),
        lax.psum_scatter(
            grad_pack[6].astype(jnp.bfloat16), "dp", scatter_dimension=0, tiled=True
        ).astype(jnp.float32),
        lax.psum_scatter(
            grad_pack[7].astype(jnp.bfloat16), "dp", scatter_dimension=0, tiled=True
        ).astype(jnp.float32),
        lax.psum_scatter(
            grad_pack[8].astype(jnp.bfloat16), "dp", scatter_dimension=0, tiled=True
        ).astype(jnp.float32),
        lax.psum_scatter(
            grad_pack[9].astype(jnp.bfloat16), "dp", scatter_dimension=0, tiled=True
        ).astype(jnp.float32),
    )
    layer_total = (
        lax.psum(parted[0].astype(jnp.bfloat16), "group").astype(jnp.float32),
        lax.psum(parted[1].astype(jnp.bfloat16), "group").astype(jnp.float32),
        lax.psum(parted[2].astype(jnp.bfloat16), "group").astype(jnp.float32),
        lax.psum(parted[3].astype(jnp.bfloat16), "group").astype(jnp.float32),
        lax.psum(parted[4].astype(jnp.bfloat16), "group").astype(jnp.float32),
        lax.psum(parted[5].astype(jnp.bfloat16), "group").astype(jnp.float32),
    )
    edge_total = (
        lax.psum(parted[6].astype(jnp.bfloat16), ("section", "group")).astype(jnp.float32),
        lax.psum(parted[7].astype(jnp.bfloat16), ("section", "group")).astype(jnp.float32),
        lax.psum(parted[8].astype(jnp.bfloat16), ("section", "group")).astype(jnp.float32),
        lax.psum(parted[9].astype(jnp.bfloat16), ("section", "group")).astype(jnp.float32),
    )
    token_loss = jnp.concatenate(losses)
    return (
        token_loss,
        edge_total[0],
        edge_total[1],
        layer_total[0],
        layer_total[1],
        layer_total[2],
        layer_total[3],
        layer_total[4],
        layer_total[5],
        edge_total[2],
        edge_total[3],
    )


MESH = pl.DeviceIdType.MESH
ANYWHERE = pl.BlockSpec(memory_space=pl.ANY)


def pick(index, values):
    out = values[-1]
    for at in range(len(values) - 2, -1, -1):
        out = jnp.where(index == at, values[at], out)
    return out


def rows_at(start, size):
    return pl.ds(pl.multiple_of(start, 8), size)


def remote(src, dst, send_sem, recv_sem, device):
    return pltpu.make_async_remote_copy(
        src_ref=src,
        dst_ref=dst,
        send_sem=send_sem,
        recv_sem=recv_sem,
        device_id=device,
        device_id_type=MESH,
    )


def gather_kernel(count, first_order, last_order, *refs):
    shards = refs[:count]
    wholes = refs[count : 2 * count]
    own_sem, zsend, zrecv, psend, precv, gate = refs[2 * count : 2 * count + 6]
    stage = refs[2 * count + 6 :]
    sec = lax.axis_index("section")
    grp = lax.axis_index("group")
    pos = lax.axis_index("dp")
    beside = ((sec, grp ^ 1, pos), (sec, grp ^ 2, pos))
    above = (sec, grp, pos + 1)
    below = (sec, grp, pos - 1)
    partner = (1 - sec, grp, pos)
    barrier = pltpu.get_barrier_semaphore()
    both = bool(last_order)

    def greet(device):
        pl.semaphore_signal(barrier, inc=1, device_id=device, device_id_type=MESH)

    def meet():
        for device in beside + ((partner,) if both else ()):
            greet(device)

        @pl.when(pos > 0)
        def _():
            greet(below)

        @pl.when(pos < 3)
        def _():
            greet(above)

        at_end = (pos == 0) | (pos == 3)
        pl.semaphore_wait(barrier, jnp.where(at_end, 3, 4) + (1 if both else 0))

    turn = [pick(pos, v) for v in ((3, 1, 3, 1), (2, 3, 1, 2), (1, 2, 2, 3))]

    def run(order, before, middle):
        def rows_of(slot):
            return shards[order[slot][0]].shape[0]

        def part_of(slot):
            _, _, size, whole_line = order[slot]
            return size if whole_line else size // 4

        def shift(slot, who):
            _, lo, _, whole_line = order[slot]
            return lo if whole_line else lo + who * part_of(slot)

        def block(slot, origin, who):
            return rows_at(origin * rows_of(slot) + shift(slot, who), part_of(slot))

        staged = sorted({entry[0] for entry in order})

        def load_own(idx):
            return pltpu.make_async_copy(shards[idx], stage[idx], own_sem.at[idx])

        def store_own(idx):
            rows = shards[idx].shape[0]
            return pltpu.make_async_copy(
                stage[idx], wholes[idx].at[rows_at(pos * rows, rows)], own_sem.at[idx]
            )

        def own_ends(slot):
            idx = order[slot][0]
            src = shards[idx].at[rows_at(shift(slot, grp), part_of(slot))]
            dst = wholes[idx].at[block(slot, pos, grp)]
            return (
                (pos < 3, remote(src, dst, zsend.at[slot, 0], zrecv.at[slot, 1], above)),
                (pos > 0, remote(src, dst, zsend.at[slot, 1], zrecv.at[slot, 3], below)),
            )

        def start_own(slot):
            for goes, copy in own_ends(slot):
                pl.when(goes)(copy.start)

        def origin_of(j):
            return lax.rem(pos - turn[j] + 4, 4)

        def arrived(slot, j):
            here = wholes[order[slot][0]].at[block(slot, origin_of(j), grp)]
            return remote(here, here, zsend.at[slot, 2 + j], zrecv.at[slot, turn[j]], partner)

        def onward(slot, j):
            step = jnp.where(turn[j] <= pos, 1, -1)
            to = pos + step
            here = wholes[order[slot][0]].at[block(slot, origin_of(j), grp)]
            landed = jnp.clip(turn[j] + step, 0, 3)
            copy = remote(
                here,
                here,
                zsend.at[slot, 2 + j],
                zrecv.at[slot, landed],
                (sec, grp, jnp.clip(to, 0, 3)),
            )
            return (to >= 0) & (to <= 3), copy

        def plane(slot, j, way):
            idx = order[slot][0]
            origin = origin_of(j)
            if way < 2:
                here = wholes[idx].at[block(slot, origin, grp)]
                return remote(here, here, psend.at[slot, j, way], precv.at[slot, j, way], beside[way])
            half = shards[idx].shape[1] // 2
            there = wholes[idx].at[
                block(slot, origin, grp ^ (way - 1)), pl.ds(half * (way - 2), half)
            ]
            return remote(
                there, there, psend.at[slot, j, way], precv.at[slot, j, way], beside[3 - way]
            )

        items = [(slot, j) for slot in range(len(order)) for j in range(3)]
        crossing = [item for item in items if not order[item[0]][3]]

        def first(slot, j):
            arrived(slot, j).wait_recv()
            goes, copy = onward(slot, j)
            pl.when(goes)(copy.start)
            if (slot, j) in crossing:
                plane(slot, j, 0).start()
                plane(slot, j, 1).start()

        def second(slot, j):
            if (slot, j) in crossing:
                for way in (0, 1):
                    plane(slot, j, way).wait_recv()
                    plane(slot, j, way + 2).start()

        if before is not None:
            before()
        for slot in range(len(order)):
            start_own(slot)
        for idx in staged:
            load_own(idx).start()
        lag = 2
        for at in range(len(items) + lag):
            if at < len(items):
                slot, j = items[at]
                if j == 2 and slot < len(staged):
                    load_own(staged[slot]).wait()
                    store_own(staged[slot]).start()
                first(slot, j)
            if at == len(items) - 1 and middle is not None:
                middle()
            if at >= lag:
                second(*items[at - lag])
        for slot, j in crossing:
            plane(slot, j, 2).wait_recv()
            plane(slot, j, 3).wait_recv()
        for idx in staged:
            store_own(idx).wait()
        for slot in range(len(order)):
            for goes, copy in own_ends(slot):
                pl.when(goes)(copy.wait_send)
        for slot, j in items:
            goes, copy = onward(slot, j)
            pl.when(goes)(copy.wait_send)
        for slot, j in crossing:
            for way in range(4):
                plane(slot, j, way).wait_send()

    def let_go():
        pl.semaphore_signal(gate, inc=1, device_id=partner, device_id_type=MESH)

    def hold():
        pl.semaphore_wait(gate, 1)

    if both:
        meet()

        @pl.when(sec == 0)
        def _():
            run(first_order, None, let_go)

        @pl.when(sec == 1)
        def _():
            run(last_order, hold, None)

    else:

        @pl.when(sec == 0)
        def _():
            meet()
            run(first_order, None, None)


def gather_all(shards, first_order, last_order, collective_id):
    count = len(shards)
    slots = max(len(first_order), len(last_order))
    return pl.pallas_call(
        functools.partial(gather_kernel, count, first_order, last_order),
        out_shape=[jax.ShapeDtypeStruct((s.shape[0] * 4, s.shape[1]), s.dtype) for s in shards],
        in_specs=[ANYWHERE] * count,
        out_specs=[ANYWHERE] * count,
        scratch_shapes=[
            pltpu.SemaphoreType.DMA((count,)),
            pltpu.SemaphoreType.DMA((slots, 5)),
            pltpu.SemaphoreType.DMA((slots, 4)),
            pltpu.SemaphoreType.DMA((slots, 3, 4)),
            pltpu.SemaphoreType.DMA((slots, 3, 4)),
            pltpu.SemaphoreType.REGULAR,
        ]
        + [pltpu.VMEM(s.shape, s.dtype) for s in shards],
        compiler_params=pltpu.CompilerParams(
            collective_id=collective_id, has_side_effects=True, vmem_limit_bytes=60 << 20
        ),
    )(*shards)


def swap_kernel(rows_ref, ids_ref, out_ref, ids_out, own_sem, send_sem, recv_sem):
    sec = lax.axis_index("section")
    grp = lax.axis_index("group")
    pos = lax.axis_index("dp")

    @pl.when(sec == 0)
    def _():
        barrier = pltpu.get_barrier_semaphore()
        peers = [(sec, grp, lax.rem(pos + k, 4)) for k in (1, 2, 3)]
        sides = [(sec, grp ^ j, pos) for j in (1, 2, 3)]
        for device in peers + sides:
            pl.semaphore_signal(barrier, inc=1, device_id=device, device_id_type=MESH)
        pl.semaphore_wait(barrier, 6)
        copies = []
        for k, device in enumerate(peers):
            copies.append(
                remote(rows_ref.at[device[2]], out_ref.at[pos], send_sem.at[k], recv_sem.at[k], device)
            )
        for k, device in enumerate(sides):
            copies.append(
                remote(ids_ref, ids_out.at[grp], send_sem.at[3 + k], recv_sem.at[3 + k], device)
            )
        for copy in copies:
            copy.start()
        own_rows = pltpu.make_async_copy(rows_ref.at[pos], out_ref.at[pos], own_sem.at[0])
        own_ids = pltpu.make_async_copy(ids_ref, ids_out.at[grp], own_sem.at[1])
        own_rows.start()
        own_ids.start()
        own_rows.wait()
        own_ids.wait()
        for copy in copies:
            copy.wait()


def swap_rows(rows, ids, collective_id):
    in_vmem = pl.BlockSpec(memory_space=pltpu.VMEM)
    return pl.pallas_call(
        swap_kernel,
        out_shape=[
            jax.ShapeDtypeStruct(rows.shape, rows.dtype),
            jax.ShapeDtypeStruct((4,) + ids.shape, ids.dtype),
        ],
        in_specs=[in_vmem] * 2,
        out_specs=[in_vmem] * 2,
        scratch_shapes=[
            pltpu.SemaphoreType.DMA((2,)),
            pltpu.SemaphoreType.DMA((6,)),
            pltpu.SemaphoreType.DMA((6,)),
        ],
        compiler_params=pltpu.CompilerParams(collective_id=collective_id, has_side_effects=True),
    )(rows, ids)


IN_VMEM = pl.BlockSpec(memory_space=pltpu.VMEM)
IN_SMEM = pl.BlockSpec(memory_space=pltpu.SMEM)
ROOT_HALF = 0.7071067811865476
ROOT_TWO_PI = 0.3989422804014327


def dot_nn(left, right):
    return lax.dot_general(
        left, right, (((1,), (0,)), ((), ())), preferred_element_type=jnp.float32
    )


def dot_nt(left, right):
    return lax.dot_general(
        left, right, (((1,), (1,)), ((), ())), preferred_element_type=jnp.float32
    )


def dot_tn(left, right):
    return lax.dot_general(
        left, right, (((0,), (0,)), ((), ())), preferred_element_type=jnp.float32
    )


def unit_rows(v):
    center = v - jnp.mean(v, -1, keepdims=True)
    scale = lax.rsqrt(jnp.mean(center * center, -1, keepdims=True) + EPS)
    return center * scale, scale


def split_heads(pair):
    low = lax.broadcasted_iota(jnp.int32, pair.shape, 1) < HEAD
    nothing = jnp.zeros_like(pair)
    return jnp.concatenate([jnp.where(low, pair, nothing), jnp.where(low, nothing, pair)], 0)


def join_heads(stacked):
    half = stacked.shape[0] // 2
    low = lax.broadcasted_iota(jnp.int32, (half, stacked.shape[1]), 1) < HEAD
    return jnp.where(low, stacked[:half], stacked[half:])


def pair_scores(keys, stacked_queries, key_count):
    scores = dot_nt(keys, stacked_queries) * 0.125
    valid = lax.broadcasted_iota(jnp.int32, scores.shape, 0) < key_count
    return jnp.where(valid, scores, MASKED)


STRIP = 64


def forward_kernel(only, tile, given, *refs):
    x, gain_attn, gain_mlp, counts, wq, wp, wu, wd = refs[:8]
    rest = refs[8 + given :]
    outs = rest[:KEPT_COUNT]
    qv, pv, uv, dv = rest[KEPT_COUNT : KEPT_COUNT + 4]
    kept = rest[KEPT_COUNT + 4 : 2 * KEPT_COUNT + 4]
    a, att, m, acc, wsem, osem = rest[2 * KEPT_COUNT + 4 :]
    xv, at_t, qkv, lse, att_t, mid, m_t, pre, act_t, out = kept
    rows, width = a.shape
    units = dv.shape[0]

    def store(idx):
        return pltpu.make_async_copy(kept[idx], outs[idx], osem.at[idx])

    def run():
        loads = []

        def load(src, dst):
            copy = pltpu.make_async_copy(src, dst, wsem.at[len(loads)])
            copy.start()
            loads.append(copy)

        for lo in range(0, 3 * width, tile):
            load(wq.at[:, pl.ds(lo, tile)], qv.at[:, pl.ds(lo, tile)])
        load(wp, pv)
        for lo in range(0, units, tile):
            load(wu.at[:, pl.ds(lo, tile)], uv.at[:, pl.ds(lo, tile)])
            load(wd.at[pl.ds(lo, tile)], dv.at[pl.ds(lo, tile)])
        loads = iter(loads)
        for lo in range(0, rows, STRIP):
            here = pl.ds(lo, STRIP)
            xv[here, :] = x[here, :].astype(jnp.float32)
            a[here, :] = (unit_rows(xv[here, :])[0] * gain_attn[...]).astype(jnp.bfloat16)
        store(0).start()
        for lo in range(0, 3 * width, tile):
            next(loads).wait()
            cols = pl.ds(lo, tile)
            qkv[:, cols] = dot_nn(a[...], qv[:, cols]).astype(jnp.bfloat16)
        store(2).start()
        for lo in range(0, width, 256):
            at_t[pl.ds(lo, 256), :] = a[:, pl.ds(lo, 256)].T
        store(1).start()
        pairs = width // 128
        for seq in range(rows // LEN):
            here = pl.ds(seq * LEN, LEN)
            for pair in range(pairs):
                stacked = split_heads(qkv[here, pl.ds(pair * 128, 128)])
                scores = pair_scores(qkv[here, pl.ds(width + pair * 128, 128)], stacked, counts[seq])
                top = jnp.max(scores, 0, keepdims=True)
                power = jnp.exp(scores - top)
                total = jnp.sum(power, 0, keepdims=True)
                lse[seq * pairs + pair] = top + jnp.log(total)
                probs = (power * (1.0 / total)).astype(jnp.bfloat16)
                mixed = dot_tn(probs, qkv[here, pl.ds(2 * width + pair * 128, 128)])
                att[here, pl.ds(pair * 128, 128)] = join_heads(mixed).astype(jnp.bfloat16)
        store(3).start()
        for lo in range(0, width, 256):
            att_t[pl.ds(lo, 256), :] = att[:, pl.ds(lo, 256)].T
        store(4).start()
        next(loads).wait()
        for lo in range(0, width, tile):
            cols = pl.ds(lo, tile)
            mid[:, cols] = xv[:, cols] + dot_nn(att[...], pv[:, cols])
        for lo in range(0, rows, STRIP):
            here = pl.ds(lo, STRIP)
            m[here, :] = (unit_rows(mid[here, :])[0] * gain_mlp[...]).astype(jnp.bfloat16)
        store(5).start()
        acc[...] = mid[...]
        for lo in range(0, units, tile):
            cols = pl.ds(lo, tile)
            next(loads).wait()
            before = dot_nn(m[...], uv[:, cols])
            pre[:, cols] = before
            active = (0.5 * before * (1.0 + lax.erf(before * ROOT_HALF))).astype(jnp.bfloat16)
            act_t[cols, :] = active.T
            next(loads).wait()
            acc[...] += dot_nn(active, dv[cols, :])
        store(7).start()
        store(8).start()
        for lo in range(0, width, 256):
            m_t[pl.ds(lo, 256), :] = m[:, pl.ds(lo, 256)].T
        store(6).start()
        out[...] = acc[...]
        store(9).start()
        for idx in range(KEPT_COUNT):
            store(idx).wait()

    pl.when(lax.axis_index("section") == only)(run)


KEPT_COUNT = 10


def kept_shapes(rows, width, units):
    f32, low = jnp.float32, jnp.bfloat16
    return [
        jax.ShapeDtypeStruct(shape, kind)
        for shape, kind in (
            ((rows, width), f32),
            ((width, rows), low),
            ((rows, 3 * width), low),
            ((rows // LEN * width // 128, 1, 2 * LEN), f32),
            ((width, rows), low),
            ((rows, width), f32),
            ((width, rows), low),
            ((rows, units), f32),
            ((units, rows), low),
            ((rows, width), f32),
        )
    ]


def run_forward(only, x, gain_attn, gain_mlp, counts, weights, kept):
    wq, wp, wu, wd = weights
    rows, width = x.shape
    units = wd.shape[0]
    tile = 512
    shapes = kept_shapes(rows, width, units)
    low = jnp.bfloat16
    given = 0 if kept is None else KEPT_COUNT
    in_specs = [IN_VMEM] * 3 + [IN_SMEM] + [ANYWHERE] * (4 + given)
    return pl.pallas_call(
        functools.partial(forward_kernel, only, tile, given),
        out_shape=shapes,
        in_specs=in_specs,
        out_specs=[ANYWHERE] * KEPT_COUNT,
        input_output_aliases={8 + idx: idx for idx in range(given)},
        scratch_shapes=[pltpu.VMEM(w.shape, w.dtype) for w in weights]
        + [pltpu.VMEM(s.shape, s.dtype) for s in shapes]
        + [
            pltpu.VMEM((rows, width), low),
            pltpu.VMEM((rows, width), low),
            pltpu.VMEM((rows, width), low),
            pltpu.VMEM((rows, width), jnp.float32),
            pltpu.SemaphoreType.DMA((3 * width // tile + 1 + 2 * units // tile,)),
            pltpu.SemaphoreType.DMA((KEPT_COUNT,)),
        ],
        compiler_params=pltpu.CompilerParams(vmem_limit_bytes=56 << 20),
    )(x, gain_attn, gain_mlp, counts, wq, wp, wu, wd, *(kept or ()))


GRAD_COUNT = 6


def grad_shapes(rows, width, units):
    f32, low = jnp.float32, jnp.bfloat16
    return [
        jax.ShapeDtypeStruct(shape, kind)
        for shape, kind in (
            ((rows, width), low),
            ((rows, units), low),
            ((rows, width), low),
            ((rows, 3 * width), low),
            ((rows, width), low),
            ((8, width), f32),
        )
    ]


def norm_pull(v, gain, upstream):
    unit, scale = unit_rows(v)
    pulled = upstream * gain
    inner = jnp.mean(pulled * unit, -1, keepdims=True)
    grad = (pulled - jnp.mean(pulled, -1, keepdims=True) - unit * inner) * scale
    return grad, jnp.sum(upstream * unit, 0, keepdims=True)


def backward_kernel(only, tile, given, *refs):
    grad, gain_attn, gain_mlp, counts, x_in, qkv_in, lse_in, mid_in, pre_in, wq, wp, wu, wd = refs[:13]
    rest = refs[13 + given :]
    outs = rest[:GRAD_COUNT]
    qv, pv, uv, dv = rest[GRAD_COUNT : GRAD_COUNT + 4]
    made = rest[GRAD_COUNT + 4 : 2 * GRAD_COUNT + 4]
    x, qkv, lse, mid, pre, gm, gmid, gatt, wsem, ksem, osem = rest[2 * GRAD_COUNT + 4 :]
    gy, gpre, gz, gqkv, gx, gains = made
    rows, width = gm.shape
    units = dv.shape[0]

    def store(idx):
        return pltpu.make_async_copy(made[idx], outs[idx], osem.at[idx])

    def run():
        loads = []

        def load(src, dst):
            copy = pltpu.make_async_copy(src, dst, wsem.at[len(loads)])
            copy.start()
            loads.append(copy)

        kept = [
            pltpu.make_async_copy(src, dst, ksem.at[idx])
            for idx, (src, dst) in enumerate(
                ((pre_in, pre), (mid_in, mid), (qkv_in, qkv), (lse_in, lse), (x_in, x))
            )
        ]
        kept[0].start()
        for lo in range(0, units, tile):
            load(wd.at[pl.ds(lo, tile)], dv.at[pl.ds(lo, tile)])
            load(wu.at[:, pl.ds(lo, tile)], uv.at[:, pl.ds(lo, tile)])
        for copy in kept[1:]:
            copy.start()
        load(wp, pv)
        load(wq, qv)
        loads = iter(loads)
        gy[...] = grad[...].astype(jnp.bfloat16)
        store(0).start()
        gains[...] = jnp.zeros_like(gains)
        kept[0].wait()
        gm[...] = jnp.zeros_like(gm)
        for lo in range(0, units, tile):
            cols = pl.ds(lo, tile)
            next(loads).wait()
            pulled = dot_nt(gy[...], dv[cols, :])
            before = pre[:, cols]
            slope = 0.5 * (1.0 + lax.erf(before * ROOT_HALF)) + before * (
                ROOT_TWO_PI * jnp.exp(-0.5 * before * before)
            )
            low = (pulled * slope).astype(jnp.bfloat16)
            gpre[:, cols] = low
            next(loads).wait()
            gm[...] += dot_nt(low, uv[:, cols])
        store(1).start()
        kept[1].wait()
        for lo in range(0, rows, STRIP):
            here = pl.ds(lo, STRIP)
            step, gain = norm_pull(mid[here, :], gain_mlp[...], gm[here, :])
            total = grad[here, :].astype(jnp.float32) + step
            gmid[here, :] = total
            gz[here, :] = total.astype(jnp.bfloat16)
            gains[1:2, :] += gain
        store(2).start()
        next(loads).wait()
        gatt[...] = dot_nt(gz[...], pv[...]).astype(jnp.bfloat16)
        kept[2].wait()
        kept[3].wait()
        pairs = width // 128
        for seq in range(rows // LEN):
            here = pl.ds(seq * LEN, LEN)
            for pair in range(pairs):
                own = pl.ds(pair * 128, 128)
                stacked = split_heads(qkv[here, own])
                pulled = split_heads(gatt[here, own])
                keys = qkv[here, pl.ds(width + pair * 128, 128)]
                values = qkv[here, pl.ds(2 * width + pair * 128, 128)]
                probs = jnp.exp(pair_scores(keys, stacked, counts[seq]) - lse[seq * pairs + pair])
                gprobs = dot_nt(values, pulled)
                inner = jnp.sum(probs * gprobs, 0, keepdims=True)
                gscores = (probs * (gprobs - inner)).astype(jnp.bfloat16)
                gqkv[here, own] = (join_heads(dot_tn(gscores, keys)) * 0.125).astype(jnp.bfloat16)
                gqkv[here, pl.ds(width + pair * 128, 128)] = (dot_nn(gscores, stacked) * 0.125).astype(
                    jnp.bfloat16
                )
                gqkv[here, pl.ds(2 * width + pair * 128, 128)] = dot_nn(
                    probs.astype(jnp.bfloat16), pulled
                ).astype(jnp.bfloat16)
        store(3).start()
        next(loads).wait()
        for lo in range(0, width, 256):
            gm[:, pl.ds(lo, 256)] = dot_nt(gqkv[...], qv[pl.ds(lo, 256), :])
        kept[4].wait()
        for lo in range(0, rows, STRIP):
            here = pl.ds(lo, STRIP)
            step, gain = norm_pull(x[here, :], gain_attn[...], gm[here, :])
            gx[here, :] = (gmid[here, :] + step).astype(jnp.bfloat16)
            gains[0:1, :] += gain
        store(4).start()
        store(5).start()
        for idx in range(GRAD_COUNT):
            store(idx).wait()

    pl.when(lax.axis_index("section") == only)(run)


def run_backward(only, grad, gain_attn, gain_mlp, counts, kept, weights, made):
    wq, wp, wu, wd = weights
    x, _, qkv, lse, _, mid, _, pre, _, _ = kept
    rows, width = x.shape
    units = wd.shape[0]
    tile = 512
    shapes = grad_shapes(rows, width, units)
    low, f32 = jnp.bfloat16, jnp.float32
    given = 0 if made is None else GRAD_COUNT
    in_specs = [IN_VMEM] * 3 + [IN_SMEM] + [ANYWHERE] * (9 + given)
    return pl.pallas_call(
        functools.partial(backward_kernel, only, tile, given),
        out_shape=shapes,
        in_specs=in_specs,
        out_specs=[ANYWHERE] * GRAD_COUNT,
        input_output_aliases={13 + idx: idx for idx in range(given)},
        scratch_shapes=[pltpu.VMEM(w.shape, w.dtype) for w in weights]
        + [pltpu.VMEM(s.shape, s.dtype) for s in shapes]
        + [pltpu.VMEM(s.shape, s.dtype) for s in (x, qkv, lse, mid, pre)]
        + [
            pltpu.VMEM((rows, width), f32),
            pltpu.VMEM((rows, width), f32),
            pltpu.VMEM((rows, width), low),
            pltpu.SemaphoreType.DMA((2 + 2 * units // tile,)),
            pltpu.SemaphoreType.DMA((5,)),
            pltpu.SemaphoreType.DMA((GRAD_COUNT,)),
        ],
        compiler_params=pltpu.CompilerParams(vmem_limit_bytes=56 << 20),
    )(grad, gain_attn, gain_mlp, counts, x, qkv, lse, mid, pre, wq, wp, wu, wd, *(made or ()))


def vocabulary_kernel(only, tile, proj, ids, scale, table, gproj_out, loss_out, gtable, tv, gt, gp, tsem, gsem):
    rows, emb = proj.shape
    vocab = tv.shape[0]
    count = vocab // tile

    def run():
        for at in range(count):
            here = pl.ds(at * tile, tile)
            pltpu.make_async_copy(table.at[here], tv.at[here], tsem.at[at]).start()

        def logits_of(at):
            return dot_nt(tv[rows_at(at * tile, tile), :], proj[...])

        def hits_of(at):
            names = lax.broadcasted_iota(jnp.int32, (tile, rows), 0) + at * tile
            return names == ids[...]

        def stats(at, carry):
            top, total, picked = carry
            here = rows_at(at * tile, tile)
            pltpu.make_async_copy(table.at[here], tv.at[here], tsem.at[at]).wait()
            logits = logits_of(at)
            higher = jnp.maximum(top, jnp.max(logits, 0, keepdims=True))
            total = total * jnp.exp(top - higher) + jnp.sum(jnp.exp(logits - higher), 0, keepdims=True)
            picked = picked + jnp.sum(jnp.where(hits_of(at), logits, 0.0), 0, keepdims=True)
            return higher, total, picked

        start = (
            jnp.full((1, rows), MASKED, jnp.float32),
            jnp.zeros((1, rows), jnp.float32),
            jnp.zeros((1, rows), jnp.float32),
        )
        top, total, picked = lax.fori_loop(0, count, stats, start)
        log_total = top + jnp.log(total)
        loss_out[...] = jnp.where(scale[...] > 0, log_total - picked, 0.0)
        gp[...] = jnp.zeros_like(gp)

        def gstore(at):
            return pltpu.make_async_copy(
                gt.at[rows_at(at * tile, tile)], gtable.at[rows_at(at * tile, tile)], gsem.at[at]
            )

        def pull(at, carry):
            here = rows_at(at * tile, tile)
            probs = jnp.exp(logits_of(at) - log_total)
            grads = ((probs - jnp.where(hits_of(at), 1.0, 0.0)) * scale[...]).astype(jnp.bfloat16)
            gp[...] += dot_tn(grads, tv[here, :])
            gt[here, :] = dot_nn(grads, proj[...]).astype(jnp.bfloat16)
            gstore(at).start()
            return carry

        lax.fori_loop(0, count, pull, 0)
        gproj_out[...] = gp[...].astype(jnp.bfloat16)

        def done(at, carry):
            gstore(at).wait()
            return carry

        lax.fori_loop(0, count, done, 0)

    pl.when(lax.axis_index("section") == only)(run)


def run_vocabulary(only, proj, ids, scale, table):
    rows, emb = proj.shape
    vocab = table.shape[0]
    tile = 1024
    return pl.pallas_call(
        functools.partial(vocabulary_kernel, only, tile),
        out_shape=[
            jax.ShapeDtypeStruct((rows, emb), jnp.bfloat16),
            jax.ShapeDtypeStruct((1, rows), jnp.float32),
            jax.ShapeDtypeStruct(table.shape, jnp.bfloat16),
        ],
        in_specs=[IN_VMEM] * 3 + [ANYWHERE],
        out_specs=[IN_VMEM] * 2 + [ANYWHERE],
        scratch_shapes=[
            pltpu.VMEM(table.shape, table.dtype),
            pltpu.VMEM(table.shape, jnp.bfloat16),
            pltpu.VMEM((rows, emb), jnp.float32),
            pltpu.SemaphoreType.DMA((vocab // tile,)),
            pltpu.SemaphoreType.DMA((vocab // tile,)),
        ],
        compiler_params=pltpu.CompilerParams(vmem_limit_bytes=40 << 20),
    )(proj, ids, scale, table)


def strip_of(rows, columns):
    strip = 16
    while 2 * strip * columns <= 65536 and rows % (2 * strip) == 0:
        strip = 2 * strip
    return strip


def add_rows(store, terms, rows, columns):
    strip = strip_of(rows, columns)

    def body(at, carry):
        here = rows_at(at * strip, strip)
        total = terms[0](here).astype(jnp.float32)
        for term in terms[1:]:
            total = total + term(here).astype(jnp.float32)
        store(here, total)
        return carry

    lax.fori_loop(0, rows // strip, body, 0)


def reduce_kernel(plan, spots, only, extras, pace, refs_of, *refs):
    body = functools.partial(reduce_body, plan, spots, extras, pace, refs_of(refs))
    if only is None:
        body()
    else:
        pl.when(lax.axis_index("section") == only)(body)


def stage_blocks(order):
    left = list(range(16))
    kept = []
    for bit in order:
        left = [r for r in left if not (r >> bit) & 1]
        kept.append(left)
    return kept


def reduce_body(plan, spots, extras, pace, named):
    arrays, outs = named["arrays"], named["outs"]
    own, got1, got2, got3, got4, land = (
        named[k] for k in ("own", "got1", "got2", "got3", "got4", "land")
    )
    ssem, rsem, own_sem, s4, r4, fin_sem = named["sems"]
    got = (got1, got2, got3, got4)
    count = len(plan)
    sec = lax.axis_index("section")
    grp = lax.axis_index("group")
    pos = lax.axis_index("dp")
    beside = ((sec, grp ^ 1, pos), (sec, grp ^ 2, pos))
    swaps = beside + ((sec, grp, pos ^ 1), (sec, grp, pos ^ 2))
    sides = [(sec, grp ^ j, pos) for j in (1, 2, 3)]
    line_peers = [(sec, grp, lax.rem(pos + k, 4)) for k in (1, 2, 3)]
    steps = [(jg, jz) for jg in range(4) for jz in range(4)][1:]
    kept = [stage_blocks(piece[1]) for piece in plan]

    def other(j):
        return (sec, grp ^ steps[j][0], lax.rem(pos + steps[j][1], 4))

    with_gains = "gains" in extras
    spreads = "spread" in extras
    looked = "looked" in extras
    if with_gains:
        peers = [other(j) for j in range(15)]
    elif looked:
        peers = sides + line_peers
    else:
        peers = list(swaps)
    barrier = pltpu.get_barrier_semaphore()
    for device in peers:
        pl.semaphore_signal(barrier, inc=1, device_id=device, device_id_type=MESH)
    pl.semaphore_wait(barrier, len(peers))

    def rows_of(p):
        return arrays[plan[p][0]].shape[0] // 4

    def columns_of(p):
        return arrays[plan[p][0]].shape[1]

    def sub_of(p):
        return rows_of(p) // 4 // plan[p][3]

    def block(p, r):
        line, who = pos ^ (r >> 2), grp ^ (r & 3)
        start = line * rows_of(p) + who * (rows_of(p) // 4) + plan[p][2] * sub_of(p)
        return arrays[plan[p][0]].at[rows_at(start, sub_of(p))]

    def spot(p, r):
        return kept[p][0].index(r)

    def swap(p, stage, at):
        bit = plan[p][1][stage]
        r = kept[p][stage][at] | (1 << bit)
        src = block(p, r) if stage == 0 else own[p].at[spot(p, r)]
        return remote(
            src, got[stage][p].at[at], ssem.at[p, stage, at], rsem.at[p, stage, at], swaps[bit]
        )

    def load_own(p, at):
        return pltpu.make_async_copy(block(p, kept[p][0][at]), own[p].at[at], own_sem.at[p, at])

    def order_of(p, stage):
        places = range(len(kept[p][stage]))
        if stage == 3:
            return list(places)
        bit = plan[p][1][stage + 1]
        return sorted(places, key=lambda at: 1 - ((kept[p][stage][at] >> bit) & 1))

    def begin(p):
        for at in order_of(p, 0):
            swap(p, 0, at).start()
            load_own(p, at).start()

    def advance(p, stage):
        for at in order_of(p, stage):
            r = kept[p][stage][at]
            place = spot(p, r)
            if stage == 0:
                load_own(p, at).wait()
            swap(p, stage, at).wait_recv()
            terms = [
                lambda here, place=place: own[p][place, here, :],
                lambda here, at=at: got[stage][p][at, here, :],
            ]
            if stage == 3:
                settle(p, terms)
                return

            def store(here, total, place=place):
                own[p][place, here, :] = total.astype(jnp.bfloat16)

            add_rows(store, terms, sub_of(p), columns_of(p))
            bit = plan[p][1][stage + 1]
            if (r >> bit) & 1:
                swap(p, stage + 1, kept[p][stage + 1].index(r ^ (1 << bit))).start()

    pending = {}

    def write_out(p, who, term):
        rings = named["rings"][spots[p]]
        turn = pending.setdefault(spots[p], [])
        slot = len(turn) % 2
        if len(turn) >= 2:
            turn[-2].wait()
        ring = rings.at[slot]

        def store(here, total):
            rings[slot, here, :] = total

        add_rows(store, term, sub_of(p), columns_of(p))
        start = who * (rows_of(p) // 4) + plan[p][2] * sub_of(p)
        copy = pltpu.make_async_copy(
            ring, outs[plan[p][0]].at[rows_at(start, sub_of(p))], named["ring_sem"].at[spots[p], slot]
        )
        copy.start()
        turn.append(copy)

    def drain():
        for turn in pending.values():
            for copy in turn[-2:]:
                copy.wait()

    def spread(p, way):
        if way < 2:
            here = land[p].at[grp]
            return remote(here, here, s4.at[p, way], r4.at[p, way], beside[way])
        half = columns_of(p) // 2
        there = land[p].at[grp ^ (way - 1), :, pl.ds(half * (way - 2), half)]
        return remote(there, there, s4.at[p, way], r4.at[p, way], beside[3 - way])

    def settle(p, terms):
        mine = grp if spreads else 0

        def store(here, total):
            land[p][mine, here, :] = total.astype(jnp.bfloat16)

        add_rows(store, terms, sub_of(p), columns_of(p))
        if spreads:
            spread(p, 0).start()
            spread(p, 1).start()
        else:
            own_out(p).start()

    def own_out(p):
        return pltpu.make_async_copy(
            land[p].at[0], outs[plan[p][0]].at[rows_at(plan[p][2] * sub_of(p), sub_of(p))], fin_sem.at[p]
        )

    def arrival(p, way):
        who = (grp ^ 1, grp ^ 2)[way]
        return remote(land[p].at[who], land[p].at[who], s4.at[p, way], r4.at[p, way], beside[way])

    def pass_on(p):
        if spreads:
            for way in (0, 1):
                arrival(p, way).wait_recv()
                spread(p, way + 2).start()

    def write_near(p):
        if spreads:
            for who in (grp, grp ^ 1, grp ^ 2):
                write_out(p, who, [lambda here, who=who: land[p][who, here, :]])

    def write_far(p):
        if spreads:
            spread(p, 2).wait_recv()
            spread(p, 3).wait_recv()
            write_out(p, grp ^ 3, [lambda here: land[p][grp ^ 3, here, :]])

    if with_gains:
        gain_in, gain_got, sg, rg, gain_sem = named["gain_scratch"]

        def gain_copy(j):
            device = other(j)
            return remote(gain_in.at[device[2]], gain_got.at[j], sg.at[j], rg.at[j], device)

        gain_load = pltpu.make_async_copy(named["gains"], gain_in, gain_sem)
        gain_load.start()

    if looked:
        looks, looks_own, sl, rl, table_fin, tland, tsum = named["look_scratch"]
        ids, look_in, fin_in = named["look_in"]
        vocab_quarter = fin_in.shape[0]
        look_load = pltpu.make_async_copy(look_in, looks.at[grp, pos], looks_own.at[0])
        fin_load = pltpu.make_async_copy(fin_in, table_fin, looks_own.at[1])

        def look_line(k):
            here = looks.at[grp, pos]
            return remote(here, here, sl.at[k], rl.at[k], line_peers[k])

        def look_side(k):
            here = looks.at[grp]
            return remote(here, here, sl.at[3 + k], rl.at[3 + k], sides[k])

        def table_spread(way):
            if way < 2:
                here = tland.at[grp]
                return remote(here, here, sl.at[6 + way], rl.at[6 + way], beside[way])
            half = tland.shape[2] // 2
            there = tland.at[grp ^ (way - 1), :, pl.ds(half * (way - 2), half)]
            return remote(there, there, sl.at[6 + way], rl.at[6 + way], beside[3 - way])

        def table_out(who):
            return pltpu.make_async_copy(
                tland.at[who],
                named["table_out"].at[rows_at(who * vocab_quarter, vocab_quarter)],
                looks_own.at[2 + who],
            )

        def look_begin():
            look_load.start()
            fin_load.start()
            look_load.wait()
            for k in range(3):
                look_line(k).start()

        def look_middle():
            for k in range(3):
                look_line(k).wait_recv()
            for k in range(3):
                look_side(k).start()

        def look_sum():
            for k in range(3):
                look_side(k).wait_recv()
            fin_load.wait()
            base = pos * (4 * vocab_quarter) + grp * vocab_quarter
            tall = 256
            names = lax.broadcasted_iota(jnp.int32, (tall, ids.shape[2]), 0)

            def body(at, carry):
                here = rows_at(at * tall, tall)
                total = table_fin[here, :].astype(jnp.float32)
                for g in range(4):
                    for z in range(4):
                        hit = names + (base + at * tall) == ids[g * 4 + z]
                        total = total + dot_nn(
                            jnp.where(hit, 1.0, 0.0).astype(jnp.bfloat16), looks[g, z]
                        )
                tland[grp, here, :] = total.astype(jnp.bfloat16)
                return carry

            lax.fori_loop(0, vocab_quarter // tall, body, 0)
            table_spread(0).start()
            table_spread(1).start()

        def look_pass():
            for way in (0, 1):
                who = (grp ^ 1, grp ^ 2)[way]
                remote(
                    tland.at[who], tland.at[who], sl.at[6 + way], rl.at[6 + way], beside[way]
                ).wait_recv()
                table_spread(way + 2).start()

        def look_end():
            table_spread(2).wait_recv()
            table_spread(3).wait_recv()
            for who in range(4):
                table_out(who).start()
            for who in range(4):
                table_out(who).wait()
            for k in range(3):
                look_line(k).wait_send()
                look_side(k).wait_send()
            for way in range(4):
                table_spread(way).wait_send()

        def on_first(run):
            pl.when(sec == 0)(run)

    else:

        def on_first(run):
            pass

        look_begin = look_middle = look_sum = look_pass = look_end = None

    ahead, lag, lag_end = pace
    on_first(look_begin)
    for p in range(min(ahead, count)):
        begin(p)
    if with_gains:
        gain_load.wait()
        for j in range(15):
            gain_copy(j).start()
    delays = [0, lag, 2 * lag, 3 * lag, 3 * lag + lag_end, 3 * lag + 2 * lag_end, 3 * lag + 3 * lag_end]
    for at in range(count + delays[-1]):
        if ahead + at < count:
            begin(ahead + at)
        for stage in range(4):
            if 0 <= at - delays[stage] < count:
                advance(at - delays[stage], stage)
        for run, delay in zip((pass_on, write_near, write_far), delays[4:]):
            if 0 <= at - delay < count:
                run(at - delay)
        for when, run in ((1, look_middle), (3, look_sum), (5, look_pass)):
            if at == when * (count + delays[3]) // 6:
                on_first(run)
    if with_gains:
        for j in range(15):
            gain_copy(j).wait_recv()
        total = gain_in[pos]
        for j in range(15):
            total = total + gain_got[j]
        named["gain_out"][...] = total
    on_first(look_end)
    drain()
    for p in range(count):
        if spreads:
            for way in range(4):
                spread(p, way).wait_send()
        else:
            own_out(p).wait()
        for stage in range(4):
            for at in range(len(kept[p][stage])):
                swap(p, stage, at).wait_send()
    if with_gains:
        for j in range(15):
            gain_copy(j).wait_send()


def reduce_all(arrays, plan, only, collective_id, pace, gains=None, look=None, spread=True):
    low, f32, dma = jnp.bfloat16, jnp.float32, pltpu.SemaphoreType.DMA
    extras = ("spread",) * spread + ("gains",) * (gains is not None) + ("looked",) * (look is not None)
    count = len(plan)
    inputs = list(arrays)
    kind = f32 if spread else low
    share = 4 if spread else 16
    outs = [jax.ShapeDtypeStruct((x.shape[0] // share, x.shape[1]), kind) for x in arrays]
    out_specs = [ANYWHERE] * len(arrays)
    in_specs = [ANYWHERE] * len(arrays)
    names = ["own", "got1", "got2", "got3", "got4", "land"]
    scratch = {name: [] for name in names}
    ring_shapes = []
    spots = []
    for src, _, _, chunks in plan:
        rows, columns = arrays[src].shape[0] // 4, arrays[src].shape[1]
        sub = rows // 4 // chunks
        for name, blocks in zip(names, (8, 8, 4, 2, 1, 4 if spread else 1)):
            scratch[name].append(pltpu.VMEM((blocks, sub, columns), low))
        if (sub, columns) not in ring_shapes:
            ring_shapes.append((sub, columns))
        spots.append(ring_shapes.index((sub, columns)))
    flat = [item for name in names for item in scratch[name]]
    sems = [dma((count, 4, 8))] * 2 + [dma((count, 8))] + [dma((count, 4))] * 2 + [dma((count,))]
    tail = []
    if spread:
        tail += [pltpu.VMEM((2,) + shape, f32) for shape in ring_shapes] + [dma((len(ring_shapes), 2))]
    if gains is not None:
        inputs.append(gains)
        in_specs.append(ANYWHERE)
        outs.append(jax.ShapeDtypeStruct(gains.shape[1:], f32))
        out_specs.append(IN_VMEM)
        tail += [
            pltpu.VMEM(gains.shape, f32),
            pltpu.VMEM((15,) + gains.shape[1:], f32),
            dma((15,)),
            dma((15,)),
            dma,
        ]
    if look is not None:
        ids, rows_in, fin_in = look
        inputs += [ids, rows_in, fin_in]
        in_specs += [IN_VMEM, ANYWHERE, ANYWHERE]
        quarter, emb = fin_in.shape
        outs.append(jax.ShapeDtypeStruct((4 * quarter, emb), low))
        out_specs.append(ANYWHERE)
        tail += [
            pltpu.VMEM((4, 4) + rows_in.shape, low),
            dma((6,)),
            dma((10,)),
            dma((10,)),
            pltpu.VMEM(fin_in.shape, low),
            pltpu.VMEM((4, quarter, emb), low),
            pltpu.VMEM((8, 128), f32),
        ]

    def refs_of(refs):
        at = 0

        def take(n):
            nonlocal at
            at += n
            return list(refs[at - n : at])

        named = {"arrays": take(len(arrays))}
        if gains is not None:
            named["gains"] = take(1)[0]
        if look is not None:
            named["look_in"] = take(3)
        named["outs"] = take(len(arrays))
        if gains is not None:
            named["gain_out"] = take(1)[0]
        if look is not None:
            named["table_out"] = take(1)[0]
        for name in names:
            named[name] = take(count)
        named["sems"] = take(6)
        if spread:
            named["rings"] = take(len(ring_shapes))
            named["ring_sem"] = take(1)[0]
        if gains is not None:
            named["gain_scratch"] = take(5)
        if look is not None:
            named["look_scratch"] = take(7)
        return named

    return pl.pallas_call(
        functools.partial(reduce_kernel, plan, tuple(spots), only, extras, pace, refs_of),
        out_shape=outs,
        in_specs=in_specs,
        out_specs=out_specs,
        scratch_shapes=flat + sems + tail,
        compiler_params=pltpu.CompilerParams(
            collective_id=collective_id, has_side_effects=True, vmem_limit_bytes=60 << 20
        ),
    )(*inputs)


def nothing_like(run):
    return jax.tree.map(lambda a: jnp.zeros(a.shape, a.dtype), jax.eval_shape(run))


def only_on(live, run):
    return lax.cond(live, run, lambda: nothing_like(run))


X_FIRST = (0, 1, 2, 3)
Y_FIRST = (1, 0, 2, 3)
Z_THEN_X = (2, 0, 1, 3)
Z_THEN_Y = (2, 1, 0, 3)
ORDERS = (X_FIRST, Z_THEN_Y, Y_FIRST, Z_THEN_X)
LAYER_PLAN = (
    tuple((0, ORDERS[chunk], chunk, 4) for chunk in range(4))
    + tuple((1, ORDERS[chunk], chunk, 4) for chunk in range(4))
    + tuple((4, ORDERS[chunk], chunk, 4) for chunk in range(4))
    + ((3, Y_FIRST, 0, 2), (3, Z_THEN_X, 1, 2), (2, X_FIRST, 0, 1))
)
TABLE_PLAN = tuple((0, ORDERS[chunk], chunk, 4) for chunk in range(4))
LAYER_PACE = (8, 4, 2)
TABLE_PACE = (4, 2, 1)


def after(value, *others):
    return lax.optimization_barrier((value,) + others)[0]


def per_device(
    tokens,
    lengths,
    levels,
    noise_rows,
    embed_table,
    w_in,
    ln_attn,
    w_qkv,
    w_proj,
    ln_mlp,
    w_up,
    w_down,
    ln_final,
    w_out,
):
    sec = lax.axis_index("section")
    pos = lax.axis_index("dp")
    first_section = sec == 0
    last_section = sec == 1
    rows = tokens.shape[0]
    seqs = lengths.shape[0]
    length = rows // seqs
    width = w_out.shape[0] * 4
    emb = w_out.shape[1]
    vocab_part = embed_table.shape[0]
    gains = jnp.concatenate(
        [ln_attn, ln_mlp, ln_final[None], jnp.zeros((13, ln_final.shape[0]), jnp.bfloat16)], 0
    )
    ids = jnp.concatenate([tokens.reshape(-1, 128), jnp.zeros((8 - rows // 128, 128), jnp.int32)], 0)
    shards = (w_qkv[0], w_proj[0], w_up[0], w_down[0], w_in, w_out, gains, ids)
    sizes = [s.shape[0] for s in shards]

    def entry(idx, whole=False):
        return (idx, 0, sizes[idx], whole)

    half = sizes[3] // 2
    wholes = gather_all(
        shards,
        (entry(7, True), entry(6, True), entry(4), entry(0), entry(1), entry(2), entry(3)),
        (entry(6, True), entry(0), entry(1, True), entry(2), (3, 0, half, True), (3, half, half, False), entry(5)),
        0,
    )
    qkv_weight, proj_weight, up_weight, down_weight, in_weight, out_weight, gain_all, line_ids = wholes
    gain_all = gain_all.reshape(4, 16, -1).astype(jnp.float32)
    gain_attn = gain_all[:, 0].reshape(-1)
    gain_mlp = gain_all[:, 1].reshape(-1)
    final_gain = gain_all[:, 2].reshape(-1)
    weights = (qkv_weight, proj_weight, up_weight, down_weight)
    gain_attn = gain_attn[None]
    gain_mlp = gain_mlp[None]
    key_valid = jnp.arange(length, dtype=jnp.int32)[None, :] < lengths[:, None]
    loss_scale = LOSS_GAIN / math.sqrt(rows * lax.axis_size(("group", "dp")))

    def look_up():
        local = line_ids.reshape(4, 8, 128)[:, : rows // 128].reshape(-1) - pos * vocab_part
        hit = local[:, None] == lax.broadcasted_iota(jnp.int32, (1, vocab_part), 1)
        return product(hit.astype(jnp.bfloat16), embed_table).astype(jnp.bfloat16)

    looked_parts = only_on(first_section, look_up).reshape(4, rows, emb)
    looked_parts, all_ids = swap_rows(looked_parts, line_ids, 1)
    all_tokens = all_ids.reshape(16, 8, 128)[:, : rows // 128].reshape(-1)
    noise_level = jnp.exp(LOG_LOW + levels.astype(jnp.float32) * (LOG_SPAN / (LEVELS - 1)))
    scale_in = lax.rsqrt(EMB_VAR + noise_level * noise_level)
    row_level = jnp.repeat(noise_level, length)[:, None]
    row_scale = jnp.repeat(scale_in, length)[:, None]

    def front():
        looked = jnp.sum(looked_parts.astype(jnp.float32), 0)
        mixed_in = ((looked + row_level * noise_rows.astype(jnp.float32)) * row_scale).astype(
            jnp.bfloat16
        )
        return mixed_in, product(mixed_in, in_weight)

    mixed_in, x_first = only_on(first_section, front)
    kept = run_forward(0, x_first, gain_attn, gain_mlp, lengths, weights, None)
    out_first = kept[9].astype(jnp.bfloat16)
    (table_full,) = gather_all(
        (after(embed_table, out_first),), ((0, 0, vocab_part, False),), (), 2
    )
    x_second = passed_along(after(out_first, table_full), "section", 1)
    kept = run_forward(1, x_second, gain_attn, gain_mlp, lengths, weights, kept)
    final_in = normed(kept[9], final_gain).astype(jnp.bfloat16)
    projected = product(final_in, out_weight).astype(jnp.bfloat16)
    projected = passed_along(projected, "section", -1)
    valid_scale = jnp.where(key_valid.reshape(1, -1), loss_scale, 0.0)
    grad_proj_a, entropy, table_g = run_vocabulary(
        0, projected, tokens[None], valid_scale, table_full
    )
    grad_proj = passed_along(grad_proj_a, "section", 1)
    (table_fin,) = reduce_all(
        (after(table_g, grad_proj),),
        TABLE_PLAN,
        0,
        3,
        TABLE_PACE,
        spread=False,
    )
    grad_top, gain_final = norm_back(kept[9], final_gain, product_nt(grad_proj, out_weight))
    made = run_backward(1, grad_top, gain_attn, gain_mlp, lengths, kept, weights, None)
    grad_first = passed_along(after(made[4], table_fin), "section", -1)
    made = run_backward(0, grad_first, gain_attn, gain_mlp, lengths, kept, weights, made)
    shape = in_weight.shape

    def front_edge():
        looked_grad = (product_nt(made[4], in_weight) * row_scale).astype(jnp.bfloat16)
        return product_tn(mixed_in, made[4]).astype(jnp.bfloat16), looked_grad

    def back_edge():
        edge = product_tn(final_in, grad_proj).astype(jnp.bfloat16)
        edge = edge.reshape(4, shape[0] // 4, shape[1]).reshape(shape)
        return edge, jnp.zeros((rows, emb), jnp.bfloat16)

    edge_g, looked_grad = lax.cond(first_section, front_edge, back_edge)
    gain_rows = made[5] + jnp.concatenate(
        [jnp.zeros((2, width)), gain_final[None], jnp.zeros((5, width))], 0
    )
    gain_rows = gain_rows.reshape(8, 4, width // 4).transpose(1, 0, 2)

    def grads_of(rows_at_once, grads):
        return product(rows_at_once, grads).astype(jnp.bfloat16)

    order = (
        grads_of(kept[6], made[1]),
        grads_of(kept[8], made[0]),
        edge_g,
        grads_of(kept[4], made[2]),
        grads_of(kept[1], made[3]),
    )
    up_r, down_r, edge_r, proj_r, qkv_r, gain_r, table_r = reduce_all(
        order,
        LAYER_PLAN,
        None,
        4,
        LAYER_PACE,
        gains=gain_rows,
        look=(all_tokens.reshape(16, 1, rows), looked_grad, table_fin),
    )
    loss_low = after(entropy, gain_r)[0].astype(jnp.bfloat16)
    mine = (table_r, edge_r, gain_r, loss_low)
    theirs = lax.ppermute(mine, "section", [(0, 1), (1, 0)])

    def pair_of(at):
        low = jnp.where(first_section, mine[at], theirs[at])
        high = jnp.where(first_section, theirs[at], mine[at])
        return low, high

    table_out = pair_of(0)[0].astype(jnp.float32)
    in_r, out_r = pair_of(1)
    final_r = pair_of(2)[1][2]
    token_loss = pair_of(3)[0]
    return (
        token_loss,
        table_out,
        in_r,
        gain_r[0][None],
        qkv_r[None],
        proj_r[None],
        gain_r[1][None],
        up_r[None],
        down_r[None],
        final_r,
        out_r.reshape(-1, emb),
    )


def solution(mesh):
    placed = (
        P(("group", "dp")),
        P(("group", "dp")),
        P(("group", "dp")),
        P(("group", "dp"), None),
        P("dp", None),
        P("dp", None),
        P("section", "dp"),
        P("section", "dp", None),
        P("section", "dp", None),
        P("section", "dp"),
        P("section", "dp", None),
        P("section", "dp", None),
        P("dp"),
        P("dp", None),
    )
    fits = (mesh.shape["section"], mesh.shape["group"], mesh.shape["dp"]) == (2, 4, 4)
    return jax.shard_map(
        per_device if fits else per_device_general,
        mesh=mesh,
        in_specs=placed,
        out_specs=(
            P(("group", "dp")),
            P("dp", None),
            P("dp", None),
            P("section", "dp"),
            P("section", "dp", None),
            P("section", "dp", None),
            P("section", "dp"),
            P("section", "dp", None),
            P("section", "dp", None),
            P("dp"),
            P("dp", None),
        ),
        check_vma=False,
    )
```

```python
import functools
import math

import jax
import jax.numpy as jnp
from jax import lax
from jax.experimental import pallas as pl
from jax.experimental.pallas import tpu as pltpu
from jax.sharding import PartitionSpec as P

HEAD = 64
LEVELS = 64
LEN = 128
MB = 2


EPS = 1e-05
LOG_LOW = -2.995732273553991
LOG_SPAN = 2.995732273553991
EMB_VAR = 0.015625
MASKED = -1e30
LOSS_GAIN = 16.0


def passed_along(x, axis, by):
    count = lax.axis_size(axis)
    pairs = [(i, i + by) for i in range(count) if 0 <= i + by < count]
    return lax.ppermute(x, axis, pairs)


def product(left_side, right_side):
    return jnp.dot(left_side, right_side, preferred_element_type=jnp.float32)


def product_tn(left_side, right_side):
    return lax.dot_general(
        left_side, right_side, (((0,), (0,)), ((), ())), preferred_element_type=jnp.float32
    )


def product_nt(left_side, right_side):
    return lax.dot_general(
        left_side, right_side, (((1,), (1,)), ((), ())), preferred_element_type=jnp.float32
    )


def normed(inputs, gain_vec):
    center = inputs - jnp.mean(inputs, -1, keepdims=True)
    return center * lax.rsqrt(jnp.mean(center * center, -1, keepdims=True) + EPS) * gain_vec


def norm_back(inputs, gain_vec, upstream):
    output, pullback = jax.vjp(normed, inputs, gain_vec)
    return pullback(upstream)


def gelu_exact(values_in):
    return jax.nn.gelu(values_in, approximate=False)


def attn_scores(split_rows, key_valid):
    scores = (
        jnp.einsum(
            "qhd,khd->hqk", split_rows[:, 0], split_rows[:, 1], preferred_element_type=jnp.float32
        )
        * 0.125
    )
    return jnp.where(key_valid[None, None, :], scores, MASKED)


def attend(qkv_rows, key_valid):
    length = qkv_rows.shape[0]
    model_width = qkv_rows.shape[1] // 3
    split_rows = qkv_rows.reshape(length, 3, model_width // HEAD, HEAD)
    scores = attn_scores(split_rows, key_valid)
    row_max = jnp.max(scores, -1, keepdims=True)
    log_total = row_max + jnp.log(jnp.sum(jnp.exp(scores - row_max), -1, keepdims=True))
    probs_low = jnp.exp(scores - log_total).astype(jnp.bfloat16)
    mixed_rows = jnp.einsum(
        "hqk,khd->qhd", probs_low, split_rows[:, 2], preferred_element_type=jnp.float32
    )
    return (mixed_rows.reshape(length, model_width).astype(jnp.bfloat16), log_total)


def attend_back(qkv_rows, key_valid, log_total, grad_mixed):
    length = qkv_rows.shape[0]
    model_width = qkv_rows.shape[1] // 3
    head_count = model_width // HEAD
    split_rows = qkv_rows.reshape(length, 3, head_count, HEAD)
    grad_heads = grad_mixed.reshape(length, head_count, HEAD)
    probs_full = jnp.exp(attn_scores(split_rows, key_valid) - log_total)
    grad_values = jnp.einsum(
        "hqk,qhd->khd",
        probs_full.astype(jnp.bfloat16),
        grad_heads,
        preferred_element_type=jnp.float32,
    )
    grad_probs = jnp.einsum(
        "qhd,khd->hqk", grad_heads, split_rows[:, 2], preferred_element_type=jnp.float32
    )
    grad_scores = (
        probs_full * (grad_probs - jnp.sum(grad_probs * probs_full, -1, keepdims=True))
    ).astype(jnp.bfloat16)
    grad_query = (
        jnp.einsum(
            "hqk,khd->qhd", grad_scores, split_rows[:, 1], preferred_element_type=jnp.float32
        )
        * 0.125
    )
    grad_key = (
        jnp.einsum(
            "hqk,qhd->khd", grad_scores, split_rows[:, 0], preferred_element_type=jnp.float32
        )
        * 0.125
    )
    stacked = jnp.stack([grad_query, grad_key, grad_values], 1).reshape(length, 3 * model_width)
    return stacked.astype(jnp.bfloat16)


def layer_forward(hidden, key_valid, weights):
    gain_attn, qkv_weight, proj_weight, gain_mlp, up_weight, down_weight = weights
    normed_in = normed(hidden, gain_attn).astype(jnp.bfloat16)
    qkv_rows = product(normed_in, qkv_weight).astype(jnp.bfloat16)
    mixed_rows, log_total = attend(qkv_rows, key_valid)
    hidden_mid = hidden + product(mixed_rows, proj_weight)
    mlp_in = normed(hidden_mid, gain_mlp).astype(jnp.bfloat16)
    pre_act = product(mlp_in, up_weight)
    activated = gelu_exact(pre_act).astype(jnp.bfloat16)
    hidden_out = hidden_mid + product(activated, down_weight)
    return (
        hidden_out,
        (
            hidden,
            normed_in,
            qkv_rows,
            log_total,
            mixed_rows,
            hidden_mid,
            mlp_in,
            pre_act,
            activated,
        ),
    )


def empty_kept(length, model_width, hidden_units, head_count):
    return (
        jnp.zeros((length, model_width), jnp.float32),
        jnp.zeros((length, model_width), jnp.bfloat16),
        jnp.zeros((length, 3 * model_width), jnp.bfloat16),
        jnp.zeros((head_count, length, 1), jnp.float32),
        jnp.zeros((length, model_width), jnp.bfloat16),
        jnp.zeros((length, model_width), jnp.float32),
        jnp.zeros((length, model_width), jnp.bfloat16),
        jnp.zeros((length, hidden_units), jnp.float32),
        jnp.zeros((length, hidden_units), jnp.bfloat16),
    )


def layer_backward(kept_vals, grad_out, key_valid, weights):
    hidden, normed_in, qkv_rows, log_total, mixed_rows, hidden_mid, mlp_in, pre_act, activated = (
        kept_vals
    )
    gain_attn, qkv_weight, proj_weight, gain_mlp, up_weight, down_weight = weights
    grad_low = grad_out.astype(jnp.bfloat16)
    grad_activated = product_nt(grad_low, down_weight)
    grad_pre = jax.vjp(gelu_exact, pre_act)[1](grad_activated)[0].astype(jnp.bfloat16)
    grad_mlp_in = product_nt(grad_pre, up_weight)
    grad_mid_norm, grad_gain_mlp = norm_back(hidden_mid, gain_mlp, grad_mlp_in)
    grad_mid = grad_out + grad_mid_norm
    grad_mid_low = grad_mid.astype(jnp.bfloat16)
    grad_mixed = product_nt(grad_mid_low, proj_weight).astype(jnp.bfloat16)
    grad_qkv = attend_back(qkv_rows, key_valid, log_total, grad_mixed)
    grad_normed = product_nt(grad_qkv, qkv_weight)
    grad_in_norm, grad_gain_attn = norm_back(hidden, gain_attn, grad_normed)
    records = (activated, grad_low, mlp_in, grad_pre, mixed_rows, grad_mid_low, normed_in, grad_qkv)
    return (grad_mid + grad_in_norm, (grad_gain_attn, grad_gain_mlp), records)


def layer_zero(length, model_width, hidden_units):
    records = (
        jnp.zeros((length, hidden_units), jnp.bfloat16),
        jnp.zeros((length, model_width), jnp.bfloat16),
        jnp.zeros((length, model_width), jnp.bfloat16),
        jnp.zeros((length, hidden_units), jnp.bfloat16),
        jnp.zeros((length, model_width), jnp.bfloat16),
        jnp.zeros((length, model_width), jnp.bfloat16),
        jnp.zeros((length, model_width), jnp.bfloat16),
        jnp.zeros((length, 3 * model_width), jnp.bfloat16),
    )
    gains = (jnp.zeros((model_width,), jnp.float32), jnp.zeros((model_width,), jnp.float32))
    return (jnp.zeros((length, model_width), jnp.float32), gains, records)


def layer_grads(records):
    activated, grad_low, mlp_in, grad_pre, mixed_rows, grad_mid_low, normed_in, grad_qkv = records
    return (
        product_tn(normed_in, grad_qkv),
        product_tn(mixed_rows, grad_mid_low),
        product_tn(mlp_in, grad_pre),
        product_tn(activated, grad_low),
    )


def embed_inputs(token_ids, noise_block, level_id, table_full):
    noise_level = jnp.exp(LOG_LOW + level_id.astype(jnp.float32) * (LOG_SPAN / (LEVELS - 1)))
    scale_in = lax.rsqrt(EMB_VAR + noise_level * noise_level)
    looked = jnp.take(table_full, token_ids, axis=0).astype(jnp.float32)
    mixed_in = ((looked + noise_level * noise_block.astype(jnp.float32)) * scale_in).astype(
        jnp.bfloat16
    )
    return (mixed_in, scale_in)


def embed_backward(token_ids, noise_block, level_id, grad_start, table_full, in_weight):
    mixed_in, scale_in = embed_inputs(token_ids, noise_block, level_id, table_full)
    grad_low = grad_start.astype(jnp.bfloat16)
    grad_looked = product_nt(grad_low, in_weight) * scale_in
    return (mixed_in, grad_low, grad_looked)


def embed_zero(length, model_width, emb_width):
    return (
        jnp.zeros((length, emb_width), jnp.bfloat16),
        jnp.zeros((length, model_width), jnp.bfloat16),
        jnp.zeros((length, emb_width), jnp.float32),
    )


def tail_pass(hidden, token_ids, key_valid, final_gain, out_weight, table_full, loss_scale):
    final_in = normed(hidden, final_gain).astype(jnp.bfloat16)
    projected = product(final_in, out_weight).astype(jnp.bfloat16)
    logits = product_nt(projected, table_full)
    row_max = jnp.max(logits, -1, keepdims=True)
    log_total = row_max + jnp.log(jnp.sum(jnp.exp(logits - row_max), -1, keepdims=True))
    vocab_ids = lax.broadcasted_iota(jnp.int32, logits.shape, 1)
    target_hit = vocab_ids == token_ids[:, None]
    picked = jnp.sum(jnp.where(target_hit, logits, 0.0), -1)
    entropy = jnp.where(key_valid, log_total[:, 0] - picked, 0.0)
    row_scale = jnp.where(key_valid, loss_scale, 0.0)[:, None]
    grad_logits = (
        (jnp.exp(logits - log_total) - target_hit.astype(jnp.float32)) * row_scale
    ).astype(jnp.bfloat16)
    grad_proj = product(grad_logits, table_full).astype(jnp.bfloat16)
    grad_final = product_nt(grad_proj, out_weight)
    grad_hidden, grad_gain = norm_back(hidden, final_gain, grad_final)
    return (grad_hidden, entropy, grad_gain, (grad_logits, projected, final_in, grad_proj))


def tail_zero(length, model_width, emb_width, vocab_rows):
    records = (
        jnp.zeros((length, vocab_rows), jnp.bfloat16),
        jnp.zeros((length, emb_width), jnp.bfloat16),
        jnp.zeros((length, model_width), jnp.bfloat16),
        jnp.zeros((length, emb_width), jnp.bfloat16),
    )
    return (
        jnp.zeros((length, model_width), jnp.float32),
        jnp.zeros((length,), jnp.float32),
        jnp.zeros((model_width,), jnp.float32),
        records,
    )


def edge_grads(tail_records, embed_records, token_ids):
    grad_logits, projected, final_in, grad_proj = tail_records
    mixed_in, grad_low, grad_looked = embed_records
    table_grad = product_tn(grad_logits, projected).at[token_ids].add(grad_looked)
    return (table_grad, product_tn(mixed_in, grad_low), product_tn(final_in, grad_proj))


def joined_rows(record_list):
    return jax.tree.map(lambda *pieces: jnp.concatenate(pieces, 0), *record_list)


def assemble(gain_attn_sum, gain_mlp_sum, layer_set, edge_set, gain_final_sum):
    return (
        gain_attn_sum[None],
        layer_set[0][None],
        layer_set[1][None],
        gain_mlp_sum[None],
        layer_set[2][None],
        layer_set[3][None],
        edge_set[0],
        edge_set[1],
        gain_final_sum,
        edge_set[2],
    )


def per_device_general(
    tokens,
    lengths,
    levels,
    noise_rows,
    embed_table,
    w_in,
    ln_attn,
    w_qkv,
    w_proj,
    ln_mlp,
    w_up,
    w_down,
    ln_final,
    w_out,
):
    gathered = (
        lax.all_gather(embed_table, "dp", axis=0, tiled=True),
        lax.all_gather(w_in, "dp", axis=0, tiled=True),
        lax.all_gather(ln_attn, "dp", axis=1, tiled=True),
        lax.all_gather(w_qkv, "dp", axis=1, tiled=True),
        lax.all_gather(w_proj, "dp", axis=1, tiled=True),
        lax.all_gather(ln_mlp, "dp", axis=1, tiled=True),
        lax.all_gather(w_up, "dp", axis=1, tiled=True),
        lax.all_gather(w_down, "dp", axis=1, tiled=True),
        lax.all_gather(ln_final, "dp", axis=0, tiled=True),
        lax.all_gather(w_out, "dp", axis=0, tiled=True),
    )
    table_full = gathered[0]
    in_weight = gathered[1]
    layer_weights = (
        gathered[2][0].astype(jnp.float32),
        gathered[3][0],
        gathered[4][0],
        gathered[5][0].astype(jnp.float32),
        gathered[6][0],
        gathered[7][0],
    )
    final_gain = gathered[8].astype(jnp.float32)
    out_weight = gathered[9]
    model_width = out_weight.shape[0]
    emb_width = out_weight.shape[1]
    vocab_rows = table_full.shape[0]
    hidden_units = layer_weights[4].shape[1]
    head_count = model_width // HEAD
    section_index = lax.axis_index("section")
    first_section = section_index == 0
    token_grid = tokens.reshape(MB, LEN)
    noise_grid = noise_rows.reshape(MB, LEN, noise_rows.shape[1])
    positions = jnp.arange(LEN, dtype=jnp.int32)
    valid_grid = positions[None, :] < lengths[:, None]
    loss_scale = LOSS_GAIN / math.sqrt(tokens.shape[0] * lax.axis_size(("group", "dp")))
    gain_attn_sum = jnp.zeros((model_width,), jnp.float32)
    gain_mlp_sum = jnp.zeros((model_width,), jnp.float32)
    gain_final_sum = jnp.zeros((model_width,), jnp.float32)
    recv_act = jnp.zeros((LEN, model_width), jnp.bfloat16)
    recv_grad = jnp.zeros((LEN, model_width), jnp.bfloat16)
    zero_rows = jnp.zeros((LEN, model_width), jnp.float32)
    kept_ticks = {}
    layer_recs = {}
    tail_recs = {}
    embed_recs = {}
    losses = []
    for moment in range(MB + 2):
        offset = moment - section_index
        fwd_valid = (offset >= 0) & (offset < MB)
        fwd_index = jnp.clip(offset, 0, MB - 1)
        ids_now = lax.dynamic_index_in_dim(token_grid, fwd_index, 0, False)
        noise_now = lax.dynamic_index_in_dim(noise_grid, fwd_index, 0, False)
        level_now = lax.dynamic_index_in_dim(levels, fwd_index, 0, False)
        valid_now = lax.dynamic_index_in_dim(valid_grid, fwd_index, 0, False)

        def first_input():
            mixed_in, scale_in = embed_inputs(ids_now, noise_now, level_now, table_full)
            return product(mixed_in, in_weight)

        layer_input = lax.cond(first_section, first_input, lambda: recv_act.astype(jnp.float32))
        hidden_out, kept_now = lax.cond(
            fwd_valid,
            lambda: layer_forward(layer_input, valid_now, layer_weights),
            lambda: (zero_rows, empty_kept(LEN, model_width, hidden_units, head_count)),
        )
        kept_ticks[moment] = kept_now
        tail_live = jnp.logical_not(first_section) & fwd_valid
        tail_grad, entropy, final_step, tail_now = lax.cond(
            tail_live,
            lambda: tail_pass(
                hidden_out, ids_now, valid_now, final_gain, out_weight, table_full, loss_scale
            ),
            lambda: tail_zero(LEN, model_width, emb_width, vocab_rows),
        )
        tail_recs[moment] = tail_now
        gain_final_sum = gain_final_sum + final_step
        back_tick = moment - 2
        late_live = 0 <= back_tick < MB
        late_index = min(max(back_tick, 0), MB - 1)
        kept_late = kept_ticks[back_tick] if back_tick >= 0 else kept_now
        kept_back = lax.cond(first_section, lambda: kept_late, lambda: kept_now)
        grad_top = jnp.where(first_section, recv_grad.astype(jnp.float32), tail_grad)
        valid_back = jnp.where(first_section, valid_grid[late_index], valid_now)
        back_live = jnp.where(first_section, late_live, fwd_valid)
        grad_start, gain_pair, layer_now = lax.cond(
            back_live,
            lambda: layer_backward(kept_back, grad_top, valid_back, layer_weights),
            lambda: layer_zero(LEN, model_width, hidden_units),
        )
        layer_recs[moment] = layer_now
        gain_attn_sum = gain_attn_sum + gain_pair[0]
        gain_mlp_sum = gain_mlp_sum + gain_pair[1]
        if late_live:
            embed_now = lax.cond(
                first_section,
                lambda: embed_backward(
                    token_grid[late_index],
                    noise_grid[late_index],
                    levels[late_index],
                    grad_start,
                    table_full,
                    in_weight,
                ),
                lambda: embed_zero(LEN, model_width, emb_width),
            )
        else:
            embed_now = embed_zero(LEN, model_width, emb_width)
        embed_recs[moment] = embed_now
        if moment < MB:
            recv_act = passed_along(hidden_out.astype(jnp.bfloat16), "section", 1)
        if 1 <= moment <= MB:
            entropy_low = entropy.astype(jnp.bfloat16)
            recv_grad, loss_back = passed_along(
                (grad_start.astype(jnp.bfloat16), entropy_low), "section", -1
            )
            losses.append(jnp.where(first_section, loss_back, entropy_low))
    chosen = [
        jax.tree.map(
            lambda early, late: jnp.where(first_section, early, late),
            layer_recs[micro + 2],
            layer_recs[micro + 1],
        )
        for micro in range(MB)
    ]
    all_layer = layer_grads(joined_rows(chosen))
    all_tail = joined_rows([tail_recs[micro + 1] for micro in range(MB)])
    all_embed = joined_rows([embed_recs[micro + 2] for micro in range(MB)])
    all_edge = edge_grads(all_tail, all_embed, tokens)
    grad_pack = assemble(gain_attn_sum, gain_mlp_sum, all_layer, all_edge, gain_final_sum)
    parted = (
        lax.psum_scatter(
            grad_pack[0].astype(jnp.bfloat16), "dp", scatter_dimension=1, tiled=True
        ).astype(jnp.float32),
        lax.psum_scatter(
            grad_pack[1].astype(jnp.bfloat16), "dp", scatter_dimension=1, tiled=True
        ).astype(jnp.float32),
        lax.psum_scatter(
            grad_pack[2].astype(jnp.bfloat16), "dp", scatter_dimension=1, tiled=True
        ).astype(jnp.float32),
        lax.psum_scatter(
            grad_pack[3].astype(jnp.bfloat16), "dp", scatter_dimension=1, tiled=True
        ).astype(jnp.float32),
        lax.psum_scatter(
            grad_pack[4].astype(jnp.bfloat16), "dp", scatter_dimension=1, tiled=True
        ).astype(jnp.float32),
        lax.psum_scatter(
            grad_pack[5].astype(jnp.bfloat16), "dp", scatter_dimension=1, tiled=True
        ).astype(jnp.float32),
        lax.psum_scatter(
            grad_pack[6].astype(jnp.bfloat16), "dp", scatter_dimension=0, tiled=True
        ).astype(jnp.float32),
        lax.psum_scatter(
            grad_pack[7].astype(jnp.bfloat16), "dp", scatter_dimension=0, tiled=True
        ).astype(jnp.float32),
        lax.psum_scatter(
            grad_pack[8].astype(jnp.bfloat16), "dp", scatter_dimension=0, tiled=True
        ).astype(jnp.float32),
        lax.psum_scatter(
            grad_pack[9].astype(jnp.bfloat16), "dp", scatter_dimension=0, tiled=True
        ).astype(jnp.float32),
    )
    layer_total = (
        lax.psum(parted[0].astype(jnp.bfloat16), "group").astype(jnp.float32),
        lax.psum(parted[1].astype(jnp.bfloat16), "group").astype(jnp.float32),
        lax.psum(parted[2].astype(jnp.bfloat16), "group").astype(jnp.float32),
        lax.psum(parted[3].astype(jnp.bfloat16), "group").astype(jnp.float32),
        lax.psum(parted[4].astype(jnp.bfloat16), "group").astype(jnp.float32),
        lax.psum(parted[5].astype(jnp.bfloat16), "group").astype(jnp.float32),
    )
    edge_total = (
        lax.psum(parted[6].astype(jnp.bfloat16), ("section", "group")).astype(jnp.float32),
        lax.psum(parted[7].astype(jnp.bfloat16), ("section", "group")).astype(jnp.float32),
        lax.psum(parted[8].astype(jnp.bfloat16), ("section", "group")).astype(jnp.float32),
        lax.psum(parted[9].astype(jnp.bfloat16), ("section", "group")).astype(jnp.float32),
    )
    token_loss = jnp.concatenate(losses)
    return (
        token_loss,
        edge_total[0],
        edge_total[1],
        layer_total[0],
        layer_total[1],
        layer_total[2],
        layer_total[3],
        layer_total[4],
        layer_total[5],
        edge_total[2],
        edge_total[3],
    )


MESH = pl.DeviceIdType.MESH
ANYWHERE = pl.BlockSpec(memory_space=pl.ANY)


def pick(index, values):
    out = values[-1]
    for at in range(len(values) - 2, -1, -1):
        out = jnp.where(index == at, values[at], out)
    return out


def rows_at(start, size):
    return pl.ds(pl.multiple_of(start, 8), size)


def remote(src, dst, send_sem, recv_sem, device):
    return pltpu.make_async_remote_copy(
        src_ref=src,
        dst_ref=dst,
        send_sem=send_sem,
        recv_sem=recv_sem,
        device_id=device,
        device_id_type=MESH,
    )


def gather_kernel(count, first_order, last_order, *refs):
    shards = refs[:count]
    wholes = refs[count : 2 * count]
    own_sem, zsend, zrecv, psend, precv, gate = refs[2 * count : 2 * count + 6]
    stage = refs[2 * count + 6 :]
    sec = lax.axis_index("section")
    grp = lax.axis_index("group")
    pos = lax.axis_index("dp")
    beside = ((sec, grp ^ 1, pos), (sec, grp ^ 2, pos))
    above = (sec, grp, pos + 1)
    below = (sec, grp, pos - 1)
    partner = (1 - sec, grp, pos)
    barrier = pltpu.get_barrier_semaphore()
    both = bool(last_order)

    def greet(device):
        pl.semaphore_signal(barrier, inc=1, device_id=device, device_id_type=MESH)

    def meet():
        for device in beside + ((partner,) if both else ()):
            greet(device)

        @pl.when(pos > 0)
        def _():
            greet(below)

        @pl.when(pos < 3)
        def _():
            greet(above)

        at_end = (pos == 0) | (pos == 3)
        pl.semaphore_wait(barrier, jnp.where(at_end, 3, 4) + (1 if both else 0))

    turn = [pick(pos, v) for v in ((3, 1, 3, 1), (2, 3, 1, 2), (1, 2, 2, 3))]

    def run(order, before, middle):
        def rows_of(slot):
            return shards[order[slot][0]].shape[0]

        def part_of(slot):
            _, _, size, whole_line = order[slot]
            return size if whole_line else size // 4

        def shift(slot, who):
            _, lo, _, whole_line = order[slot]
            return lo if whole_line else lo + who * part_of(slot)

        def block(slot, origin, who):
            return rows_at(origin * rows_of(slot) + shift(slot, who), part_of(slot))

        staged = sorted({entry[0] for entry in order})

        def load_own(idx):
            return pltpu.make_async_copy(shards[idx], stage[idx], own_sem.at[idx])

        def store_own(idx):
            rows = shards[idx].shape[0]
            return pltpu.make_async_copy(
                stage[idx], wholes[idx].at[rows_at(pos * rows, rows)], own_sem.at[idx]
            )

        def own_ends(slot):
            idx = order[slot][0]
            src = shards[idx].at[rows_at(shift(slot, grp), part_of(slot))]
            dst = wholes[idx].at[block(slot, pos, grp)]
            return (
                (pos < 3, remote(src, dst, zsend.at[slot, 0], zrecv.at[slot, 1], above)),
                (pos > 0, remote(src, dst, zsend.at[slot, 1], zrecv.at[slot, 3], below)),
            )

        def start_own(slot):
            for goes, copy in own_ends(slot):
                pl.when(goes)(copy.start)

        def origin_of(j):
            return lax.rem(pos - turn[j] + 4, 4)

        def arrived(slot, j):
            here = wholes[order[slot][0]].at[block(slot, origin_of(j), grp)]
            return remote(here, here, zsend.at[slot, 2 + j], zrecv.at[slot, turn[j]], partner)

        def onward(slot, j):
            step = jnp.where(turn[j] <= pos, 1, -1)
            to = pos + step
            here = wholes[order[slot][0]].at[block(slot, origin_of(j), grp)]
            landed = jnp.clip(turn[j] + step, 0, 3)
            copy = remote(
                here,
                here,
                zsend.at[slot, 2 + j],
                zrecv.at[slot, landed],
                (sec, grp, jnp.clip(to, 0, 3)),
            )
            return (to >= 0) & (to <= 3), copy

        def plane(slot, j, way):
            idx = order[slot][0]
            origin = origin_of(j)
            if way < 2:
                here = wholes[idx].at[block(slot, origin, grp)]
                return remote(here, here, psend.at[slot, j, way], precv.at[slot, j, way], beside[way])
            half = shards[idx].shape[1] // 2
            there = wholes[idx].at[
                block(slot, origin, grp ^ (way - 1)), pl.ds(half * (way - 2), half)
            ]
            return remote(
                there, there, psend.at[slot, j, way], precv.at[slot, j, way], beside[3 - way]
            )

        items = [(slot, j) for j in range(3) for slot in range(len(order))]
        crossing = [item for item in items if not order[item[0]][3]]

        def first(slot, j):
            arrived(slot, j).wait_recv()
            goes, copy = onward(slot, j)
            pl.when(goes)(copy.start)
            if (slot, j) in crossing:
                plane(slot, j, 0).start()
                plane(slot, j, 1).start()

        def second(slot, j):
            if (slot, j) in crossing:
                for way in (0, 1):
                    plane(slot, j, way).wait_recv()
                    plane(slot, j, way + 2).start()

        if before is not None:
            before()
        for slot in range(len(order)):
            start_own(slot)
        for idx in staged:
            load_own(idx).start()
        lag = 4
        for at in range(len(items) + lag):
            if at < len(items):
                slot, j = items[at]
                if j == 1 and slot < len(staged):
                    load_own(staged[slot]).wait()
                    store_own(staged[slot]).start()
                first(slot, j)
            if at == len(items) - 1 and middle is not None:
                middle()
            if at >= lag:
                second(*items[at - lag])
        for slot, j in crossing:
            plane(slot, j, 2).wait_recv()
            plane(slot, j, 3).wait_recv()
        for idx in staged:
            store_own(idx).wait()
        for slot in range(len(order)):
            for goes, copy in own_ends(slot):
                pl.when(goes)(copy.wait_send)
        for slot, j in items:
            goes, copy = onward(slot, j)
            pl.when(goes)(copy.wait_send)
        for slot, j in crossing:
            for way in range(4):
                plane(slot, j, way).wait_send()

    def let_go():
        pl.semaphore_signal(gate, inc=1, device_id=partner, device_id_type=MESH)

    def hold():
        pl.semaphore_wait(gate, 1)

    if both:
        meet()

        @pl.when(sec == 0)
        def _():
            run(first_order, None, let_go)

        @pl.when(sec == 1)
        def _():
            run(last_order, hold, None)

    else:

        @pl.when(sec == 0)
        def _():
            meet()
            run(first_order, None, None)


def gather_all(shards, first_order, last_order, collective_id):
    count = len(shards)
    slots = max(len(first_order), len(last_order))
    return pl.pallas_call(
        functools.partial(gather_kernel, count, first_order, last_order),
        out_shape=[jax.ShapeDtypeStruct((s.shape[0] * 4, s.shape[1]), s.dtype) for s in shards],
        in_specs=[ANYWHERE] * count,
        out_specs=[ANYWHERE] * count,
        scratch_shapes=[
            pltpu.SemaphoreType.DMA((count,)),
            pltpu.SemaphoreType.DMA((slots, 5)),
            pltpu.SemaphoreType.DMA((slots, 4)),
            pltpu.SemaphoreType.DMA((slots, 3, 4)),
            pltpu.SemaphoreType.DMA((slots, 3, 4)),
            pltpu.SemaphoreType.REGULAR,
        ]
        + [pltpu.VMEM(s.shape, s.dtype) for s in shards],
        compiler_params=pltpu.CompilerParams(
            collective_id=collective_id, has_side_effects=True, vmem_limit_bytes=60 << 20
        ),
    )(*shards)


def swap_kernel(rows_ref, ids_ref, out_ref, ids_out, own_sem, send_sem, recv_sem):
    sec = lax.axis_index("section")
    grp = lax.axis_index("group")
    pos = lax.axis_index("dp")

    @pl.when(sec == 0)
    def _():
        barrier = pltpu.get_barrier_semaphore()
        peers = [(sec, grp, lax.rem(pos + k, 4)) for k in (1, 2, 3)]
        sides = [(sec, grp ^ j, pos) for j in (1, 2, 3)]
        for device in peers + sides:
            pl.semaphore_signal(barrier, inc=1, device_id=device, device_id_type=MESH)
        pl.semaphore_wait(barrier, 6)
        copies = []
        for k, device in enumerate(peers):
            copies.append(
                remote(rows_ref.at[device[2]], out_ref.at[pos], send_sem.at[k], recv_sem.at[k], device)
            )
        for k, device in enumerate(sides):
            copies.append(
                remote(ids_ref, ids_out.at[grp], send_sem.at[3 + k], recv_sem.at[3 + k], device)
            )
        for copy in copies:
            copy.start()
        own_rows = pltpu.make_async_copy(rows_ref.at[pos], out_ref.at[pos], own_sem.at[0])
        own_ids = pltpu.make_async_copy(ids_ref, ids_out.at[grp], own_sem.at[1])
        own_rows.start()
        own_ids.start()
        own_rows.wait()
        own_ids.wait()
        for copy in copies:
            copy.wait()


def swap_rows(rows, ids, collective_id):
    in_vmem = pl.BlockSpec(memory_space=pltpu.VMEM)
    return pl.pallas_call(
        swap_kernel,
        out_shape=[
            jax.ShapeDtypeStruct(rows.shape, rows.dtype),
            jax.ShapeDtypeStruct((4,) + ids.shape, ids.dtype),
        ],
        in_specs=[in_vmem] * 2,
        out_specs=[in_vmem] * 2,
        scratch_shapes=[
            pltpu.SemaphoreType.DMA((2,)),
            pltpu.SemaphoreType.DMA((6,)),
            pltpu.SemaphoreType.DMA((6,)),
        ],
        compiler_params=pltpu.CompilerParams(collective_id=collective_id, has_side_effects=True),
    )(rows, ids)


IN_VMEM = pl.BlockSpec(memory_space=pltpu.VMEM)
IN_SMEM = pl.BlockSpec(memory_space=pltpu.SMEM)
ROOT_HALF = 0.7071067811865476
ROOT_TWO_PI = 0.3989422804014327


def dot_nn(left, right):
    return lax.dot_general(
        left, right, (((1,), (0,)), ((), ())), preferred_element_type=jnp.float32
    )


def dot_nt(left, right):
    return lax.dot_general(
        left, right, (((1,), (1,)), ((), ())), preferred_element_type=jnp.float32
    )


def dot_tn(left, right):
    return lax.dot_general(
        left, right, (((0,), (0,)), ((), ())), preferred_element_type=jnp.float32
    )


def unit_rows(v):
    center = v - jnp.mean(v, -1, keepdims=True)
    scale = lax.rsqrt(jnp.mean(center * center, -1, keepdims=True) + EPS)
    return center * scale, scale


def split_heads(pair):
    low = lax.broadcasted_iota(jnp.int32, pair.shape, 1) < HEAD
    nothing = jnp.zeros_like(pair)
    return jnp.concatenate([jnp.where(low, pair, nothing), jnp.where(low, nothing, pair)], 0)


def join_heads(stacked):
    half = stacked.shape[0] // 2
    low = lax.broadcasted_iota(jnp.int32, (half, stacked.shape[1]), 1) < HEAD
    return jnp.where(low, stacked[:half], stacked[half:])


def pair_scores(keys, stacked_queries, key_count):
    scores = dot_nt(keys, stacked_queries) * 0.125
    valid = lax.broadcasted_iota(jnp.int32, scores.shape, 0) < key_count
    return jnp.where(valid, scores, MASKED)


STRIP = 64


def forward_kernel(only, tile, given, *refs):
    x, gain_attn, gain_mlp, counts, wq, wp, wu, wd = refs[:8]
    rest = refs[8 + given :]
    outs = rest[:KEPT_COUNT]
    qv, pv, uv, dv = rest[KEPT_COUNT : KEPT_COUNT + 4]
    kept = rest[KEPT_COUNT + 4 : 2 * KEPT_COUNT + 4]
    a, att, m, acc, wsem, osem = rest[2 * KEPT_COUNT + 4 :]
    xv, at_t, qkv, lse, att_t, mid, m_t, pre, act_t, out = kept
    rows, width = a.shape
    units = dv.shape[0]

    def store(idx):
        return pltpu.make_async_copy(kept[idx], outs[idx], osem.at[idx])

    def run():
        loads = []

        def load(src, dst):
            copy = pltpu.make_async_copy(src, dst, wsem.at[len(loads)])
            copy.start()
            loads.append(copy)

        for lo in range(0, 3 * width, tile):
            load(wq.at[:, pl.ds(lo, tile)], qv.at[:, pl.ds(lo, tile)])
        load(wp, pv)
        for lo in range(0, units, tile):
            load(wu.at[:, pl.ds(lo, tile)], uv.at[:, pl.ds(lo, tile)])
            load(wd.at[pl.ds(lo, tile)], dv.at[pl.ds(lo, tile)])
        loads = iter(loads)
        for lo in range(0, rows, STRIP):
            here = pl.ds(lo, STRIP)
            xv[here, :] = x[here, :].astype(jnp.float32)
            a[here, :] = (unit_rows(xv[here, :])[0] * gain_attn[...]).astype(jnp.bfloat16)
        store(0).start()
        for lo in range(0, 3 * width, tile):
            next(loads).wait()
            cols = pl.ds(lo, tile)
            qkv[:, cols] = dot_nn(a[...], qv[:, cols]).astype(jnp.bfloat16)
        store(2).start()
        for lo in range(0, width, 256):
            at_t[pl.ds(lo, 256), :] = a[:, pl.ds(lo, 256)].T
        store(1).start()
        pairs = width // 128
        for seq in range(rows // LEN):
            here = pl.ds(seq * LEN, LEN)
            for pair in range(pairs):
                stacked = split_heads(qkv[here, pl.ds(pair * 128, 128)])
                scores = pair_scores(qkv[here, pl.ds(width + pair * 128, 128)], stacked, counts[seq])
                top = jnp.max(scores, 0, keepdims=True)
                power = jnp.exp(scores - top)
                total = jnp.sum(power, 0, keepdims=True)
                lse[seq * pairs + pair] = top + jnp.log(total)
                probs = (power * (1.0 / total)).astype(jnp.bfloat16)
                mixed = dot_tn(probs, qkv[here, pl.ds(2 * width + pair * 128, 128)])
                att[here, pl.ds(pair * 128, 128)] = join_heads(mixed).astype(jnp.bfloat16)
        store(3).start()
        for lo in range(0, width, 256):
            att_t[pl.ds(lo, 256), :] = att[:, pl.ds(lo, 256)].T
        store(4).start()
        next(loads).wait()
        for lo in range(0, width, tile):
            cols = pl.ds(lo, tile)
            mid[:, cols] = xv[:, cols] + dot_nn(att[...], pv[:, cols])
        for lo in range(0, rows, STRIP):
            here = pl.ds(lo, STRIP)
            m[here, :] = (unit_rows(mid[here, :])[0] * gain_mlp[...]).astype(jnp.bfloat16)
        store(5).start()
        acc[...] = mid[...]
        for lo in range(0, units, tile):
            cols = pl.ds(lo, tile)
            next(loads).wait()
            before = dot_nn(m[...], uv[:, cols])
            pre[:, cols] = before
            active = (0.5 * before * (1.0 + lax.erf(before * ROOT_HALF))).astype(jnp.bfloat16)
            act_t[cols, :] = active.T
            next(loads).wait()
            acc[...] += dot_nn(active, dv[cols, :])
        store(7).start()
        store(8).start()
        for lo in range(0, width, 256):
            m_t[pl.ds(lo, 256), :] = m[:, pl.ds(lo, 256)].T
        store(6).start()
        out[...] = acc[...]
        store(9).start()
        for idx in range(KEPT_COUNT):
            store(idx).wait()

    pl.when(lax.axis_index("section") == only)(run)


KEPT_COUNT = 10


def kept_shapes(rows, width, units):
    f32, low = jnp.float32, jnp.bfloat16
    return [
        jax.ShapeDtypeStruct(shape, kind)
        for shape, kind in (
            ((rows, width), f32),
            ((width, rows), low),
            ((rows, 3 * width), low),
            ((rows // LEN * width // 128, 1, 2 * LEN), f32),
            ((width, rows), low),
            ((rows, width), f32),
            ((width, rows), low),
            ((rows, units), f32),
            ((units, rows), low),
            ((rows, width), f32),
        )
    ]


def run_forward(only, x, gain_attn, gain_mlp, counts, weights, kept):
    wq, wp, wu, wd = weights
    rows, width = x.shape
    units = wd.shape[0]
    tile = 512
    shapes = kept_shapes(rows, width, units)
    low = jnp.bfloat16
    given = 0 if kept is None else KEPT_COUNT
    in_specs = [IN_VMEM] * 3 + [IN_SMEM] + [ANYWHERE] * (4 + given)
    return pl.pallas_call(
        functools.partial(forward_kernel, only, tile, given),
        out_shape=shapes,
        in_specs=in_specs,
        out_specs=[ANYWHERE] * KEPT_COUNT,
        input_output_aliases={8 + idx: idx for idx in range(given)},
        scratch_shapes=[pltpu.VMEM(w.shape, w.dtype) for w in weights]
        + [pltpu.VMEM(s.shape, s.dtype) for s in shapes]
        + [
            pltpu.VMEM((rows, width), low),
            pltpu.VMEM((rows, width), low),
            pltpu.VMEM((rows, width), low),
            pltpu.VMEM((rows, width), jnp.float32),
            pltpu.SemaphoreType.DMA((3 * width // tile + 1 + 2 * units // tile,)),
            pltpu.SemaphoreType.DMA((KEPT_COUNT,)),
        ],
        compiler_params=pltpu.CompilerParams(vmem_limit_bytes=56 << 20),
    )(x, gain_attn, gain_mlp, counts, wq, wp, wu, wd, *(kept or ()))


GRAD_COUNT = 6


def grad_shapes(rows, width, units):
    f32, low = jnp.float32, jnp.bfloat16
    return [
        jax.ShapeDtypeStruct(shape, kind)
        for shape, kind in (
            ((rows, width), low),
            ((rows, units), low),
            ((rows, width), low),
            ((rows, 3 * width), low),
            ((rows, width), low),
            ((8, width), f32),
        )
    ]


def norm_pull(v, gain, upstream):
    unit, scale = unit_rows(v)
    pulled = upstream * gain
    inner = jnp.mean(pulled * unit, -1, keepdims=True)
    grad = (pulled - jnp.mean(pulled, -1, keepdims=True) - unit * inner) * scale
    return grad, jnp.sum(upstream * unit, 0, keepdims=True)


def backward_kernel(only, tile, given, *refs):
    grad, gain_attn, gain_mlp, counts, x_in, qkv_in, lse_in, mid_in, pre_in, wq, wp, wu, wd = refs[:13]
    rest = refs[13 + given :]
    outs = rest[:GRAD_COUNT]
    qv, pv, uv, dv = rest[GRAD_COUNT : GRAD_COUNT + 4]
    made = rest[GRAD_COUNT + 4 : 2 * GRAD_COUNT + 4]
    x, qkv, lse, mid, pre, gm, gmid, gatt, wsem, ksem, osem = rest[2 * GRAD_COUNT + 4 :]
    gy, gpre, gz, gqkv, gx, gains = made
    rows, width = gm.shape
    units = dv.shape[0]

    def store(idx):
        return pltpu.make_async_copy(made[idx], outs[idx], osem.at[idx])

    def run():
        loads = []

        def load(src, dst):
            copy = pltpu.make_async_copy(src, dst, wsem.at[len(loads)])
            copy.start()
            loads.append(copy)

        kept = [
            pltpu.make_async_copy(src, dst, ksem.at[idx])
            for idx, (src, dst) in enumerate(
                ((pre_in, pre), (mid_in, mid), (qkv_in, qkv), (lse_in, lse), (x_in, x))
            )
        ]
        kept[0].start()
        for lo in range(0, units, tile):
            load(wd.at[pl.ds(lo, tile)], dv.at[pl.ds(lo, tile)])
            load(wu.at[:, pl.ds(lo, tile)], uv.at[:, pl.ds(lo, tile)])
        for copy in kept[1:]:
            copy.start()
        load(wp, pv)
        load(wq, qv)
        loads = iter(loads)
        gy[...] = grad[...].astype(jnp.bfloat16)
        store(0).start()
        gains[...] = jnp.zeros_like(gains)
        kept[0].wait()
        gm[...] = jnp.zeros_like(gm)
        for lo in range(0, units, tile):
            cols = pl.ds(lo, tile)
            next(loads).wait()
            pulled = dot_nt(gy[...], dv[cols, :])
            before = pre[:, cols]
            slope = 0.5 * (1.0 + lax.erf(before * ROOT_HALF)) + before * (
                ROOT_TWO_PI * jnp.exp(-0.5 * before * before)
            )
            low = (pulled * slope).astype(jnp.bfloat16)
            gpre[:, cols] = low
            next(loads).wait()
            gm[...] += dot_nt(low, uv[:, cols])
        store(1).start()
        kept[1].wait()
        for lo in range(0, rows, STRIP):
            here = pl.ds(lo, STRIP)
            step, gain = norm_pull(mid[here, :], gain_mlp[...], gm[here, :])
            total = grad[here, :].astype(jnp.float32) + step
            gmid[here, :] = total
            gz[here, :] = total.astype(jnp.bfloat16)
            gains[1:2, :] += gain
        store(2).start()
        next(loads).wait()
        gatt[...] = dot_nt(gz[...], pv[...]).astype(jnp.bfloat16)
        kept[2].wait()
        kept[3].wait()
        pairs = width // 128
        for seq in range(rows // LEN):
            here = pl.ds(seq * LEN, LEN)
            for pair in range(pairs):
                own = pl.ds(pair * 128, 128)
                stacked = split_heads(qkv[here, own])
                pulled = split_heads(gatt[here, own])
                keys = qkv[here, pl.ds(width + pair * 128, 128)]
                values = qkv[here, pl.ds(2 * width + pair * 128, 128)]
                probs = jnp.exp(pair_scores(keys, stacked, counts[seq]) - lse[seq * pairs + pair])
                gprobs = dot_nt(values, pulled)
                inner = jnp.sum(probs * gprobs, 0, keepdims=True)
                gscores = (probs * (gprobs - inner)).astype(jnp.bfloat16)
                gqkv[here, own] = (join_heads(dot_tn(gscores, keys)) * 0.125).astype(jnp.bfloat16)
                gqkv[here, pl.ds(width + pair * 128, 128)] = (dot_nn(gscores, stacked) * 0.125).astype(
                    jnp.bfloat16
                )
                gqkv[here, pl.ds(2 * width + pair * 128, 128)] = dot_nn(
                    probs.astype(jnp.bfloat16), pulled
                ).astype(jnp.bfloat16)
        store(3).start()
        next(loads).wait()
        for lo in range(0, width, 256):
            gm[:, pl.ds(lo, 256)] = dot_nt(gqkv[...], qv[pl.ds(lo, 256), :])
        kept[4].wait()
        for lo in range(0, rows, STRIP):
            here = pl.ds(lo, STRIP)
            step, gain = norm_pull(x[here, :], gain_attn[...], gm[here, :])
            gx[here, :] = (gmid[here, :] + step).astype(jnp.bfloat16)
            gains[0:1, :] += gain
        store(4).start()
        store(5).start()
        for idx in range(GRAD_COUNT):
            store(idx).wait()

    pl.when(lax.axis_index("section") == only)(run)


def run_backward(only, grad, gain_attn, gain_mlp, counts, kept, weights, made):
    wq, wp, wu, wd = weights
    x, _, qkv, lse, _, mid, _, pre, _, _ = kept
    rows, width = x.shape
    units = wd.shape[0]
    tile = 512
    shapes = grad_shapes(rows, width, units)
    low, f32 = jnp.bfloat16, jnp.float32
    given = 0 if made is None else GRAD_COUNT
    in_specs = [IN_VMEM] * 3 + [IN_SMEM] + [ANYWHERE] * (9 + given)
    return pl.pallas_call(
        functools.partial(backward_kernel, only, tile, given),
        out_shape=shapes,
        in_specs=in_specs,
        out_specs=[ANYWHERE] * GRAD_COUNT,
        input_output_aliases={13 + idx: idx for idx in range(given)},
        scratch_shapes=[pltpu.VMEM(w.shape, w.dtype) for w in weights]
        + [pltpu.VMEM(s.shape, s.dtype) for s in shapes]
        + [pltpu.VMEM(s.shape, s.dtype) for s in (x, qkv, lse, mid, pre)]
        + [
            pltpu.VMEM((rows, width), f32),
            pltpu.VMEM((rows, width), f32),
            pltpu.VMEM((rows, width), low),
            pltpu.SemaphoreType.DMA((2 + 2 * units // tile,)),
            pltpu.SemaphoreType.DMA((5,)),
            pltpu.SemaphoreType.DMA((GRAD_COUNT,)),
        ],
        compiler_params=pltpu.CompilerParams(vmem_limit_bytes=56 << 20),
    )(grad, gain_attn, gain_mlp, counts, x, qkv, lse, mid, pre, wq, wp, wu, wd, *(made or ()))


def vocabulary_kernel(only, tile, proj, ids, scale, table, gproj_out, loss_out, gtable, *scratch):
    tv, gt, pall, gp, gsend, gin, stat, stats, whole, tsem, gsem, psem, prem, ssem, srem, qsem, qrem = scratch
    rows = proj.shape[0]
    vocab = tv.shape[0]
    count = vocab // tile
    sec = lax.axis_index("section")
    grp = lax.axis_index("group")
    pos = lax.axis_index("dp")
    peers = [(sec, grp, lax.rem(pos + k, 4)) for k in (1, 2, 3)]
    places = [lax.rem(pos + k, 4) for k in (1, 2, 3)]

    def run():
        load = pltpu.make_async_copy(table, tv, tsem)
        load.start()
        barrier = pltpu.get_barrier_semaphore()
        for device in peers:
            pl.semaphore_signal(barrier, inc=1, device_id=device, device_id_type=MESH)
        pall[pos] = proj[...]
        pl.semaphore_wait(barrier, 3)
        first = [
            remote(pall.at[pos], pall.at[pos], psem.at[k], prem.at[k], peers[k]) for k in range(3)
        ]
        for copy in first:
            copy.start()
        load.wait()
        for copy in first:
            copy.wait()
        line_rows = pall[...].reshape(4 * rows, pall.shape[2])

        def logits_of(at):
            return dot_nt(tv[rows_at(at * tile, tile), :], line_rows)

        def hits_of(at):
            names = lax.broadcasted_iota(jnp.int32, (tile, 4 * rows), 0) + (at * tile + pos * vocab)
            return names == ids[...]

        stat[0:1, :] = jnp.full((1, 4 * rows), MASKED, jnp.float32)
        stat[1:8, :] = jnp.zeros((7, 4 * rows), jnp.float32)

        def measure(at, carry):
            logits = logits_of(at)
            top = stat[0:1, :]
            higher = jnp.maximum(top, jnp.max(logits, 0, keepdims=True))
            stat[1:2, :] = stat[1:2, :] * jnp.exp(top - higher) + jnp.sum(
                jnp.exp(logits - higher), 0, keepdims=True
            )
            stat[2:3, :] += jnp.sum(jnp.where(hits_of(at), logits, 0.0), 0, keepdims=True)
            stat[0:1, :] = higher
            return carry

        lax.fori_loop(0, count, measure, 0)
        second = [
            remote(stat, stats.at[pos], ssem.at[k], srem.at[k], peers[k]) for k in range(3)
        ]
        for copy in second:
            copy.start()
        stats[pos] = stat[...]
        for copy in second:
            copy.wait()
        top = stats[0, 0:1, :]
        for z in (1, 2, 3):
            top = jnp.maximum(top, stats[z, 0:1, :])
        total = jnp.zeros_like(top)
        picked = jnp.zeros_like(top)
        for z in range(4):
            total = total + stats[z, 1:2, :] * jnp.exp(stats[z, 0:1, :] - top)
            picked = picked + stats[z, 2:3, :]
        log_total = top + jnp.log(total)
        whole[...] = jnp.where(scale[...] > 0, log_total - picked, 0.0)
        loss_out[...] = whole[:, pl.ds(pl.multiple_of(pos * rows, 128), rows)]
        gp[...] = jnp.zeros_like(gp)

        def pull(at, carry):
            here = rows_at(at * tile, tile)
            probs = jnp.exp(logits_of(at) - log_total)
            grads = ((probs - jnp.where(hits_of(at), 1.0, 0.0)) * scale[...]).astype(jnp.bfloat16)
            gp[...] += dot_tn(grads, tv[here, :])
            gt[here, :] = dot_nn(grads, line_rows).astype(jnp.bfloat16)
            return carry

        lax.fori_loop(0, count, pull, 0)
        keep = pltpu.make_async_copy(gt, gtable, gsem)
        keep.start()
        gsend[...] = gp[...].astype(jnp.bfloat16).reshape(gsend.shape)
        third = [
            remote(gsend.at[places[k]], gin.at[k], qsem.at[k], qrem.at[k], peers[k])
            for k in range(3)
        ]
        for copy in third:
            copy.start()
        summed = gp[rows_at(pos * rows, rows), :]
        for k in range(3):
            third[k].wait_recv()
            summed = summed + gin[k].astype(jnp.float32)
        gproj_out[...] = summed.astype(jnp.bfloat16)
        for copy in third:
            copy.wait_send()
        keep.wait()

    pl.when(sec == only)(run)


def run_vocabulary(only, proj, ids, scale, table, collective_id):
    rows, emb = proj.shape
    vocab = table.shape[0]
    low, f32, dma = jnp.bfloat16, jnp.float32, pltpu.SemaphoreType.DMA
    return pl.pallas_call(
        functools.partial(vocabulary_kernel, only, 512),
        out_shape=[
            jax.ShapeDtypeStruct((rows, emb), low),
            jax.ShapeDtypeStruct((1, rows), f32),
            jax.ShapeDtypeStruct(table.shape, low),
        ],
        in_specs=[IN_VMEM] * 3 + [ANYWHERE],
        out_specs=[IN_VMEM] * 2 + [ANYWHERE],
        scratch_shapes=[
            pltpu.VMEM(table.shape, low),
            pltpu.VMEM(table.shape, low),
            pltpu.VMEM((4, rows, emb), low),
            pltpu.VMEM((4 * rows, emb), f32),
            pltpu.VMEM((4, rows, emb), low),
            pltpu.VMEM((3, rows, emb), low),
            pltpu.VMEM((8, 4 * rows), f32),
            pltpu.VMEM((4, 8, 4 * rows), f32),
            pltpu.VMEM((1, 4 * rows), f32),
            dma,
            dma,
        ]
        + [dma((3,))] * 6,
        compiler_params=pltpu.CompilerParams(
            collective_id=collective_id, has_side_effects=True, vmem_limit_bytes=60 << 20
        ),
    )(proj, ids, scale, table)


def strip_of(rows, columns):
    strip = 16
    while 2 * strip * columns <= 65536 and rows % (2 * strip) == 0:
        strip = 2 * strip
    return strip


def add_rows(store, terms, rows, columns):
    strip = strip_of(rows, columns)

    def body(at, carry):
        here = rows_at(at * strip, strip)
        total = terms[0](here).astype(jnp.float32)
        for term in terms[1:]:
            total = total + term(here).astype(jnp.float32)
        store(here, total)
        return carry

    lax.fori_loop(0, rows // strip, body, 0)


def reduce_kernel(plan, spots, only, extras, pace, refs_of, *refs):
    body = functools.partial(reduce_body, plan, spots, extras, pace, refs_of(refs))
    if only is None:
        body()
    else:
        pl.when(lax.axis_index("section") == only)(body)


def stage_blocks(order):
    left = list(range(1 << len(order)))
    kept = []
    for bit in order:
        left = [r for r in left if not (r >> bit) & 1]
        kept.append(left)
    return kept


def reduce_body(plan, spots, extras, pace, named):
    arrays, outs = named["arrays"], named["outs"]
    own, got1, got2, got3, got4, land = (
        named[k] for k in ("own", "got1", "got2", "got3", "got4", "land")
    )
    ssem, rsem, own_sem, s4, r4, fin_sem = named["sems"]
    got = (got1, got2, got3, got4)
    count = len(plan)
    sec = lax.axis_index("section")
    grp = lax.axis_index("group")
    pos = lax.axis_index("dp")
    beside = ((sec, grp ^ 1, pos), (sec, grp ^ 2, pos))
    swaps = beside + ((sec, grp, pos ^ 1), (sec, grp, pos ^ 2))
    sides = [(sec, grp ^ j, pos) for j in (1, 2, 3)]
    line_peers = [(sec, grp, lax.rem(pos + k, 4)) for k in (1, 2, 3)]
    steps = [(jg, jz) for jg in range(4) for jz in range(4)][1:]
    kept = [stage_blocks(piece[1]) for piece in plan]

    def other(j):
        return (sec, grp ^ steps[j][0], lax.rem(pos + steps[j][1], 4))

    with_gains = "gains" in extras
    spreads = "spread" in extras
    looked = "looked" in extras
    if with_gains:
        peers = [other(j) for j in range(15)]
    elif looked:
        peers = sides + line_peers
    else:
        peers = [swaps[bit] for bit in sorted(plan[0][1])]
    barrier = pltpu.get_barrier_semaphore()
    for device in peers:
        pl.semaphore_signal(barrier, inc=1, device_id=device, device_id_type=MESH)
    pl.semaphore_wait(barrier, len(peers))

    def rows_of(p):
        return arrays[plan[p][0]].shape[0] // (len(kept[p][0]) // 2)

    def columns_of(p):
        return arrays[plan[p][0]].shape[1]

    def sub_of(p):
        return rows_of(p) // 4 // plan[p][3]

    def block(p, r):
        who = grp ^ (r & 3)
        line = pos ^ (r >> 2) if len(plan[p][1]) == 4 else 0
        start = line * rows_of(p) + who * (rows_of(p) // 4) + plan[p][2] * sub_of(p)
        return arrays[plan[p][0]].at[rows_at(start, sub_of(p))]

    def spot(p, r):
        return kept[p][0].index(r)

    def swap(p, stage, at):
        bit = plan[p][1][stage]
        r = kept[p][stage][at] | (1 << bit)
        src = block(p, r) if stage == 0 else own[p].at[spot(p, r)]
        return remote(
            src, got[stage][p].at[at], ssem.at[p, stage, at], rsem.at[p, stage, at], swaps[bit]
        )

    def load_own(p, at):
        return pltpu.make_async_copy(block(p, kept[p][0][at]), own[p].at[at], own_sem.at[p, at])

    def order_of(p, stage):
        places = range(len(kept[p][stage]))
        if stage == len(plan[p][1]) - 1:
            return list(places)
        bit = plan[p][1][stage + 1]
        return sorted(places, key=lambda at: 1 - ((kept[p][stage][at] >> bit) & 1))

    def begin(p):
        for at in order_of(p, 0):
            swap(p, 0, at).start()
            load_own(p, at).start()

    def advance(p, stage):
        for at in order_of(p, stage):
            r = kept[p][stage][at]
            place = spot(p, r)
            if stage == 0:
                load_own(p, at).wait()
            swap(p, stage, at).wait_recv()
            terms = [
                lambda here, place=place: own[p][place, here, :],
                lambda here, at=at: got[stage][p][at, here, :],
            ]
            if stage == len(plan[p][1]) - 1:
                settle(p, terms)
                return

            def store(here, total, place=place):
                own[p][place, here, :] = total.astype(jnp.bfloat16)

            add_rows(store, terms, sub_of(p), columns_of(p))
            bit = plan[p][1][stage + 1]
            if (r >> bit) & 1:
                swap(p, stage + 1, kept[p][stage + 1].index(r ^ (1 << bit))).start()

    pending = {}

    def write_out(p, who, term):
        rings = named["rings"][spots[p]]
        turn = pending.setdefault(spots[p], [])
        slot = len(turn) % 2
        if len(turn) >= 2:
            turn[-2].wait()
        ring = rings.at[slot]

        def store(here, total):
            rings[slot, here, :] = total

        add_rows(store, term, sub_of(p), columns_of(p))
        start = who * (rows_of(p) // 4) + plan[p][2] * sub_of(p)
        copy = pltpu.make_async_copy(
            ring, outs[plan[p][0]].at[rows_at(start, sub_of(p))], named["ring_sem"].at[spots[p], slot]
        )
        copy.start()
        turn.append(copy)

    def drain():
        for turn in pending.values():
            for copy in turn[-2:]:
                copy.wait()

    def spread(p, way):
        if way < 2:
            here = land[p].at[grp]
            return remote(here, here, s4.at[p, way], r4.at[p, way], beside[way])
        half = columns_of(p) // 2
        there = land[p].at[grp ^ (way - 1), :, pl.ds(half * (way - 2), half)]
        return remote(there, there, s4.at[p, way], r4.at[p, way], beside[3 - way])

    def settle(p, terms):
        mine = grp if spreads else 0

        def store(here, total):
            land[p][mine, here, :] = total.astype(jnp.bfloat16)

        add_rows(store, terms, sub_of(p), columns_of(p))
        if spreads:
            spread(p, 0).start()
            spread(p, 1).start()
        else:
            own_out(p).start()

    def own_out(p):
        return pltpu.make_async_copy(
            land[p].at[0], outs[plan[p][0]].at[rows_at(plan[p][2] * sub_of(p), sub_of(p))], fin_sem.at[p]
        )

    def arrival(p, way):
        who = (grp ^ 1, grp ^ 2)[way]
        return remote(land[p].at[who], land[p].at[who], s4.at[p, way], r4.at[p, way], beside[way])

    def pass_on(p):
        if spreads:
            for way in (0, 1):
                arrival(p, way).wait_recv()
                spread(p, way + 2).start()

    def write_near(p):
        if spreads:
            for who in (grp, grp ^ 1, grp ^ 2):
                write_out(p, who, [lambda here, who=who: land[p][who, here, :]])

    def write_far(p):
        if spreads:
            spread(p, 2).wait_recv()
            spread(p, 3).wait_recv()
            write_out(p, grp ^ 3, [lambda here: land[p][grp ^ 3, here, :]])

    if with_gains:
        gain_in, gain_got, sg, rg, gain_sem = named["gain_scratch"]

        def gain_copy(j):
            device = other(j)
            return remote(gain_in.at[device[2]], gain_got.at[j], sg.at[j], rg.at[j], device)

        gain_load = pltpu.make_async_copy(named["gains"], gain_in, gain_sem)
        gain_load.start()

    if looked:
        looks, looks_own, sl, rl, table_fin, tland, tsum = named["look_scratch"]
        ids, look_in, fin_in = named["look_in"]
        vocab_quarter = fin_in.shape[0]
        look_load = pltpu.make_async_copy(look_in, looks.at[grp, pos], looks_own.at[0])
        fin_load = pltpu.make_async_copy(fin_in, table_fin, looks_own.at[1])

        def look_line(k):
            here = looks.at[grp, pos]
            return remote(here, here, sl.at[k], rl.at[k], line_peers[k])

        def look_side(k):
            here = looks.at[grp]
            return remote(here, here, sl.at[3 + k], rl.at[3 + k], sides[k])

        def table_spread(way):
            if way < 2:
                here = tland.at[grp]
                return remote(here, here, sl.at[6 + way], rl.at[6 + way], beside[way])
            half = tland.shape[2] // 2
            there = tland.at[grp ^ (way - 1), :, pl.ds(half * (way - 2), half)]
            return remote(there, there, sl.at[6 + way], rl.at[6 + way], beside[3 - way])

        def table_out(who):
            return pltpu.make_async_copy(
                tland.at[who],
                named["table_out"].at[rows_at(who * vocab_quarter, vocab_quarter)],
                looks_own.at[2 + who],
            )

        def look_begin():
            look_load.start()
            fin_load.start()
            look_load.wait()
            for k in range(3):
                look_line(k).start()

        def look_middle():
            for k in range(3):
                look_line(k).wait_recv()
            for k in range(3):
                look_side(k).start()

        def look_sum():
            for k in range(3):
                look_side(k).wait_recv()
            fin_load.wait()
            base = pos * (4 * vocab_quarter) + grp * vocab_quarter
            tall = 256
            names = lax.broadcasted_iota(jnp.int32, (tall, ids.shape[2]), 0)

            def body(at, carry):
                here = rows_at(at * tall, tall)
                total = table_fin[here, :].astype(jnp.float32)
                for g in range(4):
                    for z in range(4):
                        hit = names + (base + at * tall) == ids[g * 4 + z]
                        total = total + dot_nn(
                            jnp.where(hit, 1.0, 0.0).astype(jnp.bfloat16), looks[g, z]
                        )
                tland[grp, here, :] = total.astype(jnp.bfloat16)
                return carry

            lax.fori_loop(0, vocab_quarter // tall, body, 0)
            table_spread(0).start()
            table_spread(1).start()

        def look_pass():
            for way in (0, 1):
                who = (grp ^ 1, grp ^ 2)[way]
                remote(
                    tland.at[who], tland.at[who], sl.at[6 + way], rl.at[6 + way], beside[way]
                ).wait_recv()
                table_spread(way + 2).start()

        def look_end():
            table_spread(2).wait_recv()
            table_spread(3).wait_recv()
            for who in range(4):
                table_out(who).start()
            for who in range(4):
                table_out(who).wait()
            for k in range(3):
                look_line(k).wait_send()
                look_side(k).wait_send()
            for way in range(4):
                table_spread(way).wait_send()

        def on_first(run):
            pl.when(sec == 0)(run)

    else:

        def on_first(run):
            pass

        look_begin = look_middle = look_sum = look_pass = look_end = None

    ahead, lag, lag_end = pace
    on_first(look_begin)
    for p in range(min(ahead, count)):
        begin(p)
    if with_gains:
        gain_load.wait()
        for j in range(15):
            gain_copy(j).start()
    delays = [0, lag, 2 * lag, 3 * lag, 3 * lag + lag_end, 3 * lag + 2 * lag_end, 3 * lag + 3 * lag_end]
    for at in range(count + delays[-1]):
        if ahead + at < count:
            begin(ahead + at)
        for stage in range(len(plan[0][1])):
            if 0 <= at - delays[stage] < count:
                advance(at - delays[stage], stage)
        for run, delay in zip((pass_on, write_near, write_far), delays[4:]):
            if 0 <= at - delay < count:
                run(at - delay)
        for when, run in ((1, look_middle), (3, look_sum), (5, look_pass)):
            if at == when * (count + delays[3]) // 6:
                on_first(run)
    if with_gains:
        for j in range(15):
            gain_copy(j).wait_recv()
        total = gain_in[pos]
        for j in range(15):
            total = total + gain_got[j]
        named["gain_out"][...] = total
    on_first(look_end)
    drain()
    for p in range(count):
        if spreads:
            for way in range(4):
                spread(p, way).wait_send()
        else:
            own_out(p).wait()
        for stage in range(len(plan[p][1])):
            for at in range(len(kept[p][stage])):
                swap(p, stage, at).wait_send()
    if with_gains:
        for j in range(15):
            gain_copy(j).wait_send()


def reduce_all(arrays, plan, only, collective_id, pace, gains=None, look=None, spread=True):
    low, f32, dma = jnp.bfloat16, jnp.float32, pltpu.SemaphoreType.DMA
    extras = ("spread",) * spread + ("gains",) * (gains is not None) + ("looked",) * (look is not None)
    count = len(plan)
    inputs = list(arrays)
    kind = f32 if spread else low
    lines = 4 if len(plan[0][1]) == 4 else 1
    share = lines if spread else 4 * lines
    outs = [jax.ShapeDtypeStruct((x.shape[0] // share, x.shape[1]), kind) for x in arrays]
    out_specs = [ANYWHERE] * len(arrays)
    in_specs = [ANYWHERE] * len(arrays)
    names = ["own", "got1", "got2", "got3", "got4", "land"]
    scratch = {name: [] for name in names}
    ring_shapes = []
    spots = []
    for src, _, _, chunks in plan:
        rows, columns = arrays[src].shape[0] // lines, arrays[src].shape[1]
        sub = rows // 4 // chunks
        held = (8, 8, 4, 2, 1) if lines == 4 else (2, 2, 1, 0, 0)
        for name, blocks in zip(names, held + (4 if spread else 1,)):
            shape = (blocks, sub, columns) if blocks else (8, 128)
            scratch[name].append(pltpu.VMEM(shape, low))
        if (sub, columns) not in ring_shapes:
            ring_shapes.append((sub, columns))
        spots.append(ring_shapes.index((sub, columns)))
    flat = [item for name in names for item in scratch[name]]
    sems = [dma((count, 4, 8))] * 2 + [dma((count, 8))] + [dma((count, 4))] * 2 + [dma((count,))]
    tail = []
    if spread:
        tail += [pltpu.VMEM((2,) + shape, f32) for shape in ring_shapes] + [dma((len(ring_shapes), 2))]
    if gains is not None:
        inputs.append(gains)
        in_specs.append(ANYWHERE)
        outs.append(jax.ShapeDtypeStruct(gains.shape[1:], f32))
        out_specs.append(IN_VMEM)
        tail += [
            pltpu.VMEM(gains.shape, f32),
            pltpu.VMEM((15,) + gains.shape[1:], f32),
            dma((15,)),
            dma((15,)),
            dma,
        ]
    if look is not None:
        ids, rows_in, fin_in = look
        inputs += [ids, rows_in, fin_in]
        in_specs += [IN_VMEM, ANYWHERE, ANYWHERE]
        quarter, emb = fin_in.shape
        outs.append(jax.ShapeDtypeStruct((4 * quarter, emb), low))
        out_specs.append(ANYWHERE)
        tail += [
            pltpu.VMEM((4, 4) + rows_in.shape, low),
            dma((6,)),
            dma((10,)),
            dma((10,)),
            pltpu.VMEM(fin_in.shape, low),
            pltpu.VMEM((4, quarter, emb), low),
            pltpu.VMEM((8, 128), f32),
        ]

    def refs_of(refs):
        at = 0

        def take(n):
            nonlocal at
            at += n
            return list(refs[at - n : at])

        named = {"arrays": take(len(arrays))}
        if gains is not None:
            named["gains"] = take(1)[0]
        if look is not None:
            named["look_in"] = take(3)
        named["outs"] = take(len(arrays))
        if gains is not None:
            named["gain_out"] = take(1)[0]
        if look is not None:
            named["table_out"] = take(1)[0]
        for name in names:
            named[name] = take(count)
        named["sems"] = take(6)
        if spread:
            named["rings"] = take(len(ring_shapes))
            named["ring_sem"] = take(1)[0]
        if gains is not None:
            named["gain_scratch"] = take(5)
        if look is not None:
            named["look_scratch"] = take(7)
        return named

    return pl.pallas_call(
        functools.partial(reduce_kernel, plan, tuple(spots), only, extras, pace, refs_of),
        out_shape=outs,
        in_specs=in_specs,
        out_specs=out_specs,
        scratch_shapes=flat + sems + tail,
        compiler_params=pltpu.CompilerParams(
            collective_id=collective_id, has_side_effects=True, vmem_limit_bytes=60 << 20
        ),
    )(*inputs)


def nothing_like(run):
    return jax.tree.map(lambda a: jnp.zeros(a.shape, a.dtype), jax.eval_shape(run))


def only_on(live, run):
    return lax.cond(live, run, lambda: nothing_like(run))


X_FIRST = (0, 1, 2, 3)
Y_FIRST = (1, 0, 2, 3)
Z_THEN_X = (2, 0, 1, 3)
Z_THEN_Y = (2, 1, 0, 3)
ORDERS = (X_FIRST, Z_THEN_Y, Y_FIRST, Z_THEN_X)
LAYER_PLAN = (
    tuple((0, ORDERS[chunk], chunk, 4) for chunk in range(4))
    + tuple((1, ORDERS[chunk], chunk, 4) for chunk in range(4))
    + tuple((4, ORDERS[chunk], chunk, 4) for chunk in range(4))
    + ((3, Y_FIRST, 0, 2), (3, Z_THEN_X, 1, 2), (2, X_FIRST, 0, 1))
)
TABLE_PLAN = tuple((0, ((0, 1), (1, 0))[chunk % 2], chunk, 4) for chunk in range(4))
LAYER_PACE = (8, 4, 2)
TABLE_PACE = (4, 2, 1)


def after(value, *others):
    return lax.optimization_barrier((value,) + others)[0]


def per_device(
    tokens,
    lengths,
    levels,
    noise_rows,
    embed_table,
    w_in,
    ln_attn,
    w_qkv,
    w_proj,
    ln_mlp,
    w_up,
    w_down,
    ln_final,
    w_out,
):
    sec = lax.axis_index("section")
    pos = lax.axis_index("dp")
    first_section = sec == 0
    last_section = sec == 1
    rows = tokens.shape[0]
    seqs = lengths.shape[0]
    length = rows // seqs
    width = w_out.shape[0] * 4
    emb = w_out.shape[1]
    vocab_part = embed_table.shape[0]
    gains = jnp.concatenate(
        [ln_attn, ln_mlp, ln_final[None], jnp.zeros((13, ln_final.shape[0]), jnp.bfloat16)], 0
    )
    ids = jnp.concatenate(
        [
            tokens.reshape(-1, 128),
            jnp.concatenate([lengths, jnp.zeros((128 - seqs,), jnp.int32)])[None],
            jnp.zeros((7 - rows // 128, 128), jnp.int32),
        ],
        0,
    )
    shards = (w_qkv[0], w_proj[0], w_up[0], w_down[0], w_in, w_out, gains, ids)
    sizes = [s.shape[0] for s in shards]

    def cut(idx, count, whole=False):
        return tuple((idx, at * sizes[idx] // count, sizes[idx] // count, whole) for at in range(count))

    layer = cut(0, 2) + cut(2, 2) + cut(3, 2)
    wholes = gather_all(
        shards,
        cut(7, 1, True) + cut(6, 1, True) + cut(4, 1) + layer + cut(1, 4, True),
        cut(6, 1, True) + layer + cut(5, 1) + cut(1, 4, True),
        0,
    )
    qkv_weight, proj_weight, up_weight, down_weight, in_weight, out_weight, gain_all, line_ids = wholes
    gain_all = gain_all.reshape(4, 16, -1).astype(jnp.float32)
    gain_attn = gain_all[:, 0].reshape(-1)
    gain_mlp = gain_all[:, 1].reshape(-1)
    final_gain = gain_all[:, 2].reshape(-1)
    weights = (qkv_weight, proj_weight, up_weight, down_weight)
    gain_attn = gain_attn[None]
    gain_mlp = gain_mlp[None]
    loss_scale = LOSS_GAIN / math.sqrt(rows * lax.axis_size(("group", "dp")))

    def look_up():
        local = line_ids.reshape(4, 8, 128)[:, : rows // 128].reshape(-1) - pos * vocab_part
        hit = local[:, None] == lax.broadcasted_iota(jnp.int32, (1, vocab_part), 1)
        return product(hit.astype(jnp.bfloat16), embed_table).astype(jnp.bfloat16)

    looked_parts = only_on(first_section, look_up).reshape(4, rows, emb)
    looked_parts, all_ids = swap_rows(looked_parts, line_ids, 1)
    all_tokens = all_ids.reshape(16, 8, 128)[:, : rows // 128].reshape(-1)
    noise_level = jnp.exp(LOG_LOW + levels.astype(jnp.float32) * (LOG_SPAN / (LEVELS - 1)))
    scale_in = lax.rsqrt(EMB_VAR + noise_level * noise_level)
    row_level = jnp.repeat(noise_level, length)[:, None]
    row_scale = jnp.repeat(scale_in, length)[:, None]

    def front():
        looked = jnp.sum(looked_parts.astype(jnp.float32), 0)
        mixed_in = ((looked + row_level * noise_rows.astype(jnp.float32)) * row_scale).astype(
            jnp.bfloat16
        )
        return mixed_in, product(mixed_in, in_weight)

    mixed_in, x_first = only_on(first_section, front)
    kept = run_forward(0, x_first, gain_attn, gain_mlp, lengths, weights, None)
    out_first = kept[9].astype(jnp.bfloat16)
    x_second = passed_along(out_first, "section", 1)
    kept = run_forward(1, x_second, gain_attn, gain_mlp, lengths, weights, kept)
    final_in = normed(kept[9], final_gain).astype(jnp.bfloat16)
    projected = product(final_in, out_weight).astype(jnp.bfloat16)
    projected = passed_along(projected, "section", -1)
    line_parts = line_ids.reshape(4, 8, 128)
    line_tokens = line_parts[:, : rows // 128].reshape(1, -1)
    line_counts = line_parts[:, rows // 128, :seqs].reshape(-1, 1)
    line_valid = jnp.arange(length, dtype=jnp.int32)[None, :] < line_counts
    line_scale = jnp.where(line_valid.reshape(1, -1), loss_scale, 0.0)
    grad_proj_a, entropy, table_g = run_vocabulary(
        0, projected, line_tokens, line_scale, embed_table, 2
    )
    grad_proj = passed_along(grad_proj_a, "section", 1)
    (table_fin,) = reduce_all(
        (after(table_g, grad_proj),),
        TABLE_PLAN,
        0,
        3,
        TABLE_PACE,
        spread=False,
    )
    grad_top, gain_final = norm_back(kept[9], final_gain, product_nt(grad_proj, out_weight))
    made = run_backward(1, grad_top, gain_attn, gain_mlp, lengths, kept, weights, None)
    grad_first = passed_along(after(made[4], table_fin), "section", -1)
    made = run_backward(0, grad_first, gain_attn, gain_mlp, lengths, kept, weights, made)
    shape = in_weight.shape

    def front_edge():
        looked_grad = (product_nt(made[4], in_weight) * row_scale).astype(jnp.bfloat16)
        return product_tn(mixed_in, made[4]).astype(jnp.bfloat16), looked_grad

    def back_edge():
        edge = product_tn(final_in, grad_proj).astype(jnp.bfloat16)
        edge = edge.reshape(4, shape[0] // 4, shape[1]).reshape(shape)
        return edge, jnp.zeros((rows, emb), jnp.bfloat16)

    edge_g, looked_grad = lax.cond(first_section, front_edge, back_edge)
    gain_rows = made[5] + jnp.concatenate(
        [jnp.zeros((2, width)), gain_final[None], jnp.zeros((5, width))], 0
    )
    gain_rows = gain_rows.reshape(8, 4, width // 4).transpose(1, 0, 2)

    def grads_of(rows_at_once, grads):
        return product(rows_at_once, grads).astype(jnp.bfloat16)

    order = (
        grads_of(kept[6], made[1]),
        grads_of(kept[8], made[0]),
        edge_g,
        grads_of(kept[4], made[2]),
        grads_of(kept[1], made[3]),
    )
    up_r, down_r, edge_r, proj_r, qkv_r, gain_r, table_r = reduce_all(
        order,
        LAYER_PLAN,
        None,
        4,
        LAYER_PACE,
        gains=gain_rows,
        look=(all_tokens.reshape(16, 1, rows), looked_grad, table_fin),
    )
    loss_low = after(entropy, gain_r)[0].astype(jnp.bfloat16)
    mine = (table_r, edge_r, gain_r, loss_low)
    theirs = lax.ppermute(mine, "section", [(0, 1), (1, 0)])

    def pair_of(at):
        low = jnp.where(first_section, mine[at], theirs[at])
        high = jnp.where(first_section, theirs[at], mine[at])
        return low, high

    table_out = pair_of(0)[0].astype(jnp.float32)
    in_r, out_r = pair_of(1)
    final_r = pair_of(2)[1][2]
    token_loss = pair_of(3)[0]
    return (
        token_loss,
        table_out,
        in_r,
        gain_r[0][None],
        qkv_r[None],
        proj_r[None],
        gain_r[1][None],
        up_r[None],
        down_r[None],
        final_r,
        out_r.reshape(-1, emb),
    )


def solution(mesh):
    placed = (
        P(("group", "dp")),
        P(("group", "dp")),
        P(("group", "dp")),
        P(("group", "dp"), None),
        P("dp", None),
        P("dp", None),
        P("section", "dp"),
        P("section", "dp", None),
        P("section", "dp", None),
        P("section", "dp"),
        P("section", "dp", None),
        P("section", "dp", None),
        P("dp"),
        P("dp", None),
    )
    fits = (mesh.shape["section"], mesh.shape["group"], mesh.shape["dp"]) == (2, 4, 4)
    return jax.shard_map(
        per_device if fits else per_device_general,
        mesh=mesh,
        in_specs=placed,
        out_specs=(
            P(("group", "dp")),
            P("dp", None),
            P("dp", None),
            P("section", "dp"),
            P("section", "dp", None),
            P("section", "dp", None),
            P("section", "dp"),
            P("section", "dp", None),
            P("section", "dp", None),
            P("dp"),
            P("dp", None),
        ),
        check_vma=False,
    )
```

```python
import functools
import math

import jax
import jax.numpy as jnp
from jax import lax
from jax.experimental import pallas as pl
from jax.experimental.pallas import tpu as pltpu
from jax.sharding import PartitionSpec as P

HEAD = 64
LEVELS = 64
LEN = 128
MB = 2


EPS = 1e-05
LOG_LOW = -2.995732273553991
LOG_SPAN = 2.995732273553991
EMB_VAR = 0.015625
MASKED = -1e30
LOSS_GAIN = 16.0


def passed_along(x, axis, by):
    count = lax.axis_size(axis)
    pairs = [(i, i + by) for i in range(count) if 0 <= i + by < count]
    return lax.ppermute(x, axis, pairs)


def product(left_side, right_side):
    return jnp.dot(left_side, right_side, preferred_element_type=jnp.float32)


def product_tn(left_side, right_side):
    return lax.dot_general(
        left_side, right_side, (((0,), (0,)), ((), ())), preferred_element_type=jnp.float32
    )


def product_nt(left_side, right_side):
    return lax.dot_general(
        left_side, right_side, (((1,), (1,)), ((), ())), preferred_element_type=jnp.float32
    )


def normed(inputs, gain_vec):
    center = inputs - jnp.mean(inputs, -1, keepdims=True)
    return center * lax.rsqrt(jnp.mean(center * center, -1, keepdims=True) + EPS) * gain_vec


def norm_back(inputs, gain_vec, upstream):
    output, pullback = jax.vjp(normed, inputs, gain_vec)
    return pullback(upstream)


def gelu_exact(values_in):
    return jax.nn.gelu(values_in, approximate=False)


def attn_scores(split_rows, key_valid):
    scores = (
        jnp.einsum(
            "qhd,khd->hqk", split_rows[:, 0], split_rows[:, 1], preferred_element_type=jnp.float32
        )
        * 0.125
    )
    return jnp.where(key_valid[None, None, :], scores, MASKED)


def attend(qkv_rows, key_valid):
    length = qkv_rows.shape[0]
    model_width = qkv_rows.shape[1] // 3
    split_rows = qkv_rows.reshape(length, 3, model_width // HEAD, HEAD)
    scores = attn_scores(split_rows, key_valid)
    row_max = jnp.max(scores, -1, keepdims=True)
    log_total = row_max + jnp.log(jnp.sum(jnp.exp(scores - row_max), -1, keepdims=True))
    probs_low = jnp.exp(scores - log_total).astype(jnp.bfloat16)
    mixed_rows = jnp.einsum(
        "hqk,khd->qhd", probs_low, split_rows[:, 2], preferred_element_type=jnp.float32
    )
    return (mixed_rows.reshape(length, model_width).astype(jnp.bfloat16), log_total)


def attend_back(qkv_rows, key_valid, log_total, grad_mixed):
    length = qkv_rows.shape[0]
    model_width = qkv_rows.shape[1] // 3
    head_count = model_width // HEAD
    split_rows = qkv_rows.reshape(length, 3, head_count, HEAD)
    grad_heads = grad_mixed.reshape(length, head_count, HEAD)
    probs_full = jnp.exp(attn_scores(split_rows, key_valid) - log_total)
    grad_values = jnp.einsum(
        "hqk,qhd->khd",
        probs_full.astype(jnp.bfloat16),
        grad_heads,
        preferred_element_type=jnp.float32,
    )
    grad_probs = jnp.einsum(
        "qhd,khd->hqk", grad_heads, split_rows[:, 2], preferred_element_type=jnp.float32
    )
    grad_scores = (
        probs_full * (grad_probs - jnp.sum(grad_probs * probs_full, -1, keepdims=True))
    ).astype(jnp.bfloat16)
    grad_query = (
        jnp.einsum(
            "hqk,khd->qhd", grad_scores, split_rows[:, 1], preferred_element_type=jnp.float32
        )
        * 0.125
    )
    grad_key = (
        jnp.einsum(
            "hqk,qhd->khd", grad_scores, split_rows[:, 0], preferred_element_type=jnp.float32
        )
        * 0.125
    )
    stacked = jnp.stack([grad_query, grad_key, grad_values], 1).reshape(length, 3 * model_width)
    return stacked.astype(jnp.bfloat16)


def layer_forward(hidden, key_valid, weights):
    gain_attn, qkv_weight, proj_weight, gain_mlp, up_weight, down_weight = weights
    normed_in = normed(hidden, gain_attn).astype(jnp.bfloat16)
    qkv_rows = product(normed_in, qkv_weight).astype(jnp.bfloat16)
    mixed_rows, log_total = attend(qkv_rows, key_valid)
    hidden_mid = hidden + product(mixed_rows, proj_weight)
    mlp_in = normed(hidden_mid, gain_mlp).astype(jnp.bfloat16)
    pre_act = product(mlp_in, up_weight)
    activated = gelu_exact(pre_act).astype(jnp.bfloat16)
    hidden_out = hidden_mid + product(activated, down_weight)
    return (
        hidden_out,
        (
            hidden,
            normed_in,
            qkv_rows,
            log_total,
            mixed_rows,
            hidden_mid,
            mlp_in,
            pre_act,
            activated,
        ),
    )


def empty_kept(length, model_width, hidden_units, head_count):
    return (
        jnp.zeros((length, model_width), jnp.float32),
        jnp.zeros((length, model_width), jnp.bfloat16),
        jnp.zeros((length, 3 * model_width), jnp.bfloat16),
        jnp.zeros((head_count, length, 1), jnp.float32),
        jnp.zeros((length, model_width), jnp.bfloat16),
        jnp.zeros((length, model_width), jnp.float32),
        jnp.zeros((length, model_width), jnp.bfloat16),
        jnp.zeros((length, hidden_units), jnp.float32),
        jnp.zeros((length, hidden_units), jnp.bfloat16),
    )


def layer_backward(kept_vals, grad_out, key_valid, weights):
    hidden, normed_in, qkv_rows, log_total, mixed_rows, hidden_mid, mlp_in, pre_act, activated = (
        kept_vals
    )
    gain_attn, qkv_weight, proj_weight, gain_mlp, up_weight, down_weight = weights
    grad_low = grad_out.astype(jnp.bfloat16)
    grad_activated = product_nt(grad_low, down_weight)
    grad_pre = jax.vjp(gelu_exact, pre_act)[1](grad_activated)[0].astype(jnp.bfloat16)
    grad_mlp_in = product_nt(grad_pre, up_weight)
    grad_mid_norm, grad_gain_mlp = norm_back(hidden_mid, gain_mlp, grad_mlp_in)
    grad_mid = grad_out + grad_mid_norm
    grad_mid_low = grad_mid.astype(jnp.bfloat16)
    grad_mixed = product_nt(grad_mid_low, proj_weight).astype(jnp.bfloat16)
    grad_qkv = attend_back(qkv_rows, key_valid, log_total, grad_mixed)
    grad_normed = product_nt(grad_qkv, qkv_weight)
    grad_in_norm, grad_gain_attn = norm_back(hidden, gain_attn, grad_normed)
    records = (activated, grad_low, mlp_in, grad_pre, mixed_rows, grad_mid_low, normed_in, grad_qkv)
    return (grad_mid + grad_in_norm, (grad_gain_attn, grad_gain_mlp), records)


def layer_zero(length, model_width, hidden_units):
    records = (
        jnp.zeros((length, hidden_units), jnp.bfloat16),
        jnp.zeros((length, model_width), jnp.bfloat16),
        jnp.zeros((length, model_width), jnp.bfloat16),
        jnp.zeros((length, hidden_units), jnp.bfloat16),
        jnp.zeros((length, model_width), jnp.bfloat16),
        jnp.zeros((length, model_width), jnp.bfloat16),
        jnp.zeros((length, model_width), jnp.bfloat16),
        jnp.zeros((length, 3 * model_width), jnp.bfloat16),
    )
    gains = (jnp.zeros((model_width,), jnp.float32), jnp.zeros((model_width,), jnp.float32))
    return (jnp.zeros((length, model_width), jnp.float32), gains, records)


def layer_grads(records):
    activated, grad_low, mlp_in, grad_pre, mixed_rows, grad_mid_low, normed_in, grad_qkv = records
    return (
        product_tn(normed_in, grad_qkv),
        product_tn(mixed_rows, grad_mid_low),
        product_tn(mlp_in, grad_pre),
        product_tn(activated, grad_low),
    )


def embed_inputs(token_ids, noise_block, level_id, table_full):
    noise_level = jnp.exp(LOG_LOW + level_id.astype(jnp.float32) * (LOG_SPAN / (LEVELS - 1)))
    scale_in = lax.rsqrt(EMB_VAR + noise_level * noise_level)
    looked = jnp.take(table_full, token_ids, axis=0).astype(jnp.float32)
    mixed_in = ((looked + noise_level * noise_block.astype(jnp.float32)) * scale_in).astype(
        jnp.bfloat16
    )
    return (mixed_in, scale_in)


def embed_backward(token_ids, noise_block, level_id, grad_start, table_full, in_weight):
    mixed_in, scale_in = embed_inputs(token_ids, noise_block, level_id, table_full)
    grad_low = grad_start.astype(jnp.bfloat16)
    grad_looked = product_nt(grad_low, in_weight) * scale_in
    return (mixed_in, grad_low, grad_looked)


def embed_zero(length, model_width, emb_width):
    return (
        jnp.zeros((length, emb_width), jnp.bfloat16),
        jnp.zeros((length, model_width), jnp.bfloat16),
        jnp.zeros((length, emb_width), jnp.float32),
    )


def tail_pass(hidden, token_ids, key_valid, final_gain, out_weight, table_full, loss_scale):
    final_in = normed(hidden, final_gain).astype(jnp.bfloat16)
    projected = product(final_in, out_weight).astype(jnp.bfloat16)
    logits = product_nt(projected, table_full)
    row_max = jnp.max(logits, -1, keepdims=True)
    log_total = row_max + jnp.log(jnp.sum(jnp.exp(logits - row_max), -1, keepdims=True))
    vocab_ids = lax.broadcasted_iota(jnp.int32, logits.shape, 1)
    target_hit = vocab_ids == token_ids[:, None]
    picked = jnp.sum(jnp.where(target_hit, logits, 0.0), -1)
    entropy = jnp.where(key_valid, log_total[:, 0] - picked, 0.0)
    row_scale = jnp.where(key_valid, loss_scale, 0.0)[:, None]
    grad_logits = (
        (jnp.exp(logits - log_total) - target_hit.astype(jnp.float32)) * row_scale
    ).astype(jnp.bfloat16)
    grad_proj = product(grad_logits, table_full).astype(jnp.bfloat16)
    grad_final = product_nt(grad_proj, out_weight)
    grad_hidden, grad_gain = norm_back(hidden, final_gain, grad_final)
    return (grad_hidden, entropy, grad_gain, (grad_logits, projected, final_in, grad_proj))


def tail_zero(length, model_width, emb_width, vocab_rows):
    records = (
        jnp.zeros((length, vocab_rows), jnp.bfloat16),
        jnp.zeros((length, emb_width), jnp.bfloat16),
        jnp.zeros((length, model_width), jnp.bfloat16),
        jnp.zeros((length, emb_width), jnp.bfloat16),
    )
    return (
        jnp.zeros((length, model_width), jnp.float32),
        jnp.zeros((length,), jnp.float32),
        jnp.zeros((model_width,), jnp.float32),
        records,
    )


def edge_grads(tail_records, embed_records, token_ids):
    grad_logits, projected, final_in, grad_proj = tail_records
    mixed_in, grad_low, grad_looked = embed_records
    table_grad = product_tn(grad_logits, projected).at[token_ids].add(grad_looked)
    return (table_grad, product_tn(mixed_in, grad_low), product_tn(final_in, grad_proj))


def joined_rows(record_list):
    return jax.tree.map(lambda *pieces: jnp.concatenate(pieces, 0), *record_list)


def assemble(gain_attn_sum, gain_mlp_sum, layer_set, edge_set, gain_final_sum):
    return (
        gain_attn_sum[None],
        layer_set[0][None],
        layer_set[1][None],
        gain_mlp_sum[None],
        layer_set[2][None],
        layer_set[3][None],
        edge_set[0],
        edge_set[1],
        gain_final_sum,
        edge_set[2],
    )


def per_device_general(
    tokens,
    lengths,
    levels,
    noise_rows,
    embed_table,
    w_in,
    ln_attn,
    w_qkv,
    w_proj,
    ln_mlp,
    w_up,
    w_down,
    ln_final,
    w_out,
):
    gathered = (
        lax.all_gather(embed_table, "dp", axis=0, tiled=True),
        lax.all_gather(w_in, "dp", axis=0, tiled=True),
        lax.all_gather(ln_attn, "dp", axis=1, tiled=True),
        lax.all_gather(w_qkv, "dp", axis=1, tiled=True),
        lax.all_gather(w_proj, "dp", axis=1, tiled=True),
        lax.all_gather(ln_mlp, "dp", axis=1, tiled=True),
        lax.all_gather(w_up, "dp", axis=1, tiled=True),
        lax.all_gather(w_down, "dp", axis=1, tiled=True),
        lax.all_gather(ln_final, "dp", axis=0, tiled=True),
        lax.all_gather(w_out, "dp", axis=0, tiled=True),
    )
    table_full = gathered[0]
    in_weight = gathered[1]
    layer_weights = (
        gathered[2][0].astype(jnp.float32),
        gathered[3][0],
        gathered[4][0],
        gathered[5][0].astype(jnp.float32),
        gathered[6][0],
        gathered[7][0],
    )
    final_gain = gathered[8].astype(jnp.float32)
    out_weight = gathered[9]
    model_width = out_weight.shape[0]
    emb_width = out_weight.shape[1]
    vocab_rows = table_full.shape[0]
    hidden_units = layer_weights[4].shape[1]
    head_count = model_width // HEAD
    section_index = lax.axis_index("section")
    first_section = section_index == 0
    token_grid = tokens.reshape(MB, LEN)
    noise_grid = noise_rows.reshape(MB, LEN, noise_rows.shape[1])
    positions = jnp.arange(LEN, dtype=jnp.int32)
    valid_grid = positions[None, :] < lengths[:, None]
    loss_scale = LOSS_GAIN / math.sqrt(tokens.shape[0] * lax.axis_size(("group", "dp")))
    gain_attn_sum = jnp.zeros((model_width,), jnp.float32)
    gain_mlp_sum = jnp.zeros((model_width,), jnp.float32)
    gain_final_sum = jnp.zeros((model_width,), jnp.float32)
    recv_act = jnp.zeros((LEN, model_width), jnp.bfloat16)
    recv_grad = jnp.zeros((LEN, model_width), jnp.bfloat16)
    zero_rows = jnp.zeros((LEN, model_width), jnp.float32)
    kept_ticks = {}
    layer_recs = {}
    tail_recs = {}
    embed_recs = {}
    losses = []
    for moment in range(MB + 2):
        offset = moment - section_index
        fwd_valid = (offset >= 0) & (offset < MB)
        fwd_index = jnp.clip(offset, 0, MB - 1)
        ids_now = lax.dynamic_index_in_dim(token_grid, fwd_index, 0, False)
        noise_now = lax.dynamic_index_in_dim(noise_grid, fwd_index, 0, False)
        level_now = lax.dynamic_index_in_dim(levels, fwd_index, 0, False)
        valid_now = lax.dynamic_index_in_dim(valid_grid, fwd_index, 0, False)

        def first_input():
            mixed_in, scale_in = embed_inputs(ids_now, noise_now, level_now, table_full)
            return product(mixed_in, in_weight)

        layer_input = lax.cond(first_section, first_input, lambda: recv_act.astype(jnp.float32))
        hidden_out, kept_now = lax.cond(
            fwd_valid,
            lambda: layer_forward(layer_input, valid_now, layer_weights),
            lambda: (zero_rows, empty_kept(LEN, model_width, hidden_units, head_count)),
        )
        kept_ticks[moment] = kept_now
        tail_live = jnp.logical_not(first_section) & fwd_valid
        tail_grad, entropy, final_step, tail_now = lax.cond(
            tail_live,
            lambda: tail_pass(
                hidden_out, ids_now, valid_now, final_gain, out_weight, table_full, loss_scale
            ),
            lambda: tail_zero(LEN, model_width, emb_width, vocab_rows),
        )
        tail_recs[moment] = tail_now
        gain_final_sum = gain_final_sum + final_step
        back_tick = moment - 2
        late_live = 0 <= back_tick < MB
        late_index = min(max(back_tick, 0), MB - 1)
        kept_late = kept_ticks[back_tick] if back_tick >= 0 else kept_now
        kept_back = lax.cond(first_section, lambda: kept_late, lambda: kept_now)
        grad_top = jnp.where(first_section, recv_grad.astype(jnp.float32), tail_grad)
        valid_back = jnp.where(first_section, valid_grid[late_index], valid_now)
        back_live = jnp.where(first_section, late_live, fwd_valid)
        grad_start, gain_pair, layer_now = lax.cond(
            back_live,
            lambda: layer_backward(kept_back, grad_top, valid_back, layer_weights),
            lambda: layer_zero(LEN, model_width, hidden_units),
        )
        layer_recs[moment] = layer_now
        gain_attn_sum = gain_attn_sum + gain_pair[0]
        gain_mlp_sum = gain_mlp_sum + gain_pair[1]
        if late_live:
            embed_now = lax.cond(
                first_section,
                lambda: embed_backward(
                    token_grid[late_index],
                    noise_grid[late_index],
                    levels[late_index],
                    grad_start,
                    table_full,
                    in_weight,
                ),
                lambda: embed_zero(LEN, model_width, emb_width),
            )
        else:
            embed_now = embed_zero(LEN, model_width, emb_width)
        embed_recs[moment] = embed_now
        if moment < MB:
            recv_act = passed_along(hidden_out.astype(jnp.bfloat16), "section", 1)
        if 1 <= moment <= MB:
            entropy_low = entropy.astype(jnp.bfloat16)
            recv_grad, loss_back = passed_along(
                (grad_start.astype(jnp.bfloat16), entropy_low), "section", -1
            )
            losses.append(jnp.where(first_section, loss_back, entropy_low))
    chosen = [
        jax.tree.map(
            lambda early, late: jnp.where(first_section, early, late),
            layer_recs[micro + 2],
            layer_recs[micro + 1],
        )
        for micro in range(MB)
    ]
    all_layer = layer_grads(joined_rows(chosen))
    all_tail = joined_rows([tail_recs[micro + 1] for micro in range(MB)])
    all_embed = joined_rows([embed_recs[micro + 2] for micro in range(MB)])
    all_edge = edge_grads(all_tail, all_embed, tokens)
    grad_pack = assemble(gain_attn_sum, gain_mlp_sum, all_layer, all_edge, gain_final_sum)
    parted = (
        lax.psum_scatter(
            grad_pack[0].astype(jnp.bfloat16), "dp", scatter_dimension=1, tiled=True
        ).astype(jnp.float32),
        lax.psum_scatter(
            grad_pack[1].astype(jnp.bfloat16), "dp", scatter_dimension=1, tiled=True
        ).astype(jnp.float32),
        lax.psum_scatter(
            grad_pack[2].astype(jnp.bfloat16), "dp", scatter_dimension=1, tiled=True
        ).astype(jnp.float32),
        lax.psum_scatter(
            grad_pack[3].astype(jnp.bfloat16), "dp", scatter_dimension=1, tiled=True
        ).astype(jnp.float32),
        lax.psum_scatter(
            grad_pack[4].astype(jnp.bfloat16), "dp", scatter_dimension=1, tiled=True
        ).astype(jnp.float32),
        lax.psum_scatter(
            grad_pack[5].astype(jnp.bfloat16), "dp", scatter_dimension=1, tiled=True
        ).astype(jnp.float32),
        lax.psum_scatter(
            grad_pack[6].astype(jnp.bfloat16), "dp", scatter_dimension=0, tiled=True
        ).astype(jnp.float32),
        lax.psum_scatter(
            grad_pack[7].astype(jnp.bfloat16), "dp", scatter_dimension=0, tiled=True
        ).astype(jnp.float32),
        lax.psum_scatter(
            grad_pack[8].astype(jnp.bfloat16), "dp", scatter_dimension=0, tiled=True
        ).astype(jnp.float32),
        lax.psum_scatter(
            grad_pack[9].astype(jnp.bfloat16), "dp", scatter_dimension=0, tiled=True
        ).astype(jnp.float32),
    )
    layer_total = (
        lax.psum(parted[0].astype(jnp.bfloat16), "group").astype(jnp.float32),
        lax.psum(parted[1].astype(jnp.bfloat16), "group").astype(jnp.float32),
        lax.psum(parted[2].astype(jnp.bfloat16), "group").astype(jnp.float32),
        lax.psum(parted[3].astype(jnp.bfloat16), "group").astype(jnp.float32),
        lax.psum(parted[4].astype(jnp.bfloat16), "group").astype(jnp.float32),
        lax.psum(parted[5].astype(jnp.bfloat16), "group").astype(jnp.float32),
    )
    edge_total = (
        lax.psum(parted[6].astype(jnp.bfloat16), ("section", "group")).astype(jnp.float32),
        lax.psum(parted[7].astype(jnp.bfloat16), ("section", "group")).astype(jnp.float32),
        lax.psum(parted[8].astype(jnp.bfloat16), ("section", "group")).astype(jnp.float32),
        lax.psum(parted[9].astype(jnp.bfloat16), ("section", "group")).astype(jnp.float32),
    )
    token_loss = jnp.concatenate(losses)
    return (
        token_loss,
        edge_total[0],
        edge_total[1],
        layer_total[0],
        layer_total[1],
        layer_total[2],
        layer_total[3],
        layer_total[4],
        layer_total[5],
        edge_total[2],
        edge_total[3],
    )


MESH = pl.DeviceIdType.MESH
ANYWHERE = pl.BlockSpec(memory_space=pl.ANY)


def pick(index, values):
    out = values[-1]
    for at in range(len(values) - 2, -1, -1):
        out = jnp.where(index == at, values[at], out)
    return out


def rows_at(start, size):
    return pl.ds(pl.multiple_of(start, 8), size)


def remote(src, dst, send_sem, recv_sem, device):
    return pltpu.make_async_remote_copy(
        src_ref=src,
        dst_ref=dst,
        send_sem=send_sem,
        recv_sem=recv_sem,
        device_id=device,
        device_id_type=MESH,
    )


def gather_kernel(count, first_order, last_order, *refs):
    shards = refs[:count]
    wholes = refs[count : 2 * count]
    own_sem, zsend, zrecv, psend, precv, gate = refs[2 * count : 2 * count + 6]
    stage = refs[2 * count + 6 :]
    sec = lax.axis_index("section")
    grp = lax.axis_index("group")
    pos = lax.axis_index("dp")
    beside = ((sec, grp ^ 1, pos), (sec, grp ^ 2, pos))
    above = (sec, grp, pos + 1)
    below = (sec, grp, pos - 1)
    partner = (1 - sec, grp, pos)
    barrier = pltpu.get_barrier_semaphore()
    both = bool(last_order)

    def greet(device):
        pl.semaphore_signal(barrier, inc=1, device_id=device, device_id_type=MESH)

    def meet():
        for device in beside + ((partner,) if both else ()):
            greet(device)

        @pl.when(pos > 0)
        def _():
            greet(below)

        @pl.when(pos < 3)
        def _():
            greet(above)

        at_end = (pos == 0) | (pos == 3)
        pl.semaphore_wait(barrier, jnp.where(at_end, 3, 4) + (1 if both else 0))

    turn = [pick(pos, v) for v in ((3, 1, 3, 1), (2, 3, 1, 2), (1, 2, 2, 3))]

    def run(order, before, middle):
        def rows_of(slot):
            return shards[order[slot][0]].shape[0]

        def part_of(slot):
            _, _, size, whole_line = order[slot]
            return size if whole_line else size // 4

        def shift(slot, who):
            _, lo, _, whole_line = order[slot]
            return lo if whole_line else lo + who * part_of(slot)

        def block(slot, origin, who):
            return rows_at(origin * rows_of(slot) + shift(slot, who), part_of(slot))

        staged = sorted({entry[0] for entry in order})

        def load_own(idx):
            return pltpu.make_async_copy(shards[idx], stage[idx], own_sem.at[idx])

        def store_own(idx):
            rows = shards[idx].shape[0]
            return pltpu.make_async_copy(
                stage[idx], wholes[idx].at[rows_at(pos * rows, rows)], own_sem.at[idx]
            )

        def own_ends(slot):
            idx = order[slot][0]
            src = shards[idx].at[rows_at(shift(slot, grp), part_of(slot))]
            dst = wholes[idx].at[block(slot, pos, grp)]
            return (
                (pos < 3, remote(src, dst, zsend.at[slot, 0], zrecv.at[slot, 1], above)),
                (pos > 0, remote(src, dst, zsend.at[slot, 1], zrecv.at[slot, 3], below)),
            )

        def start_own(slot):
            for goes, copy in own_ends(slot):
                pl.when(goes)(copy.start)

        def origin_of(j):
            return lax.rem(pos - turn[j] + 4, 4)

        def arrived(slot, j):
            here = wholes[order[slot][0]].at[block(slot, origin_of(j), grp)]
            return remote(here, here, zsend.at[slot, 2 + j], zrecv.at[slot, turn[j]], partner)

        def onward(slot, j):
            step = jnp.where(turn[j] <= pos, 1, -1)
            to = pos + step
            here = wholes[order[slot][0]].at[block(slot, origin_of(j), grp)]
            landed = jnp.clip(turn[j] + step, 0, 3)
            copy = remote(
                here,
                here,
                zsend.at[slot, 2 + j],
                zrecv.at[slot, landed],
                (sec, grp, jnp.clip(to, 0, 3)),
            )
            return (to >= 0) & (to <= 3), copy

        def plane(slot, j, way):
            idx = order[slot][0]
            origin = origin_of(j)
            if way < 2:
                here = wholes[idx].at[block(slot, origin, grp)]
                return remote(here, here, psend.at[slot, j, way], precv.at[slot, j, way], beside[way])
            half = shards[idx].shape[1] // 2
            there = wholes[idx].at[
                block(slot, origin, grp ^ (way - 1)), pl.ds(half * (way - 2), half)
            ]
            return remote(
                there, there, psend.at[slot, j, way], precv.at[slot, j, way], beside[3 - way]
            )

        items = [(slot, j) for j in range(3) for slot in range(len(order))]
        crossing = [item for item in items if not order[item[0]][3]]

        def first(slot, j):
            arrived(slot, j).wait_recv()
            goes, copy = onward(slot, j)
            pl.when(goes)(copy.start)
            if (slot, j) in crossing:
                plane(slot, j, 0).start()
                plane(slot, j, 1).start()

        def second(slot, j):
            if (slot, j) in crossing:
                for way in (0, 1):
                    plane(slot, j, way).wait_recv()
                    plane(slot, j, way + 2).start()

        if before is not None:
            before()
        for slot in range(len(order)):
            start_own(slot)
        for idx in staged:
            load_own(idx).start()
        lag = 4
        for at in range(len(items) + lag):
            if at < len(items):
                slot, j = items[at]
                if j == 1 and slot < len(staged):
                    load_own(staged[slot]).wait()
                    store_own(staged[slot]).start()
                first(slot, j)
            if at == len(items) - 1 and middle is not None:
                middle()
            if at >= lag:
                second(*items[at - lag])
        for slot, j in crossing:
            plane(slot, j, 2).wait_recv()
            plane(slot, j, 3).wait_recv()
        for idx in staged:
            store_own(idx).wait()
        for slot in range(len(order)):
            for goes, copy in own_ends(slot):
                pl.when(goes)(copy.wait_send)
        for slot, j in items:
            goes, copy = onward(slot, j)
            pl.when(goes)(copy.wait_send)
        for slot, j in crossing:
            for way in range(4):
                plane(slot, j, way).wait_send()

    def let_go():
        pl.semaphore_signal(gate, inc=1, device_id=partner, device_id_type=MESH)

    def hold():
        pl.semaphore_wait(gate, 1)

    if both:
        meet()

        @pl.when(sec == 0)
        def _():
            run(first_order, None, let_go)

        @pl.when(sec == 1)
        def _():
            run(last_order, hold, None)

    else:

        @pl.when(sec == 0)
        def _():
            meet()
            run(first_order, None, None)


def gather_all(shards, first_order, last_order, collective_id):
    count = len(shards)
    slots = max(len(first_order), len(last_order))
    return pl.pallas_call(
        functools.partial(gather_kernel, count, first_order, last_order),
        out_shape=[jax.ShapeDtypeStruct((s.shape[0] * 4, s.shape[1]), s.dtype) for s in shards],
        in_specs=[ANYWHERE] * count,
        out_specs=[ANYWHERE] * count,
        scratch_shapes=[
            pltpu.SemaphoreType.DMA((count,)),
            pltpu.SemaphoreType.DMA((slots, 5)),
            pltpu.SemaphoreType.DMA((slots, 4)),
            pltpu.SemaphoreType.DMA((slots, 3, 4)),
            pltpu.SemaphoreType.DMA((slots, 3, 4)),
            pltpu.SemaphoreType.REGULAR,
        ]
        + [pltpu.VMEM(s.shape, s.dtype) for s in shards],
        compiler_params=pltpu.CompilerParams(
            collective_id=collective_id, has_side_effects=True, vmem_limit_bytes=60 << 20
        ),
    )(*shards)


def swap_kernel(rows_ref, ids_ref, out_ref, ids_out, own_sem, send_sem, recv_sem):
    sec = lax.axis_index("section")
    grp = lax.axis_index("group")
    pos = lax.axis_index("dp")

    @pl.when(sec == 0)
    def _():
        barrier = pltpu.get_barrier_semaphore()
        peers = [(sec, grp, lax.rem(pos + k, 4)) for k in (1, 2, 3)]
        sides = [(sec, grp ^ j, pos) for j in (1, 2, 3)]
        for device in peers + sides:
            pl.semaphore_signal(barrier, inc=1, device_id=device, device_id_type=MESH)
        pl.semaphore_wait(barrier, 6)
        copies = []
        for k, device in enumerate(peers):
            copies.append(
                remote(rows_ref.at[device[2]], out_ref.at[pos], send_sem.at[k], recv_sem.at[k], device)
            )
        for k, device in enumerate(sides):
            copies.append(
                remote(ids_ref, ids_out.at[grp], send_sem.at[3 + k], recv_sem.at[3 + k], device)
            )
        for copy in copies:
            copy.start()
        own_rows = pltpu.make_async_copy(rows_ref.at[pos], out_ref.at[pos], own_sem.at[0])
        own_ids = pltpu.make_async_copy(ids_ref, ids_out.at[grp], own_sem.at[1])
        own_rows.start()
        own_ids.start()
        own_rows.wait()
        own_ids.wait()
        for copy in copies:
            copy.wait()


def swap_rows(rows, ids, collective_id):
    in_vmem = pl.BlockSpec(memory_space=pltpu.VMEM)
    return pl.pallas_call(
        swap_kernel,
        out_shape=[
            jax.ShapeDtypeStruct(rows.shape, rows.dtype),
            jax.ShapeDtypeStruct((4,) + ids.shape, ids.dtype),
        ],
        in_specs=[in_vmem] * 2,
        out_specs=[in_vmem] * 2,
        scratch_shapes=[
            pltpu.SemaphoreType.DMA((2,)),
            pltpu.SemaphoreType.DMA((6,)),
            pltpu.SemaphoreType.DMA((6,)),
        ],
        compiler_params=pltpu.CompilerParams(collective_id=collective_id, has_side_effects=True),
    )(rows, ids)


IN_VMEM = pl.BlockSpec(memory_space=pltpu.VMEM)
IN_SMEM = pl.BlockSpec(memory_space=pltpu.SMEM)
ROOT_HALF = 0.7071067811865476
ROOT_TWO_PI = 0.3989422804014327


def dot_nn(left, right):
    return lax.dot_general(
        left, right, (((1,), (0,)), ((), ())), preferred_element_type=jnp.float32
    )


def dot_nt(left, right):
    return lax.dot_general(
        left, right, (((1,), (1,)), ((), ())), preferred_element_type=jnp.float32
    )


def dot_tn(left, right):
    return lax.dot_general(
        left, right, (((0,), (0,)), ((), ())), preferred_element_type=jnp.float32
    )


def unit_rows(v):
    center = v - jnp.mean(v, -1, keepdims=True)
    scale = lax.rsqrt(jnp.mean(center * center, -1, keepdims=True) + EPS)
    return center * scale, scale


def split_heads(pair):
    low = lax.broadcasted_iota(jnp.int32, pair.shape, 1) < HEAD
    nothing = jnp.zeros_like(pair)
    return jnp.concatenate([jnp.where(low, pair, nothing), jnp.where(low, nothing, pair)], 0)


def join_heads(stacked):
    half = stacked.shape[0] // 2
    low = lax.broadcasted_iota(jnp.int32, (half, stacked.shape[1]), 1) < HEAD
    return jnp.where(low, stacked[:half], stacked[half:])


def pair_scores(keys, stacked_queries, key_count):
    scores = dot_nt(keys, stacked_queries) * 0.125
    valid = lax.broadcasted_iota(jnp.int32, scores.shape, 0) < key_count
    return jnp.where(valid, scores, MASKED)


STRIP = 64


def forward_kernel(only, tile, given, *refs):
    x, gain_attn, gain_mlp, counts, gain_final, wo, wq, wp, wu, wd = refs[:10]
    rest = refs[10 + given :]
    outs = rest[:KEPT_COUNT]
    last = rest[KEPT_COUNT : KEPT_COUNT + 1 + only]
    rest = rest[1 + only :]
    qv, pv, uv, dv = rest[KEPT_COUNT : KEPT_COUNT + 4]
    kept = rest[KEPT_COUNT + 4 : 2 * KEPT_COUNT + 4]
    a, att, m, acc, wsem, osem = rest[2 * KEPT_COUNT + 4 :]
    xv, at_t, qkv, lse, att_t, mid, m_t, pre, act_t, out = kept
    rows, width = a.shape
    units = dv.shape[0]

    def store(idx):
        return pltpu.make_async_copy(kept[idx], outs[idx], osem.at[idx])

    def run():
        loads = []

        def load(src, dst):
            copy = pltpu.make_async_copy(src, dst, wsem.at[len(loads)])
            copy.start()
            loads.append(copy)

        for lo in range(0, 3 * width, tile):
            load(wq.at[:, pl.ds(lo, tile)], qv.at[:, pl.ds(lo, tile)])
        load(wp, pv)
        for lo in range(0, units, tile):
            load(wu.at[:, pl.ds(lo, tile)], uv.at[:, pl.ds(lo, tile)])
            load(wd.at[pl.ds(lo, tile)], dv.at[pl.ds(lo, tile)])
        loads = iter(loads)
        for lo in range(0, rows, STRIP):
            here = pl.ds(lo, STRIP)
            xv[here, :] = x[here, :].astype(jnp.float32)
            a[here, :] = (unit_rows(xv[here, :])[0] * gain_attn[...]).astype(jnp.bfloat16)
        store(0).start()
        for lo in range(0, 3 * width, tile):
            next(loads).wait()
            cols = pl.ds(lo, tile)
            qkv[:, cols] = dot_nn(a[...], qv[:, cols]).astype(jnp.bfloat16)
        store(2).start()
        for lo in range(0, width, 256):
            at_t[pl.ds(lo, 256), :] = a[:, pl.ds(lo, 256)].T
        store(1).start()
        pairs = width // 128
        for seq in range(rows // LEN):
            here = pl.ds(seq * LEN, LEN)
            for pair in range(pairs):
                stacked = split_heads(qkv[here, pl.ds(pair * 128, 128)])
                scores = pair_scores(qkv[here, pl.ds(width + pair * 128, 128)], stacked, counts[seq])
                top = jnp.max(scores, 0, keepdims=True)
                power = jnp.exp(scores - top)
                total = jnp.sum(power, 0, keepdims=True)
                lse[seq * pairs + pair] = top + jnp.log(total)
                probs = (power * (1.0 / total)).astype(jnp.bfloat16)
                mixed = dot_tn(probs, qkv[here, pl.ds(2 * width + pair * 128, 128)])
                att[here, pl.ds(pair * 128, 128)] = join_heads(mixed).astype(jnp.bfloat16)
        store(3).start()
        for lo in range(0, width, 256):
            att_t[pl.ds(lo, 256), :] = att[:, pl.ds(lo, 256)].T
        store(4).start()
        next(loads).wait()
        for lo in range(0, width, tile):
            cols = pl.ds(lo, tile)
            mid[:, cols] = xv[:, cols] + dot_nn(att[...], pv[:, cols])
        for lo in range(0, rows, STRIP):
            here = pl.ds(lo, STRIP)
            m[here, :] = (unit_rows(mid[here, :])[0] * gain_mlp[...]).astype(jnp.bfloat16)
        store(5).start()
        acc[...] = mid[...]
        for lo in range(0, units, tile):
            cols = pl.ds(lo, tile)
            next(loads).wait()
            before = dot_nn(m[...], uv[:, cols])
            pre[:, cols] = before
            active = (0.5 * before * (1.0 + lax.erf(before * ROOT_HALF))).astype(jnp.bfloat16)
            act_t[cols, :] = active.T
            next(loads).wait()
            acc[...] += dot_nn(active, dv[cols, :])
        store(7).start()
        store(8).start()
        for lo in range(0, width, 256):
            m_t[pl.ds(lo, 256), :] = m[:, pl.ds(lo, 256)].T
        store(6).start()
        out[...] = acc[...]
        store(9).start()
        if only == 0:
            last[0][...] = acc[...].astype(jnp.bfloat16)
        else:
            for lo in range(0, rows, STRIP):
                here = pl.ds(lo, STRIP)
                last[0][here, :] = (unit_rows(acc[here, :])[0] * gain_final[...]).astype(jnp.bfloat16)
            last[1][...] = dot_nn(last[0][...], wo[...]).astype(jnp.bfloat16)
        for idx in range(KEPT_COUNT):
            store(idx).wait()

    pl.when(lax.axis_index("section") == only)(run)


KEPT_COUNT = 10


def kept_shapes(rows, width, units):
    f32, low = jnp.float32, jnp.bfloat16
    return [
        jax.ShapeDtypeStruct(shape, kind)
        for shape, kind in (
            ((rows, width), f32),
            ((width, rows), low),
            ((rows, 3 * width), low),
            ((rows // LEN * width // 128, 1, 2 * LEN), f32),
            ((width, rows), low),
            ((rows, width), f32),
            ((width, rows), low),
            ((rows, units), f32),
            ((units, rows), low),
            ((rows, width), f32),
        )
    ]


def run_forward(only, x, gain_attn, gain_mlp, counts, gain_final, out_weight, weights, kept):
    wq, wp, wu, wd = weights
    rows, width = x.shape
    units = wd.shape[0]
    tile = 512
    shapes = kept_shapes(rows, width, units)
    low = jnp.bfloat16
    given = 0 if kept is None else KEPT_COUNT
    in_specs = [IN_VMEM] * 3 + [IN_SMEM] + [IN_VMEM] * 2 + [ANYWHERE] * (4 + given)
    extra = [jax.ShapeDtypeStruct((rows, width), low)]
    if only == 1:
        extra.append(jax.ShapeDtypeStruct((rows, out_weight.shape[1]), low))
    return pl.pallas_call(
        functools.partial(forward_kernel, only, tile, given),
        out_shape=shapes + extra,
        in_specs=in_specs,
        out_specs=[ANYWHERE] * KEPT_COUNT + [IN_VMEM] * len(extra),
        input_output_aliases={10 + idx: idx for idx in range(given)},
        scratch_shapes=[pltpu.VMEM(w.shape, w.dtype) for w in weights]
        + [pltpu.VMEM(s.shape, s.dtype) for s in shapes]
        + [
            pltpu.VMEM((rows, width), low),
            pltpu.VMEM((rows, width), low),
            pltpu.VMEM((rows, width), low),
            pltpu.VMEM((rows, width), jnp.float32),
            pltpu.SemaphoreType.DMA((3 * width // tile + 1 + 2 * units // tile,)),
            pltpu.SemaphoreType.DMA((KEPT_COUNT,)),
        ],
        compiler_params=pltpu.CompilerParams(vmem_limit_bytes=56 << 20),
    )(x, gain_attn, gain_mlp, counts, gain_final, out_weight, wq, wp, wu, wd, *(kept or ()))


GRAD_COUNT = 6


def grad_shapes(rows, width, units):
    f32, low = jnp.float32, jnp.bfloat16
    return [
        jax.ShapeDtypeStruct(shape, kind)
        for shape, kind in (
            ((rows, width), low),
            ((rows, units), low),
            ((rows, width), low),
            ((rows, 3 * width), low),
            ((rows, width), low),
            ((8, width), f32),
        )
    ]


def norm_pull(v, gain, upstream):
    unit, scale = unit_rows(v)
    pulled = upstream * gain
    inner = jnp.mean(pulled * unit, -1, keepdims=True)
    grad = (pulled - jnp.mean(pulled, -1, keepdims=True) - unit * inner) * scale
    return grad, jnp.sum(upstream * unit, 0, keepdims=True)


def backward_kernel(only, tile, given, *refs):
    grad_in, gain_attn, gain_mlp, counts, gain_final, wo, out_in = refs[:7]
    x_in, qkv_in, lse_in, mid_in, pre_in, wq, wp, wu, wd = refs[7:16]
    rest = refs[16 + given :]
    outs = rest[:GRAD_COUNT]
    qv, pv, uv, dv = rest[GRAD_COUNT : GRAD_COUNT + 4]
    made = rest[GRAD_COUNT + 4 : 2 * GRAD_COUNT + 4]
    x, qkv, lse, mid, pre, gm, gmid, gatt, gtop, wsem, ksem, osem = rest[2 * GRAD_COUNT + 4 :]
    grad = gtop if only == 1 else grad_in
    gy, gpre, gz, gqkv, gx, gains = made
    rows, width = gm.shape
    units = dv.shape[0]

    def store(idx):
        return pltpu.make_async_copy(made[idx], outs[idx], osem.at[idx])

    def run():
        loads = []

        def load(src, dst):
            copy = pltpu.make_async_copy(src, dst, wsem.at[len(loads)])
            copy.start()
            loads.append(copy)

        kept = [
            pltpu.make_async_copy(src, dst, ksem.at[idx])
            for idx, (src, dst) in enumerate(
                ((pre_in, pre), (mid_in, mid), (qkv_in, qkv), (lse_in, lse), (x_in, x))
            )
        ]
        if only == 1:
            kept.append(pltpu.make_async_copy(out_in, gtop, ksem.at[5]))
            kept[5].start()
        kept[0].start()
        for lo in range(0, units, tile):
            load(wd.at[pl.ds(lo, tile)], dv.at[pl.ds(lo, tile)])
            load(wu.at[:, pl.ds(lo, tile)], uv.at[:, pl.ds(lo, tile)])
        for copy in kept[1:5]:
            copy.start()
        load(wp, pv)
        load(wq, qv)
        loads = iter(loads)
        gains[...] = jnp.zeros_like(gains)
        if only == 1:
            for copy in kept[5:]:
                copy.wait()
            gmid[...] = dot_nt(grad_in[...], wo[...])
            for lo in range(0, rows, STRIP):
                here = pl.ds(lo, STRIP)
                step, gain = norm_pull(gtop[here, :], gain_final[...], gmid[here, :])
                gtop[here, :] = step
                gains[2:3, :] += gain
        gy[...] = grad[...].astype(jnp.bfloat16)
        store(0).start()
        kept[0].wait()
        gm[...] = jnp.zeros_like(gm)
        for lo in range(0, units, tile):
            cols = pl.ds(lo, tile)
            next(loads).wait()
            pulled = dot_nt(gy[...], dv[cols, :])
            before = pre[:, cols]
            slope = 0.5 * (1.0 + lax.erf(before * ROOT_HALF)) + before * (
                ROOT_TWO_PI * jnp.exp(-0.5 * before * before)
            )
            low = (pulled * slope).astype(jnp.bfloat16)
            gpre[:, cols] = low
            next(loads).wait()
            gm[...] += dot_nt(low, uv[:, cols])
        store(1).start()
        kept[1].wait()
        for lo in range(0, rows, STRIP):
            here = pl.ds(lo, STRIP)
            step, gain = norm_pull(mid[here, :], gain_mlp[...], gm[here, :])
            total = grad[here, :].astype(jnp.float32) + step
            gmid[here, :] = total
            gz[here, :] = total.astype(jnp.bfloat16)
            gains[1:2, :] += gain
        store(2).start()
        next(loads).wait()
        gatt[...] = dot_nt(gz[...], pv[...]).astype(jnp.bfloat16)
        kept[2].wait()
        kept[3].wait()
        pairs = width // 128
        for seq in range(rows // LEN):
            here = pl.ds(seq * LEN, LEN)
            for pair in range(pairs):
                own = pl.ds(pair * 128, 128)
                stacked = split_heads(qkv[here, own])
                pulled = split_heads(gatt[here, own])
                keys = qkv[here, pl.ds(width + pair * 128, 128)]
                values = qkv[here, pl.ds(2 * width + pair * 128, 128)]
                probs = jnp.exp(pair_scores(keys, stacked, counts[seq]) - lse[seq * pairs + pair])
                gprobs = dot_nt(values, pulled)
                inner = jnp.sum(probs * gprobs, 0, keepdims=True)
                gscores = (probs * (gprobs - inner)).astype(jnp.bfloat16)
                gqkv[here, own] = (join_heads(dot_tn(gscores, keys)) * 0.125).astype(jnp.bfloat16)
                gqkv[here, pl.ds(width + pair * 128, 128)] = (dot_nn(gscores, stacked) * 0.125).astype(
                    jnp.bfloat16
                )
                gqkv[here, pl.ds(2 * width + pair * 128, 128)] = dot_nn(
                    probs.astype(jnp.bfloat16), pulled
                ).astype(jnp.bfloat16)
        store(3).start()
        next(loads).wait()
        for lo in range(0, width, 256):
            gm[:, pl.ds(lo, 256)] = dot_nt(gqkv[...], qv[pl.ds(lo, 256), :])
        kept[4].wait()
        for lo in range(0, rows, STRIP):
            here = pl.ds(lo, STRIP)
            step, gain = norm_pull(x[here, :], gain_attn[...], gm[here, :])
            gx[here, :] = (gmid[here, :] + step).astype(jnp.bfloat16)
            gains[0:1, :] += gain
        store(4).start()
        store(5).start()
        for idx in range(GRAD_COUNT):
            store(idx).wait()

    pl.when(lax.axis_index("section") == only)(run)


def run_backward(only, grad, gain_attn, gain_mlp, counts, gain_final, out_weight, kept, weights, made):
    wq, wp, wu, wd = weights
    x, _, qkv, lse, _, mid, _, pre, _, out = kept
    rows, width = x.shape
    units = wd.shape[0]
    tile = 512
    shapes = grad_shapes(rows, width, units)
    low, f32 = jnp.bfloat16, jnp.float32
    given = 0 if made is None else GRAD_COUNT
    in_specs = [IN_VMEM] * 3 + [IN_SMEM] + [IN_VMEM] * 2 + [ANYWHERE] * (10 + given)
    return pl.pallas_call(
        functools.partial(backward_kernel, only, tile, given),
        out_shape=shapes,
        in_specs=in_specs,
        out_specs=[ANYWHERE] * GRAD_COUNT,
        input_output_aliases={16 + idx: idx for idx in range(given)},
        scratch_shapes=[pltpu.VMEM(w.shape, w.dtype) for w in weights]
        + [pltpu.VMEM(s.shape, s.dtype) for s in shapes]
        + [pltpu.VMEM(s.shape, s.dtype) for s in (x, qkv, lse, mid, pre)]
        + [
            pltpu.VMEM((rows, width), f32),
            pltpu.VMEM((rows, width), f32),
            pltpu.VMEM((rows, width), low),
            pltpu.VMEM((rows, width), f32),
            pltpu.SemaphoreType.DMA((2 + 2 * units // tile,)),
            pltpu.SemaphoreType.DMA((6,)),
            pltpu.SemaphoreType.DMA((GRAD_COUNT,)),
        ],
        compiler_params=pltpu.CompilerParams(vmem_limit_bytes=56 << 20),
    )(
        grad, gain_attn, gain_mlp, counts, gain_final, out_weight, out, x, qkv, lse, mid, pre, wq, wp, wu, wd, *(made or ())
    )


def vocabulary_kernel(only, tile, proj, ids, scale, table, gproj_out, loss_out, gtable, *scratch):
    tv, gt, gt32, pall, gp, gsend, gin, stat, stats, whole, tsem, gsem, psem, prem, ssem, srem, qsem, qrem = scratch
    rows = proj.shape[0]
    vocab = tv.shape[0]
    count = vocab // tile
    sec = lax.axis_index("section")
    grp = lax.axis_index("group")
    pos = lax.axis_index("dp")
    peers = [(sec, grp, lax.rem(pos + k, 4)) for k in (1, 2, 3)]
    places = [lax.rem(pos + k, 4) for k in (1, 2, 3)]

    def run():
        load = pltpu.make_async_copy(table, tv, tsem)
        load.start()
        barrier = pltpu.get_barrier_semaphore()
        for device in peers:
            pl.semaphore_signal(barrier, inc=1, device_id=device, device_id_type=MESH)
        pall[pos] = proj[...]
        pl.semaphore_wait(barrier, 3)
        first = [
            remote(pall.at[pos], pall.at[pos], psem.at[k], prem.at[k], peers[k]) for k in range(3)
        ]
        for copy in first:
            copy.start()
        load.wait()

        def logits_of(at, z):
            return dot_nt(tv[rows_at(at * tile, tile), :], pall[z])

        def lanes(z):
            return pl.ds(pl.multiple_of(z * rows, 128), rows)

        def hits_of(at, z):
            names = lax.broadcasted_iota(jnp.int32, (tile, rows), 0) + (at * tile + pos * vocab)
            return names == ids[:, lanes(z)]

        stat[0:1, :] = jnp.full((1, 4 * rows), MASKED, jnp.float32)
        stat[1:8, :] = jnp.zeros((7, 4 * rows), jnp.float32)

        def measure_block(z):
            def measure(at, carry):
                top, total, picked = carry
                logits = logits_of(at, z)
                higher = jnp.maximum(top, jnp.max(logits, 0, keepdims=True))
                total = total * jnp.exp(top - higher) + jnp.sum(
                    jnp.exp(logits - higher), 0, keepdims=True
                )
                picked = picked + jnp.sum(jnp.where(hits_of(at, z), logits, 0.0), 0, keepdims=True)
                return higher, total, picked

            zero = jnp.zeros((1, rows), jnp.float32)
            top, total, picked = lax.fori_loop(0, count, measure, (zero + MASKED, zero, zero))
            stat[0:1, lanes(z)] = top
            stat[1:2, lanes(z)] = total
            stat[2:3, lanes(z)] = picked

        measure_block(pos)
        for k in (2, 1, 0):
            first[k].wait_recv()
            measure_block(lax.rem(pos + 3 - k, 4))
        second = [
            remote(stat, stats.at[pos], ssem.at[k], srem.at[k], peers[k]) for k in range(3)
        ]
        for copy in second:
            copy.start()
        stats[pos] = stat[...]
        gt32[...] = jnp.zeros_like(gt32)
        for copy in second:
            copy.wait()
        top = stats[0, 0:1, :]
        for z in (1, 2, 3):
            top = jnp.maximum(top, stats[z, 0:1, :])
        total = jnp.zeros_like(top)
        picked = jnp.zeros_like(top)
        for z in range(4):
            total = total + stats[z, 1:2, :] * jnp.exp(stats[z, 0:1, :] - top)
            picked = picked + stats[z, 2:3, :]
        whole[0:1, :] = top + jnp.log(total)
        whole[1:2, :] = jnp.where(scale[...] > 0, whole[0:1, :] - picked, 0.0)
        loss_out[...] = whole[1:2, lanes(pos)]

        def pull_block(z):
            log_total = whole[0:1, lanes(z)]
            weight = scale[:, lanes(z)]
            gp[...] = jnp.zeros_like(gp)

            def pull(at, carry):
                here = rows_at(at * tile, tile)
                probs = jnp.exp(logits_of(at, z) - log_total)
                grads = ((probs - jnp.where(hits_of(at, z), 1.0, 0.0)) * weight).astype(jnp.bfloat16)
                gp[...] += dot_tn(grads, tv[here, :])
                gt32[here, :] += dot_nn(grads, pall[z])
                return carry

            lax.fori_loop(0, count, pull, 0)

        third = [
            remote(gsend.at[k], gin.at[k], qsem.at[k], qrem.at[k], peers[k]) for k in range(3)
        ]
        for k in (1, 0, 2):
            pull_block(places[k])
            gsend[k] = gp[...].astype(jnp.bfloat16)
            third[k].start()
        pull_block(pos)
        summed = gp[...]
        for k in range(3):
            third[k].wait_recv()
            summed = summed + gin[k].astype(jnp.float32)
        gproj_out[...] = summed.astype(jnp.bfloat16)
        gt[...] = gt32[...].astype(jnp.bfloat16)
        keep = pltpu.make_async_copy(gt, gtable, gsem)
        keep.start()
        for copy in third + first:
            copy.wait_send()
        keep.wait()

    pl.when(sec == only)(run)


def run_vocabulary(only, proj, ids, scale, table, collective_id):
    rows, emb = proj.shape
    vocab = table.shape[0]
    low, f32, dma = jnp.bfloat16, jnp.float32, pltpu.SemaphoreType.DMA
    return pl.pallas_call(
        functools.partial(vocabulary_kernel, only, 512),
        out_shape=[
            jax.ShapeDtypeStruct((rows, emb), low),
            jax.ShapeDtypeStruct((1, rows), f32),
            jax.ShapeDtypeStruct(table.shape, low),
        ],
        in_specs=[IN_VMEM] * 3 + [ANYWHERE],
        out_specs=[IN_VMEM] * 2 + [ANYWHERE],
        scratch_shapes=[
            pltpu.VMEM(table.shape, low),
            pltpu.VMEM(table.shape, low),
            pltpu.VMEM(table.shape, f32),
            pltpu.VMEM((4, rows, emb), low),
            pltpu.VMEM((rows, emb), f32),
            pltpu.VMEM((3, rows, emb), low),
            pltpu.VMEM((3, rows, emb), low),
            pltpu.VMEM((8, 4 * rows), f32),
            pltpu.VMEM((4, 8, 4 * rows), f32),
            pltpu.VMEM((8, 4 * rows), f32),
            dma,
            dma,
        ]
        + [dma((3,))] * 6,
        compiler_params=pltpu.CompilerParams(
            collective_id=collective_id, has_side_effects=True, vmem_limit_bytes=60 << 20
        ),
    )(proj, ids, scale, table)


def run_products(pairs):
    count = len(pairs)
    low, dma = jnp.bfloat16, pltpu.SemaphoreType.DMA
    tall, wide = 256, 1024

    def kernel(*refs):
        lefts, rights, outs, lv, rv, rings = (refs[at * count : (at + 1) * count] for at in range(6))
        lsem, rsem, osem = refs[6 * count :]
        loads = []
        for at in range(count):
            loads.append(
                (
                    pltpu.make_async_copy(lefts[at], lv[at], lsem.at[at]),
                    pltpu.make_async_copy(rights[at], rv[at], rsem.at[at]),
                )
            )
            for copy in loads[-1]:
                copy.start()
        for at in range(count):
            for copy in loads[at]:
                copy.wait()
            rows, columns = outs[at].shape
            turn = []
            for lo in range(0, rows, tall):
                slot = len(turn) % 2
                if len(turn) >= 2:
                    turn[-2].wait()
                for left in range(0, columns, wide):
                    cols = pl.ds(left, wide)
                    rings[at][slot, :, cols] = dot_nn(
                        lv[at][pl.ds(lo, tall), :], rv[at][:, cols]
                    ).astype(low)
                copy = pltpu.make_async_copy(
                    rings[at].at[slot], outs[at].at[pl.ds(lo, tall)], osem.at[at, slot]
                )
                copy.start()
                turn.append(copy)
            pending.append(turn[-2:])
        for turn in pending:
            for copy in turn:
                copy.wait()
        pending.clear()

    pending = []
    lefts = [left for left, _ in pairs]
    rights = [right for _, right in pairs]
    return pl.pallas_call(
        kernel,
        out_shape=[
            jax.ShapeDtypeStruct((left.shape[0], right.shape[1]), low) for left, right in pairs
        ],
        in_specs=[ANYWHERE] * (2 * count),
        out_specs=[ANYWHERE] * count,
        scratch_shapes=[pltpu.VMEM(x.shape, x.dtype) for x in lefts + rights]
        + [pltpu.VMEM((2, tall, right.shape[1]), low) for right in rights]
        + [dma((count,)), dma((count,)), dma((count, 2))],
        compiler_params=pltpu.CompilerParams(vmem_limit_bytes=40 << 20),
    )(*lefts, *rights)


def widen_kernel(mine_first, *refs):
    narrow, (table_a, table_b), wide, table_out = refs[:4], refs[4:6], refs[6:10], refs[10]
    for src, dst in zip(narrow, wide):
        dst[...] = src[...].astype(jnp.float32)

    @pl.when(lax.axis_index("section") == mine_first)
    def _():
        table_out[...] = table_a[...].astype(jnp.float32)

    @pl.when(lax.axis_index("section") != mine_first)
    def _():
        table_out[...] = table_b[...].astype(jnp.float32)


def widen(arrays, table_mine, table_theirs):
    steps = 8
    inputs = list(arrays) + [table_mine, table_theirs]

    def spec(x):
        return pl.BlockSpec((x.shape[0] // steps, x.shape[1]), lambda at: (at, 0))

    outs = list(arrays) + [table_mine]
    return pl.pallas_call(
        functools.partial(widen_kernel, 0),
        grid=(steps,),
        out_shape=[jax.ShapeDtypeStruct(x.shape, jnp.float32) for x in outs],
        in_specs=[spec(x) for x in inputs],
        out_specs=[spec(x) for x in outs],
        compiler_params=pltpu.CompilerParams(vmem_limit_bytes=40 << 20),
    )(*inputs)


def strip_of(rows, columns):
    strip = 16
    while 2 * strip * columns <= 65536 and rows % (2 * strip) == 0:
        strip = 2 * strip
    return strip


def add_rows(store, terms, rows, columns):
    strip = strip_of(rows, columns)

    def body(at, carry):
        here = rows_at(at * strip, strip)
        total = terms[0](here).astype(jnp.float32)
        for term in terms[1:]:
            total = total + term(here).astype(jnp.float32)
        store(here, total)
        return carry

    lax.fori_loop(0, rows // strip, body, 0)


def reduce_kernel(plan, only, extras, pace, refs_of, *refs):
    body = functools.partial(reduce_body, plan, extras, pace, refs_of(refs))
    if only is None:
        body()
    else:
        pl.when(lax.axis_index("section") == only)(body)


def stage_blocks(order):
    left = list(range(1 << len(order)))
    kept = []
    for bit in order:
        left = [r for r in left if not (r >> bit) & 1]
        kept.append(left)
    return kept


def reduce_body(plan, extras, pace, named):
    arrays, outs = named["arrays"], named["outs"]
    own, got1, got2, got3, got4, land = (
        named[k] for k in ("own", "got1", "got2", "got3", "got4", "land")
    )
    ssem, rsem, own_sem, s4, r4, fin_sem = named["sems"]
    got = (got1, got2, got3, got4)
    count = len(plan)
    sec = lax.axis_index("section")
    grp = lax.axis_index("group")
    pos = lax.axis_index("dp")
    beside = ((sec, grp ^ 1, pos), (sec, grp ^ 2, pos))
    swaps = beside + ((sec, grp, pos ^ 1), (sec, grp, pos ^ 2))
    sides = [(sec, grp ^ j, pos) for j in (1, 2, 3)]
    line_peers = [(sec, grp, lax.rem(pos + k, 4)) for k in (1, 2, 3)]
    steps = [(jg, jz) for jg in range(4) for jz in range(4)][1:]
    kept = [stage_blocks(piece[1]) for piece in plan]

    def other(j):
        return (sec, grp ^ steps[j][0], lax.rem(pos + steps[j][1], 4))

    with_gains = "gains" in extras
    spreads = "spread" in extras
    looked = "looked" in extras
    if with_gains:
        peers = [other(j) for j in range(15)]
    elif looked:
        peers = sides + line_peers
    else:
        peers = [swaps[bit] for bit in sorted(plan[0][1])]
    barrier = pltpu.get_barrier_semaphore()
    for device in peers:
        pl.semaphore_signal(barrier, inc=1, device_id=device, device_id_type=MESH)
    pl.semaphore_wait(barrier, len(peers))

    def rows_of(p):
        return arrays[plan[p][0]].shape[0] // (len(kept[p][0]) // 2)

    def columns_of(p):
        return arrays[plan[p][0]].shape[1]

    def sub_of(p):
        return rows_of(p) // 4 // plan[p][3]

    def block(p, r):
        who = grp ^ (r & 3)
        line = pos ^ (r >> 2) if len(plan[p][1]) == 4 else 0
        start = line * rows_of(p) + who * (rows_of(p) // 4) + plan[p][2] * sub_of(p)
        return arrays[plan[p][0]].at[rows_at(start, sub_of(p))]

    def spot(p, r):
        return kept[p][0].index(r)

    def swap(p, stage, at):
        bit = plan[p][1][stage]
        r = kept[p][stage][at] | (1 << bit)
        src = block(p, r) if stage == 0 else own[p].at[spot(p, r)]
        return remote(
            src, got[stage][p].at[at], ssem.at[p, stage, at], rsem.at[p, stage, at], swaps[bit]
        )

    def load_own(p, at):
        return pltpu.make_async_copy(block(p, kept[p][0][at]), own[p].at[at], own_sem.at[p, at])

    def order_of(p, stage):
        places = range(len(kept[p][stage]))
        if stage == len(plan[p][1]) - 1:
            return list(places)
        bit = plan[p][1][stage + 1]
        return sorted(places, key=lambda at: 1 - ((kept[p][stage][at] >> bit) & 1))

    def begin(p):
        for at in order_of(p, 0):
            swap(p, 0, at).start()
            load_own(p, at).start()

    def advance(p, stage):
        for at in order_of(p, stage):
            r = kept[p][stage][at]
            place = spot(p, r)
            if stage == 0:
                load_own(p, at).wait()
            swap(p, stage, at).wait_recv()
            terms = [
                lambda here, place=place: own[p][place, here, :],
                lambda here, at=at: got[stage][p][at, here, :],
            ]
            if stage == len(plan[p][1]) - 1:
                settle(p, terms)
                return

            def store(here, total, place=place):
                own[p][place, here, :] = total.astype(jnp.bfloat16)

            add_rows(store, terms, sub_of(p), columns_of(p))
            bit = plan[p][1][stage + 1]
            if (r >> bit) & 1:
                swap(p, stage + 1, kept[p][stage + 1].index(r ^ (1 << bit))).start()

    def write_out(p, who, at):
        start = who * (rows_of(p) // 4) + plan[p][2] * sub_of(p)
        return pltpu.make_async_copy(
            land[p].at[who], outs[plan[p][0]].at[rows_at(start, sub_of(p))], named["out_sem"].at[p, at]
        )

    def spread(p, way):
        if way < 2:
            here = land[p].at[grp]
            return remote(here, here, s4.at[p, way], r4.at[p, way], beside[way])
        half = columns_of(p) // 2
        there = land[p].at[grp ^ (way - 1), :, pl.ds(half * (way - 2), half)]
        return remote(there, there, s4.at[p, way], r4.at[p, way], beside[3 - way])

    def settle(p, terms):
        mine = grp if spreads else 0

        def store(here, total):
            land[p][mine, here, :] = total.astype(jnp.bfloat16)

        add_rows(store, terms, sub_of(p), columns_of(p))
        if spreads:
            spread(p, 0).start()
            spread(p, 1).start()
        else:
            own_out(p).start()

    def own_out(p):
        return pltpu.make_async_copy(
            land[p].at[0], outs[plan[p][0]].at[rows_at(plan[p][2] * sub_of(p), sub_of(p))], fin_sem.at[p]
        )

    def arrival(p, way):
        who = (grp ^ 1, grp ^ 2)[way]
        return remote(land[p].at[who], land[p].at[who], s4.at[p, way], r4.at[p, way], beside[way])

    def pass_on(p):
        if spreads:
            for way in (0, 1):
                arrival(p, way).wait_recv()
                spread(p, way + 2).start()

    def write_near(p):
        if spreads:
            for at, who in enumerate((grp, grp ^ 1, grp ^ 2)):
                write_out(p, who, at).start()

    def write_far(p):
        if spreads:
            spread(p, 2).wait_recv()
            spread(p, 3).wait_recv()
            write_out(p, grp ^ 3, 3).start()

    if with_gains:
        gain_in, gain_got, sg, rg, gain_sem = named["gain_scratch"]

        def gain_copy(j):
            device = other(j)
            return remote(gain_in.at[device[2]], gain_got.at[j], sg.at[j], rg.at[j], device)

        gain_load = pltpu.make_async_copy(named["gains"], gain_in, gain_sem)
        gain_load.start()

    if looked:
        looks, looks_own, sl, rl, table_fin, tland, tsum = named["look_scratch"]
        ids, look_in, fin_in = named["look_in"]
        vocab_quarter = fin_in.shape[0]
        look_load = pltpu.make_async_copy(look_in, looks.at[grp, pos], looks_own.at[0])
        fin_load = pltpu.make_async_copy(fin_in, table_fin, looks_own.at[1])

        def look_line(k):
            here = looks.at[grp, pos]
            return remote(here, here, sl.at[k], rl.at[k], line_peers[k])

        def look_side(k):
            here = looks.at[grp]
            return remote(here, here, sl.at[3 + k], rl.at[3 + k], sides[k])

        def table_spread(way):
            if way < 2:
                here = tland.at[grp]
                return remote(here, here, sl.at[6 + way], rl.at[6 + way], beside[way])
            half = tland.shape[2] // 2
            there = tland.at[grp ^ (way - 1), :, pl.ds(half * (way - 2), half)]
            return remote(there, there, sl.at[6 + way], rl.at[6 + way], beside[3 - way])

        def table_out(who):
            return pltpu.make_async_copy(
                tland.at[who],
                named["table_out"].at[rows_at(who * vocab_quarter, vocab_quarter)],
                looks_own.at[2 + who],
            )

        def look_begin():
            look_load.start()
            fin_load.start()
            look_load.wait()
            for k in range(3):
                look_line(k).start()

        def look_middle():
            for k in range(3):
                look_line(k).wait_recv()
            for k in range(3):
                look_side(k).start()

        def look_sum():
            for k in range(3):
                look_side(k).wait_recv()
            fin_load.wait()
            base = pos * (4 * vocab_quarter) + grp * vocab_quarter
            tall = 256
            names = lax.broadcasted_iota(jnp.int32, (tall, ids.shape[2]), 0)

            def body(at, carry):
                here = rows_at(at * tall, tall)
                total = table_fin[here, :].astype(jnp.float32)
                for g in range(4):
                    for z in range(4):
                        hit = names + (base + at * tall) == ids[g * 4 + z]
                        total = total + dot_nn(
                            jnp.where(hit, 1.0, 0.0).astype(jnp.bfloat16), looks[g, z]
                        )
                tland[grp, here, :] = total.astype(jnp.bfloat16)
                return carry

            lax.fori_loop(0, vocab_quarter // tall, body, 0)
            table_spread(0).start()
            table_spread(1).start()

        def look_pass():
            for way in (0, 1):
                who = (grp ^ 1, grp ^ 2)[way]
                remote(
                    tland.at[who], tland.at[who], sl.at[6 + way], rl.at[6 + way], beside[way]
                ).wait_recv()
                table_spread(way + 2).start()

        def look_end():
            table_spread(2).wait_recv()
            table_spread(3).wait_recv()
            for who in range(4):
                table_out(who).start()
            for who in range(4):
                table_out(who).wait()
            for k in range(3):
                look_line(k).wait_send()
                look_side(k).wait_send()
            for way in range(4):
                table_spread(way).wait_send()

        def on_first(run):
            pl.when(sec == 0)(run)

    else:

        def on_first(run):
            pass

        look_begin = look_middle = look_sum = look_pass = look_end = None

    ahead, lag, lag_end = pace
    on_first(look_begin)
    for p in range(min(ahead, count)):
        begin(p)
    if with_gains:
        gain_load.wait()
        for j in range(15):
            gain_copy(j).start()
    delays = [0, lag, 2 * lag, 3 * lag, 3 * lag + lag_end, 3 * lag + 2 * lag_end, 3 * lag + 3 * lag_end]
    for at in range(count + delays[-1]):
        if ahead + at < count:
            begin(ahead + at)
        for stage in range(len(plan[0][1])):
            if 0 <= at - delays[stage] < count:
                advance(at - delays[stage], stage)
        for run, delay in zip((pass_on, write_near, write_far), delays[4:]):
            if 0 <= at - delay < count:
                run(at - delay)
        for when, run in ((1, look_middle), (3, look_sum), (5, look_pass)):
            if at == when * (count + delays[3]) // 6:
                on_first(run)
    if with_gains:
        for j in range(15):
            gain_copy(j).wait_recv()
        total = gain_in[pos]
        for j in range(15):
            total = total + gain_got[j]
        named["gain_out"][...] = total
    on_first(look_end)
    for p in range(count):
        if spreads:
            for at, who in enumerate((grp, grp ^ 1, grp ^ 2, grp ^ 3)):
                write_out(p, who, at).wait()
            for way in range(4):
                spread(p, way).wait_send()
        else:
            own_out(p).wait()
        for stage in range(len(plan[p][1])):
            for at in range(len(kept[p][stage])):
                swap(p, stage, at).wait_send()
    if with_gains:
        for j in range(15):
            gain_copy(j).wait_send()


def reduce_all(arrays, plan, only, collective_id, pace, gains=None, look=None, spread=True):
    low, f32, dma = jnp.bfloat16, jnp.float32, pltpu.SemaphoreType.DMA
    extras = ("spread",) * spread + ("gains",) * (gains is not None) + ("looked",) * (look is not None)
    count = len(plan)
    inputs = list(arrays)
    lines = 4 if len(plan[0][1]) == 4 else 1
    share = lines if spread else 4 * lines
    outs = [jax.ShapeDtypeStruct((x.shape[0] // share, x.shape[1]), low) for x in arrays]
    out_specs = [ANYWHERE] * len(arrays)
    in_specs = [ANYWHERE] * len(arrays)
    names = ["own", "got1", "got2", "got3", "got4", "land"]
    scratch = {name: [] for name in names}
    for src, _, _, chunks in plan:
        rows, columns = arrays[src].shape[0] // lines, arrays[src].shape[1]
        sub = rows // 4 // chunks
        held = (8, 8, 4, 2, 1) if lines == 4 else (2, 2, 1, 0, 0)
        for name, blocks in zip(names, held + (4 if spread else 1,)):
            shape = (blocks, sub, columns) if blocks else (8, 128)
            scratch[name].append(pltpu.VMEM(shape, low))
    flat = [item for name in names for item in scratch[name]]
    sems = [dma((count, 4, 8))] * 2 + [dma((count, 8))] + [dma((count, 4))] * 2 + [dma((count,))]
    tail = []
    if spread:
        tail += [dma((count, 4))]
    if gains is not None:
        inputs.append(gains)
        in_specs.append(ANYWHERE)
        outs.append(jax.ShapeDtypeStruct(gains.shape[1:], f32))
        out_specs.append(IN_VMEM)
        tail += [
            pltpu.VMEM(gains.shape, f32),
            pltpu.VMEM((15,) + gains.shape[1:], f32),
            dma((15,)),
            dma((15,)),
            dma,
        ]
    if look is not None:
        ids, rows_in, fin_in = look
        inputs += [ids, rows_in, fin_in]
        in_specs += [IN_VMEM, ANYWHERE, ANYWHERE]
        quarter, emb = fin_in.shape
        outs.append(jax.ShapeDtypeStruct((4 * quarter, emb), low))
        out_specs.append(ANYWHERE)
        tail += [
            pltpu.VMEM((4, 4) + rows_in.shape, low),
            dma((6,)),
            dma((10,)),
            dma((10,)),
            pltpu.VMEM(fin_in.shape, low),
            pltpu.VMEM((4, quarter, emb), low),
            pltpu.VMEM((8, 128), f32),
        ]

    def refs_of(refs):
        at = 0

        def take(n):
            nonlocal at
            at += n
            return list(refs[at - n : at])

        named = {"arrays": take(len(arrays))}
        if gains is not None:
            named["gains"] = take(1)[0]
        if look is not None:
            named["look_in"] = take(3)
        named["outs"] = take(len(arrays))
        if gains is not None:
            named["gain_out"] = take(1)[0]
        if look is not None:
            named["table_out"] = take(1)[0]
        for name in names:
            named[name] = take(count)
        named["sems"] = take(6)
        if spread:
            named["out_sem"] = take(1)[0]
        if gains is not None:
            named["gain_scratch"] = take(5)
        if look is not None:
            named["look_scratch"] = take(7)
        return named

    return pl.pallas_call(
        functools.partial(reduce_kernel, plan, only, extras, pace, refs_of),
        out_shape=outs,
        in_specs=in_specs,
        out_specs=out_specs,
        scratch_shapes=flat + sems + tail,
        compiler_params=pltpu.CompilerParams(
            collective_id=collective_id, has_side_effects=True, vmem_limit_bytes=60 << 20
        ),
    )(*inputs)


def nothing_like(run):
    return jax.tree.map(lambda a: jnp.zeros(a.shape, a.dtype), jax.eval_shape(run))


def only_on(live, run):
    return lax.cond(live, run, lambda: nothing_like(run))


X_FIRST = (0, 1, 2, 3)
Y_FIRST = (1, 0, 2, 3)
Z_THEN_X = (2, 0, 1, 3)
Z_THEN_Y = (2, 1, 0, 3)
ORDERS = (X_FIRST, Z_THEN_Y, Y_FIRST, Z_THEN_X)
LAYER_PLAN = (
    tuple((0, ORDERS[chunk], chunk, 4) for chunk in range(4))
    + tuple((1, ORDERS[chunk], chunk, 4) for chunk in range(4))
    + tuple((4, ORDERS[chunk], chunk, 4) for chunk in range(4))
    + ((3, Y_FIRST, 0, 2), (3, Z_THEN_X, 1, 2), (2, X_FIRST, 0, 1))
)
TABLE_PLAN = tuple((0, ((0, 1), (1, 0))[chunk % 2], chunk, 4) for chunk in range(4))
LAYER_PACE = (8, 4, 2)
TABLE_PACE = (4, 2, 1)


def after(value, *others):
    return lax.optimization_barrier((value,) + others)[0]


def per_device(
    tokens,
    lengths,
    levels,
    noise_rows,
    embed_table,
    w_in,
    ln_attn,
    w_qkv,
    w_proj,
    ln_mlp,
    w_up,
    w_down,
    ln_final,
    w_out,
):
    sec = lax.axis_index("section")
    pos = lax.axis_index("dp")
    first_section = sec == 0
    last_section = sec == 1
    rows = tokens.shape[0]
    seqs = lengths.shape[0]
    length = rows // seqs
    width = w_out.shape[0] * 4
    emb = w_out.shape[1]
    vocab_part = embed_table.shape[0]
    gains = jnp.concatenate(
        [ln_attn, ln_mlp, ln_final[None], jnp.zeros((13, ln_final.shape[0]), jnp.bfloat16)], 0
    )
    ids = jnp.concatenate(
        [
            tokens.reshape(-1, 128),
            jnp.concatenate([lengths, jnp.zeros((128 - seqs,), jnp.int32)])[None],
            jnp.zeros((7 - rows // 128, 128), jnp.int32),
        ],
        0,
    )
    shards = (w_qkv[0], w_proj[0], w_up[0], w_down[0], w_in, w_out, gains, ids)
    sizes = [s.shape[0] for s in shards]

    def cut(idx, count, whole=False):
        return tuple((idx, at * sizes[idx] // count, sizes[idx] // count, whole) for at in range(count))

    layer = cut(0, 2) + cut(2, 2) + cut(3, 2)
    wholes = gather_all(
        shards,
        cut(7, 1, True) + cut(6, 1, True) + cut(4, 1) + layer + cut(1, 4, True),
        cut(6, 1, True) + layer + cut(5, 1) + cut(1, 4, True),
        0,
    )
    qkv_weight, proj_weight, up_weight, down_weight, in_weight, out_weight, gain_all, line_ids = wholes
    gain_all = gain_all.reshape(4, 16, -1).astype(jnp.float32)
    gain_attn = gain_all[:, 0].reshape(-1)
    gain_mlp = gain_all[:, 1].reshape(-1)
    final_gain = gain_all[:, 2].reshape(-1)
    weights = (qkv_weight, proj_weight, up_weight, down_weight)
    gain_attn = gain_attn[None]
    gain_mlp = gain_mlp[None]
    final_gain = final_gain[None]
    loss_scale = LOSS_GAIN / math.sqrt(rows * lax.axis_size(("group", "dp")))

    def look_up():
        local = line_ids.reshape(4, 8, 128)[:, : rows // 128].reshape(-1) - pos * vocab_part
        hit = local[:, None] == lax.broadcasted_iota(jnp.int32, (1, vocab_part), 1)
        return product(hit.astype(jnp.bfloat16), embed_table).astype(jnp.bfloat16)

    looked_parts = only_on(first_section, look_up).reshape(4, rows, emb)
    looked_parts, all_ids = swap_rows(looked_parts, line_ids, 1)
    all_tokens = all_ids.reshape(16, 8, 128)[:, : rows // 128].reshape(-1)
    noise_level = jnp.exp(LOG_LOW + levels.astype(jnp.float32) * (LOG_SPAN / (LEVELS - 1)))
    scale_in = lax.rsqrt(EMB_VAR + noise_level * noise_level)
    row_level = jnp.repeat(noise_level, length)[:, None]
    row_scale = jnp.repeat(scale_in, length)[:, None]

    def front():
        looked = jnp.sum(looked_parts.astype(jnp.float32), 0)
        mixed_in = ((looked + row_level * noise_rows.astype(jnp.float32)) * row_scale).astype(
            jnp.bfloat16
        )
        return mixed_in, product(mixed_in, in_weight)

    mixed_in, x_first = only_on(first_section, front)
    *kept, out_first = run_forward(
        0, x_first, gain_attn, gain_mlp, lengths, final_gain, out_weight, weights, None
    )
    x_second = passed_along(out_first, "section", 1)
    *kept, final_in, projected = run_forward(
        1, x_second, gain_attn, gain_mlp, lengths, final_gain, out_weight, weights, kept
    )
    projected = passed_along(projected, "section", -1)
    line_parts = line_ids.reshape(4, 8, 128)
    line_tokens = line_parts[:, : rows // 128].reshape(1, -1)
    line_counts = line_parts[:, rows // 128, :seqs].reshape(-1, 1)
    line_valid = jnp.arange(length, dtype=jnp.int32)[None, :] < line_counts
    line_scale = jnp.where(line_valid.reshape(1, -1), loss_scale, 0.0)
    grad_proj_a, entropy, table_g = run_vocabulary(
        0, projected, line_tokens, line_scale, embed_table, 2
    )
    grad_proj = passed_along(grad_proj_a, "section", 1)
    (table_fin,) = reduce_all(
        (after(table_g, grad_proj),),
        TABLE_PLAN,
        0,
        3,
        TABLE_PACE,
        spread=False,
    )
    made = run_backward(
        1, grad_proj, gain_attn, gain_mlp, lengths, final_gain, out_weight, kept, weights, None
    )
    grad_first = passed_along(after(made[4], table_fin), "section", -1)
    made = run_backward(
        0, grad_first, gain_attn, gain_mlp, lengths, final_gain, out_weight, kept, weights, made
    )
    shape = in_weight.shape

    def front_edge():
        looked_grad = (product_nt(made[4], in_weight) * row_scale).astype(jnp.bfloat16)
        return product_tn(mixed_in, made[4]).astype(jnp.bfloat16), looked_grad

    def back_edge():
        edge = product_tn(final_in, grad_proj).astype(jnp.bfloat16)
        edge = edge.reshape(4, shape[0] // 4, shape[1]).reshape(shape)
        return edge, jnp.zeros((rows, emb), jnp.bfloat16)

    edge_g, looked_grad = lax.cond(first_section, front_edge, back_edge)
    gain_rows = made[5]
    gain_rows = gain_rows.reshape(8, 4, width // 4).transpose(1, 0, 2)

    up_g, down_g, proj_g, qkv_g = run_products(
        ((kept[6], made[1]), (kept[8], made[0]), (kept[4], made[2]), (kept[1], made[3]))
    )
    order = (up_g, down_g, edge_g, proj_g, qkv_g)
    up_r, down_r, edge_r, proj_r, qkv_r, gain_r, table_r = reduce_all(
        order,
        LAYER_PLAN,
        None,
        4,
        LAYER_PACE,
        gains=gain_rows,
        look=(all_tokens.reshape(16, 1, rows), looked_grad, table_fin),
    )
    loss_low = after(entropy, gain_r)[0].astype(jnp.bfloat16)
    mine = (table_r, edge_r, gain_r, loss_low)
    theirs = lax.ppermute(mine, "section", [(0, 1), (1, 0)])

    def pair_of(at):
        low = jnp.where(first_section, mine[at], theirs[at])
        high = jnp.where(first_section, theirs[at], mine[at])
        return low, high

    up_r, down_r, proj_r, qkv_r, table_out = widen((up_r, down_r, proj_r, qkv_r), table_r, theirs[0])
    in_r, out_r = pair_of(1)
    final_r = pair_of(2)[1][2]
    token_loss = pair_of(3)[0]
    return (
        token_loss,
        table_out,
        in_r.astype(jnp.float32),
        gain_r[0][None],
        qkv_r[None],
        proj_r[None],
        gain_r[1][None],
        up_r[None],
        down_r[None],
        final_r,
        out_r.astype(jnp.float32).reshape(-1, emb),
    )


def solution(mesh):
    placed = (
        P(("group", "dp")),
        P(("group", "dp")),
        P(("group", "dp")),
        P(("group", "dp"), None),
        P("dp", None),
        P("dp", None),
        P("section", "dp"),
        P("section", "dp", None),
        P("section", "dp", None),
        P("section", "dp"),
        P("section", "dp", None),
        P("section", "dp", None),
        P("dp"),
        P("dp", None),
    )
    fits = (mesh.shape["section"], mesh.shape["group"], mesh.shape["dp"]) == (2, 4, 4)
    return jax.shard_map(
        per_device if fits else per_device_general,
        mesh=mesh,
        in_specs=placed,
        out_specs=(
            P(("group", "dp")),
            P("dp", None),
            P("dp", None),
            P("section", "dp"),
            P("section", "dp", None),
            P("section", "dp", None),
            P("section", "dp"),
            P("section", "dp", None),
            P("section", "dp", None),
            P("dp"),
            P("dp", None),
        ),
        check_vma=False,
    )
```

```python
import functools
import math

import jax
import jax.numpy as jnp
from jax import lax
from jax.experimental import pallas as pl
from jax.experimental.pallas import tpu as pltpu
from jax.sharding import PartitionSpec as P

HEAD = 64
LEVELS = 64
LEN = 128
MB = 2


EPS = 1e-05
LOG_LOW = -2.995732273553991
LOG_SPAN = 2.995732273553991
EMB_VAR = 0.015625
MASKED = -1e30
LOSS_GAIN = 16.0


def passed_along(x, axis, by):
    count = lax.axis_size(axis)
    pairs = [(i, i + by) for i in range(count) if 0 <= i + by < count]
    return lax.ppermute(x, axis, pairs)


def product(left_side, right_side):
    return jnp.dot(left_side, right_side, preferred_element_type=jnp.float32)


def product_tn(left_side, right_side):
    return lax.dot_general(
        left_side, right_side, (((0,), (0,)), ((), ())), preferred_element_type=jnp.float32
    )


def product_nt(left_side, right_side):
    return lax.dot_general(
        left_side, right_side, (((1,), (1,)), ((), ())), preferred_element_type=jnp.float32
    )


def normed(inputs, gain_vec):
    center = inputs - jnp.mean(inputs, -1, keepdims=True)
    return center * lax.rsqrt(jnp.mean(center * center, -1, keepdims=True) + EPS) * gain_vec


def norm_back(inputs, gain_vec, upstream):
    output, pullback = jax.vjp(normed, inputs, gain_vec)
    return pullback(upstream)


def gelu_exact(values_in):
    return jax.nn.gelu(values_in, approximate=False)


def attn_scores(split_rows, key_valid):
    scores = (
        jnp.einsum(
            "qhd,khd->hqk", split_rows[:, 0], split_rows[:, 1], preferred_element_type=jnp.float32
        )
        * 0.125
    )
    return jnp.where(key_valid[None, None, :], scores, MASKED)


def attend(qkv_rows, key_valid):
    length = qkv_rows.shape[0]
    model_width = qkv_rows.shape[1] // 3
    split_rows = qkv_rows.reshape(length, 3, model_width // HEAD, HEAD)
    scores = attn_scores(split_rows, key_valid)
    row_max = jnp.max(scores, -1, keepdims=True)
    log_total = row_max + jnp.log(jnp.sum(jnp.exp(scores - row_max), -1, keepdims=True))
    probs_low = jnp.exp(scores - log_total).astype(jnp.bfloat16)
    mixed_rows = jnp.einsum(
        "hqk,khd->qhd", probs_low, split_rows[:, 2], preferred_element_type=jnp.float32
    )
    return (mixed_rows.reshape(length, model_width).astype(jnp.bfloat16), log_total)


def attend_back(qkv_rows, key_valid, log_total, grad_mixed):
    length = qkv_rows.shape[0]
    model_width = qkv_rows.shape[1] // 3
    head_count = model_width // HEAD
    split_rows = qkv_rows.reshape(length, 3, head_count, HEAD)
    grad_heads = grad_mixed.reshape(length, head_count, HEAD)
    probs_full = jnp.exp(attn_scores(split_rows, key_valid) - log_total)
    grad_values = jnp.einsum(
        "hqk,qhd->khd",
        probs_full.astype(jnp.bfloat16),
        grad_heads,
        preferred_element_type=jnp.float32,
    )
    grad_probs = jnp.einsum(
        "qhd,khd->hqk", grad_heads, split_rows[:, 2], preferred_element_type=jnp.float32
    )
    grad_scores = (
        probs_full * (grad_probs - jnp.sum(grad_probs * probs_full, -1, keepdims=True))
    ).astype(jnp.bfloat16)
    grad_query = (
        jnp.einsum(
            "hqk,khd->qhd", grad_scores, split_rows[:, 1], preferred_element_type=jnp.float32
        )
        * 0.125
    )
    grad_key = (
        jnp.einsum(
            "hqk,qhd->khd", grad_scores, split_rows[:, 0], preferred_element_type=jnp.float32
        )
        * 0.125
    )
    stacked = jnp.stack([grad_query, grad_key, grad_values], 1).reshape(length, 3 * model_width)
    return stacked.astype(jnp.bfloat16)


def layer_forward(hidden, key_valid, weights):
    gain_attn, qkv_weight, proj_weight, gain_mlp, up_weight, down_weight = weights
    normed_in = normed(hidden, gain_attn).astype(jnp.bfloat16)
    qkv_rows = product(normed_in, qkv_weight).astype(jnp.bfloat16)
    mixed_rows, log_total = attend(qkv_rows, key_valid)
    hidden_mid = hidden + product(mixed_rows, proj_weight)
    mlp_in = normed(hidden_mid, gain_mlp).astype(jnp.bfloat16)
    pre_act = product(mlp_in, up_weight)
    activated = gelu_exact(pre_act).astype(jnp.bfloat16)
    hidden_out = hidden_mid + product(activated, down_weight)
    return (
        hidden_out,
        (
            hidden,
            normed_in,
            qkv_rows,
            log_total,
            mixed_rows,
            hidden_mid,
            mlp_in,
            pre_act,
            activated,
        ),
    )


def empty_kept(length, model_width, hidden_units, head_count):
    return (
        jnp.zeros((length, model_width), jnp.float32),
        jnp.zeros((length, model_width), jnp.bfloat16),
        jnp.zeros((length, 3 * model_width), jnp.bfloat16),
        jnp.zeros((head_count, length, 1), jnp.float32),
        jnp.zeros((length, model_width), jnp.bfloat16),
        jnp.zeros((length, model_width), jnp.float32),
        jnp.zeros((length, model_width), jnp.bfloat16),
        jnp.zeros((length, hidden_units), jnp.float32),
        jnp.zeros((length, hidden_units), jnp.bfloat16),
    )


def layer_backward(kept_vals, grad_out, key_valid, weights):
    hidden, normed_in, qkv_rows, log_total, mixed_rows, hidden_mid, mlp_in, pre_act, activated = (
        kept_vals
    )
    gain_attn, qkv_weight, proj_weight, gain_mlp, up_weight, down_weight = weights
    grad_low = grad_out.astype(jnp.bfloat16)
    grad_activated = product_nt(grad_low, down_weight)
    grad_pre = jax.vjp(gelu_exact, pre_act)[1](grad_activated)[0].astype(jnp.bfloat16)
    grad_mlp_in = product_nt(grad_pre, up_weight)
    grad_mid_norm, grad_gain_mlp = norm_back(hidden_mid, gain_mlp, grad_mlp_in)
    grad_mid = grad_out + grad_mid_norm
    grad_mid_low = grad_mid.astype(jnp.bfloat16)
    grad_mixed = product_nt(grad_mid_low, proj_weight).astype(jnp.bfloat16)
    grad_qkv = attend_back(qkv_rows, key_valid, log_total, grad_mixed)
    grad_normed = product_nt(grad_qkv, qkv_weight)
    grad_in_norm, grad_gain_attn = norm_back(hidden, gain_attn, grad_normed)
    records = (activated, grad_low, mlp_in, grad_pre, mixed_rows, grad_mid_low, normed_in, grad_qkv)
    return (grad_mid + grad_in_norm, (grad_gain_attn, grad_gain_mlp), records)


def layer_zero(length, model_width, hidden_units):
    records = (
        jnp.zeros((length, hidden_units), jnp.bfloat16),
        jnp.zeros((length, model_width), jnp.bfloat16),
        jnp.zeros((length, model_width), jnp.bfloat16),
        jnp.zeros((length, hidden_units), jnp.bfloat16),
        jnp.zeros((length, model_width), jnp.bfloat16),
        jnp.zeros((length, model_width), jnp.bfloat16),
        jnp.zeros((length, model_width), jnp.bfloat16),
        jnp.zeros((length, 3 * model_width), jnp.bfloat16),
    )
    gains = (jnp.zeros((model_width,), jnp.float32), jnp.zeros((model_width,), jnp.float32))
    return (jnp.zeros((length, model_width), jnp.float32), gains, records)


def layer_grads(records):
    activated, grad_low, mlp_in, grad_pre, mixed_rows, grad_mid_low, normed_in, grad_qkv = records
    return (
        product_tn(normed_in, grad_qkv),
        product_tn(mixed_rows, grad_mid_low),
        product_tn(mlp_in, grad_pre),
        product_tn(activated, grad_low),
    )


def embed_inputs(token_ids, noise_block, level_id, table_full):
    noise_level = jnp.exp(LOG_LOW + level_id.astype(jnp.float32) * (LOG_SPAN / (LEVELS - 1)))
    scale_in = lax.rsqrt(EMB_VAR + noise_level * noise_level)
    looked = jnp.take(table_full, token_ids, axis=0).astype(jnp.float32)
    mixed_in = ((looked + noise_level * noise_block.astype(jnp.float32)) * scale_in).astype(
        jnp.bfloat16
    )
    return (mixed_in, scale_in)


def embed_backward(token_ids, noise_block, level_id, grad_start, table_full, in_weight):
    mixed_in, scale_in = embed_inputs(token_ids, noise_block, level_id, table_full)
    grad_low = grad_start.astype(jnp.bfloat16)
    grad_looked = product_nt(grad_low, in_weight) * scale_in
    return (mixed_in, grad_low, grad_looked)


def embed_zero(length, model_width, emb_width):
    return (
        jnp.zeros((length, emb_width), jnp.bfloat16),
        jnp.zeros((length, model_width), jnp.bfloat16),
        jnp.zeros((length, emb_width), jnp.float32),
    )


def tail_pass(hidden, token_ids, key_valid, final_gain, out_weight, table_full, loss_scale):
    final_in = normed(hidden, final_gain).astype(jnp.bfloat16)
    projected = product(final_in, out_weight).astype(jnp.bfloat16)
    logits = product_nt(projected, table_full)
    row_max = jnp.max(logits, -1, keepdims=True)
    log_total = row_max + jnp.log(jnp.sum(jnp.exp(logits - row_max), -1, keepdims=True))
    vocab_ids = lax.broadcasted_iota(jnp.int32, logits.shape, 1)
    target_hit = vocab_ids == token_ids[:, None]
    picked = jnp.sum(jnp.where(target_hit, logits, 0.0), -1)
    entropy = jnp.where(key_valid, log_total[:, 0] - picked, 0.0)
    row_scale = jnp.where(key_valid, loss_scale, 0.0)[:, None]
    grad_logits = (
        (jnp.exp(logits - log_total) - target_hit.astype(jnp.float32)) * row_scale
    ).astype(jnp.bfloat16)
    grad_proj = product(grad_logits, table_full).astype(jnp.bfloat16)
    grad_final = product_nt(grad_proj, out_weight)
    grad_hidden, grad_gain = norm_back(hidden, final_gain, grad_final)
    return (grad_hidden, entropy, grad_gain, (grad_logits, projected, final_in, grad_proj))


def tail_zero(length, model_width, emb_width, vocab_rows):
    records = (
        jnp.zeros((length, vocab_rows), jnp.bfloat16),
        jnp.zeros((length, emb_width), jnp.bfloat16),
        jnp.zeros((length, model_width), jnp.bfloat16),
        jnp.zeros((length, emb_width), jnp.bfloat16),
    )
    return (
        jnp.zeros((length, model_width), jnp.float32),
        jnp.zeros((length,), jnp.float32),
        jnp.zeros((model_width,), jnp.float32),
        records,
    )


def edge_grads(tail_records, embed_records, token_ids):
    grad_logits, projected, final_in, grad_proj = tail_records
    mixed_in, grad_low, grad_looked = embed_records
    table_grad = product_tn(grad_logits, projected).at[token_ids].add(grad_looked)
    return (table_grad, product_tn(mixed_in, grad_low), product_tn(final_in, grad_proj))


def joined_rows(record_list):
    return jax.tree.map(lambda *pieces: jnp.concatenate(pieces, 0), *record_list)


def assemble(gain_attn_sum, gain_mlp_sum, layer_set, edge_set, gain_final_sum):
    return (
        gain_attn_sum[None],
        layer_set[0][None],
        layer_set[1][None],
        gain_mlp_sum[None],
        layer_set[2][None],
        layer_set[3][None],
        edge_set[0],
        edge_set[1],
        gain_final_sum,
        edge_set[2],
    )


def per_device_general(
    tokens,
    lengths,
    levels,
    noise_rows,
    embed_table,
    w_in,
    ln_attn,
    w_qkv,
    w_proj,
    ln_mlp,
    w_up,
    w_down,
    ln_final,
    w_out,
):
    gathered = (
        lax.all_gather(embed_table, "dp", axis=0, tiled=True),
        lax.all_gather(w_in, "dp", axis=0, tiled=True),
        lax.all_gather(ln_attn, "dp", axis=1, tiled=True),
        lax.all_gather(w_qkv, "dp", axis=1, tiled=True),
        lax.all_gather(w_proj, "dp", axis=1, tiled=True),
        lax.all_gather(ln_mlp, "dp", axis=1, tiled=True),
        lax.all_gather(w_up, "dp", axis=1, tiled=True),
        lax.all_gather(w_down, "dp", axis=1, tiled=True),
        lax.all_gather(ln_final, "dp", axis=0, tiled=True),
        lax.all_gather(w_out, "dp", axis=0, tiled=True),
    )
    table_full = gathered[0]
    in_weight = gathered[1]
    layer_weights = (
        gathered[2][0].astype(jnp.float32),
        gathered[3][0],
        gathered[4][0],
        gathered[5][0].astype(jnp.float32),
        gathered[6][0],
        gathered[7][0],
    )
    final_gain = gathered[8].astype(jnp.float32)
    out_weight = gathered[9]
    model_width = out_weight.shape[0]
    emb_width = out_weight.shape[1]
    vocab_rows = table_full.shape[0]
    hidden_units = layer_weights[4].shape[1]
    head_count = model_width // HEAD
    section_index = lax.axis_index("section")
    first_section = section_index == 0
    token_grid = tokens.reshape(MB, LEN)
    noise_grid = noise_rows.reshape(MB, LEN, noise_rows.shape[1])
    positions = jnp.arange(LEN, dtype=jnp.int32)
    valid_grid = positions[None, :] < lengths[:, None]
    loss_scale = LOSS_GAIN / math.sqrt(tokens.shape[0] * lax.axis_size(("group", "dp")))
    gain_attn_sum = jnp.zeros((model_width,), jnp.float32)
    gain_mlp_sum = jnp.zeros((model_width,), jnp.float32)
    gain_final_sum = jnp.zeros((model_width,), jnp.float32)
    recv_act = jnp.zeros((LEN, model_width), jnp.bfloat16)
    recv_grad = jnp.zeros((LEN, model_width), jnp.bfloat16)
    zero_rows = jnp.zeros((LEN, model_width), jnp.float32)
    kept_ticks = {}
    layer_recs = {}
    tail_recs = {}
    embed_recs = {}
    losses = []
    for moment in range(MB + 2):
        offset = moment - section_index
        fwd_valid = (offset >= 0) & (offset < MB)
        fwd_index = jnp.clip(offset, 0, MB - 1)
        ids_now = lax.dynamic_index_in_dim(token_grid, fwd_index, 0, False)
        noise_now = lax.dynamic_index_in_dim(noise_grid, fwd_index, 0, False)
        level_now = lax.dynamic_index_in_dim(levels, fwd_index, 0, False)
        valid_now = lax.dynamic_index_in_dim(valid_grid, fwd_index, 0, False)

        def first_input():
            mixed_in, scale_in = embed_inputs(ids_now, noise_now, level_now, table_full)
            return product(mixed_in, in_weight)

        layer_input = lax.cond(first_section, first_input, lambda: recv_act.astype(jnp.float32))
        hidden_out, kept_now = lax.cond(
            fwd_valid,
            lambda: layer_forward(layer_input, valid_now, layer_weights),
            lambda: (zero_rows, empty_kept(LEN, model_width, hidden_units, head_count)),
        )
        kept_ticks[moment] = kept_now
        tail_live = jnp.logical_not(first_section) & fwd_valid
        tail_grad, entropy, final_step, tail_now = lax.cond(
            tail_live,
            lambda: tail_pass(
                hidden_out, ids_now, valid_now, final_gain, out_weight, table_full, loss_scale
            ),
            lambda: tail_zero(LEN, model_width, emb_width, vocab_rows),
        )
        tail_recs[moment] = tail_now
        gain_final_sum = gain_final_sum + final_step
        back_tick = moment - 2
        late_live = 0 <= back_tick < MB
        late_index = min(max(back_tick, 0), MB - 1)
        kept_late = kept_ticks[back_tick] if back_tick >= 0 else kept_now
        kept_back = lax.cond(first_section, lambda: kept_late, lambda: kept_now)
        grad_top = jnp.where(first_section, recv_grad.astype(jnp.float32), tail_grad)
        valid_back = jnp.where(first_section, valid_grid[late_index], valid_now)
        back_live = jnp.where(first_section, late_live, fwd_valid)
        grad_start, gain_pair, layer_now = lax.cond(
            back_live,
            lambda: layer_backward(kept_back, grad_top, valid_back, layer_weights),
            lambda: layer_zero(LEN, model_width, hidden_units),
        )
        layer_recs[moment] = layer_now
        gain_attn_sum = gain_attn_sum + gain_pair[0]
        gain_mlp_sum = gain_mlp_sum + gain_pair[1]
        if late_live:
            embed_now = lax.cond(
                first_section,
                lambda: embed_backward(
                    token_grid[late_index],
                    noise_grid[late_index],
                    levels[late_index],
                    grad_start,
                    table_full,
                    in_weight,
                ),
                lambda: embed_zero(LEN, model_width, emb_width),
            )
        else:
            embed_now = embed_zero(LEN, model_width, emb_width)
        embed_recs[moment] = embed_now
        if moment < MB:
            recv_act = passed_along(hidden_out.astype(jnp.bfloat16), "section", 1)
        if 1 <= moment <= MB:
            entropy_low = entropy.astype(jnp.bfloat16)
            recv_grad, loss_back = passed_along(
                (grad_start.astype(jnp.bfloat16), entropy_low), "section", -1
            )
            losses.append(jnp.where(first_section, loss_back, entropy_low))
    chosen = [
        jax.tree.map(
            lambda early, late: jnp.where(first_section, early, late),
            layer_recs[micro + 2],
            layer_recs[micro + 1],
        )
        for micro in range(MB)
    ]
    all_layer = layer_grads(joined_rows(chosen))
    all_tail = joined_rows([tail_recs[micro + 1] for micro in range(MB)])
    all_embed = joined_rows([embed_recs[micro + 2] for micro in range(MB)])
    all_edge = edge_grads(all_tail, all_embed, tokens)
    grad_pack = assemble(gain_attn_sum, gain_mlp_sum, all_layer, all_edge, gain_final_sum)
    parted = (
        lax.psum_scatter(
            grad_pack[0].astype(jnp.bfloat16), "dp", scatter_dimension=1, tiled=True
        ).astype(jnp.float32),
        lax.psum_scatter(
            grad_pack[1].astype(jnp.bfloat16), "dp", scatter_dimension=1, tiled=True
        ).astype(jnp.float32),
        lax.psum_scatter(
            grad_pack[2].astype(jnp.bfloat16), "dp", scatter_dimension=1, tiled=True
        ).astype(jnp.float32),
        lax.psum_scatter(
            grad_pack[3].astype(jnp.bfloat16), "dp", scatter_dimension=1, tiled=True
        ).astype(jnp.float32),
        lax.psum_scatter(
            grad_pack[4].astype(jnp.bfloat16), "dp", scatter_dimension=1, tiled=True
        ).astype(jnp.float32),
        lax.psum_scatter(
            grad_pack[5].astype(jnp.bfloat16), "dp", scatter_dimension=1, tiled=True
        ).astype(jnp.float32),
        lax.psum_scatter(
            grad_pack[6].astype(jnp.bfloat16), "dp", scatter_dimension=0, tiled=True
        ).astype(jnp.float32),
        lax.psum_scatter(
            grad_pack[7].astype(jnp.bfloat16), "dp", scatter_dimension=0, tiled=True
        ).astype(jnp.float32),
        lax.psum_scatter(
            grad_pack[8].astype(jnp.bfloat16), "dp", scatter_dimension=0, tiled=True
        ).astype(jnp.float32),
        lax.psum_scatter(
            grad_pack[9].astype(jnp.bfloat16), "dp", scatter_dimension=0, tiled=True
        ).astype(jnp.float32),
    )
    layer_total = (
        lax.psum(parted[0].astype(jnp.bfloat16), "group").astype(jnp.float32),
        lax.psum(parted[1].astype(jnp.bfloat16), "group").astype(jnp.float32),
        lax.psum(parted[2].astype(jnp.bfloat16), "group").astype(jnp.float32),
        lax.psum(parted[3].astype(jnp.bfloat16), "group").astype(jnp.float32),
        lax.psum(parted[4].astype(jnp.bfloat16), "group").astype(jnp.float32),
        lax.psum(parted[5].astype(jnp.bfloat16), "group").astype(jnp.float32),
    )
    edge_total = (
        lax.psum(parted[6].astype(jnp.bfloat16), ("section", "group")).astype(jnp.float32),
        lax.psum(parted[7].astype(jnp.bfloat16), ("section", "group")).astype(jnp.float32),
        lax.psum(parted[8].astype(jnp.bfloat16), ("section", "group")).astype(jnp.float32),
        lax.psum(parted[9].astype(jnp.bfloat16), ("section", "group")).astype(jnp.float32),
    )
    token_loss = jnp.concatenate(losses)
    return (
        token_loss,
        edge_total[0],
        edge_total[1],
        layer_total[0],
        layer_total[1],
        layer_total[2],
        layer_total[3],
        layer_total[4],
        layer_total[5],
        edge_total[2],
        edge_total[3],
    )


MESH = pl.DeviceIdType.MESH
ANYWHERE = pl.BlockSpec(memory_space=pl.ANY)


def pick(index, values):
    out = values[-1]
    for at in range(len(values) - 2, -1, -1):
        out = jnp.where(index == at, values[at], out)
    return out


def rows_at(start, size):
    return pl.ds(pl.multiple_of(start, 8), size)


def remote(src, dst, send_sem, recv_sem, device):
    return pltpu.make_async_remote_copy(
        src_ref=src,
        dst_ref=dst,
        send_sem=send_sem,
        recv_sem=recv_sem,
        device_id=device,
        device_id_type=MESH,
    )


def gather_kernel(count, first_order, last_order, *refs):
    shards = refs[:count]
    wholes = refs[count : 2 * count]
    own_sem, zsend, zrecv, psend, precv, gate = refs[2 * count : 2 * count + 6]
    stage = refs[2 * count + 6 :]
    sec = lax.axis_index("section")
    grp = lax.axis_index("group")
    pos = lax.axis_index("dp")
    beside = ((sec, grp ^ 1, pos), (sec, grp ^ 2, pos))
    above = (sec, grp, pos + 1)
    below = (sec, grp, pos - 1)
    partner = (1 - sec, grp, pos)
    barrier = pltpu.get_barrier_semaphore()
    both = bool(last_order)

    def greet(device):
        pl.semaphore_signal(barrier, inc=1, device_id=device, device_id_type=MESH)

    def meet():
        for device in beside + ((partner,) if both else ()):
            greet(device)

        @pl.when(pos > 0)
        def _():
            greet(below)

        @pl.when(pos < 3)
        def _():
            greet(above)

        at_end = (pos == 0) | (pos == 3)
        pl.semaphore_wait(barrier, jnp.where(at_end, 3, 4) + (1 if both else 0))

    turn = [pick(pos, v) for v in ((3, 1, 3, 1), (2, 3, 1, 2), (1, 2, 2, 3))]

    def run(order, before, middle):
        def rows_of(slot):
            return shards[order[slot][0]].shape[0]

        def part_of(slot):
            _, _, size, whole_line = order[slot]
            return size if whole_line else size // 4

        def shift(slot, who):
            _, lo, _, whole_line = order[slot]
            return lo if whole_line else lo + who * part_of(slot)

        def block(slot, origin, who):
            return rows_at(origin * rows_of(slot) + shift(slot, who), part_of(slot))

        staged = sorted({entry[0] for entry in order})

        def load_own(idx):
            return pltpu.make_async_copy(shards[idx], stage[idx], own_sem.at[idx])

        def store_own(idx):
            rows = shards[idx].shape[0]
            return pltpu.make_async_copy(
                stage[idx], wholes[idx].at[rows_at(pos * rows, rows)], own_sem.at[idx]
            )

        def own_ends(slot):
            idx = order[slot][0]
            src = shards[idx].at[rows_at(shift(slot, grp), part_of(slot))]
            dst = wholes[idx].at[block(slot, pos, grp)]
            return (
                (pos < 3, remote(src, dst, zsend.at[slot, 0], zrecv.at[slot, 1], above)),
                (pos > 0, remote(src, dst, zsend.at[slot, 1], zrecv.at[slot, 3], below)),
            )

        def start_own(slot):
            for goes, copy in own_ends(slot):
                pl.when(goes)(copy.start)

        def origin_of(j):
            return lax.rem(pos - turn[j] + 4, 4)

        def arrived(slot, j):
            here = wholes[order[slot][0]].at[block(slot, origin_of(j), grp)]
            return remote(here, here, zsend.at[slot, 2 + j], zrecv.at[slot, turn[j]], partner)

        def onward(slot, j):
            step = jnp.where(turn[j] <= pos, 1, -1)
            to = pos + step
            here = wholes[order[slot][0]].at[block(slot, origin_of(j), grp)]
            landed = jnp.clip(turn[j] + step, 0, 3)
            copy = remote(
                here,
                here,
                zsend.at[slot, 2 + j],
                zrecv.at[slot, landed],
                (sec, grp, jnp.clip(to, 0, 3)),
            )
            return (to >= 0) & (to <= 3), copy

        def plane(slot, j, way):
            idx = order[slot][0]
            origin = origin_of(j)
            if way < 2:
                here = wholes[idx].at[block(slot, origin, grp)]
                return remote(here, here, psend.at[slot, j, way], precv.at[slot, j, way], beside[way])
            half = shards[idx].shape[1] // 2
            there = wholes[idx].at[
                block(slot, origin, grp ^ (way - 1)), pl.ds(half * (way - 2), half)
            ]
            return remote(
                there, there, psend.at[slot, j, way], precv.at[slot, j, way], beside[3 - way]
            )

        items = [(slot, j) for j in range(3) for slot in range(len(order))]
        crossing = [item for item in items if not order[item[0]][3]]

        def first(slot, j):
            arrived(slot, j).wait_recv()
            goes, copy = onward(slot, j)
            pl.when(goes)(copy.start)
            if (slot, j) in crossing:
                plane(slot, j, 0).start()
                plane(slot, j, 1).start()

        def second(slot, j):
            if (slot, j) in crossing:
                for way in (0, 1):
                    plane(slot, j, way).wait_recv()
                    plane(slot, j, way + 2).start()

        if before is not None:
            before()
        for slot in range(len(order)):
            start_own(slot)
        for idx in staged:
            load_own(idx).start()
        lag = 4
        for at in range(len(items) + lag):
            if at < len(items):
                slot, j = items[at]
                if j == 1 and slot < len(staged):
                    load_own(staged[slot]).wait()
                    store_own(staged[slot]).start()
                first(slot, j)
            if at == len(items) - 1 and middle is not None:
                middle()
            if at >= lag:
                second(*items[at - lag])
        for slot, j in crossing:
            plane(slot, j, 2).wait_recv()
            plane(slot, j, 3).wait_recv()
        for idx in staged:
            store_own(idx).wait()
        for slot in range(len(order)):
            for goes, copy in own_ends(slot):
                pl.when(goes)(copy.wait_send)
        for slot, j in items:
            goes, copy = onward(slot, j)
            pl.when(goes)(copy.wait_send)
        for slot, j in crossing:
            for way in range(4):
                plane(slot, j, way).wait_send()

    def let_go():
        pl.semaphore_signal(gate, inc=1, device_id=partner, device_id_type=MESH)

    def hold():
        pl.semaphore_wait(gate, 1)

    if both:
        meet()

        @pl.when(sec == 0)
        def _():
            run(first_order, None, let_go)

        @pl.when(sec == 1)
        def _():
            run(last_order, hold, None)

    else:

        @pl.when(sec == 0)
        def _():
            meet()
            run(first_order, None, None)


def gather_all(shards, first_order, last_order, collective_id):
    count = len(shards)
    slots = max(len(first_order), len(last_order))
    return pl.pallas_call(
        functools.partial(gather_kernel, count, first_order, last_order),
        out_shape=[jax.ShapeDtypeStruct((s.shape[0] * 4, s.shape[1]), s.dtype) for s in shards],
        in_specs=[ANYWHERE] * count,
        out_specs=[ANYWHERE] * count,
        scratch_shapes=[
            pltpu.SemaphoreType.DMA((count,)),
            pltpu.SemaphoreType.DMA((slots, 5)),
            pltpu.SemaphoreType.DMA((slots, 4)),
            pltpu.SemaphoreType.DMA((slots, 3, 4)),
            pltpu.SemaphoreType.DMA((slots, 3, 4)),
            pltpu.SemaphoreType.REGULAR,
        ]
        + [pltpu.VMEM(s.shape, s.dtype) for s in shards],
        compiler_params=pltpu.CompilerParams(
            collective_id=collective_id, has_side_effects=True, vmem_limit_bytes=60 << 20
        ),
    )(*shards)


def swap_kernel(rows_ref, ids_ref, out_ref, ids_out, own_sem, send_sem, recv_sem):
    sec = lax.axis_index("section")
    grp = lax.axis_index("group")
    pos = lax.axis_index("dp")

    @pl.when(sec == 0)
    def _():
        barrier = pltpu.get_barrier_semaphore()
        peers = [(sec, grp, lax.rem(pos + k, 4)) for k in (1, 2, 3)]
        sides = [(sec, grp ^ j, pos) for j in (1, 2, 3)]
        for device in peers + sides:
            pl.semaphore_signal(barrier, inc=1, device_id=device, device_id_type=MESH)
        pl.semaphore_wait(barrier, 6)
        copies = []
        for k, device in enumerate(peers):
            copies.append(
                remote(rows_ref.at[device[2]], out_ref.at[pos], send_sem.at[k], recv_sem.at[k], device)
            )
        for k, device in enumerate(sides):
            copies.append(
                remote(ids_ref, ids_out.at[grp], send_sem.at[3 + k], recv_sem.at[3 + k], device)
            )
        for copy in copies:
            copy.start()
        own_rows = pltpu.make_async_copy(rows_ref.at[pos], out_ref.at[pos], own_sem.at[0])
        own_ids = pltpu.make_async_copy(ids_ref, ids_out.at[grp], own_sem.at[1])
        own_rows.start()
        own_ids.start()
        own_rows.wait()
        own_ids.wait()
        for copy in copies:
            copy.wait()


def swap_rows(rows, ids, collective_id):
    in_vmem = pl.BlockSpec(memory_space=pltpu.VMEM)
    return pl.pallas_call(
        swap_kernel,
        out_shape=[
            jax.ShapeDtypeStruct(rows.shape, rows.dtype),
            jax.ShapeDtypeStruct((4,) + ids.shape, ids.dtype),
        ],
        in_specs=[in_vmem] * 2,
        out_specs=[in_vmem] * 2,
        scratch_shapes=[
            pltpu.SemaphoreType.DMA((2,)),
            pltpu.SemaphoreType.DMA((6,)),
            pltpu.SemaphoreType.DMA((6,)),
        ],
        compiler_params=pltpu.CompilerParams(collective_id=collective_id, has_side_effects=True),
    )(rows, ids)


IN_VMEM = pl.BlockSpec(memory_space=pltpu.VMEM)
IN_SMEM = pl.BlockSpec(memory_space=pltpu.SMEM)
ROOT_HALF = 0.7071067811865476
ROOT_TWO_PI = 0.3989422804014327


def dot_nn(left, right):
    return lax.dot_general(
        left, right, (((1,), (0,)), ((), ())), preferred_element_type=jnp.float32
    )


def dot_nt(left, right):
    return lax.dot_general(
        left, right, (((1,), (1,)), ((), ())), preferred_element_type=jnp.float32
    )


def dot_tn(left, right):
    return lax.dot_general(
        left, right, (((0,), (0,)), ((), ())), preferred_element_type=jnp.float32
    )


def unit_rows(v):
    center = v - jnp.mean(v, -1, keepdims=True)
    scale = lax.rsqrt(jnp.mean(center * center, -1, keepdims=True) + EPS)
    return center * scale, scale


def split_heads(pair):
    low = lax.broadcasted_iota(jnp.int32, pair.shape, 1) < HEAD
    nothing = jnp.zeros_like(pair)
    return jnp.concatenate([jnp.where(low, pair, nothing), jnp.where(low, nothing, pair)], 0)


def join_heads(stacked):
    half = stacked.shape[0] // 2
    low = lax.broadcasted_iota(jnp.int32, (half, stacked.shape[1]), 1) < HEAD
    return jnp.where(low, stacked[:half], stacked[half:])


def pair_scores(keys, stacked_queries, key_count):
    scores = dot_nt(keys, stacked_queries) * 0.125
    valid = lax.broadcasted_iota(jnp.int32, scores.shape, 0) < key_count
    return jnp.where(valid, scores, MASKED)


STRIP = 64


def forward_kernel(only, tile, given, *refs):
    x, gain_attn, gain_mlp, counts, gain_final, wo, wq, wp, wu, wd = refs[:10]
    rest = refs[10 + given :]
    outs = rest[:KEPT_COUNT]
    last = rest[KEPT_COUNT : KEPT_COUNT + 1 + only]
    rest = rest[1 + only :]
    qv, pv, uv, dv = rest[KEPT_COUNT : KEPT_COUNT + 4]
    kept = rest[KEPT_COUNT + 4 : 2 * KEPT_COUNT + 4]
    a, att, m, acc, wsem, osem = rest[2 * KEPT_COUNT + 4 :]
    xv, at_t, qkv, lse, att_t, mid, m_t, pre, act_t, out = kept
    rows, width = a.shape
    units = dv.shape[0]

    def store(idx):
        return pltpu.make_async_copy(kept[idx], outs[idx], osem.at[idx])

    def run():
        loads = []

        def load(src, dst):
            copy = pltpu.make_async_copy(src, dst, wsem.at[len(loads)])
            copy.start()
            loads.append(copy)

        for lo in range(0, 3 * width, tile):
            load(wq.at[:, pl.ds(lo, tile)], qv.at[:, pl.ds(lo, tile)])
        load(wp, pv)
        for lo in range(0, units, tile):
            load(wu.at[:, pl.ds(lo, tile)], uv.at[:, pl.ds(lo, tile)])
            load(wd.at[pl.ds(lo, tile)], dv.at[pl.ds(lo, tile)])
        loads = iter(loads)
        for lo in range(0, rows, STRIP):
            here = pl.ds(lo, STRIP)
            xv[here, :] = x[here, :].astype(jnp.float32)
            a[here, :] = (unit_rows(xv[here, :])[0] * gain_attn[...]).astype(jnp.bfloat16)
        store(0).start()
        for lo in range(0, 3 * width, tile):
            next(loads).wait()
            cols = pl.ds(lo, tile)
            qkv[:, cols] = dot_nn(a[...], qv[:, cols]).astype(jnp.bfloat16)
        store(2).start()
        for lo in range(0, width, 256):
            at_t[pl.ds(lo, 256), :] = a[:, pl.ds(lo, 256)].T
        store(1).start()
        pairs = width // 128
        for seq in range(rows // LEN):
            here = pl.ds(seq * LEN, LEN)
            for pair in range(pairs):
                stacked = split_heads(qkv[here, pl.ds(pair * 128, 128)])
                scores = pair_scores(qkv[here, pl.ds(width + pair * 128, 128)], stacked, counts[seq])
                top = jnp.max(scores, 0, keepdims=True)
                power = jnp.exp(scores - top)
                total = jnp.sum(power, 0, keepdims=True)
                lse[seq * pairs + pair] = top + jnp.log(total)
                probs = (power * (1.0 / total)).astype(jnp.bfloat16)
                mixed = dot_tn(probs, qkv[here, pl.ds(2 * width + pair * 128, 128)])
                att[here, pl.ds(pair * 128, 128)] = join_heads(mixed).astype(jnp.bfloat16)
        store(3).start()
        for lo in range(0, width, 256):
            att_t[pl.ds(lo, 256), :] = att[:, pl.ds(lo, 256)].T
        store(4).start()
        next(loads).wait()
        for lo in range(0, width, tile):
            cols = pl.ds(lo, tile)
            mid[:, cols] = xv[:, cols] + dot_nn(att[...], pv[:, cols])
        for lo in range(0, rows, STRIP):
            here = pl.ds(lo, STRIP)
            m[here, :] = (unit_rows(mid[here, :])[0] * gain_mlp[...]).astype(jnp.bfloat16)
        store(5).start()
        acc[...] = mid[...]
        for lo in range(0, units, tile):
            cols = pl.ds(lo, tile)
            next(loads).wait()
            before = dot_nn(m[...], uv[:, cols])
            pre[:, cols] = before
            active = (0.5 * before * (1.0 + lax.erf(before * ROOT_HALF))).astype(jnp.bfloat16)
            act_t[cols, :] = active.T
            next(loads).wait()
            acc[...] += dot_nn(active, dv[cols, :])
        store(7).start()
        store(8).start()
        for lo in range(0, width, 256):
            m_t[pl.ds(lo, 256), :] = m[:, pl.ds(lo, 256)].T
        store(6).start()
        out[...] = acc[...]
        store(9).start()
        if only == 0:
            last[0][...] = acc[...].astype(jnp.bfloat16)
        else:
            for lo in range(0, rows, STRIP):
                here = pl.ds(lo, STRIP)
                last[0][here, :] = (unit_rows(acc[here, :])[0] * gain_final[...]).astype(jnp.bfloat16)
            last[1][...] = dot_nn(last[0][...], wo[...]).astype(jnp.bfloat16)
        for idx in range(KEPT_COUNT):
            store(idx).wait()

    pl.when(lax.axis_index("section") == only)(run)


KEPT_COUNT = 10


def kept_shapes(rows, width, units):
    f32, low = jnp.float32, jnp.bfloat16
    return [
        jax.ShapeDtypeStruct(shape, kind)
        for shape, kind in (
            ((rows, width), f32),
            ((width, rows), low),
            ((rows, 3 * width), low),
            ((rows // LEN * width // 128, 1, 2 * LEN), f32),
            ((width, rows), low),
            ((rows, width), f32),
            ((width, rows), low),
            ((rows, units), f32),
            ((units, rows), low),
            ((rows, width), f32),
        )
    ]


def run_forward(only, x, gain_attn, gain_mlp, counts, gain_final, out_weight, weights, kept):
    wq, wp, wu, wd = weights
    rows, width = x.shape
    units = wd.shape[0]
    tile = 512
    shapes = kept_shapes(rows, width, units)
    low = jnp.bfloat16
    given = 0 if kept is None else KEPT_COUNT
    in_specs = [IN_VMEM] * 3 + [IN_SMEM] + [IN_VMEM] * 2 + [ANYWHERE] * (4 + given)
    extra = [jax.ShapeDtypeStruct((rows, width), low)]
    if only == 1:
        extra.append(jax.ShapeDtypeStruct((rows, out_weight.shape[1]), low))
    return pl.pallas_call(
        functools.partial(forward_kernel, only, tile, given),
        out_shape=shapes + extra,
        in_specs=in_specs,
        out_specs=[ANYWHERE] * KEPT_COUNT + [IN_VMEM] * len(extra),
        input_output_aliases={10 + idx: idx for idx in range(given)},
        scratch_shapes=[pltpu.VMEM(w.shape, w.dtype) for w in weights]
        + [pltpu.VMEM(s.shape, s.dtype) for s in shapes]
        + [
            pltpu.VMEM((rows, width), low),
            pltpu.VMEM((rows, width), low),
            pltpu.VMEM((rows, width), low),
            pltpu.VMEM((rows, width), jnp.float32),
            pltpu.SemaphoreType.DMA((3 * width // tile + 1 + 2 * units // tile,)),
            pltpu.SemaphoreType.DMA((KEPT_COUNT,)),
        ],
        compiler_params=pltpu.CompilerParams(vmem_limit_bytes=56 << 20),
    )(x, gain_attn, gain_mlp, counts, gain_final, out_weight, wq, wp, wu, wd, *(kept or ()))


GRAD_COUNT = 6


def grad_shapes(rows, width, units):
    f32, low = jnp.float32, jnp.bfloat16
    return [
        jax.ShapeDtypeStruct(shape, kind)
        for shape, kind in (
            ((rows, width), low),
            ((rows, units), low),
            ((rows, width), low),
            ((rows, 3 * width), low),
            ((rows, width), low),
            ((8, width), f32),
        )
    ]


def norm_pull(v, gain, upstream):
    unit, scale = unit_rows(v)
    pulled = upstream * gain
    inner = jnp.mean(pulled * unit, -1, keepdims=True)
    grad = (pulled - jnp.mean(pulled, -1, keepdims=True) - unit * inner) * scale
    return grad, jnp.sum(upstream * unit, 0, keepdims=True)


def backward_kernel(only, tile, given, *refs):
    grad_in, gain_attn, gain_mlp, counts, gain_final, wo, out_in = refs[:7]
    x_in, qkv_in, lse_in, mid_in, pre_in, wq, wp, wu, wd = refs[7:16]
    rest = refs[16 + given :]
    outs = rest[:GRAD_COUNT]
    qv, pv, uv, dv = rest[GRAD_COUNT : GRAD_COUNT + 4]
    made = rest[GRAD_COUNT + 4 : 2 * GRAD_COUNT + 4]
    x, qkv, lse, mid, pre, gm, gmid, gatt, gtop, wsem, ksem, osem = rest[2 * GRAD_COUNT + 4 :]
    grad = gtop if only == 1 else grad_in
    gy, gpre, gz, gqkv, gx, gains = made
    rows, width = gm.shape
    units = dv.shape[0]

    def store(idx):
        return pltpu.make_async_copy(made[idx], outs[idx], osem.at[idx])

    def run():
        loads = []

        def load(src, dst):
            copy = pltpu.make_async_copy(src, dst, wsem.at[len(loads)])
            copy.start()
            loads.append(copy)

        kept = [
            pltpu.make_async_copy(src, dst, ksem.at[idx])
            for idx, (src, dst) in enumerate(
                ((pre_in, pre), (mid_in, mid), (qkv_in, qkv), (lse_in, lse), (x_in, x))
            )
        ]
        if only == 1:
            kept.append(pltpu.make_async_copy(out_in, gtop, ksem.at[5]))
            kept[5].start()
        kept[0].start()
        for lo in range(0, units, tile):
            load(wd.at[pl.ds(lo, tile)], dv.at[pl.ds(lo, tile)])
            load(wu.at[:, pl.ds(lo, tile)], uv.at[:, pl.ds(lo, tile)])
        for copy in kept[1:5]:
            copy.start()
        load(wp, pv)
        load(wq, qv)
        loads = iter(loads)
        gains[...] = jnp.zeros_like(gains)
        if only == 1:
            for copy in kept[5:]:
                copy.wait()
            gmid[...] = dot_nt(grad_in[...], wo[...])
            for lo in range(0, rows, STRIP):
                here = pl.ds(lo, STRIP)
                step, gain = norm_pull(gtop[here, :], gain_final[...], gmid[here, :])
                gtop[here, :] = step
                gains[2:3, :] += gain
        gy[...] = grad[...].astype(jnp.bfloat16)
        store(0).start()
        kept[0].wait()
        gm[...] = jnp.zeros_like(gm)
        for lo in range(0, units, tile):
            cols = pl.ds(lo, tile)
            next(loads).wait()
            pulled = dot_nt(gy[...], dv[cols, :])
            before = pre[:, cols]
            slope = 0.5 * (1.0 + lax.erf(before * ROOT_HALF)) + before * (
                ROOT_TWO_PI * jnp.exp(-0.5 * before * before)
            )
            low = (pulled * slope).astype(jnp.bfloat16)
            gpre[:, cols] = low
            next(loads).wait()
            gm[...] += dot_nt(low, uv[:, cols])
        store(1).start()
        kept[1].wait()
        for lo in range(0, rows, STRIP):
            here = pl.ds(lo, STRIP)
            step, gain = norm_pull(mid[here, :], gain_mlp[...], gm[here, :])
            total = grad[here, :].astype(jnp.float32) + step
            gmid[here, :] = total
            gz[here, :] = total.astype(jnp.bfloat16)
            gains[1:2, :] += gain
        store(2).start()
        next(loads).wait()
        gatt[...] = dot_nt(gz[...], pv[...]).astype(jnp.bfloat16)
        kept[2].wait()
        kept[3].wait()
        pairs = width // 128
        for seq in range(rows // LEN):
            here = pl.ds(seq * LEN, LEN)
            for pair in range(pairs):
                own = pl.ds(pair * 128, 128)
                stacked = split_heads(qkv[here, own])
                pulled = split_heads(gatt[here, own])
                keys = qkv[here, pl.ds(width + pair * 128, 128)]
                values = qkv[here, pl.ds(2 * width + pair * 128, 128)]
                probs = jnp.exp(pair_scores(keys, stacked, counts[seq]) - lse[seq * pairs + pair])
                gprobs = dot_nt(values, pulled)
                inner = jnp.sum(probs * gprobs, 0, keepdims=True)
                gscores = (probs * (gprobs - inner)).astype(jnp.bfloat16)
                gqkv[here, own] = (join_heads(dot_tn(gscores, keys)) * 0.125).astype(jnp.bfloat16)
                gqkv[here, pl.ds(width + pair * 128, 128)] = (dot_nn(gscores, stacked) * 0.125).astype(
                    jnp.bfloat16
                )
                gqkv[here, pl.ds(2 * width + pair * 128, 128)] = dot_nn(
                    probs.astype(jnp.bfloat16), pulled
                ).astype(jnp.bfloat16)
        store(3).start()
        next(loads).wait()
        for lo in range(0, width, 256):
            gm[:, pl.ds(lo, 256)] = dot_nt(gqkv[...], qv[pl.ds(lo, 256), :])
        kept[4].wait()
        for lo in range(0, rows, STRIP):
            here = pl.ds(lo, STRIP)
            step, gain = norm_pull(x[here, :], gain_attn[...], gm[here, :])
            gx[here, :] = (gmid[here, :] + step).astype(jnp.bfloat16)
            gains[0:1, :] += gain
        store(4).start()
        store(5).start()
        for idx in range(GRAD_COUNT):
            store(idx).wait()

    pl.when(lax.axis_index("section") == only)(run)


def run_backward(only, grad, gain_attn, gain_mlp, counts, gain_final, out_weight, kept, weights, made):
    wq, wp, wu, wd = weights
    x, _, qkv, lse, _, mid, _, pre, _, out = kept
    rows, width = x.shape
    units = wd.shape[0]
    tile = 512
    shapes = grad_shapes(rows, width, units)
    low, f32 = jnp.bfloat16, jnp.float32
    given = 0 if made is None else GRAD_COUNT
    in_specs = [IN_VMEM] * 3 + [IN_SMEM] + [IN_VMEM] * 2 + [ANYWHERE] * (10 + given)
    return pl.pallas_call(
        functools.partial(backward_kernel, only, tile, given),
        out_shape=shapes,
        in_specs=in_specs,
        out_specs=[ANYWHERE] * GRAD_COUNT,
        input_output_aliases={16 + idx: idx for idx in range(given)},
        scratch_shapes=[pltpu.VMEM(w.shape, w.dtype) for w in weights]
        + [pltpu.VMEM(s.shape, s.dtype) for s in shapes]
        + [pltpu.VMEM(s.shape, s.dtype) for s in (x, qkv, lse, mid, pre)]
        + [
            pltpu.VMEM((rows, width), f32),
            pltpu.VMEM((rows, width), f32),
            pltpu.VMEM((rows, width), low),
            pltpu.VMEM((rows, width), f32),
            pltpu.SemaphoreType.DMA((2 + 2 * units // tile,)),
            pltpu.SemaphoreType.DMA((6,)),
            pltpu.SemaphoreType.DMA((GRAD_COUNT,)),
        ],
        compiler_params=pltpu.CompilerParams(vmem_limit_bytes=56 << 20),
    )(
        grad, gain_attn, gain_mlp, counts, gain_final, out_weight, out, x, qkv, lse, mid, pre, wq, wp, wu, wd, *(made or ())
    )


def vocabulary_kernel(tile, proj, ids, scale, table, gproj_out, loss_out, gtable, *scratch):
    tv, gt, pall, gp, gsend, gin, stat, stats, whole, tsem, gsem, psem, prem, ssem, srem, qsem, qrem = scratch
    rows = proj.shape[0]
    vocab = tv.shape[0]
    count = vocab // tile
    sec = lax.axis_index("section")
    grp = lax.axis_index("group")
    pos = lax.axis_index("dp")
    places = [lax.rem(pos + k, 4) for k in range(4)]
    peers = [(sec, grp, place) for place in places[1:]]
    across = [(1 - sec, grp, place) for place in places]
    barrier = pltpu.get_barrier_semaphore()

    def hand(k):
        return remote(proj, pall.at[pos], psem.at[k], prem.at[k], across[k])

    def back(k):
        return remote(gsend.at[places[k]], gin.at[k], qsem.at[k], qrem.at[k], across[k])

    def greet(devices):
        for device in devices:
            pl.semaphore_signal(barrier, inc=1, device_id=device, device_id_type=MESH)

    def give():
        greet(across)
        pl.semaphore_wait(barrier, 4)
        for k in (2, 1, 3, 0):
            hand(k).start()
        for k in range(4):
            back(k).wait_recv()
        summed = gin[0].astype(jnp.float32)
        for k in (1, 2, 3):
            summed = summed + gin[k].astype(jnp.float32)
        gproj_out[...] = summed.astype(jnp.bfloat16)
        for k in range(4):
            hand(k).wait_send()

    def score():
        load = pltpu.make_async_copy(table, tv, tsem)
        load.start()
        greet(across + peers)
        pl.semaphore_wait(barrier, 7)
        load.wait()
        for k in range(4):
            hand(k).wait_recv()
        line_rows = pall[...].reshape(4 * rows, pall.shape[2])

        def logits_of(at):
            return dot_nt(tv[rows_at(at * tile, tile), :], line_rows)

        def hits_of(at):
            names = lax.broadcasted_iota(jnp.int32, (tile, 4 * rows), 0) + (at * tile + pos * vocab)
            return names == ids[...]

        stat[0:1, :] = jnp.full((1, 4 * rows), MASKED, jnp.float32)
        stat[1:8, :] = jnp.zeros((7, 4 * rows), jnp.float32)

        def measure(at, carry):
            logits = logits_of(at)
            top = stat[0:1, :]
            higher = jnp.maximum(top, jnp.max(logits, 0, keepdims=True))
            stat[1:2, :] = stat[1:2, :] * jnp.exp(top - higher) + jnp.sum(
                jnp.exp(logits - higher), 0, keepdims=True
            )
            stat[2:3, :] += jnp.sum(jnp.where(hits_of(at), logits, 0.0), 0, keepdims=True)
            stat[0:1, :] = higher
            return carry

        lax.fori_loop(0, count, measure, 0)
        second = [
            remote(stat, stats.at[pos], ssem.at[k], srem.at[k], peers[k]) for k in range(3)
        ]
        for copy in second:
            copy.start()
        stats[pos] = stat[...]
        gp[...] = jnp.zeros_like(gp)
        for copy in second:
            copy.wait()
        top = stats[0, 0:1, :]
        for z in (1, 2, 3):
            top = jnp.maximum(top, stats[z, 0:1, :])
        total = jnp.zeros_like(top)
        picked = jnp.zeros_like(top)
        for z in range(4):
            total = total + stats[z, 1:2, :] * jnp.exp(stats[z, 0:1, :] - top)
            picked = picked + stats[z, 2:3, :]
        log_total = top + jnp.log(total)
        whole[...] = jnp.where(scale[...] > 0, log_total - picked, 0.0)
        loss_out[...] = whole[:, pl.ds(pl.multiple_of(pos * rows, 128), rows)]

        def pull(at, carry):
            here = rows_at(at * tile, tile)
            probs = jnp.exp(logits_of(at) - log_total)
            grads = ((probs - jnp.where(hits_of(at), 1.0, 0.0)) * scale[...]).astype(jnp.bfloat16)
            gp[...] += dot_tn(grads, tv[here, :])
            gt[here, :] = dot_nn(grads, line_rows).astype(jnp.bfloat16)
            return carry

        lax.fori_loop(0, count, pull, 0)
        gsend[...] = gp[...].astype(jnp.bfloat16).reshape(gsend.shape)
        for k in (2, 1, 3, 0):
            back(k).start()
        keep = pltpu.make_async_copy(gt, gtable, gsem)
        keep.start()
        for k in range(4):
            back(k).wait_send()
        keep.wait()

    pl.when(sec == 0)(score)
    pl.when(sec == 1)(give)


def run_vocabulary(proj, ids, scale, table, collective_id):
    rows, emb = proj.shape
    low, f32, dma = jnp.bfloat16, jnp.float32, pltpu.SemaphoreType.DMA
    return pl.pallas_call(
        functools.partial(vocabulary_kernel, 1024),
        out_shape=[
            jax.ShapeDtypeStruct((rows, emb), low),
            jax.ShapeDtypeStruct((1, rows), f32),
            jax.ShapeDtypeStruct(table.shape, low),
        ],
        in_specs=[IN_VMEM] * 3 + [ANYWHERE],
        out_specs=[IN_VMEM] * 2 + [ANYWHERE],
        scratch_shapes=[
            pltpu.VMEM(table.shape, low),
            pltpu.VMEM(table.shape, low),
            pltpu.VMEM((4, rows, emb), low),
            pltpu.VMEM((4 * rows, emb), f32),
            pltpu.VMEM((4, rows, emb), low),
            pltpu.VMEM((4, rows, emb), low),
            pltpu.VMEM((8, 4 * rows), f32),
            pltpu.VMEM((4, 8, 4 * rows), f32),
            pltpu.VMEM((1, 4 * rows), f32),
            dma,
            dma,
            dma((4,)),
            dma((4,)),
            dma((3,)),
            dma((3,)),
            dma((4,)),
            dma((4,)),
        ],
        compiler_params=pltpu.CompilerParams(
            collective_id=collective_id, has_side_effects=True, vmem_limit_bytes=60 << 20
        ),
    )(proj, ids, scale, table)


def widen_kernel(count, *refs):
    for src, dst in zip(refs[:count], refs[count:]):
        dst[...] = src[...].astype(jnp.float32)


def widen(arrays):
    steps = 8

    def spec(x):
        return pl.BlockSpec((x.shape[0] // steps, x.shape[1]), lambda at: (at, 0))

    size = sum(x.size for x in arrays)
    return pl.pallas_call(
        functools.partial(widen_kernel, len(arrays)),
        grid=(steps,),
        out_shape=[jax.ShapeDtypeStruct(x.shape, jnp.float32) for x in arrays],
        in_specs=[spec(x) for x in arrays],
        out_specs=[spec(x) for x in arrays],
        cost_estimate=pl.CostEstimate(flops=size, bytes_accessed=6 * size, transcendentals=0),
        compiler_params=pltpu.CompilerParams(vmem_limit_bytes=60 << 20),
    )(*arrays)


def strip_of(rows, columns):
    strip = 16
    while 2 * strip * columns <= 65536 and rows % (2 * strip) == 0:
        strip = 2 * strip
    return strip


def add_rows(store, terms, rows, columns):
    strip = strip_of(rows, columns)

    def body(at, carry):
        here = rows_at(at * strip, strip)
        total = terms[0](here).astype(jnp.float32)
        for term in terms[1:]:
            total = total + term(here).astype(jnp.float32)
        store(here, total)
        return carry

    lax.fori_loop(0, rows // strip, body, 0)


def reduce_kernel(plan, only, extras, pace, refs_of, *refs):
    body = functools.partial(reduce_body, plan, extras, pace, refs_of(refs))
    if only is None:
        body()
    else:
        pl.when(lax.axis_index("section") == only)(body)


def stage_blocks(order):
    left = list(range(1 << len(order)))
    kept = []
    for bit in order:
        left = [r for r in left if not (r >> bit) & 1]
        kept.append(left)
    return kept


def reduce_body(plan, extras, pace, named):
    arrays, outs = named["arrays"], named["outs"]
    own, got1, got2, got3, got4, land = (
        named[k] for k in ("own", "got1", "got2", "got3", "got4", "land")
    )
    ssem, rsem, own_sem, s4, r4, fin_sem = named["sems"]
    got = (got1, got2, got3, got4)
    count = len(plan)
    sec = lax.axis_index("section")
    grp = lax.axis_index("group")
    pos = lax.axis_index("dp")
    beside = ((sec, grp ^ 1, pos), (sec, grp ^ 2, pos))
    swaps = beside + ((sec, grp, pos ^ 1), (sec, grp, pos ^ 2))
    sides = [(sec, grp ^ j, pos) for j in (1, 2, 3)]
    line_peers = [(sec, grp, lax.rem(pos + k, 4)) for k in (1, 2, 3)]
    steps = [(jg, jz) for jg in range(4) for jz in range(4)][1:]
    kept = [stage_blocks(piece[1]) for piece in plan]

    def other(j):
        return (sec, grp ^ steps[j][0], lax.rem(pos + steps[j][1], 4))

    with_gains = "gains" in extras
    spreads = "spread" in extras
    looked = "looked" in extras
    if with_gains:
        peers = [other(j) for j in range(15)]
    elif looked:
        peers = sides + line_peers
    else:
        peers = [swaps[bit] for bit in sorted(plan[0][1])]
    barrier = pltpu.get_barrier_semaphore()
    for device in peers:
        pl.semaphore_signal(barrier, inc=1, device_id=device, device_id_type=MESH)
    pl.semaphore_wait(barrier, len(peers))

    def rows_of(p):
        return arrays[plan[p][0]].shape[0] // (len(kept[p][0]) // 2)

    def columns_of(p):
        return arrays[plan[p][0]].shape[1]

    def sub_of(p):
        return rows_of(p) // 4 // plan[p][3]

    def block(p, r):
        who = grp ^ (r & 3)
        line = pos ^ (r >> 2) if len(plan[p][1]) == 4 else 0
        start = line * rows_of(p) + who * (rows_of(p) // 4) + plan[p][2] * sub_of(p)
        return arrays[plan[p][0]].at[rows_at(start, sub_of(p))]

    def spot(p, r):
        return kept[p][0].index(r)

    def swap(p, stage, at):
        bit = plan[p][1][stage]
        r = kept[p][stage][at] | (1 << bit)
        src = block(p, r) if stage == 0 else own[p].at[spot(p, r)]
        return remote(
            src, got[stage][p].at[at], ssem.at[p, stage, at], rsem.at[p, stage, at], swaps[bit]
        )

    def load_own(p, at):
        return pltpu.make_async_copy(block(p, kept[p][0][at]), own[p].at[at], own_sem.at[p, at])

    def order_of(p, stage):
        places = range(len(kept[p][stage]))
        if stage == len(plan[p][1]) - 1:
            return list(places)
        bit = plan[p][1][stage + 1]
        return sorted(places, key=lambda at: 1 - ((kept[p][stage][at] >> bit) & 1))

    def begin(p):
        for at in order_of(p, 0):
            swap(p, 0, at).start()
            load_own(p, at).start()

    def advance(p, stage):
        for at in order_of(p, stage):
            r = kept[p][stage][at]
            place = spot(p, r)
            if stage == 0:
                load_own(p, at).wait()
            swap(p, stage, at).wait_recv()
            terms = [
                lambda here, place=place: own[p][place, here, :],
                lambda here, at=at: got[stage][p][at, here, :],
            ]
            if stage == len(plan[p][1]) - 1:
                settle(p, terms)
                return

            def store(here, total, place=place):
                own[p][place, here, :] = total.astype(jnp.bfloat16)

            add_rows(store, terms, sub_of(p), columns_of(p))
            bit = plan[p][1][stage + 1]
            if (r >> bit) & 1:
                swap(p, stage + 1, kept[p][stage + 1].index(r ^ (1 << bit))).start()

    def write_out(p, who, at):
        start = who * (rows_of(p) // 4) + plan[p][2] * sub_of(p)
        return pltpu.make_async_copy(
            land[p].at[who], outs[plan[p][0]].at[rows_at(start, sub_of(p))], named["out_sem"].at[p, at]
        )

    def spread(p, way):
        if way < 2:
            here = land[p].at[grp]
            return remote(here, here, s4.at[p, way], r4.at[p, way], beside[way])
        half = columns_of(p) // 2
        there = land[p].at[grp ^ (way - 1), :, pl.ds(half * (way - 2), half)]
        return remote(there, there, s4.at[p, way], r4.at[p, way], beside[3 - way])

    def settle(p, terms):
        mine = grp if spreads else 0

        def store(here, total):
            land[p][mine, here, :] = total.astype(jnp.bfloat16)

        add_rows(store, terms, sub_of(p), columns_of(p))
        if spreads:
            spread(p, 0).start()
            spread(p, 1).start()
        else:
            own_out(p).start()

    def own_out(p):
        return pltpu.make_async_copy(
            land[p].at[0], outs[plan[p][0]].at[rows_at(plan[p][2] * sub_of(p), sub_of(p))], fin_sem.at[p]
        )

    def arrival(p, way):
        who = (grp ^ 1, grp ^ 2)[way]
        return remote(land[p].at[who], land[p].at[who], s4.at[p, way], r4.at[p, way], beside[way])

    def pass_on(p):
        if spreads:
            for way in (0, 1):
                arrival(p, way).wait_recv()
                spread(p, way + 2).start()

    def write_near(p):
        if spreads:
            for at, who in enumerate((grp, grp ^ 1, grp ^ 2)):
                write_out(p, who, at).start()

    def write_far(p):
        if spreads:
            spread(p, 2).wait_recv()
            spread(p, 3).wait_recv()
            write_out(p, grp ^ 3, 3).start()

    if with_gains:
        gain_in, gain_got, sg, rg, gain_sem = named["gain_scratch"]

        def gain_copy(j):
            device = other(j)
            return remote(gain_in.at[device[2]], gain_got.at[j], sg.at[j], rg.at[j], device)

        gain_load = pltpu.make_async_copy(named["gains"], gain_in, gain_sem)
        gain_load.start()

    if looked:
        looks, looks_own, sl, rl, table_fin, tland, tsum = named["look_scratch"]
        ids, look_in, fin_in = named["look_in"]
        vocab_quarter = fin_in.shape[0]
        look_load = pltpu.make_async_copy(look_in, looks.at[grp, pos], looks_own.at[0])
        fin_load = pltpu.make_async_copy(fin_in, table_fin, looks_own.at[1])

        def look_line(k):
            here = looks.at[grp, pos]
            return remote(here, here, sl.at[k], rl.at[k], line_peers[k])

        def look_side(k):
            here = looks.at[grp]
            return remote(here, here, sl.at[3 + k], rl.at[3 + k], sides[k])

        def table_spread(way):
            if way < 2:
                here = tland.at[grp]
                return remote(here, here, sl.at[6 + way], rl.at[6 + way], beside[way])
            half = tland.shape[2] // 2
            there = tland.at[grp ^ (way - 1), :, pl.ds(half * (way - 2), half)]
            return remote(there, there, sl.at[6 + way], rl.at[6 + way], beside[3 - way])

        def table_out(who):
            return pltpu.make_async_copy(
                tland.at[who],
                named["table_out"].at[rows_at(who * vocab_quarter, vocab_quarter)],
                looks_own.at[2 + who],
            )

        def look_begin():
            look_load.start()
            fin_load.start()
            look_load.wait()
            for k in range(3):
                look_line(k).start()

        def look_middle():
            for k in range(3):
                look_line(k).wait_recv()
            for k in range(3):
                look_side(k).start()

        def look_sum():
            for k in range(3):
                look_side(k).wait_recv()
            fin_load.wait()
            base = pos * (4 * vocab_quarter) + grp * vocab_quarter
            tall = 256
            names = lax.broadcasted_iota(jnp.int32, (tall, ids.shape[2]), 0)

            def body(at, carry):
                here = rows_at(at * tall, tall)
                total = table_fin[here, :].astype(jnp.float32)
                for g in range(4):
                    for z in range(4):
                        hit = names + (base + at * tall) == ids[g * 4 + z]
                        total = total + dot_nn(
                            jnp.where(hit, 1.0, 0.0).astype(jnp.bfloat16), looks[g, z]
                        )
                tland[grp, here, :] = total.astype(jnp.bfloat16)
                return carry

            lax.fori_loop(0, vocab_quarter // tall, body, 0)
            table_spread(0).start()
            table_spread(1).start()

        def look_pass():
            for way in (0, 1):
                who = (grp ^ 1, grp ^ 2)[way]
                remote(
                    tland.at[who], tland.at[who], sl.at[6 + way], rl.at[6 + way], beside[way]
                ).wait_recv()
                table_spread(way + 2).start()

        def look_end():
            table_spread(2).wait_recv()
            table_spread(3).wait_recv()
            for who in range(4):
                table_out(who).start()
            for who in range(4):
                table_out(who).wait()
            for k in range(3):
                look_line(k).wait_send()
                look_side(k).wait_send()
            for way in range(4):
                table_spread(way).wait_send()

        def on_first(run):
            pl.when(sec == 0)(run)

    else:

        def on_first(run):
            pass

        look_begin = look_middle = look_sum = look_pass = look_end = None

    ahead, lag, lag_end = pace
    on_first(look_begin)
    for p in range(min(ahead, count)):
        begin(p)
    if with_gains:
        gain_load.wait()
        for j in range(15):
            gain_copy(j).start()
    delays = [0, lag, 2 * lag, 3 * lag, 3 * lag + lag_end, 3 * lag + 2 * lag_end, 3 * lag + 3 * lag_end]
    for at in range(count + delays[-1]):
        if ahead + at < count:
            begin(ahead + at)
        for stage in range(len(plan[0][1])):
            if 0 <= at - delays[stage] < count:
                advance(at - delays[stage], stage)
        for run, delay in zip((pass_on, write_near, write_far), delays[4:]):
            if 0 <= at - delay < count:
                run(at - delay)
        for when, run in ((1, look_middle), (3, look_sum), (5, look_pass)):
            if at == when * (count + delays[3]) // 6:
                on_first(run)
    if with_gains:
        for j in range(15):
            gain_copy(j).wait_recv()
        total = gain_in[pos]
        for j in range(15):
            total = total + gain_got[j]
        named["gain_out"][...] = total
    on_first(look_end)
    for p in range(count):
        if spreads:
            for at, who in enumerate((grp, grp ^ 1, grp ^ 2, grp ^ 3)):
                write_out(p, who, at).wait()
            for way in range(4):
                spread(p, way).wait_send()
        else:
            own_out(p).wait()
        for stage in range(len(plan[p][1])):
            for at in range(len(kept[p][stage])):
                swap(p, stage, at).wait_send()
    if with_gains:
        for j in range(15):
            gain_copy(j).wait_send()


def reduce_all(arrays, plan, only, collective_id, pace, gains=None, look=None, spread=True):
    low, f32, dma = jnp.bfloat16, jnp.float32, pltpu.SemaphoreType.DMA
    extras = ("spread",) * spread + ("gains",) * (gains is not None) + ("looked",) * (look is not None)
    count = len(plan)
    inputs = list(arrays)
    lines = 4 if len(plan[0][1]) == 4 else 1
    share = lines if spread else 4 * lines
    outs = [jax.ShapeDtypeStruct((x.shape[0] // share, x.shape[1]), low) for x in arrays]
    out_specs = [ANYWHERE] * len(arrays)
    in_specs = [ANYWHERE] * len(arrays)
    names = ["own", "got1", "got2", "got3", "got4", "land"]
    scratch = {name: [] for name in names}
    for src, _, _, chunks in plan:
        rows, columns = arrays[src].shape[0] // lines, arrays[src].shape[1]
        sub = rows // 4 // chunks
        held = (8, 8, 4, 2, 1) if lines == 4 else (2, 2, 1, 0, 0)
        for name, blocks in zip(names, held + (4 if spread else 1,)):
            shape = (blocks, sub, columns) if blocks else (8, 128)
            scratch[name].append(pltpu.VMEM(shape, low))
    flat = [item for name in names for item in scratch[name]]
    sems = [dma((count, 4, 8))] * 2 + [dma((count, 8))] + [dma((count, 4))] * 2 + [dma((count,))]
    tail = []
    if spread:
        tail += [dma((count, 4))]
    if gains is not None:
        inputs.append(gains)
        in_specs.append(ANYWHERE)
        outs.append(jax.ShapeDtypeStruct(gains.shape[1:], f32))
        out_specs.append(IN_VMEM)
        tail += [
            pltpu.VMEM(gains.shape, f32),
            pltpu.VMEM((15,) + gains.shape[1:], f32),
            dma((15,)),
            dma((15,)),
            dma,
        ]
    if look is not None:
        ids, rows_in, fin_in = look
        inputs += [ids, rows_in, fin_in]
        in_specs += [IN_VMEM, ANYWHERE, ANYWHERE]
        quarter, emb = fin_in.shape
        outs.append(jax.ShapeDtypeStruct((4 * quarter, emb), low))
        out_specs.append(ANYWHERE)
        tail += [
            pltpu.VMEM((4, 4) + rows_in.shape, low),
            dma((6,)),
            dma((10,)),
            dma((10,)),
            pltpu.VMEM(fin_in.shape, low),
            pltpu.VMEM((4, quarter, emb), low),
            pltpu.VMEM((8, 128), f32),
        ]

    def refs_of(refs):
        at = 0

        def take(n):
            nonlocal at
            at += n
            return list(refs[at - n : at])

        named = {"arrays": take(len(arrays))}
        if gains is not None:
            named["gains"] = take(1)[0]
        if look is not None:
            named["look_in"] = take(3)
        named["outs"] = take(len(arrays))
        if gains is not None:
            named["gain_out"] = take(1)[0]
        if look is not None:
            named["table_out"] = take(1)[0]
        for name in names:
            named[name] = take(count)
        named["sems"] = take(6)
        if spread:
            named["out_sem"] = take(1)[0]
        if gains is not None:
            named["gain_scratch"] = take(5)
        if look is not None:
            named["look_scratch"] = take(7)
        return named

    return pl.pallas_call(
        functools.partial(reduce_kernel, plan, only, extras, pace, refs_of),
        out_shape=outs,
        in_specs=in_specs,
        out_specs=out_specs,
        scratch_shapes=flat + sems + tail,
        compiler_params=pltpu.CompilerParams(
            collective_id=collective_id, has_side_effects=True, vmem_limit_bytes=60 << 20
        ),
    )(*inputs)

def nothing_like(run):
    return jax.tree.map(lambda a: jnp.zeros(a.shape, a.dtype), jax.eval_shape(run))


def only_on(live, run):
    return lax.cond(live, run, lambda: nothing_like(run))


X_FIRST = (0, 1, 2, 3)
Y_FIRST = (1, 0, 2, 3)
Z_THEN_X = (2, 0, 1, 3)
Z_THEN_Y = (2, 1, 0, 3)
ORDERS = (X_FIRST, Z_THEN_Y, Y_FIRST, Z_THEN_X)
LAYER_PLAN = (
    tuple((0, ORDERS[chunk], chunk, 4) for chunk in range(4))
    + tuple((1, ORDERS[chunk], chunk, 4) for chunk in range(4))
    + tuple((4, ORDERS[chunk], chunk, 4) for chunk in range(4))
    + ((3, Y_FIRST, 0, 2), (3, Z_THEN_X, 1, 2), (2, X_FIRST, 0, 1))
)
TABLE_PLAN = tuple((0, ((0, 1), (1, 0))[chunk % 2], chunk, 4) for chunk in range(4))
LAYER_PACE = (8, 4, 2)
TABLE_PACE = (4, 2, 1)


def after(value, *others):
    return lax.optimization_barrier((value,) + others)[0]


def per_device(
    tokens,
    lengths,
    levels,
    noise_rows,
    embed_table,
    w_in,
    ln_attn,
    w_qkv,
    w_proj,
    ln_mlp,
    w_up,
    w_down,
    ln_final,
    w_out,
):
    sec = lax.axis_index("section")
    pos = lax.axis_index("dp")
    first_section = sec == 0
    last_section = sec == 1
    rows = tokens.shape[0]
    seqs = lengths.shape[0]
    length = rows // seqs
    width = w_out.shape[0] * 4
    emb = w_out.shape[1]
    vocab_part = embed_table.shape[0]
    gains = jnp.concatenate(
        [ln_attn, ln_mlp, ln_final[None], jnp.zeros((13, ln_final.shape[0]), jnp.bfloat16)], 0
    )
    ids = jnp.concatenate(
        [
            tokens.reshape(-1, 128),
            jnp.concatenate([lengths, jnp.zeros((128 - seqs,), jnp.int32)])[None],
            jnp.zeros((7 - rows // 128, 128), jnp.int32),
        ],
        0,
    )
    shards = (w_qkv[0], w_proj[0], w_up[0], w_down[0], w_in, w_out, gains, ids)
    sizes = [s.shape[0] for s in shards]

    def cut(idx, count, whole=False):
        return tuple((idx, at * sizes[idx] // count, sizes[idx] // count, whole) for at in range(count))

    layer = cut(0, 2) + cut(2, 2) + cut(3, 2)
    wholes = gather_all(
        shards,
        cut(7, 1, True) + cut(6, 1, True) + cut(4, 1) + layer + cut(1, 4, True),
        cut(6, 1, True) + layer + cut(5, 1) + cut(1, 4, True),
        0,
    )
    qkv_weight, proj_weight, up_weight, down_weight, in_weight, out_weight, gain_all, line_ids = wholes
    gain_all = gain_all.reshape(4, 16, -1).astype(jnp.float32)
    gain_attn = gain_all[:, 0].reshape(-1)
    gain_mlp = gain_all[:, 1].reshape(-1)
    final_gain = gain_all[:, 2].reshape(-1)
    weights = (qkv_weight, proj_weight, up_weight, down_weight)
    gain_attn = gain_attn[None]
    gain_mlp = gain_mlp[None]
    final_gain = final_gain[None]
    loss_scale = LOSS_GAIN / math.sqrt(rows * lax.axis_size(("group", "dp")))

    def look_up():
        local = line_ids.reshape(4, 8, 128)[:, : rows // 128].reshape(-1) - pos * vocab_part
        hit = local[:, None] == lax.broadcasted_iota(jnp.int32, (1, vocab_part), 1)
        return product(hit.astype(jnp.bfloat16), embed_table).astype(jnp.bfloat16)

    looked_parts = only_on(first_section, look_up).reshape(4, rows, emb)
    looked_parts, all_ids = swap_rows(looked_parts, line_ids, 1)
    all_tokens = all_ids.reshape(16, 8, 128)[:, : rows // 128].reshape(-1)
    noise_level = jnp.exp(LOG_LOW + levels.astype(jnp.float32) * (LOG_SPAN / (LEVELS - 1)))
    scale_in = lax.rsqrt(EMB_VAR + noise_level * noise_level)
    row_level = jnp.repeat(noise_level, length)[:, None]
    row_scale = jnp.repeat(scale_in, length)[:, None]

    def front():
        looked = jnp.sum(looked_parts.astype(jnp.float32), 0)
        mixed_in = ((looked + row_level * noise_rows.astype(jnp.float32)) * row_scale).astype(
            jnp.bfloat16
        )
        return mixed_in, product(mixed_in, in_weight)

    mixed_in, x_first = only_on(first_section, front)
    *kept, out_first = run_forward(
        0, x_first, gain_attn, gain_mlp, lengths, final_gain, out_weight, weights, None
    )
    x_second = passed_along(out_first, "section", 1)
    *kept, final_in, projected = run_forward(
        1, x_second, gain_attn, gain_mlp, lengths, final_gain, out_weight, weights, kept
    )
    line_parts = line_ids.reshape(4, 8, 128)
    line_tokens = line_parts[:, : rows // 128].reshape(1, -1)
    line_counts = line_parts[:, rows // 128, :seqs].reshape(-1, 1)
    line_valid = jnp.arange(length, dtype=jnp.int32)[None, :] < line_counts
    line_scale = jnp.where(line_valid.reshape(1, -1), loss_scale, 0.0)
    grad_proj, entropy, table_g = run_vocabulary(projected, line_tokens, line_scale, embed_table, 2)
    (table_fin,) = reduce_all(
        (table_g,),
        TABLE_PLAN,
        0,
        3,
        TABLE_PACE,
        spread=False,
    )
    made = run_backward(
        1, grad_proj, gain_attn, gain_mlp, lengths, final_gain, out_weight, kept, weights, None
    )
    grad_first = passed_along(after(made[4], table_fin), "section", -1)
    made = run_backward(
        0, grad_first, gain_attn, gain_mlp, lengths, final_gain, out_weight, kept, weights, made
    )
    shape = in_weight.shape

    def front_edge():
        looked_grad = (product_nt(made[4], in_weight) * row_scale).astype(jnp.bfloat16)
        return product_tn(mixed_in, made[4]).astype(jnp.bfloat16), looked_grad

    def back_edge():
        edge = product_tn(final_in, grad_proj).astype(jnp.bfloat16)
        edge = edge.reshape(4, shape[0] // 4, shape[1]).reshape(shape)
        return edge, jnp.zeros((rows, emb), jnp.bfloat16)

    edge_g, looked_grad = lax.cond(first_section, front_edge, back_edge)
    gain_rows = made[5]
    gain_rows = gain_rows.reshape(8, 4, width // 4).transpose(1, 0, 2)

    def grads_of(rows_at_once, grads):
        return product(rows_at_once, grads).astype(jnp.bfloat16)

    order = (
        grads_of(kept[6], made[1]),
        grads_of(kept[8], made[0]),
        edge_g,
        grads_of(kept[4], made[2]),
        grads_of(kept[1], made[3]),
    )
    up_r, down_r, edge_r, proj_r, qkv_r, gain_r, table_r = reduce_all(
        order,
        LAYER_PLAN,
        None,
        4,
        LAYER_PACE,
        gains=gain_rows,
        look=(all_tokens.reshape(16, 1, rows), looked_grad, table_fin),
    )
    loss_low = after(entropy, gain_r)[0].astype(jnp.bfloat16)
    mine = (table_r, edge_r, gain_r, loss_low)
    theirs = lax.ppermute(mine, "section", [(0, 1), (1, 0)])

    def pair_of(at):
        low = jnp.where(first_section, mine[at], theirs[at])
        high = jnp.where(first_section, theirs[at], mine[at])
        return low, high

    up_r, down_r, proj_r, qkv_r = widen((up_r, down_r, proj_r, qkv_r))
    table_out = pair_of(0)[0].astype(jnp.float32)
    in_r, out_r = pair_of(1)
    final_r = pair_of(2)[1][2]
    token_loss = pair_of(3)[0]
    return (
        token_loss,
        table_out,
        in_r.astype(jnp.float32),
        gain_r[0][None],
        qkv_r[None],
        proj_r[None],
        gain_r[1][None],
        up_r[None],
        down_r[None],
        final_r,
        out_r.astype(jnp.float32).reshape(-1, emb),
    )


def solution(mesh):
    placed = (
        P(("group", "dp")),
        P(("group", "dp")),
        P(("group", "dp")),
        P(("group", "dp"), None),
        P("dp", None),
        P("dp", None),
        P("section", "dp"),
        P("section", "dp", None),
        P("section", "dp", None),
        P("section", "dp"),
        P("section", "dp", None),
        P("section", "dp", None),
        P("dp"),
        P("dp", None),
    )
    fits = (mesh.shape["section"], mesh.shape["group"], mesh.shape["dp"]) == (2, 4, 4)
    return jax.shard_map(
        per_device if fits else per_device_general,
        mesh=mesh,
        in_specs=placed,
        out_specs=(
            P(("group", "dp")),
            P("dp", None),
            P("dp", None),
            P("section", "dp"),
            P("section", "dp", None),
            P("section", "dp", None),
            P("section", "dp"),
            P("section", "dp", None),
            P("section", "dp", None),
            P("dp"),
            P("dp", None),
        ),
        check_vma=False,
    )
```

```python
import functools
import math

import jax
import jax.numpy as jnp
from jax import lax
from jax.experimental import pallas as pl
from jax.experimental.pallas import tpu as pltpu
from jax.sharding import PartitionSpec as P

HEAD = 64
LEVELS = 64
LEN = 128
MB = 2


EPS = 1e-05
LOG_LOW = -2.995732273553991
LOG_SPAN = 2.995732273553991
EMB_VAR = 0.015625
MASKED = -1e30
LOSS_GAIN = 16.0


def passed_along(x, axis, by):
    count = lax.axis_size(axis)
    pairs = [(i, i + by) for i in range(count) if 0 <= i + by < count]
    return lax.ppermute(x, axis, pairs)


def product(left_side, right_side):
    return jnp.dot(left_side, right_side, preferred_element_type=jnp.float32)


def product_tn(left_side, right_side):
    return lax.dot_general(
        left_side, right_side, (((0,), (0,)), ((), ())), preferred_element_type=jnp.float32
    )


def product_nt(left_side, right_side):
    return lax.dot_general(
        left_side, right_side, (((1,), (1,)), ((), ())), preferred_element_type=jnp.float32
    )


def normed(inputs, gain_vec):
    center = inputs - jnp.mean(inputs, -1, keepdims=True)
    return center * lax.rsqrt(jnp.mean(center * center, -1, keepdims=True) + EPS) * gain_vec


def norm_back(inputs, gain_vec, upstream):
    output, pullback = jax.vjp(normed, inputs, gain_vec)
    return pullback(upstream)


def gelu_exact(values_in):
    return jax.nn.gelu(values_in, approximate=False)


def attn_scores(split_rows, key_valid):
    scores = (
        jnp.einsum(
            "qhd,khd->hqk", split_rows[:, 0], split_rows[:, 1], preferred_element_type=jnp.float32
        )
        * 0.125
    )
    return jnp.where(key_valid[None, None, :], scores, MASKED)


def attend(qkv_rows, key_valid):
    length = qkv_rows.shape[0]
    model_width = qkv_rows.shape[1] // 3
    split_rows = qkv_rows.reshape(length, 3, model_width // HEAD, HEAD)
    scores = attn_scores(split_rows, key_valid)
    row_max = jnp.max(scores, -1, keepdims=True)
    log_total = row_max + jnp.log(jnp.sum(jnp.exp(scores - row_max), -1, keepdims=True))
    probs_low = jnp.exp(scores - log_total).astype(jnp.bfloat16)
    mixed_rows = jnp.einsum(
        "hqk,khd->qhd", probs_low, split_rows[:, 2], preferred_element_type=jnp.float32
    )
    return (mixed_rows.reshape(length, model_width).astype(jnp.bfloat16), log_total)


def attend_back(qkv_rows, key_valid, log_total, grad_mixed):
    length = qkv_rows.shape[0]
    model_width = qkv_rows.shape[1] // 3
    head_count = model_width // HEAD
    split_rows = qkv_rows.reshape(length, 3, head_count, HEAD)
    grad_heads = grad_mixed.reshape(length, head_count, HEAD)
    probs_full = jnp.exp(attn_scores(split_rows, key_valid) - log_total)
    grad_values = jnp.einsum(
        "hqk,qhd->khd",
        probs_full.astype(jnp.bfloat16),
        grad_heads,
        preferred_element_type=jnp.float32,
    )
    grad_probs = jnp.einsum(
        "qhd,khd->hqk", grad_heads, split_rows[:, 2], preferred_element_type=jnp.float32
    )
    grad_scores = (
        probs_full * (grad_probs - jnp.sum(grad_probs * probs_full, -1, keepdims=True))
    ).astype(jnp.bfloat16)
    grad_query = (
        jnp.einsum(
            "hqk,khd->qhd", grad_scores, split_rows[:, 1], preferred_element_type=jnp.float32
        )
        * 0.125
    )
    grad_key = (
        jnp.einsum(
            "hqk,qhd->khd", grad_scores, split_rows[:, 0], preferred_element_type=jnp.float32
        )
        * 0.125
    )
    stacked = jnp.stack([grad_query, grad_key, grad_values], 1).reshape(length, 3 * model_width)
    return stacked.astype(jnp.bfloat16)


def layer_forward(hidden, key_valid, weights):
    gain_attn, qkv_weight, proj_weight, gain_mlp, up_weight, down_weight = weights
    normed_in = normed(hidden, gain_attn).astype(jnp.bfloat16)
    qkv_rows = product(normed_in, qkv_weight).astype(jnp.bfloat16)
    mixed_rows, log_total = attend(qkv_rows, key_valid)
    hidden_mid = hidden + product(mixed_rows, proj_weight)
    mlp_in = normed(hidden_mid, gain_mlp).astype(jnp.bfloat16)
    pre_act = product(mlp_in, up_weight)
    activated = gelu_exact(pre_act).astype(jnp.bfloat16)
    hidden_out = hidden_mid + product(activated, down_weight)
    return (
        hidden_out,
        (
            hidden,
            normed_in,
            qkv_rows,
            log_total,
            mixed_rows,
            hidden_mid,
            mlp_in,
            pre_act,
            activated,
        ),
    )


def empty_kept(length, model_width, hidden_units, head_count):
    return (
        jnp.zeros((length, model_width), jnp.float32),
        jnp.zeros((length, model_width), jnp.bfloat16),
        jnp.zeros((length, 3 * model_width), jnp.bfloat16),
        jnp.zeros((head_count, length, 1), jnp.float32),
        jnp.zeros((length, model_width), jnp.bfloat16),
        jnp.zeros((length, model_width), jnp.float32),
        jnp.zeros((length, model_width), jnp.bfloat16),
        jnp.zeros((length, hidden_units), jnp.float32),
        jnp.zeros((length, hidden_units), jnp.bfloat16),
    )


def layer_backward(kept_vals, grad_out, key_valid, weights):
    hidden, normed_in, qkv_rows, log_total, mixed_rows, hidden_mid, mlp_in, pre_act, activated = (
        kept_vals
    )
    gain_attn, qkv_weight, proj_weight, gain_mlp, up_weight, down_weight = weights
    grad_low = grad_out.astype(jnp.bfloat16)
    grad_activated = product_nt(grad_low, down_weight)
    grad_pre = jax.vjp(gelu_exact, pre_act)[1](grad_activated)[0].astype(jnp.bfloat16)
    grad_mlp_in = product_nt(grad_pre, up_weight)
    grad_mid_norm, grad_gain_mlp = norm_back(hidden_mid, gain_mlp, grad_mlp_in)
    grad_mid = grad_out + grad_mid_norm
    grad_mid_low = grad_mid.astype(jnp.bfloat16)
    grad_mixed = product_nt(grad_mid_low, proj_weight).astype(jnp.bfloat16)
    grad_qkv = attend_back(qkv_rows, key_valid, log_total, grad_mixed)
    grad_normed = product_nt(grad_qkv, qkv_weight)
    grad_in_norm, grad_gain_attn = norm_back(hidden, gain_attn, grad_normed)
    records = (activated, grad_low, mlp_in, grad_pre, mixed_rows, grad_mid_low, normed_in, grad_qkv)
    return (grad_mid + grad_in_norm, (grad_gain_attn, grad_gain_mlp), records)


def layer_zero(length, model_width, hidden_units):
    records = (
        jnp.zeros((length, hidden_units), jnp.bfloat16),
        jnp.zeros((length, model_width), jnp.bfloat16),
        jnp.zeros((length, model_width), jnp.bfloat16),
        jnp.zeros((length, hidden_units), jnp.bfloat16),
        jnp.zeros((length, model_width), jnp.bfloat16),
        jnp.zeros((length, model_width), jnp.bfloat16),
        jnp.zeros((length, model_width), jnp.bfloat16),
        jnp.zeros((length, 3 * model_width), jnp.bfloat16),
    )
    gains = (jnp.zeros((model_width,), jnp.float32), jnp.zeros((model_width,), jnp.float32))
    return (jnp.zeros((length, model_width), jnp.float32), gains, records)


def layer_grads(records):
    activated, grad_low, mlp_in, grad_pre, mixed_rows, grad_mid_low, normed_in, grad_qkv = records
    return (
        product_tn(normed_in, grad_qkv),
        product_tn(mixed_rows, grad_mid_low),
        product_tn(mlp_in, grad_pre),
        product_tn(activated, grad_low),
    )


def embed_inputs(token_ids, noise_block, level_id, table_full):
    noise_level = jnp.exp(LOG_LOW + level_id.astype(jnp.float32) * (LOG_SPAN / (LEVELS - 1)))
    scale_in = lax.rsqrt(EMB_VAR + noise_level * noise_level)
    looked = jnp.take(table_full, token_ids, axis=0).astype(jnp.float32)
    mixed_in = ((looked + noise_level * noise_block.astype(jnp.float32)) * scale_in).astype(
        jnp.bfloat16
    )
    return (mixed_in, scale_in)


def embed_backward(token_ids, noise_block, level_id, grad_start, table_full, in_weight):
    mixed_in, scale_in = embed_inputs(token_ids, noise_block, level_id, table_full)
    grad_low = grad_start.astype(jnp.bfloat16)
    grad_looked = product_nt(grad_low, in_weight) * scale_in
    return (mixed_in, grad_low, grad_looked)


def embed_zero(length, model_width, emb_width):
    return (
        jnp.zeros((length, emb_width), jnp.bfloat16),
        jnp.zeros((length, model_width), jnp.bfloat16),
        jnp.zeros((length, emb_width), jnp.float32),
    )


def tail_pass(hidden, token_ids, key_valid, final_gain, out_weight, table_full, loss_scale):
    final_in = normed(hidden, final_gain).astype(jnp.bfloat16)
    projected = product(final_in, out_weight).astype(jnp.bfloat16)
    logits = product_nt(projected, table_full)
    row_max = jnp.max(logits, -1, keepdims=True)
    log_total = row_max + jnp.log(jnp.sum(jnp.exp(logits - row_max), -1, keepdims=True))
    vocab_ids = lax.broadcasted_iota(jnp.int32, logits.shape, 1)
    target_hit = vocab_ids == token_ids[:, None]
    picked = jnp.sum(jnp.where(target_hit, logits, 0.0), -1)
    entropy = jnp.where(key_valid, log_total[:, 0] - picked, 0.0)
    row_scale = jnp.where(key_valid, loss_scale, 0.0)[:, None]
    grad_logits = (
        (jnp.exp(logits - log_total) - target_hit.astype(jnp.float32)) * row_scale
    ).astype(jnp.bfloat16)
    grad_proj = product(grad_logits, table_full).astype(jnp.bfloat16)
    grad_final = product_nt(grad_proj, out_weight)
    grad_hidden, grad_gain = norm_back(hidden, final_gain, grad_final)
    return (grad_hidden, entropy, grad_gain, (grad_logits, projected, final_in, grad_proj))


def tail_zero(length, model_width, emb_width, vocab_rows):
    records = (
        jnp.zeros((length, vocab_rows), jnp.bfloat16),
        jnp.zeros((length, emb_width), jnp.bfloat16),
        jnp.zeros((length, model_width), jnp.bfloat16),
        jnp.zeros((length, emb_width), jnp.bfloat16),
    )
    return (
        jnp.zeros((length, model_width), jnp.float32),
        jnp.zeros((length,), jnp.float32),
        jnp.zeros((model_width,), jnp.float32),
        records,
    )


def edge_grads(tail_records, embed_records, token_ids):
    grad_logits, projected, final_in, grad_proj = tail_records
    mixed_in, grad_low, grad_looked = embed_records
    table_grad = product_tn(grad_logits, projected).at[token_ids].add(grad_looked)
    return (table_grad, product_tn(mixed_in, grad_low), product_tn(final_in, grad_proj))


def joined_rows(record_list):
    return jax.tree.map(lambda *pieces: jnp.concatenate(pieces, 0), *record_list)


def assemble(gain_attn_sum, gain_mlp_sum, layer_set, edge_set, gain_final_sum):
    return (
        gain_attn_sum[None],
        layer_set[0][None],
        layer_set[1][None],
        gain_mlp_sum[None],
        layer_set[2][None],
        layer_set[3][None],
        edge_set[0],
        edge_set[1],
        gain_final_sum,
        edge_set[2],
    )


def per_device_general(
    tokens,
    lengths,
    levels,
    noise_rows,
    embed_table,
    w_in,
    ln_attn,
    w_qkv,
    w_proj,
    ln_mlp,
    w_up,
    w_down,
    ln_final,
    w_out,
):
    gathered = (
        lax.all_gather(embed_table, "dp", axis=0, tiled=True),
        lax.all_gather(w_in, "dp", axis=0, tiled=True),
        lax.all_gather(ln_attn, "dp", axis=1, tiled=True),
        lax.all_gather(w_qkv, "dp", axis=1, tiled=True),
        lax.all_gather(w_proj, "dp", axis=1, tiled=True),
        lax.all_gather(ln_mlp, "dp", axis=1, tiled=True),
        lax.all_gather(w_up, "dp", axis=1, tiled=True),
        lax.all_gather(w_down, "dp", axis=1, tiled=True),
        lax.all_gather(ln_final, "dp", axis=0, tiled=True),
        lax.all_gather(w_out, "dp", axis=0, tiled=True),
    )
    table_full = gathered[0]
    in_weight = gathered[1]
    layer_weights = (
        gathered[2][0].astype(jnp.float32),
        gathered[3][0],
        gathered[4][0],
        gathered[5][0].astype(jnp.float32),
        gathered[6][0],
        gathered[7][0],
    )
    final_gain = gathered[8].astype(jnp.float32)
    out_weight = gathered[9]
    model_width = out_weight.shape[0]
    emb_width = out_weight.shape[1]
    vocab_rows = table_full.shape[0]
    hidden_units = layer_weights[4].shape[1]
    head_count = model_width // HEAD
    section_index = lax.axis_index("section")
    first_section = section_index == 0
    token_grid = tokens.reshape(MB, LEN)
    noise_grid = noise_rows.reshape(MB, LEN, noise_rows.shape[1])
    positions = jnp.arange(LEN, dtype=jnp.int32)
    valid_grid = positions[None, :] < lengths[:, None]
    loss_scale = LOSS_GAIN / math.sqrt(tokens.shape[0] * lax.axis_size(("group", "dp")))
    gain_attn_sum = jnp.zeros((model_width,), jnp.float32)
    gain_mlp_sum = jnp.zeros((model_width,), jnp.float32)
    gain_final_sum = jnp.zeros((model_width,), jnp.float32)
    recv_act = jnp.zeros((LEN, model_width), jnp.bfloat16)
    recv_grad = jnp.zeros((LEN, model_width), jnp.bfloat16)
    zero_rows = jnp.zeros((LEN, model_width), jnp.float32)
    kept_ticks = {}
    layer_recs = {}
    tail_recs = {}
    embed_recs = {}
    losses = []
    for moment in range(MB + 2):
        offset = moment - section_index
        fwd_valid = (offset >= 0) & (offset < MB)
        fwd_index = jnp.clip(offset, 0, MB - 1)
        ids_now = lax.dynamic_index_in_dim(token_grid, fwd_index, 0, False)
        noise_now = lax.dynamic_index_in_dim(noise_grid, fwd_index, 0, False)
        level_now = lax.dynamic_index_in_dim(levels, fwd_index, 0, False)
        valid_now = lax.dynamic_index_in_dim(valid_grid, fwd_index, 0, False)

        def first_input():
            mixed_in, scale_in = embed_inputs(ids_now, noise_now, level_now, table_full)
            return product(mixed_in, in_weight)

        layer_input = lax.cond(first_section, first_input, lambda: recv_act.astype(jnp.float32))
        hidden_out, kept_now = lax.cond(
            fwd_valid,
            lambda: layer_forward(layer_input, valid_now, layer_weights),
            lambda: (zero_rows, empty_kept(LEN, model_width, hidden_units, head_count)),
        )
        kept_ticks[moment] = kept_now
        tail_live = jnp.logical_not(first_section) & fwd_valid
        tail_grad, entropy, final_step, tail_now = lax.cond(
            tail_live,
            lambda: tail_pass(
                hidden_out, ids_now, valid_now, final_gain, out_weight, table_full, loss_scale
            ),
            lambda: tail_zero(LEN, model_width, emb_width, vocab_rows),
        )
        tail_recs[moment] = tail_now
        gain_final_sum = gain_final_sum + final_step
        back_tick = moment - 2
        late_live = 0 <= back_tick < MB
        late_index = min(max(back_tick, 0), MB - 1)
        kept_late = kept_ticks[back_tick] if back_tick >= 0 else kept_now
        kept_back = lax.cond(first_section, lambda: kept_late, lambda: kept_now)
        grad_top = jnp.where(first_section, recv_grad.astype(jnp.float32), tail_grad)
        valid_back = jnp.where(first_section, valid_grid[late_index], valid_now)
        back_live = jnp.where(first_section, late_live, fwd_valid)
        grad_start, gain_pair, layer_now = lax.cond(
            back_live,
            lambda: layer_backward(kept_back, grad_top, valid_back, layer_weights),
            lambda: layer_zero(LEN, model_width, hidden_units),
        )
        layer_recs[moment] = layer_now
        gain_attn_sum = gain_attn_sum + gain_pair[0]
        gain_mlp_sum = gain_mlp_sum + gain_pair[1]
        if late_live:
            embed_now = lax.cond(
                first_section,
                lambda: embed_backward(
                    token_grid[late_index],
                    noise_grid[late_index],
                    levels[late_index],
                    grad_start,
                    table_full,
                    in_weight,
                ),
                lambda: embed_zero(LEN, model_width, emb_width),
            )
        else:
            embed_now = embed_zero(LEN, model_width, emb_width)
        embed_recs[moment] = embed_now
        if moment < MB:
            recv_act = passed_along(hidden_out.astype(jnp.bfloat16), "section", 1)
        if 1 <= moment <= MB:
            entropy_low = entropy.astype(jnp.bfloat16)
            recv_grad, loss_back = passed_along(
                (grad_start.astype(jnp.bfloat16), entropy_low), "section", -1
            )
            losses.append(jnp.where(first_section, loss_back, entropy_low))
    chosen = [
        jax.tree.map(
            lambda early, late: jnp.where(first_section, early, late),
            layer_recs[micro + 2],
            layer_recs[micro + 1],
        )
        for micro in range(MB)
    ]
    all_layer = layer_grads(joined_rows(chosen))
    all_tail = joined_rows([tail_recs[micro + 1] for micro in range(MB)])
    all_embed = joined_rows([embed_recs[micro + 2] for micro in range(MB)])
    all_edge = edge_grads(all_tail, all_embed, tokens)
    grad_pack = assemble(gain_attn_sum, gain_mlp_sum, all_layer, all_edge, gain_final_sum)
    parted = (
        lax.psum_scatter(
            grad_pack[0].astype(jnp.bfloat16), "dp", scatter_dimension=1, tiled=True
        ).astype(jnp.float32),
        lax.psum_scatter(
            grad_pack[1].astype(jnp.bfloat16), "dp", scatter_dimension=1, tiled=True
        ).astype(jnp.float32),
        lax.psum_scatter(
            grad_pack[2].astype(jnp.bfloat16), "dp", scatter_dimension=1, tiled=True
        ).astype(jnp.float32),
        lax.psum_scatter(
            grad_pack[3].astype(jnp.bfloat16), "dp", scatter_dimension=1, tiled=True
        ).astype(jnp.float32),
        lax.psum_scatter(
            grad_pack[4].astype(jnp.bfloat16), "dp", scatter_dimension=1, tiled=True
        ).astype(jnp.float32),
        lax.psum_scatter(
            grad_pack[5].astype(jnp.bfloat16), "dp", scatter_dimension=1, tiled=True
        ).astype(jnp.float32),
        lax.psum_scatter(
            grad_pack[6].astype(jnp.bfloat16), "dp", scatter_dimension=0, tiled=True
        ).astype(jnp.float32),
        lax.psum_scatter(
            grad_pack[7].astype(jnp.bfloat16), "dp", scatter_dimension=0, tiled=True
        ).astype(jnp.float32),
        lax.psum_scatter(
            grad_pack[8].astype(jnp.bfloat16), "dp", scatter_dimension=0, tiled=True
        ).astype(jnp.float32),
        lax.psum_scatter(
            grad_pack[9].astype(jnp.bfloat16), "dp", scatter_dimension=0, tiled=True
        ).astype(jnp.float32),
    )
    layer_total = (
        lax.psum(parted[0].astype(jnp.bfloat16), "group").astype(jnp.float32),
        lax.psum(parted[1].astype(jnp.bfloat16), "group").astype(jnp.float32),
        lax.psum(parted[2].astype(jnp.bfloat16), "group").astype(jnp.float32),
        lax.psum(parted[3].astype(jnp.bfloat16), "group").astype(jnp.float32),
        lax.psum(parted[4].astype(jnp.bfloat16), "group").astype(jnp.float32),
        lax.psum(parted[5].astype(jnp.bfloat16), "group").astype(jnp.float32),
    )
    edge_total = (
        lax.psum(parted[6].astype(jnp.bfloat16), ("section", "group")).astype(jnp.float32),
        lax.psum(parted[7].astype(jnp.bfloat16), ("section", "group")).astype(jnp.float32),
        lax.psum(parted[8].astype(jnp.bfloat16), ("section", "group")).astype(jnp.float32),
        lax.psum(parted[9].astype(jnp.bfloat16), ("section", "group")).astype(jnp.float32),
    )
    token_loss = jnp.concatenate(losses)
    return (
        token_loss,
        edge_total[0],
        edge_total[1],
        layer_total[0],
        layer_total[1],
        layer_total[2],
        layer_total[3],
        layer_total[4],
        layer_total[5],
        edge_total[2],
        edge_total[3],
    )


MESH = pl.DeviceIdType.MESH
ANYWHERE = pl.BlockSpec(memory_space=pl.ANY)


def pick(index, values):
    out = values[-1]
    for at in range(len(values) - 2, -1, -1):
        out = jnp.where(index == at, values[at], out)
    return out


def rows_at(start, size):
    return pl.ds(pl.multiple_of(start, 8), size)


def remote(src, dst, send_sem, recv_sem, device):
    return pltpu.make_async_remote_copy(
        src_ref=src,
        dst_ref=dst,
        send_sem=send_sem,
        recv_sem=recv_sem,
        device_id=device,
        device_id_type=MESH,
    )


def gather_kernel(count, first_order, last_order, *refs):
    shards = refs[:count]
    wholes = refs[count : 2 * count]
    own_sem, zsend, zrecv, psend, precv, gate = refs[2 * count : 2 * count + 6]
    stage = refs[2 * count + 6 :]
    sec = lax.axis_index("section")
    grp = lax.axis_index("group")
    pos = lax.axis_index("dp")
    beside = ((sec, grp ^ 1, pos), (sec, grp ^ 2, pos))
    above = (sec, grp, pos + 1)
    below = (sec, grp, pos - 1)
    partner = (1 - sec, grp, pos)
    barrier = pltpu.get_barrier_semaphore()
    both = bool(last_order)

    def greet(device):
        pl.semaphore_signal(barrier, inc=1, device_id=device, device_id_type=MESH)

    def meet():
        for device in beside + ((partner,) if both else ()):
            greet(device)

        @pl.when(pos > 0)
        def _():
            greet(below)

        @pl.when(pos < 3)
        def _():
            greet(above)

        at_end = (pos == 0) | (pos == 3)
        pl.semaphore_wait(barrier, jnp.where(at_end, 3, 4) + (1 if both else 0))

    turn = [pick(pos, v) for v in ((3, 1, 3, 1), (2, 3, 1, 2), (1, 2, 2, 3))]

    def run(order, before, middle):
        def rows_of(slot):
            return shards[order[slot][0]].shape[0]

        def part_of(slot):
            _, _, size, whole_line = order[slot]
            return size if whole_line else size // 4

        def shift(slot, who):
            _, lo, _, whole_line = order[slot]
            return lo if whole_line else lo + who * part_of(slot)

        def block(slot, origin, who):
            return rows_at(origin * rows_of(slot) + shift(slot, who), part_of(slot))

        staged = sorted({entry[0] for entry in order})

        def load_own(idx):
            return pltpu.make_async_copy(shards[idx], stage[idx], own_sem.at[idx])

        def store_own(idx):
            rows = shards[idx].shape[0]
            return pltpu.make_async_copy(
                stage[idx], wholes[idx].at[rows_at(pos * rows, rows)], own_sem.at[idx]
            )

        def own_ends(slot):
            idx = order[slot][0]
            src = shards[idx].at[rows_at(shift(slot, grp), part_of(slot))]
            dst = wholes[idx].at[block(slot, pos, grp)]
            return (
                (pos < 3, remote(src, dst, zsend.at[slot, 0], zrecv.at[slot, 1], above)),
                (pos > 0, remote(src, dst, zsend.at[slot, 1], zrecv.at[slot, 3], below)),
            )

        def start_own(slot):
            for goes, copy in own_ends(slot):
                pl.when(goes)(copy.start)

        def origin_of(j):
            return lax.rem(pos - turn[j] + 4, 4)

        def arrived(slot, j):
            here = wholes[order[slot][0]].at[block(slot, origin_of(j), grp)]
            return remote(here, here, zsend.at[slot, 2 + j], zrecv.at[slot, turn[j]], partner)

        def onward(slot, j):
            step = jnp.where(turn[j] <= pos, 1, -1)
            to = pos + step
            here = wholes[order[slot][0]].at[block(slot, origin_of(j), grp)]
            landed = jnp.clip(turn[j] + step, 0, 3)
            copy = remote(
                here,
                here,
                zsend.at[slot, 2 + j],
                zrecv.at[slot, landed],
                (sec, grp, jnp.clip(to, 0, 3)),
            )
            return (to >= 0) & (to <= 3), copy

        def plane(slot, j, way):
            idx = order[slot][0]
            origin = origin_of(j)
            if way < 2:
                here = wholes[idx].at[block(slot, origin, grp)]
                return remote(here, here, psend.at[slot, j, way], precv.at[slot, j, way], beside[way])
            half = shards[idx].shape[1] // 2
            there = wholes[idx].at[
                block(slot, origin, grp ^ (way - 1)), pl.ds(half * (way - 2), half)
            ]
            return remote(
                there, there, psend.at[slot, j, way], precv.at[slot, j, way], beside[3 - way]
            )

        items = [(slot, j) for j in range(3) for slot in range(len(order))]
        crossing = [item for item in items if not order[item[0]][3]]

        def first(slot, j):
            arrived(slot, j).wait_recv()
            goes, copy = onward(slot, j)
            pl.when(goes)(copy.start)
            if (slot, j) in crossing:
                plane(slot, j, 0).start()
                plane(slot, j, 1).start()

        def second(slot, j):
            if (slot, j) in crossing:
                for way in (0, 1):
                    plane(slot, j, way).wait_recv()
                    plane(slot, j, way + 2).start()

        if before is not None:
            before()
        for slot in range(len(order)):
            start_own(slot)
        for idx in staged:
            load_own(idx).start()
        lag = 4
        for at in range(len(items) + lag):
            if at < len(items):
                slot, j = items[at]
                if j == 1 and slot < len(staged):
                    load_own(staged[slot]).wait()
                    store_own(staged[slot]).start()
                first(slot, j)
            if at == len(items) - 1 and middle is not None:
                middle()
            if at >= lag:
                second(*items[at - lag])
        for slot, j in crossing:
            plane(slot, j, 2).wait_recv()
            plane(slot, j, 3).wait_recv()
        for idx in staged:
            store_own(idx).wait()
        for slot in range(len(order)):
            for goes, copy in own_ends(slot):
                pl.when(goes)(copy.wait_send)
        for slot, j in items:
            goes, copy = onward(slot, j)
            pl.when(goes)(copy.wait_send)
        for slot, j in crossing:
            for way in range(4):
                plane(slot, j, way).wait_send()

    def let_go():
        pl.semaphore_signal(gate, inc=1, device_id=partner, device_id_type=MESH)

    def hold():
        pl.semaphore_wait(gate, 1)

    if both:
        meet()

        @pl.when(sec == 0)
        def _():
            run(first_order, None, let_go)

        @pl.when(sec == 1)
        def _():
            run(last_order, hold, None)

    else:

        @pl.when(sec == 0)
        def _():
            meet()
            run(first_order, None, None)


def gather_all(shards, first_order, last_order, collective_id):
    count = len(shards)
    slots = max(len(first_order), len(last_order))
    return pl.pallas_call(
        functools.partial(gather_kernel, count, first_order, last_order),
        out_shape=[jax.ShapeDtypeStruct((s.shape[0] * 4, s.shape[1]), s.dtype) for s in shards],
        in_specs=[ANYWHERE] * count,
        out_specs=[ANYWHERE] * count,
        scratch_shapes=[
            pltpu.SemaphoreType.DMA((count,)),
            pltpu.SemaphoreType.DMA((slots, 5)),
            pltpu.SemaphoreType.DMA((slots, 4)),
            pltpu.SemaphoreType.DMA((slots, 3, 4)),
            pltpu.SemaphoreType.DMA((slots, 3, 4)),
            pltpu.SemaphoreType.REGULAR,
        ]
        + [pltpu.VMEM(s.shape, s.dtype) for s in shards],
        compiler_params=pltpu.CompilerParams(
            collective_id=collective_id, has_side_effects=True, vmem_limit_bytes=60 << 20
        ),
    )(*shards)


def swap_kernel(rows_ref, ids_ref, out_ref, ids_out, own_sem, send_sem, recv_sem):
    sec = lax.axis_index("section")
    grp = lax.axis_index("group")
    pos = lax.axis_index("dp")

    @pl.when(sec == 0)
    def _():
        barrier = pltpu.get_barrier_semaphore()
        peers = [(sec, grp, lax.rem(pos + k, 4)) for k in (1, 2, 3)]
        sides = [(sec, grp ^ j, pos) for j in (1, 2, 3)]
        for device in peers + sides:
            pl.semaphore_signal(barrier, inc=1, device_id=device, device_id_type=MESH)
        pl.semaphore_wait(barrier, 6)
        copies = []
        for k, device in enumerate(peers):
            copies.append(
                remote(rows_ref.at[device[2]], out_ref.at[pos], send_sem.at[k], recv_sem.at[k], device)
            )
        for k, device in enumerate(sides):
            copies.append(
                remote(ids_ref, ids_out.at[grp], send_sem.at[3 + k], recv_sem.at[3 + k], device)
            )
        for copy in copies:
            copy.start()
        own_rows = pltpu.make_async_copy(rows_ref.at[pos], out_ref.at[pos], own_sem.at[0])
        own_ids = pltpu.make_async_copy(ids_ref, ids_out.at[grp], own_sem.at[1])
        own_rows.start()
        own_ids.start()
        own_rows.wait()
        own_ids.wait()
        for copy in copies:
            copy.wait()


def swap_rows(rows, ids, collective_id):
    in_vmem = pl.BlockSpec(memory_space=pltpu.VMEM)
    return pl.pallas_call(
        swap_kernel,
        out_shape=[
            jax.ShapeDtypeStruct(rows.shape, rows.dtype),
            jax.ShapeDtypeStruct((4,) + ids.shape, ids.dtype),
        ],
        in_specs=[in_vmem] * 2,
        out_specs=[in_vmem] * 2,
        scratch_shapes=[
            pltpu.SemaphoreType.DMA((2,)),
            pltpu.SemaphoreType.DMA((6,)),
            pltpu.SemaphoreType.DMA((6,)),
        ],
        compiler_params=pltpu.CompilerParams(collective_id=collective_id, has_side_effects=True),
    )(rows, ids)


IN_VMEM = pl.BlockSpec(memory_space=pltpu.VMEM)
IN_SMEM = pl.BlockSpec(memory_space=pltpu.SMEM)
ROOT_HALF = 0.7071067811865476
ROOT_TWO_PI = 0.3989422804014327


def dot_nn(left, right):
    return lax.dot_general(
        left, right, (((1,), (0,)), ((), ())), preferred_element_type=jnp.float32
    )


def dot_nt(left, right):
    return lax.dot_general(
        left, right, (((1,), (1,)), ((), ())), preferred_element_type=jnp.float32
    )


def dot_tn(left, right):
    return lax.dot_general(
        left, right, (((0,), (0,)), ((), ())), preferred_element_type=jnp.float32
    )


def unit_rows(v):
    center = v - jnp.mean(v, -1, keepdims=True)
    scale = lax.rsqrt(jnp.mean(center * center, -1, keepdims=True) + EPS)
    return center * scale, scale


def split_heads(pair):
    low = lax.broadcasted_iota(jnp.int32, pair.shape, 1) < HEAD
    nothing = jnp.zeros_like(pair)
    return jnp.concatenate([jnp.where(low, pair, nothing), jnp.where(low, nothing, pair)], 0)


def join_heads(stacked):
    half = stacked.shape[0] // 2
    low = lax.broadcasted_iota(jnp.int32, (half, stacked.shape[1]), 1) < HEAD
    return jnp.where(low, stacked[:half], stacked[half:])


def pair_scores(keys, stacked_queries, key_count):
    scores = dot_nt(keys, stacked_queries) * 0.125
    valid = lax.broadcasted_iota(jnp.int32, scores.shape, 0) < key_count
    return jnp.where(valid, scores, MASKED)


STRIP = 64


def forward_kernel(only, tile, given, *refs):
    x, gain_attn, gain_mlp, counts, gain_final, wo, wq, wp, wu, wd = refs[:10]
    rest = refs[10 + given :]
    outs = rest[:KEPT_COUNT]
    last = rest[KEPT_COUNT : KEPT_COUNT + 1 + only]
    rest = rest[1 + only :]
    qv, pv, uv, dv = rest[KEPT_COUNT : KEPT_COUNT + 4]
    kept = rest[KEPT_COUNT + 4 : 2 * KEPT_COUNT + 4]
    a, att, m, acc, wsem, osem = rest[2 * KEPT_COUNT + 4 :]
    xv, at_t, qkv, lse, att_t, mid, m_t, pre, act_t, out = kept
    rows, width = a.shape
    units = dv.shape[0]

    def store(idx):
        return pltpu.make_async_copy(kept[idx], outs[idx], osem.at[idx])

    def run():
        loads = []

        def load(src, dst):
            copy = pltpu.make_async_copy(src, dst, wsem.at[len(loads)])
            copy.start()
            loads.append(copy)

        for lo in range(0, 3 * width, tile):
            load(wq.at[:, pl.ds(lo, tile)], qv.at[:, pl.ds(lo, tile)])
        load(wp, pv)
        for lo in range(0, units, tile):
            load(wu.at[:, pl.ds(lo, tile)], uv.at[:, pl.ds(lo, tile)])
            load(wd.at[pl.ds(lo, tile)], dv.at[pl.ds(lo, tile)])
        loads = iter(loads)
        for lo in range(0, rows, STRIP):
            here = pl.ds(lo, STRIP)
            xv[here, :] = x[here, :].astype(jnp.float32)
            a[here, :] = (unit_rows(xv[here, :])[0] * gain_attn[...]).astype(jnp.bfloat16)
        store(0).start()
        for lo in range(0, 3 * width, tile):
            next(loads).wait()
            cols = pl.ds(lo, tile)
            qkv[:, cols] = dot_nn(a[...], qv[:, cols]).astype(jnp.bfloat16)
        store(2).start()
        for lo in range(0, width, 256):
            at_t[pl.ds(lo, 256), :] = a[:, pl.ds(lo, 256)].T
        store(1).start()
        pairs = width // 128
        for seq in range(rows // LEN):
            here = pl.ds(seq * LEN, LEN)
            for pair in range(pairs):
                stacked = split_heads(qkv[here, pl.ds(pair * 128, 128)])
                scores = pair_scores(qkv[here, pl.ds(width + pair * 128, 128)], stacked, counts[seq])
                top = jnp.max(scores, 0, keepdims=True)
                power = jnp.exp(scores - top)
                total = jnp.sum(power, 0, keepdims=True)
                lse[seq * pairs + pair] = top + jnp.log(total)
                probs = (power * (1.0 / total)).astype(jnp.bfloat16)
                mixed = dot_tn(probs, qkv[here, pl.ds(2 * width + pair * 128, 128)])
                att[here, pl.ds(pair * 128, 128)] = join_heads(mixed).astype(jnp.bfloat16)
        store(3).start()
        for lo in range(0, width, 256):
            att_t[pl.ds(lo, 256), :] = att[:, pl.ds(lo, 256)].T
        store(4).start()
        next(loads).wait()
        for lo in range(0, width, tile):
            cols = pl.ds(lo, tile)
            mid[:, cols] = xv[:, cols] + dot_nn(att[...], pv[:, cols])
        for lo in range(0, rows, STRIP):
            here = pl.ds(lo, STRIP)
            m[here, :] = (unit_rows(mid[here, :])[0] * gain_mlp[...]).astype(jnp.bfloat16)
        store(5).start()
        acc[...] = mid[...]
        for lo in range(0, units, tile):
            cols = pl.ds(lo, tile)
            next(loads).wait()
            before = dot_nn(m[...], uv[:, cols])
            pre[:, cols] = before
            active = (0.5 * before * (1.0 + lax.erf(before * ROOT_HALF))).astype(jnp.bfloat16)
            act_t[cols, :] = active.T
            next(loads).wait()
            acc[...] += dot_nn(active, dv[cols, :])
        store(7).start()
        store(8).start()
        for lo in range(0, width, 256):
            m_t[pl.ds(lo, 256), :] = m[:, pl.ds(lo, 256)].T
        store(6).start()
        out[...] = acc[...]
        store(9).start()
        if only == 0:
            last[0][...] = acc[...].astype(jnp.bfloat16)
        else:
            for lo in range(0, rows, STRIP):
                here = pl.ds(lo, STRIP)
                last[0][here, :] = (unit_rows(acc[here, :])[0] * gain_final[...]).astype(jnp.bfloat16)
            last[1][...] = dot_nn(last[0][...], wo[...]).astype(jnp.bfloat16)
        for idx in range(KEPT_COUNT):
            store(idx).wait()

    pl.when(lax.axis_index("section") == only)(run)


KEPT_COUNT = 10


def kept_shapes(rows, width, units):
    f32, low = jnp.float32, jnp.bfloat16
    return [
        jax.ShapeDtypeStruct(shape, kind)
        for shape, kind in (
            ((rows, width), f32),
            ((width, rows), low),
            ((rows, 3 * width), low),
            ((rows // LEN * width // 128, 1, 2 * LEN), f32),
            ((width, rows), low),
            ((rows, width), f32),
            ((width, rows), low),
            ((rows, units), f32),
            ((units, rows), low),
            ((rows, width), f32),
        )
    ]


def run_forward(only, x, gain_attn, gain_mlp, counts, gain_final, out_weight, weights, kept):
    wq, wp, wu, wd = weights
    rows, width = x.shape
    units = wd.shape[0]
    tile = 512
    shapes = kept_shapes(rows, width, units)
    low = jnp.bfloat16
    given = 0 if kept is None else KEPT_COUNT
    in_specs = [IN_VMEM] * 3 + [IN_SMEM] + [IN_VMEM] * 2 + [ANYWHERE] * (4 + given)
    extra = [jax.ShapeDtypeStruct((rows, width), low)]
    if only == 1:
        extra.append(jax.ShapeDtypeStruct((rows, out_weight.shape[1]), low))
    return pl.pallas_call(
        functools.partial(forward_kernel, only, tile, given),
        out_shape=shapes + extra,
        in_specs=in_specs,
        out_specs=[ANYWHERE] * KEPT_COUNT + [IN_VMEM] * len(extra),
        input_output_aliases={10 + idx: idx for idx in range(given)},
        scratch_shapes=[pltpu.VMEM(w.shape, w.dtype) for w in weights]
        + [pltpu.VMEM(s.shape, s.dtype) for s in shapes]
        + [
            pltpu.VMEM((rows, width), low),
            pltpu.VMEM((rows, width), low),
            pltpu.VMEM((rows, width), low),
            pltpu.VMEM((rows, width), jnp.float32),
            pltpu.SemaphoreType.DMA((3 * width // tile + 1 + 2 * units // tile,)),
            pltpu.SemaphoreType.DMA((KEPT_COUNT,)),
        ],
        compiler_params=pltpu.CompilerParams(vmem_limit_bytes=56 << 20),
    )(x, gain_attn, gain_mlp, counts, gain_final, out_weight, wq, wp, wu, wd, *(kept or ()))


GRAD_COUNT = 6


def grad_shapes(rows, width, units):
    f32, low = jnp.float32, jnp.bfloat16
    return [
        jax.ShapeDtypeStruct(shape, kind)
        for shape, kind in (
            ((rows, width), low),
            ((rows, units), low),
            ((rows, width), low),
            ((rows, 3 * width), low),
            ((rows, width), low),
            ((8, width), f32),
        )
    ]


def norm_pull(v, gain, upstream):
    unit, scale = unit_rows(v)
    pulled = upstream * gain
    inner = jnp.mean(pulled * unit, -1, keepdims=True)
    grad = (pulled - jnp.mean(pulled, -1, keepdims=True) - unit * inner) * scale
    return grad, jnp.sum(upstream * unit, 0, keepdims=True)


def backward_kernel(only, tile, given, *refs):
    grad_in, gain_attn, gain_mlp, counts, gain_final, wo, out_in = refs[:7]
    x_in, qkv_in, lse_in, mid_in, pre_in, wq, wp, wu, wd = refs[7:16]
    rest = refs[16 + given :]
    outs = rest[:GRAD_COUNT]
    qv, pv, uv, dv = rest[GRAD_COUNT : GRAD_COUNT + 4]
    made = rest[GRAD_COUNT + 4 : 2 * GRAD_COUNT + 4]
    x, qkv, lse, mid, pre, gm, gmid, gatt, gtop, wsem, ksem, osem = rest[2 * GRAD_COUNT + 4 :]
    grad = gtop if only == 1 else grad_in
    gy, gpre, gz, gqkv, gx, gains = made
    rows, width = gm.shape
    units = dv.shape[0]

    def store(idx):
        return pltpu.make_async_copy(made[idx], outs[idx], osem.at[idx])

    def run():
        loads = []

        def load(src, dst):
            copy = pltpu.make_async_copy(src, dst, wsem.at[len(loads)])
            copy.start()
            loads.append(copy)

        kept = [
            pltpu.make_async_copy(src, dst, ksem.at[idx])
            for idx, (src, dst) in enumerate(
                ((pre_in, pre), (mid_in, mid), (qkv_in, qkv), (lse_in, lse), (x_in, x))
            )
        ]
        if only == 1:
            kept.append(pltpu.make_async_copy(out_in, gtop, ksem.at[5]))
            kept[5].start()
        kept[0].start()
        for lo in range(0, units, tile):
            load(wd.at[pl.ds(lo, tile)], dv.at[pl.ds(lo, tile)])
            load(wu.at[:, pl.ds(lo, tile)], uv.at[:, pl.ds(lo, tile)])
        for copy in kept[1:5]:
            copy.start()
        load(wp, pv)
        load(wq, qv)
        loads = iter(loads)
        gains[...] = jnp.zeros_like(gains)
        if only == 1:
            for copy in kept[5:]:
                copy.wait()
            gmid[...] = dot_nt(grad_in[...], wo[...])
            for lo in range(0, rows, STRIP):
                here = pl.ds(lo, STRIP)
                step, gain = norm_pull(gtop[here, :], gain_final[...], gmid[here, :])
                gtop[here, :] = step
                gains[2:3, :] += gain
        gy[...] = grad[...].astype(jnp.bfloat16)
        store(0).start()
        kept[0].wait()
        gm[...] = jnp.zeros_like(gm)
        for lo in range(0, units, tile):
            cols = pl.ds(lo, tile)
            next(loads).wait()
            pulled = dot_nt(gy[...], dv[cols, :])
            before = pre[:, cols]
            slope = 0.5 * (1.0 + lax.erf(before * ROOT_HALF)) + before * (
                ROOT_TWO_PI * jnp.exp(-0.5 * before * before)
            )
            low = (pulled * slope).astype(jnp.bfloat16)
            gpre[:, cols] = low
            next(loads).wait()
            gm[...] += dot_nt(low, uv[:, cols])
        store(1).start()
        kept[1].wait()
        for lo in range(0, rows, STRIP):
            here = pl.ds(lo, STRIP)
            step, gain = norm_pull(mid[here, :], gain_mlp[...], gm[here, :])
            total = grad[here, :].astype(jnp.float32) + step
            gmid[here, :] = total
            gz[here, :] = total.astype(jnp.bfloat16)
            gains[1:2, :] += gain
        store(2).start()
        next(loads).wait()
        gatt[...] = dot_nt(gz[...], pv[...]).astype(jnp.bfloat16)
        kept[2].wait()
        kept[3].wait()
        pairs = width // 128
        for seq in range(rows // LEN):
            here = pl.ds(seq * LEN, LEN)
            for pair in range(pairs):
                own = pl.ds(pair * 128, 128)
                stacked = split_heads(qkv[here, own])
                pulled = split_heads(gatt[here, own])
                keys = qkv[here, pl.ds(width + pair * 128, 128)]
                values = qkv[here, pl.ds(2 * width + pair * 128, 128)]
                probs = jnp.exp(pair_scores(keys, stacked, counts[seq]) - lse[seq * pairs + pair])
                gprobs = dot_nt(values, pulled)
                inner = jnp.sum(probs * gprobs, 0, keepdims=True)
                gscores = (probs * (gprobs - inner)).astype(jnp.bfloat16)
                gqkv[here, own] = (join_heads(dot_tn(gscores, keys)) * 0.125).astype(jnp.bfloat16)
                gqkv[here, pl.ds(width + pair * 128, 128)] = (dot_nn(gscores, stacked) * 0.125).astype(
                    jnp.bfloat16
                )
                gqkv[here, pl.ds(2 * width + pair * 128, 128)] = dot_nn(
                    probs.astype(jnp.bfloat16), pulled
                ).astype(jnp.bfloat16)
        store(3).start()
        next(loads).wait()
        for lo in range(0, width, 256):
            gm[:, pl.ds(lo, 256)] = dot_nt(gqkv[...], qv[pl.ds(lo, 256), :])
        kept[4].wait()
        for lo in range(0, rows, STRIP):
            here = pl.ds(lo, STRIP)
            step, gain = norm_pull(x[here, :], gain_attn[...], gm[here, :])
            gx[here, :] = (gmid[here, :] + step).astype(jnp.bfloat16)
            gains[0:1, :] += gain
        store(4).start()
        store(5).start()
        for idx in range(GRAD_COUNT):
            store(idx).wait()

    pl.when(lax.axis_index("section") == only)(run)


def run_backward(only, grad, gain_attn, gain_mlp, counts, gain_final, out_weight, kept, weights, made):
    wq, wp, wu, wd = weights
    x, _, qkv, lse, _, mid, _, pre, _, out = kept
    rows, width = x.shape
    units = wd.shape[0]
    tile = 512
    shapes = grad_shapes(rows, width, units)
    low, f32 = jnp.bfloat16, jnp.float32
    given = 0 if made is None else GRAD_COUNT
    in_specs = [IN_VMEM] * 3 + [IN_SMEM] + [IN_VMEM] * 2 + [ANYWHERE] * (10 + given)
    return pl.pallas_call(
        functools.partial(backward_kernel, only, tile, given),
        out_shape=shapes,
        in_specs=in_specs,
        out_specs=[ANYWHERE] * GRAD_COUNT,
        input_output_aliases={16 + idx: idx for idx in range(given)},
        scratch_shapes=[pltpu.VMEM(w.shape, w.dtype) for w in weights]
        + [pltpu.VMEM(s.shape, s.dtype) for s in shapes]
        + [pltpu.VMEM(s.shape, s.dtype) for s in (x, qkv, lse, mid, pre)]
        + [
            pltpu.VMEM((rows, width), f32),
            pltpu.VMEM((rows, width), f32),
            pltpu.VMEM((rows, width), low),
            pltpu.VMEM((rows, width), f32),
            pltpu.SemaphoreType.DMA((2 + 2 * units // tile,)),
            pltpu.SemaphoreType.DMA((6,)),
            pltpu.SemaphoreType.DMA((GRAD_COUNT,)),
        ],
        compiler_params=pltpu.CompilerParams(vmem_limit_bytes=56 << 20),
    )(
        grad, gain_attn, gain_mlp, counts, gain_final, out_weight, out, x, qkv, lse, mid, pre, wq, wp, wu, wd, *(made or ())
    )


def vocabulary_kernel(tile, proj, ids, scale, table, gproj_out, loss_out, gtable, *scratch):
    tv, gt, pall, gp, gsend, gin, stat, stats, whole, tsem, gsem, psem, prem, ssem, srem, qsem, qrem = scratch
    rows = proj.shape[0]
    vocab = tv.shape[0]
    count = vocab // tile
    sec = lax.axis_index("section")
    grp = lax.axis_index("group")
    pos = lax.axis_index("dp")
    places = [lax.rem(pos + k, 4) for k in range(4)]
    peers = [(sec, grp, place) for place in places[1:]]
    across = [(1 - sec, grp, place) for place in places]
    barrier = pltpu.get_barrier_semaphore()

    def hand(k):
        return remote(proj, pall.at[pos], psem.at[k], prem.at[k], across[k])

    def back(k):
        return remote(gsend.at[places[k]], gin.at[k], qsem.at[k], qrem.at[k], across[k])

    def greet(devices):
        for device in devices:
            pl.semaphore_signal(barrier, inc=1, device_id=device, device_id_type=MESH)

    def give():
        greet(across)
        pl.semaphore_wait(barrier, 4)
        for k in (2, 1, 3, 0):
            hand(k).start()
        for k in range(4):
            back(k).wait_recv()
        summed = gin[0].astype(jnp.float32)
        for k in (1, 2, 3):
            summed = summed + gin[k].astype(jnp.float32)
        gproj_out[...] = summed.astype(jnp.bfloat16)
        for k in range(4):
            hand(k).wait_send()

    def score():
        load = pltpu.make_async_copy(table, tv, tsem)
        load.start()
        greet(across + peers)
        pl.semaphore_wait(barrier, 7)
        load.wait()
        for k in range(4):
            hand(k).wait_recv()
        line_rows = pall[...].reshape(4 * rows, pall.shape[2])

        def logits_of(at):
            return dot_nt(tv[rows_at(at * tile, tile), :], line_rows)

        def hits_of(at):
            names = lax.broadcasted_iota(jnp.int32, (tile, 4 * rows), 0) + (at * tile + pos * vocab)
            return names == ids[...]

        stat[0:1, :] = jnp.full((1, 4 * rows), MASKED, jnp.float32)
        stat[1:8, :] = jnp.zeros((7, 4 * rows), jnp.float32)

        def measure(at, carry):
            logits = logits_of(at)
            top = stat[0:1, :]
            higher = jnp.maximum(top, jnp.max(logits, 0, keepdims=True))
            stat[1:2, :] = stat[1:2, :] * jnp.exp(top - higher) + jnp.sum(
                jnp.exp(logits - higher), 0, keepdims=True
            )
            stat[2:3, :] += jnp.sum(jnp.where(hits_of(at), logits, 0.0), 0, keepdims=True)
            stat[0:1, :] = higher
            return carry

        lax.fori_loop(0, count, measure, 0)
        second = [
            remote(stat, stats.at[pos], ssem.at[k], srem.at[k], peers[k]) for k in range(3)
        ]
        for copy in second:
            copy.start()
        stats[pos] = stat[...]
        gp[...] = jnp.zeros_like(gp)
        for copy in second:
            copy.wait()
        top = stats[0, 0:1, :]
        for z in (1, 2, 3):
            top = jnp.maximum(top, stats[z, 0:1, :])
        total = jnp.zeros_like(top)
        picked = jnp.zeros_like(top)
        for z in range(4):
            total = total + stats[z, 1:2, :] * jnp.exp(stats[z, 0:1, :] - top)
            picked = picked + stats[z, 2:3, :]
        log_total = top + jnp.log(total)
        whole[...] = jnp.where(scale[...] > 0, log_total - picked, 0.0)
        loss_out[...] = whole[:, pl.ds(pl.multiple_of(pos * rows, 128), rows)]

        def pull(at, carry):
            here = rows_at(at * tile, tile)
            probs = jnp.exp(logits_of(at) - log_total)
            grads = ((probs - jnp.where(hits_of(at), 1.0, 0.0)) * scale[...]).astype(jnp.bfloat16)
            gp[...] += dot_tn(grads, tv[here, :])
            gt[here, :] = dot_nn(grads, line_rows).astype(jnp.bfloat16)
            return carry

        lax.fori_loop(0, count, pull, 0)
        gsend[...] = gp[...].astype(jnp.bfloat16).reshape(gsend.shape)
        for k in (2, 1, 3, 0):
            back(k).start()
        keep = pltpu.make_async_copy(gt, gtable, gsem)
        keep.start()
        for k in range(4):
            back(k).wait_send()
        keep.wait()

    pl.when(sec == 0)(score)
    pl.when(sec == 1)(give)


def run_vocabulary(proj, ids, scale, table, collective_id):
    rows, emb = proj.shape
    low, f32, dma = jnp.bfloat16, jnp.float32, pltpu.SemaphoreType.DMA
    return pl.pallas_call(
        functools.partial(vocabulary_kernel, 1024),
        out_shape=[
            jax.ShapeDtypeStruct((rows, emb), low),
            jax.ShapeDtypeStruct((1, rows), f32),
            jax.ShapeDtypeStruct(table.shape, low),
        ],
        in_specs=[IN_VMEM] * 3 + [ANYWHERE],
        out_specs=[IN_VMEM] * 2 + [ANYWHERE],
        scratch_shapes=[
            pltpu.VMEM(table.shape, low),
            pltpu.VMEM(table.shape, low),
            pltpu.VMEM((4, rows, emb), low),
            pltpu.VMEM((4 * rows, emb), f32),
            pltpu.VMEM((4, rows, emb), low),
            pltpu.VMEM((4, rows, emb), low),
            pltpu.VMEM((8, 4 * rows), f32),
            pltpu.VMEM((4, 8, 4 * rows), f32),
            pltpu.VMEM((1, 4 * rows), f32),
            dma,
            dma,
            dma((4,)),
            dma((4,)),
            dma((3,)),
            dma((3,)),
            dma((4,)),
            dma((4,)),
        ],
        compiler_params=pltpu.CompilerParams(
            collective_id=collective_id, has_side_effects=True, vmem_limit_bytes=60 << 20
        ),
    )(proj, ids, scale, table)


def widen_kernel(count, *refs):
    for src, dst in zip(refs[:count], refs[count:]):
        dst[...] = src[...].astype(jnp.float32)


def widen(arrays):
    steps = 8

    def spec(x):
        return pl.BlockSpec((x.shape[0] // steps, x.shape[1]), lambda at: (at, 0))

    size = sum(x.size for x in arrays)
    return pl.pallas_call(
        functools.partial(widen_kernel, len(arrays)),
        grid=(steps,),
        out_shape=[jax.ShapeDtypeStruct(x.shape, jnp.float32) for x in arrays],
        in_specs=[spec(x) for x in arrays],
        out_specs=[spec(x) for x in arrays],
        cost_estimate=pl.CostEstimate(flops=size, bytes_accessed=6 * size, transcendentals=0),
        compiler_params=pltpu.CompilerParams(vmem_limit_bytes=60 << 20),
    )(*arrays)


def strip_of(rows, columns):
    strip = 16
    while 2 * strip * columns <= 65536 and rows % (2 * strip) == 0:
        strip = 2 * strip
    return strip


def add_rows(store, terms, rows, columns):
    strip = strip_of(rows, columns)

    def body(at, carry):
        here = rows_at(at * strip, strip)
        total = terms[0](here).astype(jnp.float32)
        for term in terms[1:]:
            total = total + term(here).astype(jnp.float32)
        store(here, total)
        return carry

    lax.fori_loop(0, rows // strip, body, 0)


def reduce_kernel(plan, only, extras, pace, refs_of, *refs):
    body = functools.partial(reduce_body, plan, extras, pace, refs_of(refs))
    if only is None:
        body()
    else:
        pl.when(lax.axis_index("section") == only)(body)


def stage_blocks(order):
    left = list(range(1 << len(order)))
    kept = []
    for bit in order:
        left = [r for r in left if not (r >> bit) & 1]
        kept.append(left)
    return kept


def reduce_body(plan, extras, pace, named):
    arrays, outs, shapes = named["arrays"], named["outs"], named["shapes"]
    lefts, rights, made = named["lefts"], named["rights"], named["made"]
    own, got1, got2, got3, got4, land = (
        named[k] for k in ("own", "got1", "got2", "got3", "got4", "land")
    )
    ssem, rsem, own_sem, s4, r4, fin_sem = named["sems"]
    got = (got1, got2, got3, got4)
    count = len(plan)
    sec = lax.axis_index("section")
    grp = lax.axis_index("group")
    pos = lax.axis_index("dp")
    beside = ((sec, grp ^ 1, pos), (sec, grp ^ 2, pos))
    swaps = beside + ((sec, grp, pos ^ 1), (sec, grp, pos ^ 2))
    sides = [(sec, grp ^ j, pos) for j in (1, 2, 3)]
    line_peers = [(sec, grp, lax.rem(pos + k, 4)) for k in (1, 2, 3)]
    steps = [(jg, jz) for jg in range(4) for jz in range(4)][1:]
    kept = [stage_blocks(piece[1]) for piece in plan]

    def other(j):
        return (sec, grp ^ steps[j][0], lax.rem(pos + steps[j][1], 4))

    with_gains = "gains" in extras
    spreads = "spread" in extras
    looked = "looked" in extras
    if with_gains:
        peers = [other(j) for j in range(15)]
    elif looked:
        peers = sides + line_peers
    else:
        peers = [swaps[bit] for bit in sorted(plan[0][1])]
    barrier = pltpu.get_barrier_semaphore()
    for device in peers:
        pl.semaphore_signal(barrier, inc=1, device_id=device, device_id_type=MESH)
    pl.semaphore_wait(barrier, len(peers))

    def rows_of(p):
        return shapes[plan[p][0]][0] // (len(kept[p][0]) // 2)

    def columns_of(p):
        return shapes[plan[p][0]][1]

    def sub_of(p):
        return rows_of(p) // 4 // plan[p][3]

    def block_rows(p, r):
        who = grp ^ (r & 3)
        line = pos ^ (r >> 2) if len(plan[p][1]) == 4 else 0
        start = line * rows_of(p) + who * (rows_of(p) // 4) + plan[p][2] * sub_of(p)
        return rows_at(start, sub_of(p))

    def block(p, r):
        return arrays[plan[p][0]].at[block_rows(p, r)]

    def is_product(p):
        return plan[p][0] in lefts

    def load_factors(src):
        hbm_left, left, hbm_right, right = lefts[src] + rights[src]
        sem = named["factor_sem"]
        return (
            pltpu.make_async_copy(hbm_left, left, sem.at[src, 0]),
            pltpu.make_async_copy(hbm_right, right, sem.at[src, 1]),
        )

    ready = []

    def multiply(p, blocks, store):
        src = plan[p][0]
        left, right = lefts[src][1], rights[src][1]
        if src not in ready:
            for copy in load_factors(src):
                copy.wait()
            ready.append(src)
        rows = jnp.concatenate([left[block_rows(p, r), :] for r in blocks], 0)
        wide = min(columns_of(p), 1024)

        def body(at, carry):
            cols = pl.ds(pl.multiple_of(at * wide, 128), wide)
            total = dot_nn(rows, right[:, cols])
            store(cols, total.reshape(len(blocks), sub_of(p), wide))
            return carry

        lax.fori_loop(0, columns_of(p) // wide, body, 0)

    def spot(p, r):
        return kept[p][0].index(r)

    def swap(p, stage, at):
        bit = plan[p][1][stage]
        r = kept[p][stage][at] | (1 << bit)
        if stage:
            src = own[p].at[spot(p, r)]
        else:
            src = made[p].at[at] if is_product(p) else block(p, r)
        return remote(
            src, got[stage][p].at[at], ssem.at[p, stage, at], rsem.at[p, stage, at], swaps[bit]
        )

    def load_own(p, at):
        return pltpu.make_async_copy(block(p, kept[p][0][at]), own[p].at[at], own_sem.at[p, at])

    def order_of(p, stage):
        places = range(len(kept[p][stage]))
        if stage == len(plan[p][1]) - 1:
            return list(places)
        bit = plan[p][1][stage + 1]
        return sorted(places, key=lambda at: 1 - ((kept[p][stage][at] >> bit) & 1))

    def begin(p):
        if is_product(p):

            def store(cols, total):
                made[p][:, :, cols] = total.astype(jnp.bfloat16)

            multiply(p, [r | (1 << plan[p][1][0]) for r in kept[p][0]], store)
        for at in order_of(p, 0):
            swap(p, 0, at).start()
            if not is_product(p):
                load_own(p, at).start()

    def advance(p, stage):
        if stage == 0 and is_product(p):
            for at in order_of(p, 0):
                swap(p, 0, at).wait_recv()

            def store_sum(cols, total):
                total = total + got1[p][:, :, cols].astype(jnp.float32)
                got1[p][:, :, cols] = total.astype(jnp.bfloat16)

            multiply(p, kept[p][0], store_sum)
            bit = plan[p][1][1]
            for at in order_of(p, 0):
                r = kept[p][0][at]
                if (r >> bit) & 1:
                    swap(p, 1, kept[p][1].index(r ^ (1 << bit))).start()
            return
        for at in order_of(p, stage):
            r = kept[p][stage][at]
            place = spot(p, r)
            if stage == 0:
                load_own(p, at).wait()
            swap(p, stage, at).wait_recv()
            terms = [
                lambda here, place=place: own[p][place, here, :],
                lambda here, at=at: got[stage][p][at, here, :],
            ]
            if stage == len(plan[p][1]) - 1:
                settle(p, terms)
                return

            def store(here, total, place=place):
                own[p][place, here, :] = total.astype(jnp.bfloat16)

            add_rows(store, terms, sub_of(p), columns_of(p))
            bit = plan[p][1][stage + 1]
            if (r >> bit) & 1:
                swap(p, stage + 1, kept[p][stage + 1].index(r ^ (1 << bit))).start()

    def write_out(p, who, at):
        start = who * (rows_of(p) // 4) + plan[p][2] * sub_of(p)
        return pltpu.make_async_copy(
            land[p].at[who], outs[plan[p][0]].at[rows_at(start, sub_of(p))], named["out_sem"].at[p, at]
        )

    def spread(p, way):
        if way < 2:
            here = land[p].at[grp]
            return remote(here, here, s4.at[p, way], r4.at[p, way], beside[way])
        half = columns_of(p) // 2
        there = land[p].at[grp ^ (way - 1), :, pl.ds(half * (way - 2), half)]
        return remote(there, there, s4.at[p, way], r4.at[p, way], beside[3 - way])

    def settle(p, terms):
        mine = grp if spreads else 0

        def store(here, total):
            land[p][mine, here, :] = total.astype(jnp.bfloat16)

        add_rows(store, terms, sub_of(p), columns_of(p))
        if spreads:
            spread(p, 0).start()
            spread(p, 1).start()
        else:
            own_out(p).start()

    def own_out(p):
        return pltpu.make_async_copy(
            land[p].at[0], outs[plan[p][0]].at[rows_at(plan[p][2] * sub_of(p), sub_of(p))], fin_sem.at[p]
        )

    def arrival(p, way):
        who = (grp ^ 1, grp ^ 2)[way]
        return remote(land[p].at[who], land[p].at[who], s4.at[p, way], r4.at[p, way], beside[way])

    def pass_on(p):
        if spreads:
            for way in (0, 1):
                arrival(p, way).wait_recv()
                spread(p, way + 2).start()

    def write_near(p):
        if spreads:
            for at, who in enumerate((grp, grp ^ 1, grp ^ 2)):
                write_out(p, who, at).start()

    def write_far(p):
        if spreads:
            spread(p, 2).wait_recv()
            spread(p, 3).wait_recv()
            write_out(p, grp ^ 3, 3).start()

    if with_gains:
        gain_in, gain_got, sg, rg, gain_sem = named["gain_scratch"]

        def gain_copy(j):
            device = other(j)
            return remote(gain_in.at[device[2]], gain_got.at[j], sg.at[j], rg.at[j], device)

        gain_load = pltpu.make_async_copy(named["gains"], gain_in, gain_sem)
        gain_load.start()

    if looked:
        looks, looks_own, sl, rl, table_fin, tland, tsum = named["look_scratch"]
        ids, look_in, fin_in = named["look_in"]
        vocab_quarter = fin_in.shape[0]
        look_load = pltpu.make_async_copy(look_in, looks.at[grp, pos], looks_own.at[0])
        fin_load = pltpu.make_async_copy(fin_in, table_fin, looks_own.at[1])

        def look_line(k):
            here = looks.at[grp, pos]
            return remote(here, here, sl.at[k], rl.at[k], line_peers[k])

        def look_side(k):
            here = looks.at[grp]
            return remote(here, here, sl.at[3 + k], rl.at[3 + k], sides[k])

        def table_spread(way):
            if way < 2:
                here = tland.at[grp]
                return remote(here, here, sl.at[6 + way], rl.at[6 + way], beside[way])
            half = tland.shape[2] // 2
            there = tland.at[grp ^ (way - 1), :, pl.ds(half * (way - 2), half)]
            return remote(there, there, sl.at[6 + way], rl.at[6 + way], beside[3 - way])

        def table_out(who):
            return pltpu.make_async_copy(
                tland.at[who],
                named["table_out"].at[rows_at(who * vocab_quarter, vocab_quarter)],
                looks_own.at[2 + who],
            )

        def look_begin():
            look_load.start()
            fin_load.start()
            look_load.wait()
            for k in range(3):
                look_line(k).start()

        def look_middle():
            for k in range(3):
                look_line(k).wait_recv()
            for k in range(3):
                look_side(k).start()

        def look_sum():
            for k in range(3):
                look_side(k).wait_recv()
            fin_load.wait()
            base = pos * (4 * vocab_quarter) + grp * vocab_quarter
            tall = 256
            names = lax.broadcasted_iota(jnp.int32, (tall, ids.shape[2]), 0)

            def body(at, carry):
                here = rows_at(at * tall, tall)
                total = table_fin[here, :].astype(jnp.float32)
                for g in range(4):
                    for z in range(4):
                        hit = names + (base + at * tall) == ids[g * 4 + z]
                        total = total + dot_nn(
                            jnp.where(hit, 1.0, 0.0).astype(jnp.bfloat16), looks[g, z]
                        )
                tland[grp, here, :] = total.astype(jnp.bfloat16)
                return carry

            lax.fori_loop(0, vocab_quarter // tall, body, 0)
            table_spread(0).start()
            table_spread(1).start()

        def look_pass():
            for way in (0, 1):
                who = (grp ^ 1, grp ^ 2)[way]
                remote(
                    tland.at[who], tland.at[who], sl.at[6 + way], rl.at[6 + way], beside[way]
                ).wait_recv()
                table_spread(way + 2).start()

        def look_end():
            table_spread(2).wait_recv()
            table_spread(3).wait_recv()
            for who in range(4):
                table_out(who).start()
            for who in range(4):
                table_out(who).wait()
            for k in range(3):
                look_line(k).wait_send()
                look_side(k).wait_send()
            for way in range(4):
                table_spread(way).wait_send()

        def on_first(run):
            pl.when(sec == 0)(run)

    else:

        def on_first(run):
            pass

        look_begin = look_middle = look_sum = look_pass = look_end = None

    ahead, lag, lag_end = pace
    for piece in plan:
        if piece[0] in lefts and piece[0] not in ready:
            ready.append(piece[0])
            for copy in load_factors(piece[0]):
                copy.start()
    ready.clear()
    on_first(look_begin)
    for p in range(min(ahead, count)):
        begin(p)
    if with_gains:
        gain_load.wait()
        for j in range(15):
            gain_copy(j).start()
    delays = [0, lag, 2 * lag, 3 * lag, 3 * lag + lag_end, 3 * lag + 2 * lag_end, 3 * lag + 3 * lag_end]
    for at in range(count + delays[-1]):
        if ahead + at < count:
            begin(ahead + at)
        for stage in range(len(plan[0][1])):
            if 0 <= at - delays[stage] < count:
                advance(at - delays[stage], stage)
        for run, delay in zip((pass_on, write_near, write_far), delays[4:]):
            if 0 <= at - delay < count:
                run(at - delay)
        for when, run in ((1, look_middle), (3, look_sum), (5, look_pass)):
            if at == when * (count + delays[3]) // 6:
                on_first(run)
    if with_gains:
        for j in range(15):
            gain_copy(j).wait_recv()
        total = gain_in[pos]
        for j in range(15):
            total = total + gain_got[j]
        named["gain_out"][...] = total
    on_first(look_end)
    for p in range(count):
        if spreads:
            for at, who in enumerate((grp, grp ^ 1, grp ^ 2, grp ^ 3)):
                write_out(p, who, at).wait()
            for way in range(4):
                spread(p, way).wait_send()
        else:
            own_out(p).wait()
        for stage in range(len(plan[p][1])):
            for at in range(len(kept[p][stage])):
                swap(p, stage, at).wait_send()
    if with_gains:
        for j in range(15):
            gain_copy(j).wait_send()


def reduce_all(arrays, plan, only, collective_id, pace, gains=None, look=None, spread=True):
    low, f32, dma = jnp.bfloat16, jnp.float32, pltpu.SemaphoreType.DMA
    extras = ("spread",) * spread + ("gains",) * (gains is not None) + ("looked",) * (look is not None)
    count = len(plan)
    factors = {src: x for src, x in enumerate(arrays) if isinstance(x, tuple)}
    plain = [x for x in arrays if not isinstance(x, tuple)]
    flat_factors = [part for x in factors.values() for part in x]
    inputs = plain + flat_factors
    sizes = [(x[0].shape[0], x[1].shape[1]) if isinstance(x, tuple) else x.shape for x in arrays]
    lines = 4 if len(plan[0][1]) == 4 else 1
    share = lines if spread else 4 * lines
    outs = [jax.ShapeDtypeStruct((rows // share, columns), low) for rows, columns in sizes]
    out_specs = [ANYWHERE] * len(arrays)
    in_specs = [ANYWHERE] * len(inputs)
    names = ["own", "got1", "got2", "got3", "got4", "land"]
    scratch = {name: [] for name in names}
    for src, _, _, chunks in plan:
        rows, columns = sizes[src][0] // lines, sizes[src][1]
        sub = rows // 4 // chunks
        held = (8, 8, 4, 2, 1) if lines == 4 else (2, 2, 1, 0, 0)
        for name, blocks in zip(names, held + (4 if spread else 1,)):
            shape = (blocks, sub, columns) if blocks else (8, 128)
            scratch[name].append(pltpu.VMEM(shape, low))
    flat = [item for name in names for item in scratch[name]]
    sems = [dma((count, 4, 8))] * 2 + [dma((count, 8))] + [dma((count, 4))] * 2 + [dma((count,))]
    tail = []
    if factors:
        tail += [pltpu.VMEM(x.shape, low) for x in flat_factors] + [dma((len(arrays), 2))]
    if spread:
        tail += [dma((count, 4))]
    if gains is not None:
        inputs.append(gains)
        in_specs.append(ANYWHERE)
        outs.append(jax.ShapeDtypeStruct(gains.shape[1:], f32))
        out_specs.append(IN_VMEM)
        tail += [
            pltpu.VMEM(gains.shape, f32),
            pltpu.VMEM((15,) + gains.shape[1:], f32),
            dma((15,)),
            dma((15,)),
            dma,
        ]
    if look is not None:
        ids, rows_in, fin_in = look
        inputs += [ids, rows_in, fin_in]
        in_specs += [IN_VMEM, ANYWHERE, ANYWHERE]
        quarter, emb = fin_in.shape
        outs.append(jax.ShapeDtypeStruct((4 * quarter, emb), low))
        out_specs.append(ANYWHERE)
        tail += [
            pltpu.VMEM((4, 4) + rows_in.shape, low),
            dma((6,)),
            dma((10,)),
            dma((10,)),
            pltpu.VMEM(fin_in.shape, low),
            pltpu.VMEM((4, quarter, emb), low),
            pltpu.VMEM((8, 128), f32),
        ]

    def refs_of(refs):
        at = 0

        def take(n):
            nonlocal at
            at += n
            return list(refs[at - n : at])

        plain_refs = iter(take(len(plain)))
        named = {"shapes": sizes, "arrays": [None if src in factors else next(plain_refs) for src in range(len(arrays))]}
        pair_refs = take(len(flat_factors))
        if gains is not None:
            named["gains"] = take(1)[0]
        if look is not None:
            named["look_in"] = take(3)
        named["outs"] = take(len(arrays))
        if gains is not None:
            named["gain_out"] = take(1)[0]
        if look is not None:
            named["table_out"] = take(1)[0]
        for name in names:
            named[name] = take(count)
        named["sems"] = take(6)
        pair_bufs = take(len(flat_factors))
        named["lefts"], named["rights"], named["made"] = {}, {}, {}
        for nth, src in enumerate(factors):
            named["lefts"][src] = (pair_refs[2 * nth], pair_bufs[2 * nth])
            named["rights"][src] = (pair_refs[2 * nth + 1], pair_bufs[2 * nth + 1])
        if factors:
            named["factor_sem"] = take(1)[0]
        for p in range(count):
            if plan[p][0] in factors:
                named["made"][p] = named["own"][p]
                named["own"][p] = named["got1"][p]
        if spread:
            named["out_sem"] = take(1)[0]
        if gains is not None:
            named["gain_scratch"] = take(5)
        if look is not None:
            named["look_scratch"] = take(7)
        return named

    return pl.pallas_call(
        functools.partial(reduce_kernel, plan, only, extras, pace, refs_of),
        out_shape=outs,
        in_specs=in_specs,
        out_specs=out_specs,
        scratch_shapes=flat + sems + tail,
        compiler_params=pltpu.CompilerParams(
            collective_id=collective_id, has_side_effects=True, vmem_limit_bytes=60 << 20
        ),
    )(*inputs)


def nothing_like(run):
    return jax.tree.map(lambda a: jnp.zeros(a.shape, a.dtype), jax.eval_shape(run))


def only_on(live, run):
    return lax.cond(live, run, lambda: nothing_like(run))


X_FIRST = (0, 1, 2, 3)
Y_FIRST = (1, 0, 2, 3)
Z_THEN_X = (2, 0, 1, 3)
Z_THEN_Y = (2, 1, 0, 3)
ORDERS = (X_FIRST, Z_THEN_Y, Y_FIRST, Z_THEN_X)
LAYER_PLAN = (
    tuple((0, ORDERS[chunk], chunk, 4) for chunk in range(4))
    + tuple((1, ORDERS[chunk], chunk, 4) for chunk in range(4))
    + ((4, X_FIRST, 0, 4), (4, Y_FIRST, 1, 4), (4, X_FIRST, 2, 4), (4, Z_THEN_Y, 3, 4))
    + ((3, X_FIRST, 0, 2), (3, Y_FIRST, 1, 2), (2, X_FIRST, 0, 1))
)
TABLE_PLAN = tuple((0, ((0, 1), (1, 0))[chunk % 2], chunk, 4) for chunk in range(4))
LAYER_PACE = (8, 4, 2)
TABLE_PACE = (4, 2, 1)


def after(value, *others):
    return lax.optimization_barrier((value,) + others)[0]


def per_device(
    tokens,
    lengths,
    levels,
    noise_rows,
    embed_table,
    w_in,
    ln_attn,
    w_qkv,
    w_proj,
    ln_mlp,
    w_up,
    w_down,
    ln_final,
    w_out,
):
    sec = lax.axis_index("section")
    pos = lax.axis_index("dp")
    first_section = sec == 0
    last_section = sec == 1
    rows = tokens.shape[0]
    seqs = lengths.shape[0]
    length = rows // seqs
    width = w_out.shape[0] * 4
    emb = w_out.shape[1]
    vocab_part = embed_table.shape[0]
    gains = jnp.concatenate(
        [ln_attn, ln_mlp, ln_final[None], jnp.zeros((13, ln_final.shape[0]), jnp.bfloat16)], 0
    )
    ids = jnp.concatenate(
        [
            tokens.reshape(-1, 128),
            jnp.concatenate([lengths, jnp.zeros((128 - seqs,), jnp.int32)])[None],
            jnp.zeros((7 - rows // 128, 128), jnp.int32),
        ],
        0,
    )
    shards = (w_qkv[0], w_proj[0], w_up[0], w_down[0], w_in, w_out, gains, ids)
    sizes = [s.shape[0] for s in shards]

    def cut(idx, count, whole=False):
        return tuple((idx, at * sizes[idx] // count, sizes[idx] // count, whole) for at in range(count))

    layer = cut(0, 2) + cut(2, 2) + cut(3, 2)
    wholes = gather_all(
        shards,
        cut(7, 1, True) + cut(6, 1, True) + cut(4, 1) + layer + cut(1, 4, True),
        cut(6, 1, True) + layer + cut(5, 1) + cut(1, 4, True),
        0,
    )
    qkv_weight, proj_weight, up_weight, down_weight, in_weight, out_weight, gain_all, line_ids = wholes
    gain_all = gain_all.reshape(4, 16, -1).astype(jnp.float32)
    gain_attn = gain_all[:, 0].reshape(-1)
    gain_mlp = gain_all[:, 1].reshape(-1)
    final_gain = gain_all[:, 2].reshape(-1)
    weights = (qkv_weight, proj_weight, up_weight, down_weight)
    gain_attn = gain_attn[None]
    gain_mlp = gain_mlp[None]
    final_gain = final_gain[None]
    loss_scale = LOSS_GAIN / math.sqrt(rows * lax.axis_size(("group", "dp")))

    def look_up():
        local = line_ids.reshape(4, 8, 128)[:, : rows // 128].reshape(-1) - pos * vocab_part
        hit = local[:, None] == lax.broadcasted_iota(jnp.int32, (1, vocab_part), 1)
        return product(hit.astype(jnp.bfloat16), embed_table).astype(jnp.bfloat16)

    looked_parts = only_on(first_section, look_up).reshape(4, rows, emb)
    looked_parts, all_ids = swap_rows(looked_parts, line_ids, 1)
    all_tokens = all_ids.reshape(16, 8, 128)[:, : rows // 128].reshape(-1)
    noise_level = jnp.exp(LOG_LOW + levels.astype(jnp.float32) * (LOG_SPAN / (LEVELS - 1)))
    scale_in = lax.rsqrt(EMB_VAR + noise_level * noise_level)
    row_level = jnp.repeat(noise_level, length)[:, None]
    row_scale = jnp.repeat(scale_in, length)[:, None]

    def front():
        looked = jnp.sum(looked_parts.astype(jnp.float32), 0)
        mixed_in = ((looked + row_level * noise_rows.astype(jnp.float32)) * row_scale).astype(
            jnp.bfloat16
        )
        return mixed_in, product(mixed_in, in_weight)

    mixed_in, x_first = only_on(first_section, front)
    *kept, out_first = run_forward(
        0, x_first, gain_attn, gain_mlp, lengths, final_gain, out_weight, weights, None
    )
    x_second = passed_along(out_first, "section", 1)
    *kept, final_in, projected = run_forward(
        1, x_second, gain_attn, gain_mlp, lengths, final_gain, out_weight, weights, kept
    )
    line_parts = line_ids.reshape(4, 8, 128)
    line_tokens = line_parts[:, : rows // 128].reshape(1, -1)
    line_counts = line_parts[:, rows // 128, :seqs].reshape(-1, 1)
    line_valid = jnp.arange(length, dtype=jnp.int32)[None, :] < line_counts
    line_scale = jnp.where(line_valid.reshape(1, -1), loss_scale, 0.0)
    grad_proj, entropy, table_g = run_vocabulary(projected, line_tokens, line_scale, embed_table, 2)
    (table_fin,) = reduce_all(
        (table_g,),
        TABLE_PLAN,
        0,
        3,
        TABLE_PACE,
        spread=False,
    )
    made = run_backward(
        1, grad_proj, gain_attn, gain_mlp, lengths, final_gain, out_weight, kept, weights, None
    )
    grad_first = passed_along(after(made[4], table_fin), "section", -1)
    made = run_backward(
        0, grad_first, gain_attn, gain_mlp, lengths, final_gain, out_weight, kept, weights, made
    )
    shape = in_weight.shape

    def front_edge():
        looked_grad = (product_nt(made[4], in_weight) * row_scale).astype(jnp.bfloat16)
        return product_tn(mixed_in, made[4]).astype(jnp.bfloat16), looked_grad

    def back_edge():
        edge = product_tn(final_in, grad_proj).astype(jnp.bfloat16)
        edge = edge.reshape(4, shape[0] // 4, shape[1]).reshape(shape)
        return edge, jnp.zeros((rows, emb), jnp.bfloat16)

    edge_g, looked_grad = lax.cond(first_section, front_edge, back_edge)
    gain_rows = made[5]
    gain_rows = gain_rows.reshape(8, 4, width // 4).transpose(1, 0, 2)

    order = (
        (kept[6], made[1]),
        (kept[8], made[0]),
        edge_g,
        (kept[4], made[2]),
        (kept[1], made[3]),
    )
    up_r, down_r, edge_r, proj_r, qkv_r, gain_r, table_r = reduce_all(
        order,
        LAYER_PLAN,
        None,
        4,
        LAYER_PACE,
        gains=gain_rows,
        look=(all_tokens.reshape(16, 1, rows), looked_grad, table_fin),
    )
    loss_low = after(entropy, gain_r)[0].astype(jnp.bfloat16)
    mine = (table_r, edge_r, gain_r, loss_low)
    theirs = lax.ppermute(mine, "section", [(0, 1), (1, 0)])

    def pair_of(at):
        low = jnp.where(first_section, mine[at], theirs[at])
        high = jnp.where(first_section, theirs[at], mine[at])
        return low, high

    up_r, down_r, proj_r, qkv_r = widen((up_r, down_r, proj_r, qkv_r))
    table_out = pair_of(0)[0].astype(jnp.float32)
    in_r, out_r = pair_of(1)
    final_r = pair_of(2)[1][2]
    token_loss = pair_of(3)[0]
    return (
        token_loss,
        table_out,
        in_r.astype(jnp.float32),
        gain_r[0][None],
        qkv_r[None],
        proj_r[None],
        gain_r[1][None],
        up_r[None],
        down_r[None],
        final_r,
        out_r.astype(jnp.float32).reshape(-1, emb),
    )


def solution(mesh):
    placed = (
        P(("group", "dp")),
        P(("group", "dp")),
        P(("group", "dp")),
        P(("group", "dp"), None),
        P("dp", None),
        P("dp", None),
        P("section", "dp"),
        P("section", "dp", None),
        P("section", "dp", None),
        P("section", "dp"),
        P("section", "dp", None),
        P("section", "dp", None),
        P("dp"),
        P("dp", None),
    )
    fits = (mesh.shape["section"], mesh.shape["group"], mesh.shape["dp"]) == (2, 4, 4)
    return jax.shard_map(
        per_device if fits else per_device_general,
        mesh=mesh,
        in_specs=placed,
        out_specs=(
            P(("group", "dp")),
            P("dp", None),
            P("dp", None),
            P("section", "dp"),
            P("section", "dp", None),
            P("section", "dp", None),
            P("section", "dp"),
            P("section", "dp", None),
            P("section", "dp", None),
            P("dp"),
            P("dp", None),
        ),
        check_vma=False,
    )
```

```python
import functools
import math

import jax
import jax.numpy as jnp
from jax import lax
from jax.experimental import pallas as pl
from jax.experimental.pallas import tpu as pltpu
from jax.sharding import PartitionSpec as P

HEAD = 64
LEVELS = 64
LEN = 128
MB = 2


EPS = 1e-05
LOG_LOW = -2.995732273553991
LOG_SPAN = 2.995732273553991
EMB_VAR = 0.015625
MASKED = -1e30
LOSS_GAIN = 16.0


def passed_along(x, axis, by):
    count = lax.axis_size(axis)
    pairs = [(i, i + by) for i in range(count) if 0 <= i + by < count]
    return lax.ppermute(x, axis, pairs)


def product(left_side, right_side):
    return jnp.dot(left_side, right_side, preferred_element_type=jnp.float32)


def product_tn(left_side, right_side):
    return lax.dot_general(
        left_side, right_side, (((0,), (0,)), ((), ())), preferred_element_type=jnp.float32
    )


def product_nt(left_side, right_side):
    return lax.dot_general(
        left_side, right_side, (((1,), (1,)), ((), ())), preferred_element_type=jnp.float32
    )


def normed(inputs, gain_vec):
    center = inputs - jnp.mean(inputs, -1, keepdims=True)
    return center * lax.rsqrt(jnp.mean(center * center, -1, keepdims=True) + EPS) * gain_vec


def norm_back(inputs, gain_vec, upstream):
    output, pullback = jax.vjp(normed, inputs, gain_vec)
    return pullback(upstream)


def gelu_exact(values_in):
    return jax.nn.gelu(values_in, approximate=False)


def attn_scores(split_rows, key_valid):
    scores = (
        jnp.einsum(
            "qhd,khd->hqk", split_rows[:, 0], split_rows[:, 1], preferred_element_type=jnp.float32
        )
        * 0.125
    )
    return jnp.where(key_valid[None, None, :], scores, MASKED)


def attend(qkv_rows, key_valid):
    length = qkv_rows.shape[0]
    model_width = qkv_rows.shape[1] // 3
    split_rows = qkv_rows.reshape(length, 3, model_width // HEAD, HEAD)
    scores = attn_scores(split_rows, key_valid)
    row_max = jnp.max(scores, -1, keepdims=True)
    log_total = row_max + jnp.log(jnp.sum(jnp.exp(scores - row_max), -1, keepdims=True))
    probs_low = jnp.exp(scores - log_total).astype(jnp.bfloat16)
    mixed_rows = jnp.einsum(
        "hqk,khd->qhd", probs_low, split_rows[:, 2], preferred_element_type=jnp.float32
    )
    return (mixed_rows.reshape(length, model_width).astype(jnp.bfloat16), log_total)


def attend_back(qkv_rows, key_valid, log_total, grad_mixed):
    length = qkv_rows.shape[0]
    model_width = qkv_rows.shape[1] // 3
    head_count = model_width // HEAD
    split_rows = qkv_rows.reshape(length, 3, head_count, HEAD)
    grad_heads = grad_mixed.reshape(length, head_count, HEAD)
    probs_full = jnp.exp(attn_scores(split_rows, key_valid) - log_total)
    grad_values = jnp.einsum(
        "hqk,qhd->khd",
        probs_full.astype(jnp.bfloat16),
        grad_heads,
        preferred_element_type=jnp.float32,
    )
    grad_probs = jnp.einsum(
        "qhd,khd->hqk", grad_heads, split_rows[:, 2], preferred_element_type=jnp.float32
    )
    grad_scores = (
        probs_full * (grad_probs - jnp.sum(grad_probs * probs_full, -1, keepdims=True))
    ).astype(jnp.bfloat16)
    grad_query = (
        jnp.einsum(
            "hqk,khd->qhd", grad_scores, split_rows[:, 1], preferred_element_type=jnp.float32
        )
        * 0.125
    )
    grad_key = (
        jnp.einsum(
            "hqk,qhd->khd", grad_scores, split_rows[:, 0], preferred_element_type=jnp.float32
        )
        * 0.125
    )
    stacked = jnp.stack([grad_query, grad_key, grad_values], 1).reshape(length, 3 * model_width)
    return stacked.astype(jnp.bfloat16)


def layer_forward(hidden, key_valid, weights):
    gain_attn, qkv_weight, proj_weight, gain_mlp, up_weight, down_weight = weights
    normed_in = normed(hidden, gain_attn).astype(jnp.bfloat16)
    qkv_rows = product(normed_in, qkv_weight).astype(jnp.bfloat16)
    mixed_rows, log_total = attend(qkv_rows, key_valid)
    hidden_mid = hidden + product(mixed_rows, proj_weight)
    mlp_in = normed(hidden_mid, gain_mlp).astype(jnp.bfloat16)
    pre_act = product(mlp_in, up_weight)
    activated = gelu_exact(pre_act).astype(jnp.bfloat16)
    hidden_out = hidden_mid + product(activated, down_weight)
    return (
        hidden_out,
        (
            hidden,
            normed_in,
            qkv_rows,
            log_total,
            mixed_rows,
            hidden_mid,
            mlp_in,
            pre_act,
            activated,
        ),
    )


def empty_kept(length, model_width, hidden_units, head_count):
    return (
        jnp.zeros((length, model_width), jnp.float32),
        jnp.zeros((length, model_width), jnp.bfloat16),
        jnp.zeros((length, 3 * model_width), jnp.bfloat16),
        jnp.zeros((head_count, length, 1), jnp.float32),
        jnp.zeros((length, model_width), jnp.bfloat16),
        jnp.zeros((length, model_width), jnp.float32),
        jnp.zeros((length, model_width), jnp.bfloat16),
        jnp.zeros((length, hidden_units), jnp.float32),
        jnp.zeros((length, hidden_units), jnp.bfloat16),
    )


def layer_backward(kept_vals, grad_out, key_valid, weights):
    hidden, normed_in, qkv_rows, log_total, mixed_rows, hidden_mid, mlp_in, pre_act, activated = (
        kept_vals
    )
    gain_attn, qkv_weight, proj_weight, gain_mlp, up_weight, down_weight = weights
    grad_low = grad_out.astype(jnp.bfloat16)
    grad_activated = product_nt(grad_low, down_weight)
    grad_pre = jax.vjp(gelu_exact, pre_act)[1](grad_activated)[0].astype(jnp.bfloat16)
    grad_mlp_in = product_nt(grad_pre, up_weight)
    grad_mid_norm, grad_gain_mlp = norm_back(hidden_mid, gain_mlp, grad_mlp_in)
    grad_mid = grad_out + grad_mid_norm
    grad_mid_low = grad_mid.astype(jnp.bfloat16)
    grad_mixed = product_nt(grad_mid_low, proj_weight).astype(jnp.bfloat16)
    grad_qkv = attend_back(qkv_rows, key_valid, log_total, grad_mixed)
    grad_normed = product_nt(grad_qkv, qkv_weight)
    grad_in_norm, grad_gain_attn = norm_back(hidden, gain_attn, grad_normed)
    records = (activated, grad_low, mlp_in, grad_pre, mixed_rows, grad_mid_low, normed_in, grad_qkv)
    return (grad_mid + grad_in_norm, (grad_gain_attn, grad_gain_mlp), records)


def layer_zero(length, model_width, hidden_units):
    records = (
        jnp.zeros((length, hidden_units), jnp.bfloat16),
        jnp.zeros((length, model_width), jnp.bfloat16),
        jnp.zeros((length, model_width), jnp.bfloat16),
        jnp.zeros((length, hidden_units), jnp.bfloat16),
        jnp.zeros((length, model_width), jnp.bfloat16),
        jnp.zeros((length, model_width), jnp.bfloat16),
        jnp.zeros((length, model_width), jnp.bfloat16),
        jnp.zeros((length, 3 * model_width), jnp.bfloat16),
    )
    gains = (jnp.zeros((model_width,), jnp.float32), jnp.zeros((model_width,), jnp.float32))
    return (jnp.zeros((length, model_width), jnp.float32), gains, records)


def layer_grads(records):
    activated, grad_low, mlp_in, grad_pre, mixed_rows, grad_mid_low, normed_in, grad_qkv = records
    return (
        product_tn(normed_in, grad_qkv),
        product_tn(mixed_rows, grad_mid_low),
        product_tn(mlp_in, grad_pre),
        product_tn(activated, grad_low),
    )


def embed_inputs(token_ids, noise_block, level_id, table_full):
    noise_level = jnp.exp(LOG_LOW + level_id.astype(jnp.float32) * (LOG_SPAN / (LEVELS - 1)))
    scale_in = lax.rsqrt(EMB_VAR + noise_level * noise_level)
    looked = jnp.take(table_full, token_ids, axis=0).astype(jnp.float32)
    mixed_in = ((looked + noise_level * noise_block.astype(jnp.float32)) * scale_in).astype(
        jnp.bfloat16
    )
    return (mixed_in, scale_in)


def embed_backward(token_ids, noise_block, level_id, grad_start, table_full, in_weight):
    mixed_in, scale_in = embed_inputs(token_ids, noise_block, level_id, table_full)
    grad_low = grad_start.astype(jnp.bfloat16)
    grad_looked = product_nt(grad_low, in_weight) * scale_in
    return (mixed_in, grad_low, grad_looked)


def embed_zero(length, model_width, emb_width):
    return (
        jnp.zeros((length, emb_width), jnp.bfloat16),
        jnp.zeros((length, model_width), jnp.bfloat16),
        jnp.zeros((length, emb_width), jnp.float32),
    )


def tail_pass(hidden, token_ids, key_valid, final_gain, out_weight, table_full, loss_scale):
    final_in = normed(hidden, final_gain).astype(jnp.bfloat16)
    projected = product(final_in, out_weight).astype(jnp.bfloat16)
    logits = product_nt(projected, table_full)
    row_max = jnp.max(logits, -1, keepdims=True)
    log_total = row_max + jnp.log(jnp.sum(jnp.exp(logits - row_max), -1, keepdims=True))
    vocab_ids = lax.broadcasted_iota(jnp.int32, logits.shape, 1)
    target_hit = vocab_ids == token_ids[:, None]
    picked = jnp.sum(jnp.where(target_hit, logits, 0.0), -1)
    entropy = jnp.where(key_valid, log_total[:, 0] - picked, 0.0)
    row_scale = jnp.where(key_valid, loss_scale, 0.0)[:, None]
    grad_logits = (
        (jnp.exp(logits - log_total) - target_hit.astype(jnp.float32)) * row_scale
    ).astype(jnp.bfloat16)
    grad_proj = product(grad_logits, table_full).astype(jnp.bfloat16)
    grad_final = product_nt(grad_proj, out_weight)
    grad_hidden, grad_gain = norm_back(hidden, final_gain, grad_final)
    return (grad_hidden, entropy, grad_gain, (grad_logits, projected, final_in, grad_proj))


def tail_zero(length, model_width, emb_width, vocab_rows):
    records = (
        jnp.zeros((length, vocab_rows), jnp.bfloat16),
        jnp.zeros((length, emb_width), jnp.bfloat16),
        jnp.zeros((length, model_width), jnp.bfloat16),
        jnp.zeros((length, emb_width), jnp.bfloat16),
    )
    return (
        jnp.zeros((length, model_width), jnp.float32),
        jnp.zeros((length,), jnp.float32),
        jnp.zeros((model_width,), jnp.float32),
        records,
    )


def edge_grads(tail_records, embed_records, token_ids):
    grad_logits, projected, final_in, grad_proj = tail_records
    mixed_in, grad_low, grad_looked = embed_records
    table_grad = product_tn(grad_logits, projected).at[token_ids].add(grad_looked)
    return (table_grad, product_tn(mixed_in, grad_low), product_tn(final_in, grad_proj))


def joined_rows(record_list):
    return jax.tree.map(lambda *pieces: jnp.concatenate(pieces, 0), *record_list)


def assemble(gain_attn_sum, gain_mlp_sum, layer_set, edge_set, gain_final_sum):
    return (
        gain_attn_sum[None],
        layer_set[0][None],
        layer_set[1][None],
        gain_mlp_sum[None],
        layer_set[2][None],
        layer_set[3][None],
        edge_set[0],
        edge_set[1],
        gain_final_sum,
        edge_set[2],
    )


def per_device_general(
    tokens,
    lengths,
    levels,
    noise_rows,
    embed_table,
    w_in,
    ln_attn,
    w_qkv,
    w_proj,
    ln_mlp,
    w_up,
    w_down,
    ln_final,
    w_out,
):
    gathered = (
        lax.all_gather(embed_table, "dp", axis=0, tiled=True),
        lax.all_gather(w_in, "dp", axis=0, tiled=True),
        lax.all_gather(ln_attn, "dp", axis=1, tiled=True),
        lax.all_gather(w_qkv, "dp", axis=1, tiled=True),
        lax.all_gather(w_proj, "dp", axis=1, tiled=True),
        lax.all_gather(ln_mlp, "dp", axis=1, tiled=True),
        lax.all_gather(w_up, "dp", axis=1, tiled=True),
        lax.all_gather(w_down, "dp", axis=1, tiled=True),
        lax.all_gather(ln_final, "dp", axis=0, tiled=True),
        lax.all_gather(w_out, "dp", axis=0, tiled=True),
    )
    table_full = gathered[0]
    in_weight = gathered[1]
    layer_weights = (
        gathered[2][0].astype(jnp.float32),
        gathered[3][0],
        gathered[4][0],
        gathered[5][0].astype(jnp.float32),
        gathered[6][0],
        gathered[7][0],
    )
    final_gain = gathered[8].astype(jnp.float32)
    out_weight = gathered[9]
    model_width = out_weight.shape[0]
    emb_width = out_weight.shape[1]
    vocab_rows = table_full.shape[0]
    hidden_units = layer_weights[4].shape[1]
    head_count = model_width // HEAD
    section_index = lax.axis_index("section")
    first_section = section_index == 0
    token_grid = tokens.reshape(MB, LEN)
    noise_grid = noise_rows.reshape(MB, LEN, noise_rows.shape[1])
    positions = jnp.arange(LEN, dtype=jnp.int32)
    valid_grid = positions[None, :] < lengths[:, None]
    loss_scale = LOSS_GAIN / math.sqrt(tokens.shape[0] * lax.axis_size(("group", "dp")))
    gain_attn_sum = jnp.zeros((model_width,), jnp.float32)
    gain_mlp_sum = jnp.zeros((model_width,), jnp.float32)
    gain_final_sum = jnp.zeros((model_width,), jnp.float32)
    recv_act = jnp.zeros((LEN, model_width), jnp.bfloat16)
    recv_grad = jnp.zeros((LEN, model_width), jnp.bfloat16)
    zero_rows = jnp.zeros((LEN, model_width), jnp.float32)
    kept_ticks = {}
    layer_recs = {}
    tail_recs = {}
    embed_recs = {}
    losses = []
    for moment in range(MB + 2):
        offset = moment - section_index
        fwd_valid = (offset >= 0) & (offset < MB)
        fwd_index = jnp.clip(offset, 0, MB - 1)
        ids_now = lax.dynamic_index_in_dim(token_grid, fwd_index, 0, False)
        noise_now = lax.dynamic_index_in_dim(noise_grid, fwd_index, 0, False)
        level_now = lax.dynamic_index_in_dim(levels, fwd_index, 0, False)
        valid_now = lax.dynamic_index_in_dim(valid_grid, fwd_index, 0, False)

        def first_input():
            mixed_in, scale_in = embed_inputs(ids_now, noise_now, level_now, table_full)
            return product(mixed_in, in_weight)

        layer_input = lax.cond(first_section, first_input, lambda: recv_act.astype(jnp.float32))
        hidden_out, kept_now = lax.cond(
            fwd_valid,
            lambda: layer_forward(layer_input, valid_now, layer_weights),
            lambda: (zero_rows, empty_kept(LEN, model_width, hidden_units, head_count)),
        )
        kept_ticks[moment] = kept_now
        tail_live = jnp.logical_not(first_section) & fwd_valid
        tail_grad, entropy, final_step, tail_now = lax.cond(
            tail_live,
            lambda: tail_pass(
                hidden_out, ids_now, valid_now, final_gain, out_weight, table_full, loss_scale
            ),
            lambda: tail_zero(LEN, model_width, emb_width, vocab_rows),
        )
        tail_recs[moment] = tail_now
        gain_final_sum = gain_final_sum + final_step
        back_tick = moment - 2
        late_live = 0 <= back_tick < MB
        late_index = min(max(back_tick, 0), MB - 1)
        kept_late = kept_ticks[back_tick] if back_tick >= 0 else kept_now
        kept_back = lax.cond(first_section, lambda: kept_late, lambda: kept_now)
        grad_top = jnp.where(first_section, recv_grad.astype(jnp.float32), tail_grad)
        valid_back = jnp.where(first_section, valid_grid[late_index], valid_now)
        back_live = jnp.where(first_section, late_live, fwd_valid)
        grad_start, gain_pair, layer_now = lax.cond(
            back_live,
            lambda: layer_backward(kept_back, grad_top, valid_back, layer_weights),
            lambda: layer_zero(LEN, model_width, hidden_units),
        )
        layer_recs[moment] = layer_now
        gain_attn_sum = gain_attn_sum + gain_pair[0]
        gain_mlp_sum = gain_mlp_sum + gain_pair[1]
        if late_live:
            embed_now = lax.cond(
                first_section,
                lambda: embed_backward(
                    token_grid[late_index],
                    noise_grid[late_index],
                    levels[late_index],
                    grad_start,
                    table_full,
                    in_weight,
                ),
                lambda: embed_zero(LEN, model_width, emb_width),
            )
        else:
            embed_now = embed_zero(LEN, model_width, emb_width)
        embed_recs[moment] = embed_now
        if moment < MB:
            recv_act = passed_along(hidden_out.astype(jnp.bfloat16), "section", 1)
        if 1 <= moment <= MB:
            entropy_low = entropy.astype(jnp.bfloat16)
            recv_grad, loss_back = passed_along(
                (grad_start.astype(jnp.bfloat16), entropy_low), "section", -1
            )
            losses.append(jnp.where(first_section, loss_back, entropy_low))
    chosen = [
        jax.tree.map(
            lambda early, late: jnp.where(first_section, early, late),
            layer_recs[micro + 2],
            layer_recs[micro + 1],
        )
        for micro in range(MB)
    ]
    all_layer = layer_grads(joined_rows(chosen))
    all_tail = joined_rows([tail_recs[micro + 1] for micro in range(MB)])
    all_embed = joined_rows([embed_recs[micro + 2] for micro in range(MB)])
    all_edge = edge_grads(all_tail, all_embed, tokens)
    grad_pack = assemble(gain_attn_sum, gain_mlp_sum, all_layer, all_edge, gain_final_sum)
    parted = (
        lax.psum_scatter(
            grad_pack[0].astype(jnp.bfloat16), "dp", scatter_dimension=1, tiled=True
        ).astype(jnp.float32),
        lax.psum_scatter(
            grad_pack[1].astype(jnp.bfloat16), "dp", scatter_dimension=1, tiled=True
        ).astype(jnp.float32),
        lax.psum_scatter(
            grad_pack[2].astype(jnp.bfloat16), "dp", scatter_dimension=1, tiled=True
        ).astype(jnp.float32),
        lax.psum_scatter(
            grad_pack[3].astype(jnp.bfloat16), "dp", scatter_dimension=1, tiled=True
        ).astype(jnp.float32),
        lax.psum_scatter(
            grad_pack[4].astype(jnp.bfloat16), "dp", scatter_dimension=1, tiled=True
        ).astype(jnp.float32),
        lax.psum_scatter(
            grad_pack[5].astype(jnp.bfloat16), "dp", scatter_dimension=1, tiled=True
        ).astype(jnp.float32),
        lax.psum_scatter(
            grad_pack[6].astype(jnp.bfloat16), "dp", scatter_dimension=0, tiled=True
        ).astype(jnp.float32),
        lax.psum_scatter(
            grad_pack[7].astype(jnp.bfloat16), "dp", scatter_dimension=0, tiled=True
        ).astype(jnp.float32),
        lax.psum_scatter(
            grad_pack[8].astype(jnp.bfloat16), "dp", scatter_dimension=0, tiled=True
        ).astype(jnp.float32),
        lax.psum_scatter(
            grad_pack[9].astype(jnp.bfloat16), "dp", scatter_dimension=0, tiled=True
        ).astype(jnp.float32),
    )
    layer_total = (
        lax.psum(parted[0].astype(jnp.bfloat16), "group").astype(jnp.float32),
        lax.psum(parted[1].astype(jnp.bfloat16), "group").astype(jnp.float32),
        lax.psum(parted[2].astype(jnp.bfloat16), "group").astype(jnp.float32),
        lax.psum(parted[3].astype(jnp.bfloat16), "group").astype(jnp.float32),
        lax.psum(parted[4].astype(jnp.bfloat16), "group").astype(jnp.float32),
        lax.psum(parted[5].astype(jnp.bfloat16), "group").astype(jnp.float32),
    )
    edge_total = (
        lax.psum(parted[6].astype(jnp.bfloat16), ("section", "group")).astype(jnp.float32),
        lax.psum(parted[7].astype(jnp.bfloat16), ("section", "group")).astype(jnp.float32),
        lax.psum(parted[8].astype(jnp.bfloat16), ("section", "group")).astype(jnp.float32),
        lax.psum(parted[9].astype(jnp.bfloat16), ("section", "group")).astype(jnp.float32),
    )
    token_loss = jnp.concatenate(losses)
    return (
        token_loss,
        edge_total[0],
        edge_total[1],
        layer_total[0],
        layer_total[1],
        layer_total[2],
        layer_total[3],
        layer_total[4],
        layer_total[5],
        edge_total[2],
        edge_total[3],
    )


MESH = pl.DeviceIdType.MESH
ANYWHERE = pl.BlockSpec(memory_space=pl.ANY)


def pick(index, values):
    out = values[-1]
    for at in range(len(values) - 2, -1, -1):
        out = jnp.where(index == at, values[at], out)
    return out


def rows_at(start, size):
    return pl.ds(pl.multiple_of(start, 8), size)


def remote(src, dst, send_sem, recv_sem, device):
    return pltpu.make_async_remote_copy(
        src_ref=src,
        dst_ref=dst,
        send_sem=send_sem,
        recv_sem=recv_sem,
        device_id=device,
        device_id_type=MESH,
    )


def gather_kernel(count, first_order, last_order, *refs):
    shards = refs[:count]
    wholes = refs[count : 2 * count]
    own_sem, zsend, zrecv, psend, precv, gate = refs[2 * count : 2 * count + 6]
    stage = refs[2 * count + 6 :]
    sec = lax.axis_index("section")
    grp = lax.axis_index("group")
    pos = lax.axis_index("dp")
    beside = ((sec, grp ^ 1, pos), (sec, grp ^ 2, pos))
    above = (sec, grp, pos + 1)
    below = (sec, grp, pos - 1)
    partner = (1 - sec, grp, pos)
    barrier = pltpu.get_barrier_semaphore()
    both = bool(last_order)

    def greet(device):
        pl.semaphore_signal(barrier, inc=1, device_id=device, device_id_type=MESH)

    def meet():
        for device in beside + ((partner,) if both else ()):
            greet(device)

        @pl.when(pos > 0)
        def _():
            greet(below)

        @pl.when(pos < 3)
        def _():
            greet(above)

        at_end = (pos == 0) | (pos == 3)
        pl.semaphore_wait(barrier, jnp.where(at_end, 3, 4) + (1 if both else 0))

    turn = [pick(pos, v) for v in ((3, 1, 3, 1), (2, 3, 1, 2), (1, 2, 2, 3))]

    def run(order, before, middle):
        def rows_of(slot):
            return shards[order[slot][0]].shape[0]

        def part_of(slot):
            _, _, size, whole_line = order[slot]
            return size if whole_line else size // 4

        def shift(slot, who):
            _, lo, _, whole_line = order[slot]
            return lo if whole_line else lo + who * part_of(slot)

        def block(slot, origin, who):
            return rows_at(origin * rows_of(slot) + shift(slot, who), part_of(slot))

        staged = sorted({entry[0] for entry in order})

        def load_own(idx):
            return pltpu.make_async_copy(shards[idx], stage[idx], own_sem.at[idx])

        def store_own(idx):
            rows = shards[idx].shape[0]
            return pltpu.make_async_copy(
                stage[idx], wholes[idx].at[rows_at(pos * rows, rows)], own_sem.at[idx]
            )

        def own_ends(slot):
            idx = order[slot][0]
            src = shards[idx].at[rows_at(shift(slot, grp), part_of(slot))]
            dst = wholes[idx].at[block(slot, pos, grp)]
            return (
                (pos < 3, remote(src, dst, zsend.at[slot, 0], zrecv.at[slot, 1], above)),
                (pos > 0, remote(src, dst, zsend.at[slot, 1], zrecv.at[slot, 3], below)),
            )

        def start_own(slot):
            for goes, copy in own_ends(slot):
                pl.when(goes)(copy.start)

        def origin_of(j):
            return lax.rem(pos - turn[j] + 4, 4)

        def arrived(slot, j):
            here = wholes[order[slot][0]].at[block(slot, origin_of(j), grp)]
            return remote(here, here, zsend.at[slot, 2 + j], zrecv.at[slot, turn[j]], partner)

        def onward(slot, j):
            step = jnp.where(turn[j] <= pos, 1, -1)
            to = pos + step
            here = wholes[order[slot][0]].at[block(slot, origin_of(j), grp)]
            landed = jnp.clip(turn[j] + step, 0, 3)
            copy = remote(
                here,
                here,
                zsend.at[slot, 2 + j],
                zrecv.at[slot, landed],
                (sec, grp, jnp.clip(to, 0, 3)),
            )
            return (to >= 0) & (to <= 3), copy

        def plane(slot, j, way):
            idx = order[slot][0]
            origin = origin_of(j)
            if way < 2:
                here = wholes[idx].at[block(slot, origin, grp)]
                return remote(here, here, psend.at[slot, j, way], precv.at[slot, j, way], beside[way])
            half = shards[idx].shape[1] // 2
            there = wholes[idx].at[
                block(slot, origin, grp ^ (way - 1)), pl.ds(half * (way - 2), half)
            ]
            return remote(
                there, there, psend.at[slot, j, way], precv.at[slot, j, way], beside[3 - way]
            )

        items = [(slot, j) for j in range(3) for slot in range(len(order))]
        crossing = [item for item in items if not order[item[0]][3]]

        def first(slot, j):
            arrived(slot, j).wait_recv()
            goes, copy = onward(slot, j)
            pl.when(goes)(copy.start)
            if (slot, j) in crossing:
                plane(slot, j, 0).start()
                plane(slot, j, 1).start()

        def second(slot, j):
            if (slot, j) in crossing:
                for way in (0, 1):
                    plane(slot, j, way).wait_recv()
                    plane(slot, j, way + 2).start()

        if before is not None:
            before()
        for slot in range(len(order)):
            start_own(slot)
        for idx in staged:
            load_own(idx).start()
        lag = 4
        for at in range(len(items) + lag):
            if at < len(items):
                slot, j = items[at]
                if j == 1 and slot < len(staged):
                    load_own(staged[slot]).wait()
                    store_own(staged[slot]).start()
                first(slot, j)
            if at == len(items) - 1 and middle is not None:
                middle()
            if at >= lag:
                second(*items[at - lag])
        for slot, j in crossing:
            plane(slot, j, 2).wait_recv()
            plane(slot, j, 3).wait_recv()
        for idx in staged:
            store_own(idx).wait()
        for slot in range(len(order)):
            for goes, copy in own_ends(slot):
                pl.when(goes)(copy.wait_send)
        for slot, j in items:
            goes, copy = onward(slot, j)
            pl.when(goes)(copy.wait_send)
        for slot, j in crossing:
            for way in range(4):
                plane(slot, j, way).wait_send()

    def let_go():
        pl.semaphore_signal(gate, inc=1, device_id=partner, device_id_type=MESH)

    def hold():
        pl.semaphore_wait(gate, 1)

    if both:
        meet()

        @pl.when(sec == 0)
        def _():
            run(first_order, None, let_go)

        @pl.when(sec == 1)
        def _():
            run(last_order, hold, None)

    else:

        @pl.when(sec == 0)
        def _():
            meet()
            run(first_order, None, None)


def gather_all(shards, first_order, last_order, collective_id):
    count = len(shards)
    slots = max(len(first_order), len(last_order))
    return pl.pallas_call(
        functools.partial(gather_kernel, count, first_order, last_order),
        out_shape=[jax.ShapeDtypeStruct((s.shape[0] * 4, s.shape[1]), s.dtype) for s in shards],
        in_specs=[ANYWHERE] * count,
        out_specs=[ANYWHERE] * count,
        scratch_shapes=[
            pltpu.SemaphoreType.DMA((count,)),
            pltpu.SemaphoreType.DMA((slots, 5)),
            pltpu.SemaphoreType.DMA((slots, 4)),
            pltpu.SemaphoreType.DMA((slots, 3, 4)),
            pltpu.SemaphoreType.DMA((slots, 3, 4)),
            pltpu.SemaphoreType.REGULAR,
        ]
        + [pltpu.VMEM(s.shape, s.dtype) for s in shards],
        compiler_params=pltpu.CompilerParams(
            collective_id=collective_id, has_side_effects=True, vmem_limit_bytes=60 << 20
        ),
    )(*shards)


def swap_kernel(rows_ref, ids_ref, out_ref, ids_out, own_sem, send_sem, recv_sem):
    sec = lax.axis_index("section")
    grp = lax.axis_index("group")
    pos = lax.axis_index("dp")

    @pl.when(sec == 0)
    def _():
        barrier = pltpu.get_barrier_semaphore()
        peers = [(sec, grp, lax.rem(pos + k, 4)) for k in (1, 2, 3)]
        sides = [(sec, grp ^ j, pos) for j in (1, 2, 3)]
        for device in peers + sides:
            pl.semaphore_signal(barrier, inc=1, device_id=device, device_id_type=MESH)
        pl.semaphore_wait(barrier, 6)
        copies = []
        for k, device in enumerate(peers):
            copies.append(
                remote(rows_ref.at[device[2]], out_ref.at[pos], send_sem.at[k], recv_sem.at[k], device)
            )
        for k, device in enumerate(sides):
            copies.append(
                remote(ids_ref, ids_out.at[grp], send_sem.at[3 + k], recv_sem.at[3 + k], device)
            )
        for copy in copies:
            copy.start()
        own_rows = pltpu.make_async_copy(rows_ref.at[pos], out_ref.at[pos], own_sem.at[0])
        own_ids = pltpu.make_async_copy(ids_ref, ids_out.at[grp], own_sem.at[1])
        own_rows.start()
        own_ids.start()
        own_rows.wait()
        own_ids.wait()
        for copy in copies:
            copy.wait()


def swap_rows(rows, ids, collective_id):
    in_vmem = pl.BlockSpec(memory_space=pltpu.VMEM)
    return pl.pallas_call(
        swap_kernel,
        out_shape=[
            jax.ShapeDtypeStruct(rows.shape, rows.dtype),
            jax.ShapeDtypeStruct((4,) + ids.shape, ids.dtype),
        ],
        in_specs=[in_vmem] * 2,
        out_specs=[in_vmem] * 2,
        scratch_shapes=[
            pltpu.SemaphoreType.DMA((2,)),
            pltpu.SemaphoreType.DMA((6,)),
            pltpu.SemaphoreType.DMA((6,)),
        ],
        compiler_params=pltpu.CompilerParams(collective_id=collective_id, has_side_effects=True),
    )(rows, ids)


IN_VMEM = pl.BlockSpec(memory_space=pltpu.VMEM)
IN_SMEM = pl.BlockSpec(memory_space=pltpu.SMEM)
ROOT_HALF = 0.7071067811865476
ROOT_TWO_PI = 0.3989422804014327


def dot_nn(left, right):
    return lax.dot_general(
        left, right, (((1,), (0,)), ((), ())), preferred_element_type=jnp.float32
    )


def dot_nt(left, right):
    return lax.dot_general(
        left, right, (((1,), (1,)), ((), ())), preferred_element_type=jnp.float32
    )


def dot_tn(left, right):
    return lax.dot_general(
        left, right, (((0,), (0,)), ((), ())), preferred_element_type=jnp.float32
    )


def unit_rows(v):
    center = v - jnp.mean(v, -1, keepdims=True)
    scale = lax.rsqrt(jnp.mean(center * center, -1, keepdims=True) + EPS)
    return center * scale, scale


def split_heads(pair):
    low = lax.broadcasted_iota(jnp.int32, pair.shape, 1) < HEAD
    nothing = jnp.zeros_like(pair)
    return jnp.concatenate([jnp.where(low, pair, nothing), jnp.where(low, nothing, pair)], 0)


def join_heads(stacked):
    half = stacked.shape[0] // 2
    low = lax.broadcasted_iota(jnp.int32, (half, stacked.shape[1]), 1) < HEAD
    return jnp.where(low, stacked[:half], stacked[half:])


def pair_scores(keys, stacked_queries, key_count):
    scores = dot_nt(keys, stacked_queries) * 0.125
    valid = lax.broadcasted_iota(jnp.int32, scores.shape, 0) < key_count
    return jnp.where(valid, scores, MASKED)


STRIP = 64


def forward_kernel(only, tile, given, *refs):
    x, gain_attn, gain_mlp, counts, gain_final, wo, wq, wp, wu, wd = refs[:10]
    rest = refs[10 + given :]
    outs = rest[:KEPT_COUNT]
    last = rest[KEPT_COUNT : KEPT_COUNT + 1 + only]
    rest = rest[1 + only :]
    qv, pv, uv, dv = rest[KEPT_COUNT : KEPT_COUNT + 4]
    kept = rest[KEPT_COUNT + 4 : 2 * KEPT_COUNT + 4]
    a, att, m, acc, wsem, osem = rest[2 * KEPT_COUNT + 4 :]
    xv, at_t, qkv, lse, att_t, mid, m_t, pre, act_t, out = kept
    rows, width = a.shape
    units = dv.shape[0]

    def store(idx):
        return pltpu.make_async_copy(kept[idx], outs[idx], osem.at[idx])

    def run():
        loads = []

        def load(src, dst):
            copy = pltpu.make_async_copy(src, dst, wsem.at[len(loads)])
            copy.start()
            loads.append(copy)

        for lo in range(0, 3 * width, tile):
            load(wq.at[:, pl.ds(lo, tile)], qv.at[:, pl.ds(lo, tile)])
        load(wp, pv)
        for lo in range(0, units, tile):
            load(wu.at[:, pl.ds(lo, tile)], uv.at[:, pl.ds(lo, tile)])
            load(wd.at[pl.ds(lo, tile)], dv.at[pl.ds(lo, tile)])
        loads = iter(loads)
        for lo in range(0, rows, STRIP):
            here = pl.ds(lo, STRIP)
            xv[here, :] = x[here, :].astype(jnp.float32)
            a[here, :] = (unit_rows(xv[here, :])[0] * gain_attn[...]).astype(jnp.bfloat16)
        store(0).start()
        for lo in range(0, 3 * width, tile):
            next(loads).wait()
            cols = pl.ds(lo, tile)
            qkv[:, cols] = dot_nn(a[...], qv[:, cols]).astype(jnp.bfloat16)
        store(2).start()
        for lo in range(0, width, 256):
            at_t[pl.ds(lo, 256), :] = a[:, pl.ds(lo, 256)].T
        store(1).start()
        pairs = width // 128
        for seq in range(rows // LEN):
            here = pl.ds(seq * LEN, LEN)
            for pair in range(pairs):
                stacked = split_heads(qkv[here, pl.ds(pair * 128, 128)])
                scores = pair_scores(qkv[here, pl.ds(width + pair * 128, 128)], stacked, counts[seq])
                top = jnp.max(scores, 0, keepdims=True)
                power = jnp.exp(scores - top)
                total = jnp.sum(power, 0, keepdims=True)
                lse[seq * pairs + pair] = top + jnp.log(total)
                probs = (power * (1.0 / total)).astype(jnp.bfloat16)
                mixed = dot_tn(probs, qkv[here, pl.ds(2 * width + pair * 128, 128)])
                att[here, pl.ds(pair * 128, 128)] = join_heads(mixed).astype(jnp.bfloat16)
        store(3).start()
        for lo in range(0, width, 256):
            att_t[pl.ds(lo, 256), :] = att[:, pl.ds(lo, 256)].T
        store(4).start()
        next(loads).wait()
        for lo in range(0, width, tile):
            cols = pl.ds(lo, tile)
            mid[:, cols] = xv[:, cols] + dot_nn(att[...], pv[:, cols])
        for lo in range(0, rows, STRIP):
            here = pl.ds(lo, STRIP)
            m[here, :] = (unit_rows(mid[here, :])[0] * gain_mlp[...]).astype(jnp.bfloat16)
        store(5).start()
        acc[...] = mid[...]
        for lo in range(0, units, tile):
            cols = pl.ds(lo, tile)
            next(loads).wait()
            before = dot_nn(m[...], uv[:, cols])
            pre[:, cols] = before
            active = (0.5 * before * (1.0 + lax.erf(before * ROOT_HALF))).astype(jnp.bfloat16)
            act_t[cols, :] = active.T
            next(loads).wait()
            acc[...] += dot_nn(active, dv[cols, :])
        store(7).start()
        store(8).start()
        for lo in range(0, width, 256):
            m_t[pl.ds(lo, 256), :] = m[:, pl.ds(lo, 256)].T
        store(6).start()
        out[...] = acc[...]
        store(9).start()
        if only == 0:
            last[0][...] = acc[...].astype(jnp.bfloat16)
        else:
            for lo in range(0, rows, STRIP):
                here = pl.ds(lo, STRIP)
                last[0][here, :] = (unit_rows(acc[here, :])[0] * gain_final[...]).astype(jnp.bfloat16)
            last[1][...] = dot_nn(last[0][...], wo[...]).astype(jnp.bfloat16)
        for idx in range(KEPT_COUNT):
            store(idx).wait()

    pl.when(lax.axis_index("section") == only)(run)


KEPT_COUNT = 10


def kept_shapes(rows, width, units):
    f32, low = jnp.float32, jnp.bfloat16
    return [
        jax.ShapeDtypeStruct(shape, kind)
        for shape, kind in (
            ((rows, width), f32),
            ((width, rows), low),
            ((rows, 3 * width), low),
            ((rows // LEN * width // 128, 1, 2 * LEN), f32),
            ((width, rows), low),
            ((rows, width), f32),
            ((width, rows), low),
            ((rows, units), f32),
            ((units, rows), low),
            ((rows, width), f32),
        )
    ]


def run_forward(only, x, gain_attn, gain_mlp, counts, gain_final, out_weight, weights, kept):
    wq, wp, wu, wd = weights
    rows, width = x.shape
    units = wd.shape[0]
    tile = 512
    shapes = kept_shapes(rows, width, units)
    low = jnp.bfloat16
    given = 0 if kept is None else KEPT_COUNT
    in_specs = [IN_VMEM] * 3 + [IN_SMEM] + [IN_VMEM, IN_VMEM if only == 1 else ANYWHERE] + [ANYWHERE] * (4 + given)
    extra = [jax.ShapeDtypeStruct((rows, width), low)]
    if only == 1:
        extra.append(jax.ShapeDtypeStruct((rows, out_weight.shape[1]), low))
    return pl.pallas_call(
        functools.partial(forward_kernel, only, tile, given),
        out_shape=shapes + extra,
        in_specs=in_specs,
        out_specs=[ANYWHERE] * KEPT_COUNT + [IN_VMEM] * len(extra),
        input_output_aliases={10 + idx: idx for idx in range(given)},
        scratch_shapes=[pltpu.VMEM(w.shape, w.dtype) for w in weights]
        + [pltpu.VMEM(s.shape, s.dtype) for s in shapes]
        + [
            pltpu.VMEM((rows, width), low),
            pltpu.VMEM((rows, width), low),
            pltpu.VMEM((rows, width), low),
            pltpu.VMEM((rows, width), jnp.float32),
            pltpu.SemaphoreType.DMA((3 * width // tile + 1 + 2 * units // tile,)),
            pltpu.SemaphoreType.DMA((KEPT_COUNT,)),
        ],
        compiler_params=pltpu.CompilerParams(vmem_limit_bytes=56 << 20),
    )(x, gain_attn, gain_mlp, counts, gain_final, out_weight, wq, wp, wu, wd, *(kept or ()))


GRAD_COUNT = 6


def grad_shapes(rows, width, units):
    f32, low = jnp.float32, jnp.bfloat16
    return [
        jax.ShapeDtypeStruct(shape, kind)
        for shape, kind in (
            ((rows, width), low),
            ((rows, units), low),
            ((rows, width), low),
            ((rows, 3 * width), low),
            ((rows, width), low),
            ((8, width), f32),
        )
    ]


def norm_pull(v, gain, upstream):
    unit, scale = unit_rows(v)
    pulled = upstream * gain
    inner = jnp.mean(pulled * unit, -1, keepdims=True)
    grad = (pulled - jnp.mean(pulled, -1, keepdims=True) - unit * inner) * scale
    return grad, jnp.sum(upstream * unit, 0, keepdims=True)


def backward_kernel(only, tile, given, *refs):
    grad_in, gain_attn, gain_mlp, counts, gain_final, wo, out_in = refs[:7]
    x_in, qkv_in, lse_in, mid_in, pre_in, wq, wp, wu, wd = refs[7:16]
    rest = refs[16 + given :]
    outs = rest[:GRAD_COUNT]
    qv, pv, uv, dv = rest[GRAD_COUNT : GRAD_COUNT + 4]
    made = rest[GRAD_COUNT + 4 : 2 * GRAD_COUNT + 4]
    x, qkv, lse, mid, pre, gm, gmid, gatt, gtop, wsem, ksem, osem = rest[2 * GRAD_COUNT + 4 :]
    grad = gtop if only == 1 else grad_in
    gy, gpre, gz, gqkv, gx, gains = made
    rows, width = gm.shape
    units = dv.shape[0]

    def store(idx):
        return pltpu.make_async_copy(made[idx], outs[idx], osem.at[idx])

    def run():
        loads = []

        def load(src, dst):
            copy = pltpu.make_async_copy(src, dst, wsem.at[len(loads)])
            copy.start()
            loads.append(copy)

        kept = [
            pltpu.make_async_copy(src, dst, ksem.at[idx])
            for idx, (src, dst) in enumerate(
                ((pre_in, pre), (mid_in, mid), (qkv_in, qkv), (lse_in, lse), (x_in, x))
            )
        ]
        if only == 1:
            kept.append(pltpu.make_async_copy(out_in, gtop, ksem.at[5]))
            kept[5].start()
        kept[0].start()
        for lo in range(0, units, tile):
            load(wd.at[pl.ds(lo, tile)], dv.at[pl.ds(lo, tile)])
            load(wu.at[:, pl.ds(lo, tile)], uv.at[:, pl.ds(lo, tile)])
        for copy in kept[1:5]:
            copy.start()
        load(wp, pv)
        load(wq, qv)
        loads = iter(loads)
        gains[...] = jnp.zeros_like(gains)
        if only == 1:
            for copy in kept[5:]:
                copy.wait()
            gmid[...] = dot_nt(grad_in[...], wo[...])
            for lo in range(0, rows, STRIP):
                here = pl.ds(lo, STRIP)
                step, gain = norm_pull(gtop[here, :], gain_final[...], gmid[here, :])
                gtop[here, :] = step
                gains[2:3, :] += gain
        gy[...] = grad[...].astype(jnp.bfloat16)
        store(0).start()
        kept[0].wait()
        gm[...] = jnp.zeros_like(gm)
        for lo in range(0, units, tile):
            cols = pl.ds(lo, tile)
            next(loads).wait()
            pulled = dot_nt(gy[...], dv[cols, :])
            before = pre[:, cols]
            slope = 0.5 * (1.0 + lax.erf(before * ROOT_HALF)) + before * (
                ROOT_TWO_PI * jnp.exp(-0.5 * before * before)
            )
            low = (pulled * slope).astype(jnp.bfloat16)
            gpre[:, cols] = low
            next(loads).wait()
            gm[...] += dot_nt(low, uv[:, cols])
        store(1).start()
        kept[1].wait()
        for lo in range(0, rows, STRIP):
            here = pl.ds(lo, STRIP)
            step, gain = norm_pull(mid[here, :], gain_mlp[...], gm[here, :])
            total = grad[here, :].astype(jnp.float32) + step
            gmid[here, :] = total
            gz[here, :] = total.astype(jnp.bfloat16)
            gains[1:2, :] += gain
        store(2).start()
        next(loads).wait()
        gatt[...] = dot_nt(gz[...], pv[...]).astype(jnp.bfloat16)
        kept[2].wait()
        kept[3].wait()
        pairs = width // 128
        for seq in range(rows // LEN):
            here = pl.ds(seq * LEN, LEN)
            for pair in range(pairs):
                own = pl.ds(pair * 128, 128)
                stacked = split_heads(qkv[here, own])
                pulled = split_heads(gatt[here, own])
                keys = qkv[here, pl.ds(width + pair * 128, 128)]
                values = qkv[here, pl.ds(2 * width + pair * 128, 128)]
                probs = jnp.exp(pair_scores(keys, stacked, counts[seq]) - lse[seq * pairs + pair])
                gprobs = dot_nt(values, pulled)
                inner = jnp.sum(probs * gprobs, 0, keepdims=True)
                gscores = (probs * (gprobs - inner)).astype(jnp.bfloat16)
                gqkv[here, own] = (join_heads(dot_tn(gscores, keys)) * 0.125).astype(jnp.bfloat16)
                gqkv[here, pl.ds(width + pair * 128, 128)] = (dot_nn(gscores, stacked) * 0.125).astype(
                    jnp.bfloat16
                )
                gqkv[here, pl.ds(2 * width + pair * 128, 128)] = dot_nn(
                    probs.astype(jnp.bfloat16), pulled
                ).astype(jnp.bfloat16)
        store(3).start()
        next(loads).wait()
        for lo in range(0, width, 256):
            gm[:, pl.ds(lo, 256)] = dot_nt(gqkv[...], qv[pl.ds(lo, 256), :])
        kept[4].wait()
        for lo in range(0, rows, STRIP):
            here = pl.ds(lo, STRIP)
            step, gain = norm_pull(x[here, :], gain_attn[...], gm[here, :])
            gx[here, :] = (gmid[here, :] + step).astype(jnp.bfloat16)
            gains[0:1, :] += gain
        store(4).start()
        store(5).start()
        for idx in range(GRAD_COUNT):
            store(idx).wait()

    pl.when(lax.axis_index("section") == only)(run)


def run_backward(only, grad, gain_attn, gain_mlp, counts, gain_final, out_weight, kept, weights, made):
    wq, wp, wu, wd = weights
    x, _, qkv, lse, _, mid, _, pre, _, out = kept
    rows, width = x.shape
    units = wd.shape[0]
    tile = 512
    shapes = grad_shapes(rows, width, units)
    low, f32 = jnp.bfloat16, jnp.float32
    given = 0 if made is None else GRAD_COUNT
    in_specs = [IN_VMEM] * 3 + [IN_SMEM] + [IN_VMEM, IN_VMEM if only == 1 else ANYWHERE] + [ANYWHERE] * (10 + given)
    return pl.pallas_call(
        functools.partial(backward_kernel, only, tile, given),
        out_shape=shapes,
        in_specs=in_specs,
        out_specs=[ANYWHERE] * GRAD_COUNT,
        input_output_aliases={16 + idx: idx for idx in range(given)},
        scratch_shapes=[pltpu.VMEM(w.shape, w.dtype) for w in weights]
        + [pltpu.VMEM(s.shape, s.dtype) for s in shapes]
        + [pltpu.VMEM(s.shape, s.dtype) for s in (x, qkv, lse, mid, pre)]
        + [
            pltpu.VMEM((rows, width), f32),
            pltpu.VMEM((rows, width), f32),
            pltpu.VMEM((rows, width), low),
            pltpu.VMEM((rows, width), f32),
            pltpu.SemaphoreType.DMA((2 + 2 * units // tile,)),
            pltpu.SemaphoreType.DMA((6,)),
            pltpu.SemaphoreType.DMA((GRAD_COUNT,)),
        ],
        compiler_params=pltpu.CompilerParams(vmem_limit_bytes=56 << 20),
    )(
        grad, gain_attn, gain_mlp, counts, gain_final, out_weight, out, x, qkv, lse, mid, pre, wq, wp, wu, wd, *(made or ())
    )


def vocabulary_kernel(tile, proj, ids, scale, table, gproj_out, loss_out, gtable, *scratch):
    tv, gt, pall, gp, gsend, gin, stat, stats, whole, tsem, gsem, psem, prem, ssem, srem, qsem, qrem = scratch
    rows = proj.shape[0]
    vocab = tv.shape[0]
    count = vocab // tile
    sec = lax.axis_index("section")
    grp = lax.axis_index("group")
    pos = lax.axis_index("dp")
    places = [lax.rem(pos + k, 4) for k in range(4)]
    peers = [(sec, grp, place) for place in places[1:]]
    across = [(1 - sec, grp, place) for place in places]
    barrier = pltpu.get_barrier_semaphore()

    def hand(k):
        return remote(proj, pall.at[pos], psem.at[k], prem.at[k], across[k])

    def back(k):
        return remote(gsend.at[places[k]], gin.at[k], qsem.at[k], qrem.at[k], across[k])

    def greet(devices):
        for device in devices:
            pl.semaphore_signal(barrier, inc=1, device_id=device, device_id_type=MESH)

    def give():
        greet(across)
        pl.semaphore_wait(barrier, 4)
        for k in (2, 1, 3, 0):
            hand(k).start()
        for k in range(4):
            back(k).wait_recv()
        summed = gin[0].astype(jnp.float32)
        for k in (1, 2, 3):
            summed = summed + gin[k].astype(jnp.float32)
        gproj_out[...] = summed.astype(jnp.bfloat16)
        for k in range(4):
            hand(k).wait_send()

    def score():
        load = pltpu.make_async_copy(table, tv, tsem)
        load.start()
        greet(across + peers)
        pl.semaphore_wait(barrier, 7)
        load.wait()
        for k in range(4):
            hand(k).wait_recv()
        line_rows = pall[...].reshape(4 * rows, pall.shape[2])

        def logits_of(at):
            return dot_nt(tv[rows_at(at * tile, tile), :], line_rows)

        def hits_of(at):
            names = lax.broadcasted_iota(jnp.int32, (tile, 4 * rows), 0) + (at * tile + pos * vocab)
            return names == ids[...]

        stat[0:1, :] = jnp.full((1, 4 * rows), MASKED, jnp.float32)
        stat[1:8, :] = jnp.zeros((7, 4 * rows), jnp.float32)

        def measure(at, carry):
            logits = logits_of(at)
            top = stat[0:1, :]
            higher = jnp.maximum(top, jnp.max(logits, 0, keepdims=True))
            stat[1:2, :] = stat[1:2, :] * jnp.exp(top - higher) + jnp.sum(
                jnp.exp(logits - higher), 0, keepdims=True
            )
            stat[2:3, :] += jnp.sum(jnp.where(hits_of(at), logits, 0.0), 0, keepdims=True)
            stat[0:1, :] = higher
            return carry

        lax.fori_loop(0, count, measure, 0)
        second = [
            remote(stat, stats.at[pos], ssem.at[k], srem.at[k], peers[k]) for k in range(3)
        ]
        for copy in second:
            copy.start()
        stats[pos] = stat[...]
        gp[...] = jnp.zeros_like(gp)
        for copy in second:
            copy.wait()
        top = stats[0, 0:1, :]
        for z in (1, 2, 3):
            top = jnp.maximum(top, stats[z, 0:1, :])
        total = jnp.zeros_like(top)
        picked = jnp.zeros_like(top)
        for z in range(4):
            total = total + stats[z, 1:2, :] * jnp.exp(stats[z, 0:1, :] - top)
            picked = picked + stats[z, 2:3, :]
        log_total = top + jnp.log(total)
        whole[...] = jnp.where(scale[...] > 0, log_total - picked, 0.0)
        loss_out[...] = whole[:, pl.ds(pl.multiple_of(pos * rows, 128), rows)]

        def pull(at, carry):
            here = rows_at(at * tile, tile)
            probs = jnp.exp(logits_of(at) - log_total)
            grads = ((probs - jnp.where(hits_of(at), 1.0, 0.0)) * scale[...]).astype(jnp.bfloat16)
            gp[...] += dot_tn(grads, tv[here, :])
            gt[here, :] = dot_nn(grads, line_rows).astype(jnp.bfloat16)
            return carry

        lax.fori_loop(0, count, pull, 0)
        gsend[...] = gp[...].astype(jnp.bfloat16).reshape(gsend.shape)
        for k in (2, 1, 3, 0):
            back(k).start()
        keep = pltpu.make_async_copy(gt, gtable, gsem)
        keep.start()
        for k in range(4):
            back(k).wait_send()
        keep.wait()

    pl.when(sec == 0)(score)
    pl.when(sec == 1)(give)


def run_vocabulary(proj, ids, scale, table, collective_id):
    rows, emb = proj.shape
    low, f32, dma = jnp.bfloat16, jnp.float32, pltpu.SemaphoreType.DMA
    return pl.pallas_call(
        functools.partial(vocabulary_kernel, 1024),
        out_shape=[
            jax.ShapeDtypeStruct((rows, emb), low),
            jax.ShapeDtypeStruct((1, rows), f32),
            jax.ShapeDtypeStruct(table.shape, low),
        ],
        in_specs=[IN_VMEM] * 3 + [ANYWHERE],
        out_specs=[IN_VMEM] * 2 + [ANYWHERE],
        scratch_shapes=[
            pltpu.VMEM(table.shape, low),
            pltpu.VMEM(table.shape, low),
            pltpu.VMEM((4, rows, emb), low),
            pltpu.VMEM((4 * rows, emb), f32),
            pltpu.VMEM((4, rows, emb), low),
            pltpu.VMEM((4, rows, emb), low),
            pltpu.VMEM((8, 4 * rows), f32),
            pltpu.VMEM((4, 8, 4 * rows), f32),
            pltpu.VMEM((1, 4 * rows), f32),
            dma,
            dma,
            dma((4,)),
            dma((4,)),
            dma((3,)),
            dma((3,)),
            dma((4,)),
            dma((4,)),
        ],
        compiler_params=pltpu.CompilerParams(
            collective_id=collective_id, has_side_effects=True, vmem_limit_bytes=60 << 20
        ),
    )(proj, ids, scale, table)


def widen_kernel(count, *refs):
    for src, dst in zip(refs[:count], refs[count:]):
        dst[...] = src[...].astype(jnp.float32)


def widen(arrays):
    steps = 8

    def spec(x):
        return pl.BlockSpec((x.shape[0] // steps, x.shape[1]), lambda at: (at, 0))

    size = sum(x.size for x in arrays)
    return pl.pallas_call(
        functools.partial(widen_kernel, len(arrays)),
        grid=(steps,),
        out_shape=[jax.ShapeDtypeStruct(x.shape, jnp.float32) for x in arrays],
        in_specs=[spec(x) for x in arrays],
        out_specs=[spec(x) for x in arrays],
        cost_estimate=pl.CostEstimate(flops=size, bytes_accessed=6 * size, transcendentals=0),
        compiler_params=pltpu.CompilerParams(vmem_limit_bytes=60 << 20),
    )(*arrays)


def strip_of(rows, columns):
    strip = 16
    while 2 * strip * columns <= 65536 and rows % (2 * strip) == 0:
        strip = 2 * strip
    return strip


def add_rows(store, terms, rows, columns):
    strip = strip_of(rows, columns)

    def body(at, carry):
        here = rows_at(at * strip, strip)
        total = terms[0](here).astype(jnp.float32)
        for term in terms[1:]:
            total = total + term(here).astype(jnp.float32)
        store(here, total)
        return carry

    lax.fori_loop(0, rows // strip, body, 0)


def reduce_kernel(plan, only, extras, pace, refs_of, *refs):
    body = functools.partial(reduce_body, plan, extras, pace, refs_of(refs))
    if only is None:
        body()
    else:
        pl.when(lax.axis_index("section") == only)(body)


def stage_blocks(order):
    left = list(range(1 << len(order)))
    kept = []
    for bit in order:
        left = [r for r in left if not (r >> bit) & 1]
        kept.append(left)
    return kept


def reduce_body(plan, extras, pace, named):
    arrays, outs, shapes = named["arrays"], named["outs"], named["shapes"]
    lefts, rights, made = named["lefts"], named["rights"], named["made"]
    own, got1, got2, got3, got4, land = (
        named[k] for k in ("own", "got1", "got2", "got3", "got4", "land")
    )
    ssem, rsem, own_sem, s4, r4, fin_sem = named["sems"]
    got = (got1, got2, got3, got4)
    count = len(plan)
    sec = lax.axis_index("section")
    grp = lax.axis_index("group")
    pos = lax.axis_index("dp")
    beside = ((sec, grp ^ 1, pos), (sec, grp ^ 2, pos))
    swaps = beside + ((sec, grp, pos ^ 1), (sec, grp, pos ^ 2))
    sides = [(sec, grp ^ j, pos) for j in (1, 2, 3)]
    line_peers = [(sec, grp, lax.rem(pos + k, 4)) for k in (1, 2, 3)]
    steps = [(jg, jz) for jg in range(4) for jz in range(4)][1:]
    kept = [stage_blocks(piece[1]) for piece in plan]

    def other(j):
        return (sec, grp ^ steps[j][0], lax.rem(pos + steps[j][1], 4))

    with_gains = "gains" in extras
    spreads = "spread" in extras
    looked = "looked" in extras
    if with_gains:
        peers = [other(j) for j in range(15)]
    elif looked:
        peers = sides + line_peers
    else:
        peers = [swaps[bit] for bit in sorted(plan[0][1])]
    barrier = pltpu.get_barrier_semaphore()
    for device in peers:
        pl.semaphore_signal(barrier, inc=1, device_id=device, device_id_type=MESH)
    pl.semaphore_wait(barrier, len(peers))

    def rows_of(p):
        return shapes[plan[p][0]][0] // (len(kept[p][0]) // 2)

    def columns_of(p):
        return shapes[plan[p][0]][1]

    def sub_of(p):
        return rows_of(p) // 4 // plan[p][3]

    def block_rows(p, r):
        who = grp ^ (r & 3)
        line = pos ^ (r >> 2) if len(plan[p][1]) == 4 else 0
        start = line * rows_of(p) + who * (rows_of(p) // 4) + plan[p][2] * sub_of(p)
        return rows_at(start, sub_of(p))

    def block(p, r):
        return arrays[plan[p][0]].at[block_rows(p, r)]

    def is_product(p):
        return plan[p][0] in lefts

    def load_factors(src):
        hbm_left, left, hbm_right, right = lefts[src] + rights[src]
        sem = named["factor_sem"]
        return (
            pltpu.make_async_copy(hbm_left, left, sem.at[src, 0]),
            pltpu.make_async_copy(hbm_right, right, sem.at[src, 1]),
        )

    ready = []

    def multiply(p, blocks, store):
        src = plan[p][0]
        left, right = lefts[src][1], rights[src][1]
        if src not in ready:
            for copy in load_factors(src):
                copy.wait()
            ready.append(src)
        rows = jnp.concatenate([left[block_rows(p, r), :] for r in blocks], 0)
        wide = min(columns_of(p), 1024)

        def body(at, carry):
            cols = pl.ds(pl.multiple_of(at * wide, 128), wide)
            total = dot_nn(rows, right[:, cols])
            store(cols, total.reshape(len(blocks), sub_of(p), wide))
            return carry

        lax.fori_loop(0, columns_of(p) // wide, body, 0)

    def spot(p, r):
        return kept[p][0].index(r)

    def swap(p, stage, at):
        bit = plan[p][1][stage]
        r = kept[p][stage][at] | (1 << bit)
        if stage:
            src = own[p].at[spot(p, r)]
        else:
            src = made[p].at[at] if is_product(p) else block(p, r)
        return remote(
            src, got[stage][p].at[at], ssem.at[p, stage, at], rsem.at[p, stage, at], swaps[bit]
        )

    def load_own(p, at):
        return pltpu.make_async_copy(block(p, kept[p][0][at]), own[p].at[at], own_sem.at[p, at])

    def order_of(p, stage):
        places = range(len(kept[p][stage]))
        if stage == len(plan[p][1]) - 1:
            return list(places)
        bit = plan[p][1][stage + 1]
        return sorted(places, key=lambda at: 1 - ((kept[p][stage][at] >> bit) & 1))

    def begin(p):
        if is_product(p):

            def store(cols, total):
                made[p][:, :, cols] = total.astype(jnp.bfloat16)

            multiply(p, [r | (1 << plan[p][1][0]) for r in kept[p][0]], store)
        for at in order_of(p, 0):
            swap(p, 0, at).start()
            if not is_product(p):
                load_own(p, at).start()

    def advance(p, stage):
        if stage == 0 and is_product(p):
            for at in order_of(p, 0):
                swap(p, 0, at).wait_recv()

            def store_sum(cols, total):
                total = total + got1[p][:, :, cols].astype(jnp.float32)
                got1[p][:, :, cols] = total.astype(jnp.bfloat16)

            multiply(p, kept[p][0], store_sum)
            bit = plan[p][1][1]
            for at in order_of(p, 0):
                r = kept[p][0][at]
                if (r >> bit) & 1:
                    swap(p, 1, kept[p][1].index(r ^ (1 << bit))).start()
            return
        for at in order_of(p, stage):
            r = kept[p][stage][at]
            place = spot(p, r)
            if stage == 0:
                load_own(p, at).wait()
            swap(p, stage, at).wait_recv()
            terms = [
                lambda here, place=place: own[p][place, here, :],
                lambda here, at=at: got[stage][p][at, here, :],
            ]
            if stage == len(plan[p][1]) - 1:
                settle(p, terms)
                return

            def store(here, total, place=place):
                own[p][place, here, :] = total.astype(jnp.bfloat16)

            add_rows(store, terms, sub_of(p), columns_of(p))
            bit = plan[p][1][stage + 1]
            if (r >> bit) & 1:
                swap(p, stage + 1, kept[p][stage + 1].index(r ^ (1 << bit))).start()

    def write_out(p, who, at):
        start = who * (rows_of(p) // 4) + plan[p][2] * sub_of(p)
        return pltpu.make_async_copy(
            land[p].at[who], outs[plan[p][0]].at[rows_at(start, sub_of(p))], named["out_sem"].at[p, at]
        )

    def spread(p, way):
        if way < 2:
            here = land[p].at[grp]
            return remote(here, here, s4.at[p, way], r4.at[p, way], beside[way])
        half = columns_of(p) // 2
        there = land[p].at[grp ^ (way - 1), :, pl.ds(half * (way - 2), half)]
        return remote(there, there, s4.at[p, way], r4.at[p, way], beside[3 - way])

    def settle(p, terms):
        mine = grp if spreads else 0

        def store(here, total):
            land[p][mine, here, :] = total.astype(jnp.bfloat16)

        add_rows(store, terms, sub_of(p), columns_of(p))
        if spreads:
            spread(p, 0).start()
            spread(p, 1).start()
        else:
            own_out(p).start()

    def own_out(p):
        return pltpu.make_async_copy(
            land[p].at[0], outs[plan[p][0]].at[rows_at(plan[p][2] * sub_of(p), sub_of(p))], fin_sem.at[p]
        )

    def arrival(p, way):
        who = (grp ^ 1, grp ^ 2)[way]
        return remote(land[p].at[who], land[p].at[who], s4.at[p, way], r4.at[p, way], beside[way])

    def pass_on(p):
        if spreads:
            for way in (0, 1):
                arrival(p, way).wait_recv()
                spread(p, way + 2).start()

    def write_near(p):
        if spreads:
            for at, who in enumerate((grp, grp ^ 1, grp ^ 2)):
                write_out(p, who, at).start()

    def write_far(p):
        if spreads:
            spread(p, 2).wait_recv()
            spread(p, 3).wait_recv()
            write_out(p, grp ^ 3, 3).start()

    if with_gains:
        gain_in, gain_got, sg, rg, gain_sem = named["gain_scratch"]

        def gain_copy(j):
            device = other(j)
            return remote(gain_in.at[device[2]], gain_got.at[j], sg.at[j], rg.at[j], device)

        gain_load = pltpu.make_async_copy(named["gains"], gain_in, gain_sem)
        gain_load.start()

    if looked:
        looks, looks_own, sl, rl, table_fin, tland, tsum = named["look_scratch"]
        ids, look_in, fin_in = named["look_in"]
        vocab_quarter = fin_in.shape[0]
        look_load = pltpu.make_async_copy(look_in, looks.at[grp, pos], looks_own.at[0])
        fin_load = pltpu.make_async_copy(fin_in, table_fin, looks_own.at[1])

        def look_line(k):
            here = looks.at[grp, pos]
            return remote(here, here, sl.at[k], rl.at[k], line_peers[k])

        def look_side(k):
            here = looks.at[grp]
            return remote(here, here, sl.at[3 + k], rl.at[3 + k], sides[k])

        def table_spread(way):
            if way < 2:
                here = tland.at[grp]
                return remote(here, here, sl.at[6 + way], rl.at[6 + way], beside[way])
            half = tland.shape[2] // 2
            there = tland.at[grp ^ (way - 1), :, pl.ds(half * (way - 2), half)]
            return remote(there, there, sl.at[6 + way], rl.at[6 + way], beside[3 - way])

        def table_out(who):
            return pltpu.make_async_copy(
                tland.at[who],
                named["table_out"].at[rows_at(who * vocab_quarter, vocab_quarter)],
                looks_own.at[2 + who],
            )

        def look_begin():
            look_load.start()
            fin_load.start()
            look_load.wait()
            for k in range(3):
                look_line(k).start()

        def look_middle():
            for k in range(3):
                look_line(k).wait_recv()
            for k in range(3):
                look_side(k).start()

        def look_sum():
            for k in range(3):
                look_side(k).wait_recv()
            fin_load.wait()
            base = pos * (4 * vocab_quarter) + grp * vocab_quarter
            tall = 256
            names = lax.broadcasted_iota(jnp.int32, (tall, ids.shape[2]), 0)

            def body(at, carry):
                here = rows_at(at * tall, tall)
                total = table_fin[here, :].astype(jnp.float32)
                for g in range(4):
                    for z in range(4):
                        hit = names + (base + at * tall) == ids[g * 4 + z]
                        total = total + dot_nn(
                            jnp.where(hit, 1.0, 0.0).astype(jnp.bfloat16), looks[g, z]
                        )
                tland[grp, here, :] = total.astype(jnp.bfloat16)
                return carry

            lax.fori_loop(0, vocab_quarter // tall, body, 0)
            table_spread(0).start()
            table_spread(1).start()

        def look_pass():
            for way in (0, 1):
                who = (grp ^ 1, grp ^ 2)[way]
                remote(
                    tland.at[who], tland.at[who], sl.at[6 + way], rl.at[6 + way], beside[way]
                ).wait_recv()
                table_spread(way + 2).start()

        def look_end():
            table_spread(2).wait_recv()
            table_spread(3).wait_recv()
            for who in range(4):
                table_out(who).start()
            for who in range(4):
                table_out(who).wait()
            for k in range(3):
                look_line(k).wait_send()
                look_side(k).wait_send()
            for way in range(4):
                table_spread(way).wait_send()

        def on_first(run):
            pl.when(sec == 0)(run)

    else:

        def on_first(run):
            pass

        look_begin = look_middle = look_sum = look_pass = look_end = None

    ahead, lag, lag_end = pace
    for piece in plan:
        if piece[0] in lefts and piece[0] not in ready:
            ready.append(piece[0])
            for copy in load_factors(piece[0]):
                copy.start()
    ready.clear()
    on_first(look_begin)
    for p in range(min(ahead, count)):
        begin(p)
    if with_gains:
        gain_load.wait()
        for j in range(15):
            gain_copy(j).start()
    delays = [0, lag, 2 * lag, 3 * lag, 3 * lag + lag_end, 3 * lag + 2 * lag_end, 3 * lag + 3 * lag_end]
    for at in range(count + delays[-1]):
        if ahead + at < count:
            begin(ahead + at)
        for stage in range(len(plan[0][1])):
            if 0 <= at - delays[stage] < count:
                advance(at - delays[stage], stage)
        for run, delay in zip((pass_on, write_near, write_far), delays[4:]):
            if 0 <= at - delay < count:
                run(at - delay)
        for when, run in ((1, look_middle), (3, look_sum), (5, look_pass)):
            if at == when * (count + delays[3]) // 6:
                on_first(run)
    if with_gains:
        for j in range(15):
            gain_copy(j).wait_recv()
        total = gain_in[pos]
        for j in range(15):
            total = total + gain_got[j]
        named["gain_out"][...] = total
    on_first(look_end)
    for p in range(count):
        if spreads:
            for at, who in enumerate((grp, grp ^ 1, grp ^ 2, grp ^ 3)):
                write_out(p, who, at).wait()
            for way in range(4):
                spread(p, way).wait_send()
        else:
            own_out(p).wait()
        for stage in range(len(plan[p][1])):
            for at in range(len(kept[p][stage])):
                swap(p, stage, at).wait_send()
    if with_gains:
        for j in range(15):
            gain_copy(j).wait_send()


def reduce_all(arrays, plan, only, collective_id, pace, gains=None, look=None, spread=True):
    low, f32, dma = jnp.bfloat16, jnp.float32, pltpu.SemaphoreType.DMA
    extras = ("spread",) * spread + ("gains",) * (gains is not None) + ("looked",) * (look is not None)
    count = len(plan)
    factors = {src: x for src, x in enumerate(arrays) if isinstance(x, tuple)}
    plain = [x for x in arrays if not isinstance(x, tuple)]
    flat_factors = [part for x in factors.values() for part in x]
    inputs = plain + flat_factors
    sizes = [(x[0].shape[0], x[1].shape[1]) if isinstance(x, tuple) else x.shape for x in arrays]
    lines = 4 if len(plan[0][1]) == 4 else 1
    share = lines if spread else 4 * lines
    outs = [jax.ShapeDtypeStruct((rows // share, columns), low) for rows, columns in sizes]
    out_specs = [ANYWHERE] * len(arrays)
    in_specs = [ANYWHERE] * len(inputs)
    names = ["own", "got1", "got2", "got3", "got4", "land"]
    scratch = {name: [] for name in names}
    for src, _, _, chunks in plan:
        rows, columns = sizes[src][0] // lines, sizes[src][1]
        sub = rows // 4 // chunks
        held = (8, 8, 4, 2, 1) if lines == 4 else (2, 2, 1, 0, 0)
        for name, blocks in zip(names, held + (4 if spread else 1,)):
            shape = (blocks, sub, columns) if blocks else (8, 128)
            scratch[name].append(pltpu.VMEM(shape, low))
    flat = [item for name in names for item in scratch[name]]
    sems = [dma((count, 4, 8))] * 2 + [dma((count, 8))] + [dma((count, 4))] * 2 + [dma((count,))]
    tail = []
    if factors:
        tail += [pltpu.VMEM(x.shape, low) for x in flat_factors] + [dma((len(arrays), 2))]
    if spread:
        tail += [dma((count, 4))]
    if gains is not None:
        inputs.append(gains)
        in_specs.append(ANYWHERE)
        outs.append(jax.ShapeDtypeStruct(gains.shape[1:], f32))
        out_specs.append(IN_VMEM)
        tail += [
            pltpu.VMEM(gains.shape, f32),
            pltpu.VMEM((15,) + gains.shape[1:], f32),
            dma((15,)),
            dma((15,)),
            dma,
        ]
    if look is not None:
        ids, rows_in, fin_in = look
        inputs += [ids, rows_in, fin_in]
        in_specs += [IN_VMEM, ANYWHERE, ANYWHERE]
        quarter, emb = fin_in.shape
        outs.append(jax.ShapeDtypeStruct((4 * quarter, emb), low))
        out_specs.append(ANYWHERE)
        tail += [
            pltpu.VMEM((4, 4) + rows_in.shape, low),
            dma((6,)),
            dma((10,)),
            dma((10,)),
            pltpu.VMEM(fin_in.shape, low),
            pltpu.VMEM((4, quarter, emb), low),
            pltpu.VMEM((8, 128), f32),
        ]

    def refs_of(refs):
        at = 0

        def take(n):
            nonlocal at
            at += n
            return list(refs[at - n : at])

        plain_refs = iter(take(len(plain)))
        named = {"shapes": sizes, "arrays": [None if src in factors else next(plain_refs) for src in range(len(arrays))]}
        pair_refs = take(len(flat_factors))
        if gains is not None:
            named["gains"] = take(1)[0]
        if look is not None:
            named["look_in"] = take(3)
        named["outs"] = take(len(arrays))
        if gains is not None:
            named["gain_out"] = take(1)[0]
        if look is not None:
            named["table_out"] = take(1)[0]
        for name in names:
            named[name] = take(count)
        named["sems"] = take(6)
        pair_bufs = take(len(flat_factors))
        named["lefts"], named["rights"], named["made"] = {}, {}, {}
        for nth, src in enumerate(factors):
            named["lefts"][src] = (pair_refs[2 * nth], pair_bufs[2 * nth])
            named["rights"][src] = (pair_refs[2 * nth + 1], pair_bufs[2 * nth + 1])
        if factors:
            named["factor_sem"] = take(1)[0]
        for p in range(count):
            if plan[p][0] in factors:
                named["made"][p] = named["own"][p]
                named["own"][p] = named["got1"][p]
        if spread:
            named["out_sem"] = take(1)[0]
        if gains is not None:
            named["gain_scratch"] = take(5)
        if look is not None:
            named["look_scratch"] = take(7)
        return named

    return pl.pallas_call(
        functools.partial(reduce_kernel, plan, only, extras, pace, refs_of),
        out_shape=outs,
        in_specs=in_specs,
        out_specs=out_specs,
        scratch_shapes=flat + sems + tail,
        compiler_params=pltpu.CompilerParams(
            collective_id=collective_id, has_side_effects=True, vmem_limit_bytes=60 << 20
        ),
    )(*inputs)


def nothing_like(run):
    return jax.tree.map(lambda a: jnp.zeros(a.shape, a.dtype), jax.eval_shape(run))


def only_on(live, run):
    return lax.cond(live, run, lambda: nothing_like(run))


X_FIRST = (0, 1, 2, 3)
Y_FIRST = (1, 0, 2, 3)
Z_THEN_X = (2, 0, 1, 3)
Z_THEN_Y = (2, 1, 0, 3)
ORDERS = (X_FIRST, Z_THEN_Y, Y_FIRST, Z_THEN_X)
LAYER_PLAN = (
    tuple((0, ORDERS[chunk], chunk, 4) for chunk in range(4))
    + tuple((1, ORDERS[chunk], chunk, 4) for chunk in range(4))
    + tuple((4, ORDERS[chunk], chunk, 4) for chunk in range(4))
    + ((3, Y_FIRST, 0, 2), (3, Z_THEN_X, 1, 2), (2, X_FIRST, 0, 1))
)
TABLE_PLAN = tuple((0, ((0, 1), (1, 0))[chunk % 2], chunk, 4) for chunk in range(4))
LAYER_PACE = (8, 5, 4)
TABLE_PACE = (4, 2, 1)


def after(value, *others):
    return lax.optimization_barrier((value,) + others)[0]


def per_device(
    tokens,
    lengths,
    levels,
    noise_rows,
    embed_table,
    w_in,
    ln_attn,
    w_qkv,
    w_proj,
    ln_mlp,
    w_up,
    w_down,
    ln_final,
    w_out,
):
    sec = lax.axis_index("section")
    pos = lax.axis_index("dp")
    first_section = sec == 0
    last_section = sec == 1
    rows = tokens.shape[0]
    seqs = lengths.shape[0]
    length = rows // seqs
    width = w_out.shape[0] * 4
    emb = w_out.shape[1]
    vocab_part = embed_table.shape[0]
    gains = jnp.concatenate(
        [ln_attn, ln_mlp, ln_final[None], jnp.zeros((13, ln_final.shape[0]), jnp.bfloat16)], 0
    )
    ids = jnp.concatenate(
        [
            tokens.reshape(-1, 128),
            jnp.concatenate([lengths, jnp.zeros((128 - seqs,), jnp.int32)])[None],
            jnp.zeros((7 - rows // 128, 128), jnp.int32),
        ],
        0,
    )
    shards = (w_qkv[0], w_proj[0], w_up[0], w_down[0], w_in, w_out, gains, ids)
    sizes = [s.shape[0] for s in shards]

    def cut(idx, count, whole=False):
        return tuple((idx, at * sizes[idx] // count, sizes[idx] // count, whole) for at in range(count))

    layer = cut(0, 2) + cut(2, 2) + cut(3, 2)
    wholes = gather_all(
        shards,
        cut(7, 1, True) + cut(6, 1, True) + cut(4, 1) + layer + cut(1, 4, True),
        cut(6, 1, True) + layer + cut(5, 1) + cut(1, 4, True),
        0,
    )
    qkv_weight, proj_weight, up_weight, down_weight, in_weight, out_weight, gain_all, line_ids = wholes
    gain_all = gain_all.reshape(4, 16, -1).astype(jnp.float32)
    gain_attn = gain_all[:, 0].reshape(-1)
    gain_mlp = gain_all[:, 1].reshape(-1)
    final_gain = gain_all[:, 2].reshape(-1)
    weights = (qkv_weight, proj_weight, up_weight, down_weight)
    gain_attn = gain_attn[None]
    gain_mlp = gain_mlp[None]
    final_gain = final_gain[None]
    loss_scale = LOSS_GAIN / math.sqrt(rows * lax.axis_size(("group", "dp")))

    def look_up():
        local = line_ids.reshape(4, 8, 128)[:, : rows // 128].reshape(-1) - pos * vocab_part
        hit = local[:, None] == lax.broadcasted_iota(jnp.int32, (1, vocab_part), 1)
        return product(hit.astype(jnp.bfloat16), embed_table).astype(jnp.bfloat16)

    looked_parts = only_on(first_section, look_up).reshape(4, rows, emb)
    looked_parts, all_ids = swap_rows(looked_parts, line_ids, 1)
    all_tokens = all_ids.reshape(16, 8, 128)[:, : rows // 128].reshape(-1)
    noise_level = jnp.exp(LOG_LOW + levels.astype(jnp.float32) * (LOG_SPAN / (LEVELS - 1)))
    scale_in = lax.rsqrt(EMB_VAR + noise_level * noise_level)
    row_level = jnp.repeat(noise_level, length)[:, None]
    row_scale = jnp.repeat(scale_in, length)[:, None]

    def front():
        looked = jnp.sum(looked_parts.astype(jnp.float32), 0)
        mixed_in = ((looked + row_level * noise_rows.astype(jnp.float32)) * row_scale).astype(
            jnp.bfloat16
        )
        return mixed_in, product(mixed_in, in_weight)

    mixed_in, x_first = only_on(first_section, front)
    *kept, out_first = run_forward(
        0, x_first, gain_attn, gain_mlp, lengths, final_gain, out_weight, weights, None
    )
    x_second = passed_along(out_first, "section", 1)
    *kept, final_in, projected = run_forward(
        1, x_second, gain_attn, gain_mlp, lengths, final_gain, out_weight, weights, kept
    )
    line_parts = line_ids.reshape(4, 8, 128)
    line_tokens = line_parts[:, : rows // 128].reshape(1, -1)
    line_counts = line_parts[:, rows // 128, :seqs].reshape(-1, 1)
    line_valid = jnp.arange(length, dtype=jnp.int32)[None, :] < line_counts
    line_scale = jnp.where(line_valid.reshape(1, -1), loss_scale, 0.0)
    grad_proj, entropy, table_g = run_vocabulary(projected, line_tokens, line_scale, embed_table, 2)
    (table_fin,) = reduce_all(
        (table_g,),
        TABLE_PLAN,
        0,
        3,
        TABLE_PACE,
        spread=False,
    )
    made = run_backward(
        1, grad_proj, gain_attn, gain_mlp, lengths, final_gain, out_weight, kept, weights, None
    )
    grad_first = passed_along(after(made[4], table_fin), "section", -1)
    made = run_backward(
        0, grad_first, gain_attn, gain_mlp, lengths, final_gain, out_weight, kept, weights, made
    )
    shape = in_weight.shape

    def front_edge():
        looked_grad = (product_nt(made[4], in_weight) * row_scale).astype(jnp.bfloat16)
        return product_tn(mixed_in, made[4]).astype(jnp.bfloat16), looked_grad

    def back_edge():
        edge = product_tn(final_in, grad_proj).astype(jnp.bfloat16)
        edge = edge.reshape(4, shape[0] // 4, shape[1]).reshape(shape)
        return edge, jnp.zeros((rows, emb), jnp.bfloat16)

    edge_g, looked_grad = lax.cond(first_section, front_edge, back_edge)
    gain_rows = made[5]
    gain_rows = gain_rows.reshape(8, 4, width // 4).transpose(1, 0, 2)

    order = (
        (kept[6], made[1]),
        (kept[8], made[0]),
        edge_g,
        (kept[4], made[2]),
        (kept[1], made[3]),
    )
    up_r, down_r, edge_r, proj_r, qkv_r, gain_r, table_r = reduce_all(
        order,
        LAYER_PLAN,
        None,
        4,
        LAYER_PACE,
        gains=gain_rows,
        look=(all_tokens.reshape(16, 1, rows), looked_grad, table_fin),
    )
    loss_low = after(entropy, gain_r)[0].astype(jnp.bfloat16)
    mine = (table_r, edge_r, gain_r, loss_low)
    theirs = lax.ppermute(mine, "section", [(0, 1), (1, 0)])

    def pair_of(at):
        low = jnp.where(first_section, mine[at], theirs[at])
        high = jnp.where(first_section, theirs[at], mine[at])
        return low, high

    up_r, down_r, proj_r, qkv_r = widen((up_r, down_r, proj_r, qkv_r))
    table_out = pair_of(0)[0].astype(jnp.float32)
    in_r, out_r = pair_of(1)
    final_r = pair_of(2)[1][2]
    token_loss = pair_of(3)[0]
    return (
        token_loss,
        table_out,
        in_r.astype(jnp.float32),
        gain_r[0][None],
        qkv_r[None],
        proj_r[None],
        gain_r[1][None],
        up_r[None],
        down_r[None],
        final_r,
        out_r.astype(jnp.float32).reshape(-1, emb),
    )


def solution(mesh):
    placed = (
        P(("group", "dp")),
        P(("group", "dp")),
        P(("group", "dp")),
        P(("group", "dp"), None),
        P("dp", None),
        P("dp", None),
        P("section", "dp"),
        P("section", "dp", None),
        P("section", "dp", None),
        P("section", "dp"),
        P("section", "dp", None),
        P("section", "dp", None),
        P("dp"),
        P("dp", None),
    )
    fits = (mesh.shape["section"], mesh.shape["group"], mesh.shape["dp"]) == (2, 4, 4)
    return jax.shard_map(
        per_device if fits else per_device_general,
        mesh=mesh,
        in_specs=placed,
        out_specs=(
            P(("group", "dp")),
            P("dp", None),
            P("dp", None),
            P("section", "dp"),
            P("section", "dp", None),
            P("section", "dp", None),
            P("section", "dp"),
            P("section", "dp", None),
            P("section", "dp", None),
            P("dp"),
            P("dp", None),
        ),
        check_vma=False,
    )
```

```python
import functools
import math

import jax
import jax.numpy as jnp
from jax import lax
from jax.experimental import pallas as pl
from jax.experimental.pallas import tpu as pltpu
from jax.sharding import PartitionSpec as P

HEAD = 64
LEVELS = 64
LEN = 128
MB = 2


EPS = 1e-05
LOG_LOW = -2.995732273553991
LOG_SPAN = 2.995732273553991
EMB_VAR = 0.015625
MASKED = -1e30
LOSS_GAIN = 16.0


def passed_along(x, axis, by):
    count = lax.axis_size(axis)
    pairs = [(i, i + by) for i in range(count) if 0 <= i + by < count]
    return lax.ppermute(x, axis, pairs)


def product(left_side, right_side):
    return jnp.dot(left_side, right_side, preferred_element_type=jnp.float32)


def product_tn(left_side, right_side):
    return lax.dot_general(
        left_side, right_side, (((0,), (0,)), ((), ())), preferred_element_type=jnp.float32
    )


def product_nt(left_side, right_side):
    return lax.dot_general(
        left_side, right_side, (((1,), (1,)), ((), ())), preferred_element_type=jnp.float32
    )


def normed(inputs, gain_vec):
    center = inputs - jnp.mean(inputs, -1, keepdims=True)
    return center * lax.rsqrt(jnp.mean(center * center, -1, keepdims=True) + EPS) * gain_vec


def norm_back(inputs, gain_vec, upstream):
    output, pullback = jax.vjp(normed, inputs, gain_vec)
    return pullback(upstream)


def gelu_exact(values_in):
    return jax.nn.gelu(values_in, approximate=False)


def attn_scores(split_rows, key_valid):
    scores = (
        jnp.einsum(
            "qhd,khd->hqk", split_rows[:, 0], split_rows[:, 1], preferred_element_type=jnp.float32
        )
        * 0.125
    )
    return jnp.where(key_valid[None, None, :], scores, MASKED)


def attend(qkv_rows, key_valid):
    length = qkv_rows.shape[0]
    model_width = qkv_rows.shape[1] // 3
    split_rows = qkv_rows.reshape(length, 3, model_width // HEAD, HEAD)
    scores = attn_scores(split_rows, key_valid)
    row_max = jnp.max(scores, -1, keepdims=True)
    log_total = row_max + jnp.log(jnp.sum(jnp.exp(scores - row_max), -1, keepdims=True))
    probs_low = jnp.exp(scores - log_total).astype(jnp.bfloat16)
    mixed_rows = jnp.einsum(
        "hqk,khd->qhd", probs_low, split_rows[:, 2], preferred_element_type=jnp.float32
    )
    return (mixed_rows.reshape(length, model_width).astype(jnp.bfloat16), log_total)


def attend_back(qkv_rows, key_valid, log_total, grad_mixed):
    length = qkv_rows.shape[0]
    model_width = qkv_rows.shape[1] // 3
    head_count = model_width // HEAD
    split_rows = qkv_rows.reshape(length, 3, head_count, HEAD)
    grad_heads = grad_mixed.reshape(length, head_count, HEAD)
    probs_full = jnp.exp(attn_scores(split_rows, key_valid) - log_total)
    grad_values = jnp.einsum(
        "hqk,qhd->khd",
        probs_full.astype(jnp.bfloat16),
        grad_heads,
        preferred_element_type=jnp.float32,
    )
    grad_probs = jnp.einsum(
        "qhd,khd->hqk", grad_heads, split_rows[:, 2], preferred_element_type=jnp.float32
    )
    grad_scores = (
        probs_full * (grad_probs - jnp.sum(grad_probs * probs_full, -1, keepdims=True))
    ).astype(jnp.bfloat16)
    grad_query = (
        jnp.einsum(
            "hqk,khd->qhd", grad_scores, split_rows[:, 1], preferred_element_type=jnp.float32
        )
        * 0.125
    )
    grad_key = (
        jnp.einsum(
            "hqk,qhd->khd", grad_scores, split_rows[:, 0], preferred_element_type=jnp.float32
        )
        * 0.125
    )
    stacked = jnp.stack([grad_query, grad_key, grad_values], 1).reshape(length, 3 * model_width)
    return stacked.astype(jnp.bfloat16)


def layer_forward(hidden, key_valid, weights):
    gain_attn, qkv_weight, proj_weight, gain_mlp, up_weight, down_weight = weights
    normed_in = normed(hidden, gain_attn).astype(jnp.bfloat16)
    qkv_rows = product(normed_in, qkv_weight).astype(jnp.bfloat16)
    mixed_rows, log_total = attend(qkv_rows, key_valid)
    hidden_mid = hidden + product(mixed_rows, proj_weight)
    mlp_in = normed(hidden_mid, gain_mlp).astype(jnp.bfloat16)
    pre_act = product(mlp_in, up_weight)
    activated = gelu_exact(pre_act).astype(jnp.bfloat16)
    hidden_out = hidden_mid + product(activated, down_weight)
    return (
        hidden_out,
        (
            hidden,
            normed_in,
            qkv_rows,
            log_total,
            mixed_rows,
            hidden_mid,
            mlp_in,
            pre_act,
            activated,
        ),
    )


def empty_kept(length, model_width, hidden_units, head_count):
    return (
        jnp.zeros((length, model_width), jnp.float32),
        jnp.zeros((length, model_width), jnp.bfloat16),
        jnp.zeros((length, 3 * model_width), jnp.bfloat16),
        jnp.zeros((head_count, length, 1), jnp.float32),
        jnp.zeros((length, model_width), jnp.bfloat16),
        jnp.zeros((length, model_width), jnp.float32),
        jnp.zeros((length, model_width), jnp.bfloat16),
        jnp.zeros((length, hidden_units), jnp.float32),
        jnp.zeros((length, hidden_units), jnp.bfloat16),
    )


def layer_backward(kept_vals, grad_out, key_valid, weights):
    hidden, normed_in, qkv_rows, log_total, mixed_rows, hidden_mid, mlp_in, pre_act, activated = (
        kept_vals
    )
    gain_attn, qkv_weight, proj_weight, gain_mlp, up_weight, down_weight = weights
    grad_low = grad_out.astype(jnp.bfloat16)
    grad_activated = product_nt(grad_low, down_weight)
    grad_pre = jax.vjp(gelu_exact, pre_act)[1](grad_activated)[0].astype(jnp.bfloat16)
    grad_mlp_in = product_nt(grad_pre, up_weight)
    grad_mid_norm, grad_gain_mlp = norm_back(hidden_mid, gain_mlp, grad_mlp_in)
    grad_mid = grad_out + grad_mid_norm
    grad_mid_low = grad_mid.astype(jnp.bfloat16)
    grad_mixed = product_nt(grad_mid_low, proj_weight).astype(jnp.bfloat16)
    grad_qkv = attend_back(qkv_rows, key_valid, log_total, grad_mixed)
    grad_normed = product_nt(grad_qkv, qkv_weight)
    grad_in_norm, grad_gain_attn = norm_back(hidden, gain_attn, grad_normed)
    records = (activated, grad_low, mlp_in, grad_pre, mixed_rows, grad_mid_low, normed_in, grad_qkv)
    return (grad_mid + grad_in_norm, (grad_gain_attn, grad_gain_mlp), records)


def layer_zero(length, model_width, hidden_units):
    records = (
        jnp.zeros((length, hidden_units), jnp.bfloat16),
        jnp.zeros((length, model_width), jnp.bfloat16),
        jnp.zeros((length, model_width), jnp.bfloat16),
        jnp.zeros((length, hidden_units), jnp.bfloat16),
        jnp.zeros((length, model_width), jnp.bfloat16),
        jnp.zeros((length, model_width), jnp.bfloat16),
        jnp.zeros((length, model_width), jnp.bfloat16),
        jnp.zeros((length, 3 * model_width), jnp.bfloat16),
    )
    gains = (jnp.zeros((model_width,), jnp.float32), jnp.zeros((model_width,), jnp.float32))
    return (jnp.zeros((length, model_width), jnp.float32), gains, records)


def layer_grads(records):
    activated, grad_low, mlp_in, grad_pre, mixed_rows, grad_mid_low, normed_in, grad_qkv = records
    return (
        product_tn(normed_in, grad_qkv),
        product_tn(mixed_rows, grad_mid_low),
        product_tn(mlp_in, grad_pre),
        product_tn(activated, grad_low),
    )


def embed_inputs(token_ids, noise_block, level_id, table_full):
    noise_level = jnp.exp(LOG_LOW + level_id.astype(jnp.float32) * (LOG_SPAN / (LEVELS - 1)))
    scale_in = lax.rsqrt(EMB_VAR + noise_level * noise_level)
    looked = jnp.take(table_full, token_ids, axis=0).astype(jnp.float32)
    mixed_in = ((looked + noise_level * noise_block.astype(jnp.float32)) * scale_in).astype(
        jnp.bfloat16
    )
    return (mixed_in, scale_in)


def embed_backward(token_ids, noise_block, level_id, grad_start, table_full, in_weight):
    mixed_in, scale_in = embed_inputs(token_ids, noise_block, level_id, table_full)
    grad_low = grad_start.astype(jnp.bfloat16)
    grad_looked = product_nt(grad_low, in_weight) * scale_in
    return (mixed_in, grad_low, grad_looked)


def embed_zero(length, model_width, emb_width):
    return (
        jnp.zeros((length, emb_width), jnp.bfloat16),
        jnp.zeros((length, model_width), jnp.bfloat16),
        jnp.zeros((length, emb_width), jnp.float32),
    )


def tail_pass(hidden, token_ids, key_valid, final_gain, out_weight, table_full, loss_scale):
    final_in = normed(hidden, final_gain).astype(jnp.bfloat16)
    projected = product(final_in, out_weight).astype(jnp.bfloat16)
    logits = product_nt(projected, table_full)
    row_max = jnp.max(logits, -1, keepdims=True)
    log_total = row_max + jnp.log(jnp.sum(jnp.exp(logits - row_max), -1, keepdims=True))
    vocab_ids = lax.broadcasted_iota(jnp.int32, logits.shape, 1)
    target_hit = vocab_ids == token_ids[:, None]
    picked = jnp.sum(jnp.where(target_hit, logits, 0.0), -1)
    entropy = jnp.where(key_valid, log_total[:, 0] - picked, 0.0)
    row_scale = jnp.where(key_valid, loss_scale, 0.0)[:, None]
    grad_logits = (
        (jnp.exp(logits - log_total) - target_hit.astype(jnp.float32)) * row_scale
    ).astype(jnp.bfloat16)
    grad_proj = product(grad_logits, table_full).astype(jnp.bfloat16)
    grad_final = product_nt(grad_proj, out_weight)
    grad_hidden, grad_gain = norm_back(hidden, final_gain, grad_final)
    return (grad_hidden, entropy, grad_gain, (grad_logits, projected, final_in, grad_proj))


def tail_zero(length, model_width, emb_width, vocab_rows):
    records = (
        jnp.zeros((length, vocab_rows), jnp.bfloat16),
        jnp.zeros((length, emb_width), jnp.bfloat16),
        jnp.zeros((length, model_width), jnp.bfloat16),
        jnp.zeros((length, emb_width), jnp.bfloat16),
    )
    return (
        jnp.zeros((length, model_width), jnp.float32),
        jnp.zeros((length,), jnp.float32),
        jnp.zeros((model_width,), jnp.float32),
        records,
    )


def edge_grads(tail_records, embed_records, token_ids):
    grad_logits, projected, final_in, grad_proj = tail_records
    mixed_in, grad_low, grad_looked = embed_records
    table_grad = product_tn(grad_logits, projected).at[token_ids].add(grad_looked)
    return (table_grad, product_tn(mixed_in, grad_low), product_tn(final_in, grad_proj))


def joined_rows(record_list):
    return jax.tree.map(lambda *pieces: jnp.concatenate(pieces, 0), *record_list)


def assemble(gain_attn_sum, gain_mlp_sum, layer_set, edge_set, gain_final_sum):
    return (
        gain_attn_sum[None],
        layer_set[0][None],
        layer_set[1][None],
        gain_mlp_sum[None],
        layer_set[2][None],
        layer_set[3][None],
        edge_set[0],
        edge_set[1],
        gain_final_sum,
        edge_set[2],
    )


def per_device_general(
    tokens,
    lengths,
    levels,
    noise_rows,
    embed_table,
    w_in,
    ln_attn,
    w_qkv,
    w_proj,
    ln_mlp,
    w_up,
    w_down,
    ln_final,
    w_out,
):
    gathered = (
        lax.all_gather(embed_table, "dp", axis=0, tiled=True),
        lax.all_gather(w_in, "dp", axis=0, tiled=True),
        lax.all_gather(ln_attn, "dp", axis=1, tiled=True),
        lax.all_gather(w_qkv, "dp", axis=1, tiled=True),
        lax.all_gather(w_proj, "dp", axis=1, tiled=True),
        lax.all_gather(ln_mlp, "dp", axis=1, tiled=True),
        lax.all_gather(w_up, "dp", axis=1, tiled=True),
        lax.all_gather(w_down, "dp", axis=1, tiled=True),
        lax.all_gather(ln_final, "dp", axis=0, tiled=True),
        lax.all_gather(w_out, "dp", axis=0, tiled=True),
    )
    table_full = gathered[0]
    in_weight = gathered[1]
    layer_weights = (
        gathered[2][0].astype(jnp.float32),
        gathered[3][0],
        gathered[4][0],
        gathered[5][0].astype(jnp.float32),
        gathered[6][0],
        gathered[7][0],
    )
    final_gain = gathered[8].astype(jnp.float32)
    out_weight = gathered[9]
    model_width = out_weight.shape[0]
    emb_width = out_weight.shape[1]
    vocab_rows = table_full.shape[0]
    hidden_units = layer_weights[4].shape[1]
    head_count = model_width // HEAD
    section_index = lax.axis_index("section")
    first_section = section_index == 0
    token_grid = tokens.reshape(MB, LEN)
    noise_grid = noise_rows.reshape(MB, LEN, noise_rows.shape[1])
    positions = jnp.arange(LEN, dtype=jnp.int32)
    valid_grid = positions[None, :] < lengths[:, None]
    loss_scale = LOSS_GAIN / math.sqrt(tokens.shape[0] * lax.axis_size(("group", "dp")))
    gain_attn_sum = jnp.zeros((model_width,), jnp.float32)
    gain_mlp_sum = jnp.zeros((model_width,), jnp.float32)
    gain_final_sum = jnp.zeros((model_width,), jnp.float32)
    recv_act = jnp.zeros((LEN, model_width), jnp.bfloat16)
    recv_grad = jnp.zeros((LEN, model_width), jnp.bfloat16)
    zero_rows = jnp.zeros((LEN, model_width), jnp.float32)
    kept_ticks = {}
    layer_recs = {}
    tail_recs = {}
    embed_recs = {}
    losses = []
    for moment in range(MB + 2):
        offset = moment - section_index
        fwd_valid = (offset >= 0) & (offset < MB)
        fwd_index = jnp.clip(offset, 0, MB - 1)
        ids_now = lax.dynamic_index_in_dim(token_grid, fwd_index, 0, False)
        noise_now = lax.dynamic_index_in_dim(noise_grid, fwd_index, 0, False)
        level_now = lax.dynamic_index_in_dim(levels, fwd_index, 0, False)
        valid_now = lax.dynamic_index_in_dim(valid_grid, fwd_index, 0, False)

        def first_input():
            mixed_in, scale_in = embed_inputs(ids_now, noise_now, level_now, table_full)
            return product(mixed_in, in_weight)

        layer_input = lax.cond(first_section, first_input, lambda: recv_act.astype(jnp.float32))
        hidden_out, kept_now = lax.cond(
            fwd_valid,
            lambda: layer_forward(layer_input, valid_now, layer_weights),
            lambda: (zero_rows, empty_kept(LEN, model_width, hidden_units, head_count)),
        )
        kept_ticks[moment] = kept_now
        tail_live = jnp.logical_not(first_section) & fwd_valid
        tail_grad, entropy, final_step, tail_now = lax.cond(
            tail_live,
            lambda: tail_pass(
                hidden_out, ids_now, valid_now, final_gain, out_weight, table_full, loss_scale
            ),
            lambda: tail_zero(LEN, model_width, emb_width, vocab_rows),
        )
        tail_recs[moment] = tail_now
        gain_final_sum = gain_final_sum + final_step
        back_tick = moment - 2
        late_live = 0 <= back_tick < MB
        late_index = min(max(back_tick, 0), MB - 1)
        kept_late = kept_ticks[back_tick] if back_tick >= 0 else kept_now
        kept_back = lax.cond(first_section, lambda: kept_late, lambda: kept_now)
        grad_top = jnp.where(first_section, recv_grad.astype(jnp.float32), tail_grad)
        valid_back = jnp.where(first_section, valid_grid[late_index], valid_now)
        back_live = jnp.where(first_section, late_live, fwd_valid)
        grad_start, gain_pair, layer_now = lax.cond(
            back_live,
            lambda: layer_backward(kept_back, grad_top, valid_back, layer_weights),
            lambda: layer_zero(LEN, model_width, hidden_units),
        )
        layer_recs[moment] = layer_now
        gain_attn_sum = gain_attn_sum + gain_pair[0]
        gain_mlp_sum = gain_mlp_sum + gain_pair[1]
        if late_live:
            embed_now = lax.cond(
                first_section,
                lambda: embed_backward(
                    token_grid[late_index],
                    noise_grid[late_index],
                    levels[late_index],
                    grad_start,
                    table_full,
                    in_weight,
                ),
                lambda: embed_zero(LEN, model_width, emb_width),
            )
        else:
            embed_now = embed_zero(LEN, model_width, emb_width)
        embed_recs[moment] = embed_now
        if moment < MB:
            recv_act = passed_along(hidden_out.astype(jnp.bfloat16), "section", 1)
        if 1 <= moment <= MB:
            entropy_low = entropy.astype(jnp.bfloat16)
            recv_grad, loss_back = passed_along(
                (grad_start.astype(jnp.bfloat16), entropy_low), "section", -1
            )
            losses.append(jnp.where(first_section, loss_back, entropy_low))
    chosen = [
        jax.tree.map(
            lambda early, late: jnp.where(first_section, early, late),
            layer_recs[micro + 2],
            layer_recs[micro + 1],
        )
        for micro in range(MB)
    ]
    all_layer = layer_grads(joined_rows(chosen))
    all_tail = joined_rows([tail_recs[micro + 1] for micro in range(MB)])
    all_embed = joined_rows([embed_recs[micro + 2] for micro in range(MB)])
    all_edge = edge_grads(all_tail, all_embed, tokens)
    grad_pack = assemble(gain_attn_sum, gain_mlp_sum, all_layer, all_edge, gain_final_sum)
    parted = (
        lax.psum_scatter(
            grad_pack[0].astype(jnp.bfloat16), "dp", scatter_dimension=1, tiled=True
        ).astype(jnp.float32),
        lax.psum_scatter(
            grad_pack[1].astype(jnp.bfloat16), "dp", scatter_dimension=1, tiled=True
        ).astype(jnp.float32),
        lax.psum_scatter(
            grad_pack[2].astype(jnp.bfloat16), "dp", scatter_dimension=1, tiled=True
        ).astype(jnp.float32),
        lax.psum_scatter(
            grad_pack[3].astype(jnp.bfloat16), "dp", scatter_dimension=1, tiled=True
        ).astype(jnp.float32),
        lax.psum_scatter(
            grad_pack[4].astype(jnp.bfloat16), "dp", scatter_dimension=1, tiled=True
        ).astype(jnp.float32),
        lax.psum_scatter(
            grad_pack[5].astype(jnp.bfloat16), "dp", scatter_dimension=1, tiled=True
        ).astype(jnp.float32),
        lax.psum_scatter(
            grad_pack[6].astype(jnp.bfloat16), "dp", scatter_dimension=0, tiled=True
        ).astype(jnp.float32),
        lax.psum_scatter(
            grad_pack[7].astype(jnp.bfloat16), "dp", scatter_dimension=0, tiled=True
        ).astype(jnp.float32),
        lax.psum_scatter(
            grad_pack[8].astype(jnp.bfloat16), "dp", scatter_dimension=0, tiled=True
        ).astype(jnp.float32),
        lax.psum_scatter(
            grad_pack[9].astype(jnp.bfloat16), "dp", scatter_dimension=0, tiled=True
        ).astype(jnp.float32),
    )
    layer_total = (
        lax.psum(parted[0].astype(jnp.bfloat16), "group").astype(jnp.float32),
        lax.psum(parted[1].astype(jnp.bfloat16), "group").astype(jnp.float32),
        lax.psum(parted[2].astype(jnp.bfloat16), "group").astype(jnp.float32),
        lax.psum(parted[3].astype(jnp.bfloat16), "group").astype(jnp.float32),
        lax.psum(parted[4].astype(jnp.bfloat16), "group").astype(jnp.float32),
        lax.psum(parted[5].astype(jnp.bfloat16), "group").astype(jnp.float32),
    )
    edge_total = (
        lax.psum(parted[6].astype(jnp.bfloat16), ("section", "group")).astype(jnp.float32),
        lax.psum(parted[7].astype(jnp.bfloat16), ("section", "group")).astype(jnp.float32),
        lax.psum(parted[8].astype(jnp.bfloat16), ("section", "group")).astype(jnp.float32),
        lax.psum(parted[9].astype(jnp.bfloat16), ("section", "group")).astype(jnp.float32),
    )
    token_loss = jnp.concatenate(losses)
    return (
        token_loss,
        edge_total[0],
        edge_total[1],
        layer_total[0],
        layer_total[1],
        layer_total[2],
        layer_total[3],
        layer_total[4],
        layer_total[5],
        edge_total[2],
        edge_total[3],
    )


MESH = pl.DeviceIdType.MESH
ANYWHERE = pl.BlockSpec(memory_space=pl.ANY)


def pick(index, values):
    out = values[-1]
    for at in range(len(values) - 2, -1, -1):
        out = jnp.where(index == at, values[at], out)
    return out


def rows_at(start, size):
    return pl.ds(pl.multiple_of(start, 8), size)


def remote(src, dst, send_sem, recv_sem, device):
    return pltpu.make_async_remote_copy(
        src_ref=src,
        dst_ref=dst,
        send_sem=send_sem,
        recv_sem=recv_sem,
        device_id=device,
        device_id_type=MESH,
    )


def gather_kernel(count, first_order, last_order, *refs):
    shards = refs[:count]
    wholes = refs[count : 2 * count]
    own_sem, zsend, zrecv, psend, precv, gate = refs[2 * count : 2 * count + 6]
    stage = refs[2 * count + 6 :]
    sec = lax.axis_index("section")
    grp = lax.axis_index("group")
    pos = lax.axis_index("dp")
    beside = ((sec, grp ^ 1, pos), (sec, grp ^ 2, pos))
    above = (sec, grp, pos + 1)
    below = (sec, grp, pos - 1)
    partner = (1 - sec, grp, pos)
    barrier = pltpu.get_barrier_semaphore()
    both = bool(last_order)

    def greet(device):
        pl.semaphore_signal(barrier, inc=1, device_id=device, device_id_type=MESH)

    def meet():
        for device in beside + ((partner,) if both else ()):
            greet(device)

        @pl.when(pos > 0)
        def _():
            greet(below)

        @pl.when(pos < 3)
        def _():
            greet(above)

        at_end = (pos == 0) | (pos == 3)
        pl.semaphore_wait(barrier, jnp.where(at_end, 3, 4) + (1 if both else 0))

    turn = [pick(pos, v) for v in ((3, 1, 3, 1), (2, 3, 1, 2), (1, 2, 2, 3))]

    def run(order, before, middle):
        def rows_of(slot):
            return shards[order[slot][0]].shape[0]

        def part_of(slot):
            _, _, size, whole_line = order[slot]
            return size if whole_line else size // 4

        def shift(slot, who):
            _, lo, _, whole_line = order[slot]
            return lo if whole_line else lo + who * part_of(slot)

        def block(slot, origin, who):
            return rows_at(origin * rows_of(slot) + shift(slot, who), part_of(slot))

        staged = sorted({entry[0] for entry in order})

        def load_own(idx):
            return pltpu.make_async_copy(shards[idx], stage[idx], own_sem.at[idx])

        def store_own(idx):
            rows = shards[idx].shape[0]
            return pltpu.make_async_copy(
                stage[idx], wholes[idx].at[rows_at(pos * rows, rows)], own_sem.at[idx]
            )

        def own_ends(slot):
            idx = order[slot][0]
            src = shards[idx].at[rows_at(shift(slot, grp), part_of(slot))]
            dst = wholes[idx].at[block(slot, pos, grp)]
            return (
                (pos < 3, remote(src, dst, zsend.at[slot, 0], zrecv.at[slot, 1], above)),
                (pos > 0, remote(src, dst, zsend.at[slot, 1], zrecv.at[slot, 3], below)),
            )

        def start_own(slot):
            for goes, copy in own_ends(slot):
                pl.when(goes)(copy.start)

        def origin_of(j):
            return lax.rem(pos - turn[j] + 4, 4)

        def arrived(slot, j):
            here = wholes[order[slot][0]].at[block(slot, origin_of(j), grp)]
            return remote(here, here, zsend.at[slot, 2 + j], zrecv.at[slot, turn[j]], partner)

        def onward(slot, j):
            step = jnp.where(turn[j] <= pos, 1, -1)
            to = pos + step
            here = wholes[order[slot][0]].at[block(slot, origin_of(j), grp)]
            landed = jnp.clip(turn[j] + step, 0, 3)
            copy = remote(
                here,
                here,
                zsend.at[slot, 2 + j],
                zrecv.at[slot, landed],
                (sec, grp, jnp.clip(to, 0, 3)),
            )
            return (to >= 0) & (to <= 3), copy

        def plane(slot, j, way):
            idx = order[slot][0]
            origin = origin_of(j)
            if way < 2:
                here = wholes[idx].at[block(slot, origin, grp)]
                return remote(here, here, psend.at[slot, j, way], precv.at[slot, j, way], beside[way])
            half = shards[idx].shape[1] // 2
            there = wholes[idx].at[
                block(slot, origin, grp ^ (way - 1)), pl.ds(half * (way - 2), half)
            ]
            return remote(
                there, there, psend.at[slot, j, way], precv.at[slot, j, way], beside[3 - way]
            )

        items = [(slot, j) for j in range(3) for slot in range(len(order))]
        crossing = [item for item in items if not order[item[0]][3]]

        def first(slot, j):
            arrived(slot, j).wait_recv()
            goes, copy = onward(slot, j)
            pl.when(goes)(copy.start)
            if (slot, j) in crossing:
                plane(slot, j, 0).start()
                plane(slot, j, 1).start()

        def second(slot, j):
            if (slot, j) in crossing:
                for way in (0, 1):
                    plane(slot, j, way).wait_recv()
                    plane(slot, j, way + 2).start()

        if before is not None:
            before()
        for slot in range(len(order)):
            start_own(slot)
        for idx in staged:
            load_own(idx).start()
        lag = 4
        for at in range(len(items) + lag):
            if at < len(items):
                slot, j = items[at]
                if j == 1 and slot < len(staged):
                    load_own(staged[slot]).wait()
                    store_own(staged[slot]).start()
                first(slot, j)
            if at == len(items) - 1 and middle is not None:
                middle()
            if at >= lag:
                second(*items[at - lag])
        for slot, j in crossing:
            plane(slot, j, 2).wait_recv()
            plane(slot, j, 3).wait_recv()
        for idx in staged:
            store_own(idx).wait()
        for slot in range(len(order)):
            for goes, copy in own_ends(slot):
                pl.when(goes)(copy.wait_send)
        for slot, j in items:
            goes, copy = onward(slot, j)
            pl.when(goes)(copy.wait_send)
        for slot, j in crossing:
            for way in range(4):
                plane(slot, j, way).wait_send()

    def let_go():
        pl.semaphore_signal(gate, inc=1, device_id=partner, device_id_type=MESH)

    def hold():
        pl.semaphore_wait(gate, 1)

    if both:
        meet()

        @pl.when(sec == 0)
        def _():
            run(first_order, None, let_go)

        @pl.when(sec == 1)
        def _():
            run(last_order, hold, None)

    else:

        @pl.when(sec == 0)
        def _():
            meet()
            run(first_order, None, None)


def gather_all(shards, first_order, last_order, collective_id):
    count = len(shards)
    slots = max(len(first_order), len(last_order))
    return pl.pallas_call(
        functools.partial(gather_kernel, count, first_order, last_order),
        out_shape=[jax.ShapeDtypeStruct((s.shape[0] * 4, s.shape[1]), s.dtype) for s in shards],
        in_specs=[ANYWHERE] * count,
        out_specs=[ANYWHERE] * count,
        scratch_shapes=[
            pltpu.SemaphoreType.DMA((count,)),
            pltpu.SemaphoreType.DMA((slots, 5)),
            pltpu.SemaphoreType.DMA((slots, 4)),
            pltpu.SemaphoreType.DMA((slots, 3, 4)),
            pltpu.SemaphoreType.DMA((slots, 3, 4)),
            pltpu.SemaphoreType.REGULAR,
        ]
        + [pltpu.VMEM(s.shape, s.dtype) for s in shards],
        compiler_params=pltpu.CompilerParams(
            collective_id=collective_id, has_side_effects=True, vmem_limit_bytes=60 << 20
        ),
    )(*shards)


def swap_kernel(rows_ref, ids_ref, out_ref, ids_out, own_sem, send_sem, recv_sem):
    sec = lax.axis_index("section")
    grp = lax.axis_index("group")
    pos = lax.axis_index("dp")

    @pl.when(sec == 0)
    def _():
        barrier = pltpu.get_barrier_semaphore()
        peers = [(sec, grp, lax.rem(pos + k, 4)) for k in (1, 2, 3)]
        sides = [(sec, grp ^ j, pos) for j in (1, 2, 3)]
        for device in peers + sides:
            pl.semaphore_signal(barrier, inc=1, device_id=device, device_id_type=MESH)
        pl.semaphore_wait(barrier, 6)
        copies = []
        for k, device in enumerate(peers):
            copies.append(
                remote(rows_ref.at[device[2]], out_ref.at[pos], send_sem.at[k], recv_sem.at[k], device)
            )
        for k, device in enumerate(sides):
            copies.append(
                remote(ids_ref, ids_out.at[grp], send_sem.at[3 + k], recv_sem.at[3 + k], device)
            )
        for copy in copies:
            copy.start()
        own_rows = pltpu.make_async_copy(rows_ref.at[pos], out_ref.at[pos], own_sem.at[0])
        own_ids = pltpu.make_async_copy(ids_ref, ids_out.at[grp], own_sem.at[1])
        own_rows.start()
        own_ids.start()
        own_rows.wait()
        own_ids.wait()
        for copy in copies:
            copy.wait()


def swap_rows(rows, ids, collective_id):
    in_vmem = pl.BlockSpec(memory_space=pltpu.VMEM)
    return pl.pallas_call(
        swap_kernel,
        out_shape=[
            jax.ShapeDtypeStruct(rows.shape, rows.dtype),
            jax.ShapeDtypeStruct((4,) + ids.shape, ids.dtype),
        ],
        in_specs=[in_vmem] * 2,
        out_specs=[in_vmem] * 2,
        scratch_shapes=[
            pltpu.SemaphoreType.DMA((2,)),
            pltpu.SemaphoreType.DMA((6,)),
            pltpu.SemaphoreType.DMA((6,)),
        ],
        compiler_params=pltpu.CompilerParams(collective_id=collective_id, has_side_effects=True),
    )(rows, ids)


IN_VMEM = pl.BlockSpec(memory_space=pltpu.VMEM)
IN_SMEM = pl.BlockSpec(memory_space=pltpu.SMEM)
ROOT_HALF = 0.7071067811865476
ROOT_TWO_PI = 0.3989422804014327


def dot_nn(left, right):
    return lax.dot_general(
        left, right, (((1,), (0,)), ((), ())), preferred_element_type=jnp.float32
    )


def dot_nt(left, right):
    return lax.dot_general(
        left, right, (((1,), (1,)), ((), ())), preferred_element_type=jnp.float32
    )


def dot_tn(left, right):
    return lax.dot_general(
        left, right, (((0,), (0,)), ((), ())), preferred_element_type=jnp.float32
    )


def unit_rows(v):
    center = v - jnp.mean(v, -1, keepdims=True)
    scale = lax.rsqrt(jnp.mean(center * center, -1, keepdims=True) + EPS)
    return center * scale, scale


def split_heads(pair):
    low = lax.broadcasted_iota(jnp.int32, pair.shape, 1) < HEAD
    nothing = jnp.zeros_like(pair)
    return jnp.concatenate([jnp.where(low, pair, nothing), jnp.where(low, nothing, pair)], 0)


def join_heads(stacked):
    half = stacked.shape[0] // 2
    low = lax.broadcasted_iota(jnp.int32, (half, stacked.shape[1]), 1) < HEAD
    return jnp.where(low, stacked[:half], stacked[half:])


def pair_scores(keys, stacked_queries, key_count):
    scores = dot_nt(keys, stacked_queries) * 0.125
    valid = lax.broadcasted_iota(jnp.int32, scores.shape, 0) < key_count
    return jnp.where(valid, scores, MASKED)


STRIP = 64


def forward_kernel(only, tile, given, *refs):
    x, gain_attn, gain_mlp, counts, gain_final, wo, wq, wp, wu, wd = refs[:10]
    rest = refs[10 + given :]
    outs = rest[:KEPT_COUNT]
    last = rest[KEPT_COUNT : KEPT_COUNT + 1 + only]
    rest = rest[1 + only :]
    qv, pv, uv, dv = rest[KEPT_COUNT : KEPT_COUNT + 4]
    kept = rest[KEPT_COUNT + 4 : 2 * KEPT_COUNT + 4]
    a, att, m, acc, wsem, osem = rest[2 * KEPT_COUNT + 4 :]
    xv, at_t, qkv, lse, att_t, mid, m_t, pre, act_t, out = kept
    rows, width = a.shape
    units = dv.shape[0]

    def store(idx):
        return pltpu.make_async_copy(kept[idx], outs[idx], osem.at[idx])

    def run():
        loads = []

        def load(src, dst):
            copy = pltpu.make_async_copy(src, dst, wsem.at[len(loads)])
            copy.start()
            loads.append(copy)

        for lo in range(0, 3 * width, tile):
            load(wq.at[:, pl.ds(lo, tile)], qv.at[:, pl.ds(lo, tile)])
        load(wp, pv)
        for lo in range(0, units, tile):
            load(wu.at[:, pl.ds(lo, tile)], uv.at[:, pl.ds(lo, tile)])
            load(wd.at[pl.ds(lo, tile)], dv.at[pl.ds(lo, tile)])
        loads = iter(loads)
        for lo in range(0, rows, STRIP):
            here = pl.ds(lo, STRIP)
            xv[here, :] = x[here, :].astype(jnp.float32)
            a[here, :] = (unit_rows(xv[here, :])[0] * gain_attn[...]).astype(jnp.bfloat16)
        store(0).start()
        for lo in range(0, 3 * width, tile):
            next(loads).wait()
            cols = pl.ds(lo, tile)
            qkv[:, cols] = dot_nn(a[...], qv[:, cols]).astype(jnp.bfloat16)
        store(2).start()
        for lo in range(0, width, 256):
            at_t[pl.ds(lo, 256), :] = a[:, pl.ds(lo, 256)].T
        store(1).start()
        pairs = width // 128
        for seq in range(rows // LEN):
            here = pl.ds(seq * LEN, LEN)
            for pair in range(pairs):
                stacked = split_heads(qkv[here, pl.ds(pair * 128, 128)])
                scores = pair_scores(qkv[here, pl.ds(width + pair * 128, 128)], stacked, counts[seq])
                top = jnp.max(scores, 0, keepdims=True)
                power = jnp.exp(scores - top)
                total = jnp.sum(power, 0, keepdims=True)
                lse[seq * pairs + pair] = top + jnp.log(total)
                probs = (power * (1.0 / total)).astype(jnp.bfloat16)
                mixed = dot_tn(probs, qkv[here, pl.ds(2 * width + pair * 128, 128)])
                att[here, pl.ds(pair * 128, 128)] = join_heads(mixed).astype(jnp.bfloat16)
        store(3).start()
        for lo in range(0, width, 256):
            att_t[pl.ds(lo, 256), :] = att[:, pl.ds(lo, 256)].T
        store(4).start()
        next(loads).wait()
        for lo in range(0, width, tile):
            cols = pl.ds(lo, tile)
            mid[:, cols] = xv[:, cols] + dot_nn(att[...], pv[:, cols])
        for lo in range(0, rows, STRIP):
            here = pl.ds(lo, STRIP)
            m[here, :] = (unit_rows(mid[here, :])[0] * gain_mlp[...]).astype(jnp.bfloat16)
        store(5).start()
        acc[...] = mid[...]
        for lo in range(0, units, tile):
            cols = pl.ds(lo, tile)
            next(loads).wait()
            before = dot_nn(m[...], uv[:, cols])
            pre[:, cols] = before
            active = (0.5 * before * (1.0 + lax.erf(before * ROOT_HALF))).astype(jnp.bfloat16)
            act_t[cols, :] = active.T
            next(loads).wait()
            acc[...] += dot_nn(active, dv[cols, :])
        store(7).start()
        store(8).start()
        for lo in range(0, width, 256):
            m_t[pl.ds(lo, 256), :] = m[:, pl.ds(lo, 256)].T
        store(6).start()
        out[...] = acc[...]
        store(9).start()
        if only == 0:
            last[0][...] = acc[...].astype(jnp.bfloat16)
        else:
            for lo in range(0, rows, STRIP):
                here = pl.ds(lo, STRIP)
                last[0][here, :] = (unit_rows(acc[here, :])[0] * gain_final[...]).astype(jnp.bfloat16)
            last[1][...] = dot_nn(last[0][...], wo[...]).astype(jnp.bfloat16)
        for idx in range(KEPT_COUNT):
            store(idx).wait()

    pl.when(lax.axis_index("section") == only)(run)


KEPT_COUNT = 10


def kept_shapes(rows, width, units):
    f32, low = jnp.float32, jnp.bfloat16
    return [
        jax.ShapeDtypeStruct(shape, kind)
        for shape, kind in (
            ((rows, width), f32),
            ((width, rows), low),
            ((rows, 3 * width), low),
            ((rows // LEN * width // 128, 1, 2 * LEN), f32),
            ((width, rows), low),
            ((rows, width), f32),
            ((width, rows), low),
            ((rows, units), f32),
            ((units, rows), low),
            ((rows, width), f32),
        )
    ]


def run_forward(only, x, gain_attn, gain_mlp, counts, gain_final, out_weight, weights, kept):
    wq, wp, wu, wd = weights
    rows, width = x.shape
    units = wd.shape[0]
    tile = 512
    shapes = kept_shapes(rows, width, units)
    low = jnp.bfloat16
    given = 0 if kept is None else KEPT_COUNT
    in_specs = [IN_VMEM] * 3 + [IN_SMEM] + [IN_VMEM, IN_VMEM if only == 1 else ANYWHERE] + [ANYWHERE] * (4 + given)
    extra = [jax.ShapeDtypeStruct((rows, width), low)]
    if only == 1:
        extra.append(jax.ShapeDtypeStruct((rows, out_weight.shape[1]), low))
    return pl.pallas_call(
        functools.partial(forward_kernel, only, tile, given),
        out_shape=shapes + extra,
        in_specs=in_specs,
        out_specs=[ANYWHERE] * KEPT_COUNT + [IN_VMEM] * len(extra),
        input_output_aliases={10 + idx: idx for idx in range(given)},
        scratch_shapes=[pltpu.VMEM(w.shape, w.dtype) for w in weights]
        + [pltpu.VMEM(s.shape, s.dtype) for s in shapes]
        + [
            pltpu.VMEM((rows, width), low),
            pltpu.VMEM((rows, width), low),
            pltpu.VMEM((rows, width), low),
            pltpu.VMEM((rows, width), jnp.float32),
            pltpu.SemaphoreType.DMA((3 * width // tile + 1 + 2 * units // tile,)),
            pltpu.SemaphoreType.DMA((KEPT_COUNT,)),
        ],
        compiler_params=pltpu.CompilerParams(vmem_limit_bytes=56 << 20),
    )(x, gain_attn, gain_mlp, counts, gain_final, out_weight, wq, wp, wu, wd, *(kept or ()))


GRAD_COUNT = 6


def grad_shapes(rows, width, units):
    f32, low = jnp.float32, jnp.bfloat16
    return [
        jax.ShapeDtypeStruct(shape, kind)
        for shape, kind in (
            ((rows, width), low),
            ((rows, units), low),
            ((rows, width), low),
            ((rows, 3 * width), low),
            ((rows, width), low),
            ((8, width), f32),
        )
    ]


def norm_pull(v, gain, upstream):
    unit, scale = unit_rows(v)
    pulled = upstream * gain
    inner = jnp.mean(pulled * unit, -1, keepdims=True)
    grad = (pulled - jnp.mean(pulled, -1, keepdims=True) - unit * inner) * scale
    return grad, jnp.sum(upstream * unit, 0, keepdims=True)


def backward_kernel(only, tile, given, *refs):
    grad_in, gain_attn, gain_mlp, counts, gain_final, wo, out_in = refs[:7]
    x_in, qkv_in, lse_in, mid_in, pre_in, wq, wp, wu, wd = refs[7:16]
    rest = refs[16 + given :]
    outs = rest[:GRAD_COUNT]
    qv, pv, uv, dv = rest[GRAD_COUNT : GRAD_COUNT + 4]
    made = rest[GRAD_COUNT + 4 : 2 * GRAD_COUNT + 4]
    x, qkv, lse, mid, pre, gm, gmid, gatt, gtop, wsem, ksem, osem = rest[2 * GRAD_COUNT + 4 :]
    grad = gtop if only == 1 else grad_in
    gy, gpre, gz, gqkv, gx, gains = made
    rows, width = gm.shape
    units = dv.shape[0]

    def store(idx):
        return pltpu.make_async_copy(made[idx], outs[idx], osem.at[idx])

    def run():
        loads = []

        def load(src, dst):
            copy = pltpu.make_async_copy(src, dst, wsem.at[len(loads)])
            copy.start()
            loads.append(copy)

        kept = [
            pltpu.make_async_copy(src, dst, ksem.at[idx])
            for idx, (src, dst) in enumerate(
                ((pre_in, pre), (mid_in, mid), (qkv_in, qkv), (lse_in, lse), (x_in, x))
            )
        ]
        if only == 1:
            kept.append(pltpu.make_async_copy(out_in, gtop, ksem.at[5]))
            kept[5].start()
        kept[0].start()
        for lo in range(0, units, tile):
            load(wd.at[pl.ds(lo, tile)], dv.at[pl.ds(lo, tile)])
            load(wu.at[:, pl.ds(lo, tile)], uv.at[:, pl.ds(lo, tile)])
        for copy in kept[1:5]:
            copy.start()
        load(wp, pv)
        load(wq, qv)
        loads = iter(loads)
        gains[...] = jnp.zeros_like(gains)
        if only == 1:
            for copy in kept[5:]:
                copy.wait()
            gmid[...] = dot_nt(grad_in[...], wo[...])
            for lo in range(0, rows, STRIP):
                here = pl.ds(lo, STRIP)
                step, gain = norm_pull(gtop[here, :], gain_final[...], gmid[here, :])
                gtop[here, :] = step
                gains[2:3, :] += gain
        gy[...] = grad[...].astype(jnp.bfloat16)
        store(0).start()
        kept[0].wait()
        gm[...] = jnp.zeros_like(gm)
        for lo in range(0, units, tile):
            cols = pl.ds(lo, tile)
            next(loads).wait()
            pulled = dot_nt(gy[...], dv[cols, :])
            before = pre[:, cols]
            slope = 0.5 * (1.0 + lax.erf(before * ROOT_HALF)) + before * (
                ROOT_TWO_PI * jnp.exp(-0.5 * before * before)
            )
            low = (pulled * slope).astype(jnp.bfloat16)
            gpre[:, cols] = low
            next(loads).wait()
            gm[...] += dot_nt(low, uv[:, cols])
        store(1).start()
        kept[1].wait()
        for lo in range(0, rows, STRIP):
            here = pl.ds(lo, STRIP)
            step, gain = norm_pull(mid[here, :], gain_mlp[...], gm[here, :])
            total = grad[here, :].astype(jnp.float32) + step
            gmid[here, :] = total
            gz[here, :] = total.astype(jnp.bfloat16)
            gains[1:2, :] += gain
        store(2).start()
        next(loads).wait()
        gatt[...] = dot_nt(gz[...], pv[...]).astype(jnp.bfloat16)
        kept[2].wait()
        kept[3].wait()
        pairs = width // 128
        for seq in range(rows // LEN):
            here = pl.ds(seq * LEN, LEN)
            for pair in range(pairs):
                own = pl.ds(pair * 128, 128)
                stacked = split_heads(qkv[here, own])
                pulled = split_heads(gatt[here, own])
                keys = qkv[here, pl.ds(width + pair * 128, 128)]
                values = qkv[here, pl.ds(2 * width + pair * 128, 128)]
                probs = jnp.exp(pair_scores(keys, stacked, counts[seq]) - lse[seq * pairs + pair])
                gprobs = dot_nt(values, pulled)
                inner = jnp.sum(probs * gprobs, 0, keepdims=True)
                gscores = (probs * (gprobs - inner)).astype(jnp.bfloat16)
                gqkv[here, own] = (join_heads(dot_tn(gscores, keys)) * 0.125).astype(jnp.bfloat16)
                gqkv[here, pl.ds(width + pair * 128, 128)] = (dot_nn(gscores, stacked) * 0.125).astype(
                    jnp.bfloat16
                )
                gqkv[here, pl.ds(2 * width + pair * 128, 128)] = dot_nn(
                    probs.astype(jnp.bfloat16), pulled
                ).astype(jnp.bfloat16)
        store(3).start()
        next(loads).wait()
        for lo in range(0, width, 256):
            gm[:, pl.ds(lo, 256)] = dot_nt(gqkv[...], qv[pl.ds(lo, 256), :])
        kept[4].wait()
        for lo in range(0, rows, STRIP):
            here = pl.ds(lo, STRIP)
            step, gain = norm_pull(x[here, :], gain_attn[...], gm[here, :])
            gx[here, :] = (gmid[here, :] + step).astype(jnp.bfloat16)
            gains[0:1, :] += gain
        store(4).start()
        store(5).start()
        for idx in range(GRAD_COUNT):
            store(idx).wait()

    pl.when(lax.axis_index("section") == only)(run)


def run_backward(only, grad, gain_attn, gain_mlp, counts, gain_final, out_weight, kept, weights, made):
    wq, wp, wu, wd = weights
    x, _, qkv, lse, _, mid, _, pre, _, out = kept
    rows, width = x.shape
    units = wd.shape[0]
    tile = 512
    shapes = grad_shapes(rows, width, units)
    low, f32 = jnp.bfloat16, jnp.float32
    given = 0 if made is None else GRAD_COUNT
    in_specs = [IN_VMEM] * 3 + [IN_SMEM] + [IN_VMEM, IN_VMEM if only == 1 else ANYWHERE] + [ANYWHERE] * (10 + given)
    return pl.pallas_call(
        functools.partial(backward_kernel, only, tile, given),
        out_shape=shapes,
        in_specs=in_specs,
        out_specs=[ANYWHERE] * GRAD_COUNT,
        input_output_aliases={16 + idx: idx for idx in range(given)},
        scratch_shapes=[pltpu.VMEM(w.shape, w.dtype) for w in weights]
        + [pltpu.VMEM(s.shape, s.dtype) for s in shapes]
        + [pltpu.VMEM(s.shape, s.dtype) for s in (x, qkv, lse, mid, pre)]
        + [
            pltpu.VMEM((rows, width), f32),
            pltpu.VMEM((rows, width), f32),
            pltpu.VMEM((rows, width), low),
            pltpu.VMEM((rows, width), f32),
            pltpu.SemaphoreType.DMA((2 + 2 * units // tile,)),
            pltpu.SemaphoreType.DMA((6,)),
            pltpu.SemaphoreType.DMA((GRAD_COUNT,)),
        ],
        compiler_params=pltpu.CompilerParams(vmem_limit_bytes=56 << 20),
    )(
        grad, gain_attn, gain_mlp, counts, gain_final, out_weight, out, x, qkv, lse, mid, pre, wq, wp, wu, wd, *(made or ())
    )


def vocabulary_kernel(tile, proj, ids, scale, table, gproj_out, loss_out, gtable, *scratch):
    tv, gt, pall, gp, gsend, gin, stat, stats, whole, tsem, gsem, psem, prem, ssem, srem, qsem, qrem = scratch
    rows = proj.shape[0]
    vocab = tv.shape[0]
    count = vocab // tile
    sec = lax.axis_index("section")
    grp = lax.axis_index("group")
    pos = lax.axis_index("dp")
    places = [lax.rem(pos + k, 4) for k in range(4)]
    peers = [(sec, grp, place) for place in places[1:]]
    across = [(1 - sec, grp, place) for place in places]
    barrier = pltpu.get_barrier_semaphore()

    def hand(k):
        return remote(proj, pall.at[pos], psem.at[k], prem.at[k], across[k])

    def back(k):
        return remote(gsend.at[places[k]], gin.at[k], qsem.at[k], qrem.at[k], across[k])

    def greet(devices):
        for device in devices:
            pl.semaphore_signal(barrier, inc=1, device_id=device, device_id_type=MESH)

    def give():
        greet(across)
        pl.semaphore_wait(barrier, 4)
        for k in (2, 1, 3, 0):
            hand(k).start()
        for k in range(4):
            back(k).wait_recv()
        summed = gin[0].astype(jnp.float32)
        for k in (1, 2, 3):
            summed = summed + gin[k].astype(jnp.float32)
        gproj_out[...] = summed.astype(jnp.bfloat16)
        for k in range(4):
            hand(k).wait_send()

    def score():
        load = pltpu.make_async_copy(table, tv, tsem)
        load.start()
        greet(across + peers)
        pl.semaphore_wait(barrier, 7)
        load.wait()
        for k in range(4):
            hand(k).wait_recv()
        line_rows = pall[...].reshape(4 * rows, pall.shape[2])

        def logits_of(at):
            return dot_nt(tv[rows_at(at * tile, tile), :], line_rows)

        def hits_of(at):
            names = lax.broadcasted_iota(jnp.int32, (tile, 4 * rows), 0) + (at * tile + pos * vocab)
            return names == ids[...]

        stat[0:1, :] = jnp.full((1, 4 * rows), MASKED, jnp.float32)
        stat[1:8, :] = jnp.zeros((7, 4 * rows), jnp.float32)

        def measure(at, carry):
            logits = logits_of(at)
            top = stat[0:1, :]
            higher = jnp.maximum(top, jnp.max(logits, 0, keepdims=True))
            stat[1:2, :] = stat[1:2, :] * jnp.exp(top - higher) + jnp.sum(
                jnp.exp(logits - higher), 0, keepdims=True
            )
            stat[2:3, :] += jnp.sum(jnp.where(hits_of(at), logits, 0.0), 0, keepdims=True)
            stat[0:1, :] = higher
            return carry

        lax.fori_loop(0, count, measure, 0)
        second = [
            remote(stat, stats.at[pos], ssem.at[k], srem.at[k], peers[k]) for k in range(3)
        ]
        for copy in second:
            copy.start()
        stats[pos] = stat[...]
        gp[...] = jnp.zeros_like(gp)
        for copy in second:
            copy.wait()
        top = stats[0, 0:1, :]
        for z in (1, 2, 3):
            top = jnp.maximum(top, stats[z, 0:1, :])
        total = jnp.zeros_like(top)
        picked = jnp.zeros_like(top)
        for z in range(4):
            total = total + stats[z, 1:2, :] * jnp.exp(stats[z, 0:1, :] - top)
            picked = picked + stats[z, 2:3, :]
        log_total = top + jnp.log(total)
        whole[...] = jnp.where(scale[...] > 0, log_total - picked, 0.0)
        loss_out[...] = whole[:, pl.ds(pl.multiple_of(pos * rows, 128), rows)]

        def pull(at, carry):
            here = rows_at(at * tile, tile)
            probs = jnp.exp(logits_of(at) - log_total)
            grads = ((probs - jnp.where(hits_of(at), 1.0, 0.0)) * scale[...]).astype(jnp.bfloat16)
            gp[...] += dot_tn(grads, tv[here, :])
            gt[here, :] = dot_nn(grads, line_rows).astype(jnp.bfloat16)
            return carry

        lax.fori_loop(0, count, pull, 0)
        gsend[...] = gp[...].astype(jnp.bfloat16).reshape(gsend.shape)
        for k in (2, 1, 3, 0):
            back(k).start()
        keep = pltpu.make_async_copy(gt, gtable, gsem)
        keep.start()
        for k in range(4):
            back(k).wait_send()
        keep.wait()

    pl.when(sec == 0)(score)
    pl.when(sec == 1)(give)


def run_vocabulary(proj, ids, scale, table, collective_id):
    rows, emb = proj.shape
    low, f32, dma = jnp.bfloat16, jnp.float32, pltpu.SemaphoreType.DMA
    return pl.pallas_call(
        functools.partial(vocabulary_kernel, 1024),
        out_shape=[
            jax.ShapeDtypeStruct((rows, emb), low),
            jax.ShapeDtypeStruct((1, rows), f32),
            jax.ShapeDtypeStruct(table.shape, low),
        ],
        in_specs=[IN_VMEM] * 3 + [ANYWHERE],
        out_specs=[IN_VMEM] * 2 + [ANYWHERE],
        scratch_shapes=[
            pltpu.VMEM(table.shape, low),
            pltpu.VMEM(table.shape, low),
            pltpu.VMEM((4, rows, emb), low),
            pltpu.VMEM((4 * rows, emb), f32),
            pltpu.VMEM((4, rows, emb), low),
            pltpu.VMEM((4, rows, emb), low),
            pltpu.VMEM((8, 4 * rows), f32),
            pltpu.VMEM((4, 8, 4 * rows), f32),
            pltpu.VMEM((1, 4 * rows), f32),
            dma,
            dma,
            dma((4,)),
            dma((4,)),
            dma((3,)),
            dma((3,)),
            dma((4,)),
            dma((4,)),
        ],
        compiler_params=pltpu.CompilerParams(
            collective_id=collective_id, has_side_effects=True, vmem_limit_bytes=60 << 20
        ),
    )(proj, ids, scale, table)


def widen_kernel(count, *refs):
    for src, dst in zip(refs[:count], refs[count:]):
        dst[...] = src[...].astype(jnp.float32)


def widen(arrays):
    steps = 8

    def spec(x):
        return pl.BlockSpec((x.shape[0] // steps, x.shape[1]), lambda at: (at, 0))

    size = sum(x.size for x in arrays)
    return pl.pallas_call(
        functools.partial(widen_kernel, len(arrays)),
        grid=(steps,),
        out_shape=[jax.ShapeDtypeStruct(x.shape, jnp.float32) for x in arrays],
        in_specs=[spec(x) for x in arrays],
        out_specs=[spec(x) for x in arrays],
        cost_estimate=pl.CostEstimate(flops=size, bytes_accessed=6 * size, transcendentals=0),
        compiler_params=pltpu.CompilerParams(vmem_limit_bytes=60 << 20),
    )(*arrays)


def strip_of(rows, columns):
    strip = 16
    while 2 * strip * columns <= 65536 and rows % (2 * strip) == 0:
        strip = 2 * strip
    return strip


def add_rows(store, terms, rows, columns):
    strip = strip_of(rows, columns)

    def body(at, carry):
        here = rows_at(at * strip, strip)
        total = terms[0](here).astype(jnp.float32)
        for term in terms[1:]:
            total = total + term(here).astype(jnp.float32)
        store(here, total)
        return carry

    lax.fori_loop(0, rows // strip, body, 0)


def reduce_kernel(plan, only, extras, pace, refs_of, *refs):
    body = functools.partial(reduce_body, plan, extras, pace, refs_of(refs))
    if only is None:
        body()
    else:
        pl.when(lax.axis_index("section") == only)(body)


def stage_blocks(order):
    left = list(range(1 << len(order)))
    kept = []
    for bit in order:
        left = [r for r in left if not (r >> bit) & 1]
        kept.append(left)
    return kept


def reduce_body(plan, extras, pace, named):
    arrays, outs, shapes = named["arrays"], named["outs"], named["shapes"]
    lefts, rights, made = named["lefts"], named["rights"], named["made"]
    own, got1, got2, got3, got4, land = (
        named[k] for k in ("own", "got1", "got2", "got3", "got4", "land")
    )
    ssem, rsem, own_sem, s4, r4, fin_sem = named["sems"]
    got = (got1, got2, got3, got4)
    count = len(plan)
    sec = lax.axis_index("section")
    grp = lax.axis_index("group")
    pos = lax.axis_index("dp")
    beside = ((sec, grp ^ 1, pos), (sec, grp ^ 2, pos))
    swaps = beside + ((sec, grp, pos ^ 1), (sec, grp, pos ^ 2))
    sides = [(sec, grp ^ j, pos) for j in (1, 2, 3)]
    line_peers = [(sec, grp, lax.rem(pos + k, 4)) for k in (1, 2, 3)]
    steps = [(jg, jz) for jg in range(4) for jz in range(4)][1:]
    kept = [stage_blocks(piece[1]) for piece in plan]

    def other(j):
        return (sec, grp ^ steps[j][0], lax.rem(pos + steps[j][1], 4))

    with_gains = "gains" in extras
    spreads = "spread" in extras
    looked = "looked" in extras
    if with_gains:
        peers = [other(j) for j in range(15)]
    elif looked:
        peers = sides + line_peers
    else:
        peers = [swaps[bit] for bit in sorted(plan[0][1])]
    barrier = pltpu.get_barrier_semaphore()
    for device in peers:
        pl.semaphore_signal(barrier, inc=1, device_id=device, device_id_type=MESH)
    pl.semaphore_wait(barrier, len(peers))

    def rows_of(p):
        return shapes[plan[p][0]][0] // (len(kept[p][0]) // 2)

    def columns_of(p):
        return shapes[plan[p][0]][1]

    def sub_of(p):
        return rows_of(p) // 4 // plan[p][3]

    def block_rows(p, r):
        who = grp ^ (r & 3)
        line = pos ^ (r >> 2) if len(plan[p][1]) == 4 else 0
        start = line * rows_of(p) + who * (rows_of(p) // 4) + plan[p][2] * sub_of(p)
        return rows_at(start, sub_of(p))

    def block(p, r):
        return arrays[plan[p][0]].at[block_rows(p, r)]

    def is_product(p):
        return plan[p][0] in lefts

    def load_factors(src):
        hbm_left, left, hbm_right, right = lefts[src] + rights[src]
        sem = named["factor_sem"]
        return (
            pltpu.make_async_copy(hbm_left, left, sem.at[src, 0]),
            pltpu.make_async_copy(hbm_right, right, sem.at[src, 1]),
        )

    ready = []

    def multiply(p, blocks, store):
        src = plan[p][0]
        left, right = lefts[src][1], rights[src][1]
        if src not in ready:
            for copy in load_factors(src):
                copy.wait()
            ready.append(src)
        rows = jnp.concatenate([left[block_rows(p, r), :] for r in blocks], 0)
        wide = min(columns_of(p), 1024)

        def body(at, carry):
            cols = pl.ds(pl.multiple_of(at * wide, 128), wide)
            total = dot_nn(rows, right[:, cols])
            store(cols, total.reshape(len(blocks), sub_of(p), wide))
            return carry

        lax.fori_loop(0, columns_of(p) // wide, body, 0)

    def spot(p, r):
        return kept[p][0].index(r)

    def swap(p, stage, at):
        bit = plan[p][1][stage]
        r = kept[p][stage][at] | (1 << bit)
        if stage:
            src = own[p].at[spot(p, r)]
        else:
            src = made[p].at[at] if is_product(p) else block(p, r)
        return remote(
            src, got[stage][p].at[at], ssem.at[p, stage, at], rsem.at[p, stage, at], swaps[bit]
        )

    def load_own(p, at):
        return pltpu.make_async_copy(block(p, kept[p][0][at]), own[p].at[at], own_sem.at[p, at])

    def order_of(p, stage):
        places = range(len(kept[p][stage]))
        if stage == len(plan[p][1]) - 1:
            return list(places)
        bit = plan[p][1][stage + 1]
        return sorted(places, key=lambda at: 1 - ((kept[p][stage][at] >> bit) & 1))

    def begin(p):
        if is_product(p):

            def store(cols, total):
                made[p][:, :, cols] = total.astype(jnp.bfloat16)

            multiply(p, [r | (1 << plan[p][1][0]) for r in kept[p][0]], store)
        for at in order_of(p, 0):
            swap(p, 0, at).start()
            if not is_product(p):
                load_own(p, at).start()

    def advance(p, stage):
        if stage == 0 and is_product(p):
            for at in order_of(p, 0):
                swap(p, 0, at).wait_recv()

            def store_sum(cols, total):
                total = total + got1[p][:, :, cols].astype(jnp.float32)
                got1[p][:, :, cols] = total.astype(jnp.bfloat16)

            multiply(p, kept[p][0], store_sum)
            bit = plan[p][1][1]
            for at in order_of(p, 0):
                r = kept[p][0][at]
                if (r >> bit) & 1:
                    swap(p, 1, kept[p][1].index(r ^ (1 << bit))).start()
            return
        for at in order_of(p, stage):
            r = kept[p][stage][at]
            place = spot(p, r)
            if stage == 0:
                load_own(p, at).wait()
            swap(p, stage, at).wait_recv()
            terms = [
                lambda here, place=place: own[p][place, here, :],
                lambda here, at=at: got[stage][p][at, here, :],
            ]
            if stage == len(plan[p][1]) - 1:
                settle(p, terms)
                return

            def store(here, total, place=place):
                own[p][place, here, :] = total.astype(jnp.bfloat16)

            add_rows(store, terms, sub_of(p), columns_of(p))
            bit = plan[p][1][stage + 1]
            if (r >> bit) & 1:
                swap(p, stage + 1, kept[p][stage + 1].index(r ^ (1 << bit))).start()

    def write_out(p, who, at):
        start = who * (rows_of(p) // 4) + plan[p][2] * sub_of(p)
        return pltpu.make_async_copy(
            land[p].at[who], outs[plan[p][0]].at[rows_at(start, sub_of(p))], named["out_sem"].at[p, at]
        )

    def spread(p, way):
        if way < 2:
            here = land[p].at[grp]
            return remote(here, here, s4.at[p, way], r4.at[p, way], beside[way])
        half = columns_of(p) // 2
        there = land[p].at[grp ^ (way - 1), :, pl.ds(half * (way - 2), half)]
        return remote(there, there, s4.at[p, way], r4.at[p, way], beside[3 - way])

    def settle(p, terms):
        mine = grp if spreads else 0

        def store(here, total):
            land[p][mine, here, :] = total.astype(jnp.bfloat16)

        add_rows(store, terms, sub_of(p), columns_of(p))
        if spreads:
            spread(p, 0).start()
            spread(p, 1).start()
        else:
            own_out(p).start()

    def own_out(p):
        return pltpu.make_async_copy(
            land[p].at[0], outs[plan[p][0]].at[rows_at(plan[p][2] * sub_of(p), sub_of(p))], fin_sem.at[p]
        )

    def arrival(p, way):
        who = (grp ^ 1, grp ^ 2)[way]
        return remote(land[p].at[who], land[p].at[who], s4.at[p, way], r4.at[p, way], beside[way])

    def pass_on(p):
        if spreads:
            for way in (0, 1):
                arrival(p, way).wait_recv()
                spread(p, way + 2).start()

    def write_near(p):
        if spreads:
            for at, who in enumerate((grp, grp ^ 1, grp ^ 2)):
                write_out(p, who, at).start()

    def write_far(p):
        if spreads:
            spread(p, 2).wait_recv()
            spread(p, 3).wait_recv()
            write_out(p, grp ^ 3, 3).start()

    if with_gains:
        gain_in, gain_got, sg, rg, gain_sem = named["gain_scratch"]

        def gain_copy(j):
            device = other(j)
            return remote(gain_in.at[device[2]], gain_got.at[j], sg.at[j], rg.at[j], device)

        gain_load = pltpu.make_async_copy(named["gains"], gain_in, gain_sem)
        gain_load.start()

    if looked:
        looks, looks_own, sl, rl, table_fin, tland, tsum = named["look_scratch"]
        ids, look_in, fin_in = named["look_in"]
        vocab_quarter = fin_in.shape[0]
        look_load = pltpu.make_async_copy(look_in, looks.at[grp, pos], looks_own.at[0])
        fin_load = pltpu.make_async_copy(fin_in, table_fin, looks_own.at[1])

        def look_line(k):
            here = looks.at[grp, pos]
            return remote(here, here, sl.at[k], rl.at[k], line_peers[k])

        def look_side(k):
            here = looks.at[grp]
            return remote(here, here, sl.at[3 + k], rl.at[3 + k], sides[k])

        def table_spread(way):
            if way < 2:
                here = tland.at[grp]
                return remote(here, here, sl.at[6 + way], rl.at[6 + way], beside[way])
            half = tland.shape[2] // 2
            there = tland.at[grp ^ (way - 1), :, pl.ds(half * (way - 2), half)]
            return remote(there, there, sl.at[6 + way], rl.at[6 + way], beside[3 - way])

        def table_out(who):
            return pltpu.make_async_copy(
                tland.at[who],
                named["table_out"].at[rows_at(who * vocab_quarter, vocab_quarter)],
                looks_own.at[2 + who],
            )

        def look_begin():
            look_load.start()
            fin_load.start()
            look_load.wait()
            for k in range(3):
                look_line(k).start()

        def look_middle():
            for k in range(3):
                look_line(k).wait_recv()
            for k in range(3):
                look_side(k).start()

        def look_sum():
            for k in range(3):
                look_side(k).wait_recv()
            fin_load.wait()
            base = pos * (4 * vocab_quarter) + grp * vocab_quarter
            tall = 256
            names = lax.broadcasted_iota(jnp.int32, (tall, ids.shape[2]), 0)

            def body(at, carry):
                here = rows_at(at * tall, tall)
                total = table_fin[here, :].astype(jnp.float32)
                for g in range(4):
                    for z in range(4):
                        hit = names + (base + at * tall) == ids[g * 4 + z]
                        total = total + dot_nn(
                            jnp.where(hit, 1.0, 0.0).astype(jnp.bfloat16), looks[g, z]
                        )
                tland[grp, here, :] = total.astype(jnp.bfloat16)
                return carry

            lax.fori_loop(0, vocab_quarter // tall, body, 0)
            table_spread(0).start()
            table_spread(1).start()

        def look_pass():
            for way in (0, 1):
                who = (grp ^ 1, grp ^ 2)[way]
                remote(
                    tland.at[who], tland.at[who], sl.at[6 + way], rl.at[6 + way], beside[way]
                ).wait_recv()
                table_spread(way + 2).start()

        def look_end():
            table_spread(2).wait_recv()
            table_spread(3).wait_recv()
            for who in range(4):
                table_out(who).start()
            for who in range(4):
                table_out(who).wait()
            for k in range(3):
                look_line(k).wait_send()
                look_side(k).wait_send()
            for way in range(4):
                table_spread(way).wait_send()

        def on_first(run):
            pl.when(sec == 0)(run)

    else:

        def on_first(run):
            pass

        look_begin = look_middle = look_sum = look_pass = look_end = None

    ahead, lag, lag_end = pace
    for piece in plan:
        if piece[0] in lefts and piece[0] not in ready:
            ready.append(piece[0])
            for copy in load_factors(piece[0]):
                copy.start()
    ready.clear()
    on_first(look_begin)
    for p in range(min(ahead, count)):
        begin(p)
    if with_gains:
        gain_load.wait()
        for j in range(15):
            gain_copy(j).start()
    delays = [0, lag, 2 * lag, 3 * lag, 3 * lag + lag_end, 3 * lag + 2 * lag_end, 3 * lag + 3 * lag_end]
    for at in range(count + delays[-1]):
        if ahead + at < count:
            begin(ahead + at)
        for stage in range(len(plan[0][1])):
            if 0 <= at - delays[stage] < count:
                advance(at - delays[stage], stage)
        for run, delay in zip((pass_on, write_near, write_far), delays[4:]):
            if 0 <= at - delay < count:
                run(at - delay)
        for when, run in ((1, look_middle), (3, look_sum), (5, look_pass)):
            if at == when * (count + delays[3]) // 6:
                on_first(run)
    if with_gains:
        for j in range(15):
            gain_copy(j).wait_recv()
        total = gain_in[pos]
        for j in range(15):
            total = total + gain_got[j]
        named["gain_out"][...] = total
    on_first(look_end)
    for p in range(count):
        if spreads:
            for at, who in enumerate((grp, grp ^ 1, grp ^ 2, grp ^ 3)):
                write_out(p, who, at).wait()
            for way in range(4):
                spread(p, way).wait_send()
        else:
            own_out(p).wait()
        for stage in range(len(plan[p][1])):
            for at in range(len(kept[p][stage])):
                swap(p, stage, at).wait_send()
    if with_gains:
        for j in range(15):
            gain_copy(j).wait_send()


def reduce_all(arrays, plan, only, collective_id, pace, gains=None, look=None, spread=True):
    low, f32, dma = jnp.bfloat16, jnp.float32, pltpu.SemaphoreType.DMA
    extras = ("spread",) * spread + ("gains",) * (gains is not None) + ("looked",) * (look is not None)
    count = len(plan)
    factors = {src: x for src, x in enumerate(arrays) if isinstance(x, tuple)}
    plain = [x for x in arrays if not isinstance(x, tuple)]
    flat_factors = [part for x in factors.values() for part in x]
    inputs = plain + flat_factors
    sizes = [(x[0].shape[0], x[1].shape[1]) if isinstance(x, tuple) else x.shape for x in arrays]
    lines = 4 if len(plan[0][1]) == 4 else 1
    share = lines if spread else 4 * lines
    outs = [jax.ShapeDtypeStruct((rows // share, columns), low) for rows, columns in sizes]
    out_specs = [ANYWHERE] * len(arrays)
    in_specs = [ANYWHERE] * len(inputs)
    names = ["own", "got1", "got2", "got3", "got4", "land"]
    scratch = {name: [] for name in names}
    for src, _, _, chunks in plan:
        rows, columns = sizes[src][0] // lines, sizes[src][1]
        sub = rows // 4 // chunks
        held = (8, 8, 4, 2, 1) if lines == 4 else (2, 2, 1, 0, 0)
        for name, blocks in zip(names, held + (4 if spread else 1,)):
            shape = (blocks, sub, columns) if blocks else (8, 128)
            scratch[name].append(pltpu.VMEM(shape, low))
    flat = [item for name in names for item in scratch[name]]
    sems = [dma((count, 4, 8))] * 2 + [dma((count, 8))] + [dma((count, 4))] * 2 + [dma((count,))]
    tail = []
    if factors:
        tail += [pltpu.VMEM(x.shape, low) for x in flat_factors] + [dma((len(arrays), 2))]
    if spread:
        tail += [dma((count, 4))]
    if gains is not None:
        inputs.append(gains)
        in_specs.append(ANYWHERE)
        outs.append(jax.ShapeDtypeStruct(gains.shape[1:], f32))
        out_specs.append(IN_VMEM)
        tail += [
            pltpu.VMEM(gains.shape, f32),
            pltpu.VMEM((15,) + gains.shape[1:], f32),
            dma((15,)),
            dma((15,)),
            dma,
        ]
    if look is not None:
        ids, rows_in, fin_in = look
        inputs += [ids, rows_in, fin_in]
        in_specs += [IN_VMEM, ANYWHERE, ANYWHERE]
        quarter, emb = fin_in.shape
        outs.append(jax.ShapeDtypeStruct((4 * quarter, emb), low))
        out_specs.append(ANYWHERE)
        tail += [
            pltpu.VMEM((4, 4) + rows_in.shape, low),
            dma((6,)),
            dma((10,)),
            dma((10,)),
            pltpu.VMEM(fin_in.shape, low),
            pltpu.VMEM((4, quarter, emb), low),
            pltpu.VMEM((8, 128), f32),
        ]

    def refs_of(refs):
        at = 0

        def take(n):
            nonlocal at
            at += n
            return list(refs[at - n : at])

        plain_refs = iter(take(len(plain)))
        named = {"shapes": sizes, "arrays": [None if src in factors else next(plain_refs) for src in range(len(arrays))]}
        pair_refs = take(len(flat_factors))
        if gains is not None:
            named["gains"] = take(1)[0]
        if look is not None:
            named["look_in"] = take(3)
        named["outs"] = take(len(arrays))
        if gains is not None:
            named["gain_out"] = take(1)[0]
        if look is not None:
            named["table_out"] = take(1)[0]
        for name in names:
            named[name] = take(count)
        named["sems"] = take(6)
        pair_bufs = take(len(flat_factors))
        named["lefts"], named["rights"], named["made"] = {}, {}, {}
        for nth, src in enumerate(factors):
            named["lefts"][src] = (pair_refs[2 * nth], pair_bufs[2 * nth])
            named["rights"][src] = (pair_refs[2 * nth + 1], pair_bufs[2 * nth + 1])
        if factors:
            named["factor_sem"] = take(1)[0]
        for p in range(count):
            if plan[p][0] in factors:
                named["made"][p] = named["own"][p]
                named["own"][p] = named["got1"][p]
        if spread:
            named["out_sem"] = take(1)[0]
        if gains is not None:
            named["gain_scratch"] = take(5)
        if look is not None:
            named["look_scratch"] = take(7)
        return named

    return pl.pallas_call(
        functools.partial(reduce_kernel, plan, only, extras, pace, refs_of),
        out_shape=outs,
        in_specs=in_specs,
        out_specs=out_specs,
        scratch_shapes=flat + sems + tail,
        compiler_params=pltpu.CompilerParams(
            collective_id=collective_id, has_side_effects=True, vmem_limit_bytes=60 << 20
        ),
    )(*inputs)


def nothing_like(run):
    return jax.tree.map(lambda a: jnp.zeros(a.shape, a.dtype), jax.eval_shape(run))


def only_on(live, run):
    return lax.cond(live, run, lambda: nothing_like(run))


X_FIRST = (0, 1, 2, 3)
Y_FIRST = (1, 0, 2, 3)
Z_THEN_X = (2, 0, 1, 3)
Z_THEN_Y = (2, 1, 0, 3)
ORDERS = (X_FIRST, Z_THEN_Y, Y_FIRST, Z_THEN_X)
LAYER_PLAN = (
    tuple((0, ORDERS[chunk], chunk, 4) for chunk in range(4))
    + tuple((1, ORDERS[chunk], chunk, 4) for chunk in range(4))
    + tuple((4, ORDERS[chunk], chunk, 4) for chunk in range(4))
    + ((3, Y_FIRST, 0, 2), (3, Z_THEN_X, 1, 2), (2, X_FIRST, 0, 1))
)
TABLE_PLAN = tuple((0, ((0, 1), (1, 0))[chunk % 2], chunk, 4) for chunk in range(4))
LAYER_PACE = (6, 5, 6)
TABLE_PACE = (4, 2, 1)


def after(value, *others):
    return lax.optimization_barrier((value,) + others)[0]


def per_device(
    tokens,
    lengths,
    levels,
    noise_rows,
    embed_table,
    w_in,
    ln_attn,
    w_qkv,
    w_proj,
    ln_mlp,
    w_up,
    w_down,
    ln_final,
    w_out,
):
    sec = lax.axis_index("section")
    pos = lax.axis_index("dp")
    first_section = sec == 0
    last_section = sec == 1
    rows = tokens.shape[0]
    seqs = lengths.shape[0]
    length = rows // seqs
    width = w_out.shape[0] * 4
    emb = w_out.shape[1]
    vocab_part = embed_table.shape[0]
    gains = jnp.concatenate(
        [ln_attn, ln_mlp, ln_final[None], jnp.zeros((13, ln_final.shape[0]), jnp.bfloat16)], 0
    )
    ids = jnp.concatenate(
        [
            tokens.reshape(-1, 128),
            jnp.concatenate([lengths, jnp.zeros((128 - seqs,), jnp.int32)])[None],
            jnp.zeros((7 - rows // 128, 128), jnp.int32),
        ],
        0,
    )
    shards = (w_qkv[0], w_proj[0], w_up[0], w_down[0], w_in, w_out, gains, ids)
    sizes = [s.shape[0] for s in shards]

    def cut(idx, count, whole=False):
        return tuple((idx, at * sizes[idx] // count, sizes[idx] // count, whole) for at in range(count))

    layer = cut(0, 2) + cut(2, 2) + cut(3, 2)
    wholes = gather_all(
        shards,
        cut(7, 1, True) + cut(6, 1, True) + cut(4, 1) + layer + cut(1, 4, True),
        cut(6, 1, True) + layer + cut(5, 1) + cut(1, 4, True),
        0,
    )
    qkv_weight, proj_weight, up_weight, down_weight, in_weight, out_weight, gain_all, line_ids = wholes
    gain_all = gain_all.reshape(4, 16, -1).astype(jnp.float32)
    gain_attn = gain_all[:, 0].reshape(-1)
    gain_mlp = gain_all[:, 1].reshape(-1)
    final_gain = gain_all[:, 2].reshape(-1)
    weights = (qkv_weight, proj_weight, up_weight, down_weight)
    gain_attn = gain_attn[None]
    gain_mlp = gain_mlp[None]
    final_gain = final_gain[None]
    loss_scale = LOSS_GAIN / math.sqrt(rows * lax.axis_size(("group", "dp")))

    def look_up():
        local = line_ids.reshape(4, 8, 128)[:, : rows // 128].reshape(-1) - pos * vocab_part
        hit = local[:, None] == lax.broadcasted_iota(jnp.int32, (1, vocab_part), 1)
        return product(hit.astype(jnp.bfloat16), embed_table).astype(jnp.bfloat16)

    looked_parts = only_on(first_section, look_up).reshape(4, rows, emb)
    looked_parts, all_ids = swap_rows(looked_parts, line_ids, 1)
    all_tokens = all_ids.reshape(16, 8, 128)[:, : rows // 128].reshape(-1)
    noise_level = jnp.exp(LOG_LOW + levels.astype(jnp.float32) * (LOG_SPAN / (LEVELS - 1)))
    scale_in = lax.rsqrt(EMB_VAR + noise_level * noise_level)
    row_level = jnp.repeat(noise_level, length)[:, None]
    row_scale = jnp.repeat(scale_in, length)[:, None]

    def front():
        looked = jnp.sum(looked_parts.astype(jnp.float32), 0)
        mixed_in = ((looked + row_level * noise_rows.astype(jnp.float32)) * row_scale).astype(
            jnp.bfloat16
        )
        return mixed_in, product(mixed_in, in_weight)

    mixed_in, x_first = only_on(first_section, front)
    *kept, out_first = run_forward(
        0, x_first, gain_attn, gain_mlp, lengths, final_gain, out_weight, weights, None
    )
    x_second = passed_along(out_first, "section", 1)
    *kept, final_in, projected = run_forward(
        1, x_second, gain_attn, gain_mlp, lengths, final_gain, out_weight, weights, kept
    )
    line_parts = line_ids.reshape(4, 8, 128)
    line_tokens = line_parts[:, : rows // 128].reshape(1, -1)
    line_counts = line_parts[:, rows // 128, :seqs].reshape(-1, 1)
    line_valid = jnp.arange(length, dtype=jnp.int32)[None, :] < line_counts
    line_scale = jnp.where(line_valid.reshape(1, -1), loss_scale, 0.0)
    grad_proj, entropy, table_g = run_vocabulary(projected, line_tokens, line_scale, embed_table, 2)
    (table_fin,) = reduce_all(
        (table_g,),
        TABLE_PLAN,
        0,
        3,
        TABLE_PACE,
        spread=False,
    )
    made = run_backward(
        1, grad_proj, gain_attn, gain_mlp, lengths, final_gain, out_weight, kept, weights, None
    )
    grad_first = passed_along(after(made[4], table_fin), "section", -1)
    made = run_backward(
        0, grad_first, gain_attn, gain_mlp, lengths, final_gain, out_weight, kept, weights, made
    )
    shape = in_weight.shape

    def front_edge():
        looked_grad = (product_nt(made[4], in_weight) * row_scale).astype(jnp.bfloat16)
        return product_tn(mixed_in, made[4]).astype(jnp.bfloat16), looked_grad

    def back_edge():
        edge = product_tn(final_in, grad_proj).astype(jnp.bfloat16)
        edge = edge.reshape(4, shape[0] // 4, shape[1]).reshape(shape)
        return edge, jnp.zeros((rows, emb), jnp.bfloat16)

    edge_g, looked_grad = lax.cond(first_section, front_edge, back_edge)
    gain_rows = made[5]
    gain_rows = gain_rows.reshape(8, 4, width // 4).transpose(1, 0, 2)

    order = (
        (kept[6], made[1]),
        (kept[8], made[0]),
        edge_g,
        (kept[4], made[2]),
        (kept[1], made[3]),
    )
    up_r, down_r, edge_r, proj_r, qkv_r, gain_r, table_r = reduce_all(
        order,
        LAYER_PLAN,
        None,
        4,
        LAYER_PACE,
        gains=gain_rows,
        look=(all_tokens.reshape(16, 1, rows), looked_grad, table_fin),
    )
    loss_low = after(entropy, gain_r)[0].astype(jnp.bfloat16)
    mine = (table_r, edge_r, gain_r, loss_low)
    theirs = lax.ppermute(mine, "section", [(0, 1), (1, 0)])

    def pair_of(at):
        low = jnp.where(first_section, mine[at], theirs[at])
        high = jnp.where(first_section, theirs[at], mine[at])
        return low, high

    up_r, down_r, proj_r, qkv_r = widen((up_r, down_r, proj_r, qkv_r))
    table_out = pair_of(0)[0].astype(jnp.float32)
    in_r, out_r = pair_of(1)
    final_r = pair_of(2)[1][2]
    token_loss = pair_of(3)[0]
    return (
        token_loss,
        table_out,
        in_r.astype(jnp.float32),
        gain_r[0][None],
        qkv_r[None],
        proj_r[None],
        gain_r[1][None],
        up_r[None],
        down_r[None],
        final_r,
        out_r.astype(jnp.float32).reshape(-1, emb),
    )


def solution(mesh):
    placed = (
        P(("group", "dp")),
        P(("group", "dp")),
        P(("group", "dp")),
        P(("group", "dp"), None),
        P("dp", None),
        P("dp", None),
        P("section", "dp"),
        P("section", "dp", None),
        P("section", "dp", None),
        P("section", "dp"),
        P("section", "dp", None),
        P("section", "dp", None),
        P("dp"),
        P("dp", None),
    )
    fits = (mesh.shape["section"], mesh.shape["group"], mesh.shape["dp"]) == (2, 4, 4)
    return jax.shard_map(
        per_device if fits else per_device_general,
        mesh=mesh,
        in_specs=placed,
        out_specs=(
            P(("group", "dp")),
            P("dp", None),
            P("dp", None),
            P("section", "dp"),
            P("section", "dp", None),
            P("section", "dp", None),
            P("section", "dp"),
            P("section", "dp", None),
            P("section", "dp", None),
            P("dp"),
            P("dp", None),
        ),
        check_vma=False,
    )
```
